32 devices in a mesh: gx: 4 (over z), gy: 8 (over y, x, core).
Axes of the slice: x: 2, y: 2, z: 4, core: 2. Of those that a mesh axis runs over, the one named last changes fastest.
Arguments:
- tokens: bfloat16 [4096, 2048], P(('gx', 'gy')), may hold values from -6 to 6
- cotangent: bfloat16 [4096, 2048], P(('gx', 'gy')), may hold values from -6 to 6
- expert_ids: int32 [4096, 8], P(('gx', 'gy')), may hold values from 0 to 15, all different within a row; in each aligned block of 128 rows (0 to 127, 128 to 255, ...) at most 96 rows name the same one
- doc_ids: int32 [4096], P('gx'), may hold values from 0 to 7, never falling along the last dimension, each value on 1 to 1024 neighbouring positions
- clip_rank: int32 [1], replicated, may hold values from 2 to 13
- attn_gain: float32 [2048], replicated, may hold values from 0.5 to 1.5
- moe_gain: float32 [2048], replicated, may hold values from 0.5 to 1.5
- query_gain: float32 [128], replicated, may hold values from 0.25 to 1.75
- key_gain: float32 [128], replicated, may hold values from 0.25 to 1.75
- query_weight: bfloat16 [2048, 2048], P('gx', 'gy')
- key_weight: bfloat16 [2048, 2048], P('gx', 'gy')
- value_weight: bfloat16 [2048, 2048], P('gx', 'gy'), may hold values from -0.125 to 0.125
- out_weight: bfloat16 [2048, 2048], P('gy', 'gx'), may hold values from -2 to 2
- router_weight: bfloat16 [2048, 16], replicated, may hold values from -0.0625 to 0.0625
- gate_weight: bfloat16 [32, 2048, 512], P(('gx', 'gy')), may hold values from -0.125 to 0.125
- up_weight: bfloat16 [32, 2048, 512], P(('gx', 'gy')), may hold values from -0.125 to 0.125
- down_weight: bfloat16 [32, 512, 2048], P(('gx', 'gy')), may hold values from -0.75 to 0.75
Outputs:
- output: bfloat16 [4096, 2048], P(('gx', 'gy'))
- input_grad: float32 [4096, 2048], P(('gx', 'gy'))
- attn_gain_grad: float32 [2048], replicated
- moe_gain_grad: float32 [2048], replicated
- query_gain_grad: float32 [128], replicated
- key_gain_grad: float32 [128], replicated
- query_grad: float32 [2048, 2048], P('gx', 'gy')
- key_grad: float32 [2048, 2048], P('gx', 'gy')
- value_grad: float32 [2048, 2048], P('gx', 'gy')
- out_grad: float32 [2048, 2048], P('gy', 'gx')
- router_grad: float32 [2048, 16], replicated
- gate_grad: float32 [32, 2048, 512], P(('gx', 'gy'))
- up_grad: float32 [32, 2048, 512], P(('gx', 'gy'))
- down_grad: float32 [32, 512, 2048], P(('gx', 'gy'))
- query_clipped: bfloat16 [2048, 2048], P('gx', 'gy')
- key_clipped: bfloat16 [2048, 2048], P('gx', 'gy')
- clip_factors: float32 [16], replicated
The draws below stay inside these ranges and needn't reach their ends.
Inputs may be any that keep to these rules, and one draw needn't show every extreme that they name: `expert_ids`: each row names 8 different experts. Among the 128 rows of one device no expert is named more than 96 times, and in every draw some device names some expert exactly 96 times. `doc_ids`: never falls from one token to the next; each value covers 1 to 1024 consecutive tokens, and one covers exactly 1024.
All inputs are finite; a program needn't handle non-finite values.
Results may differ from the reference program's by a relative error of at most 0.015.
Values may be sent and summed in bfloat16 or wider, within the bound.
A program may use at most 256 MiB of HBM per device.

```python
import math
import jax
import jax.numpy as jnp
import numpy as np
from jax import lax

D = 2048
NH = 16
HD = 128
FF_E = 1024
TOP = 8
TOK_DEV = 128
EXPERTS = 16
HALF = 512
SEQ = 1024
TOKENS = 4096
CAP = 96
QB = 512
N_GX = 4
N_GY = 8


def paired_projections(key):
    base = jax.random.fold_in(key, 4711)
    first_key, second_key, order_key = jax.random.split(base, 3)
    scale = D ** (-0.5)
    query_part = jnp.clip(jax.random.normal(first_key, (D, D), jnp.float32), -6.0, 6.0) * scale
    noise_part = jnp.clip(jax.random.normal(second_key, (D, D), jnp.float32), -6.0, 6.0) * scale
    ranks = jax.random.permutation(order_key, NH).astype(jnp.float32)
    mixing = 0.9 * ranks / (NH - 1)
    columns = jnp.repeat(mixing, HD)[None, :]
    key_part = columns * query_part + jnp.sqrt(1.0 - columns * columns) * noise_part
    return (query_part, key_part)


def draw_query_weight(key, part):
    return paired_projections(key)[0].astype(jnp.bfloat16)


def draw_key_weight(key, part):
    return paired_projections(key)[1].astype(jnp.bfloat16)


def levels(own_key, shape, shards, least, top_value):
    def one(position, shards_of):
        heights = jax.random.uniform(jax.random.fold_in(jax.random.fold_in(own_key, 6), position), (shards_of,), jnp.float32, least / len(shards), top_value / len(shards))
        return jnp.repeat(jnp.exp(heights), shape[position] // shards_of).reshape((-1,) + (1,) * (len(shape) - position - 1))

    loudness = one(*shards[0])
    for cut in shards[1:]:
        loudness = loudness * one(*cut)
    return loudness


def split_up(number_of, total, most, slope):
    portions = [(1 << 20) // math.isqrt(grade ** slope) + 1 for grade in range(2, number_of + 1)]
    surplus, counts = total - most - (number_of - 1), [1] * (number_of - 1)
    while surplus > 0:
        free = [i for i in range(number_of - 1) if counts[i] < most]
        whole, budget = sum([portions[i] for i in free]), surplus
        for i in free:
            extra = min(most - counts[i], max(1, budget * portions[i] // whole), surplus)
            counts[i] = counts[i] + extra
            surplus = surplus - extra
    return np.array([most] + counts)


def uneven_parts(own_key, count, total, most, lean):
    if count == 2:
        one = jax.random.randint(own_key, (), max(1, total - most), min(most, total - 1) + 1)
        return jnp.stack([one, total - one])
    lengths = jnp.asarray(split_up(count, total, most, lean), jnp.int32)
    pairs = (count - 1) // 2
    giver, taker = lengths[1:1 + 2 * pairs:2], lengths[2:2 + 2 * pairs:2]
    margin = jnp.minimum(giver - 1, most - taker)
    passed = jax.random.randint(jax.random.fold_in(own_key, 1), (pairs,), 0, 1 << 20) % (margin + 1)
    lengths = lengths.at[1:1 + 2 * pairs:2].set(giver - passed).at[2:2 + 2 * pairs:2].set(taker + passed)
    return lengths[jax.random.permutation(jax.random.fold_in(own_key, 2), count)]


def shared_out(key, own, number, rows, count, top, most, lean):
    order = jax.random.permutation(key, count)
    packed, usual = portions_of(count, rows * top, most, lean, True), portions_of(count, rows * top, most, lean, False)
    places = jnp.arange(count)

    def named(lengths, turn):
        used = int((lengths > 0).sum())
        fixed = max(1, used // 4)
        moved = fixed + (places - fixed + turn * (used - fixed)) % max(1, count - fixed)
        return jnp.zeros((count,), jnp.int32).at[order[jnp.where(places < fixed, places, moved)]].set(jnp.asarray(lengths, jnp.int32))

    lengths = jnp.where(number % 4 == 0, named(packed, number // 4), named(usual, number - number // 4 - 1))
    mixed = jax.random.permutation(jax.random.fold_in(own, 3), count)
    source_of, sink = mixed[0:count // 2 * 2:2], mixed[1:count // 2 * 2:2]
    room = jnp.minimum(lengths[source_of] - 1, most - lengths[sink]) // 2
    room = jnp.where((source_of == order[0]) | (sink == order[0]) | (lengths[sink] == 0), 0, jnp.maximum(room, 0))
    moved = jax.random.randint(jax.random.fold_in(own, 4), (count // 2,), 0, 1 << 20) % (room + 1)
    lengths = lengths.at[source_of].add(-moved).at[sink].add(moved)
    items = jnp.searchsorted(jnp.cumsum(lengths), jnp.arange(rows * top), side="right").astype(jnp.int32)
    listing = items.reshape(top, rows).T
    listing = listing[jax.random.permutation(jax.random.fold_in(own, 1), rows)]
    turn = jax.random.randint(jax.random.fold_in(own, 2), (rows, 1), 0, top)
    return jnp.take_along_axis(listing, (jnp.arange(top)[None, :] + turn) % top, axis=1)


def portions_of(number_of, total, reach, lean, full):
    loads = [(1 << 20) // math.isqrt(grade ** lean) + 1 for grade in range(1, number_of + 1)]
    largest = reach if full else min(reach, max(-(-total // number_of), total * loads[0] // sum(loads)))
    least = 1 if total - largest >= number_of - 1 else 0
    given, spare = [largest] + [least] * (number_of - 1), total - largest - least * (number_of - 1)
    while spare > 0:
        movable = [i for i in range(1, number_of) if given[i] < largest] or [i for i in range(1, number_of) if given[i] < reach]
        mass, remaining = sum([loads[i] for i in movable]), spare
        for i in movable:
            more = min(reach - given[i], max(1, remaining * loads[i] // mass), spare)
            given[i] = given[i] + more
            spare = spare - more
    return np.array(given)


def noise(key, dims, scale, most, cuts=(), held_as=jnp.bfloat16):
    array = jax.random.normal(key, dims, jnp.float32) * scale
    if len(cuts) > 0:
        array = levels(key, dims, cuts, -0.22, 0.18) * array
    return jnp.clip(array, min=-most, max=most).astype(held_as)


def setup_inputs(seed: int = 0) -> dict:
    streams_of = jax.random.split(jax.random.key(seed), 18)
    tokens = noise(streams_of[0], (TOKENS, D), 1.0, 6.0, ((0, 32),))
    cotangent = noise(streams_of[1], (TOKENS, D), 1.0, 6.0, ((0, 32),))
    expert_ids_keys = jax.random.split(jax.random.fold_in(streams_of[2], 1), TOKENS // TOK_DEV)
    expert_ids_turns = jax.random.permutation(jax.random.fold_in(streams_of[2], 3), TOKENS // TOK_DEV)
    expert_ids = jax.vmap(lambda own, number: shared_out(jax.random.fold_in(streams_of[2], 2), own, number, TOK_DEV, EXPERTS, TOP, CAP, 1))(expert_ids_keys, expert_ids_turns).reshape((TOKENS, TOP))
    doc_ids = jnp.searchsorted(jnp.cumsum(uneven_parts(streams_of[3], 2 * N_GX, TOKENS, SEQ, 1)), jnp.arange(TOKENS), side="right").astype(jnp.int32)
    clip_rank = jax.random.randint(streams_of[4], (1,), 2, NH - 2).astype(jnp.int32)
    attn_gain = jnp.clip(1.0 + 0.1 * jax.random.normal(streams_of[5], (D,), jnp.float32), 0.5, 1.5)
    moe_gain = jnp.clip(1.0 + 0.1 * jax.random.normal(streams_of[6], (D,), jnp.float32), 0.5, 1.5)
    query_gain = jnp.clip(1.0 + 0.15 * jax.random.normal(streams_of[7], (HD,), jnp.float32), 0.25, 1.75)
    key_gain = jnp.clip(1.0 + 0.15 * jax.random.normal(streams_of[8], (HD,), jnp.float32), 0.25, 1.75)
    query_weight = draw_query_weight(jax.random.fold_in(streams_of[17], 71), 0)
    key_weight = draw_key_weight(jax.random.fold_in(streams_of[17], 71), 0)
    value_weight = noise(streams_of[11], (D, D), D ** -0.5, 0.125, ((0, 4), (1, 8)))
    out_weight = noise(streams_of[12], (D, D), (D // 256) ** -0.5, 2.0, ((0, 8), (1, 4)))
    router_weight = noise(streams_of[13], (D, EXPERTS), (4 * D) ** -0.5, 0.0625)
    gate_weight = noise(streams_of[14], (2 * EXPERTS, D, HALF), D ** -0.5, 0.125, ((0, 32),))
    up_weight = noise(streams_of[15], (2 * EXPERTS, D, HALF), D ** -0.5, 0.125, ((0, 32),))
    down_weight = noise(streams_of[16], (2 * EXPERTS, HALF, D), (FF_E // 16) ** -0.5, 0.75, ((0, 32),))
    return dict(tokens=tokens, cotangent=cotangent, expert_ids=expert_ids, doc_ids=doc_ids, clip_rank=clip_rank, attn_gain=attn_gain, moe_gain=moe_gain, query_gain=query_gain, key_gain=key_gain, query_weight=query_weight, key_weight=key_weight, value_weight=value_weight, out_weight=out_weight, router_weight=router_weight, gate_weight=gate_weight, up_weight=up_weight, down_weight=down_weight)


EPSILON = 1e-06
NEGATIVE = -1e+30

@jax.custom_vjp
def low(v):
    return lax.optimization_barrier(v.astype(jnp.bfloat16)).astype(jnp.float32)

@jax.custom_vjp
def low_back(v):
    return v

def low_keep(v):
    return (low(v), None)

def low_pass(kept, grad):
    return (grad,)

def back_keep(v):
    return (v, None)

def back_low(kept, grad):
    return (low(grad),)
low.defvjp(low_keep, low_pass)
low_back.defvjp(back_keep, back_low)

def norm_rows(values, gain_row):
    return values * lax.rsqrt(lax.optimization_barrier(jnp.mean(values * values, axis=-1, keepdims=True)) + EPSILON) * gain_row

def rotary(values):
    halfway = HD // 2
    positions = jnp.arange(SEQ, dtype=jnp.float32)
    frequency = jnp.exp(jnp.arange(halfway, dtype=jnp.float32) * (-2.0 * jnp.log(10000.0) / HD))
    angles = (positions[:, None] * frequency[None, :])[:, None, :]
    cosine = jnp.cos(angles)
    sine_table = jnp.sin(angles)
    first_half = values[..., :halfway]
    second = values[..., halfway:]
    return jnp.concatenate([first_half * cosine - second * sine_table, second * cosine + first_half * sine_table], axis=-1)

def attend_sequence(pieces):
    queries, key_rows, values, documents = pieces
    block_count = SEQ // QB

    def one_block(block_pieces):
        query_block, doc_block = block_pieces
        scores = jnp.einsum('qhd,khd->hqk', query_block, key_rows, precision=lax.Precision.HIGHEST) * HD ** (-0.5)
        scores = low_back(scores)
        same_doc = doc_block[:, None] == documents[None, :]
        scores = jnp.where(same_doc[None], scores, NEGATIVE)
        highest = lax.optimization_barrier(jnp.max(scores, axis=-1, keepdims=True))
        weights = jnp.exp(scores - highest)
        shares = weights / lax.optimization_barrier(jnp.sum(weights, axis=-1, keepdims=True))
        mixed_heads = jnp.einsum('hqk,khd->qhd', low(shares), values, precision=lax.Precision.HIGHEST)
        return (mixed_heads, lax.optimization_barrier(jnp.max(highest[..., 0], axis=-1)))
    mixed_heads, peak_blocks = lax.map(jax.checkpoint(one_block), (queries.reshape(block_count, QB, NH, HD), documents.reshape(block_count, QB)))
    return (mixed_heads.reshape(SEQ, NH * HD), lax.optimization_barrier(jnp.max(peak_blocks, axis=0)))

def route_tables(expert_ids):
    groups = N_GX * N_GY
    route_count = TOK_DEV * TOP
    flat_ids = expert_ids.reshape(groups, route_count)
    onehot = (flat_ids[:, :, None] == jnp.arange(EXPERTS, dtype=jnp.int32)[None, None, :]).astype(jnp.int32)
    earlier = jnp.cumsum(onehot, axis=1) - onehot
    slot_index = lax.optimization_barrier(jnp.sum(earlier * onehot, axis=-1))
    device_index = jnp.arange(groups, dtype=jnp.int32)[:, None]
    target = flat_ids * (CAP * groups) + device_index * CAP + slot_index
    token_index = device_index * TOK_DEV + jnp.arange(route_count, dtype=jnp.int32)[None, :] // TOP
    source = jnp.full((EXPERTS * CAP * groups,), TOKENS, jnp.int32).at[target.reshape(-1)].set(token_index.reshape(-1))
    return (target.reshape(-1), source)

def layer(inputs, attn_gain, moe_gain, query_gain, key_gain, query_weight, key_weight, value_weight, out_weight, router_weight, gate_weight, up_weight, down_weight, expert_ids, doc_ids, target, source):
    highest_prec = lax.Precision.HIGHEST
    acts = low(norm_rows(inputs, attn_gain))
    queries = low_back(jnp.dot(acts, query_weight, precision=highest_prec))
    key_rows = low_back(jnp.dot(acts, key_weight, precision=highest_prec))
    value_rows = low_back(low(jnp.dot(acts, value_weight, precision=highest_prec)))
    query_ready = low(rotary(norm_rows(queries.reshape(N_GX, SEQ, NH, HD), query_gain)))
    key_ready = low(rotary(norm_rows(key_rows.reshape(N_GX, SEQ, NH, HD), key_gain)))
    mixed, peak_seqs = lax.map(jax.checkpoint(attend_sequence), (query_ready, key_ready, value_rows.reshape(N_GX, SEQ, NH, HD), doc_ids.reshape(N_GX, SEQ)))
    mixed = low_back(low(mixed.reshape(TOKENS, D)))
    attended = low_back(jnp.dot(mixed, out_weight, precision=highest_prec))
    residual = inputs + attended
    moe_in = low(norm_rows(residual, moe_gain))
    logits = low_back(jnp.dot(moe_in, router_weight, precision=highest_prec))
    shares = jax.nn.softmax(logits, axis=-1)
    chosen = jnp.take_along_axis(shares, expert_ids, axis=-1)
    gate_share = chosen / lax.optimization_barrier(jnp.sum(chosen, axis=-1, keepdims=True))
    slot_count = CAP * N_GX * N_GY
    slot_gate = jnp.zeros((EXPERTS * slot_count,), jnp.float32).at[target].set(gate_share.reshape(-1))
    padded = jnp.concatenate([moe_in, jnp.zeros((1, D), jnp.float32)], axis=0)

    def expert_rows(pieces):
        rows_index, gate_column, gate_pair, up_pair, down_pair = pieces
        gathered = padded[rows_index]
        totals = jnp.zeros((slot_count, D), jnp.float32)
        for half_index in range(2):
            copied = low_back(gathered)
            gate_val = low_back(jnp.dot(copied, gate_pair[half_index], precision=highest_prec))
            up_val = low_back(jnp.dot(copied, up_pair[half_index], precision=highest_prec))
            hidden = low(jax.nn.silu(gate_val) * up_val)
            totals = totals + low_back(low(jnp.dot(hidden, down_pair[half_index], precision=highest_prec)))
        return gate_column[:, None] * totals
    expert_out = lax.map(jax.checkpoint(expert_rows), (source.reshape(EXPERTS, slot_count), slot_gate.reshape(EXPERTS, slot_count), gate_weight.reshape(EXPERTS, 2, D, HALF), up_weight.reshape(EXPERTS, 2, D, HALF), down_weight.reshape(EXPERTS, 2, HALF, D)))
    moe_out = jnp.zeros((TOKENS + 1, D), jnp.float32).at[source].add(expert_out.reshape(EXPERTS * slot_count, D))[:TOKENS]
    return (residual + moe_out, lax.optimization_barrier(jnp.max(peak_seqs, axis=0)))

def reference(tokens, cotangent, expert_ids, doc_ids, clip_rank, attn_gain, moe_gain, query_gain, key_gain, query_weight, key_weight, value_weight, out_weight, router_weight, gate_weight, up_weight, down_weight):
    target, source = route_tables(expert_ids)
    floats = [argument.astype(jnp.float32) for argument in (tokens, attn_gain, moe_gain, query_gain, key_gain, query_weight, key_weight, value_weight, out_weight, router_weight, gate_weight, up_weight, down_weight)]

    def forward(*params):
        return layer(*params, expert_ids, doc_ids, target, source)
    block_out, pullback, head_peaks = jax.vjp(forward, *floats, has_aux=True)
    gradients = pullback(cotangent.astype(jnp.float32))
    ranked = -jnp.sort(-head_peaks)
    limit = jnp.sum(jnp.where(jnp.arange(NH, dtype=jnp.int32) == clip_rank[0], ranked, 0.0))
    factors = jnp.where(head_peaks > limit, limit / head_peaks, 1.0)
    columns = jnp.repeat(jnp.sqrt(factors), HD)
    query_clipped = (floats[5] * columns[None, :]).astype(jnp.bfloat16)
    key_clipped = (floats[6] * columns[None, :]).astype(jnp.bfloat16)
    return (block_out.astype(jnp.bfloat16), gradients[0], gradients[1], gradients[2], gradients[3], gradients[4], gradients[5], gradients[6], gradients[7], gradients[8], gradients[9], gradients[10], gradients[11], gradients[12], query_clipped, key_clipped, factors)
```

```python
from functools import partial

import jax
import jax.numpy as jnp
from jax import lax
from jax.sharding import PartitionSpec as P

NH = 16
HD = 128
TOP = 8


EPSILON = 1e-06
NEGATIVE = -1e30


def norm_rows(values, gain_row):
    return (
        values * lax.rsqrt(jnp.mean(values * values, axis=-1, keepdims=True) + EPSILON) * gain_row
    )


def rotary(values):
    length = values.shape[0]
    halfway = values.shape[-1] // 2
    positions = jnp.arange(length, dtype=jnp.float32)
    frequency = jnp.exp(
        jnp.arange(halfway, dtype=jnp.float32) * (-2.0 * jnp.log(10000.0) / values.shape[-1])
    )
    angles = (positions[:, None] * frequency[None, :])[:, None, :]
    cosine = jnp.cos(angles)
    sine_table = jnp.sin(angles)
    first_half = values[..., :halfway]
    second = values[..., halfway:]
    return jnp.concatenate(
        [first_half * cosine - second * sine_table, second * cosine + first_half * sine_table],
        axis=-1,
    )


def prepare_heads(raw_heads, gain_row):
    return rotary(norm_rows(raw_heads, gain_row))


def route_gates(id_table, logits):
    shares = jax.nn.softmax(logits, axis=-1)
    experts = logits.shape[-1]
    matches = id_table[:, :, None] == jnp.arange(experts, dtype=jnp.int32)[None, None, :]
    chosen = jnp.sum(jnp.where(matches, shares[:, None, :], 0.0), axis=-1)
    return chosen / jnp.sum(chosen, axis=-1, keepdims=True)


def dense_gates(all_ids, logits, expert):
    shares = jax.nn.softmax(logits, axis=-1)
    columns = jnp.arange(logits.shape[-1], dtype=jnp.int32)
    routed = jnp.any(all_ids[:, :, None] == columns[None, None, :], axis=1)
    chosen = jnp.where(routed, shares, 0.0)
    own = jnp.sum(jnp.where(columns[None, :] == expert, chosen, 0.0), axis=-1)
    return own / jnp.sum(chosen, axis=-1)


def contract_rows(left_side, right_side):
    return lax.dot_general(
        left_side, right_side, (((0,), (0,)), ((), ())), preferred_element_type=jnp.float32
    )


def contract_cols(left_side, right_side):
    return lax.dot_general(
        left_side, right_side, (((1,), (1,)), ((), ())), preferred_element_type=jnp.float32
    )


def routed_experts(
    moe_in, cotangent, expert_ids, gate_share, router_weight, gate_weight, up_weight, down_weight
):
    tok_rows = moe_in.shape[0]
    experts = router_weight.shape[1]
    width_all = moe_in.shape[1]
    capacity = tok_rows * TOP * 3 // (2 * experts)
    route_count = tok_rows * TOP
    flat_ids = expert_ids.reshape(route_count)
    onehot = (flat_ids[:, None] == jnp.arange(experts, dtype=jnp.int32)[None, :]).astype(jnp.int32)
    earlier = jnp.cumsum(onehot, axis=0) - onehot
    slot_index = jnp.sum(earlier * onehot, axis=1)
    target = flat_ids * capacity + slot_index
    source = (
        jnp.full((experts * capacity,), tok_rows, jnp.int32)
        .at[target]
        .set(jnp.arange(route_count, dtype=jnp.int32) // TOP)
    )
    padded_in = jnp.concatenate([moe_in, jnp.zeros((1, width_all), jnp.bfloat16)], axis=0)
    packed = padded_in[source].reshape(experts, 1, capacity, width_all)
    outgoing = jnp.broadcast_to(packed, (experts, 2, capacity, width_all)).reshape(
        2 * experts, capacity, width_all
    )
    arrived = lax.all_to_all(outgoing, ("gx", "gy"), split_axis=0, concat_axis=1, tiled=True)[0]
    gate_in = gate_weight[0]
    up_in = up_weight[0]
    down_in = down_weight[0]
    gate_val = jnp.dot(arrived, gate_in, preferred_element_type=jnp.float32)
    up_val = jnp.dot(arrived, up_in, preferred_element_type=jnp.float32)
    hidden = (jax.nn.silu(gate_val) * up_val).astype(jnp.bfloat16)
    produced = jnp.dot(hidden, down_in, preferred_element_type=jnp.float32).astype(jnp.bfloat16)
    returned = lax.all_to_all(produced[None], ("gx", "gy"), split_axis=1, concat_axis=0, tiled=True)
    summed = (
        returned.reshape(experts, 2, capacity, width_all)
        .astype(jnp.float32)
        .sum(axis=1)
        .reshape(experts * capacity, width_all)
    )
    route_out = summed[target]
    gates_flat = gate_share.reshape(route_count)
    moe_out = jnp.sum((gates_flat[:, None] * route_out).reshape(tok_rows, TOP, width_all), axis=1)
    grad_out = cotangent.astype(jnp.float32)
    grad_gates = jnp.sum(
        route_out.reshape(tok_rows, TOP, width_all) * grad_out[:, None, :], axis=-1
    )
    slot_gate = jnp.zeros((experts * capacity,), jnp.float32).at[target].set(gates_flat)
    padded_grad = jnp.concatenate([grad_out, jnp.zeros((1, width_all), jnp.float32)], axis=0)
    grad_packed = (
        (slot_gate[:, None] * padded_grad[source])
        .astype(jnp.bfloat16)
        .reshape(experts, 1, capacity, width_all)
    )
    grad_outgoing = jnp.broadcast_to(grad_packed, (experts, 2, capacity, width_all)).reshape(
        2 * experts, capacity, width_all
    )
    grad_arrived = lax.all_to_all(
        grad_outgoing, ("gx", "gy"), split_axis=0, concat_axis=1, tiled=True
    )[0]
    rows_in, grad_use = (arrived, grad_arrived)
    gate_use, up_use, hidden_use = (gate_val, up_val, hidden)
    sigmoid_gate = jax.nn.sigmoid(gate_use)
    silu_gate = gate_use * sigmoid_gate
    grad_hidden = contract_cols(grad_use, down_in)
    down_part = contract_rows(hidden_use, grad_use)
    grad_gate = (
        grad_hidden * up_use * sigmoid_gate * (1.0 + gate_use * (1.0 - sigmoid_gate))
    ).astype(jnp.bfloat16)
    grad_up = (grad_hidden * silu_gate).astype(jnp.bfloat16)
    gate_part = contract_rows(rows_in, grad_gate)
    up_part = contract_rows(rows_in, grad_up)
    grad_in = contract_cols(grad_gate, gate_in) + contract_cols(grad_up, up_in)
    grad_back = lax.all_to_all(
        grad_in.astype(jnp.bfloat16)[None], ("gx", "gy"), split_axis=1, concat_axis=0, tiled=True
    )
    grad_summed = (
        grad_back.reshape(experts, 2, capacity, width_all)
        .astype(jnp.float32)
        .sum(axis=1)
        .reshape(experts * capacity, width_all)
    )
    grad_moe_in = jnp.sum(grad_summed[target].reshape(tok_rows, TOP, width_all), axis=1)
    return moe_out, grad_gates, grad_moe_in, gate_part, up_part, down_part


def dense_experts(
    moe_in, cotangent, expert_ids, gate_share, router_weight, gate_weight, up_weight, down_weight
):
    experts = router_weight.shape[1]
    everyone = ("gx", "gy")
    all_ids = lax.all_gather(expert_ids, everyone, axis=0, tiled=True)
    all_cot = lax.all_gather(cotangent, everyone, axis=0, tiled=True)
    all_moe = lax.all_gather(moe_in, everyone, axis=0, tiled=True)
    rank = lax.axis_index("gx") * lax.axis_size("gy") + lax.axis_index("gy")
    own_gate = dense_gates(
        all_ids, jnp.dot(all_moe, router_weight, preferred_element_type=jnp.float32), rank // 2
    )
    gate_in = gate_weight[0]
    up_in = up_weight[0]
    down_in = down_weight[0]
    gate_val = jnp.dot(all_moe, gate_in, preferred_element_type=jnp.float32)
    up_val = jnp.dot(all_moe, up_in, preferred_element_type=jnp.float32)
    sigmoid_gate = jax.nn.sigmoid(gate_val)
    silu_gate = gate_val * sigmoid_gate
    hidden = (silu_gate * up_val).astype(jnp.bfloat16)
    piece = jnp.dot(hidden, down_in, preferred_element_type=jnp.float32)
    cot_float = all_cot.astype(jnp.float32)
    gate_dots = jnp.sum(piece * cot_float, axis=-1)
    devices = lax.axis_size("gx") * lax.axis_size("gy")
    dots_back = lax.all_to_all(
        gate_dots.reshape(devices, -1), everyone, split_axis=0, concat_axis=0, tiled=True
    )
    dots_experts = dots_back.reshape(experts, 2, -1).sum(axis=1).T
    matches = expert_ids[:, :, None] == jnp.arange(experts, dtype=jnp.int32)[None, None, :]
    grad_gates = jnp.sum(jnp.where(matches, dots_experts[:, None, :], 0.0), axis=-1)
    moe_out = lax.psum_scatter(
        (piece * own_gate[:, None]).astype(jnp.bfloat16), everyone, scatter_dimension=0, tiled=True
    ).astype(jnp.float32)
    grad_use = (cot_float * own_gate[:, None]).astype(jnp.bfloat16)
    grad_hidden = contract_cols(grad_use, down_in)
    down_part = contract_rows(hidden, grad_use)
    grad_gate = (
        grad_hidden * up_val * sigmoid_gate * (1.0 + gate_val * (1.0 - sigmoid_gate))
    ).astype(jnp.bfloat16)
    grad_up = (grad_hidden * silu_gate).astype(jnp.bfloat16)
    gate_part = contract_rows(all_moe, grad_gate)
    up_part = contract_rows(all_moe, grad_up)
    grad_in = contract_cols(grad_gate, gate_in) + contract_cols(grad_up, up_in)
    grad_moe_in = lax.psum_scatter(
        grad_in.astype(jnp.bfloat16), everyone, scatter_dimension=0, tiled=True
    ).astype(jnp.float32)
    return moe_out, grad_gates, grad_moe_in, gate_part, up_part, down_part


def local(
    tokens,
    cotangent,
    expert_ids,
    doc_ids,
    clip_rank,
    attn_gain,
    moe_gain,
    query_gain,
    key_gain,
    query_weight,
    key_weight,
    value_weight,
    out_weight,
    router_weight,
    gate_weight,
    up_weight,
    down_weight,
):
    inputs = tokens.astype(jnp.float32)
    acts_float, norm_pull = jax.vjp(norm_rows, inputs, attn_gain)
    acts_low = acts_float.astype(jnp.bfloat16)
    seq_acts = lax.all_gather(acts_low, "gy", axis=0, tiled=True)
    in_weights = jnp.concatenate([query_weight, key_weight, value_weight], axis=1)
    full_in = lax.all_gather(in_weights, "gx", axis=0, tiled=True)
    out_rows = lax.all_gather(out_weight, "gx", axis=1, tiled=True)
    length = seq_acts.shape[0]
    local_width = query_weight.shape[1]
    local_heads = local_width // HD
    projected = jnp.dot(seq_acts, full_in, preferred_element_type=jnp.float32)
    queries = projected[:, :local_width]
    key_raw = projected[:, local_width : 2 * local_width]
    value_ready = (
        projected[:, 2 * local_width :].astype(jnp.bfloat16).reshape(length, local_heads, HD)
    )
    query_float, query_pull = jax.vjp(
        prepare_heads, queries.reshape(length, local_heads, HD), query_gain
    )
    key_float, key_pull = jax.vjp(prepare_heads, key_raw.reshape(length, local_heads, HD), key_gain)
    query_ready = query_float.astype(jnp.bfloat16)
    key_ready = key_float.astype(jnp.bfloat16)
    block_rows = min(512, length)
    block_count = length // block_rows
    score_scale = HD ** (-0.5)
    query_blocks = query_ready.reshape(block_count, block_rows, local_heads, HD)
    doc_blocks = doc_ids.reshape(block_count, block_rows)

    def block_scores(query_block, doc_block):
        scores = (
            jnp.einsum("qhd,khd->hqk", query_block, key_ready, preferred_element_type=jnp.float32)
            * score_scale
        )
        same_doc = doc_block[:, None] == doc_ids[None, :]
        return jnp.where(same_doc[None], scores, NEGATIVE)

    def forward_block(pieces):
        scores = block_scores(pieces[0], pieces[1])
        highest = jnp.max(scores, axis=-1, keepdims=True)
        weights = jnp.exp(scores - highest)
        totals = jnp.sum(weights, axis=-1, keepdims=True)
        shares = (weights / totals).astype(jnp.bfloat16)
        mixed_heads = jnp.einsum(
            "hqk,khd->qhd", shares, value_ready, preferred_element_type=jnp.float32
        )
        return (
            mixed_heads.astype(jnp.bfloat16),
            highest[..., 0] + jnp.log(totals[..., 0]),
            jnp.max(highest[..., 0], axis=-1),
        )

    mixed_blocks, log_totals, peak_blocks = lax.map(forward_block, (query_blocks, doc_blocks))
    mixed_seq = mixed_blocks.reshape(length, local_width)
    start_head = lax.axis_index("gy") * local_heads
    peak_local = lax.dynamic_update_slice(
        jnp.full((NH,), NEGATIVE, jnp.float32), jnp.max(peak_blocks, axis=0), (start_head,)
    )
    peak_global = lax.pmax(peak_local, ("gx", "gy"))
    attended = lax.psum_scatter(
        jnp.dot(mixed_seq, out_rows, preferred_element_type=jnp.float32).astype(jnp.bfloat16),
        "gy",
        scatter_dimension=0,
        tiled=True,
    ).astype(jnp.float32)
    residual = inputs + attended
    moe_float, moe_pull = jax.vjp(norm_rows, residual, moe_gain)
    moe_in = moe_float.astype(jnp.bfloat16)
    logits = jnp.dot(moe_in, router_weight, preferred_element_type=jnp.float32)
    gate_share, gate_pull = jax.vjp(partial(route_gates, expert_ids), logits)
    experts_pass = dense_experts if router_weight.shape[1] <= 2 * TOP else routed_experts
    moe_out, grad_gates, grad_moe_in, gate_part, up_part, down_part = experts_pass(
        moe_in,
        cotangent,
        expert_ids,
        gate_share,
        router_weight,
        gate_weight,
        up_weight,
        down_weight,
    )
    output = (residual + moe_out).astype(jnp.bfloat16)
    grad_out = cotangent.astype(jnp.float32)
    (grad_logits,) = gate_pull(grad_gates)
    grad_logits_low = grad_logits.astype(jnp.bfloat16)
    router_part = contract_rows(moe_in, grad_logits_low)
    grad_moe_in = grad_moe_in + contract_cols(grad_logits_low, router_weight)
    grad_resid_norm, moe_gain_part = moe_pull(grad_moe_in)
    grad_resid = grad_out + grad_resid_norm
    seq_grad = lax.all_gather(grad_resid.astype(jnp.bfloat16), "gy", axis=0, tiled=True)
    grad_mixed = contract_cols(seq_grad, out_rows).astype(jnp.bfloat16)
    out_part = contract_rows(seq_grad, mixed_seq)

    def backward_block(running, pieces):
        grad_key, grad_value = running
        query_block, grad_block, log_block, doc_block = pieces
        scores = block_scores(query_block, doc_block)
        weights = jnp.exp(scores - log_block[..., None])
        grad_value = grad_value + jnp.einsum(
            "hqk,qhd->khd",
            weights.astype(jnp.bfloat16),
            grad_block,
            preferred_element_type=jnp.float32,
        )
        grad_weights = jnp.einsum(
            "qhd,khd->hqk", grad_block, value_ready, preferred_element_type=jnp.float32
        )
        inner_sum = jnp.sum(weights * grad_weights, axis=-1, keepdims=True)
        grad_scores = (weights * (grad_weights - inner_sum)).astype(jnp.bfloat16)
        grad_query = (
            jnp.einsum("hqk,khd->qhd", grad_scores, key_ready, preferred_element_type=jnp.float32)
            * score_scale
        )
        grad_key = (
            grad_key
            + jnp.einsum(
                "hqk,qhd->khd", grad_scores, query_block, preferred_element_type=jnp.float32
            )
            * score_scale
        )
        return ((grad_key, grad_value), grad_query)

    empty_heads = jnp.zeros((length, local_heads, HD), jnp.float32)
    grad_mixed_blocks = grad_mixed.reshape(block_count, block_rows, local_heads, HD)
    (key_grad_heads, value_grad_heads), query_grad_blocks = lax.scan(
        backward_block,
        (empty_heads, empty_heads),
        (query_blocks, grad_mixed_blocks, log_totals, doc_blocks),
    )
    query_raw_grad, query_gain_part = query_pull(query_grad_blocks.reshape(length, local_heads, HD))
    key_raw_grad, key_gain_part = key_pull(key_grad_heads)
    grad_queries = query_raw_grad.reshape(length, local_width).astype(jnp.bfloat16)
    grad_keys = key_raw_grad.reshape(length, local_width).astype(jnp.bfloat16)
    grad_values = value_grad_heads.reshape(length, local_width).astype(jnp.bfloat16)
    grad_heads = jnp.concatenate([grad_queries, grad_keys, grad_values], axis=1)
    in_sum = lax.psum_scatter(
        contract_rows(seq_acts, grad_heads).astype(jnp.bfloat16),
        "gx",
        scatter_dimension=0,
        tiled=True,
    ).astype(jnp.float32)
    query_sum = in_sum[:, :local_width]
    key_sum = in_sum[:, local_width : 2 * local_width]
    value_sum = in_sum[:, 2 * local_width :]
    out_sum_rows = lax.psum_scatter(
        out_part.astype(jnp.bfloat16), "gx", scatter_dimension=0, tiled=True
    ).astype(jnp.float32)
    grad_acts = lax.psum_scatter(
        contract_cols(grad_heads, full_in).astype(jnp.bfloat16),
        "gy",
        scatter_dimension=0,
        tiled=True,
    ).astype(jnp.float32)
    norm_input_grad, attn_gain_part = norm_pull(grad_acts)
    input_grad = grad_resid + norm_input_grad
    attn_gain_grad, moe_gain_grad, query_gain_grad, key_gain_grad, router_grad = lax.psum(
        (attn_gain_part, moe_gain_part, query_gain_part, key_gain_part, router_part), ("gx", "gy")
    )
    ranked = -jnp.sort(-peak_global)
    limit = jnp.sum(jnp.where(jnp.arange(NH, dtype=jnp.int32) == clip_rank[0], ranked, 0.0))
    factors = jnp.where(peak_global > limit, limit / peak_global, 1.0)
    own_factors = lax.dynamic_slice_in_dim(factors, start_head, local_heads)
    columns = jnp.repeat(jnp.sqrt(own_factors), HD)
    query_clipped = (query_weight.astype(jnp.float32) * columns[None, :]).astype(jnp.bfloat16)
    key_clipped = (key_weight.astype(jnp.float32) * columns[None, :]).astype(jnp.bfloat16)
    return (
        output,
        input_grad,
        attn_gain_grad,
        moe_gain_grad,
        query_gain_grad,
        key_gain_grad,
        query_sum,
        key_sum,
        value_sum,
        out_sum_rows.T,
        router_grad,
        gate_part[None],
        up_part[None],
        down_part[None],
        query_clipped,
        key_clipped,
        factors,
    )


def solution(mesh):
    placed = (
        P(("gx", "gy"), None),
        P(("gx", "gy"), None),
        P(("gx", "gy"), None),
        P("gx"),
        P(),
        P(),
        P(),
        P(),
        P(),
        P("gx", "gy"),
        P("gx", "gy"),
        P("gx", "gy"),
        P("gy", "gx"),
        P(),
        P(("gx", "gy"), None, None),
        P(("gx", "gy"), None, None),
        P(("gx", "gy"), None, None),
    )
    return jax.shard_map(
        local,
        mesh=mesh,
        in_specs=placed,
        out_specs=(
            P(("gx", "gy"), None),
            P(("gx", "gy"), None),
            P(),
            P(),
            P(),
            P(),
            P("gx", "gy"),
            P("gx", "gy"),
            P("gx", "gy"),
            P("gy", "gx"),
            P(),
            P(("gx", "gy"), None, None),
            P(("gx", "gy"), None, None),
            P(("gx", "gy"), None, None),
            P("gx", "gy"),
            P("gx", "gy"),
            P(),
        ),
        check_vma=False,
    )
```

```python
from functools import partial

import jax
import jax.numpy as jnp
from jax import lax
from jax.experimental import pallas as pl
from jax.experimental.pallas import tpu as pltpu
from jax.sharding import PartitionSpec as P

NH = 16
HD = 128
TOP = 8


EPSILON = 1e-06
NEGATIVE = -1e30


def barrier_with(partners):
    barrier = pltpu.get_barrier_semaphore()
    for ok, device in partners:
        @pl.when(ok)
        def _():
            pl.semaphore_signal(barrier, inc=1, device_id=device, device_id_type=pl.DeviceIdType.MESH)
    pl.semaphore_wait(barrier, sum(ok.astype(jnp.int32) for ok, _ in partners))

def gather_kernel(n_z, span, own_ref, out_ref, send_sem, recv_sem, local_sem):
    z = lax.axis_index("gx"); g = lax.axis_index("gy")
    core = {"gx": z, "gy": g + 1 - 2 * (g % 2)}
    xn = {"gx": z, "gy": g + 2 - 4 * ((g // 2) % 2)}
    yn = {"gx": z, "gy": g + 4 - 8 * ((g // 4) % 2)}
    gx_ = g + 2 - 4 * ((g // 2) % 2)
    gy_ = g + 4 - 8 * ((g // 4) % 2)
    gd_ = gx_ + gy_ - g
    gc = lambda v: v + 1 - 2 * (v % 2)
    zup = {"gx": z + 1, "gy": g}; zdn = {"gx": z - 1, "gy": g}
    zb = z if n_z > 1 else 0
    partners = [(z >= 0, core), (z >= 0, xn), (z >= 0, yn)]
    if n_z > 1:
        partners += [(z < n_z - 1, zup), (z > 0, zdn)]
    barrier_with(partners)
    sends = []
    def send(ok, src, b, h, dev):
        k = len(sends)
        def make():
            return pltpu.make_async_remote_copy(
                src_ref=src, dst_ref=out_ref.at[b, h], send_sem=send_sem.at[k], recv_sem=recv_sem.at[b, h],
                device_id=dev, device_id_type=pl.DeviceIdType.MESH)
        sends.append((ok, make))
        if ok is True:
            make().start()
        else:
            @pl.when(ok)
            def _(): make().start()
    def arrive(ok, b, h):
        def go():
            pltpu.make_async_remote_copy(
                src_ref=out_ref.at[b, h], dst_ref=out_ref.at[b, h], send_sem=send_sem.at[0], recv_sem=recv_sem.at[b, h],
                device_id=core, device_id_type=pl.DeviceIdType.MESH).wait_recv()
        if ok is True:
            go()
        else:
            @pl.when(ok)
            def _(): go()
    own_b = zb * span + g
    local = pltpu.make_async_copy(own_ref, out_ref.at[own_b], local_sem)
    local.start()
    items = [(True, zb, 0)]
    for d in range(1, n_z):
        items += [(z >= d, z - d, -d), (z < n_z - d, z + d, d)]
    def and_(a, b):
        if a is True: return b
        if b is True: return a
        return jnp.logical_and(a, b)
    def first(it):
        ok, zs, d = it
        b = zs * span + g
        src = (lambda h: own_ref.at[h]) if d == 0 else (lambda h: out_ref.at[b, h])
        if d != 0:
            arrive(ok, b, 0); arrive(ok, b, 1)
        if n_z > 1:
            if d <= 0:
                for h in range(2): send(and_(ok, z < n_z - 1), src(h), b, h, zup)
            if d >= 0:
                for h in range(2): send(and_(ok, z > 0), src(h), b, h, zdn)
        send(ok, src(0), b, 0, xn)
        send(ok, src(1), b, 1, yn)
        send(ok, src(1), b, 1, xn)
        send(ok, src(0), b, 0, yn)
        send(ok, src(0), b, 0, core)
        send(ok, src(1), b, 1, core)
    def second(it):
        ok, zs, d = it
        b = zs * span + gx_
        arrive(ok, b, 0)
        send(ok, out_ref.at[b, 0], b, 0, yn)
        send(ok, out_ref.at[b, 0], b, 0, core)
        b = zs * span + gy_
        arrive(ok, b, 1)
        send(ok, out_ref.at[b, 1], b, 1, xn)
        send(ok, out_ref.at[b, 1], b, 1, core)
    def third(it):
        ok, zs, d = it
        for b, h in ((zs * span + gd_, 0), (zs * span + gd_, 1), (zs * span + gy_, 0), (zs * span + gx_, 1)):
            arrive(ok, b, h)
            send(ok, out_ref.at[b, h], b, h, core)
    n = len(items)
    for i in range(n + 2):
        if i < n: first(items[i])
        if 1 <= i <= n: second(items[i - 1])
        if i >= 2: third(items[i - 2])
    for ok, zs, d in items:
        for gg in (g, gx_, gy_, gd_):
            for h in range(2): arrive(ok, zs * span + gc(gg), h)
    local.wait()
    for ok, make in sends:
        if ok is True: make().wait_send()
        else:
            @pl.when(ok)
            def _(): make().wait_send()

def all_gather(block, both, collective_id):
    n_z = lax.axis_size("gx") if both else 1
    span = lax.axis_size("gy")
    rows, cols = block.shape
    own = block.reshape(2, rows // 2, cols)
    n_sends = (2 * n_z - 1) * 24
    out = pl.pallas_call(
        partial(gather_kernel, n_z, span),
        out_shape=jax.ShapeDtypeStruct((n_z * span, 2, rows // 2, cols), block.dtype),
        in_specs=[pl.BlockSpec(memory_space=pltpu.VMEM)],
        out_specs=pl.BlockSpec(memory_space=pl.ANY),
        scratch_shapes=[pltpu.SemaphoreType.DMA((n_sends,)), pltpu.SemaphoreType.DMA((n_z * span, 2)), pltpu.SemaphoreType.DMA],
        compiler_params=pltpu.CompilerParams(collective_id=collective_id, has_side_effects=True),
        name="gather_all" if both else "gather_plane",
    )(own)
    return out.reshape(n_z * span * rows, cols)


def add_into(dst, parts, rows):
    step = min(rows, 32)

    @pl.loop(0, rows // step)
    def _(r):
        at = pl.ds(pl.multiple_of(r * step, step), step)
        if len(parts) == 2 and dst.dtype == jnp.bfloat16:
            dst[at, :] = parts[0][at, :] + parts[1][at, :]
        else:
            total = parts[0][at, :].astype(jnp.float32)
            for term in parts[1:]:
                total = total + term[at, :].astype(jnp.float32)
            dst[at, :] = total.astype(dst.dtype)


def scatter_kernel(chain, n_i, rows, part_ref, out_ref, held, from_core, from_a, from_b, from_z,
                   load_sem, core_send, a_send, b_send, z_send, core_recv, a_recv, b_recv, z_recv):
    z = lax.axis_index("gx"); g = lax.axis_index("gy")
    flip_x = g + 2 - 4 * ((g // 2) % 2)
    flip_y = g + 4 - 8 * ((g // 4) % 2)
    flip_c = lambda v: v + 1 - 2 * (v % 2)
    quads = (flip_x + flip_y - g, flip_x, flip_y, g)
    core = {"gx": z, "gy": flip_c(g)}
    xn = {"gx": z, "gy": flip_x}
    yn = {"gx": z, "gy": flip_y}
    every = z >= 0
    partners = [(every, core), (every, xn), (every, yn)]
    if chain:
        partners += [(every, {"gx": lax.rem(z + j, n_i), "gy": g}) for j in range(1, n_i)]
    barrier_with(partners)
    mesh_id = pl.DeviceIdType.MESH

    def item(i):
        return lax.rem(z + n_i - 1 - i + n_i, n_i) if chain else i

    def block(it, gg):
        return part_ref.at[it, gg]

    def remote(src, dst, ssem, rsem, dev):
        return pltpu.make_async_remote_copy(src_ref=src, dst_ref=dst, send_sem=ssem, recv_sem=rsem, device_id=dev, device_id_type=mesh_id)

    def core_copy(i, q):
        it = item(i)
        return remote(block(it, flip_c(quads[q])), from_core.at[it, q], core_send.at[i, q], core_recv.at[it, q], core)

    def load(i, q):
        it = item(i)
        return pltpu.make_async_copy(block(it, quads[q]), held.at[it, q], load_sem.at[i, q])

    a_plan = ((0, 0, 0, xn), (0, 1, 0, yn), (1, 0, 1, xn), (2, 1, 1, yn))
    def a_copy(i, k):
        it = item(i)
        q, h, slot, dev = a_plan[k]
        return remote(held.at[it, q, h], from_a.at[it, h, slot], a_send.at[i, k], a_recv.at[it, h, slot], dev)

    b_plan = ((2, 0, yn), (1, 1, xn))
    def b_copy(i, h):
        it = item(i)
        q, _, dev = b_plan[h]
        return remote(held.at[it, q, h], from_b.at[it, h], b_send.at[i, h], b_recv.at[it, h], dev)

    def z_copy(i):
        it = item(i)
        return remote(held.at[it, 3], from_z.at[z], z_send.at[i], z_recv.at[z], {"gx": it, "gy": g})

    def z_arrival(i):
        it = item(i)
        return remote(held.at[it, 3], from_z.at[it], z_send.at[i], z_recv.at[it], core)

    for i in range(n_i):
        for q in range(4):
            core_copy(i, q).start()
            load(i, q).start()

    def stage_a(i):
        it = item(i)
        for q in range(4):
            load(i, q).wait()
            core_copy(i, q).wait_recv()
            for h in range(2):
                add_into(held.at[it, q, h], (held.at[it, q, h], from_core.at[it, q, h]), rows)
            for k in range(4):
                if a_plan[k][0] == q:
                    a_copy(i, k).start()

    def stage_b(i):
        it = item(i)
        for q, h, slot in ((2, 0, 0), (1, 1, 0), (3, 0, 1), (3, 1, 1)):
            remote(held.at[it, q, h], from_a.at[it, h, slot], a_send.at[i, 0], a_recv.at[it, h, slot], core).wait_recv()
            add_into(held.at[it, q, h], (held.at[it, q, h], from_a.at[it, h, slot]), rows)
            if slot == 0:
                b_copy(i, h).start()

    def stage_c(i):
        it = item(i)
        for h in range(2):
            b_copy(i, h).wait_recv()
            if chain:
                add_into(held.at[it, 3, h], (held.at[it, 3, h], from_b.at[it, h]), rows)
            else:
                add_into(out_ref.at[it, h], (held.at[it, 3, h], from_b.at[it, h]), rows)

    def stage_d(i):
        if i < n_i - 1:
            z_copy(i).start()
        else:
            for j in range(n_i - 1):
                z_arrival(j).wait_recv()
            for h in range(2):
                add_into(
                    out_ref.at[h],
                    [held.at[item(i), 3, h]] + [from_z.at[item(j), h] for j in range(n_i - 1)],
                    rows,
                )

    for i in range(n_i + 2):
        if i < n_i: stage_a(i)
        if 0 <= i - 1 < n_i: stage_b(i - 1)
        if 0 <= i - 2 < n_i: stage_c(i - 2)
        if chain and 0 <= i - 2 < n_i: stage_d(i - 2)
    for i in range(n_i):
        for q in range(4): core_copy(i, q).wait_send()
        for k in range(4): a_copy(i, k).wait_send()
        for h in range(2): b_copy(i, h).wait_send()
        if chain and i < n_i - 1: z_copy(i).wait_send()


def reduce_scatter(part, both, collective_id, pieces=4, out_dtype=jnp.float32):
    n_z = lax.axis_size("gx") if both else 1
    span = lax.axis_size("gy")
    total, cols = part.shape
    n_i = n_z if both else pieces
    if both:
        rows = total // (n_z * span) // 2
        shaped = part.reshape(n_z, span, 2, rows, cols)
        out_shape = (2, rows, cols)
    else:
        rows = total // span // (2 * pieces)
        shaped = part.reshape(span, pieces, 2, rows, cols).swapaxes(0, 1)
        out_shape = (pieces, 2, rows, cols)
    dma = pltpu.SemaphoreType.DMA
    half = (rows, cols)
    z_items = n_i if both else 1
    z_half = half if both else (16, 128)
    out = pl.pallas_call(
        partial(scatter_kernel, both, n_i, rows),
        out_shape=jax.ShapeDtypeStruct(out_shape, out_dtype),
        in_specs=[pl.BlockSpec(memory_space=pl.ANY)],
        out_specs=pl.BlockSpec(memory_space=pltpu.VMEM),
        scratch_shapes=[
            pltpu.VMEM((n_i, 4, 2) + half, jnp.bfloat16),
            pltpu.VMEM((n_i, 4, 2) + half, jnp.bfloat16),
            pltpu.VMEM((n_i, 2, 2) + half, jnp.bfloat16),
            pltpu.VMEM((n_i, 2) + half, jnp.bfloat16),
            pltpu.VMEM((z_items, 2) + z_half, jnp.bfloat16),
            dma((n_i, 4)), dma((n_i, 4)), dma((n_i, 4)), dma((n_i, 2)), dma((n_i,)),
            dma((n_i, 4)), dma((n_i, 2, 2)), dma((n_i, 2)), dma((n_i,)),
        ],
        compiler_params=pltpu.CompilerParams(collective_id=collective_id, has_side_effects=True, vmem_limit_bytes=60 << 20),
        name="scatter_all" if both else "scatter_plane",
    )(shaped)
    return out.reshape(total // (n_z * span), cols)


def gather_plane(block, collective_id):
    if lax.axis_size("gy") == 8:
        return all_gather(block, False, collective_id)
    return lax.all_gather(block, "gy", axis=0, tiled=True)


def scatter_plane(part, collective_id):
    if lax.axis_size("gy") == 8:
        return reduce_scatter(part, False, collective_id)
    return lax.psum_scatter(part, "gy", scatter_dimension=0, tiled=True).astype(jnp.float32)


def norm_rows(values, gain_row):
    return (
        values * lax.rsqrt(jnp.mean(values * values, axis=-1, keepdims=True) + EPSILON) * gain_row
    )


def rotary(values):
    length = values.shape[0]
    halfway = values.shape[-1] // 2
    positions = jnp.arange(length, dtype=jnp.float32)
    frequency = jnp.exp(
        jnp.arange(halfway, dtype=jnp.float32) * (-2.0 * jnp.log(10000.0) / values.shape[-1])
    )
    angles = (positions[:, None] * frequency[None, :])[:, None, :]
    cosine = jnp.cos(angles)
    sine_table = jnp.sin(angles)
    first_half = values[..., :halfway]
    second = values[..., halfway:]
    return jnp.concatenate(
        [first_half * cosine - second * sine_table, second * cosine + first_half * sine_table],
        axis=-1,
    )


def prepare_heads(raw_heads, gain_row):
    return rotary(norm_rows(raw_heads, gain_row))


def route_gates(id_table, logits):
    shares = jax.nn.softmax(logits, axis=-1)
    experts = logits.shape[-1]
    matches = id_table[:, :, None] == jnp.arange(experts, dtype=jnp.int32)[None, None, :]
    chosen = jnp.sum(jnp.where(matches, shares[:, None, :], 0.0), axis=-1)
    return chosen / jnp.sum(chosen, axis=-1, keepdims=True)


def dense_gates(all_ids, logits, expert):
    shares = jax.nn.softmax(logits, axis=-1)
    columns = jnp.arange(logits.shape[-1], dtype=jnp.int32)
    routed = jnp.any(all_ids[:, :, None] == columns[None, None, :], axis=1)
    chosen = jnp.where(routed, shares, 0.0)
    own = jnp.sum(jnp.where(columns[None, :] == expert, chosen, 0.0), axis=-1)
    return own / jnp.sum(chosen, axis=-1)


def contract_rows(left_side, right_side):
    return lax.dot_general(
        left_side, right_side, (((0,), (0,)), ((), ())), preferred_element_type=jnp.float32
    )


def contract_cols(left_side, right_side):
    return lax.dot_general(
        left_side, right_side, (((1,), (1,)), ((), ())), preferred_element_type=jnp.float32
    )


def routed_experts(
    moe_in, cotangent, expert_ids, gate_share, router_weight, gate_weight, up_weight, down_weight
):
    tok_rows = moe_in.shape[0]
    experts = router_weight.shape[1]
    width_all = moe_in.shape[1]
    capacity = tok_rows * TOP * 3 // (2 * experts)
    route_count = tok_rows * TOP
    flat_ids = expert_ids.reshape(route_count)
    onehot = (flat_ids[:, None] == jnp.arange(experts, dtype=jnp.int32)[None, :]).astype(jnp.int32)
    earlier = jnp.cumsum(onehot, axis=0) - onehot
    slot_index = jnp.sum(earlier * onehot, axis=1)
    target = flat_ids * capacity + slot_index
    source = (
        jnp.full((experts * capacity,), tok_rows, jnp.int32)
        .at[target]
        .set(jnp.arange(route_count, dtype=jnp.int32) // TOP)
    )
    padded_in = jnp.concatenate([moe_in, jnp.zeros((1, width_all), jnp.bfloat16)], axis=0)
    packed = padded_in[source].reshape(experts, 1, capacity, width_all)
    outgoing = jnp.broadcast_to(packed, (experts, 2, capacity, width_all)).reshape(
        2 * experts, capacity, width_all
    )
    arrived = lax.all_to_all(outgoing, ("gx", "gy"), split_axis=0, concat_axis=1, tiled=True)[0]
    gate_in = gate_weight[0]
    up_in = up_weight[0]
    down_in = down_weight[0]
    gate_val = jnp.dot(arrived, gate_in, preferred_element_type=jnp.float32)
    up_val = jnp.dot(arrived, up_in, preferred_element_type=jnp.float32)
    hidden = (jax.nn.silu(gate_val) * up_val).astype(jnp.bfloat16)
    produced = jnp.dot(hidden, down_in, preferred_element_type=jnp.float32).astype(jnp.bfloat16)
    returned = lax.all_to_all(produced[None], ("gx", "gy"), split_axis=1, concat_axis=0, tiled=True)
    summed = (
        returned.reshape(experts, 2, capacity, width_all)
        .astype(jnp.float32)
        .sum(axis=1)
        .reshape(experts * capacity, width_all)
    )
    route_out = summed[target]
    gates_flat = gate_share.reshape(route_count)
    moe_out = jnp.sum((gates_flat[:, None] * route_out).reshape(tok_rows, TOP, width_all), axis=1)
    grad_out = cotangent.astype(jnp.float32)
    grad_gates = jnp.sum(
        route_out.reshape(tok_rows, TOP, width_all) * grad_out[:, None, :], axis=-1
    )
    slot_gate = jnp.zeros((experts * capacity,), jnp.float32).at[target].set(gates_flat)
    padded_grad = jnp.concatenate([grad_out, jnp.zeros((1, width_all), jnp.float32)], axis=0)
    grad_packed = (
        (slot_gate[:, None] * padded_grad[source])
        .astype(jnp.bfloat16)
        .reshape(experts, 1, capacity, width_all)
    )
    grad_outgoing = jnp.broadcast_to(grad_packed, (experts, 2, capacity, width_all)).reshape(
        2 * experts, capacity, width_all
    )
    grad_arrived = lax.all_to_all(
        grad_outgoing, ("gx", "gy"), split_axis=0, concat_axis=1, tiled=True
    )[0]
    rows_in, grad_use = (arrived, grad_arrived)
    gate_use, up_use, hidden_use = (gate_val, up_val, hidden)
    sigmoid_gate = jax.nn.sigmoid(gate_use)
    silu_gate = gate_use * sigmoid_gate
    grad_hidden = contract_cols(grad_use, down_in)
    down_part = contract_rows(hidden_use, grad_use)
    grad_gate = (
        grad_hidden * up_use * sigmoid_gate * (1.0 + gate_use * (1.0 - sigmoid_gate))
    ).astype(jnp.bfloat16)
    grad_up = (grad_hidden * silu_gate).astype(jnp.bfloat16)
    gate_part = contract_rows(rows_in, grad_gate)
    up_part = contract_rows(rows_in, grad_up)
    grad_in = contract_cols(grad_gate, gate_in) + contract_cols(grad_up, up_in)
    grad_back = lax.all_to_all(
        grad_in.astype(jnp.bfloat16)[None], ("gx", "gy"), split_axis=1, concat_axis=0, tiled=True
    )
    grad_summed = (
        grad_back.reshape(experts, 2, capacity, width_all)
        .astype(jnp.float32)
        .sum(axis=1)
        .reshape(experts * capacity, width_all)
    )
    grad_moe_in = jnp.sum(grad_summed[target].reshape(tok_rows, TOP, width_all), axis=1)
    return moe_out, grad_gates, grad_moe_in, gate_part, up_part, down_part


def dense_experts(
    moe_in, cotangent, expert_ids, gate_share, router_weight, gate_weight, up_weight, down_weight
):
    experts = router_weight.shape[1]
    everyone = ("gx", "gy")
    all_ids = lax.all_gather(expert_ids, everyone, axis=0, tiled=True)
    all_cot = lax.all_gather(cotangent, everyone, axis=0, tiled=True)
    all_moe = all_gather(moe_in, True, 2)
    rank = lax.axis_index("gx") * lax.axis_size("gy") + lax.axis_index("gy")
    own_gate = dense_gates(
        all_ids, jnp.dot(all_moe, router_weight, preferred_element_type=jnp.float32), rank // 2
    )
    gate_in = gate_weight[0]
    up_in = up_weight[0]
    down_in = down_weight[0]
    gate_val = jnp.dot(all_moe, gate_in, preferred_element_type=jnp.float32)
    up_val = jnp.dot(all_moe, up_in, preferred_element_type=jnp.float32)
    sigmoid_gate = jax.nn.sigmoid(gate_val)
    silu_gate = gate_val * sigmoid_gate
    hidden = (silu_gate * up_val).astype(jnp.bfloat16)
    piece = jnp.dot(hidden, down_in, preferred_element_type=jnp.float32)
    cot_float = all_cot.astype(jnp.float32)
    gate_dots = jnp.sum(piece * cot_float, axis=-1)
    devices = lax.axis_size("gx") * lax.axis_size("gy")
    dots_back = lax.all_to_all(
        gate_dots.reshape(devices, -1), everyone, split_axis=0, concat_axis=0, tiled=True
    )
    dots_experts = dots_back.reshape(experts, 2, -1).sum(axis=1).T
    matches = expert_ids[:, :, None] == jnp.arange(experts, dtype=jnp.int32)[None, None, :]
    grad_gates = jnp.sum(jnp.where(matches, dots_experts[:, None, :], 0.0), axis=-1)
    moe_out = reduce_scatter((piece * own_gate[:, None]).astype(jnp.bfloat16), True, 4)
    grad_use = (cot_float * own_gate[:, None]).astype(jnp.bfloat16)
    grad_hidden = contract_cols(grad_use, down_in)
    down_part = contract_rows(hidden, grad_use)
    grad_gate = (
        grad_hidden * up_val * sigmoid_gate * (1.0 + gate_val * (1.0 - sigmoid_gate))
    ).astype(jnp.bfloat16)
    grad_up = (grad_hidden * silu_gate).astype(jnp.bfloat16)
    gate_part = contract_rows(all_moe, grad_gate)
    up_part = contract_rows(all_moe, grad_up)
    grad_in = contract_cols(grad_gate, gate_in) + contract_cols(grad_up, up_in)
    grad_moe_in = reduce_scatter(grad_in.astype(jnp.bfloat16), True, 4)
    return moe_out, grad_gates, grad_moe_in, gate_part, up_part, down_part


def local(
    tokens,
    cotangent,
    expert_ids,
    doc_ids,
    clip_rank,
    attn_gain,
    moe_gain,
    query_gain,
    key_gain,
    query_weight,
    key_weight,
    value_weight,
    out_weight,
    router_weight,
    gate_weight,
    up_weight,
    down_weight,
):
    inputs = tokens.astype(jnp.float32)
    acts_float, norm_pull = jax.vjp(norm_rows, inputs, attn_gain)
    acts_low = acts_float.astype(jnp.bfloat16)
    seq_acts = gather_plane(acts_low, 1)
    in_weights = jnp.concatenate([query_weight, key_weight, value_weight], axis=1)
    full_in = lax.all_gather(in_weights, "gx", axis=0, tiled=True)
    out_rows = lax.all_gather(out_weight, "gx", axis=1, tiled=True)
    length = seq_acts.shape[0]
    local_width = query_weight.shape[1]
    local_heads = local_width // HD
    projected = jnp.dot(seq_acts, full_in, preferred_element_type=jnp.float32)
    queries = projected[:, :local_width]
    key_raw = projected[:, local_width : 2 * local_width]
    value_ready = (
        projected[:, 2 * local_width :].astype(jnp.bfloat16).reshape(length, local_heads, HD)
    )
    query_float, query_pull = jax.vjp(
        prepare_heads, queries.reshape(length, local_heads, HD), query_gain
    )
    key_float, key_pull = jax.vjp(prepare_heads, key_raw.reshape(length, local_heads, HD), key_gain)
    query_ready = query_float.astype(jnp.bfloat16)
    key_ready = key_float.astype(jnp.bfloat16)
    block_rows = min(512, length)
    block_count = length // block_rows
    score_scale = HD ** (-0.5)
    query_blocks = query_ready.reshape(block_count, block_rows, local_heads, HD)
    doc_blocks = doc_ids.reshape(block_count, block_rows)

    def block_scores(query_block, doc_block):
        scores = (
            jnp.einsum("qhd,khd->hqk", query_block, key_ready, preferred_element_type=jnp.float32)
            * score_scale
        )
        same_doc = doc_block[:, None] == doc_ids[None, :]
        return jnp.where(same_doc[None], scores, NEGATIVE)

    def forward_block(pieces):
        scores = block_scores(pieces[0], pieces[1])
        highest = jnp.max(scores, axis=-1, keepdims=True)
        weights = jnp.exp(scores - highest)
        totals = jnp.sum(weights, axis=-1, keepdims=True)
        shares = (weights / totals).astype(jnp.bfloat16)
        mixed_heads = jnp.einsum(
            "hqk,khd->qhd", shares, value_ready, preferred_element_type=jnp.float32
        )
        return (
            mixed_heads.astype(jnp.bfloat16),
            highest[..., 0] + jnp.log(totals[..., 0]),
            jnp.max(highest[..., 0], axis=-1),
        )

    mixed_blocks, log_totals, peak_blocks = lax.map(forward_block, (query_blocks, doc_blocks))
    mixed_seq = mixed_blocks.reshape(length, local_width)
    start_head = lax.axis_index("gy") * local_heads
    peak_local = lax.dynamic_update_slice(
        jnp.full((NH,), NEGATIVE, jnp.float32), jnp.max(peak_blocks, axis=0), (start_head,)
    )
    peak_global = lax.pmax(peak_local, ("gx", "gy"))
    attended = scatter_plane(
        jnp.dot(mixed_seq, out_rows, preferred_element_type=jnp.float32).astype(jnp.bfloat16), 3
    )
    residual = inputs + attended
    moe_float, moe_pull = jax.vjp(norm_rows, residual, moe_gain)
    moe_in = moe_float.astype(jnp.bfloat16)
    logits = jnp.dot(moe_in, router_weight, preferred_element_type=jnp.float32)
    gate_share, gate_pull = jax.vjp(partial(route_gates, expert_ids), logits)
    experts_pass = dense_experts if lax.axis_size("gy") == 8 and router_weight.shape[1] <= 2 * TOP else routed_experts
    moe_out, grad_gates, grad_moe_in, gate_part, up_part, down_part = experts_pass(
        moe_in,
        cotangent,
        expert_ids,
        gate_share,
        router_weight,
        gate_weight,
        up_weight,
        down_weight,
    )
    output = (residual + moe_out).astype(jnp.bfloat16)
    grad_out = cotangent.astype(jnp.float32)
    (grad_logits,) = gate_pull(grad_gates)
    grad_logits_low = grad_logits.astype(jnp.bfloat16)
    router_part = contract_rows(moe_in, grad_logits_low)
    grad_moe_in = grad_moe_in + contract_cols(grad_logits_low, router_weight)
    grad_resid_norm, moe_gain_part = moe_pull(grad_moe_in)
    grad_resid = grad_out + grad_resid_norm
    seq_grad = gather_plane(grad_resid.astype(jnp.bfloat16), 1)
    grad_mixed = contract_cols(seq_grad, out_rows).astype(jnp.bfloat16)
    out_part = contract_rows(seq_grad, mixed_seq)

    def backward_block(running, pieces):
        grad_key, grad_value = running
        query_block, grad_block, log_block, doc_block = pieces
        scores = block_scores(query_block, doc_block)
        weights = jnp.exp(scores - log_block[..., None])
        grad_value = grad_value + jnp.einsum(
            "hqk,qhd->khd",
            weights.astype(jnp.bfloat16),
            grad_block,
            preferred_element_type=jnp.float32,
        )
        grad_weights = jnp.einsum(
            "qhd,khd->hqk", grad_block, value_ready, preferred_element_type=jnp.float32
        )
        inner_sum = jnp.sum(weights * grad_weights, axis=-1, keepdims=True)
        grad_scores = (weights * (grad_weights - inner_sum)).astype(jnp.bfloat16)
        grad_query = (
            jnp.einsum("hqk,khd->qhd", grad_scores, key_ready, preferred_element_type=jnp.float32)
            * score_scale
        )
        grad_key = (
            grad_key
            + jnp.einsum(
                "hqk,qhd->khd", grad_scores, query_block, preferred_element_type=jnp.float32
            )
            * score_scale
        )
        return ((grad_key, grad_value), grad_query)

    empty_heads = jnp.zeros((length, local_heads, HD), jnp.float32)
    grad_mixed_blocks = grad_mixed.reshape(block_count, block_rows, local_heads, HD)
    (key_grad_heads, value_grad_heads), query_grad_blocks = lax.scan(
        backward_block,
        (empty_heads, empty_heads),
        (query_blocks, grad_mixed_blocks, log_totals, doc_blocks),
    )
    query_raw_grad, query_gain_part = query_pull(query_grad_blocks.reshape(length, local_heads, HD))
    key_raw_grad, key_gain_part = key_pull(key_grad_heads)
    grad_queries = query_raw_grad.reshape(length, local_width).astype(jnp.bfloat16)
    grad_keys = key_raw_grad.reshape(length, local_width).astype(jnp.bfloat16)
    grad_values = value_grad_heads.reshape(length, local_width).astype(jnp.bfloat16)
    grad_heads = jnp.concatenate([grad_queries, grad_keys, grad_values], axis=1)
    in_sum = lax.psum_scatter(
        contract_rows(seq_acts, grad_heads).astype(jnp.bfloat16),
        "gx",
        scatter_dimension=0,
        tiled=True,
    ).astype(jnp.float32)
    query_sum = in_sum[:, :local_width]
    key_sum = in_sum[:, local_width : 2 * local_width]
    value_sum = in_sum[:, 2 * local_width :]
    out_sum_rows = lax.psum_scatter(
        out_part.astype(jnp.bfloat16), "gx", scatter_dimension=0, tiled=True
    ).astype(jnp.float32)
    grad_acts = scatter_plane(contract_cols(grad_heads, full_in).astype(jnp.bfloat16), 3)
    norm_input_grad, attn_gain_part = norm_pull(grad_acts)
    input_grad = grad_resid + norm_input_grad
    attn_gain_grad, moe_gain_grad, query_gain_grad, key_gain_grad, router_grad = lax.psum(
        (attn_gain_part, moe_gain_part, query_gain_part, key_gain_part, router_part), ("gx", "gy")
    )
    ranked = -jnp.sort(-peak_global)
    limit = jnp.sum(jnp.where(jnp.arange(NH, dtype=jnp.int32) == clip_rank[0], ranked, 0.0))
    factors = jnp.where(peak_global > limit, limit / peak_global, 1.0)
    own_factors = lax.dynamic_slice_in_dim(factors, start_head, local_heads)
    columns = jnp.repeat(jnp.sqrt(own_factors), HD)
    query_clipped = (query_weight.astype(jnp.float32) * columns[None, :]).astype(jnp.bfloat16)
    key_clipped = (key_weight.astype(jnp.float32) * columns[None, :]).astype(jnp.bfloat16)
    return (
        output,
        input_grad,
        attn_gain_grad,
        moe_gain_grad,
        query_gain_grad,
        key_gain_grad,
        query_sum,
        key_sum,
        value_sum,
        out_sum_rows.T,
        router_grad,
        gate_part[None],
        up_part[None],
        down_part[None],
        query_clipped,
        key_clipped,
        factors,
    )


def solution(mesh):
    placed = (
        P(("gx", "gy"), None),
        P(("gx", "gy"), None),
        P(("gx", "gy"), None),
        P("gx"),
        P(),
        P(),
        P(),
        P(),
        P(),
        P("gx", "gy"),
        P("gx", "gy"),
        P("gx", "gy"),
        P("gy", "gx"),
        P(),
        P(("gx", "gy"), None, None),
        P(("gx", "gy"), None, None),
        P(("gx", "gy"), None, None),
    )
    return jax.shard_map(
        local,
        mesh=mesh,
        in_specs=placed,
        out_specs=(
            P(("gx", "gy"), None),
            P(("gx", "gy"), None),
            P(),
            P(),
            P(),
            P(),
            P("gx", "gy"),
            P("gx", "gy"),
            P("gx", "gy"),
            P("gy", "gx"),
            P(),
            P(("gx", "gy"), None, None),
            P(("gx", "gy"), None, None),
            P(("gx", "gy"), None, None),
            P("gx", "gy"),
            P("gx", "gy"),
            P(),
        ),
        check_vma=False,
    )
```

```python
from functools import partial
from itertools import accumulate

import jax
import jax.numpy as jnp
from jax import lax
from jax.experimental import pallas as pl
from jax.experimental.pallas import tpu as pltpu
from jax.sharding import PartitionSpec as P

NH = 16
HD = 128
TOP = 8


EPSILON = 1e-06
NEGATIVE = -1e30


def barrier_with(partners):
    barrier = pltpu.get_barrier_semaphore()
    for ok, device in partners:
        @pl.when(ok)
        def _():
            pl.semaphore_signal(barrier, inc=1, device_id=device, device_id_type=pl.DeviceIdType.MESH)
    pl.semaphore_wait(barrier, sum(ok.astype(jnp.int32) for ok, _ in partners))

def always(ok, other):
    if ok is True:
        return other
    return ok if other is True else jnp.logical_and(ok, other)


def run_if(ok, action):
    if ok is True:
        action()
    else:
        pl.when(ok)(action)


def chain_gather(n_z, own_ref, out_ref, send_sem, recv_sem, local_sem):
    z = lax.axis_index("gx")
    g = lax.axis_index("gy")

    def hop(source, owner, k, peer):
        return pltpu.make_async_remote_copy(
            src_ref=source,
            dst_ref=out_ref.at[owner],
            send_sem=send_sem.at[k],
            recv_sem=recv_sem.at[owner],
            device_id={"gx": peer, "gy": g},
            device_id_type=pl.DeviceIdType.MESH,
        )

    local = pltpu.make_async_copy(own_ref, out_ref.at[z], local_sem)
    upward = [(z < n_z - 1, lambda: hop(own_ref, z, 0, z + 1))]
    downward = [(z > 0, lambda: hop(own_ref, z, n_z, z - 1))]
    for d in range(1, n_z - 1):
        upward.append(
            (
                jnp.logical_and(z >= d, z < n_z - 1),
                lambda d=d: hop(out_ref.at[z - d], z - d, d, z + 1),
            )
        )
        downward.append(
            (
                jnp.logical_and(z < n_z - d, z > 0),
                lambda d=d: hop(out_ref.at[z + d], z + d, n_z + d, z - 1),
            )
        )

    def start():
        local.start()
        for ok, copy in (upward[0], downward[0]):
            run_if(ok, lambda copy=copy: copy().start())

    def relay(d):
        run_if(z >= d, lambda: hop(own_ref, z - d, 0, z).wait_recv())
        if d < n_z - 1:
            run_if(upward[d][0], lambda: upward[d][1]().start())
        run_if(z < n_z - d, lambda: hop(own_ref, z + d, 0, z).wait_recv())
        if d < n_z - 1:
            run_if(downward[d][0], lambda: downward[d][1]().start())

    def finish():
        local.wait()
        for ok, copy in upward + downward:
            run_if(ok, lambda copy=copy: copy().wait_send())

    return start, [partial(relay, d) for d in range(1, n_z)], finish


def gather_kernel(n_z, span, own_ref, out_ref, send_sem, recv_sem, local_sem, chain=None):
    z = lax.axis_index("gx"); g = lax.axis_index("gy")
    core = {"gx": z, "gy": g + 1 - 2 * (g % 2)}
    xn = {"gx": z, "gy": g + 2 - 4 * ((g // 2) % 2)}
    yn = {"gx": z, "gy": g + 4 - 8 * ((g // 4) % 2)}
    gx_ = g + 2 - 4 * ((g // 2) % 2)
    gy_ = g + 4 - 8 * ((g // 4) % 2)
    gd_ = gx_ + gy_ - g
    gc = lambda v: v + 1 - 2 * (v % 2)
    zup = {"gx": z + 1, "gy": g}; zdn = {"gx": z - 1, "gy": g}
    zb = z if n_z > 1 else 0
    partners = [(z >= 0, core), (z >= 0, xn), (z >= 0, yn)]
    n_chain = lax.axis_size("gx") if chain else n_z
    if n_chain > 1:
        partners += [(z < n_chain - 1, zup), (z > 0, zdn)]
    barrier_with(partners)
    if chain:
        chain[0]()
    sends = []
    def send(ok, src, b, h, dev):
        k = len(sends)
        def make():
            return pltpu.make_async_remote_copy(
                src_ref=src, dst_ref=out_ref.at[b, h], send_sem=send_sem.at[k], recv_sem=recv_sem.at[b, h],
                device_id=dev, device_id_type=pl.DeviceIdType.MESH)
        sends.append((ok, make))
        if ok is True:
            make().start()
        else:
            @pl.when(ok)
            def _(): make().start()
    def arrive(ok, b, h):
        def go():
            pltpu.make_async_remote_copy(
                src_ref=out_ref.at[b, h], dst_ref=out_ref.at[b, h], send_sem=send_sem.at[0], recv_sem=recv_sem.at[b, h],
                device_id=core, device_id_type=pl.DeviceIdType.MESH).wait_recv()
        if ok is True:
            go()
        else:
            @pl.when(ok)
            def _(): go()
    own_b = zb * span + g
    local = pltpu.make_async_copy(own_ref, out_ref.at[own_b], local_sem)
    local.start()
    items = [(True, zb, 0)]
    for d in range(1, n_z):
        items += [(z >= d, z - d, -d), (z < n_z - d, z + d, d)]
    def and_(a, b):
        if a is True: return b
        if b is True: return a
        return jnp.logical_and(a, b)
    def first(it):
        ok, zs, d = it
        b = zs * span + g
        src = (lambda h: own_ref.at[h]) if d == 0 else (lambda h: out_ref.at[b, h])
        if d != 0:
            arrive(ok, b, 0); arrive(ok, b, 1)
        if n_z > 1:
            if d <= 0:
                for h in range(2): send(and_(ok, z < n_z - 1), src(h), b, h, zup)
            if d >= 0:
                for h in range(2): send(and_(ok, z > 0), src(h), b, h, zdn)
        send(ok, src(0), b, 0, xn)
        send(ok, src(1), b, 1, yn)
        send(ok, src(1), b, 1, xn)
        send(ok, src(0), b, 0, yn)
        send(ok, src(0), b, 0, core)
        send(ok, src(1), b, 1, core)
    def second(it):
        ok, zs, d = it
        b = zs * span + gx_
        arrive(ok, b, 0)
        send(ok, out_ref.at[b, 0], b, 0, yn)
        send(ok, out_ref.at[b, 0], b, 0, core)
        b = zs * span + gy_
        arrive(ok, b, 1)
        send(ok, out_ref.at[b, 1], b, 1, xn)
        send(ok, out_ref.at[b, 1], b, 1, core)
    def third(it):
        ok, zs, d = it
        for b, h in ((zs * span + gd_, 0), (zs * span + gd_, 1), (zs * span + gy_, 0), (zs * span + gx_, 1)):
            arrive(ok, b, h)
            send(ok, out_ref.at[b, h], b, h, core)
    n = len(items)
    for i in range(n + 2):
        if i < n: first(items[i])
        if 1 <= i <= n: second(items[i - 1])
        if i >= 2: third(items[i - 2])
    if chain:
        chain[1][0]()
    for ok, zs, d in items:
        for gg in (g, gx_, gy_, gd_):
            for h in range(2): arrive(ok, zs * span + gc(gg), h)
    if chain:
        for relay in chain[1][1:]:
            relay()
        chain[2]()
    local.wait()
    for ok, make in sends:
        if ok is True: make().wait_send()
        else:
            @pl.when(ok)
            def _(): make().wait_send()

def all_gather(block, both, collective_id):
    n_z = lax.axis_size("gx") if both else 1
    span = lax.axis_size("gy")
    rows, cols = block.shape
    own = block.reshape(2, rows // 2, cols)
    n_sends = (2 * n_z - 1) * 24
    out = pl.pallas_call(
        partial(gather_kernel, n_z, span),
        out_shape=jax.ShapeDtypeStruct((n_z * span, 2, rows // 2, cols), block.dtype),
        in_specs=[pl.BlockSpec(memory_space=pltpu.VMEM)],
        out_specs=pl.BlockSpec(memory_space=pl.ANY),
        scratch_shapes=[pltpu.SemaphoreType.DMA((n_sends,)), pltpu.SemaphoreType.DMA((n_z * span, 2)), pltpu.SemaphoreType.DMA],
        compiler_params=pltpu.CompilerParams(collective_id=collective_id, has_side_effects=True),
        name="gather_all" if both else "gather_plane",
    )(own)
    return out.reshape(n_z * span * rows, cols)


def add_into(dst, parts, rows):
    step = min(rows, 32)

    @pl.loop(0, rows // step)
    def _(r):
        at = pl.ds(pl.multiple_of(r * step, step), step)
        if len(parts) == 2 and dst.dtype == jnp.bfloat16:
            dst[at, :] = parts[0][at, :] + parts[1][at, :]
        else:
            total = parts[0][at, :].astype(jnp.float32)
            for term in parts[1:]:
                total = total + term[at, :].astype(jnp.float32)
            dst[at, :] = total.astype(dst.dtype)


def scatter_kernel(chain, n_i, rows, part_ref, out_ref, held, from_core, from_a, from_b, from_z,
                   load_sem, core_send, a_send, b_send, z_send, core_recv, a_recv, b_recv, z_recv, beside=None):
    z = lax.axis_index("gx"); g = lax.axis_index("gy")
    flip_x = g + 2 - 4 * ((g // 2) % 2)
    flip_y = g + 4 - 8 * ((g // 4) % 2)
    flip_c = lambda v: v + 1 - 2 * (v % 2)
    quads = (flip_x + flip_y - g, flip_x, flip_y, g)
    core = {"gx": z, "gy": flip_c(g)}
    xn = {"gx": z, "gy": flip_x}
    yn = {"gx": z, "gy": flip_y}
    every = z >= 0
    partners = [(every, core), (every, xn), (every, yn)]
    if chain:
        partners += [(every, {"gx": lax.rem(z + j, n_i), "gy": g}) for j in range(1, n_i)]
    if beside:
        n_z = lax.axis_size("gx")
        partners += [(z < n_z - 1, {"gx": z + 1, "gy": g}), (z > 0, {"gx": z - 1, "gy": g})]
    barrier_with(partners)
    if beside:
        beside[0]()
    mesh_id = pl.DeviceIdType.MESH

    def item(i):
        return lax.rem(z + n_i - 1 - i + n_i, n_i) if chain else i

    def block(it, gg):
        return part_ref.at[it, gg]

    def remote(src, dst, ssem, rsem, dev):
        return pltpu.make_async_remote_copy(src_ref=src, dst_ref=dst, send_sem=ssem, recv_sem=rsem, device_id=dev, device_id_type=mesh_id)

    def core_copy(i, q):
        it = item(i)
        return remote(block(it, flip_c(quads[q])), from_core.at[it, q], core_send.at[i, q], core_recv.at[it, q], core)

    def load(i, q):
        it = item(i)
        return pltpu.make_async_copy(block(it, quads[q]), held.at[it, q], load_sem.at[i, q])

    a_plan = ((0, 0, 0, xn), (0, 1, 0, yn), (1, 0, 1, xn), (2, 1, 1, yn))
    def a_copy(i, k):
        it = item(i)
        q, h, slot, dev = a_plan[k]
        return remote(held.at[it, q, h], from_a.at[it, h, slot], a_send.at[i, k], a_recv.at[it, h, slot], dev)

    b_plan = ((2, 0, yn), (1, 1, xn))
    def b_copy(i, h):
        it = item(i)
        q, _, dev = b_plan[h]
        return remote(held.at[it, q, h], from_b.at[it, h], b_send.at[i, h], b_recv.at[it, h], dev)

    def z_copy(i):
        it = item(i)
        return remote(held.at[it, 3], from_z.at[z], z_send.at[i], z_recv.at[z], {"gx": it, "gy": g})

    def z_arrival(i):
        it = item(i)
        return remote(held.at[it, 3], from_z.at[it], z_send.at[i], z_recv.at[it], core)

    for i in range(n_i):
        for q in range(4):
            core_copy(i, q).start()
            load(i, q).start()

    def stage_a(i):
        it = item(i)
        for q in range(4):
            load(i, q).wait()
            core_copy(i, q).wait_recv()
            for h in range(2):
                add_into(held.at[it, q, h], (held.at[it, q, h], from_core.at[it, q, h]), rows)
            for k in range(4):
                if a_plan[k][0] == q:
                    a_copy(i, k).start()

    def stage_b(i):
        it = item(i)
        for q, h, slot in ((2, 0, 0), (1, 1, 0), (3, 0, 1), (3, 1, 1)):
            remote(held.at[it, q, h], from_a.at[it, h, slot], a_send.at[i, 0], a_recv.at[it, h, slot], core).wait_recv()
            add_into(held.at[it, q, h], (held.at[it, q, h], from_a.at[it, h, slot]), rows)
            if slot == 0:
                b_copy(i, h).start()

    def stage_c(i):
        it = item(i)
        for h in range(2):
            b_copy(i, h).wait_recv()
            if chain:
                add_into(held.at[it, 3, h], (held.at[it, 3, h], from_b.at[it, h]), rows)
            else:
                add_into(out_ref.at[it, h], (held.at[it, 3, h], from_b.at[it, h]), rows)

    def stage_d(i):
        if i < n_i - 1:
            z_copy(i).start()
        else:
            for j in range(n_i - 1):
                z_arrival(j).wait_recv()
            for h in range(2):
                add_into(
                    out_ref.at[h],
                    [held.at[item(i), 3, h]] + [from_z.at[item(j), h] for j in range(n_i - 1)],
                    rows,
                )

    for i in range(n_i + 2):
        if i < n_i: stage_a(i)
        if 0 <= i - 1 < n_i: stage_b(i - 1)
        if 0 <= i - 2 < n_i: stage_c(i - 2)
        if chain and 0 <= i - 2 < n_i: stage_d(i - 2)
        if beside and i == n_i:
            beside[1][0]()
    if beside:
        for relay in beside[1][1:]:
            relay()
        beside[2]()
    for i in range(n_i):
        for q in range(4): core_copy(i, q).wait_send()
        for k in range(4): a_copy(i, k).wait_send()
        for h in range(2): b_copy(i, h).wait_send()
        if chain and i < n_i - 1: z_copy(i).wait_send()


def reduce_scatter(part, both, collective_id, pieces=4, out_dtype=jnp.float32):
    n_z = lax.axis_size("gx") if both else 1
    span = lax.axis_size("gy")
    total, cols = part.shape
    n_i = n_z if both else pieces
    if both:
        rows = total // (n_z * span) // 2
        shaped = part.reshape(n_z, span, 2, rows, cols)
        out_shape = (2, rows, cols)
    else:
        rows = total // span // (2 * pieces)
        shaped = part.reshape(span, pieces, 2, rows, cols).swapaxes(0, 1)
        out_shape = (pieces, 2, rows, cols)
    dma = pltpu.SemaphoreType.DMA
    half = (rows, cols)
    z_items = n_i if both else 1
    z_half = half if both else (16, 128)
    out = pl.pallas_call(
        partial(scatter_kernel, both, n_i, rows),
        out_shape=jax.ShapeDtypeStruct(out_shape, out_dtype),
        in_specs=[pl.BlockSpec(memory_space=pl.ANY)],
        out_specs=pl.BlockSpec(memory_space=pltpu.VMEM),
        scratch_shapes=[
            pltpu.VMEM((n_i, 4, 2) + half, jnp.bfloat16),
            pltpu.VMEM((n_i, 4, 2) + half, jnp.bfloat16),
            pltpu.VMEM((n_i, 2, 2) + half, jnp.bfloat16),
            pltpu.VMEM((n_i, 2) + half, jnp.bfloat16),
            pltpu.VMEM((z_items, 2) + z_half, jnp.bfloat16),
            dma((n_i, 4)), dma((n_i, 4)), dma((n_i, 4)), dma((n_i, 2)), dma((n_i,)),
            dma((n_i, 4)), dma((n_i, 2, 2)), dma((n_i, 2)), dma((n_i,)),
        ],
        compiler_params=pltpu.CompilerParams(collective_id=collective_id, has_side_effects=True, vmem_limit_bytes=60 << 20),
        name="scatter_all" if both else "scatter_plane",
    )(shaped)
    return out.reshape(total // (n_z * span), cols)


def sum_kernel(n_z, bits, vec_ref, out_ref, held, arrived, from_z, send_sem, z_send, recv_sem, z_recv):
    z = lax.axis_index("gx")
    g = lax.axis_index("gy")
    half = vec_ref.shape[1]
    side = lax.rem(g, 2)
    core = {"gx": z, "gy": g + 1 - 2 * (g % 2)}
    peers = [
        {"gx": z, "gy": g + bit - 2 * bit * ((g // bit) % 2)}
        for bit in (2**power for power in range(1, bits))
    ]
    others = [{"gx": lax.rem(z + j, n_z), "gy": g} for j in range(1, n_z)]
    barrier_with([(z >= 0, peer) for peer in (core, *peers, *others)])

    def remote(src, dst, ssem, rsem, peer):
        return pltpu.make_async_remote_copy(
            src_ref=src,
            dst_ref=dst,
            send_sem=ssem,
            recv_sem=rsem,
            device_id=peer,
            device_id_type=pl.DeviceIdType.MESH,
        )

    first = remote(vec_ref.at[1 - side], arrived.at[0], send_sem.at[0], recv_sem.at[0], core)
    first.start()
    first.wait()
    held[0] = vec_ref[side] + arrived[0]
    for k, peer in enumerate(peers, 1):
        step = remote(held.at[k - 1], arrived.at[k], send_sem.at[k], recv_sem.at[k], peer)
        step.start()
        step.wait()
        held[k] = held[k - 1] + arrived[k]
    copies = [
        remote(held.at[bits - 1], from_z.at[j], z_send.at[j], z_recv.at[j], peer)
        for j, peer in enumerate(others)
    ]
    for copy in copies:
        copy.start()
    for copy in copies:
        copy.wait()
    total = jnp.zeros_like(held[0])
    for owner in range(n_z):
        term = held[bits - 1]
        for j in range(1, n_z):
            term = jnp.where(lax.rem(z - j + n_z, n_z) == owner, from_z[j - 1], term)
        total = total + term
    held[bits] = total
    last = remote(held.at[bits], arrived.at[bits], send_sem.at[bits], recv_sem.at[bits], core)
    last.start()
    out_ref[side] = total
    last.wait()
    out_ref[1 - side] = arrived[bits]


def sum_everywhere(vector, collective_id):
    n_z = lax.axis_size("gx")
    bits = lax.axis_size("gy").bit_length() - 1
    lanes = 128
    length = vector.shape[0]
    rows = -(-length // (lanes * 16)) * 8
    padded = jnp.pad(vector, (0, 2 * rows * lanes - length)).reshape(2, rows, lanes)
    dma = pltpu.SemaphoreType.DMA
    out = pl.pallas_call(
        partial(sum_kernel, n_z, bits),
        out_shape=jax.ShapeDtypeStruct((2, rows, lanes), jnp.float32),
        in_specs=[pl.BlockSpec(memory_space=pltpu.VMEM)],
        out_specs=pl.BlockSpec(memory_space=pltpu.VMEM),
        scratch_shapes=[
            pltpu.VMEM((bits + 1, rows, lanes), jnp.float32),
            pltpu.VMEM((bits + 1, rows, lanes), jnp.float32),
            pltpu.VMEM((n_z - 1, rows, lanes), jnp.float32),
            dma((bits + 1,)),
            dma((n_z - 1,)),
            dma((bits + 1,)),
            dma((n_z - 1,)),
        ],
        compiler_params=pltpu.CompilerParams(collective_id=collective_id, has_side_effects=True),
        name="sum_everywhere",
    )(padded)
    return out.reshape(-1)[:length]


def enter_kernel(
    n_z,
    span,
    acts_ref,
    weight_ref,
    seq_ref,
    full_ref,
    send_sem,
    recv_sem,
    local_sem,
    chain_send,
    chain_recv,
    chain_local,
):
    chain = chain_gather(n_z, weight_ref, full_ref, chain_send, chain_recv, chain_local)
    gather_kernel(1, span, acts_ref, seq_ref, send_sem, recv_sem, local_sem, chain)


def enter(acts, weights, collective_id):
    n_z = lax.axis_size("gx")
    span = lax.axis_size("gy")
    rows, cols = acts.shape
    dma = pltpu.SemaphoreType.DMA
    seq, full = pl.pallas_call(
        partial(enter_kernel, n_z, span),
        out_shape=(
            jax.ShapeDtypeStruct((span, 2, rows // 2, cols), acts.dtype),
            jax.ShapeDtypeStruct((n_z,) + weights.shape, weights.dtype),
        ),
        in_specs=[pl.BlockSpec(memory_space=pltpu.VMEM)] * 2,
        out_specs=(pl.BlockSpec(memory_space=pl.ANY),) * 2,
        scratch_shapes=[
            dma((24,)),
            dma((span, 2)),
            dma,
            dma((2 * n_z,)),
            dma((n_z,)),
            dma,
        ],
        compiler_params=pltpu.CompilerParams(collective_id=collective_id, has_side_effects=True),
        name="enter",
    )(acts.reshape(2, rows // 2, cols), weights)
    return seq.reshape(span * rows, cols), full.reshape(n_z * weights.shape[0], weights.shape[1])


def chain_scatter(n_z, part_ref, out_ref, from_low, from_high, send_sem, low_recv, high_recv):
    z = lax.axis_index("gx")
    g = lax.axis_index("gy")
    rows = part_ref.shape[1]

    def up(dest):
        return pltpu.make_async_remote_copy(
            src_ref=part_ref.at[dest],
            dst_ref=from_low.at[dest],
            send_sem=send_sem.at[dest],
            recv_sem=low_recv.at[dest],
            device_id={"gx": z + 1, "gy": g},
            device_id_type=pl.DeviceIdType.MESH,
        )

    def down(dest):
        return pltpu.make_async_remote_copy(
            src_ref=part_ref.at[dest],
            dst_ref=from_high.at[dest],
            send_sem=send_sem.at[dest],
            recv_sem=high_recv.at[dest],
            device_id={"gx": z - 1, "gy": g},
            device_id_type=pl.DeviceIdType.MESH,
        )

    def start():
        for k in range(n_z - 1):
            run_if(z == 0, lambda k=k: up(n_z - 1 - k).start())
            run_if(z == n_z - 1, lambda k=k: down(k).start())

    def pass_up(dest):
        up(dest).wait_recv()
        add_into(part_ref.at[dest], (part_ref.at[dest], from_low.at[dest]), rows)
        up(dest).start()

    def pass_down(dest):
        down(dest).wait_recv()
        add_into(part_ref.at[dest], (part_ref.at[dest], from_high.at[dest]), rows)
        down(dest).start()

    def relay(time):
        for k in range(time):
            low, dest = time - k, n_z - 1 - k
            if 0 < low < dest:
                run_if(z == low, partial(pass_up, dest))
            high, dest = n_z - 1 - (time - k), k
            if dest < high < n_z - 1:
                run_if(z == high, partial(pass_down, dest))

    def finish():
        for dest in range(n_z):
            terms = [part_ref.at[dest]]
            terms += [from_low.at[dest]] if dest > 0 else []
            terms += [from_high.at[dest]] if dest < n_z - 1 else []

            def last(dest=dest, terms=terms):
                if dest > 0:
                    up(dest).wait_recv()
                if dest < n_z - 1:
                    down(dest).wait_recv()
                add_into(out_ref, terms, rows)

            run_if(z == dest, last)
        for dest in range(n_z):
            run_if(z != dest, lambda dest=dest: up(dest).wait_send())

    return start, [partial(relay, time) for time in range(1, n_z)], finish


def leave_kernel(
    n_i,
    rows,
    part_ref,
    weight_ref,
    out_ref,
    weight_out,
    held,
    from_core,
    from_a,
    from_b,
    from_z,
    sums,
    from_low,
    from_high,
    load_sem,
    core_send,
    a_send,
    b_send,
    z_send,
    core_recv,
    a_recv,
    b_recv,
    z_recv,
    copy_sem,
    chain_send,
    low_recv,
    high_recv,
):
    n_z = lax.axis_size("gx")
    copy = pltpu.make_async_copy(weight_ref, sums, copy_sem)
    copy.start()
    chain = chain_scatter(
        n_z, sums, weight_out, from_low, from_high, chain_send, low_recv, high_recv
    )

    def start():
        copy.wait()
        chain[0]()

    scatter_kernel(
        False,
        n_i,
        rows,
        part_ref,
        out_ref,
        held,
        from_core,
        from_a,
        from_b,
        from_z,
        load_sem,
        core_send,
        a_send,
        b_send,
        z_send,
        core_recv,
        a_recv,
        b_recv,
        z_recv,
        (start, chain[1], chain[2]),
    )


def leave(part, weight_part, collective_id, pieces=4):
    n_z = lax.axis_size("gx")
    span = lax.axis_size("gy")
    total, cols = part.shape
    rows = total // span // (2 * pieces)
    shaped = part.reshape(span, pieces, 2, rows, cols).swapaxes(0, 1)
    half = (rows, cols)
    dma = pltpu.SemaphoreType.DMA
    block = (weight_part.shape[0] // n_z, weight_part.shape[1])
    out, sums = pl.pallas_call(
        partial(leave_kernel, pieces, rows),
        out_shape=(
            jax.ShapeDtypeStruct((pieces, 2, rows, cols), jnp.float32),
            jax.ShapeDtypeStruct(block, jnp.float32),
        ),
        in_specs=[pl.BlockSpec(memory_space=pl.ANY)] * 2,
        out_specs=(pl.BlockSpec(memory_space=pltpu.VMEM),) * 2,
        scratch_shapes=[
            pltpu.VMEM((pieces, 4, 2) + half, jnp.bfloat16),
            pltpu.VMEM((pieces, 4, 2) + half, jnp.bfloat16),
            pltpu.VMEM((pieces, 2, 2) + half, jnp.bfloat16),
            pltpu.VMEM((pieces, 2) + half, jnp.bfloat16),
            pltpu.VMEM((1, 2, 16, 128), jnp.bfloat16),
            pltpu.VMEM((n_z,) + block, jnp.bfloat16),
            pltpu.VMEM((n_z,) + block, jnp.bfloat16),
            pltpu.VMEM((n_z,) + block, jnp.bfloat16),
            dma((pieces, 4)),
            dma((pieces, 4)),
            dma((pieces, 4)),
            dma((pieces, 2)),
            dma((pieces,)),
            dma((pieces, 4)),
            dma((pieces, 2, 2)),
            dma((pieces, 2)),
            dma((pieces,)),
            dma,
            dma((n_z,)),
            dma((n_z,)),
            dma((n_z,)),
        ],
        compiler_params=pltpu.CompilerParams(
            collective_id=collective_id, has_side_effects=True, vmem_limit_bytes=60 << 20
        ),
        name="leave",
    )(shaped, weight_part.reshape((n_z,) + block))
    return out.reshape(total // span, cols), sums


def gather_plane(block, collective_id):
    if lax.axis_size("gy") == 8:
        return all_gather(block, False, collective_id)
    return lax.all_gather(block, "gy", axis=0, tiled=True)


def gather_inputs(acts, weights):
    if lax.axis_size("gy") == 8:
        return enter(acts, weights, 6)
    return (
        lax.all_gather(acts, "gy", axis=0, tiled=True),
        lax.all_gather(weights, "gx", axis=0, tiled=True),
    )


def scatter_grads(acts_part, weight_part):
    if lax.axis_size("gy") == 8:
        return leave(acts_part, weight_part, 7)
    return (
        lax.psum_scatter(acts_part, "gy", scatter_dimension=0, tiled=True).astype(jnp.float32),
        lax.psum_scatter(weight_part, "gx", scatter_dimension=0, tiled=True).astype(jnp.float32),
    )


def scatter_plane(part, collective_id):
    if lax.axis_size("gy") == 8:
        return reduce_scatter(part, False, collective_id)
    return lax.psum_scatter(part, "gy", scatter_dimension=0, tiled=True).astype(jnp.float32)


def norm_rows(values, gain_row):
    return (
        values * lax.rsqrt(jnp.mean(values * values, axis=-1, keepdims=True) + EPSILON) * gain_row
    )


def rotary(values):
    length = values.shape[0]
    halfway = values.shape[-1] // 2
    positions = jnp.arange(length, dtype=jnp.float32)
    frequency = jnp.exp(
        jnp.arange(halfway, dtype=jnp.float32) * (-2.0 * jnp.log(10000.0) / values.shape[-1])
    )
    angles = (positions[:, None] * frequency[None, :])[:, None, :]
    cosine = jnp.cos(angles)
    sine_table = jnp.sin(angles)
    first_half = values[..., :halfway]
    second = values[..., halfway:]
    return jnp.concatenate(
        [first_half * cosine - second * sine_table, second * cosine + first_half * sine_table],
        axis=-1,
    )


def prepare_heads(raw_heads, gain_row):
    return rotary(norm_rows(raw_heads, gain_row))


def route_gates(id_table, logits):
    shares = jax.nn.softmax(logits, axis=-1)
    experts = logits.shape[-1]
    matches = id_table[:, :, None] == jnp.arange(experts, dtype=jnp.int32)[None, None, :]
    chosen = jnp.sum(jnp.where(matches, shares[:, None, :], 0.0), axis=-1)
    return chosen / jnp.sum(chosen, axis=-1, keepdims=True)


def dense_gates(all_ids, logits, expert):
    shares = jax.nn.softmax(logits, axis=-1)
    columns = jnp.arange(logits.shape[-1], dtype=jnp.int32)
    routed = jnp.any(all_ids[:, :, None] == columns[None, None, :], axis=1)
    chosen = jnp.where(routed, shares, 0.0)
    own = jnp.sum(jnp.where(columns[None, :] == expert, chosen, 0.0), axis=-1)
    return own / jnp.sum(chosen, axis=-1)


def contract_rows(left_side, right_side):
    return lax.dot_general(
        left_side, right_side, (((0,), (0,)), ((), ())), preferred_element_type=jnp.float32
    )


def contract_cols(left_side, right_side):
    return lax.dot_general(
        left_side, right_side, (((1,), (1,)), ((), ())), preferred_element_type=jnp.float32
    )


def routed_experts(
    moe_in, cotangent, expert_ids, gate_share, router_weight, gate_weight, up_weight, down_weight
):
    tok_rows = moe_in.shape[0]
    experts = router_weight.shape[1]
    width_all = moe_in.shape[1]
    capacity = tok_rows * TOP * 3 // (2 * experts)
    route_count = tok_rows * TOP
    flat_ids = expert_ids.reshape(route_count)
    onehot = (flat_ids[:, None] == jnp.arange(experts, dtype=jnp.int32)[None, :]).astype(jnp.int32)
    earlier = jnp.cumsum(onehot, axis=0) - onehot
    slot_index = jnp.sum(earlier * onehot, axis=1)
    target = flat_ids * capacity + slot_index
    source = (
        jnp.full((experts * capacity,), tok_rows, jnp.int32)
        .at[target]
        .set(jnp.arange(route_count, dtype=jnp.int32) // TOP)
    )
    padded_in = jnp.concatenate([moe_in, jnp.zeros((1, width_all), jnp.bfloat16)], axis=0)
    packed = padded_in[source].reshape(experts, 1, capacity, width_all)
    outgoing = jnp.broadcast_to(packed, (experts, 2, capacity, width_all)).reshape(
        2 * experts, capacity, width_all
    )
    arrived = lax.all_to_all(outgoing, ("gx", "gy"), split_axis=0, concat_axis=1, tiled=True)[0]
    gate_in = gate_weight[0]
    up_in = up_weight[0]
    down_in = down_weight[0]
    gate_val = jnp.dot(arrived, gate_in, preferred_element_type=jnp.float32)
    up_val = jnp.dot(arrived, up_in, preferred_element_type=jnp.float32)
    hidden = (jax.nn.silu(gate_val) * up_val).astype(jnp.bfloat16)
    produced = jnp.dot(hidden, down_in, preferred_element_type=jnp.float32).astype(jnp.bfloat16)
    returned = lax.all_to_all(produced[None], ("gx", "gy"), split_axis=1, concat_axis=0, tiled=True)
    summed = (
        returned.reshape(experts, 2, capacity, width_all)
        .astype(jnp.float32)
        .sum(axis=1)
        .reshape(experts * capacity, width_all)
    )
    route_out = summed[target]
    gates_flat = gate_share.reshape(route_count)
    moe_out = jnp.sum((gates_flat[:, None] * route_out).reshape(tok_rows, TOP, width_all), axis=1)
    grad_out = cotangent.astype(jnp.float32)
    grad_gates = jnp.sum(
        route_out.reshape(tok_rows, TOP, width_all) * grad_out[:, None, :], axis=-1
    )
    slot_gate = jnp.zeros((experts * capacity,), jnp.float32).at[target].set(gates_flat)
    padded_grad = jnp.concatenate([grad_out, jnp.zeros((1, width_all), jnp.float32)], axis=0)
    grad_packed = (
        (slot_gate[:, None] * padded_grad[source])
        .astype(jnp.bfloat16)
        .reshape(experts, 1, capacity, width_all)
    )
    grad_outgoing = jnp.broadcast_to(grad_packed, (experts, 2, capacity, width_all)).reshape(
        2 * experts, capacity, width_all
    )
    grad_arrived = lax.all_to_all(
        grad_outgoing, ("gx", "gy"), split_axis=0, concat_axis=1, tiled=True
    )[0]
    rows_in, grad_use = (arrived, grad_arrived)
    gate_use, up_use, hidden_use = (gate_val, up_val, hidden)
    sigmoid_gate = jax.nn.sigmoid(gate_use)
    silu_gate = gate_use * sigmoid_gate
    grad_hidden = contract_cols(grad_use, down_in)
    down_part = contract_rows(hidden_use, grad_use)
    grad_gate = (
        grad_hidden * up_use * sigmoid_gate * (1.0 + gate_use * (1.0 - sigmoid_gate))
    ).astype(jnp.bfloat16)
    grad_up = (grad_hidden * silu_gate).astype(jnp.bfloat16)
    gate_part = contract_rows(rows_in, grad_gate)
    up_part = contract_rows(rows_in, grad_up)
    grad_in = contract_cols(grad_gate, gate_in) + contract_cols(grad_up, up_in)
    grad_back = lax.all_to_all(
        grad_in.astype(jnp.bfloat16)[None], ("gx", "gy"), split_axis=1, concat_axis=0, tiled=True
    )
    grad_summed = (
        grad_back.reshape(experts, 2, capacity, width_all)
        .astype(jnp.float32)
        .sum(axis=1)
        .reshape(experts * capacity, width_all)
    )
    grad_moe_in = jnp.sum(grad_summed[target].reshape(tok_rows, TOP, width_all), axis=1)
    return moe_out, grad_gates, grad_moe_in, gate_part, up_part, down_part


def dense_experts(
    moe_in, cotangent, expert_ids, gate_share, router_weight, gate_weight, up_weight, down_weight
):
    experts = router_weight.shape[1]
    everyone = ("gx", "gy")
    all_ids = lax.all_gather(expert_ids, everyone, axis=0, tiled=True)
    all_cot = lax.all_gather(cotangent, everyone, axis=0, tiled=True)
    all_moe = all_gather(moe_in, True, 2)
    rank = lax.axis_index("gx") * lax.axis_size("gy") + lax.axis_index("gy")
    own_gate = dense_gates(
        all_ids, jnp.dot(all_moe, router_weight, preferred_element_type=jnp.float32), rank // 2
    )
    gate_in = gate_weight[0]
    up_in = up_weight[0]
    down_in = down_weight[0]
    gate_val = jnp.dot(all_moe, gate_in, preferred_element_type=jnp.float32)
    up_val = jnp.dot(all_moe, up_in, preferred_element_type=jnp.float32)
    sigmoid_gate = jax.nn.sigmoid(gate_val)
    silu_gate = gate_val * sigmoid_gate
    hidden = (silu_gate * up_val).astype(jnp.bfloat16)
    piece = jnp.dot(hidden, down_in, preferred_element_type=jnp.float32)
    cot_float = all_cot.astype(jnp.float32)
    gate_dots = jnp.sum(piece * cot_float, axis=-1)
    devices = lax.axis_size("gx") * lax.axis_size("gy")
    dots_back = lax.all_to_all(
        gate_dots.reshape(devices, -1), everyone, split_axis=0, concat_axis=0, tiled=True
    )
    dots_experts = dots_back.reshape(experts, 2, -1).sum(axis=1).T
    matches = expert_ids[:, :, None] == jnp.arange(experts, dtype=jnp.int32)[None, None, :]
    grad_gates = jnp.sum(jnp.where(matches, dots_experts[:, None, :], 0.0), axis=-1)
    moe_out = reduce_scatter((piece * own_gate[:, None]).astype(jnp.bfloat16), True, 4)
    grad_use = (cot_float * own_gate[:, None]).astype(jnp.bfloat16)
    grad_hidden = contract_cols(grad_use, down_in)
    down_part = contract_rows(hidden, grad_use)
    grad_gate = (
        grad_hidden * up_val * sigmoid_gate * (1.0 + gate_val * (1.0 - sigmoid_gate))
    ).astype(jnp.bfloat16)
    grad_up = (grad_hidden * silu_gate).astype(jnp.bfloat16)
    gate_part = contract_rows(all_moe, grad_gate)
    up_part = contract_rows(all_moe, grad_up)
    grad_in = contract_cols(grad_gate, gate_in) + contract_cols(grad_up, up_in)
    grad_moe_in = reduce_scatter(grad_in.astype(jnp.bfloat16), True, 4)
    return moe_out, grad_gates, grad_moe_in, gate_part, up_part, down_part


def local(
    tokens,
    cotangent,
    expert_ids,
    doc_ids,
    clip_rank,
    attn_gain,
    moe_gain,
    query_gain,
    key_gain,
    query_weight,
    key_weight,
    value_weight,
    out_weight,
    router_weight,
    gate_weight,
    up_weight,
    down_weight,
):
    inputs = tokens.astype(jnp.float32)
    acts_float, norm_pull = jax.vjp(norm_rows, inputs, attn_gain)
    acts_low = acts_float.astype(jnp.bfloat16)
    in_weights = jnp.concatenate([query_weight, key_weight, value_weight], axis=1)
    seq_acts, full_in = gather_inputs(acts_low, in_weights)
    out_rows = lax.all_gather(out_weight, "gx", axis=1, tiled=True)
    length = seq_acts.shape[0]
    local_width = query_weight.shape[1]
    local_heads = local_width // HD
    projected = jnp.dot(seq_acts, full_in, preferred_element_type=jnp.float32)
    queries = projected[:, :local_width]
    key_raw = projected[:, local_width : 2 * local_width]
    value_ready = (
        projected[:, 2 * local_width :].astype(jnp.bfloat16).reshape(length, local_heads, HD)
    )
    query_float, query_pull = jax.vjp(
        prepare_heads, queries.reshape(length, local_heads, HD), query_gain
    )
    key_float, key_pull = jax.vjp(prepare_heads, key_raw.reshape(length, local_heads, HD), key_gain)
    query_ready = query_float.astype(jnp.bfloat16)
    key_ready = key_float.astype(jnp.bfloat16)
    block_rows = min(512, length)
    block_count = length // block_rows
    score_scale = HD ** (-0.5)
    query_blocks = query_ready.reshape(block_count, block_rows, local_heads, HD)
    doc_blocks = doc_ids.reshape(block_count, block_rows)

    def block_scores(query_block, doc_block):
        scores = (
            jnp.einsum("qhd,khd->hqk", query_block, key_ready, preferred_element_type=jnp.float32)
            * score_scale
        )
        same_doc = doc_block[:, None] == doc_ids[None, :]
        return jnp.where(same_doc[None], scores, NEGATIVE)

    def forward_block(pieces):
        scores = block_scores(pieces[0], pieces[1])
        highest = jnp.max(scores, axis=-1, keepdims=True)
        weights = jnp.exp(scores - highest)
        totals = jnp.sum(weights, axis=-1, keepdims=True)
        shares = (weights / totals).astype(jnp.bfloat16)
        mixed_heads = jnp.einsum(
            "hqk,khd->qhd", shares, value_ready, preferred_element_type=jnp.float32
        )
        return (
            mixed_heads.astype(jnp.bfloat16),
            highest[..., 0] + jnp.log(totals[..., 0]),
            jnp.max(highest[..., 0], axis=-1),
        )

    mixed_blocks, log_totals, peak_blocks = lax.map(forward_block, (query_blocks, doc_blocks))
    mixed_seq = mixed_blocks.reshape(length, local_width)
    start_head = lax.axis_index("gy") * local_heads
    peak_slots = lax.dynamic_update_slice(
        jnp.zeros((lax.axis_size("gx"), NH), jnp.float32),
        jnp.max(peak_blocks, axis=0)[None],
        (lax.axis_index("gx"), start_head),
    )
    attended = scatter_plane(
        jnp.dot(mixed_seq, out_rows, preferred_element_type=jnp.float32).astype(jnp.bfloat16), 3
    )
    residual = inputs + attended
    moe_float, moe_pull = jax.vjp(norm_rows, residual, moe_gain)
    moe_in = moe_float.astype(jnp.bfloat16)
    logits = jnp.dot(moe_in, router_weight, preferred_element_type=jnp.float32)
    gate_share, gate_pull = jax.vjp(partial(route_gates, expert_ids), logits)
    experts_pass = dense_experts if lax.axis_size("gy") == 8 and router_weight.shape[1] <= 2 * TOP else routed_experts
    moe_out, grad_gates, grad_moe_in, gate_part, up_part, down_part = experts_pass(
        moe_in,
        cotangent,
        expert_ids,
        gate_share,
        router_weight,
        gate_weight,
        up_weight,
        down_weight,
    )
    output = (residual + moe_out).astype(jnp.bfloat16)
    grad_out = cotangent.astype(jnp.float32)
    (grad_logits,) = gate_pull(grad_gates)
    grad_logits_low = grad_logits.astype(jnp.bfloat16)
    router_part = contract_rows(moe_in, grad_logits_low)
    grad_moe_in = grad_moe_in + contract_cols(grad_logits_low, router_weight)
    grad_resid_norm, moe_gain_part = moe_pull(grad_moe_in)
    grad_resid = grad_out + grad_resid_norm
    seq_grad = gather_plane(grad_resid.astype(jnp.bfloat16), 1)
    grad_mixed = contract_cols(seq_grad, out_rows).astype(jnp.bfloat16)
    out_part = contract_rows(seq_grad, mixed_seq)

    def backward_block(running, pieces):
        grad_key, grad_value = running
        query_block, grad_block, log_block, doc_block = pieces
        scores = block_scores(query_block, doc_block)
        weights = jnp.exp(scores - log_block[..., None])
        grad_value = grad_value + jnp.einsum(
            "hqk,qhd->khd",
            weights.astype(jnp.bfloat16),
            grad_block,
            preferred_element_type=jnp.float32,
        )
        grad_weights = jnp.einsum(
            "qhd,khd->hqk", grad_block, value_ready, preferred_element_type=jnp.float32
        )
        inner_sum = jnp.sum(weights * grad_weights, axis=-1, keepdims=True)
        grad_scores = (weights * (grad_weights - inner_sum)).astype(jnp.bfloat16)
        grad_query = (
            jnp.einsum("hqk,khd->qhd", grad_scores, key_ready, preferred_element_type=jnp.float32)
            * score_scale
        )
        grad_key = (
            grad_key
            + jnp.einsum(
                "hqk,qhd->khd", grad_scores, query_block, preferred_element_type=jnp.float32
            )
            * score_scale
        )
        return ((grad_key, grad_value), grad_query)

    empty_heads = jnp.zeros((length, local_heads, HD), jnp.float32)
    grad_mixed_blocks = grad_mixed.reshape(block_count, block_rows, local_heads, HD)
    (key_grad_heads, value_grad_heads), query_grad_blocks = lax.scan(
        backward_block,
        (empty_heads, empty_heads),
        (query_blocks, grad_mixed_blocks, log_totals, doc_blocks),
    )
    query_raw_grad, query_gain_part = query_pull(query_grad_blocks.reshape(length, local_heads, HD))
    key_raw_grad, key_gain_part = key_pull(key_grad_heads)
    grad_queries = query_raw_grad.reshape(length, local_width).astype(jnp.bfloat16)
    grad_keys = key_raw_grad.reshape(length, local_width).astype(jnp.bfloat16)
    grad_values = value_grad_heads.reshape(length, local_width).astype(jnp.bfloat16)
    grad_heads = jnp.concatenate([grad_queries, grad_keys, grad_values], axis=1)
    grad_acts, in_sum = scatter_grads(
        contract_cols(grad_heads, full_in).astype(jnp.bfloat16),
        contract_rows(seq_acts, grad_heads).astype(jnp.bfloat16),
    )
    query_sum = in_sum[:, :local_width]
    key_sum = in_sum[:, local_width : 2 * local_width]
    value_sum = in_sum[:, 2 * local_width :]
    out_sum_rows = lax.psum_scatter(
        out_part.astype(jnp.bfloat16), "gx", scatter_dimension=0, tiled=True
    ).astype(jnp.float32)
    norm_input_grad, attn_gain_part = norm_pull(grad_acts)
    input_grad = grad_resid + norm_input_grad
    small = (
        attn_gain_part,
        moe_gain_part,
        query_gain_part,
        key_gain_part,
        router_part.T,
        peak_slots,
    )
    summed = sum_everywhere(jnp.concatenate([part.reshape(-1) for part in small]), 5)
    ends = list(accumulate(part.size for part in small))
    attn_gain_grad, moe_gain_grad, query_gain_grad, key_gain_grad, router_flat, peaks = (
        summed[end - part.size : end].reshape(part.shape) for end, part in zip(ends, small)
    )
    router_grad = router_flat.T
    peak_global = jnp.max(peaks, axis=0)
    ranked = -jnp.sort(-peak_global)
    limit = jnp.sum(jnp.where(jnp.arange(NH, dtype=jnp.int32) == clip_rank[0], ranked, 0.0))
    factors = jnp.where(peak_global > limit, limit / peak_global, 1.0)
    own_factors = lax.dynamic_slice_in_dim(factors, start_head, local_heads)
    columns = jnp.repeat(jnp.sqrt(own_factors), HD)
    query_clipped = (query_weight.astype(jnp.float32) * columns[None, :]).astype(jnp.bfloat16)
    key_clipped = (key_weight.astype(jnp.float32) * columns[None, :]).astype(jnp.bfloat16)
    return (
        output,
        input_grad,
        attn_gain_grad,
        moe_gain_grad,
        query_gain_grad,
        key_gain_grad,
        query_sum,
        key_sum,
        value_sum,
        out_sum_rows.T,
        router_grad,
        gate_part[None],
        up_part[None],
        down_part[None],
        query_clipped,
        key_clipped,
        factors,
    )


def solution(mesh):
    placed = (
        P(("gx", "gy"), None),
        P(("gx", "gy"), None),
        P(("gx", "gy"), None),
        P("gx"),
        P(),
        P(),
        P(),
        P(),
        P(),
        P("gx", "gy"),
        P("gx", "gy"),
        P("gx", "gy"),
        P("gy", "gx"),
        P(),
        P(("gx", "gy"), None, None),
        P(("gx", "gy"), None, None),
        P(("gx", "gy"), None, None),
    )
    return jax.shard_map(
        local,
        mesh=mesh,
        in_specs=placed,
        out_specs=(
            P(("gx", "gy"), None),
            P(("gx", "gy"), None),
            P(),
            P(),
            P(),
            P(),
            P("gx", "gy"),
            P("gx", "gy"),
            P("gx", "gy"),
            P("gy", "gx"),
            P(),
            P(("gx", "gy"), None, None),
            P(("gx", "gy"), None, None),
            P(("gx", "gy"), None, None),
            P("gx", "gy"),
            P("gx", "gy"),
            P(),
        ),
        check_vma=False,
    )
```

```python
from functools import partial
from itertools import accumulate

import jax
import jax.numpy as jnp
from jax import lax
from jax.experimental import pallas as pl
from jax.experimental.pallas import tpu as pltpu
from jax.sharding import PartitionSpec as P

NH = 16
HD = 128
TOP = 8


EPSILON = 1e-06
NEGATIVE = -1e30


def barrier_with(partners):
    barrier = pltpu.get_barrier_semaphore()
    for ok, device in partners:
        @pl.when(ok)
        def _():
            pl.semaphore_signal(barrier, inc=1, device_id=device, device_id_type=pl.DeviceIdType.MESH)
    pl.semaphore_wait(barrier, sum(ok.astype(jnp.int32) for ok, _ in partners))

def always(ok, other):
    if ok is True:
        return other
    return ok if other is True else jnp.logical_and(ok, other)


def run_if(ok, action):
    if ok is True:
        action()
    else:
        pl.when(ok)(action)


def chain_gather(n_z, own_ref, out_ref, send_sem, recv_sem, local_sem):
    z = lax.axis_index("gx")
    g = lax.axis_index("gy")

    def hop(source, owner, k, peer):
        return pltpu.make_async_remote_copy(
            src_ref=source,
            dst_ref=out_ref.at[owner],
            send_sem=send_sem.at[k],
            recv_sem=recv_sem.at[owner],
            device_id={"gx": peer, "gy": g},
            device_id_type=pl.DeviceIdType.MESH,
        )

    local = pltpu.make_async_copy(own_ref, out_ref.at[z], local_sem)
    upward = [(z < n_z - 1, lambda: hop(own_ref, z, 0, z + 1))]
    downward = [(z > 0, lambda: hop(own_ref, z, n_z, z - 1))]
    for d in range(1, n_z - 1):
        upward.append(
            (
                jnp.logical_and(z >= d, z < n_z - 1),
                lambda d=d: hop(out_ref.at[z - d], z - d, d, z + 1),
            )
        )
        downward.append(
            (
                jnp.logical_and(z < n_z - d, z > 0),
                lambda d=d: hop(out_ref.at[z + d], z + d, n_z + d, z - 1),
            )
        )

    def start():
        local.start()
        for ok, copy in (upward[0], downward[0]):
            run_if(ok, lambda copy=copy: copy().start())

    def relay(d):
        run_if(z >= d, lambda: hop(own_ref, z - d, 0, z).wait_recv())
        if d < n_z - 1:
            run_if(upward[d][0], lambda: upward[d][1]().start())
        run_if(z < n_z - d, lambda: hop(own_ref, z + d, 0, z).wait_recv())
        if d < n_z - 1:
            run_if(downward[d][0], lambda: downward[d][1]().start())

    def finish():
        local.wait()
        for ok, copy in upward + downward:
            run_if(ok, lambda copy=copy: copy().wait_send())

    return start, [partial(relay, d) for d in range(1, n_z)], finish


def gather_kernel(n_z, span, own_ref, out_ref, send_sem, recv_sem, local_sem, chain=None):
    z = lax.axis_index("gx"); g = lax.axis_index("gy")
    core = {"gx": z, "gy": g + 1 - 2 * (g % 2)}
    xn = {"gx": z, "gy": g + 2 - 4 * ((g // 2) % 2)}
    yn = {"gx": z, "gy": g + 4 - 8 * ((g // 4) % 2)}
    gx_ = g + 2 - 4 * ((g // 2) % 2)
    gy_ = g + 4 - 8 * ((g // 4) % 2)
    gd_ = gx_ + gy_ - g
    gc = lambda v: v + 1 - 2 * (v % 2)
    zup = {"gx": z + 1, "gy": g}; zdn = {"gx": z - 1, "gy": g}
    zb = z if n_z > 1 else 0
    partners = [(z >= 0, core), (z >= 0, xn), (z >= 0, yn)]
    n_chain = lax.axis_size("gx") if chain else n_z
    if n_chain > 1:
        partners += [(z < n_chain - 1, zup), (z > 0, zdn)]
    barrier_with(partners)
    if chain:
        chain[0]()
    sends = []
    def send(ok, src, b, h, dev):
        k = len(sends)
        def make():
            return pltpu.make_async_remote_copy(
                src_ref=src, dst_ref=out_ref.at[b, h], send_sem=send_sem.at[k], recv_sem=recv_sem.at[b, h],
                device_id=dev, device_id_type=pl.DeviceIdType.MESH)
        sends.append((ok, make))
        if ok is True:
            make().start()
        else:
            @pl.when(ok)
            def _(): make().start()
    def arrive(ok, b, h):
        def go():
            pltpu.make_async_remote_copy(
                src_ref=out_ref.at[b, h], dst_ref=out_ref.at[b, h], send_sem=send_sem.at[0], recv_sem=recv_sem.at[b, h],
                device_id=core, device_id_type=pl.DeviceIdType.MESH).wait_recv()
        if ok is True:
            go()
        else:
            @pl.when(ok)
            def _(): go()
    own_b = zb * span + g
    local = pltpu.make_async_copy(own_ref, out_ref.at[own_b], local_sem)
    local.start()
    items = [(True, zb, 0)]
    for d in range(1, n_z):
        items += [(z >= d, z - d, -d), (z < n_z - d, z + d, d)]
    def and_(a, b):
        if a is True: return b
        if b is True: return a
        return jnp.logical_and(a, b)
    def first(it):
        ok, zs, d = it
        b = zs * span + g
        src = (lambda h: own_ref.at[h]) if d == 0 else (lambda h: out_ref.at[b, h])
        if d != 0:
            arrive(ok, b, 0); arrive(ok, b, 1)
        if n_z > 1:
            if d <= 0:
                for h in range(2): send(and_(ok, z < n_z - 1), src(h), b, h, zup)
            if d >= 0:
                for h in range(2): send(and_(ok, z > 0), src(h), b, h, zdn)
        send(ok, src(0), b, 0, xn)
        send(ok, src(1), b, 1, yn)
        send(ok, src(1), b, 1, xn)
        send(ok, src(0), b, 0, yn)
        send(ok, src(0), b, 0, core)
        send(ok, src(1), b, 1, core)
    def second(it):
        ok, zs, d = it
        b = zs * span + gx_
        arrive(ok, b, 0)
        send(ok, out_ref.at[b, 0], b, 0, yn)
        send(ok, out_ref.at[b, 0], b, 0, core)
        b = zs * span + gy_
        arrive(ok, b, 1)
        send(ok, out_ref.at[b, 1], b, 1, xn)
        send(ok, out_ref.at[b, 1], b, 1, core)
    def third(it):
        ok, zs, d = it
        for b, h in ((zs * span + gd_, 0), (zs * span + gd_, 1), (zs * span + gy_, 0), (zs * span + gx_, 1)):
            arrive(ok, b, h)
            send(ok, out_ref.at[b, h], b, h, core)
    n = len(items)
    for i in range(n + 2):
        if i < n: first(items[i])
        if 1 <= i <= n: second(items[i - 1])
        if i >= 2: third(items[i - 2])
    if chain:
        chain[1][0]()
    for ok, zs, d in items:
        for gg in (g, gx_, gy_, gd_):
            for h in range(2): arrive(ok, zs * span + gc(gg), h)
    if chain:
        for relay in chain[1][1:]:
            relay()
        chain[2]()
    local.wait()
    for ok, make in sends:
        if ok is True: make().wait_send()
        else:
            @pl.when(ok)
            def _(): make().wait_send()

def all_gather(block, both, collective_id):
    n_z = lax.axis_size("gx") if both else 1
    span = lax.axis_size("gy")
    rows, cols = block.shape
    own = block.reshape(2, rows // 2, cols)
    n_sends = (2 * n_z - 1) * 24
    out = pl.pallas_call(
        partial(gather_kernel, n_z, span),
        out_shape=jax.ShapeDtypeStruct((n_z * span, 2, rows // 2, cols), block.dtype),
        in_specs=[pl.BlockSpec(memory_space=pltpu.VMEM)],
        out_specs=pl.BlockSpec(memory_space=pl.ANY),
        scratch_shapes=[pltpu.SemaphoreType.DMA((n_sends,)), pltpu.SemaphoreType.DMA((n_z * span, 2)), pltpu.SemaphoreType.DMA],
        compiler_params=pltpu.CompilerParams(collective_id=collective_id, has_side_effects=True),
        name="gather_all" if both else "gather_plane",
    )(own)
    return out.reshape(n_z * span * rows, cols)


def add_into(dst, parts, rows):
    step = min(rows, 32)

    @pl.loop(0, rows // step)
    def _(r):
        at = pl.ds(pl.multiple_of(r * step, step), step)
        if len(parts) == 2 and dst.dtype == jnp.bfloat16:
            dst[at, :] = parts[0][at, :] + parts[1][at, :]
        else:
            total = parts[0][at, :].astype(jnp.float32)
            for term in parts[1:]:
                total = total + term[at, :].astype(jnp.float32)
            dst[at, :] = total.astype(dst.dtype)


def scatter_kernel(chain, n_i, rows, part_ref, out_ref, held, from_core, from_a, from_b, from_z,
                   load_sem, core_send, a_send, b_send, z_send, core_recv, a_recv, b_recv, z_recv, beside=None):
    z = lax.axis_index("gx"); g = lax.axis_index("gy")
    flip_x = g + 2 - 4 * ((g // 2) % 2)
    flip_y = g + 4 - 8 * ((g // 4) % 2)
    flip_c = lambda v: v + 1 - 2 * (v % 2)
    quads = (flip_x + flip_y - g, flip_x, flip_y, g)
    core = {"gx": z, "gy": flip_c(g)}
    xn = {"gx": z, "gy": flip_x}
    yn = {"gx": z, "gy": flip_y}
    every = z >= 0
    partners = [(every, core), (every, xn), (every, yn)]
    if chain:
        partners += [(every, {"gx": lax.rem(z + j, n_i), "gy": g}) for j in range(1, n_i)]
    if beside:
        n_z = lax.axis_size("gx")
        partners += [(z < n_z - 1, {"gx": z + 1, "gy": g}), (z > 0, {"gx": z - 1, "gy": g})]
    barrier_with(partners)
    if beside:
        beside[0]()
    mesh_id = pl.DeviceIdType.MESH

    def item(i):
        return lax.rem(z + n_i - 1 - i + n_i, n_i) if chain else i

    def block(it, gg):
        return part_ref.at[it, gg]

    def remote(src, dst, ssem, rsem, dev):
        return pltpu.make_async_remote_copy(src_ref=src, dst_ref=dst, send_sem=ssem, recv_sem=rsem, device_id=dev, device_id_type=mesh_id)

    def core_copy(i, q):
        it = item(i)
        return remote(block(it, flip_c(quads[q])), from_core.at[it, q], core_send.at[i, q], core_recv.at[it, q], core)

    def load(i, q):
        it = item(i)
        return pltpu.make_async_copy(block(it, quads[q]), held.at[it, q], load_sem.at[i, q])

    a_plan = ((0, 0, 0, xn), (0, 1, 0, yn), (1, 0, 1, xn), (2, 1, 1, yn))
    def a_copy(i, k):
        it = item(i)
        q, h, slot, dev = a_plan[k]
        return remote(held.at[it, q, h], from_a.at[it, h, slot], a_send.at[i, k], a_recv.at[it, h, slot], dev)

    b_plan = ((2, 0, yn), (1, 1, xn))
    def b_copy(i, h):
        it = item(i)
        q, _, dev = b_plan[h]
        return remote(held.at[it, q, h], from_b.at[it, h], b_send.at[i, h], b_recv.at[it, h], dev)

    def z_copy(i):
        it = item(i)
        return remote(held.at[it, 3], from_z.at[z], z_send.at[i], z_recv.at[z], {"gx": it, "gy": g})

    def z_arrival(i):
        it = item(i)
        return remote(held.at[it, 3], from_z.at[it], z_send.at[i], z_recv.at[it], core)

    for i in range(n_i):
        for q in range(4):
            core_copy(i, q).start()
            load(i, q).start()

    def stage_a(i):
        it = item(i)
        for q in range(4):
            load(i, q).wait()
            core_copy(i, q).wait_recv()
            for h in range(2):
                add_into(held.at[it, q, h], (held.at[it, q, h], from_core.at[it, q, h]), rows)
            for k in range(4):
                if a_plan[k][0] == q:
                    a_copy(i, k).start()

    def stage_b(i):
        it = item(i)
        for q, h, slot in ((2, 0, 0), (1, 1, 0), (3, 0, 1), (3, 1, 1)):
            remote(held.at[it, q, h], from_a.at[it, h, slot], a_send.at[i, 0], a_recv.at[it, h, slot], core).wait_recv()
            add_into(held.at[it, q, h], (held.at[it, q, h], from_a.at[it, h, slot]), rows)
            if slot == 0:
                b_copy(i, h).start()

    def stage_c(i):
        it = item(i)
        for h in range(2):
            b_copy(i, h).wait_recv()
            if chain:
                add_into(held.at[it, 3, h], (held.at[it, 3, h], from_b.at[it, h]), rows)
            else:
                add_into(out_ref.at[it, h], (held.at[it, 3, h], from_b.at[it, h]), rows)

    def stage_d(i):
        if i < n_i - 1:
            z_copy(i).start()
        else:
            for j in range(n_i - 1):
                z_arrival(j).wait_recv()
            for h in range(2):
                add_into(
                    out_ref.at[h],
                    [held.at[item(i), 3, h]] + [from_z.at[item(j), h] for j in range(n_i - 1)],
                    rows,
                )

    for i in range(n_i + 2):
        if i < n_i: stage_a(i)
        if 0 <= i - 1 < n_i: stage_b(i - 1)
        if 0 <= i - 2 < n_i: stage_c(i - 2)
        if chain and 0 <= i - 2 < n_i: stage_d(i - 2)
        if beside and i == n_i:
            beside[1][0]()
    if beside:
        for relay in beside[1][1:]:
            relay()
        beside[2]()
    for i in range(n_i):
        for q in range(4): core_copy(i, q).wait_send()
        for k in range(4): a_copy(i, k).wait_send()
        for h in range(2): b_copy(i, h).wait_send()
        if chain and i < n_i - 1: z_copy(i).wait_send()


def reduce_scatter(part, both, collective_id, pieces=4, out_dtype=jnp.float32):
    n_z = lax.axis_size("gx") if both else 1
    span = lax.axis_size("gy")
    total, cols = part.shape
    n_i = n_z if both else pieces
    if both:
        rows = total // (n_z * span) // 2
        shaped = part.reshape(n_z, span, 2, rows, cols)
        out_shape = (2, rows, cols)
    else:
        rows = total // span // (2 * pieces)
        shaped = part.reshape(span, pieces, 2, rows, cols).swapaxes(0, 1)
        out_shape = (pieces, 2, rows, cols)
    dma = pltpu.SemaphoreType.DMA
    half = (rows, cols)
    z_items = n_i if both else 1
    z_half = half if both else (16, 128)
    out = pl.pallas_call(
        partial(scatter_kernel, both, n_i, rows),
        out_shape=jax.ShapeDtypeStruct(out_shape, out_dtype),
        in_specs=[pl.BlockSpec(memory_space=pl.ANY)],
        out_specs=pl.BlockSpec(memory_space=pltpu.VMEM),
        scratch_shapes=[
            pltpu.VMEM((n_i, 4, 2) + half, jnp.bfloat16),
            pltpu.VMEM((n_i, 4, 2) + half, jnp.bfloat16),
            pltpu.VMEM((n_i, 2, 2) + half, jnp.bfloat16),
            pltpu.VMEM((n_i, 2) + half, jnp.bfloat16),
            pltpu.VMEM((z_items, 2) + z_half, jnp.bfloat16),
            dma((n_i, 4)), dma((n_i, 4)), dma((n_i, 4)), dma((n_i, 2)), dma((n_i,)),
            dma((n_i, 4)), dma((n_i, 2, 2)), dma((n_i, 2)), dma((n_i,)),
        ],
        compiler_params=pltpu.CompilerParams(collective_id=collective_id, has_side_effects=True, vmem_limit_bytes=60 << 20),
        name="scatter_all" if both else "scatter_plane",
    )(shaped)
    return out.reshape(total // (n_z * span), cols)


def sum_kernel(n_z, bits, vec_ref, out_ref, held, arrived, from_z, send_sem, z_send, recv_sem, z_recv):
    z = lax.axis_index("gx")
    g = lax.axis_index("gy")
    half = vec_ref.shape[1]
    side = lax.rem(g, 2)
    core = {"gx": z, "gy": g + 1 - 2 * (g % 2)}
    peers = [
        {"gx": z, "gy": g + bit - 2 * bit * ((g // bit) % 2)}
        for bit in (2**power for power in range(1, bits))
    ]
    others = [{"gx": lax.rem(z + j, n_z), "gy": g} for j in range(1, n_z)]
    barrier_with([(z >= 0, peer) for peer in (core, *peers, *others)])

    def remote(src, dst, ssem, rsem, peer):
        return pltpu.make_async_remote_copy(
            src_ref=src,
            dst_ref=dst,
            send_sem=ssem,
            recv_sem=rsem,
            device_id=peer,
            device_id_type=pl.DeviceIdType.MESH,
        )

    first = remote(vec_ref.at[1 - side], arrived.at[0], send_sem.at[0], recv_sem.at[0], core)
    first.start()
    first.wait()
    held[0] = vec_ref[side] + arrived[0]
    for k, peer in enumerate(peers, 1):
        step = remote(held.at[k - 1], arrived.at[k], send_sem.at[k], recv_sem.at[k], peer)
        step.start()
        step.wait()
        held[k] = held[k - 1] + arrived[k]
    copies = [
        remote(held.at[bits - 1], from_z.at[j], z_send.at[j], z_recv.at[j], peer)
        for j, peer in enumerate(others)
    ]
    for copy in copies:
        copy.start()
    for copy in copies:
        copy.wait()
    total = jnp.zeros_like(held[0])
    for owner in range(n_z):
        term = held[bits - 1]
        for j in range(1, n_z):
            term = jnp.where(lax.rem(z - j + n_z, n_z) == owner, from_z[j - 1], term)
        total = total + term
    held[bits] = total
    last = remote(held.at[bits], arrived.at[bits], send_sem.at[bits], recv_sem.at[bits], core)
    last.start()
    out_ref[side] = total
    last.wait()
    out_ref[1 - side] = arrived[bits]


def sum_everywhere(vector, collective_id):
    n_z = lax.axis_size("gx")
    bits = lax.axis_size("gy").bit_length() - 1
    lanes = 128
    length = vector.shape[0]
    rows = -(-length // (lanes * 16)) * 8
    padded = jnp.pad(vector, (0, 2 * rows * lanes - length)).reshape(2, rows, lanes)
    dma = pltpu.SemaphoreType.DMA
    out = pl.pallas_call(
        partial(sum_kernel, n_z, bits),
        out_shape=jax.ShapeDtypeStruct((2, rows, lanes), jnp.float32),
        in_specs=[pl.BlockSpec(memory_space=pltpu.VMEM)],
        out_specs=pl.BlockSpec(memory_space=pltpu.VMEM),
        scratch_shapes=[
            pltpu.VMEM((bits + 1, rows, lanes), jnp.float32),
            pltpu.VMEM((bits + 1, rows, lanes), jnp.float32),
            pltpu.VMEM((n_z - 1, rows, lanes), jnp.float32),
            dma((bits + 1,)),
            dma((n_z - 1,)),
            dma((bits + 1,)),
            dma((n_z - 1,)),
        ],
        compiler_params=pltpu.CompilerParams(collective_id=collective_id, has_side_effects=True),
        name="sum_everywhere",
    )(padded)
    return out.reshape(-1)[:length]


def enter_kernel(
    n_z,
    span,
    acts_ref,
    weight_ref,
    seq_ref,
    full_ref,
    send_sem,
    recv_sem,
    local_sem,
    chain_send,
    chain_recv,
    chain_local,
):
    chain = chain_gather(n_z, weight_ref, full_ref, chain_send, chain_recv, chain_local)
    gather_kernel(1, span, acts_ref, seq_ref, send_sem, recv_sem, local_sem, chain)


def enter(acts, weights, collective_id):
    n_z = lax.axis_size("gx")
    span = lax.axis_size("gy")
    rows, cols = acts.shape
    dma = pltpu.SemaphoreType.DMA
    seq, full = pl.pallas_call(
        partial(enter_kernel, n_z, span),
        out_shape=(
            jax.ShapeDtypeStruct((span, 2, rows // 2, cols), acts.dtype),
            jax.ShapeDtypeStruct((n_z,) + weights.shape, weights.dtype),
        ),
        in_specs=[pl.BlockSpec(memory_space=pltpu.VMEM)] * 2,
        out_specs=(pl.BlockSpec(memory_space=pl.ANY),) * 2,
        scratch_shapes=[
            dma((24,)),
            dma((span, 2)),
            dma,
            dma((2 * n_z,)),
            dma((n_z,)),
            dma,
        ],
        compiler_params=pltpu.CompilerParams(collective_id=collective_id, has_side_effects=True),
        name="enter",
    )(acts.reshape(2, rows // 2, cols), weights)
    return seq.reshape(span * rows, cols), full.reshape(n_z * weights.shape[0], weights.shape[1])


def chain_scatter(n_z, part_ref, out_ref, from_low, from_high, send_sem, low_recv, high_recv):
    z = lax.axis_index("gx")
    g = lax.axis_index("gy")
    rows = part_ref.shape[1]

    def up(dest):
        return pltpu.make_async_remote_copy(
            src_ref=part_ref.at[dest],
            dst_ref=from_low.at[dest],
            send_sem=send_sem.at[dest],
            recv_sem=low_recv.at[dest],
            device_id={"gx": z + 1, "gy": g},
            device_id_type=pl.DeviceIdType.MESH,
        )

    def down(dest):
        return pltpu.make_async_remote_copy(
            src_ref=part_ref.at[dest],
            dst_ref=from_high.at[dest],
            send_sem=send_sem.at[dest],
            recv_sem=high_recv.at[dest],
            device_id={"gx": z - 1, "gy": g},
            device_id_type=pl.DeviceIdType.MESH,
        )

    def start():
        for k in range(n_z - 1):
            run_if(z == 0, lambda k=k: up(n_z - 1 - k).start())
            run_if(z == n_z - 1, lambda k=k: down(k).start())

    def pass_up(dest):
        up(dest).wait_recv()
        add_into(part_ref.at[dest], (part_ref.at[dest], from_low.at[dest]), rows)
        up(dest).start()

    def pass_down(dest):
        down(dest).wait_recv()
        add_into(part_ref.at[dest], (part_ref.at[dest], from_high.at[dest]), rows)
        down(dest).start()

    def relay(time):
        for k in range(time):
            low, dest = time - k, n_z - 1 - k
            if 0 < low < dest:
                run_if(z == low, partial(pass_up, dest))
            high, dest = n_z - 1 - (time - k), k
            if dest < high < n_z - 1:
                run_if(z == high, partial(pass_down, dest))

    def finish():
        for dest in range(n_z):
            terms = [part_ref.at[dest]]
            terms += [from_low.at[dest]] if dest > 0 else []
            terms += [from_high.at[dest]] if dest < n_z - 1 else []

            def last(dest=dest, terms=terms):
                if dest > 0:
                    up(dest).wait_recv()
                if dest < n_z - 1:
                    down(dest).wait_recv()
                add_into(out_ref, terms, rows)

            run_if(z == dest, last)
        for dest in range(n_z):
            run_if(z != dest, lambda dest=dest: up(dest).wait_send())

    return start, [partial(relay, time) for time in range(1, n_z)], finish


def leave_kernel(
    n_i,
    rows,
    part_ref,
    weight_ref,
    out_ref,
    weight_out,
    held,
    from_core,
    from_a,
    from_b,
    from_z,
    sums,
    from_low,
    from_high,
    load_sem,
    core_send,
    a_send,
    b_send,
    z_send,
    core_recv,
    a_recv,
    b_recv,
    z_recv,
    copy_sem,
    chain_send,
    low_recv,
    high_recv,
):
    n_z = lax.axis_size("gx")
    copy = pltpu.make_async_copy(weight_ref, sums, copy_sem)
    copy.start()
    chain = chain_scatter(
        n_z, sums, weight_out, from_low, from_high, chain_send, low_recv, high_recv
    )

    def start():
        copy.wait()
        chain[0]()

    scatter_kernel(
        False,
        n_i,
        rows,
        part_ref,
        out_ref,
        held,
        from_core,
        from_a,
        from_b,
        from_z,
        load_sem,
        core_send,
        a_send,
        b_send,
        z_send,
        core_recv,
        a_recv,
        b_recv,
        z_recv,
        (start, chain[1], chain[2]),
    )


def leave(part, weight_part, collective_id, pieces=4):
    n_z = lax.axis_size("gx")
    span = lax.axis_size("gy")
    total, cols = part.shape
    rows = total // span // (2 * pieces)
    shaped = part.reshape(span, pieces, 2, rows, cols).swapaxes(0, 1)
    half = (rows, cols)
    dma = pltpu.SemaphoreType.DMA
    block = (weight_part.shape[0] // n_z, weight_part.shape[1])
    out, sums = pl.pallas_call(
        partial(leave_kernel, pieces, rows),
        out_shape=(
            jax.ShapeDtypeStruct((pieces, 2, rows, cols), jnp.float32),
            jax.ShapeDtypeStruct(block, jnp.float32),
        ),
        in_specs=[pl.BlockSpec(memory_space=pl.ANY)] * 2,
        out_specs=(pl.BlockSpec(memory_space=pltpu.VMEM),) * 2,
        scratch_shapes=[
            pltpu.VMEM((pieces, 4, 2) + half, jnp.bfloat16),
            pltpu.VMEM((pieces, 4, 2) + half, jnp.bfloat16),
            pltpu.VMEM((pieces, 2, 2) + half, jnp.bfloat16),
            pltpu.VMEM((pieces, 2) + half, jnp.bfloat16),
            pltpu.VMEM((1, 2, 16, 128), jnp.bfloat16),
            pltpu.VMEM((n_z,) + block, jnp.bfloat16),
            pltpu.VMEM((n_z,) + block, jnp.bfloat16),
            pltpu.VMEM((n_z,) + block, jnp.bfloat16),
            dma((pieces, 4)),
            dma((pieces, 4)),
            dma((pieces, 4)),
            dma((pieces, 2)),
            dma((pieces,)),
            dma((pieces, 4)),
            dma((pieces, 2, 2)),
            dma((pieces, 2)),
            dma((pieces,)),
            dma,
            dma((n_z,)),
            dma((n_z,)),
            dma((n_z,)),
        ],
        compiler_params=pltpu.CompilerParams(
            collective_id=collective_id, has_side_effects=True, vmem_limit_bytes=60 << 20
        ),
        name="leave",
    )(shaped, weight_part.reshape((n_z,) + block))
    return out.reshape(total // span, cols), sums


def gather_plane(block, collective_id):
    if lax.axis_size("gy") == 8:
        return all_gather(block, False, collective_id)
    return lax.all_gather(block, "gy", axis=0, tiled=True)


def gather_inputs(acts, weights):
    if lax.axis_size("gy") == 8:
        return enter(acts, weights, 6)
    return (
        lax.all_gather(acts, "gy", axis=0, tiled=True),
        lax.all_gather(weights, "gx", axis=0, tiled=True),
    )


def scatter_grads(acts_part, weight_part):
    if lax.axis_size("gy") == 8:
        return leave(acts_part, weight_part, 7)
    return (
        lax.psum_scatter(acts_part, "gy", scatter_dimension=0, tiled=True).astype(jnp.float32),
        lax.psum_scatter(weight_part, "gx", scatter_dimension=0, tiled=True).astype(jnp.float32),
    )


def scatter_plane(part, collective_id):
    if lax.axis_size("gy") == 8:
        return reduce_scatter(part, False, collective_id)
    return lax.psum_scatter(part, "gy", scatter_dimension=0, tiled=True).astype(jnp.float32)


def norm_rows(values, gain_row):
    return (
        values * lax.rsqrt(jnp.mean(values * values, axis=-1, keepdims=True) + EPSILON) * gain_row
    )


def rotary(values):
    length = values.shape[0]
    halfway = values.shape[-1] // 2
    positions = jnp.arange(length, dtype=jnp.float32)
    frequency = jnp.exp(
        jnp.arange(halfway, dtype=jnp.float32) * (-2.0 * jnp.log(10000.0) / values.shape[-1])
    )
    angles = (positions[:, None] * frequency[None, :])[:, None, :]
    cosine = jnp.cos(angles)
    sine_table = jnp.sin(angles)
    first_half = values[..., :halfway]
    second = values[..., halfway:]
    return jnp.concatenate(
        [first_half * cosine - second * sine_table, second * cosine + first_half * sine_table],
        axis=-1,
    )


def prepare_heads(raw_heads, gain_row):
    return rotary(norm_rows(raw_heads, gain_row))


def route_gates(id_table, logits):
    shares = jax.nn.softmax(logits, axis=-1)
    experts = logits.shape[-1]
    matches = id_table[:, :, None] == jnp.arange(experts, dtype=jnp.int32)[None, None, :]
    chosen = jnp.sum(jnp.where(matches, shares[:, None, :], 0.0), axis=-1)
    return chosen / jnp.sum(chosen, axis=-1, keepdims=True)


def contract_rows(left_side, right_side):
    return lax.dot_general(
        left_side, right_side, (((0,), (0,)), ((), ())), preferred_element_type=jnp.float32
    )


def contract_cols(left_side, right_side):
    return lax.dot_general(
        left_side, right_side, (((1,), (1,)), ((), ())), preferred_element_type=jnp.float32
    )


def routed_experts(
    moe_in, cotangent, expert_ids, gate_share, router_weight, gate_weight, up_weight, down_weight
):
    tok_rows = moe_in.shape[0]
    experts = router_weight.shape[1]
    width_all = moe_in.shape[1]
    capacity = tok_rows * TOP * 3 // (2 * experts)
    route_count = tok_rows * TOP
    flat_ids = expert_ids.reshape(route_count)
    onehot = (flat_ids[:, None] == jnp.arange(experts, dtype=jnp.int32)[None, :]).astype(jnp.int32)
    earlier = jnp.cumsum(onehot, axis=0) - onehot
    slot_index = jnp.sum(earlier * onehot, axis=1)
    target = flat_ids * capacity + slot_index
    source = (
        jnp.full((experts * capacity,), tok_rows, jnp.int32)
        .at[target]
        .set(jnp.arange(route_count, dtype=jnp.int32) // TOP)
    )
    padded_in = jnp.concatenate([moe_in, jnp.zeros((1, width_all), jnp.bfloat16)], axis=0)
    packed = padded_in[source].reshape(experts, 1, capacity, width_all)
    outgoing = jnp.broadcast_to(packed, (experts, 2, capacity, width_all)).reshape(
        2 * experts, capacity, width_all
    )
    arrived = lax.all_to_all(outgoing, ("gx", "gy"), split_axis=0, concat_axis=1, tiled=True)[0]
    gate_in = gate_weight[0]
    up_in = up_weight[0]
    down_in = down_weight[0]
    gate_val = jnp.dot(arrived, gate_in, preferred_element_type=jnp.float32)
    up_val = jnp.dot(arrived, up_in, preferred_element_type=jnp.float32)
    hidden = (jax.nn.silu(gate_val) * up_val).astype(jnp.bfloat16)
    produced = jnp.dot(hidden, down_in, preferred_element_type=jnp.float32).astype(jnp.bfloat16)
    returned = lax.all_to_all(produced[None], ("gx", "gy"), split_axis=1, concat_axis=0, tiled=True)
    summed = (
        returned.reshape(experts, 2, capacity, width_all)
        .astype(jnp.float32)
        .sum(axis=1)
        .reshape(experts * capacity, width_all)
    )
    route_out = summed[target]
    gates_flat = gate_share.reshape(route_count)
    moe_out = jnp.sum((gates_flat[:, None] * route_out).reshape(tok_rows, TOP, width_all), axis=1)
    grad_out = cotangent.astype(jnp.float32)
    grad_gates = jnp.sum(
        route_out.reshape(tok_rows, TOP, width_all) * grad_out[:, None, :], axis=-1
    )
    slot_gate = jnp.zeros((experts * capacity,), jnp.float32).at[target].set(gates_flat)
    padded_grad = jnp.concatenate([grad_out, jnp.zeros((1, width_all), jnp.float32)], axis=0)
    grad_packed = (
        (slot_gate[:, None] * padded_grad[source])
        .astype(jnp.bfloat16)
        .reshape(experts, 1, capacity, width_all)
    )
    grad_outgoing = jnp.broadcast_to(grad_packed, (experts, 2, capacity, width_all)).reshape(
        2 * experts, capacity, width_all
    )
    grad_arrived = lax.all_to_all(
        grad_outgoing, ("gx", "gy"), split_axis=0, concat_axis=1, tiled=True
    )[0]
    rows_in, grad_use = (arrived, grad_arrived)
    gate_use, up_use, hidden_use = (gate_val, up_val, hidden)
    sigmoid_gate = jax.nn.sigmoid(gate_use)
    silu_gate = gate_use * sigmoid_gate
    grad_hidden = contract_cols(grad_use, down_in)
    down_part = contract_rows(hidden_use, grad_use)
    grad_gate = (
        grad_hidden * up_use * sigmoid_gate * (1.0 + gate_use * (1.0 - sigmoid_gate))
    ).astype(jnp.bfloat16)
    grad_up = (grad_hidden * silu_gate).astype(jnp.bfloat16)
    gate_part = contract_rows(rows_in, grad_gate)
    up_part = contract_rows(rows_in, grad_up)
    grad_in = contract_cols(grad_gate, gate_in) + contract_cols(grad_up, up_in)
    grad_back = lax.all_to_all(
        grad_in.astype(jnp.bfloat16)[None], ("gx", "gy"), split_axis=1, concat_axis=0, tiled=True
    )
    grad_summed = (
        grad_back.reshape(experts, 2, capacity, width_all)
        .astype(jnp.float32)
        .sum(axis=1)
        .reshape(experts * capacity, width_all)
    )
    grad_moe_in = jnp.sum(grad_summed[target].reshape(tok_rows, TOP, width_all), axis=1)
    return moe_out, grad_gates, grad_moe_in, gate_part, up_part, down_part


def dense_experts(
    moe_in, cotangent, expert_ids, gate_share, router_weight, gate_weight, up_weight, down_weight
):
    experts = router_weight.shape[1]
    everyone = ("gx", "gy")
    all_cot = lax.all_gather(cotangent, everyone, axis=0, tiled=True)
    matches = expert_ids[:, :, None] == jnp.arange(experts, dtype=jnp.int32)[None, None, :]
    dense_gates = jnp.sum(jnp.where(matches, gate_share[:, :, None], 0.0), axis=1)
    own_gate = lax.all_to_all(
        jnp.repeat(dense_gates.T, 2, axis=0), everyone, split_axis=0, concat_axis=0, tiled=True
    ).reshape(-1)
    all_moe = all_gather(moe_in, True, 2)
    gate_in = gate_weight[0]
    up_in = up_weight[0]
    down_in = down_weight[0]
    gate_val = jnp.dot(all_moe, gate_in, preferred_element_type=jnp.float32)
    up_val = jnp.dot(all_moe, up_in, preferred_element_type=jnp.float32)
    sigmoid_gate = jax.nn.sigmoid(gate_val)
    silu_gate = gate_val * sigmoid_gate
    hidden = (silu_gate * up_val).astype(jnp.bfloat16)
    piece = jnp.dot(hidden, down_in, preferred_element_type=jnp.float32)
    cot_float = all_cot.astype(jnp.float32)
    gate_dots = jnp.sum(piece * cot_float, axis=-1)
    devices = lax.axis_size("gx") * lax.axis_size("gy")
    dots_back = lax.all_to_all(
        gate_dots.reshape(devices, -1), everyone, split_axis=0, concat_axis=0, tiled=True
    )
    dots_experts = dots_back.reshape(experts, 2, -1).sum(axis=1).T
    grad_gates = jnp.sum(jnp.where(matches, dots_experts[:, None, :], 0.0), axis=-1)
    moe_out = lax.psum_scatter(
        (piece * own_gate[:, None]).astype(jnp.bfloat16), everyone, scatter_dimension=0, tiled=True
    ).astype(jnp.float32)
    grad_use = (cot_float * own_gate[:, None]).astype(jnp.bfloat16)
    grad_hidden = contract_cols(grad_use, down_in)
    down_part = contract_rows(hidden, grad_use)
    grad_gate = (
        grad_hidden * up_val * sigmoid_gate * (1.0 + gate_val * (1.0 - sigmoid_gate))
    ).astype(jnp.bfloat16)
    grad_up = (grad_hidden * silu_gate).astype(jnp.bfloat16)
    gate_part = contract_rows(all_moe, grad_gate)
    up_part = contract_rows(all_moe, grad_up)
    grad_in = contract_cols(grad_gate, gate_in) + contract_cols(grad_up, up_in)
    grad_moe_in = reduce_scatter(grad_in.astype(jnp.bfloat16), True, 4)
    return moe_out, grad_gates, grad_moe_in, gate_part, up_part, down_part


def local(
    tokens,
    cotangent,
    expert_ids,
    doc_ids,
    clip_rank,
    attn_gain,
    moe_gain,
    query_gain,
    key_gain,
    query_weight,
    key_weight,
    value_weight,
    out_weight,
    router_weight,
    gate_weight,
    up_weight,
    down_weight,
):
    inputs = tokens.astype(jnp.float32)
    acts_float, norm_pull = jax.vjp(norm_rows, inputs, attn_gain)
    acts_low = acts_float.astype(jnp.bfloat16)
    in_weights = jnp.concatenate([query_weight, key_weight, value_weight], axis=1)
    seq_acts, full_in = gather_inputs(acts_low, in_weights)
    seq_acts, full_in, out_weight = lax.optimization_barrier((seq_acts, full_in, out_weight))
    out_rows = lax.all_gather(out_weight, "gx", axis=1, tiled=True)
    out_rows, later_cot = lax.optimization_barrier((out_rows, cotangent))
    length = seq_acts.shape[0]
    local_width = query_weight.shape[1]
    local_heads = local_width // HD
    projected = jnp.dot(seq_acts, full_in, preferred_element_type=jnp.float32)
    queries = projected[:, :local_width]
    key_raw = projected[:, local_width : 2 * local_width]
    value_ready = (
        projected[:, 2 * local_width :].astype(jnp.bfloat16).reshape(length, local_heads, HD)
    )
    query_float, query_pull = jax.vjp(
        prepare_heads, queries.reshape(length, local_heads, HD), query_gain
    )
    key_float, key_pull = jax.vjp(prepare_heads, key_raw.reshape(length, local_heads, HD), key_gain)
    query_ready = query_float.astype(jnp.bfloat16)
    key_ready = key_float.astype(jnp.bfloat16)
    block_rows = min(512, length)
    block_count = length // block_rows
    score_scale = HD ** (-0.5)
    query_blocks = query_ready.reshape(block_count, block_rows, local_heads, HD)
    doc_blocks = doc_ids.reshape(block_count, block_rows)

    def block_scores(query_block, doc_block):
        scores = (
            jnp.einsum("qhd,khd->hqk", query_block, key_ready, preferred_element_type=jnp.float32)
            * score_scale
        )
        same_doc = doc_block[:, None] == doc_ids[None, :]
        return jnp.where(same_doc[None], scores, NEGATIVE)

    def forward_block(pieces):
        scores = block_scores(pieces[0], pieces[1])
        highest = jnp.max(scores, axis=-1, keepdims=True)
        weights = jnp.exp(scores - highest)
        totals = jnp.sum(weights, axis=-1, keepdims=True)
        shares = (weights / totals).astype(jnp.bfloat16)
        mixed_heads = jnp.einsum(
            "hqk,khd->qhd", shares, value_ready, preferred_element_type=jnp.float32
        )
        return (
            mixed_heads.astype(jnp.bfloat16),
            highest[..., 0] + jnp.log(totals[..., 0]),
            jnp.max(highest[..., 0], axis=-1),
        )

    mixed_blocks, log_totals, peak_blocks = lax.map(forward_block, (query_blocks, doc_blocks))
    mixed_seq = mixed_blocks.reshape(length, local_width)
    start_head = lax.axis_index("gy") * local_heads
    peak_slots = lax.dynamic_update_slice(
        jnp.zeros((lax.axis_size("gx"), NH), jnp.float32),
        jnp.max(peak_blocks, axis=0)[None],
        (lax.axis_index("gx"), start_head),
    )
    attended = scatter_plane(
        jnp.dot(mixed_seq, out_rows, preferred_element_type=jnp.float32).astype(jnp.bfloat16), 3
    )
    residual = inputs + attended
    moe_float, moe_pull = jax.vjp(norm_rows, residual, moe_gain)
    moe_in = moe_float.astype(jnp.bfloat16)
    logits = jnp.dot(moe_in, router_weight, preferred_element_type=jnp.float32)
    gate_share, gate_pull = jax.vjp(partial(route_gates, expert_ids), logits)
    experts_pass = dense_experts if lax.axis_size("gy") == 8 and router_weight.shape[1] <= 2 * TOP else routed_experts
    moe_out, grad_gates, grad_moe_in, gate_part, up_part, down_part = experts_pass(
        moe_in,
        later_cot,
        expert_ids,
        gate_share,
        router_weight,
        gate_weight,
        up_weight,
        down_weight,
    )
    output = (residual + moe_out).astype(jnp.bfloat16)
    grad_out = cotangent.astype(jnp.float32)
    (grad_logits,) = gate_pull(grad_gates)
    grad_logits_low = grad_logits.astype(jnp.bfloat16)
    router_part = contract_rows(moe_in, grad_logits_low)
    grad_moe_in = grad_moe_in + contract_cols(grad_logits_low, router_weight)
    grad_resid_norm, moe_gain_part = moe_pull(grad_moe_in)
    grad_resid = grad_out + grad_resid_norm
    seq_grad = gather_plane(grad_resid.astype(jnp.bfloat16), 1)
    grad_mixed = contract_cols(seq_grad, out_rows).astype(jnp.bfloat16)
    out_part = contract_rows(seq_grad, mixed_seq)

    def backward_block(running, pieces):
        grad_key, grad_value = running
        query_block, grad_block, log_block, doc_block = pieces
        scores = block_scores(query_block, doc_block)
        weights = jnp.exp(scores - log_block[..., None])
        grad_value = grad_value + jnp.einsum(
            "hqk,qhd->khd",
            weights.astype(jnp.bfloat16),
            grad_block,
            preferred_element_type=jnp.float32,
        )
        grad_weights = jnp.einsum(
            "qhd,khd->hqk", grad_block, value_ready, preferred_element_type=jnp.float32
        )
        inner_sum = jnp.sum(weights * grad_weights, axis=-1, keepdims=True)
        grad_scores = (weights * (grad_weights - inner_sum)).astype(jnp.bfloat16)
        grad_query = (
            jnp.einsum("hqk,khd->qhd", grad_scores, key_ready, preferred_element_type=jnp.float32)
            * score_scale
        )
        grad_key = (
            grad_key
            + jnp.einsum(
                "hqk,qhd->khd", grad_scores, query_block, preferred_element_type=jnp.float32
            )
            * score_scale
        )
        return ((grad_key, grad_value), grad_query)

    empty_heads = jnp.zeros((length, local_heads, HD), jnp.float32)
    grad_mixed_blocks = grad_mixed.reshape(block_count, block_rows, local_heads, HD)
    (key_grad_heads, value_grad_heads), query_grad_blocks = lax.scan(
        backward_block,
        (empty_heads, empty_heads),
        (query_blocks, grad_mixed_blocks, log_totals, doc_blocks),
    )
    query_raw_grad, query_gain_part = query_pull(query_grad_blocks.reshape(length, local_heads, HD))
    key_raw_grad, key_gain_part = key_pull(key_grad_heads)
    grad_queries = query_raw_grad.reshape(length, local_width).astype(jnp.bfloat16)
    grad_keys = key_raw_grad.reshape(length, local_width).astype(jnp.bfloat16)
    grad_values = value_grad_heads.reshape(length, local_width).astype(jnp.bfloat16)
    grad_heads = jnp.concatenate([grad_queries, grad_keys, grad_values], axis=1)
    grad_acts, in_sum = scatter_grads(
        contract_cols(grad_heads, full_in).astype(jnp.bfloat16),
        contract_rows(seq_acts, grad_heads).astype(jnp.bfloat16),
    )
    query_sum = in_sum[:, :local_width]
    key_sum = in_sum[:, local_width : 2 * local_width]
    value_sum = in_sum[:, 2 * local_width :]
    out_sum_rows = lax.psum_scatter(
        out_part.astype(jnp.bfloat16), "gx", scatter_dimension=0, tiled=True
    ).astype(jnp.float32)
    norm_input_grad, attn_gain_part = norm_pull(grad_acts)
    input_grad = grad_resid + norm_input_grad
    small = (
        attn_gain_part,
        moe_gain_part,
        query_gain_part,
        key_gain_part,
        router_part.T,
        peak_slots,
    )
    summed = sum_everywhere(jnp.concatenate([part.reshape(-1) for part in small]), 5)
    ends = list(accumulate(part.size for part in small))
    attn_gain_grad, moe_gain_grad, query_gain_grad, key_gain_grad, router_flat, peaks = (
        summed[end - part.size : end].reshape(part.shape) for end, part in zip(ends, small)
    )
    router_grad = router_flat.T
    peak_global = jnp.max(peaks, axis=0)
    ranked = -jnp.sort(-peak_global)
    limit = jnp.sum(jnp.where(jnp.arange(NH, dtype=jnp.int32) == clip_rank[0], ranked, 0.0))
    factors = jnp.where(peak_global > limit, limit / peak_global, 1.0)
    own_factors = lax.dynamic_slice_in_dim(factors, start_head, local_heads)
    columns = jnp.repeat(jnp.sqrt(own_factors), HD)
    query_clipped = (query_weight.astype(jnp.float32) * columns[None, :]).astype(jnp.bfloat16)
    key_clipped = (key_weight.astype(jnp.float32) * columns[None, :]).astype(jnp.bfloat16)
    return (
        output,
        input_grad,
        attn_gain_grad,
        moe_gain_grad,
        query_gain_grad,
        key_gain_grad,
        query_sum,
        key_sum,
        value_sum,
        out_sum_rows.T,
        router_grad,
        gate_part[None],
        up_part[None],
        down_part[None],
        query_clipped,
        key_clipped,
        factors,
    )


def solution(mesh):
    placed = (
        P(("gx", "gy"), None),
        P(("gx", "gy"), None),
        P(("gx", "gy"), None),
        P("gx"),
        P(),
        P(),
        P(),
        P(),
        P(),
        P("gx", "gy"),
        P("gx", "gy"),
        P("gx", "gy"),
        P("gy", "gx"),
        P(),
        P(("gx", "gy"), None, None),
        P(("gx", "gy"), None, None),
        P(("gx", "gy"), None, None),
    )
    return jax.shard_map(
        local,
        mesh=mesh,
        in_specs=placed,
        out_specs=(
            P(("gx", "gy"), None),
            P(("gx", "gy"), None),
            P(),
            P(),
            P(),
            P(),
            P("gx", "gy"),
            P("gx", "gy"),
            P("gx", "gy"),
            P("gy", "gx"),
            P(),
            P(("gx", "gy"), None, None),
            P(("gx", "gy"), None, None),
            P(("gx", "gy"), None, None),
            P("gx", "gy"),
            P("gx", "gy"),
            P(),
        ),
        check_vma=False,
    )
```

```python
from functools import partial
from itertools import accumulate

import jax
import jax.numpy as jnp
from jax import lax
from jax.experimental import pallas as pl
from jax.experimental.pallas import tpu as pltpu
from jax.sharding import PartitionSpec as P

NH = 16
HD = 128
TOP = 8


EPSILON = 1e-06
NEGATIVE = -1e30


def flip(index):
    return index + 1 - 2 * (index % 2)


def barrier_with(partners):
    barrier = pltpu.get_barrier_semaphore()
    for ok, device in partners:
        @pl.when(ok)
        def _():
            pl.semaphore_signal(barrier, inc=1, device_id=device, device_id_type=pl.DeviceIdType.MESH)
    pl.semaphore_wait(barrier, sum(ok.astype(jnp.int32) for ok, _ in partners))

def always(ok, other):
    if ok is True:
        return other
    return ok if other is True else jnp.logical_and(ok, other)


def run_if(ok, action):
    if ok is True:
        action()
    else:
        pl.when(ok)(action)


def chain_gather(n_z, own_ref, out_ref, send_sem, recv_sem, local_sem):
    z = lax.axis_index("gx")
    g = lax.axis_index("gy")

    def hop(source, owner, k, peer):
        return pltpu.make_async_remote_copy(
            src_ref=source,
            dst_ref=out_ref.at[owner],
            send_sem=send_sem.at[k],
            recv_sem=recv_sem.at[owner],
            device_id={"gx": peer, "gy": g},
            device_id_type=pl.DeviceIdType.MESH,
        )

    local = pltpu.make_async_copy(own_ref, out_ref.at[z], local_sem)
    upward = [(z < n_z - 1, lambda: hop(own_ref, z, 0, z + 1))]
    downward = [(z > 0, lambda: hop(own_ref, z, n_z, z - 1))]
    for d in range(1, n_z - 1):
        upward.append(
            (
                jnp.logical_and(z >= d, z < n_z - 1),
                lambda d=d: hop(out_ref.at[z - d], z - d, d, z + 1),
            )
        )
        downward.append(
            (
                jnp.logical_and(z < n_z - d, z > 0),
                lambda d=d: hop(out_ref.at[z + d], z + d, n_z + d, z - 1),
            )
        )

    def start():
        local.start()
        for ok, copy in (upward[0], downward[0]):
            run_if(ok, lambda copy=copy: copy().start())

    def relay(d):
        run_if(z >= d, lambda: hop(own_ref, z - d, 0, z).wait_recv())
        if d < n_z - 1:
            run_if(upward[d][0], lambda: upward[d][1]().start())
        run_if(z < n_z - d, lambda: hop(own_ref, z + d, 0, z).wait_recv())
        if d < n_z - 1:
            run_if(downward[d][0], lambda: downward[d][1]().start())

    def finish():
        local.wait()
        for ok, copy in upward + downward:
            run_if(ok, lambda copy=copy: copy().wait_send())

    return start, [partial(relay, d) for d in range(1, n_z)], finish


def gather_steps(n_z, span, own_ref, out_ref, send_sem, recv_sem, local_sem):
    z = lax.axis_index("gx")
    g = lax.axis_index("gy")
    flip_x = g + 2 - 4 * ((g // 2) % 2)
    flip_y = g + 4 - 8 * ((g // 4) % 2)
    flip_both = flip_x + flip_y - g
    core = {"gx": z, "gy": flip(g)}
    x_peer = {"gx": z, "gy": flip_x}
    y_peer = {"gx": z, "gy": flip_y}
    above = {"gx": z + 1, "gy": g}
    below = {"gx": z - 1, "gy": g}
    first_z = z if n_z > 1 else 0
    sends = []

    def send(ok, source, b, h, peer):
        k = len(sends)

        def make():
            return pltpu.make_async_remote_copy(
                src_ref=source,
                dst_ref=out_ref.at[b, h],
                send_sem=send_sem.at[k],
                recv_sem=recv_sem.at[b, h],
                device_id=peer,
                device_id_type=pl.DeviceIdType.MESH,
            )

        sends.append((ok, make))
        run_if(ok, lambda: make().start())

    def arrive(ok, b, h):
        def wait():
            pltpu.make_async_remote_copy(
                src_ref=out_ref.at[b, h],
                dst_ref=out_ref.at[b, h],
                send_sem=send_sem.at[0],
                recv_sem=recv_sem.at[b, h],
                device_id=core,
                device_id_type=pl.DeviceIdType.MESH,
            ).wait_recv()

        run_if(ok, wait)

    local = pltpu.make_async_copy(own_ref, out_ref.at[first_z * span + g], local_sem)
    items = [(True, first_z, 0)]
    for d in range(1, n_z):
        items += [(z >= d, z - d, -d), (z < n_z - d, z + d, d)]

    def first(item):
        ok, owner, d = item
        b = owner * span + g
        if d == 0:
            local.start()
            source = own_ref
        else:
            arrive(ok, b, 0)
            arrive(ok, b, 1)
            source = out_ref.at[b]
        for h in range(2):
            if n_z > 1 and d <= 0:
                send(always(ok, z < n_z - 1), source.at[h], b, h, above)
            if n_z > 1 and d >= 0:
                send(always(ok, z > 0), source.at[h], b, h, below)
        send(ok, source.at[0], b, 0, x_peer)
        send(ok, source.at[1], b, 1, y_peer)
        send(ok, source.at[1], b, 1, x_peer)
        send(ok, source.at[0], b, 0, y_peer)
        send(ok, source.at[0], b, 0, core)
        send(ok, source.at[1], b, 1, core)

    def second(item):
        ok, owner, _ = item
        for side, h, peer in ((flip_x, 0, y_peer), (flip_y, 1, x_peer)):
            b = owner * span + side
            arrive(ok, b, h)
            send(ok, out_ref.at[b, h], b, h, peer)
            send(ok, out_ref.at[b, h], b, h, core)

    def third(item):
        ok, owner, _ = item
        for side, h in ((flip_both, 0), (flip_both, 1), (flip_y, 0), (flip_x, 1)):
            b = owner * span + side
            arrive(ok, b, h)
            send(ok, out_ref.at[b, h], b, h, core)

    n = len(items)

    def step(i):
        if i < n:
            first(items[i])
        if 1 <= i <= n:
            second(items[i - 1])
        if i >= 2:
            third(items[i - 2])

    def finish():
        for ok, owner, _ in items:
            for side in (g, flip_x, flip_y, flip_both):
                for h in range(2):
                    arrive(ok, owner * span + flip(side), h)
        local.wait()
        for ok, make in sends:
            run_if(ok, lambda make=make: make().wait_send())

    return [partial(step, i) for i in range(n + 2)], finish


def greet(n_z):
    z = lax.axis_index("gx")
    g = lax.axis_index("gy")
    peers = [
        (z >= 0, {"gx": z, "gy": g + bit - 2 * bit * ((g // bit) % 2)}) for bit in (1, 2, 4)
    ]
    if n_z > 1:
        peers += [(z < n_z - 1, {"gx": z + 1, "gy": g}), (z > 0, {"gx": z - 1, "gy": g})]
    barrier_with(peers)


def gather_kernel(n_z, span, own_ref, out_ref, send_sem, recv_sem, local_sem):
    greet(n_z)
    steps, finish = gather_steps(n_z, span, own_ref, out_ref, send_sem, recv_sem, local_sem)
    for step in steps:
        step()
    finish()


def all_gather(block, both, collective_id):
    n_z = lax.axis_size("gx") if both else 1
    span = lax.axis_size("gy")
    rows, cols = block.shape
    own = block.reshape(2, rows // 2, cols)
    n_sends = (2 * n_z - 1) * 24
    out = pl.pallas_call(
        partial(gather_kernel, n_z, span),
        out_shape=jax.ShapeDtypeStruct((n_z * span, 2, rows // 2, cols), block.dtype),
        in_specs=[pl.BlockSpec(memory_space=pltpu.VMEM)],
        out_specs=pl.BlockSpec(memory_space=pl.ANY),
        scratch_shapes=[pltpu.SemaphoreType.DMA((n_sends,)), pltpu.SemaphoreType.DMA((n_z * span, 2)), pltpu.SemaphoreType.DMA],
        compiler_params=pltpu.CompilerParams(collective_id=collective_id, has_side_effects=True),
        name="gather_all" if both else "gather_plane",
    )(own)
    return out.reshape(n_z * span * rows, cols)


def add_into(dst, parts, rows):
    step = min(rows, 32)

    @pl.loop(0, rows // step)
    def _(r):
        at = pl.ds(pl.multiple_of(r * step, step), step)
        if len(parts) == 2 and dst.dtype == jnp.bfloat16:
            dst[at, :] = parts[0][at, :] + parts[1][at, :]
        else:
            total = parts[0][at, :].astype(jnp.float32)
            for term in parts[1:]:
                total = total + term[at, :].astype(jnp.float32)
            dst[at, :] = total.astype(dst.dtype)


def scatter_kernel(chain, n_i, rows, part_ref, out_ref, held, from_core, from_a, from_b, from_z,
                   load_sem, core_send, a_send, b_send, z_send, core_recv, a_recv, b_recv, z_recv, beside=None):
    z = lax.axis_index("gx"); g = lax.axis_index("gy")
    flip_x = g + 2 - 4 * ((g // 2) % 2)
    flip_y = g + 4 - 8 * ((g // 4) % 2)
    quads = (flip_x + flip_y - g, flip_x, flip_y, g)
    core = {"gx": z, "gy": flip(g)}
    xn = {"gx": z, "gy": flip_x}
    yn = {"gx": z, "gy": flip_y}
    every = z >= 0
    partners = [(every, core), (every, xn), (every, yn)]
    if chain:
        partners += [(every, {"gx": lax.rem(z + j, n_i), "gy": g}) for j in range(1, n_i)]
    if beside:
        n_z = lax.axis_size("gx")
        partners += [(z < n_z - 1, {"gx": z + 1, "gy": g}), (z > 0, {"gx": z - 1, "gy": g})]
    barrier_with(partners)
    if beside:
        beside[0]()
    mesh_id = pl.DeviceIdType.MESH

    def item(i):
        return lax.rem(z + n_i - 1 - i + n_i, n_i) if chain else i

    def block(it, gg):
        return part_ref.at[it, gg]

    def remote(src, dst, ssem, rsem, dev):
        return pltpu.make_async_remote_copy(src_ref=src, dst_ref=dst, send_sem=ssem, recv_sem=rsem, device_id=dev, device_id_type=mesh_id)

    def core_copy(i, q):
        it = item(i)
        return remote(block(it, flip(quads[q])), from_core.at[it, q], core_send.at[i, q], core_recv.at[it, q], core)

    def load(i, q):
        it = item(i)
        return pltpu.make_async_copy(block(it, quads[q]), held.at[it, q], load_sem.at[i, q])

    a_plan = ((0, 0, 0, xn), (0, 1, 0, yn), (1, 0, 1, xn), (2, 1, 1, yn))
    def a_copy(i, k):
        it = item(i)
        q, h, slot, dev = a_plan[k]
        return remote(held.at[it, q, h], from_a.at[it, h, slot], a_send.at[i, k], a_recv.at[it, h, slot], dev)

    b_plan = ((2, 0, yn), (1, 1, xn))
    def b_copy(i, h):
        it = item(i)
        q, _, dev = b_plan[h]
        return remote(held.at[it, q, h], from_b.at[it, h], b_send.at[i, h], b_recv.at[it, h], dev)

    def z_copy(i):
        it = item(i)
        return remote(held.at[it, 3], from_z.at[z], z_send.at[i], z_recv.at[z], {"gx": it, "gy": g})

    def z_arrival(i):
        it = item(i)
        return remote(held.at[it, 3], from_z.at[it], z_send.at[i], z_recv.at[it], core)

    for i in range(n_i):
        for q in range(4):
            core_copy(i, q).start()
            load(i, q).start()

    def stage_a(i):
        it = item(i)
        for q in range(4):
            load(i, q).wait()
            core_copy(i, q).wait_recv()
            for h in range(2):
                add_into(held.at[it, q, h], (held.at[it, q, h], from_core.at[it, q, h]), rows)
            for k in range(4):
                if a_plan[k][0] == q:
                    a_copy(i, k).start()

    def stage_b(i):
        it = item(i)
        for q, h, slot in ((2, 0, 0), (1, 1, 0), (3, 0, 1), (3, 1, 1)):
            remote(held.at[it, q, h], from_a.at[it, h, slot], a_send.at[i, 0], a_recv.at[it, h, slot], core).wait_recv()
            add_into(held.at[it, q, h], (held.at[it, q, h], from_a.at[it, h, slot]), rows)
            if slot == 0:
                b_copy(i, h).start()

    def stage_c(i):
        it = item(i)
        for h in range(2):
            b_copy(i, h).wait_recv()
            if chain:
                add_into(held.at[it, 3, h], (held.at[it, 3, h], from_b.at[it, h]), rows)
            else:
                add_into(out_ref.at[it, h], (held.at[it, 3, h], from_b.at[it, h]), rows)

    def stage_d(i):
        if i < n_i - 1:
            z_copy(i).start()
        else:
            for j in range(n_i - 1):
                z_arrival(j).wait_recv()
            for h in range(2):
                add_into(
                    out_ref.at[h],
                    [held.at[item(i), 3, h]] + [from_z.at[item(j), h] for j in range(n_i - 1)],
                    rows,
                )

    for i in range(n_i + 2):
        if i < n_i: stage_a(i)
        if 0 <= i - 1 < n_i: stage_b(i - 1)
        if 0 <= i - 2 < n_i: stage_c(i - 2)
        if chain and 0 <= i - 2 < n_i: stage_d(i - 2)
        if beside and i == n_i:
            beside[1][0]()
    if beside:
        for relay in beside[1][1:]:
            relay()
        beside[2]()
    for i in range(n_i):
        for q in range(4): core_copy(i, q).wait_send()
        for k in range(4): a_copy(i, k).wait_send()
        for h in range(2): b_copy(i, h).wait_send()
        if chain and i < n_i - 1: z_copy(i).wait_send()


def reduce_scatter(part, both, collective_id, pieces=4, out_dtype=jnp.float32):
    n_z = lax.axis_size("gx") if both else 1
    span = lax.axis_size("gy")
    total, cols = part.shape
    n_i = n_z if both else pieces
    if both:
        rows = total // (n_z * span) // 2
        shaped = part.reshape(n_z, span, 2, rows, cols)
        out_shape = (2, rows, cols)
    else:
        rows = total // span // (2 * pieces)
        shaped = part.reshape(span, pieces, 2, rows, cols).swapaxes(0, 1)
        out_shape = (pieces, 2, rows, cols)
    dma = pltpu.SemaphoreType.DMA
    half = (rows, cols)
    z_items = n_i if both else 1
    z_half = half if both else (16, 128)
    out = pl.pallas_call(
        partial(scatter_kernel, both, n_i, rows),
        out_shape=jax.ShapeDtypeStruct(out_shape, out_dtype),
        in_specs=[pl.BlockSpec(memory_space=pl.ANY)],
        out_specs=pl.BlockSpec(memory_space=pltpu.VMEM),
        scratch_shapes=[
            pltpu.VMEM((n_i, 4, 2) + half, jnp.bfloat16),
            pltpu.VMEM((n_i, 4, 2) + half, jnp.bfloat16),
            pltpu.VMEM((n_i, 2, 2) + half, jnp.bfloat16),
            pltpu.VMEM((n_i, 2) + half, jnp.bfloat16),
            pltpu.VMEM((z_items, 2) + z_half, jnp.bfloat16),
            dma((n_i, 4)), dma((n_i, 4)), dma((n_i, 4)), dma((n_i, 2)), dma((n_i,)),
            dma((n_i, 4)), dma((n_i, 2, 2)), dma((n_i, 2)), dma((n_i,)),
        ],
        compiler_params=pltpu.CompilerParams(collective_id=collective_id, has_side_effects=True, vmem_limit_bytes=60 << 20),
        name="scatter_all" if both else "scatter_plane",
    )(shaped)
    return out.reshape(total // (n_z * span), cols)


def sum_kernel(n_z, bits, vec_ref, out_ref, held, arrived, from_z, send_sem, z_send, recv_sem, z_recv):
    z = lax.axis_index("gx")
    g = lax.axis_index("gy")
    half = vec_ref.shape[1]
    side = lax.rem(g, 2)
    core = {"gx": z, "gy": g + 1 - 2 * (g % 2)}
    peers = [
        {"gx": z, "gy": g + bit - 2 * bit * ((g // bit) % 2)}
        for bit in (2**power for power in range(1, bits))
    ]
    others = [{"gx": lax.rem(z + j, n_z), "gy": g} for j in range(1, n_z)]
    barrier_with([(z >= 0, peer) for peer in (core, *peers, *others)])

    def remote(src, dst, ssem, rsem, peer):
        return pltpu.make_async_remote_copy(
            src_ref=src,
            dst_ref=dst,
            send_sem=ssem,
            recv_sem=rsem,
            device_id=peer,
            device_id_type=pl.DeviceIdType.MESH,
        )

    first = remote(vec_ref.at[1 - side], arrived.at[0], send_sem.at[0], recv_sem.at[0], core)
    first.start()
    first.wait()
    held[0] = vec_ref[side] + arrived[0]
    for k, peer in enumerate(peers, 1):
        step = remote(held.at[k - 1], arrived.at[k], send_sem.at[k], recv_sem.at[k], peer)
        step.start()
        step.wait()
        held[k] = held[k - 1] + arrived[k]
    copies = [
        remote(held.at[bits - 1], from_z.at[j], z_send.at[j], z_recv.at[j], peer)
        for j, peer in enumerate(others)
    ]
    for copy in copies:
        copy.start()
    for copy in copies:
        copy.wait()
    total = jnp.zeros_like(held[0])
    for owner in range(n_z):
        term = held[bits - 1]
        for j in range(1, n_z):
            term = jnp.where(lax.rem(z - j + n_z, n_z) == owner, from_z[j - 1], term)
        total = total + term
    held[bits] = total
    last = remote(held.at[bits], arrived.at[bits], send_sem.at[bits], recv_sem.at[bits], core)
    last.start()
    out_ref[side] = total
    last.wait()
    out_ref[1 - side] = arrived[bits]


def sum_everywhere(vector, collective_id):
    n_z = lax.axis_size("gx")
    bits = lax.axis_size("gy").bit_length() - 1
    lanes = 128
    length = vector.shape[0]
    rows = -(-length // (lanes * 16)) * 8
    padded = jnp.pad(vector, (0, 2 * rows * lanes - length)).reshape(2, rows, lanes)
    dma = pltpu.SemaphoreType.DMA
    out = pl.pallas_call(
        partial(sum_kernel, n_z, bits),
        out_shape=jax.ShapeDtypeStruct((2, rows, lanes), jnp.float32),
        in_specs=[pl.BlockSpec(memory_space=pltpu.VMEM)],
        out_specs=pl.BlockSpec(memory_space=pltpu.VMEM),
        scratch_shapes=[
            pltpu.VMEM((bits + 1, rows, lanes), jnp.float32),
            pltpu.VMEM((bits + 1, rows, lanes), jnp.float32),
            pltpu.VMEM((n_z - 1, rows, lanes), jnp.float32),
            dma((bits + 1,)),
            dma((n_z - 1,)),
            dma((bits + 1,)),
            dma((n_z - 1,)),
        ],
        compiler_params=pltpu.CompilerParams(collective_id=collective_id, has_side_effects=True),
        name="sum_everywhere",
    )(padded)
    return out.reshape(-1)[:length]


def enter_kernel(
    n_z,
    span,
    acts_ref,
    weight_ref,
    cot_ref,
    seq_ref,
    full_ref,
    all_cot_ref,
    send_sem,
    recv_sem,
    local_sem,
    chain_send,
    chain_recv,
    chain_local,
    cot_send,
    cot_recv,
    cot_local,
):
    greet(n_z)
    start, relays, end_chain = chain_gather(
        n_z, weight_ref, full_ref, chain_send, chain_recv, chain_local
    )
    near, end_near = gather_steps(1, span, acts_ref, seq_ref, send_sem, recv_sem, local_sem)
    far, end_far = gather_steps(n_z, span, cot_ref, all_cot_ref, cot_send, cot_recv, cot_local)
    start()
    near[0]()
    far[0]()
    near[1]()
    near[2]()
    for k, step in enumerate(far[1:]):
        if k % 2 == 0 and k // 2 < len(relays):
            relays[k // 2]()
        step()
    for relay in relays[len(far) // 2 :]:
        relay()
    end_chain()
    end_near()
    end_far()


def enter(acts, weights, cotangent, collective_id):
    n_z = lax.axis_size("gx")
    span = lax.axis_size("gy")
    rows, cols = acts.shape
    dma = pltpu.SemaphoreType.DMA
    half = (2, rows // 2, cols)
    seq, full, all_cot = pl.pallas_call(
        partial(enter_kernel, n_z, span),
        out_shape=(
            jax.ShapeDtypeStruct((span,) + half, acts.dtype),
            jax.ShapeDtypeStruct((n_z,) + weights.shape, weights.dtype),
            jax.ShapeDtypeStruct((n_z * span,) + half, cotangent.dtype),
        ),
        in_specs=[pl.BlockSpec(memory_space=pltpu.VMEM)] * 3,
        out_specs=(pl.BlockSpec(memory_space=pl.ANY),) * 3,
        scratch_shapes=[
            dma((24,)),
            dma((span, 2)),
            dma,
            dma((2 * n_z,)),
            dma((n_z,)),
            dma,
            dma((24 * (2 * n_z - 1),)),
            dma((n_z * span, 2)),
            dma,
        ],
        compiler_params=pltpu.CompilerParams(collective_id=collective_id, has_side_effects=True),
        name="enter",
    )(acts.reshape(half), weights, cotangent.reshape(half))
    return (
        seq.reshape(span * rows, cols),
        full.reshape(n_z * weights.shape[0], weights.shape[1]),
        all_cot.reshape(n_z * span * rows, cols),
    )


def chain_scatter(n_z, part_ref, out_ref, from_low, from_high, send_sem, low_recv, high_recv):
    z = lax.axis_index("gx")
    g = lax.axis_index("gy")
    rows = part_ref.shape[1]

    def up(dest):
        return pltpu.make_async_remote_copy(
            src_ref=part_ref.at[dest],
            dst_ref=from_low.at[dest],
            send_sem=send_sem.at[dest],
            recv_sem=low_recv.at[dest],
            device_id={"gx": z + 1, "gy": g},
            device_id_type=pl.DeviceIdType.MESH,
        )

    def down(dest):
        return pltpu.make_async_remote_copy(
            src_ref=part_ref.at[dest],
            dst_ref=from_high.at[dest],
            send_sem=send_sem.at[dest],
            recv_sem=high_recv.at[dest],
            device_id={"gx": z - 1, "gy": g},
            device_id_type=pl.DeviceIdType.MESH,
        )

    def start():
        for k in range(n_z - 1):
            run_if(z == 0, lambda k=k: up(n_z - 1 - k).start())
            run_if(z == n_z - 1, lambda k=k: down(k).start())

    def pass_up(dest):
        up(dest).wait_recv()
        add_into(part_ref.at[dest], (part_ref.at[dest], from_low.at[dest]), rows)
        up(dest).start()

    def pass_down(dest):
        down(dest).wait_recv()
        add_into(part_ref.at[dest], (part_ref.at[dest], from_high.at[dest]), rows)
        down(dest).start()

    def relay(time):
        for k in range(time):
            low, dest = time - k, n_z - 1 - k
            if 0 < low < dest:
                run_if(z == low, partial(pass_up, dest))
            high, dest = n_z - 1 - (time - k), k
            if dest < high < n_z - 1:
                run_if(z == high, partial(pass_down, dest))

    def finish():
        for dest in range(n_z):
            terms = [part_ref.at[dest]]
            terms += [from_low.at[dest]] if dest > 0 else []
            terms += [from_high.at[dest]] if dest < n_z - 1 else []

            def last(dest=dest, terms=terms):
                if dest > 0:
                    up(dest).wait_recv()
                if dest < n_z - 1:
                    down(dest).wait_recv()
                add_into(out_ref, terms, rows)

            run_if(z == dest, last)
        for dest in range(n_z):
            run_if(z != dest, lambda dest=dest: up(dest).wait_send())

    return start, [partial(relay, time) for time in range(1, n_z)], finish


def leave_kernel(
    n_i,
    rows,
    part_ref,
    weight_ref,
    out_ref,
    weight_out,
    held,
    from_core,
    from_a,
    from_b,
    from_z,
    sums,
    from_low,
    from_high,
    load_sem,
    core_send,
    a_send,
    b_send,
    z_send,
    core_recv,
    a_recv,
    b_recv,
    z_recv,
    copy_sem,
    chain_send,
    low_recv,
    high_recv,
):
    n_z = lax.axis_size("gx")
    copy = pltpu.make_async_copy(weight_ref, sums, copy_sem)
    copy.start()
    chain = chain_scatter(
        n_z, sums, weight_out, from_low, from_high, chain_send, low_recv, high_recv
    )

    def start():
        copy.wait()
        chain[0]()

    scatter_kernel(
        False,
        n_i,
        rows,
        part_ref,
        out_ref,
        held,
        from_core,
        from_a,
        from_b,
        from_z,
        load_sem,
        core_send,
        a_send,
        b_send,
        z_send,
        core_recv,
        a_recv,
        b_recv,
        z_recv,
        (start, chain[1], chain[2]),
    )


def leave(part, weight_part, collective_id, pieces=4):
    n_z = lax.axis_size("gx")
    span = lax.axis_size("gy")
    total, cols = part.shape
    rows = total // span // (2 * pieces)
    shaped = part.reshape(span, pieces, 2, rows, cols).swapaxes(0, 1)
    half = (rows, cols)
    dma = pltpu.SemaphoreType.DMA
    block = (weight_part.shape[0] // n_z, weight_part.shape[1])
    out, sums = pl.pallas_call(
        partial(leave_kernel, pieces, rows),
        out_shape=(
            jax.ShapeDtypeStruct((pieces, 2, rows, cols), jnp.float32),
            jax.ShapeDtypeStruct(block, jnp.float32),
        ),
        in_specs=[pl.BlockSpec(memory_space=pl.ANY)] * 2,
        out_specs=(pl.BlockSpec(memory_space=pltpu.VMEM),) * 2,
        scratch_shapes=[
            pltpu.VMEM((pieces, 4, 2) + half, jnp.bfloat16),
            pltpu.VMEM((pieces, 4, 2) + half, jnp.bfloat16),
            pltpu.VMEM((pieces, 2, 2) + half, jnp.bfloat16),
            pltpu.VMEM((pieces, 2) + half, jnp.bfloat16),
            pltpu.VMEM((1, 2, 16, 128), jnp.bfloat16),
            pltpu.VMEM((n_z,) + block, jnp.bfloat16),
            pltpu.VMEM((n_z,) + block, jnp.bfloat16),
            pltpu.VMEM((n_z,) + block, jnp.bfloat16),
            dma((pieces, 4)),
            dma((pieces, 4)),
            dma((pieces, 4)),
            dma((pieces, 2)),
            dma((pieces,)),
            dma((pieces, 4)),
            dma((pieces, 2, 2)),
            dma((pieces, 2)),
            dma((pieces,)),
            dma,
            dma((n_z,)),
            dma((n_z,)),
            dma((n_z,)),
        ],
        compiler_params=pltpu.CompilerParams(
            collective_id=collective_id, has_side_effects=True, vmem_limit_bytes=60 << 20
        ),
        name="leave",
    )(shaped, weight_part.reshape((n_z,) + block))
    return out.reshape(total // span, cols), sums


def expert_kernel(n_z, span, own_ref, cot_ref, share_ref, gate_ref, up_ref, down_ref,
                  all_ref, moe_part_ref, pair_ref, dots_ref, down_out,
                  moe_buf, cot_buf, share_buf, moe_stage, pair_stage, dots_buf,
                  gate_val, up_val, scaled, scaled_t, down_t,
                  send_sem, recv_sem, local_sem, fetch_sem, store_sem):
    z = lax.axis_index("gx")
    g = lax.axis_index("gy")
    rows = own_ref.shape[1]
    block = 2 * rows
    step_rows = moe_buf.shape[1]
    steps = 2 * n_z
    flip_x = g + 2 - 4 * ((g // 2) % 2)
    flip_y = g + 4 - 8 * ((g // 4) % 2)
    flip_both = flip_x + flip_y - g
    core = {"gx": z, "gy": flip(g)}
    x_peer = {"gx": z, "gy": flip_x}
    y_peer = {"gx": z, "gy": flip_y}
    above = {"gx": z + 1, "gy": g}
    below = {"gx": z - 1, "gy": g}

    order = [z]
    candidates = []
    for d in range(1, n_z):
        candidates += [(z >= d, z - d), (z < n_z - d, z + d)]
    for k in range(1, n_z):
        rank, chosen = 0, 0
        for ok, owner in candidates:
            ok = ok.astype(jnp.int32)
            rank = rank + ok
            chosen = chosen + ok * (rank == k).astype(jnp.int32) * owner
        order.append(chosen)

    onward = [(z < n_z - 1, z > 0)]
    for owner in order[1:]:
        onward.append(
            (
                jnp.logical_and(owner < z, z < n_z - 1),
                jnp.logical_and(owner > z, z > 0),
            )
        )
    barrier_with(
        [(z >= 0, core), (z >= 0, x_peer), (z >= 0, y_peer), (z < n_z - 1, above), (z > 0, below)]
    )

    def at(owner, gg, h):
        return pl.ds(pl.multiple_of((owner * span + gg) * block + h * rows, rows), rows)

    def copy(k, slot, owner, gg, h, peer, own=False):
        return pltpu.make_async_remote_copy(
            src_ref=own_ref.at[h] if own else all_ref.at[at(owner, gg, h)],
            dst_ref=all_ref.at[at(owner, gg, h)],
            send_sem=send_sem.at[k, slot],
            recv_sem=recv_sem.at[owner * span + gg, h],
            device_id=peer,
            device_id_type=pl.DeviceIdType.MESH,
        )

    sends = []

    def send(ok, *where, **options):
        k = where[0]
        slot = sum(1 for entry in sends if entry[2] == k)
        make = partial(copy, k, slot, *where[1:], **options)
        sends.append((ok, make, k))
        run_if(ok, lambda: make().start())

    def arrive(owner, gg, h):
        copy(0, 0, owner, gg, h, core).wait_recv()

    locals_ = [
        pltpu.make_async_copy(own_ref.at[h], all_ref.at[at(z, g, h)], local_sem.at[h])
        for h in range(2)
    ]

    def first(k):
        owner = order[k]
        own = k == 0
        if own:
            for item in locals_:
                item.start()
        else:
            arrive(owner, g, 0)
            arrive(owner, g, 1)
        go_up, go_down = onward[k]
        for h in range(2):
            send(go_up, k, owner, g, h, above, own=own)
            send(go_down, k, owner, g, h, below, own=own)
        send(True, k, owner, g, 0, x_peer, own=own)
        send(True, k, owner, g, 1, y_peer, own=own)
        send(True, k, owner, g, 1, x_peer, own=own)
        send(True, k, owner, g, 0, y_peer, own=own)
        send(True, k, owner, g, 0, core, own=own)
        send(True, k, owner, g, 1, core, own=own)

    def second(k):
        owner = order[k]
        arrive(owner, flip_x, 0)
        send(True, k, owner, flip_x, 0, y_peer)
        send(True, k, owner, flip_x, 0, core)
        arrive(owner, flip_y, 1)
        send(True, k, owner, flip_y, 1, x_peer)
        send(True, k, owner, flip_y, 1, core)

    def third(k):
        owner = order[k]
        for gg, h in ((flip_y, 0), (flip_x, 1), (flip_both, 0), (flip_both, 1)):
            arrive(owner, gg, h)
            send(True, k, owner, gg, h, core)

    def complete(k):
        for gg in (g, flip_x, flip_y, flip_both):
            for h in range(2):
                arrive(order[k], flip(gg), h)
        if k == 0:
            for item in locals_:
                item.wait()

    def place(s):
        k, side = (s // 2, s % 2) if isinstance(s, int) else (lax.div(s, 2), lax.rem(s, 2))
        if isinstance(s, int):
            owner = order[k]
        else:
            owner = sum((k == j).astype(jnp.int32) * order[j] for j in range(n_z))
        return pl.ds(pl.multiple_of(owner * (span * block) + side * step_rows, step_rows), step_rows)

    def parity(s):
        return s % 2 if isinstance(s, int) else lax.rem(s, 2)

    def fetches(s):
        slot = parity(s)
        return [
            pltpu.make_async_copy(source.at[place(s)], target.at[slot], fetch_sem.at[j, slot])
            for j, (source, target) in enumerate(
                ((all_ref, moe_buf), (cot_ref, cot_buf), (share_ref, share_buf))
            )
        ]

    def stores(s, chosen=(0, 1, 2)):
        slot = parity(s)
        pairs = ((moe_stage, moe_part_ref), (dots_buf, dots_ref), (pair_stage, pair_ref))
        return [
            pltpu.make_async_copy(
                pairs[j][0].at[slot], pairs[j][1].at[place(s)], store_sem.at[j, slot]
            )
            for j in chosen
        ]

    f32 = jnp.float32
    dot = partial(lax.dot_general, preferred_element_type=f32)
    plain = (((1,), (0,)), ((), ()))
    last_dims = (((1,), (1,)), ((), ()))
    first_dims = (((0,), (0,)), ((), ()))
    half_width = scaled.shape[1]
    width = moe_buf.shape[2]
    tile = 256

    def events(s, phase):
        for k in range(1, n_z):
            if k >= 2 and phase == 1:
                pl.when(s == k - 2)(partial(first, k))
            if phase == 2:
                pl.when(s == 2 * (k - 1))(partial(second, k))
            if phase == 2:
                pl.when(s == 2 * (k - 1) + 1)(partial(third, k))
            if phase == 4:
                pl.when(s == 2 * k - 1)(partial(complete, k))

    first(0)

    @pl.loop(0, width // tile)
    def _(t):
        cols = pl.ds(pl.multiple_of(t * tile, tile), tile)
        down_t[cols, :] = down_ref[:, cols].T

    second(0)
    if n_z > 1:
        first(1)
    third(0)
    complete(0)
    for item in fetches(0):
        item.start()

    @pl.loop(0, steps)
    def _(s):
        slot = lax.rem(s, 2)
        moe, cot, share = moe_buf.at[slot], cot_buf.at[slot], share_buf.at[slot]
        for item in fetches(s):
            item.wait()

        @pl.when(s >= 2)
        def _():
            for item in stores(s - 2):
                item.wait()

        wide = jnp.concatenate([share[...]] * (tile // share.shape[1]), axis=1)

        @pl.loop(0, half_width // tile)
        def _(t):
            cols = pl.ds(pl.multiple_of(t * tile, tile), tile)
            gated = dot(moe[...], gate_ref[:, cols], plain)
            lifted = dot(moe[...], up_ref[:, cols], plain)
            gate_val[:, cols] = gated
            up_val[:, cols] = lifted
            scaled[:, cols] = (gated * jax.nn.sigmoid(gated) * lifted * wide).astype(jnp.bfloat16)

        events(s, 1)
        scaled_t[...] = scaled[...].T

        @pl.loop(0, width // (2 * tile))
        def _(t):
            cols = pl.ds(pl.multiple_of(t * 2 * tile, 2 * tile), 2 * tile)
            moe_stage[slot, :, cols] = dot(scaled[...], down_ref[:, cols], plain).astype(jnp.bfloat16)

        stores(s, (0,))[0].start()
        events(s, 2)
        dots_buf[slot] = jnp.zeros(dots_buf.shape[1:], f32)

        @pl.loop(0, half_width // tile)
        def _(t):
            cols = pl.ds(pl.multiple_of(t * tile, tile), tile)
            pulled = dot(cot[...], down_t[:, cols], plain)
            gated = gate_val[:, cols]
            lifted = up_val[:, cols]
            sig = jax.nn.sigmoid(gated)
            silu = gated * sig
            product = pulled * (silu * lifted)
            lanes = share.shape[1]
            dots_buf[slot] = dots_buf[slot] + sum(
                product[:, j * lanes : (j + 1) * lanes] for j in range(tile // lanes)
            )
            pulled = pulled * wide
            pair_stage[slot, :, cols] = (pulled * lifted * sig * (1.0 + gated * (1.0 - sig))).astype(
                jnp.bfloat16
            )
            more = pl.ds(pl.multiple_of(half_width + t * tile, tile), tile)
            pair_stage[slot, :, more] = (pulled * silu).astype(jnp.bfloat16)

        for item in stores(s, (1, 2)):
            item.start()
        events(s, 3)
        events(s, 4)

        @pl.when(s < steps - 1)
        def _():
            for item in fetches(s + 1):
                item.start()

        @pl.loop(0, width // (2 * tile))
        def _(t):
            cols = pl.ds(pl.multiple_of(t * 2 * tile, 2 * tile), 2 * tile)
            grown = dot(scaled_t[...], cot[:, cols], plain)
            down_out[:, cols] = jnp.where(s == 0, 0.0, down_out[:, cols]) + grown

    for s in (steps - 2, steps - 1):
        for item in stores(s):
            item.wait()
    for ok, make, k in sends:
        run_if(ok, lambda make=make: make().wait_send())


def run_experts(moe_in, all_cot, shares, gate_w, up_w, down_w, collective_id):
    n_z = lax.axis_size("gx")
    span = lax.axis_size("gy")
    rows, width = moe_in.shape
    half = down_w.shape[0]
    total = n_z * span * rows
    step = span * rows // 2
    lanes = shares.shape[1]
    bf16, f32 = jnp.bfloat16, jnp.float32
    dma = pltpu.SemaphoreType.DMA
    vmem = pl.BlockSpec(memory_space=pltpu.VMEM)
    hbm = pl.BlockSpec(memory_space=pl.ANY)
    return pl.pallas_call(
        partial(expert_kernel, n_z, span),
        out_shape=(
            jax.ShapeDtypeStruct((total, width), bf16),
            jax.ShapeDtypeStruct((total, width), bf16),
            jax.ShapeDtypeStruct((total, 2 * half), bf16),
            jax.ShapeDtypeStruct((total, lanes), f32),
            jax.ShapeDtypeStruct((half, width), f32),
        ),
        in_specs=[vmem, hbm, hbm, vmem, vmem, vmem],
        out_specs=(hbm, hbm, hbm, hbm, vmem),
        scratch_shapes=[
            pltpu.VMEM((2, step, width), bf16),
            pltpu.VMEM((2, step, width), bf16),
            pltpu.VMEM((2, step, lanes), f32),
            pltpu.VMEM((2, step, width), bf16),
            pltpu.VMEM((2, step, 2 * half), bf16),
            pltpu.VMEM((2, step, lanes), f32),
            pltpu.VMEM((step, half), f32),
            pltpu.VMEM((step, half), f32),
            pltpu.VMEM((step, half), bf16),
            pltpu.VMEM((half, step), bf16),
            pltpu.VMEM((width, half), bf16),
            dma((n_z, 18)),
            dma((n_z * span, 2)),
            dma((2,)),
            dma((3, 2)),
            dma((3, 2)),
        ],
        compiler_params=pltpu.CompilerParams(
            collective_id=collective_id, has_side_effects=True, vmem_limit_bytes=60 << 20
        ),
        name="experts",
    )(moe_in.reshape(2, rows // 2, width), all_cot, shares, gate_w, up_w, down_w)


def pull_kernel(n_i, rows, all_ref, pair_ref, gate_ref, up_ref, out_ref, gate_out, up_out,
                held, from_core, from_a, from_b, from_z, moe_buf, pair_buf,
                fetch_sem, core_send, a_send, b_send, z_send, core_recv, a_recv, b_recv, z_recv):
    z = lax.axis_index("gx")
    g = lax.axis_index("gy")
    flip_x = g + 2 - 4 * ((g // 2) % 2)
    flip_y = g + 4 - 8 * ((g // 4) % 2)
    quads = (flip_x + flip_y - g, flip_x, flip_y, g)
    core = {"gx": z, "gy": flip(g)}
    x_peer = {"gx": z, "gy": flip_x}
    y_peer = {"gx": z, "gy": flip_y}
    along = [{"gx": lax.rem(z + j, n_i), "gy": g} for j in range(1, n_i)]
    barrier_with([(z >= 0, peer) for peer in (core, x_peer, y_peer, *along)])
    item_rows = moe_buf.shape[1]
    width = moe_buf.shape[2]
    half_width = gate_out.shape[1]
    owners = [lax.rem(z + n_i - 1 - i + n_i, n_i) for i in range(n_i)]

    def remote(src, dst, ssem, rsem, peer):
        return pltpu.make_async_remote_copy(
            src_ref=src,
            dst_ref=dst,
            send_sem=ssem,
            recv_sem=rsem,
            device_id=peer,
            device_id_type=pl.DeviceIdType.MESH,
        )

    def fetches(i):
        place = pl.ds(pl.multiple_of(owners[i] * item_rows, item_rows), item_rows)
        return [
            pltpu.make_async_copy(all_ref.at[place], moe_buf.at[i % 2], fetch_sem.at[0, i % 2]),
            pltpu.make_async_copy(pair_ref.at[place], pair_buf.at[i % 2], fetch_sem.at[1, i % 2]),
        ]

    def core_copy(i, q):
        return remote(
            held.at[i, flip(quads[q])],
            from_core.at[i, q],
            core_send.at[i, q],
            core_recv.at[i, q],
            core,
        )

    a_plan = ((0, 0, 0, x_peer), (0, 1, 0, y_peer), (1, 0, 1, x_peer), (2, 1, 1, y_peer))

    def a_copy(i, k):
        q, h, slot, peer = a_plan[k]
        return remote(
            held.at[i, quads[q], h],
            from_a.at[i, h, slot],
            a_send.at[i, k],
            a_recv.at[i, h, slot],
            peer,
        )

    b_plan = ((2, y_peer), (1, x_peer))

    def b_copy(i, h):
        q, peer = b_plan[h]
        return remote(
            held.at[i, quads[q], h], from_b.at[i, h], b_send.at[i, h], b_recv.at[i, h], peer
        )

    def z_copy(i):
        return remote(
            held.at[i, g], from_z.at[z], z_send.at[i], z_recv.at[z], {"gx": owners[i], "gy": g}
        )

    dot = partial(lax.dot_general, preferred_element_type=jnp.float32)
    last_dims = (((1,), (1,)), ((), ()))
    first_dims = (((0,), (0,)), ((), ()))

    def multiply(i):
        for copy in fetches(i):
            copy.wait()
        pair = pair_buf.at[i % 2]
        tile = 256

        @pl.loop(0, width // tile)
        def _(t):
            cols = pl.ds(pl.multiple_of(t * tile, tile), tile)
            total = dot(pair[:, :half_width], gate_ref[cols, :], last_dims)
            total = total + dot(pair[:, half_width:], up_ref[cols, :], last_dims)
            held[i, :, :, :, cols] = total.astype(jnp.bfloat16).reshape(held.shape[1:4] + (tile,))

        for q in range(4):
            core_copy(i, q).start()

    def accumulate(i):
        moe, pair = moe_buf.at[i % 2], pair_buf.at[i % 2]
        tile = 256

        @pl.loop(0, width // tile)
        def _(t):
            cols = pl.ds(pl.multiple_of(t * tile, tile), tile)
            grown = dot(moe[:, cols], pair[...], first_dims)
            if i == 0:
                gate_out[cols, :] = grown[:, :half_width]
                up_out[cols, :] = grown[:, half_width:]
            else:
                gate_out[cols, :] = gate_out[cols, :] + grown[:, :half_width]
                up_out[cols, :] = up_out[cols, :] + grown[:, half_width:]

        if i + 2 < n_i:
            for copy in fetches(i + 2):
                copy.start()

    def stage_a(i):
        for q in range(4):
            core_copy(i, q).wait_recv()
            for h in range(2):
                mine = held.at[i, quads[q], h]
                add_into(mine, (mine, from_core.at[i, q, h]), rows)
            for k in range(4):
                if a_plan[k][0] == q:
                    a_copy(i, k).start()

    def stage_b(i):
        for q, h, slot in ((2, 0, 0), (1, 1, 0), (3, 0, 1), (3, 1, 1)):
            mine, arrived = held.at[i, quads[q], h], from_a.at[i, h, slot]
            remote(mine, arrived, a_send.at[i, 0], a_recv.at[i, h, slot], core).wait_recv()
            add_into(mine, (mine, arrived), rows)
            if slot == 0:
                b_copy(i, h).start()

    def stage_c(i):
        for h in range(2):
            b_copy(i, h).wait_recv()
            mine = held.at[i, g, h]
            add_into(mine, (mine, from_b.at[i, h]), rows)
        if i < n_i - 1:
            z_copy(i).start()
        else:
            for j in range(n_i - 1):
                arrived = from_z.at[owners[j]]
                remote(held.at[j, g], arrived, z_send.at[j], z_recv.at[owners[j]], core).wait_recv()
            for h in range(2):
                terms = [held.at[i, g, h]] + [from_z.at[owners[j], h] for j in range(n_i - 1)]
                add_into(out_ref.at[h], terms, rows)

    for i in range(min(2, n_i)):
        for copy in fetches(i):
            copy.start()
    for t in range(n_i + 3):
        if t < n_i:
            multiply(t)
        if 0 <= t - 1 < n_i:
            stage_a(t - 1)
        if 0 <= t - 2 < n_i:
            stage_b(t - 2)
        if 0 <= t - 1 < n_i:
            accumulate(t - 1)
        if 0 <= t - 3 < n_i:
            stage_c(t - 3)
    for i in range(n_i):
        for q in range(4):
            core_copy(i, q).wait_send()
        for k in range(4):
            a_copy(i, k).wait_send()
        for h in range(2):
            b_copy(i, h).wait_send()
        if i < n_i - 1:
            z_copy(i).wait_send()


def pull_experts(all_moe, pair, gate_w, up_w, collective_id):
    n_i = lax.axis_size("gx")
    span = lax.axis_size("gy")
    total, width = all_moe.shape
    half_width = gate_w.shape[1]
    rows = total // (n_i * span) // 2
    half = (rows, width)
    bf16 = jnp.bfloat16
    dma = pltpu.SemaphoreType.DMA
    vmem = pl.BlockSpec(memory_space=pltpu.VMEM)
    hbm = pl.BlockSpec(memory_space=pl.ANY)
    out, gate_part, up_part = pl.pallas_call(
        partial(pull_kernel, n_i, rows),
        out_shape=(
            jax.ShapeDtypeStruct((2,) + half, jnp.float32),
            jax.ShapeDtypeStruct((width, half_width), jnp.float32),
            jax.ShapeDtypeStruct((width, half_width), jnp.float32),
        ),
        in_specs=[hbm, hbm, vmem, vmem],
        out_specs=(vmem, vmem, vmem),
        scratch_shapes=[
            pltpu.VMEM((n_i, span, 2) + half, bf16),
            pltpu.VMEM((n_i, 4, 2) + half, bf16),
            pltpu.VMEM((n_i, 2, 2) + half, bf16),
            pltpu.VMEM((n_i, 2) + half, bf16),
            pltpu.VMEM((n_i, 2) + half, bf16),
            pltpu.VMEM((2, span * 2 * rows, width), bf16),
            pltpu.VMEM((2, span * 2 * rows, 2 * half_width), bf16),
            dma((2, 2)),
            dma((n_i, 4)),
            dma((n_i, 4)),
            dma((n_i, 2)),
            dma((n_i,)),
            dma((n_i, 4)),
            dma((n_i, 2, 2)),
            dma((n_i, 2)),
            dma((n_i,)),
        ],
        compiler_params=pltpu.CompilerParams(
            collective_id=collective_id, has_side_effects=True, vmem_limit_bytes=67043328
        ),
        name="pull_experts",
    )(all_moe, pair, gate_w, up_w)
    return out.reshape(2 * rows, width), gate_part, up_part


def gather_plane(block, collective_id):
    if lax.axis_size("gy") == 8:
        return all_gather(block, False, collective_id)
    return lax.all_gather(block, "gy", axis=0, tiled=True)


def gather_inputs(acts, weights, cotangent):
    if lax.axis_size("gy") == 8:
        return enter(acts, weights, cotangent, 6)
    return (
        lax.all_gather(acts, "gy", axis=0, tiled=True),
        lax.all_gather(weights, "gx", axis=0, tiled=True),
        None,
    )


def scatter_grads(acts_part, weight_part):
    if lax.axis_size("gy") == 8:
        return leave(acts_part, weight_part, 7)
    return (
        lax.psum_scatter(acts_part, "gy", scatter_dimension=0, tiled=True).astype(jnp.float32),
        lax.psum_scatter(weight_part, "gx", scatter_dimension=0, tiled=True).astype(jnp.float32),
    )


def scatter_plane(part, collective_id):
    if lax.axis_size("gy") == 8:
        return reduce_scatter(part, False, collective_id)
    return lax.psum_scatter(part, "gy", scatter_dimension=0, tiled=True).astype(jnp.float32)


def norm_rows(values, gain_row):
    return (
        values * lax.rsqrt(jnp.mean(values * values, axis=-1, keepdims=True) + EPSILON) * gain_row
    )


def rotary(values):
    length = values.shape[0]
    halfway = values.shape[-1] // 2
    positions = jnp.arange(length, dtype=jnp.float32)
    frequency = jnp.exp(
        jnp.arange(halfway, dtype=jnp.float32) * (-2.0 * jnp.log(10000.0) / values.shape[-1])
    )
    angles = (positions[:, None] * frequency[None, :])[:, None, :]
    cosine = jnp.cos(angles)
    sine_table = jnp.sin(angles)
    first_half = values[..., :halfway]
    second = values[..., halfway:]
    return jnp.concatenate(
        [first_half * cosine - second * sine_table, second * cosine + first_half * sine_table],
        axis=-1,
    )


def prepare_heads(raw_heads, gain_row):
    return rotary(norm_rows(raw_heads, gain_row))


def route_gates(id_table, logits):
    shares = jax.nn.softmax(logits, axis=-1)
    experts = logits.shape[-1]
    matches = id_table[:, :, None] == jnp.arange(experts, dtype=jnp.int32)[None, None, :]
    chosen = jnp.sum(jnp.where(matches, shares[:, None, :], 0.0), axis=-1)
    return chosen / jnp.sum(chosen, axis=-1, keepdims=True)


def contract_rows(left_side, right_side):
    return lax.dot_general(
        left_side, right_side, (((0,), (0,)), ((), ())), preferred_element_type=jnp.float32
    )


def contract_cols(left_side, right_side):
    return lax.dot_general(
        left_side, right_side, (((1,), (1,)), ((), ())), preferred_element_type=jnp.float32
    )


def routed_experts(
    moe_in, cotangent, expert_ids, gate_share, router_weight, gate_weight, up_weight, down_weight
):
    tok_rows = moe_in.shape[0]
    experts = router_weight.shape[1]
    width_all = moe_in.shape[1]
    capacity = tok_rows * TOP * 3 // (2 * experts)
    route_count = tok_rows * TOP
    flat_ids = expert_ids.reshape(route_count)
    onehot = (flat_ids[:, None] == jnp.arange(experts, dtype=jnp.int32)[None, :]).astype(jnp.int32)
    earlier = jnp.cumsum(onehot, axis=0) - onehot
    slot_index = jnp.sum(earlier * onehot, axis=1)
    target = flat_ids * capacity + slot_index
    source = (
        jnp.full((experts * capacity,), tok_rows, jnp.int32)
        .at[target]
        .set(jnp.arange(route_count, dtype=jnp.int32) // TOP)
    )
    padded_in = jnp.concatenate([moe_in, jnp.zeros((1, width_all), jnp.bfloat16)], axis=0)
    packed = padded_in[source].reshape(experts, 1, capacity, width_all)
    outgoing = jnp.broadcast_to(packed, (experts, 2, capacity, width_all)).reshape(
        2 * experts, capacity, width_all
    )
    arrived = lax.all_to_all(outgoing, ("gx", "gy"), split_axis=0, concat_axis=1, tiled=True)[0]
    gate_in = gate_weight[0]
    up_in = up_weight[0]
    down_in = down_weight[0]
    gate_val = jnp.dot(arrived, gate_in, preferred_element_type=jnp.float32)
    up_val = jnp.dot(arrived, up_in, preferred_element_type=jnp.float32)
    hidden = (jax.nn.silu(gate_val) * up_val).astype(jnp.bfloat16)
    produced = jnp.dot(hidden, down_in, preferred_element_type=jnp.float32).astype(jnp.bfloat16)
    returned = lax.all_to_all(produced[None], ("gx", "gy"), split_axis=1, concat_axis=0, tiled=True)
    summed = (
        returned.reshape(experts, 2, capacity, width_all)
        .astype(jnp.float32)
        .sum(axis=1)
        .reshape(experts * capacity, width_all)
    )
    route_out = summed[target]
    gates_flat = gate_share.reshape(route_count)
    moe_out = jnp.sum((gates_flat[:, None] * route_out).reshape(tok_rows, TOP, width_all), axis=1)
    grad_out = cotangent.astype(jnp.float32)
    grad_gates = jnp.sum(
        route_out.reshape(tok_rows, TOP, width_all) * grad_out[:, None, :], axis=-1
    )
    slot_gate = jnp.zeros((experts * capacity,), jnp.float32).at[target].set(gates_flat)
    padded_grad = jnp.concatenate([grad_out, jnp.zeros((1, width_all), jnp.float32)], axis=0)
    grad_packed = (
        (slot_gate[:, None] * padded_grad[source])
        .astype(jnp.bfloat16)
        .reshape(experts, 1, capacity, width_all)
    )
    grad_outgoing = jnp.broadcast_to(grad_packed, (experts, 2, capacity, width_all)).reshape(
        2 * experts, capacity, width_all
    )
    grad_arrived = lax.all_to_all(
        grad_outgoing, ("gx", "gy"), split_axis=0, concat_axis=1, tiled=True
    )[0]
    rows_in, grad_use = (arrived, grad_arrived)
    gate_use, up_use, hidden_use = (gate_val, up_val, hidden)
    sigmoid_gate = jax.nn.sigmoid(gate_use)
    silu_gate = gate_use * sigmoid_gate
    grad_hidden = contract_cols(grad_use, down_in)
    down_part = contract_rows(hidden_use, grad_use)
    grad_gate = (
        grad_hidden * up_use * sigmoid_gate * (1.0 + gate_use * (1.0 - sigmoid_gate))
    ).astype(jnp.bfloat16)
    grad_up = (grad_hidden * silu_gate).astype(jnp.bfloat16)
    gate_part = contract_rows(rows_in, grad_gate)
    up_part = contract_rows(rows_in, grad_up)
    grad_in = contract_cols(grad_gate, gate_in) + contract_cols(grad_up, up_in)
    grad_back = lax.all_to_all(
        grad_in.astype(jnp.bfloat16)[None], ("gx", "gy"), split_axis=1, concat_axis=0, tiled=True
    )
    grad_summed = (
        grad_back.reshape(experts, 2, capacity, width_all)
        .astype(jnp.float32)
        .sum(axis=1)
        .reshape(experts * capacity, width_all)
    )
    grad_moe_in = jnp.sum(grad_summed[target].reshape(tok_rows, TOP, width_all), axis=1)
    return moe_out, grad_gates, grad_moe_in, gate_part, up_part, down_part


def dense_experts(
    moe_in, all_cot, expert_ids, gate_share, gate_weight, up_weight, down_weight
):
    everyone = ("gx", "gy")
    devices = lax.axis_size("gx") * lax.axis_size("gy")
    experts = devices // 2
    matches = expert_ids[:, :, None] == jnp.arange(experts, dtype=jnp.int32)[None, None, :]
    dense_gates = jnp.sum(jnp.where(matches, gate_share[:, :, None], 0.0), axis=1)
    own_gate = lax.all_to_all(
        jnp.repeat(dense_gates.T, 2, axis=0), everyone, split_axis=0, concat_axis=0, tiled=True
    ).reshape(-1)
    shares = jnp.broadcast_to(own_gate[:, None], (own_gate.shape[0], 128))
    all_moe, moe_share, pair, gate_dots, down_part = run_experts(
        moe_in, all_cot, shares, gate_weight[0], up_weight[0], down_weight[0], 8
    )
    moe_out = reduce_scatter(moe_share, True, 4)
    dots_back = lax.all_to_all(
        jnp.sum(gate_dots, axis=-1).reshape(devices, -1),
        everyone,
        split_axis=0,
        concat_axis=0,
        tiled=True,
    )
    dots_experts = dots_back.reshape(experts, 2, -1).sum(axis=1).T
    grad_gates = jnp.sum(jnp.where(matches, dots_experts[:, None, :], 0.0), axis=-1)
    grad_moe_in, gate_part, up_part = pull_experts(all_moe, pair, gate_weight[0], up_weight[0], 9)
    return moe_out, grad_gates, grad_moe_in, gate_part, up_part, down_part


def local(
    tokens,
    cotangent,
    expert_ids,
    doc_ids,
    clip_rank,
    attn_gain,
    moe_gain,
    query_gain,
    key_gain,
    query_weight,
    key_weight,
    value_weight,
    out_weight,
    router_weight,
    gate_weight,
    up_weight,
    down_weight,
):
    inputs = tokens.astype(jnp.float32)
    acts_float, norm_pull = jax.vjp(norm_rows, inputs, attn_gain)
    acts_low = acts_float.astype(jnp.bfloat16)
    in_weights = jnp.concatenate([query_weight, key_weight, value_weight], axis=1)
    seq_acts, full_in, all_cot = gather_inputs(acts_low, in_weights, cotangent)
    seq_acts, full_in, out_weight = lax.optimization_barrier((seq_acts, full_in, out_weight))
    out_rows = lax.all_gather(out_weight, "gx", axis=1, tiled=True)
    length = seq_acts.shape[0]
    local_width = query_weight.shape[1]
    local_heads = local_width // HD
    projected = jnp.dot(seq_acts, full_in, preferred_element_type=jnp.float32)
    queries = projected[:, :local_width]
    key_raw = projected[:, local_width : 2 * local_width]
    value_ready = (
        projected[:, 2 * local_width :].astype(jnp.bfloat16).reshape(length, local_heads, HD)
    )
    query_float, query_pull = jax.vjp(
        prepare_heads, queries.reshape(length, local_heads, HD), query_gain
    )
    key_float, key_pull = jax.vjp(prepare_heads, key_raw.reshape(length, local_heads, HD), key_gain)
    query_ready = query_float.astype(jnp.bfloat16)
    key_ready = key_float.astype(jnp.bfloat16)
    block_rows = min(512, length)
    block_count = length // block_rows
    score_scale = HD ** (-0.5)
    query_blocks = query_ready.reshape(block_count, block_rows, local_heads, HD)
    doc_blocks = doc_ids.reshape(block_count, block_rows)

    def block_scores(query_block, doc_block):
        scores = (
            jnp.einsum("qhd,khd->hqk", query_block, key_ready, preferred_element_type=jnp.float32)
            * score_scale
        )
        same_doc = doc_block[:, None] == doc_ids[None, :]
        return jnp.where(same_doc[None], scores, NEGATIVE)

    def forward_block(pieces):
        scores = block_scores(pieces[0], pieces[1])
        highest = jnp.max(scores, axis=-1, keepdims=True)
        weights = jnp.exp(scores - highest)
        totals = jnp.sum(weights, axis=-1, keepdims=True)
        shares = (weights / totals).astype(jnp.bfloat16)
        mixed_heads = jnp.einsum(
            "hqk,khd->qhd", shares, value_ready, preferred_element_type=jnp.float32
        )
        return (
            mixed_heads.astype(jnp.bfloat16),
            highest[..., 0] + jnp.log(totals[..., 0]),
            jnp.max(highest[..., 0], axis=-1),
        )

    mixed_blocks, log_totals, peak_blocks = lax.map(forward_block, (query_blocks, doc_blocks))
    mixed_seq = mixed_blocks.reshape(length, local_width)
    start_head = lax.axis_index("gy") * local_heads
    peak_slots = lax.dynamic_update_slice(
        jnp.zeros((lax.axis_size("gx"), NH), jnp.float32),
        jnp.max(peak_blocks, axis=0)[None],
        (lax.axis_index("gx"), start_head),
    )
    attended = scatter_plane(
        jnp.dot(mixed_seq, out_rows, preferred_element_type=jnp.float32).astype(jnp.bfloat16), 3
    )
    residual = inputs + attended
    moe_float, moe_pull = jax.vjp(norm_rows, residual, moe_gain)
    moe_in = moe_float.astype(jnp.bfloat16)
    logits = jnp.dot(moe_in, router_weight, preferred_element_type=jnp.float32)
    gate_share, gate_pull = jax.vjp(partial(route_gates, expert_ids), logits)
    if all_cot is not None and router_weight.shape[1] <= 2 * TOP:
        moe_out, grad_gates, grad_moe_in, gate_part, up_part, down_part = dense_experts(
            moe_in, all_cot, expert_ids, gate_share, gate_weight, up_weight, down_weight
        )
    else:
        moe_out, grad_gates, grad_moe_in, gate_part, up_part, down_part = routed_experts(
            moe_in,
            cotangent,
            expert_ids,
            gate_share,
            router_weight,
            gate_weight,
            up_weight,
            down_weight,
        )
    output = (residual + moe_out).astype(jnp.bfloat16)
    grad_out = cotangent.astype(jnp.float32)
    (grad_logits,) = gate_pull(grad_gates)
    grad_logits_low = grad_logits.astype(jnp.bfloat16)
    router_part = contract_rows(moe_in, grad_logits_low)
    grad_moe_in = grad_moe_in + contract_cols(grad_logits_low, router_weight)
    grad_resid_norm, moe_gain_part = moe_pull(grad_moe_in)
    grad_resid = grad_out + grad_resid_norm
    seq_grad = gather_plane(grad_resid.astype(jnp.bfloat16), 1)
    grad_mixed = contract_cols(seq_grad, out_rows).astype(jnp.bfloat16)
    out_part = contract_rows(seq_grad, mixed_seq)

    def backward_block(running, pieces):
        grad_key, grad_value = running
        query_block, grad_block, log_block, doc_block = pieces
        scores = block_scores(query_block, doc_block)
        weights = jnp.exp(scores - log_block[..., None])
        grad_value = grad_value + jnp.einsum(
            "hqk,qhd->khd",
            weights.astype(jnp.bfloat16),
            grad_block,
            preferred_element_type=jnp.float32,
        )
        grad_weights = jnp.einsum(
            "qhd,khd->hqk", grad_block, value_ready, preferred_element_type=jnp.float32
        )
        inner_sum = jnp.sum(weights * grad_weights, axis=-1, keepdims=True)
        grad_scores = (weights * (grad_weights - inner_sum)).astype(jnp.bfloat16)
        grad_query = (
            jnp.einsum("hqk,khd->qhd", grad_scores, key_ready, preferred_element_type=jnp.float32)
            * score_scale
        )
        grad_key = (
            grad_key
            + jnp.einsum(
                "hqk,qhd->khd", grad_scores, query_block, preferred_element_type=jnp.float32
            )
            * score_scale
        )
        return ((grad_key, grad_value), grad_query)

    empty_heads = jnp.zeros((length, local_heads, HD), jnp.float32)
    grad_mixed_blocks = grad_mixed.reshape(block_count, block_rows, local_heads, HD)
    (key_grad_heads, value_grad_heads), query_grad_blocks = lax.scan(
        backward_block,
        (empty_heads, empty_heads),
        (query_blocks, grad_mixed_blocks, log_totals, doc_blocks),
    )
    query_raw_grad, query_gain_part = query_pull(query_grad_blocks.reshape(length, local_heads, HD))
    key_raw_grad, key_gain_part = key_pull(key_grad_heads)
    grad_queries = query_raw_grad.reshape(length, local_width).astype(jnp.bfloat16)
    grad_keys = key_raw_grad.reshape(length, local_width).astype(jnp.bfloat16)
    grad_values = value_grad_heads.reshape(length, local_width).astype(jnp.bfloat16)
    grad_heads = jnp.concatenate([grad_queries, grad_keys, grad_values], axis=1)
    grad_acts, in_sum = scatter_grads(
        contract_cols(grad_heads, full_in).astype(jnp.bfloat16),
        contract_rows(seq_acts, grad_heads).astype(jnp.bfloat16),
    )
    query_sum = in_sum[:, :local_width]
    key_sum = in_sum[:, local_width : 2 * local_width]
    value_sum = in_sum[:, 2 * local_width :]
    out_sum_rows = lax.psum_scatter(
        out_part.astype(jnp.bfloat16), "gx", scatter_dimension=0, tiled=True
    ).astype(jnp.float32)
    norm_input_grad, attn_gain_part = norm_pull(grad_acts)
    input_grad = grad_resid + norm_input_grad
    small = (
        attn_gain_part,
        moe_gain_part,
        query_gain_part,
        key_gain_part,
        router_part.T,
        peak_slots,
    )
    summed = sum_everywhere(jnp.concatenate([part.reshape(-1) for part in small]), 5)
    ends = list(accumulate(part.size for part in small))
    attn_gain_grad, moe_gain_grad, query_gain_grad, key_gain_grad, router_flat, peaks = (
        summed[end - part.size : end].reshape(part.shape) for end, part in zip(ends, small)
    )
    router_grad = router_flat.T
    peak_global = jnp.max(peaks, axis=0)
    ranked = -jnp.sort(-peak_global)
    limit = jnp.sum(jnp.where(jnp.arange(NH, dtype=jnp.int32) == clip_rank[0], ranked, 0.0))
    factors = jnp.where(peak_global > limit, limit / peak_global, 1.0)
    own_factors = lax.dynamic_slice_in_dim(factors, start_head, local_heads)
    columns = jnp.repeat(jnp.sqrt(own_factors), HD)
    query_clipped = (query_weight.astype(jnp.float32) * columns[None, :]).astype(jnp.bfloat16)
    key_clipped = (key_weight.astype(jnp.float32) * columns[None, :]).astype(jnp.bfloat16)
    return (
        output,
        input_grad,
        attn_gain_grad,
        moe_gain_grad,
        query_gain_grad,
        key_gain_grad,
        query_sum,
        key_sum,
        value_sum,
        out_sum_rows.T,
        router_grad,
        gate_part[None],
        up_part[None],
        down_part[None],
        query_clipped,
        key_clipped,
        factors,
    )


def solution(mesh):
    placed = (
        P(("gx", "gy"), None),
        P(("gx", "gy"), None),
        P(("gx", "gy"), None),
        P("gx"),
        P(),
        P(),
        P(),
        P(),
        P(),
        P("gx", "gy"),
        P("gx", "gy"),
        P("gx", "gy"),
        P("gy", "gx"),
        P(),
        P(("gx", "gy"), None, None),
        P(("gx", "gy"), None, None),
        P(("gx", "gy"), None, None),
    )
    return jax.shard_map(
        local,
        mesh=mesh,
        in_specs=placed,
        out_specs=(
            P(("gx", "gy"), None),
            P(("gx", "gy"), None),
            P(),
            P(),
            P(),
            P(),
            P("gx", "gy"),
            P("gx", "gy"),
            P("gx", "gy"),
            P("gy", "gx"),
            P(),
            P(("gx", "gy"), None, None),
            P(("gx", "gy"), None, None),
            P(("gx", "gy"), None, None),
            P("gx", "gy"),
            P("gx", "gy"),
            P(),
        ),
        check_vma=False,
    )
```

```python
from functools import partial
from itertools import accumulate

import jax
import jax.numpy as jnp
from jax import lax
from jax.experimental import pallas as pl
from jax.experimental.pallas import tpu as pltpu
from jax.sharding import PartitionSpec as P

NH = 16
HD = 128
TOP = 8


EPSILON = 1e-06
NEGATIVE = -1e30


def flip(index):
    return index + 1 - 2 * (index % 2)


def barrier_with(partners):
    barrier = pltpu.get_barrier_semaphore()
    for ok, device in partners:
        @pl.when(ok)
        def _():
            pl.semaphore_signal(barrier, inc=1, device_id=device, device_id_type=pl.DeviceIdType.MESH)
    pl.semaphore_wait(barrier, sum(ok.astype(jnp.int32) for ok, _ in partners))

def always(ok, other):
    if ok is True:
        return other
    return ok if other is True else jnp.logical_and(ok, other)


def run_if(ok, action):
    if ok is True:
        action()
    else:
        pl.when(ok)(action)


def chain_gather(n_z, own_ref, out_ref, send_sem, recv_sem, local_sem):
    z = lax.axis_index("gx")
    g = lax.axis_index("gy")

    def hop(source, owner, k, peer):
        return pltpu.make_async_remote_copy(
            src_ref=source,
            dst_ref=out_ref.at[owner],
            send_sem=send_sem.at[k],
            recv_sem=recv_sem.at[owner],
            device_id={"gx": peer, "gy": g},
            device_id_type=pl.DeviceIdType.MESH,
        )

    local = pltpu.make_async_copy(own_ref, out_ref.at[z], local_sem)
    upward = [(z < n_z - 1, lambda: hop(own_ref, z, 0, z + 1))]
    downward = [(z > 0, lambda: hop(own_ref, z, n_z, z - 1))]
    for d in range(1, n_z - 1):
        upward.append(
            (
                jnp.logical_and(z >= d, z < n_z - 1),
                lambda d=d: hop(out_ref.at[z - d], z - d, d, z + 1),
            )
        )
        downward.append(
            (
                jnp.logical_and(z < n_z - d, z > 0),
                lambda d=d: hop(out_ref.at[z + d], z + d, n_z + d, z - 1),
            )
        )

    def start():
        local.start()
        for ok, copy in (upward[0], downward[0]):
            run_if(ok, lambda copy=copy: copy().start())

    def relay(d):
        run_if(z >= d, lambda: hop(own_ref, z - d, 0, z).wait_recv())
        if d < n_z - 1:
            run_if(upward[d][0], lambda: upward[d][1]().start())
        run_if(z < n_z - d, lambda: hop(own_ref, z + d, 0, z).wait_recv())
        if d < n_z - 1:
            run_if(downward[d][0], lambda: downward[d][1]().start())

    def finish():
        local.wait()
        for ok, copy in upward + downward:
            run_if(ok, lambda copy=copy: copy().wait_send())

    return start, [partial(relay, d) for d in range(1, n_z)], finish


def gather_steps(n_z, span, own_ref, out_ref, send_sem, recv_sem, local_sem):
    z = lax.axis_index("gx")
    g = lax.axis_index("gy")
    flip_x = g + 2 - 4 * ((g // 2) % 2)
    flip_y = g + 4 - 8 * ((g // 4) % 2)
    flip_both = flip_x + flip_y - g
    core = {"gx": z, "gy": flip(g)}
    x_peer = {"gx": z, "gy": flip_x}
    y_peer = {"gx": z, "gy": flip_y}
    above = {"gx": z + 1, "gy": g}
    below = {"gx": z - 1, "gy": g}
    first_z = z if n_z > 1 else 0
    sends = []

    def send(ok, source, b, h, peer):
        k = len(sends)

        def make():
            return pltpu.make_async_remote_copy(
                src_ref=source,
                dst_ref=out_ref.at[b, h],
                send_sem=send_sem.at[k],
                recv_sem=recv_sem.at[b, h],
                device_id=peer,
                device_id_type=pl.DeviceIdType.MESH,
            )

        sends.append((ok, make))
        run_if(ok, lambda: make().start())

    def arrive(ok, b, h):
        def wait():
            pltpu.make_async_remote_copy(
                src_ref=out_ref.at[b, h],
                dst_ref=out_ref.at[b, h],
                send_sem=send_sem.at[0],
                recv_sem=recv_sem.at[b, h],
                device_id=core,
                device_id_type=pl.DeviceIdType.MESH,
            ).wait_recv()

        run_if(ok, wait)

    local = pltpu.make_async_copy(own_ref, out_ref.at[first_z * span + g], local_sem)
    items = [(True, first_z, 0)]
    for d in range(1, n_z):
        items += [(z >= d, z - d, -d), (z < n_z - d, z + d, d)]

    def first(item):
        ok, owner, d = item
        b = owner * span + g
        if d == 0:
            local.start()
            source = own_ref
        else:
            arrive(ok, b, 0)
            arrive(ok, b, 1)
            source = out_ref.at[b]
        for h in range(2):
            if n_z > 1 and d <= 0:
                send(always(ok, z < n_z - 1), source.at[h], b, h, above)
            if n_z > 1 and d >= 0:
                send(always(ok, z > 0), source.at[h], b, h, below)
        send(ok, source.at[0], b, 0, x_peer)
        send(ok, source.at[1], b, 1, y_peer)
        send(ok, source.at[1], b, 1, x_peer)
        send(ok, source.at[0], b, 0, y_peer)
        send(ok, source.at[0], b, 0, core)
        send(ok, source.at[1], b, 1, core)

    def second(item):
        ok, owner, _ = item
        for side, h, peer in ((flip_x, 0, y_peer), (flip_y, 1, x_peer)):
            b = owner * span + side
            arrive(ok, b, h)
            send(ok, out_ref.at[b, h], b, h, peer)
            send(ok, out_ref.at[b, h], b, h, core)

    def third(item):
        ok, owner, _ = item
        for side, h in ((flip_both, 0), (flip_both, 1), (flip_y, 0), (flip_x, 1)):
            b = owner * span + side
            arrive(ok, b, h)
            send(ok, out_ref.at[b, h], b, h, core)

    n = len(items)

    def step(i):
        if i < n:
            first(items[i])
        if 1 <= i <= n:
            second(items[i - 1])
        if i >= 2:
            third(items[i - 2])

    def finish():
        for ok, owner, _ in items:
            for side in (g, flip_x, flip_y, flip_both):
                for h in range(2):
                    arrive(ok, owner * span + flip(side), h)
        local.wait()
        for ok, make in sends:
            run_if(ok, lambda make=make: make().wait_send())

    return [partial(step, i) for i in range(n + 2)], finish


def greet(n_z):
    z = lax.axis_index("gx")
    g = lax.axis_index("gy")
    peers = [
        (z >= 0, {"gx": z, "gy": g + bit - 2 * bit * ((g // bit) % 2)}) for bit in (1, 2, 4)
    ]
    if n_z > 1:
        peers += [(z < n_z - 1, {"gx": z + 1, "gy": g}), (z > 0, {"gx": z - 1, "gy": g})]
    barrier_with(peers)


def gather_kernel(n_z, span, own_ref, out_ref, send_sem, recv_sem, local_sem):
    greet(n_z)
    steps, finish = gather_steps(n_z, span, own_ref, out_ref, send_sem, recv_sem, local_sem)
    for step in steps:
        step()
    finish()


def all_gather(block, both, collective_id):
    n_z = lax.axis_size("gx") if both else 1
    span = lax.axis_size("gy")
    rows, cols = block.shape
    own = block.reshape(2, rows // 2, cols)
    n_sends = (2 * n_z - 1) * 24
    out = pl.pallas_call(
        partial(gather_kernel, n_z, span),
        out_shape=jax.ShapeDtypeStruct((n_z * span, 2, rows // 2, cols), block.dtype),
        in_specs=[pl.BlockSpec(memory_space=pltpu.VMEM)],
        out_specs=pl.BlockSpec(memory_space=pl.ANY),
        scratch_shapes=[pltpu.SemaphoreType.DMA((n_sends,)), pltpu.SemaphoreType.DMA((n_z * span, 2)), pltpu.SemaphoreType.DMA],
        compiler_params=pltpu.CompilerParams(collective_id=collective_id, has_side_effects=True),
        name="gather_all" if both else "gather_plane",
    )(own)
    return out.reshape(n_z * span * rows, cols)


def add_into(dst, parts, rows):
    step = min(rows, 32)

    @pl.loop(0, rows // step)
    def _(r):
        at = pl.ds(pl.multiple_of(r * step, step), step)
        if len(parts) == 2 and dst.dtype == jnp.bfloat16:
            dst[at, :] = parts[0][at, :] + parts[1][at, :]
        else:
            total = parts[0][at, :].astype(jnp.float32)
            for term in parts[1:]:
                total = total + term[at, :].astype(jnp.float32)
            dst[at, :] = total.astype(dst.dtype)


def scatter_kernel(chain, n_i, rows, part_ref, out_ref, held, from_core, from_a, from_b, from_z,
                   load_sem, core_send, a_send, b_send, z_send, core_recv, a_recv, b_recv, z_recv, beside=None):
    z = lax.axis_index("gx"); g = lax.axis_index("gy")
    flip_x = g + 2 - 4 * ((g // 2) % 2)
    flip_y = g + 4 - 8 * ((g // 4) % 2)
    quads = (flip_x + flip_y - g, flip_x, flip_y, g)
    core = {"gx": z, "gy": flip(g)}
    xn = {"gx": z, "gy": flip_x}
    yn = {"gx": z, "gy": flip_y}
    every = z >= 0
    partners = [(every, core), (every, xn), (every, yn)]
    if chain:
        partners += [(every, {"gx": lax.rem(z + j, n_i), "gy": g}) for j in range(1, n_i)]
    if beside:
        n_z = lax.axis_size("gx")
        partners += [(z < n_z - 1, {"gx": z + 1, "gy": g}), (z > 0, {"gx": z - 1, "gy": g})]
    barrier_with(partners)
    if beside:
        beside[0]()
    mesh_id = pl.DeviceIdType.MESH

    def item(i):
        return lax.rem(z + n_i - 1 - i + n_i, n_i) if chain else i

    def block(it, gg):
        return part_ref.at[it, gg]

    def remote(src, dst, ssem, rsem, dev):
        return pltpu.make_async_remote_copy(src_ref=src, dst_ref=dst, send_sem=ssem, recv_sem=rsem, device_id=dev, device_id_type=mesh_id)

    def core_copy(i, q):
        it = item(i)
        return remote(block(it, flip(quads[q])), from_core.at[it, q], core_send.at[i, q], core_recv.at[it, q], core)

    def load(i, q):
        it = item(i)
        return pltpu.make_async_copy(block(it, quads[q]), held.at[it, q], load_sem.at[i, q])

    a_plan = ((0, 0, 0, xn), (0, 1, 0, yn), (1, 0, 1, xn), (2, 1, 1, yn))
    def a_copy(i, k):
        it = item(i)
        q, h, slot, dev = a_plan[k]
        return remote(held.at[it, q, h], from_a.at[it, h, slot], a_send.at[i, k], a_recv.at[it, h, slot], dev)

    b_plan = ((2, 0, yn), (1, 1, xn))
    def b_copy(i, h):
        it = item(i)
        q, _, dev = b_plan[h]
        return remote(held.at[it, q, h], from_b.at[it, h], b_send.at[i, h], b_recv.at[it, h], dev)

    def z_copy(i):
        it = item(i)
        return remote(held.at[it, 3], from_z.at[z], z_send.at[i], z_recv.at[z], {"gx": it, "gy": g})

    def z_arrival(i):
        it = item(i)
        return remote(held.at[it, 3], from_z.at[it], z_send.at[i], z_recv.at[it], core)

    for i in range(n_i):
        for q in range(4):
            core_copy(i, q).start()
            load(i, q).start()

    def stage_a(i):
        it = item(i)
        for q in range(4):
            load(i, q).wait()
            core_copy(i, q).wait_recv()
            for h in range(2):
                add_into(held.at[it, q, h], (held.at[it, q, h], from_core.at[it, q, h]), rows)
            for k in range(4):
                if a_plan[k][0] == q:
                    a_copy(i, k).start()

    def stage_b(i):
        it = item(i)
        for q, h, slot in ((2, 0, 0), (1, 1, 0), (3, 0, 1), (3, 1, 1)):
            remote(held.at[it, q, h], from_a.at[it, h, slot], a_send.at[i, 0], a_recv.at[it, h, slot], core).wait_recv()
            add_into(held.at[it, q, h], (held.at[it, q, h], from_a.at[it, h, slot]), rows)
            if slot == 0:
                b_copy(i, h).start()

    def stage_c(i):
        it = item(i)
        for h in range(2):
            b_copy(i, h).wait_recv()
            if chain:
                add_into(held.at[it, 3, h], (held.at[it, 3, h], from_b.at[it, h]), rows)
            else:
                add_into(out_ref.at[it, h], (held.at[it, 3, h], from_b.at[it, h]), rows)

    def stage_d(i):
        if i < n_i - 1:
            z_copy(i).start()
        else:
            for j in range(n_i - 1):
                z_arrival(j).wait_recv()
            for h in range(2):
                add_into(
                    out_ref.at[h],
                    [held.at[item(i), 3, h]] + [from_z.at[item(j), h] for j in range(n_i - 1)],
                    rows,
                )

    for i in range(n_i + 2):
        if i < n_i: stage_a(i)
        if 0 <= i - 1 < n_i: stage_b(i - 1)
        if 0 <= i - 2 < n_i: stage_c(i - 2)
        if chain and 0 <= i - 2 < n_i: stage_d(i - 2)
        if beside and i == n_i:
            beside[1][0]()
    if beside:
        for relay in beside[1][1:]:
            relay()
        beside[2]()
    for i in range(n_i):
        for q in range(4): core_copy(i, q).wait_send()
        for k in range(4): a_copy(i, k).wait_send()
        for h in range(2): b_copy(i, h).wait_send()
        if chain and i < n_i - 1: z_copy(i).wait_send()


def scatter_plane(part, collective_id):
    span = lax.axis_size("gy")
    pieces, _, _, rows, cols = part.shape
    dma = pltpu.SemaphoreType.DMA
    half = (rows, cols)
    out = pl.pallas_call(
        partial(scatter_kernel, False, pieces, rows),
        out_shape=jax.ShapeDtypeStruct((pieces, 2, rows, cols), jnp.float32),
        in_specs=[pl.BlockSpec(memory_space=pl.ANY)],
        out_specs=pl.BlockSpec(memory_space=pltpu.VMEM),
        scratch_shapes=[
            pltpu.VMEM((pieces, 4, 2) + half, jnp.bfloat16),
            pltpu.VMEM((pieces, 4, 2) + half, jnp.bfloat16),
            pltpu.VMEM((pieces, 2, 2) + half, jnp.bfloat16),
            pltpu.VMEM((pieces, 2) + half, jnp.bfloat16),
            pltpu.VMEM((1, 2, 16, 128), jnp.bfloat16),
            dma((pieces, 4)),
            dma((pieces, 4)),
            dma((pieces, 4)),
            dma((pieces, 2)),
            dma((pieces,)),
            dma((pieces, 4)),
            dma((pieces, 2, 2)),
            dma((pieces, 2)),
            dma((pieces,)),
        ],
        compiler_params=pltpu.CompilerParams(
            collective_id=collective_id, has_side_effects=True, vmem_limit_bytes=60 << 20
        ),
        name="scatter_plane",
    )(part)
    return out.reshape(pieces * 2 * rows, cols)


def sum_kernel(n_z, bits, vec_ref, out_ref, held, arrived, from_z, send_sem, z_send, recv_sem, z_recv):
    z = lax.axis_index("gx")
    g = lax.axis_index("gy")
    half = vec_ref.shape[1]
    side = lax.rem(g, 2)
    core = {"gx": z, "gy": g + 1 - 2 * (g % 2)}
    peers = [
        {"gx": z, "gy": g + bit - 2 * bit * ((g // bit) % 2)}
        for bit in (2**power for power in range(1, bits))
    ]
    others = [{"gx": lax.rem(z + j, n_z), "gy": g} for j in range(1, n_z)]
    barrier_with([(z >= 0, peer) for peer in (core, *peers, *others)])

    def remote(src, dst, ssem, rsem, peer):
        return pltpu.make_async_remote_copy(
            src_ref=src,
            dst_ref=dst,
            send_sem=ssem,
            recv_sem=rsem,
            device_id=peer,
            device_id_type=pl.DeviceIdType.MESH,
        )

    first = remote(vec_ref.at[1 - side], arrived.at[0], send_sem.at[0], recv_sem.at[0], core)
    first.start()
    first.wait()
    held[0] = vec_ref[side] + arrived[0]
    for k, peer in enumerate(peers, 1):
        step = remote(held.at[k - 1], arrived.at[k], send_sem.at[k], recv_sem.at[k], peer)
        step.start()
        step.wait()
        held[k] = held[k - 1] + arrived[k]
    copies = [
        remote(held.at[bits - 1], from_z.at[j], z_send.at[j], z_recv.at[j], peer)
        for j, peer in enumerate(others)
    ]
    for copy in copies:
        copy.start()
    for copy in copies:
        copy.wait()
    total = jnp.zeros_like(held[0])
    for owner in range(n_z):
        term = held[bits - 1]
        for j in range(1, n_z):
            term = jnp.where(lax.rem(z - j + n_z, n_z) == owner, from_z[j - 1], term)
        total = total + term
    held[bits] = total
    last = remote(held.at[bits], arrived.at[bits], send_sem.at[bits], recv_sem.at[bits], core)
    last.start()
    out_ref[side] = total
    last.wait()
    out_ref[1 - side] = arrived[bits]


def sum_everywhere(vector, collective_id):
    n_z = lax.axis_size("gx")
    bits = lax.axis_size("gy").bit_length() - 1
    lanes = 128
    length = vector.shape[0]
    rows = -(-length // (lanes * 16)) * 8
    padded = jnp.pad(vector, (0, 2 * rows * lanes - length)).reshape(2, rows, lanes)
    dma = pltpu.SemaphoreType.DMA
    out = pl.pallas_call(
        partial(sum_kernel, n_z, bits),
        out_shape=jax.ShapeDtypeStruct((2, rows, lanes), jnp.float32),
        in_specs=[pl.BlockSpec(memory_space=pltpu.VMEM)],
        out_specs=pl.BlockSpec(memory_space=pltpu.VMEM),
        scratch_shapes=[
            pltpu.VMEM((bits + 1, rows, lanes), jnp.float32),
            pltpu.VMEM((bits + 1, rows, lanes), jnp.float32),
            pltpu.VMEM((n_z - 1, rows, lanes), jnp.float32),
            dma((bits + 1,)),
            dma((n_z - 1,)),
            dma((bits + 1,)),
            dma((n_z - 1,)),
        ],
        compiler_params=pltpu.CompilerParams(collective_id=collective_id, has_side_effects=True),
        name="sum_everywhere",
    )(padded)
    return out.reshape(-1)[:length]


def enter_kernel(
    n_z,
    span,
    acts_ref,
    weight_ref,
    cot_ref,
    seq_ref,
    full_ref,
    all_cot_ref,
    send_sem,
    recv_sem,
    local_sem,
    chain_send,
    chain_recv,
    chain_local,
    cot_send,
    cot_recv,
    cot_local,
):
    greet(n_z)
    start, relays, end_chain = chain_gather(
        n_z, weight_ref, full_ref, chain_send, chain_recv, chain_local
    )
    near, end_near = gather_steps(1, span, acts_ref, seq_ref, send_sem, recv_sem, local_sem)
    far, end_far = gather_steps(n_z, span, cot_ref, all_cot_ref, cot_send, cot_recv, cot_local)
    start()
    near[0]()
    far[0]()
    near[1]()
    near[2]()
    for k, step in enumerate(far[1:]):
        if k % 2 == 0 and k // 2 < len(relays):
            relays[k // 2]()
        step()
    for relay in relays[len(far) // 2 :]:
        relay()
    end_chain()
    end_near()
    end_far()


def enter(acts, weights, cotangent, collective_id):
    n_z = lax.axis_size("gx")
    span = lax.axis_size("gy")
    rows, cols = acts.shape
    dma = pltpu.SemaphoreType.DMA
    half = (2, rows // 2, cols)
    seq, full, all_cot = pl.pallas_call(
        partial(enter_kernel, n_z, span),
        out_shape=(
            jax.ShapeDtypeStruct((span,) + half, acts.dtype),
            jax.ShapeDtypeStruct((n_z,) + weights.shape, weights.dtype),
            jax.ShapeDtypeStruct((n_z * span,) + half, cotangent.dtype),
        ),
        in_specs=[pl.BlockSpec(memory_space=pltpu.VMEM)] * 3,
        out_specs=(pl.BlockSpec(memory_space=pl.ANY),) * 3,
        scratch_shapes=[
            dma((24,)),
            dma((span, 2)),
            dma,
            dma((2 * n_z,)),
            dma((n_z,)),
            dma,
            dma((24 * (2 * n_z - 1),)),
            dma((n_z * span, 2)),
            dma,
        ],
        compiler_params=pltpu.CompilerParams(collective_id=collective_id, has_side_effects=True),
        name="enter",
    )(acts.reshape(half), weights, cotangent.reshape(half))
    return (
        seq.reshape(span * rows, cols),
        full.reshape(n_z * weights.shape[0], weights.shape[1]),
        all_cot.reshape(n_z * span * rows, cols),
    )


def chain_scatter(n_z, part_ref, out_ref, from_low, from_high, send_sem, low_recv, high_recv):
    z = lax.axis_index("gx")
    g = lax.axis_index("gy")
    rows = part_ref.shape[1]

    def up(dest):
        return pltpu.make_async_remote_copy(
            src_ref=part_ref.at[dest],
            dst_ref=from_low.at[dest],
            send_sem=send_sem.at[dest],
            recv_sem=low_recv.at[dest],
            device_id={"gx": z + 1, "gy": g},
            device_id_type=pl.DeviceIdType.MESH,
        )

    def down(dest):
        return pltpu.make_async_remote_copy(
            src_ref=part_ref.at[dest],
            dst_ref=from_high.at[dest],
            send_sem=send_sem.at[dest],
            recv_sem=high_recv.at[dest],
            device_id={"gx": z - 1, "gy": g},
            device_id_type=pl.DeviceIdType.MESH,
        )

    def start():
        for k in range(n_z - 1):
            run_if(z == 0, lambda k=k: up(n_z - 1 - k).start())
            run_if(z == n_z - 1, lambda k=k: down(k).start())

    def pass_up(dest):
        up(dest).wait_recv()
        add_into(part_ref.at[dest], (part_ref.at[dest], from_low.at[dest]), rows)
        up(dest).start()

    def pass_down(dest):
        down(dest).wait_recv()
        add_into(part_ref.at[dest], (part_ref.at[dest], from_high.at[dest]), rows)
        down(dest).start()

    def relay(time):
        for k in range(time):
            low, dest = time - k, n_z - 1 - k
            if 0 < low < dest:
                run_if(z == low, partial(pass_up, dest))
            high, dest = n_z - 1 - (time - k), k
            if dest < high < n_z - 1:
                run_if(z == high, partial(pass_down, dest))

    def finish():
        for dest in range(n_z):
            terms = [part_ref.at[dest]]
            terms += [from_low.at[dest]] if dest > 0 else []
            terms += [from_high.at[dest]] if dest < n_z - 1 else []

            def last(dest=dest, terms=terms):
                if dest > 0:
                    up(dest).wait_recv()
                if dest < n_z - 1:
                    down(dest).wait_recv()
                add_into(out_ref, terms, rows)

            run_if(z == dest, last)
        for dest in range(n_z):
            run_if(z != dest, lambda dest=dest: up(dest).wait_send())

    return start, [partial(relay, time) for time in range(1, n_z)], finish


def leave_kernel(
    n_i,
    rows,
    part_ref,
    weight_ref,
    out_ref,
    weight_out,
    held,
    from_core,
    from_a,
    from_b,
    from_z,
    sums,
    from_low,
    from_high,
    load_sem,
    core_send,
    a_send,
    b_send,
    z_send,
    core_recv,
    a_recv,
    b_recv,
    z_recv,
    copy_sem,
    chain_send,
    low_recv,
    high_recv,
):
    n_z = lax.axis_size("gx")
    copy = pltpu.make_async_copy(weight_ref, sums, copy_sem)
    copy.start()
    chain = chain_scatter(
        n_z, sums, weight_out, from_low, from_high, chain_send, low_recv, high_recv
    )

    def start():
        copy.wait()
        chain[0]()

    scatter_kernel(
        False,
        n_i,
        rows,
        part_ref,
        out_ref,
        held,
        from_core,
        from_a,
        from_b,
        from_z,
        load_sem,
        core_send,
        a_send,
        b_send,
        z_send,
        core_recv,
        a_recv,
        b_recv,
        z_recv,
        (start, chain[1], chain[2]),
    )


def leave(part, weight_part, collective_id):
    n_z = lax.axis_size("gx")
    span = lax.axis_size("gy")
    pieces, _, _, rows, cols = part.shape
    total = span * pieces * 2 * rows
    half = (rows, cols)
    dma = pltpu.SemaphoreType.DMA
    block = (weight_part.shape[0] // n_z, weight_part.shape[1])
    out, sums = pl.pallas_call(
        partial(leave_kernel, pieces, rows),
        out_shape=(
            jax.ShapeDtypeStruct((pieces, 2, rows, cols), jnp.float32),
            jax.ShapeDtypeStruct(block, jnp.float32),
        ),
        in_specs=[pl.BlockSpec(memory_space=pl.ANY)] * 2,
        out_specs=(pl.BlockSpec(memory_space=pltpu.VMEM),) * 2,
        scratch_shapes=[
            pltpu.VMEM((pieces, 4, 2) + half, jnp.bfloat16),
            pltpu.VMEM((pieces, 4, 2) + half, jnp.bfloat16),
            pltpu.VMEM((pieces, 2, 2) + half, jnp.bfloat16),
            pltpu.VMEM((pieces, 2) + half, jnp.bfloat16),
            pltpu.VMEM((1, 2, 16, 128), jnp.bfloat16),
            pltpu.VMEM((n_z,) + block, jnp.bfloat16),
            pltpu.VMEM((n_z,) + block, jnp.bfloat16),
            pltpu.VMEM((n_z,) + block, jnp.bfloat16),
            dma((pieces, 4)),
            dma((pieces, 4)),
            dma((pieces, 4)),
            dma((pieces, 2)),
            dma((pieces,)),
            dma((pieces, 4)),
            dma((pieces, 2, 2)),
            dma((pieces, 2)),
            dma((pieces,)),
            dma,
            dma((n_z,)),
            dma((n_z,)),
            dma((n_z,)),
        ],
        compiler_params=pltpu.CompilerParams(
            collective_id=collective_id, has_side_effects=True, vmem_limit_bytes=60 << 20
        ),
        name="leave",
    )(part, weight_part.reshape((n_z,) + block))
    return out.reshape(total // span, cols), sums


def expert_kernel(n_z, span, own_ref, cot_ref, share_ref, gate_ref, up_ref, down_ref,
                  all_ref, pair_ref, dots_ref, down_out, out_ref,
                  moe_buf, cot_buf, share_buf, pair_stage, dots_buf,
                  gate_val, up_val, scaled, scaled_t, down_t,
                  held, from_core, from_a, from_b, from_z,
                  send_sem, recv_sem, local_sem, fetch_sem, store_sem,
                  core_send, a_send, b_send, z_send, core_recv, a_recv, b_recv, z_recv):
    z = lax.axis_index("gx")
    g = lax.axis_index("gy")
    rows = own_ref.shape[1]
    block = 2 * rows
    step_rows = moe_buf.shape[1]
    steps = 2 * n_z
    flip_x = g + 2 - 4 * ((g // 2) % 2)
    flip_y = g + 4 - 8 * ((g // 4) % 2)
    flip_both = flip_x + flip_y - g
    core = {"gx": z, "gy": flip(g)}
    x_peer = {"gx": z, "gy": flip_x}
    y_peer = {"gx": z, "gy": flip_y}
    above = {"gx": z + 1, "gy": g}
    below = {"gx": z - 1, "gy": g}

    order = [z]
    candidates = []
    for d in range(1, n_z):
        candidates += [(z >= d, z - d), (z < n_z - d, z + d)]
    for k in range(1, n_z):
        rank, chosen = 0, 0
        for ok, owner in candidates:
            ok = ok.astype(jnp.int32)
            rank = rank + ok
            chosen = chosen + ok * (rank == k).astype(jnp.int32) * owner
        order.append(chosen)

    onward = [(z < n_z - 1, z > 0)]
    for owner in order[1:]:
        onward.append(
            (
                jnp.logical_and(owner < z, z < n_z - 1),
                jnp.logical_and(owner > z, z > 0),
            )
        )
    along = [{"gx": lax.rem(z + j, n_z), "gy": g} for j in range(1, n_z)]
    barrier_with([(z >= 0, peer) for peer in (core, x_peer, y_peer, *along)])

    def at(owner, gg, h):
        return pl.ds(pl.multiple_of((owner * span + gg) * block + h * rows, rows), rows)

    def copy(k, slot, owner, gg, h, peer, own=False):
        return pltpu.make_async_remote_copy(
            src_ref=own_ref.at[h] if own else all_ref.at[at(owner, gg, h)],
            dst_ref=all_ref.at[at(owner, gg, h)],
            send_sem=send_sem.at[k, slot],
            recv_sem=recv_sem.at[owner * span + gg, h],
            device_id=peer,
            device_id_type=pl.DeviceIdType.MESH,
        )

    sends = []

    def send(ok, *where, **options):
        k = where[0]
        slot = sum(1 for entry in sends if entry[2] == k)
        make = partial(copy, k, slot, *where[1:], **options)
        sends.append((ok, make, k))
        run_if(ok, lambda: make().start())

    def arrive(owner, gg, h):
        copy(0, 0, owner, gg, h, core).wait_recv()

    locals_ = [
        pltpu.make_async_copy(own_ref.at[h], all_ref.at[at(z, g, h)], local_sem.at[h])
        for h in range(2)
    ]

    def first(k):
        owner = order[k]
        own = k == 0
        if own:
            for item in locals_:
                item.start()
        else:
            arrive(owner, g, 0)
            arrive(owner, g, 1)
        go_up, go_down = onward[k]
        for h in range(2):
            send(go_up, k, owner, g, h, above, own=own)
            send(go_down, k, owner, g, h, below, own=own)
        send(True, k, owner, g, 0, x_peer, own=own)
        send(True, k, owner, g, 1, y_peer, own=own)
        send(True, k, owner, g, 1, x_peer, own=own)
        send(True, k, owner, g, 0, y_peer, own=own)
        send(True, k, owner, g, 0, core, own=own)
        send(True, k, owner, g, 1, core, own=own)

    def second(k):
        owner = order[k]
        arrive(owner, flip_x, 0)
        send(True, k, owner, flip_x, 0, y_peer)
        send(True, k, owner, flip_x, 0, core)
        arrive(owner, flip_y, 1)
        send(True, k, owner, flip_y, 1, x_peer)
        send(True, k, owner, flip_y, 1, core)

    def third(k):
        owner = order[k]
        for gg, h in ((flip_y, 0), (flip_x, 1), (flip_both, 0), (flip_both, 1)):
            arrive(owner, gg, h)
            send(True, k, owner, gg, h, core)

    def complete(k):
        for gg in (g, flip_x, flip_y, flip_both):
            for h in range(2):
                arrive(order[k], flip(gg), h)
        if k == 0:
            for item in locals_:
                item.wait()

    def place(s):
        k, side = (s // 2, s % 2) if isinstance(s, int) else (lax.div(s, 2), lax.rem(s, 2))
        if isinstance(s, int):
            owner = order[k]
        else:
            owner = sum((k == j).astype(jnp.int32) * order[j] for j in range(n_z))
        return pl.ds(pl.multiple_of(owner * (span * block) + side * step_rows, step_rows), step_rows)

    def parity(s):
        return s % 2 if isinstance(s, int) else lax.rem(s, 2)

    def fetches(s):
        slot = parity(s)
        return [
            pltpu.make_async_copy(source.at[place(s)], target.at[slot], fetch_sem.at[j, slot])
            for j, (source, target) in enumerate(
                ((all_ref, moe_buf), (cot_ref, cot_buf), (share_ref, share_buf))
            )
        ]

    def stores(s):
        slot = parity(s)
        pairs = ((dots_buf, dots_ref), (pair_stage, pair_ref))
        return [
            pltpu.make_async_copy(
                pairs[j][0].at[slot], pairs[j][1].at[place(s)], store_sem.at[j, slot]
            )
            for j in range(2)
        ]

    f32 = jnp.float32
    dot = partial(lax.dot_general, preferred_element_type=f32)
    plain = (((1,), (0,)), ((), ()))
    last_dims = (((1,), (1,)), ((), ()))
    first_dims = (((0,), (0,)), ((), ()))
    half_width = scaled.shape[1]
    width = moe_buf.shape[2]
    tile = 256

    quads = (flip_both, flip_x, flip_y, g)

    def remote(src, dst, ssem, rsem, peer):
        return pltpu.make_async_remote_copy(
            src_ref=src,
            dst_ref=dst,
            send_sem=ssem,
            recv_sem=rsem,
            device_id=peer,
            device_id_type=pl.DeviceIdType.MESH,
        )

    def core_copy(k, q):
        return remote(
            held.at[k, flip(quads[q])],
            from_core.at[k, q],
            core_send.at[k, q],
            core_recv.at[k, q],
            core,
        )

    a_plan = ((0, 0, 0, x_peer), (0, 1, 0, y_peer), (1, 0, 1, x_peer), (2, 1, 1, y_peer))

    def a_copy(k, j):
        q, h, slot, peer = a_plan[j]
        return remote(
            held.at[k, quads[q], h],
            from_a.at[k, h, slot],
            a_send.at[k, j],
            a_recv.at[k, h, slot],
            peer,
        )

    b_plan = ((2, y_peer), (1, x_peer))

    def b_copy(k, h):
        q, peer = b_plan[h]
        return remote(
            held.at[k, quads[q], h], from_b.at[k, h], b_send.at[k, h], b_recv.at[k, h], peer
        )

    def z_copy(k):
        return remote(
            held.at[k, g], from_z.at[z], z_send.at[k], z_recv.at[z], {"gx": order[k], "gy": g}
        )

    def stage_core(k):
        for q in range(4):
            core_copy(k, q).start()

    def stage_a(k):
        for q in range(4):
            core_copy(k, q).wait_recv()
            for h in range(2):
                mine = held.at[k, quads[q], h]
                add_into(mine, (mine, from_core.at[k, q, h]), rows)
            for j in range(4):
                if a_plan[j][0] == q:
                    a_copy(k, j).start()

    def stage_b(k):
        for q, h, slot in ((2, 0, 0), (1, 1, 0), (3, 0, 1), (3, 1, 1)):
            mine, arrived = held.at[k, quads[q], h], from_a.at[k, h, slot]
            remote(mine, arrived, a_send.at[k, 0], a_recv.at[k, h, slot], core).wait_recv()
            add_into(mine, (mine, arrived), rows)
            if slot == 0:
                b_copy(k, h).start()

    def stage_c(k):
        for h in range(2):
            b_copy(k, h).wait_recv()
            mine = held.at[k, g, h]
            add_into(mine, (mine, from_b.at[k, h]), rows)
        if k > 0:
            z_copy(k).start()

    backs = (
        (stage_core, lambda k: 2 * k + 1, 2),
        (stage_a, lambda k: 2 * k + 2, 2),
        (stage_b, lambda k: 2 * k + 3, 2),
        (stage_c, lambda k: 2 * k + 4, 1),
    )

    def events(s, phase):
        for action, start, when in backs:
            for k in range(n_z):
                if when == phase and start(k) < steps:
                    pl.when(s == start(k))(partial(action, k))
        for k in range(1, n_z):
            if k >= 2 and phase == 1:
                pl.when(s == k - 2)(partial(first, k))
            if phase == 2:
                pl.when(s == 2 * (k - 1))(partial(second, k))
            if phase == 2:
                pl.when(s == 2 * (k - 1) + 1)(partial(third, k))
            if phase == 4:
                pl.when(s == 2 * k - 1)(partial(complete, k))

    first(0)

    @pl.loop(0, width // tile)
    def _(t):
        cols = pl.ds(pl.multiple_of(t * tile, tile), tile)
        down_t[cols, :] = down_ref[:, cols].T

    second(0)
    if n_z > 1:
        first(1)
    third(0)
    complete(0)
    for item in fetches(0):
        item.start()

    @pl.loop(0, steps)
    def _(s):
        slot = lax.rem(s, 2)
        moe, cot, share = moe_buf.at[slot], cot_buf.at[slot], share_buf.at[slot]
        for item in fetches(s):
            item.wait()

        @pl.when(s >= 2)
        def _():
            for item in stores(s - 2):
                item.wait()

        wide = jnp.concatenate([share[...]] * (tile // share.shape[1]), axis=1)

        @pl.loop(0, half_width // tile)
        def _(t):
            cols = pl.ds(pl.multiple_of(t * tile, tile), tile)
            gated = dot(moe[...], gate_ref[:, cols], plain)
            lifted = dot(moe[...], up_ref[:, cols], plain)
            gate_val[:, cols] = gated
            up_val[:, cols] = lifted
            scaled[:, cols] = (gated * jax.nn.sigmoid(gated) * lifted * wide).astype(jnp.bfloat16)

        events(s, 1)
        scaled_t[...] = scaled[...].T

        @pl.loop(0, width // (2 * tile))
        def _(t):
            cols = pl.ds(pl.multiple_of(t * 2 * tile, 2 * tile), 2 * tile)
            sent = dot(scaled[...], down_ref[:, cols], plain).astype(jnp.bfloat16)
            held[lax.div(s, 2), pl.ds(slot * (span // 2), span // 2), :, :, cols] = sent.reshape(
                (span // 2, 2, rows, 2 * tile)
            )

        events(s, 2)
        dots_buf[slot] = jnp.zeros(dots_buf.shape[1:], f32)

        @pl.loop(0, half_width // tile)
        def _(t):
            cols = pl.ds(pl.multiple_of(t * tile, tile), tile)
            pulled = dot(cot[...], down_t[:, cols], plain)
            gated = gate_val[:, cols]
            lifted = up_val[:, cols]
            sig = jax.nn.sigmoid(gated)
            silu = gated * sig
            product = pulled * (silu * lifted)
            lanes = share.shape[1]
            dots_buf[slot] = dots_buf[slot] + sum(
                product[:, j * lanes : (j + 1) * lanes] for j in range(tile // lanes)
            )
            pulled = pulled * wide
            pair_stage[slot, :, cols] = (pulled * lifted * sig * (1.0 + gated * (1.0 - sig))).astype(
                jnp.bfloat16
            )
            more = pl.ds(pl.multiple_of(half_width + t * tile, tile), tile)
            pair_stage[slot, :, more] = (pulled * silu).astype(jnp.bfloat16)

        for item in stores(s):
            item.start()
        events(s, 3)
        events(s, 4)

        @pl.when(s < steps - 1)
        def _():
            for item in fetches(s + 1):
                item.start()

        @pl.loop(0, width // (2 * tile))
        def _(t):
            cols = pl.ds(pl.multiple_of(t * 2 * tile, 2 * tile), 2 * tile)
            grown = dot(scaled_t[...], cot[:, cols], plain)
            down_out[:, cols] = jnp.where(s == 0, 0.0, down_out[:, cols]) + grown

    for t in range(steps, 2 * steps):
        for action, start, _ in backs[::-1]:
            for k in range(n_z):
                if start(k) == t:
                    action(k)
    for s in (steps - 2, steps - 1):
        for item in stores(s):
            item.wait()
    for k in range(1, n_z):
        arrived = from_z.at[order[k]]
        remote(held.at[k, g], arrived, z_send.at[k], z_recv.at[order[k]], core).wait_recv()
    for h in range(2):
        terms = [held.at[0, g, h]] + [from_z.at[order[k], h] for k in range(1, n_z)]
        add_into(out_ref.at[h], terms, rows)
    for k in range(n_z):
        for q in range(4):
            core_copy(k, q).wait_send()
        for j in range(4):
            a_copy(k, j).wait_send()
        for h in range(2):
            b_copy(k, h).wait_send()
        if k > 0:
            z_copy(k).wait_send()
    for ok, make, k in sends:
        run_if(ok, lambda make=make: make().wait_send())


def run_experts(moe_in, all_cot, shares, gate_w, up_w, down_w, collective_id):
    n_z = lax.axis_size("gx")
    span = lax.axis_size("gy")
    rows, width = moe_in.shape
    half = down_w.shape[0]
    total = n_z * span * rows
    step = span * rows // 2
    lanes = shares.shape[1]
    bf16, f32 = jnp.bfloat16, jnp.float32
    dma = pltpu.SemaphoreType.DMA
    vmem = pl.BlockSpec(memory_space=pltpu.VMEM)
    hbm = pl.BlockSpec(memory_space=pl.ANY)
    return pl.pallas_call(
        partial(expert_kernel, n_z, span),
        out_shape=(
            jax.ShapeDtypeStruct((total, width), bf16),
            jax.ShapeDtypeStruct((total, 2 * half), bf16),
            jax.ShapeDtypeStruct((total, lanes), f32),
            jax.ShapeDtypeStruct((half, width), f32),
            jax.ShapeDtypeStruct((2, rows // 2, width), f32),
        ),
        in_specs=[vmem, hbm, hbm, vmem, vmem, vmem],
        out_specs=(hbm, hbm, hbm, vmem, vmem),
        scratch_shapes=[
            pltpu.VMEM((2, step, width), bf16),
            pltpu.VMEM((2, step, width), bf16),
            pltpu.VMEM((2, step, lanes), f32),
            pltpu.VMEM((2, step, 2 * half), bf16),
            pltpu.VMEM((2, step, lanes), f32),
            pltpu.VMEM((step, half), f32),
            pltpu.VMEM((step, half), f32),
            pltpu.VMEM((step, half), bf16),
            pltpu.VMEM((half, step), bf16),
            pltpu.VMEM((width, half), bf16),
            pltpu.VMEM((n_z, span, 2, rows // 2, width), bf16),
            pltpu.VMEM((n_z, 4, 2, rows // 2, width), bf16),
            pltpu.VMEM((n_z, 2, 2, rows // 2, width), bf16),
            pltpu.VMEM((n_z, 2, rows // 2, width), bf16),
            pltpu.VMEM((n_z, 2, rows // 2, width), bf16),
            dma((n_z, 18)),
            dma((n_z * span, 2)),
            dma((2,)),
            dma((3, 2)),
            dma((2, 2)),
            dma((n_z, 4)),
            dma((n_z, 4)),
            dma((n_z, 2)),
            dma((n_z,)),
            dma((n_z, 4)),
            dma((n_z, 2, 2)),
            dma((n_z, 2)),
            dma((n_z,)),
        ],
        compiler_params=pltpu.CompilerParams(
            collective_id=collective_id, has_side_effects=True, vmem_limit_bytes=67043328
        ),
        name="experts",
    )(moe_in.reshape(2, rows // 2, width), all_cot, shares, gate_w, up_w, down_w)


def pull_kernel(n_i, rows, all_ref, pair_ref, gate_ref, up_ref, out_ref, gate_out, up_out,
                held, from_core, from_a, from_b, from_z, moe_buf, pair_buf,
                fetch_sem, core_send, a_send, b_send, z_send, core_recv, a_recv, b_recv, z_recv):
    z = lax.axis_index("gx")
    g = lax.axis_index("gy")
    flip_x = g + 2 - 4 * ((g // 2) % 2)
    flip_y = g + 4 - 8 * ((g // 4) % 2)
    quads = (flip_x + flip_y - g, flip_x, flip_y, g)
    core = {"gx": z, "gy": flip(g)}
    x_peer = {"gx": z, "gy": flip_x}
    y_peer = {"gx": z, "gy": flip_y}
    along = [{"gx": lax.rem(z + j, n_i), "gy": g} for j in range(1, n_i)]
    barrier_with([(z >= 0, peer) for peer in (core, x_peer, y_peer, *along)])
    item_rows = moe_buf.shape[1]
    width = moe_buf.shape[2]
    half_width = gate_out.shape[1]
    owners = [lax.rem(z + n_i - 1 - i + n_i, n_i) for i in range(n_i)]

    def remote(src, dst, ssem, rsem, peer):
        return pltpu.make_async_remote_copy(
            src_ref=src,
            dst_ref=dst,
            send_sem=ssem,
            recv_sem=rsem,
            device_id=peer,
            device_id_type=pl.DeviceIdType.MESH,
        )

    def fetches(i):
        place = pl.ds(pl.multiple_of(owners[i] * item_rows, item_rows), item_rows)
        return [
            pltpu.make_async_copy(all_ref.at[place], moe_buf.at[i % 2], fetch_sem.at[0, i % 2]),
            pltpu.make_async_copy(pair_ref.at[place], pair_buf.at[i % 2], fetch_sem.at[1, i % 2]),
        ]

    def core_copy(i, q):
        return remote(
            held.at[i, flip(quads[q])],
            from_core.at[i, q],
            core_send.at[i, q],
            core_recv.at[i, q],
            core,
        )

    a_plan = ((0, 0, 0, x_peer), (0, 1, 0, y_peer), (1, 0, 1, x_peer), (2, 1, 1, y_peer))

    def a_copy(i, k):
        q, h, slot, peer = a_plan[k]
        return remote(
            held.at[i, quads[q], h],
            from_a.at[i, h, slot],
            a_send.at[i, k],
            a_recv.at[i, h, slot],
            peer,
        )

    b_plan = ((2, y_peer), (1, x_peer))

    def b_copy(i, h):
        q, peer = b_plan[h]
        return remote(
            held.at[i, quads[q], h], from_b.at[i, h], b_send.at[i, h], b_recv.at[i, h], peer
        )

    def z_copy(i):
        return remote(
            held.at[i, g], from_z.at[z], z_send.at[i], z_recv.at[z], {"gx": owners[i], "gy": g}
        )

    dot = partial(lax.dot_general, preferred_element_type=jnp.float32)
    last_dims = (((1,), (1,)), ((), ()))
    first_dims = (((0,), (0,)), ((), ()))

    def multiply(i):
        for copy in fetches(i):
            copy.wait()
        pair = pair_buf.at[i % 2]
        tile = 256

        @pl.loop(0, width // tile)
        def _(t):
            cols = pl.ds(pl.multiple_of(t * tile, tile), tile)
            total = dot(pair[:, :half_width], gate_ref[cols, :], last_dims)
            total = total + dot(pair[:, half_width:], up_ref[cols, :], last_dims)
            held[i, :, :, :, cols] = total.astype(jnp.bfloat16).reshape(held.shape[1:4] + (tile,))

        for q in range(4):
            core_copy(i, q).start()

    def accumulate(i):
        moe, pair = moe_buf.at[i % 2], pair_buf.at[i % 2]
        tile = 256

        @pl.loop(0, width // tile)
        def _(t):
            cols = pl.ds(pl.multiple_of(t * tile, tile), tile)
            grown = dot(moe[:, cols], pair[...], first_dims)
            if i == 0:
                gate_out[cols, :] = grown[:, :half_width]
                up_out[cols, :] = grown[:, half_width:]
            else:
                gate_out[cols, :] = gate_out[cols, :] + grown[:, :half_width]
                up_out[cols, :] = up_out[cols, :] + grown[:, half_width:]

        if i + 2 < n_i:
            for copy in fetches(i + 2):
                copy.start()

    def stage_a(i):
        for q in range(4):
            core_copy(i, q).wait_recv()
            for h in range(2):
                mine = held.at[i, quads[q], h]
                add_into(mine, (mine, from_core.at[i, q, h]), rows)
            for k in range(4):
                if a_plan[k][0] == q:
                    a_copy(i, k).start()

    def stage_b(i):
        for q, h, slot in ((2, 0, 0), (1, 1, 0), (3, 0, 1), (3, 1, 1)):
            mine, arrived = held.at[i, quads[q], h], from_a.at[i, h, slot]
            remote(mine, arrived, a_send.at[i, 0], a_recv.at[i, h, slot], core).wait_recv()
            add_into(mine, (mine, arrived), rows)
            if slot == 0:
                b_copy(i, h).start()

    def stage_c(i):
        for h in range(2):
            b_copy(i, h).wait_recv()
            mine = held.at[i, g, h]
            add_into(mine, (mine, from_b.at[i, h]), rows)
        if i < n_i - 1:
            z_copy(i).start()
        else:
            for j in range(n_i - 1):
                arrived = from_z.at[owners[j]]
                remote(held.at[j, g], arrived, z_send.at[j], z_recv.at[owners[j]], core).wait_recv()
            for h in range(2):
                terms = [held.at[i, g, h]] + [from_z.at[owners[j], h] for j in range(n_i - 1)]
                add_into(out_ref.at[h], terms, rows)

    for i in range(min(2, n_i)):
        for copy in fetches(i):
            copy.start()
    for t in range(n_i + 3):
        if t < n_i:
            multiply(t)
        if 0 <= t - 1 < n_i:
            stage_a(t - 1)
        if 0 <= t - 2 < n_i:
            stage_b(t - 2)
        if 0 <= t - 1 < n_i:
            accumulate(t - 1)
        if 0 <= t - 3 < n_i:
            stage_c(t - 3)
    for i in range(n_i):
        for q in range(4):
            core_copy(i, q).wait_send()
        for k in range(4):
            a_copy(i, k).wait_send()
        for h in range(2):
            b_copy(i, h).wait_send()
        if i < n_i - 1:
            z_copy(i).wait_send()


def pull_experts(all_moe, pair, gate_w, up_w, collective_id):
    n_i = lax.axis_size("gx")
    span = lax.axis_size("gy")
    total, width = all_moe.shape
    half_width = gate_w.shape[1]
    rows = total // (n_i * span) // 2
    half = (rows, width)
    bf16 = jnp.bfloat16
    dma = pltpu.SemaphoreType.DMA
    vmem = pl.BlockSpec(memory_space=pltpu.VMEM)
    hbm = pl.BlockSpec(memory_space=pl.ANY)
    out, gate_part, up_part = pl.pallas_call(
        partial(pull_kernel, n_i, rows),
        out_shape=(
            jax.ShapeDtypeStruct((2,) + half, jnp.float32),
            jax.ShapeDtypeStruct((width, half_width), jnp.float32),
            jax.ShapeDtypeStruct((width, half_width), jnp.float32),
        ),
        in_specs=[hbm, hbm, vmem, vmem],
        out_specs=(vmem, vmem, vmem),
        scratch_shapes=[
            pltpu.VMEM((n_i, span, 2) + half, bf16),
            pltpu.VMEM((n_i, 4, 2) + half, bf16),
            pltpu.VMEM((n_i, 2, 2) + half, bf16),
            pltpu.VMEM((n_i, 2) + half, bf16),
            pltpu.VMEM((n_i, 2) + half, bf16),
            pltpu.VMEM((2, span * 2 * rows, width), bf16),
            pltpu.VMEM((2, span * 2 * rows, 2 * half_width), bf16),
            dma((2, 2)),
            dma((n_i, 4)),
            dma((n_i, 4)),
            dma((n_i, 2)),
            dma((n_i,)),
            dma((n_i, 4)),
            dma((n_i, 2, 2)),
            dma((n_i, 2)),
            dma((n_i,)),
        ],
        compiler_params=pltpu.CompilerParams(
            collective_id=collective_id, has_side_effects=True, vmem_limit_bytes=67043328
        ),
        name="pull_experts",
    )(all_moe, pair, gate_w, up_w)
    return out.reshape(2 * rows, width), gate_part, up_part


def turn(values, cosine, sine):
    return values * cosine + pltpu.roll(values, values.shape[-1] // 2, 1) * sine


def attend_kernel(
    heads,
    pieces,
    acts_ref,
    weight_ref,
    out_weight_ref,
    query_gain,
    key_gain,
    cosine_ref,
    sine_ref,
    row_docs,
    col_docs,
    part_ref,
    query_raw,
    key_raw,
    ready_ref,
    mixed_ref,
    totals_ref,
    peaks_ref,
):
    f32, bf16 = jnp.float32, jnp.bfloat16
    dot = partial(lax.dot_general, preferred_element_type=f32)
    plain = (((1,), (0,)), ((), ()))
    last_dims = (((1,), (1,)), ((), ()))
    length = acts_ref.shape[0]
    span = part_ref.shape[1]
    local = heads * HD
    block = 256
    scale = HD ** (-0.5)

    for source, raw, gain in ((0, query_raw, query_gain), (1, key_raw, key_gain)):
        raw[...] = dot(acts_ref[...], weight_ref[:, source * local : (source + 1) * local], plain)
        for h in range(heads):
            cols = slice(h * HD, (h + 1) * HD)

            @pl.loop(0, length // block)
            def _(t):
                at = pl.ds(pl.multiple_of(t * block, block), block)
                value = raw[at, cols]
                normed = value * lax.rsqrt(jnp.mean(value * value, axis=-1, keepdims=True) + EPSILON)
                turned = turn(normed * gain[...], cosine_ref[at, :], sine_ref[at, :])
                where = source * local + h * HD
                ready_ref[at, where : where + HD] = turned.astype(bf16)

    ready_ref[:, 2 * local :] = dot(acts_ref[...], weight_ref[:, 2 * local :], plain).astype(bf16)
    lanes = lax.broadcasted_iota(jnp.int32, (block, HD), 1)
    peaks_ref[...] = jnp.full(peaks_ref.shape, NEGATIVE, f32)

    @pl.loop(0, length // block)
    def _(t):
        at = pl.ds(pl.multiple_of(t * block, block), block)
        same = row_docs[at, :1] == col_docs[:1, :]
        kept = jnp.zeros((block, HD), f32)
        for h in range(heads):
            query = ready_ref[at, h * HD : (h + 1) * HD]
            key = ready_ref[:, local + h * HD : local + (h + 1) * HD]
            value = ready_ref[:, 2 * local + h * HD : 2 * local + (h + 1) * HD]
            scores = jnp.where(same, dot(query, key, last_dims) * scale, NEGATIVE)
            highest = jnp.max(scores, axis=-1, keepdims=True)
            weights = jnp.exp(scores - highest)
            total = jnp.sum(weights, axis=-1, keepdims=True)
            shares = (weights * (1.0 / total)).astype(bf16)
            mixed_ref[at, h * HD : (h + 1) * HD] = dot(shares, value, plain).astype(bf16)
            kept = jnp.where(lanes == h, highest + jnp.log(total), kept)
            top = jnp.max(highest, axis=0, keepdims=True)
            peaks_ref[h : h + 1, :] = jnp.maximum(peaks_ref[h : h + 1, :], top)
        totals_ref[at, :] = kept

    rows = part_ref.shape[3]

    @pl.loop(0, out_weight_ref.shape[1] // block)
    def _(t):
        cols = pl.ds(pl.multiple_of(t * block, block), block)
        sent = dot(mixed_ref[...], out_weight_ref[:, cols], plain).astype(bf16)
        sent = sent.reshape(span, pieces, 2, rows, block)
        for p in range(pieces):
            part_ref[p, :, :, :, cols] = sent[:, p]


def attend(acts, weights, out_weight, query_gain, key_gain, tables, docs, pieces=4):
    length, width = acts.shape
    local = weights.shape[1] // 3
    heads = local // HD
    span = lax.axis_size("gy")
    rows = length // (span * pieces * 2)
    f32, bf16 = jnp.float32, jnp.bfloat16
    vmem = pl.BlockSpec(memory_space=pltpu.VMEM)
    return pl.pallas_call(
        partial(attend_kernel, heads, pieces),
        out_shape=(
            jax.ShapeDtypeStruct((pieces, span, 2, rows, width), bf16),
            jax.ShapeDtypeStruct((length, local), f32),
            jax.ShapeDtypeStruct((length, local), f32),
            jax.ShapeDtypeStruct((length, 3 * local), bf16),
            jax.ShapeDtypeStruct((length, local), bf16),
            jax.ShapeDtypeStruct((length, HD), f32),
            jax.ShapeDtypeStruct((8, HD), f32),
        ),
        in_specs=[vmem] * 9,
        out_specs=(vmem,) * 7,
        compiler_params=pltpu.CompilerParams(vmem_limit_bytes=60 << 20),
        name="attend",
    )(
        acts,
        weights,
        out_weight,
        query_gain.reshape(1, HD),
        key_gain.reshape(1, HD),
        *tables,
        *docs,
    )


def attend_back_kernel(
    heads,
    pieces,
    grad_ref,
    out_weight_ref,
    mixed_ref,
    ready_ref,
    query_raw,
    key_raw,
    totals_ref,
    query_gain,
    key_gain,
    cosine_ref,
    sine_ref,
    row_docs,
    col_docs,
    acts_hbm,
    weight_hbm,
    part_ref,
    weight_part,
    out_part,
    gain_ref,
    acts_ref,
    weight_ref,
    grad_mixed,
    grad_heads,
    turned,
    key_sum,
    value_sum,
    copy_sem,
):
    f32, bf16 = jnp.float32, jnp.bfloat16
    dot = partial(lax.dot_general, preferred_element_type=f32)
    plain = (((1,), (0,)), ((), ()))
    last_dims = (((1,), (1,)), ((), ()))
    first_dims = (((0,), (0,)), ((), ()))
    length, width = grad_ref.shape
    span = part_ref.shape[1]
    rows = part_ref.shape[3]
    local = heads * HD
    block = 256
    scale = HD ** (-0.5)
    copies = [
        pltpu.make_async_copy(acts_hbm, acts_ref, copy_sem.at[0]),
        pltpu.make_async_copy(weight_hbm, weight_ref, copy_sem.at[1]),
    ]
    for copy in copies:
        copy.start()
    grad_mixed[...] = dot(grad_ref[...], out_weight_ref[...], last_dims).astype(bf16)

    @pl.loop(0, width // block)
    def _(t):
        cols = pl.ds(pl.multiple_of(t * block, block), block)
        out_part[cols, :] = dot(grad_ref[:, cols], mixed_ref[...], first_dims).astype(bf16)

    gain_ref[...] = jnp.zeros_like(gain_ref)
    for h in range(heads):
        cols = slice(h * HD, (h + 1) * HD)
        key = ready_ref[:, local + h * HD : local + (h + 1) * HD]
        value = ready_ref[:, 2 * local + h * HD : 2 * local + (h + 1) * HD]
        key_sum[...] = jnp.zeros_like(key_sum)
        value_sum[...] = jnp.zeros_like(value_sum)

        @pl.loop(0, length // block)
        def _(t):
            at = pl.ds(pl.multiple_of(t * block, block), block)
            same = row_docs[at, :1] == col_docs[:1, :]
            query = ready_ref[at, cols]
            grad = grad_mixed[at, cols]
            scores = jnp.where(same, dot(query, key, last_dims) * scale, NEGATIVE)
            weights = jnp.exp(scores - totals_ref[at, h : h + 1])
            value_sum[...] += dot(weights.astype(bf16), grad, first_dims)
            pulled = dot(grad, value, last_dims)
            inner = jnp.sum(weights * pulled, axis=-1, keepdims=True)
            grad_scores = (weights * (pulled - inner)).astype(bf16)
            turned[at, :] = dot(grad_scores, key, plain) * scale
            key_sum[...] += dot(grad_scores, query, first_dims)

        for source, raw, gain, incoming, factor in (
            (0, query_raw, query_gain, turned, 1.0),
            (1, key_raw, key_gain, key_sum, scale),
        ):

            @pl.loop(0, length // block)
            def _(t):
                at = pl.ds(pl.multiple_of(t * block, block), block)
                back = turn(incoming[at, :] * factor, cosine_ref[at, :], -sine_ref[at, :])
                item = raw[at, cols]
                inverse = lax.rsqrt(jnp.mean(item * item, axis=-1, keepdims=True) + EPSILON)
                normed = item * inverse
                gain_ref[source : source + 1, :] += jnp.sum(back * normed, axis=0, keepdims=True)
                inner = back * gain[...]
                pulled = inverse * (
                    inner - normed * jnp.mean(inner * normed, axis=-1, keepdims=True)
                )
                where = source * local + h * HD
                grad_heads[at, where : where + HD] = pulled.astype(bf16)

        where = 2 * local + h * HD
        grad_heads[:, where : where + HD] = value_sum[...].astype(bf16)

    for copy in copies:
        copy.wait()

    @pl.loop(0, width // block)
    def _(t):
        cols = pl.ds(pl.multiple_of(t * block, block), block)
        weight_part[cols, :] = dot(acts_ref[:, cols], grad_heads[...], first_dims).astype(bf16)
        sent = dot(grad_heads[...], weight_ref[cols, :], last_dims).astype(bf16)
        sent = sent.reshape(span, pieces, 2, rows, block)
        for p in range(pieces):
            part_ref[p, :, :, :, cols] = sent[:, p]


def attend_back(
    seq_grad, out_weight, saved, query_gain, key_gain, tables, docs, acts, weights, pieces=4
):
    query_raw, key_raw, ready, mixed, totals = saved
    length, width = seq_grad.shape
    local = query_raw.shape[1]
    heads = local // HD
    span = lax.axis_size("gy")
    rows = length // (span * pieces * 2)
    f32, bf16 = jnp.float32, jnp.bfloat16
    vmem = pl.BlockSpec(memory_space=pltpu.VMEM)
    hbm = pl.BlockSpec(memory_space=pl.ANY)
    return pl.pallas_call(
        partial(attend_back_kernel, heads, pieces),
        out_shape=(
            jax.ShapeDtypeStruct((pieces, span, 2, rows, width), bf16),
            jax.ShapeDtypeStruct((width, 3 * local), bf16),
            jax.ShapeDtypeStruct((width, local), bf16),
            jax.ShapeDtypeStruct((8, HD), f32),
        ),
        in_specs=[vmem] * 13 + [hbm] * 2,
        out_specs=(vmem,) * 4,
        scratch_shapes=[
            pltpu.VMEM((length, width), bf16),
            pltpu.VMEM((width, 3 * local), bf16),
            pltpu.VMEM((length, local), bf16),
            pltpu.VMEM((length, 3 * local), bf16),
            pltpu.VMEM((length, HD), f32),
            pltpu.VMEM((length, HD), f32),
            pltpu.VMEM((length, HD), f32),
            pltpu.SemaphoreType.DMA((2,)),
        ],
        compiler_params=pltpu.CompilerParams(vmem_limit_bytes=60 << 20),
        name="attend_back",
    )(
        seq_grad,
        out_weight,
        mixed,
        ready,
        query_raw,
        key_raw,
        totals,
        query_gain.reshape(1, HD),
        key_gain.reshape(1, HD),
        *tables,
        *docs,
        acts,
        weights,
    )


def norm_rows(values, gain_row):
    return (
        values * lax.rsqrt(jnp.mean(values * values, axis=-1, keepdims=True) + EPSILON) * gain_row
    )


def rotary(values):
    length = values.shape[0]
    halfway = values.shape[-1] // 2
    positions = jnp.arange(length, dtype=jnp.float32)
    frequency = jnp.exp(
        jnp.arange(halfway, dtype=jnp.float32) * (-2.0 * jnp.log(10000.0) / values.shape[-1])
    )
    angles = (positions[:, None] * frequency[None, :])[:, None, :]
    cosine = jnp.cos(angles)
    sine_table = jnp.sin(angles)
    first_half = values[..., :halfway]
    second = values[..., halfway:]
    return jnp.concatenate(
        [first_half * cosine - second * sine_table, second * cosine + first_half * sine_table],
        axis=-1,
    )


def prepare_heads(raw_heads, gain_row):
    return rotary(norm_rows(raw_heads, gain_row))


def route_gates(id_table, logits):
    shares = jax.nn.softmax(logits, axis=-1)
    experts = logits.shape[-1]
    matches = id_table[:, :, None] == jnp.arange(experts, dtype=jnp.int32)[None, None, :]
    chosen = jnp.sum(jnp.where(matches, shares[:, None, :], 0.0), axis=-1)
    return chosen / jnp.sum(chosen, axis=-1, keepdims=True)


def contract_rows(left_side, right_side):
    return lax.dot_general(
        left_side, right_side, (((0,), (0,)), ((), ())), preferred_element_type=jnp.float32
    )


def contract_cols(left_side, right_side):
    return lax.dot_general(
        left_side, right_side, (((1,), (1,)), ((), ())), preferred_element_type=jnp.float32
    )


def routed_experts(
    moe_in, cotangent, expert_ids, gate_share, router_weight, gate_weight, up_weight, down_weight
):
    tok_rows = moe_in.shape[0]
    experts = router_weight.shape[1]
    width_all = moe_in.shape[1]
    capacity = tok_rows * TOP * 3 // (2 * experts)
    route_count = tok_rows * TOP
    flat_ids = expert_ids.reshape(route_count)
    onehot = (flat_ids[:, None] == jnp.arange(experts, dtype=jnp.int32)[None, :]).astype(jnp.int32)
    earlier = jnp.cumsum(onehot, axis=0) - onehot
    slot_index = jnp.sum(earlier * onehot, axis=1)
    target = flat_ids * capacity + slot_index
    source = (
        jnp.full((experts * capacity,), tok_rows, jnp.int32)
        .at[target]
        .set(jnp.arange(route_count, dtype=jnp.int32) // TOP)
    )
    padded_in = jnp.concatenate([moe_in, jnp.zeros((1, width_all), jnp.bfloat16)], axis=0)
    packed = padded_in[source].reshape(experts, 1, capacity, width_all)
    outgoing = jnp.broadcast_to(packed, (experts, 2, capacity, width_all)).reshape(
        2 * experts, capacity, width_all
    )
    arrived = lax.all_to_all(outgoing, ("gx", "gy"), split_axis=0, concat_axis=1, tiled=True)[0]
    gate_in = gate_weight[0]
    up_in = up_weight[0]
    down_in = down_weight[0]
    gate_val = jnp.dot(arrived, gate_in, preferred_element_type=jnp.float32)
    up_val = jnp.dot(arrived, up_in, preferred_element_type=jnp.float32)
    hidden = (jax.nn.silu(gate_val) * up_val).astype(jnp.bfloat16)
    produced = jnp.dot(hidden, down_in, preferred_element_type=jnp.float32).astype(jnp.bfloat16)
    returned = lax.all_to_all(produced[None], ("gx", "gy"), split_axis=1, concat_axis=0, tiled=True)
    summed = (
        returned.reshape(experts, 2, capacity, width_all)
        .astype(jnp.float32)
        .sum(axis=1)
        .reshape(experts * capacity, width_all)
    )
    route_out = summed[target]
    gates_flat = gate_share.reshape(route_count)
    moe_out = jnp.sum((gates_flat[:, None] * route_out).reshape(tok_rows, TOP, width_all), axis=1)
    grad_out = cotangent.astype(jnp.float32)
    grad_gates = jnp.sum(
        route_out.reshape(tok_rows, TOP, width_all) * grad_out[:, None, :], axis=-1
    )
    slot_gate = jnp.zeros((experts * capacity,), jnp.float32).at[target].set(gates_flat)
    padded_grad = jnp.concatenate([grad_out, jnp.zeros((1, width_all), jnp.float32)], axis=0)
    grad_packed = (
        (slot_gate[:, None] * padded_grad[source])
        .astype(jnp.bfloat16)
        .reshape(experts, 1, capacity, width_all)
    )
    grad_outgoing = jnp.broadcast_to(grad_packed, (experts, 2, capacity, width_all)).reshape(
        2 * experts, capacity, width_all
    )
    grad_arrived = lax.all_to_all(
        grad_outgoing, ("gx", "gy"), split_axis=0, concat_axis=1, tiled=True
    )[0]
    rows_in, grad_use = (arrived, grad_arrived)
    gate_use, up_use, hidden_use = (gate_val, up_val, hidden)
    sigmoid_gate = jax.nn.sigmoid(gate_use)
    silu_gate = gate_use * sigmoid_gate
    grad_hidden = contract_cols(grad_use, down_in)
    down_part = contract_rows(hidden_use, grad_use)
    grad_gate = (
        grad_hidden * up_use * sigmoid_gate * (1.0 + gate_use * (1.0 - sigmoid_gate))
    ).astype(jnp.bfloat16)
    grad_up = (grad_hidden * silu_gate).astype(jnp.bfloat16)
    gate_part = contract_rows(rows_in, grad_gate)
    up_part = contract_rows(rows_in, grad_up)
    grad_in = contract_cols(grad_gate, gate_in) + contract_cols(grad_up, up_in)
    grad_back = lax.all_to_all(
        grad_in.astype(jnp.bfloat16)[None], ("gx", "gy"), split_axis=1, concat_axis=0, tiled=True
    )
    grad_summed = (
        grad_back.reshape(experts, 2, capacity, width_all)
        .astype(jnp.float32)
        .sum(axis=1)
        .reshape(experts * capacity, width_all)
    )
    grad_moe_in = jnp.sum(grad_summed[target].reshape(tok_rows, TOP, width_all), axis=1)
    return moe_out, grad_gates, grad_moe_in, gate_part, up_part, down_part


def dense_experts(
    moe_in, all_cot, expert_ids, gate_share, gate_weight, up_weight, down_weight
):
    everyone = ("gx", "gy")
    devices = lax.axis_size("gx") * lax.axis_size("gy")
    experts = devices // 2
    matches = expert_ids[:, :, None] == jnp.arange(experts, dtype=jnp.int32)[None, None, :]
    dense_gates = jnp.sum(jnp.where(matches, gate_share[:, :, None], 0.0), axis=1)
    own_gate = lax.all_to_all(
        jnp.repeat(dense_gates.T, 2, axis=0), everyone, split_axis=0, concat_axis=0, tiled=True
    ).reshape(-1)
    shares = jnp.broadcast_to(own_gate[:, None], (own_gate.shape[0], 128))
    all_moe, pair, gate_dots, down_part, moe_out = run_experts(
        moe_in, all_cot, shares, gate_weight[0], up_weight[0], down_weight[0], 8
    )
    moe_out = moe_out.reshape(moe_in.shape)
    dots_back = lax.all_to_all(
        jnp.sum(gate_dots, axis=-1).reshape(devices, -1),
        everyone,
        split_axis=0,
        concat_axis=0,
        tiled=True,
    )
    dots_experts = dots_back.reshape(experts, 2, -1).sum(axis=1).T
    grad_gates = jnp.sum(jnp.where(matches, dots_experts[:, None, :], 0.0), axis=-1)
    grad_moe_in, gate_part, up_part = pull_experts(all_moe, pair, gate_weight[0], up_weight[0], 9)
    return moe_out, grad_gates, grad_moe_in, gate_part, up_part, down_part


def plain_attention(
    seq_acts, full_in, out_rows, query_gain, key_gain, doc_ids
):
    local_width = full_in.shape[1] // 3
    length = seq_acts.shape[0]
    local_heads = local_width // HD
    projected = jnp.dot(seq_acts, full_in, preferred_element_type=jnp.float32)
    queries = projected[:, :local_width]
    key_raw = projected[:, local_width : 2 * local_width]
    value_ready = (
        projected[:, 2 * local_width :].astype(jnp.bfloat16).reshape(length, local_heads, HD)
    )
    query_float, query_pull = jax.vjp(
        prepare_heads, queries.reshape(length, local_heads, HD), query_gain
    )
    key_float, key_pull = jax.vjp(prepare_heads, key_raw.reshape(length, local_heads, HD), key_gain)
    query_ready = query_float.astype(jnp.bfloat16)
    key_ready = key_float.astype(jnp.bfloat16)
    block_rows = min(512, length)
    block_count = length // block_rows
    score_scale = HD ** (-0.5)
    query_blocks = query_ready.reshape(block_count, block_rows, local_heads, HD)
    doc_blocks = doc_ids.reshape(block_count, block_rows)

    def block_scores(query_block, doc_block):
        scores = (
            jnp.einsum("qhd,khd->hqk", query_block, key_ready, preferred_element_type=jnp.float32)
            * score_scale
        )
        same_doc = doc_block[:, None] == doc_ids[None, :]
        return jnp.where(same_doc[None], scores, NEGATIVE)

    def forward_block(pieces):
        scores = block_scores(pieces[0], pieces[1])
        highest = jnp.max(scores, axis=-1, keepdims=True)
        weights = jnp.exp(scores - highest)
        totals = jnp.sum(weights, axis=-1, keepdims=True)
        shares = (weights / totals).astype(jnp.bfloat16)
        mixed_heads = jnp.einsum(
            "hqk,khd->qhd", shares, value_ready, preferred_element_type=jnp.float32
        )
        return (
            mixed_heads.astype(jnp.bfloat16),
            highest[..., 0] + jnp.log(totals[..., 0]),
            jnp.max(highest[..., 0], axis=-1),
        )

    mixed_blocks, log_totals, peak_blocks = lax.map(forward_block, (query_blocks, doc_blocks))
    mixed_seq = mixed_blocks.reshape(length, local_width)
    attended = lax.psum_scatter(
        jnp.dot(mixed_seq, out_rows, preferred_element_type=jnp.float32),
        "gy",
        scatter_dimension=0,
        tiled=True,
    )

    def back(grad_resid):
        seq_grad = lax.all_gather(grad_resid.astype(jnp.bfloat16), "gy", axis=0, tiled=True)
        grad_mixed = contract_cols(seq_grad, out_rows).astype(jnp.bfloat16)
        out_part = contract_rows(seq_grad, mixed_seq)

        def backward_block(running, pieces):
            grad_key, grad_value = running
            query_block, grad_block, log_block, doc_block = pieces
            scores = block_scores(query_block, doc_block)
            weights = jnp.exp(scores - log_block[..., None])
            grad_value = grad_value + jnp.einsum(
                "hqk,qhd->khd",
                weights.astype(jnp.bfloat16),
                grad_block,
                preferred_element_type=jnp.float32,
            )
            grad_weights = jnp.einsum(
                "qhd,khd->hqk", grad_block, value_ready, preferred_element_type=jnp.float32
            )
            inner_sum = jnp.sum(weights * grad_weights, axis=-1, keepdims=True)
            grad_scores = (weights * (grad_weights - inner_sum)).astype(jnp.bfloat16)
            grad_query = (
                jnp.einsum("hqk,khd->qhd", grad_scores, key_ready, preferred_element_type=jnp.float32)
                * score_scale
            )
            grad_key = (
                grad_key
                + jnp.einsum(
                    "hqk,qhd->khd", grad_scores, query_block, preferred_element_type=jnp.float32
                )
                * score_scale
            )
            return ((grad_key, grad_value), grad_query)

        empty_heads = jnp.zeros((length, local_heads, HD), jnp.float32)
        grad_mixed_blocks = grad_mixed.reshape(block_count, block_rows, local_heads, HD)
        (key_grad_heads, value_grad_heads), query_grad_blocks = lax.scan(
            backward_block,
            (empty_heads, empty_heads),
            (query_blocks, grad_mixed_blocks, log_totals, doc_blocks),
        )
        query_raw_grad, query_gain_part = query_pull(query_grad_blocks.reshape(length, local_heads, HD))
        key_raw_grad, key_gain_part = key_pull(key_grad_heads)
        grad_queries = query_raw_grad.reshape(length, local_width).astype(jnp.bfloat16)
        grad_keys = key_raw_grad.reshape(length, local_width).astype(jnp.bfloat16)
        grad_values = value_grad_heads.reshape(length, local_width).astype(jnp.bfloat16)
        grad_heads = jnp.concatenate([grad_queries, grad_keys, grad_values], axis=1)
        acts_part = contract_cols(grad_heads, full_in).astype(jnp.bfloat16)
        in_sum = lax.psum_scatter(
            contract_rows(seq_acts, grad_heads).astype(jnp.bfloat16),
            "gx",
            scatter_dimension=0,
            tiled=True,
        ).astype(jnp.float32)
        grad_acts = lax.psum_scatter(acts_part, "gy", scatter_dimension=0, tiled=True)
        return grad_acts.astype(jnp.float32), in_sum, out_part, query_gain_part, key_gain_part

    return attended, jnp.max(peak_blocks, axis=0), back


def kernel_attention(
    seq_acts, full_in, out_rows, query_gain, key_gain, doc_ids
):
    length = seq_acts.shape[0]
    halfway = HD // 2
    frequency = jnp.exp(
        jnp.arange(halfway, dtype=jnp.float32) * (-2.0 * jnp.log(10000.0) / HD)
    )
    angles = jnp.arange(length, dtype=jnp.float32)[:, None] * frequency[None, :]
    cosine, sine = jnp.cos(angles), jnp.sin(angles)
    tables = (
        jnp.concatenate([cosine, cosine], axis=1),
        jnp.concatenate([-sine, sine], axis=1),
    )
    docs = (
        jnp.broadcast_to(doc_ids[:, None], (length, HD)),
        jnp.broadcast_to(doc_ids[None, :], (8, length)),
    )
    part, *saved, peaks = attend(
        seq_acts, full_in, out_rows, query_gain, key_gain, tables, docs
    )
    attended = scatter_plane(part, 3)
    heads = full_in.shape[1] // (3 * HD)

    def back(grad_resid):
        seq_grad = all_gather(grad_resid.astype(jnp.bfloat16), False, 1)
        part, weight_part, out_part, gains = attend_back(
            seq_grad, out_rows, saved, query_gain, key_gain, tables, docs, seq_acts, full_in
        )
        grad_acts, in_sum = leave(part, weight_part, 7)
        return grad_acts, in_sum, out_part, gains[0], gains[1]

    return attended, peaks[:heads, 0], back


def local(
    tokens,
    cotangent,
    expert_ids,
    doc_ids,
    clip_rank,
    attn_gain,
    moe_gain,
    query_gain,
    key_gain,
    query_weight,
    key_weight,
    value_weight,
    out_weight,
    router_weight,
    gate_weight,
    up_weight,
    down_weight,
):
    inputs = tokens.astype(jnp.float32)
    acts_float, norm_pull = jax.vjp(norm_rows, inputs, attn_gain)
    acts_low = acts_float.astype(jnp.bfloat16)
    in_weights = jnp.concatenate([query_weight, key_weight, value_weight], axis=1)
    by_kernels = lax.axis_size("gy") == 8
    if by_kernels:
        seq_acts, full_in, all_cot = enter(acts_low, in_weights, cotangent, 6)
    else:
        seq_acts = lax.all_gather(acts_low, "gy", axis=0, tiled=True)
        full_in = lax.all_gather(in_weights, "gx", axis=0, tiled=True)
    seq_acts, full_in, out_weight = lax.optimization_barrier((seq_acts, full_in, out_weight))
    out_rows = lax.all_gather(out_weight, "gx", axis=1, tiled=True)
    local_width = query_weight.shape[1]
    local_heads = local_width // HD
    attention = kernel_attention if by_kernels else plain_attention
    attended, own_peaks, attention_back = attention(
        seq_acts, full_in, out_rows, query_gain, key_gain, doc_ids
    )
    start_head = lax.axis_index("gy") * local_heads
    peak_slots = lax.dynamic_update_slice(
        jnp.zeros((lax.axis_size("gx"), NH), jnp.float32),
        own_peaks[None],
        (lax.axis_index("gx"), start_head),
    )
    residual = inputs + attended
    moe_float, moe_pull = jax.vjp(norm_rows, residual, moe_gain)
    moe_in = moe_float.astype(jnp.bfloat16)
    logits = jnp.dot(moe_in, router_weight, preferred_element_type=jnp.float32)
    gate_share, gate_pull = jax.vjp(partial(route_gates, expert_ids), logits)
    if by_kernels and router_weight.shape[1] <= 2 * TOP:
        moe_out, grad_gates, grad_moe_in, gate_part, up_part, down_part = dense_experts(
            moe_in, all_cot, expert_ids, gate_share, gate_weight, up_weight, down_weight
        )
    else:
        moe_out, grad_gates, grad_moe_in, gate_part, up_part, down_part = routed_experts(
            moe_in,
            cotangent,
            expert_ids,
            gate_share,
            router_weight,
            gate_weight,
            up_weight,
            down_weight,
        )
    output = (residual + moe_out).astype(jnp.bfloat16)
    grad_out = cotangent.astype(jnp.float32)
    (grad_logits,) = gate_pull(grad_gates)
    grad_logits_low = grad_logits.astype(jnp.bfloat16)
    router_part = contract_rows(moe_in, grad_logits_low)
    grad_moe_in = grad_moe_in + contract_cols(grad_logits_low, router_weight)
    grad_resid_norm, moe_gain_part = moe_pull(grad_moe_in)
    grad_resid = grad_out + grad_resid_norm
    grad_acts, in_sum, out_part, query_gain_part, key_gain_part = attention_back(grad_resid)
    query_sum = in_sum[:, :local_width]
    key_sum = in_sum[:, local_width : 2 * local_width]
    value_sum = in_sum[:, 2 * local_width :]
    out_sum_rows = lax.psum_scatter(
        out_part.astype(jnp.bfloat16), "gx", scatter_dimension=0, tiled=True
    ).astype(jnp.float32)
    norm_input_grad, attn_gain_part = norm_pull(grad_acts)
    input_grad = grad_resid + norm_input_grad
    small = (
        attn_gain_part,
        moe_gain_part,
        query_gain_part,
        key_gain_part,
        router_part.T,
        peak_slots,
    )
    summed = sum_everywhere(jnp.concatenate([part.reshape(-1) for part in small]), 5)
    ends = list(accumulate(part.size for part in small))
    attn_gain_grad, moe_gain_grad, query_gain_grad, key_gain_grad, router_flat, peaks = (
        summed[end - part.size : end].reshape(part.shape) for end, part in zip(ends, small)
    )
    router_grad = router_flat.T
    peak_global = jnp.max(peaks, axis=0)
    ranked = -jnp.sort(-peak_global)
    limit = jnp.sum(jnp.where(jnp.arange(NH, dtype=jnp.int32) == clip_rank[0], ranked, 0.0))
    factors = jnp.where(peak_global > limit, limit / peak_global, 1.0)
    own_factors = lax.dynamic_slice_in_dim(factors, start_head, local_heads)
    columns = jnp.repeat(jnp.sqrt(own_factors), HD)
    query_clipped = (query_weight.astype(jnp.float32) * columns[None, :]).astype(jnp.bfloat16)
    key_clipped = (key_weight.astype(jnp.float32) * columns[None, :]).astype(jnp.bfloat16)
    return (
        output,
        input_grad,
        attn_gain_grad,
        moe_gain_grad,
        query_gain_grad,
        key_gain_grad,
        query_sum,
        key_sum,
        value_sum,
        out_sum_rows.T,
        router_grad,
        gate_part[None],
        up_part[None],
        down_part[None],
        query_clipped,
        key_clipped,
        factors,
    )


def solution(mesh):
    placed = (
        P(("gx", "gy"), None),
        P(("gx", "gy"), None),
        P(("gx", "gy"), None),
        P("gx"),
        P(),
        P(),
        P(),
        P(),
        P(),
        P("gx", "gy"),
        P("gx", "gy"),
        P("gx", "gy"),
        P("gy", "gx"),
        P(),
        P(("gx", "gy"), None, None),
        P(("gx", "gy"), None, None),
        P(("gx", "gy"), None, None),
    )
    return jax.shard_map(
        local,
        mesh=mesh,
        in_specs=placed,
        out_specs=(
            P(("gx", "gy"), None),
            P(("gx", "gy"), None),
            P(),
            P(),
            P(),
            P(),
            P("gx", "gy"),
            P("gx", "gy"),
            P("gx", "gy"),
            P("gy", "gx"),
            P(),
            P(("gx", "gy"), None, None),
            P(("gx", "gy"), None, None),
            P(("gx", "gy"), None, None),
            P("gx", "gy"),
            P("gx", "gy"),
            P(),
        ),
        check_vma=False,
    )
```

```python
from functools import partial
from itertools import accumulate

import jax
import jax.numpy as jnp
from jax import lax
from jax.experimental import pallas as pl
from jax.experimental.pallas import tpu as pltpu
from jax.sharding import PartitionSpec as P

NH = 16
HD = 128
TOP = 8


EPSILON = 1e-06
NEGATIVE = -1e30


def flip(index):
    return index + 1 - 2 * (index % 2)


def barrier_with(partners):
    barrier = pltpu.get_barrier_semaphore()
    for ok, device in partners:
        @pl.when(ok)
        def _():
            pl.semaphore_signal(barrier, inc=1, device_id=device, device_id_type=pl.DeviceIdType.MESH)
    pl.semaphore_wait(barrier, sum(ok.astype(jnp.int32) for ok, _ in partners))

def always(ok, other):
    if ok is True:
        return other
    return ok if other is True else jnp.logical_and(ok, other)


def run_if(ok, action):
    if ok is True:
        action()
    else:
        pl.when(ok)(action)


def chain_gather(n_z, own_ref, out_ref, send_sem, recv_sem, local_sem):
    z = lax.axis_index("gx")
    g = lax.axis_index("gy")

    def hop(source, owner, k, peer):
        return pltpu.make_async_remote_copy(
            src_ref=source,
            dst_ref=out_ref.at[owner],
            send_sem=send_sem.at[k],
            recv_sem=recv_sem.at[owner],
            device_id={"gx": peer, "gy": g},
            device_id_type=pl.DeviceIdType.MESH,
        )

    local = pltpu.make_async_copy(own_ref, out_ref.at[z], local_sem)
    upward = [(z < n_z - 1, lambda: hop(own_ref, z, 0, z + 1))]
    downward = [(z > 0, lambda: hop(own_ref, z, n_z, z - 1))]
    for d in range(1, n_z - 1):
        upward.append(
            (
                jnp.logical_and(z >= d, z < n_z - 1),
                lambda d=d: hop(out_ref.at[z - d], z - d, d, z + 1),
            )
        )
        downward.append(
            (
                jnp.logical_and(z < n_z - d, z > 0),
                lambda d=d: hop(out_ref.at[z + d], z + d, n_z + d, z - 1),
            )
        )

    def start():
        local.start()
        for ok, copy in (upward[0], downward[0]):
            run_if(ok, lambda copy=copy: copy().start())

    def relay(d):
        run_if(z >= d, lambda: hop(own_ref, z - d, 0, z).wait_recv())
        if d < n_z - 1:
            run_if(upward[d][0], lambda: upward[d][1]().start())
        run_if(z < n_z - d, lambda: hop(own_ref, z + d, 0, z).wait_recv())
        if d < n_z - 1:
            run_if(downward[d][0], lambda: downward[d][1]().start())

    def finish():
        local.wait()
        for ok, copy in upward + downward:
            run_if(ok, lambda copy=copy: copy().wait_send())

    return start, [partial(relay, d) for d in range(1, n_z)], finish


def gather_steps(n_z, span, own_ref, out_ref, send_sem, recv_sem, local_sem):
    z = lax.axis_index("gx")
    g = lax.axis_index("gy")
    flip_x = g + 2 - 4 * ((g // 2) % 2)
    flip_y = g + 4 - 8 * ((g // 4) % 2)
    flip_both = flip_x + flip_y - g
    core = {"gx": z, "gy": flip(g)}
    x_peer = {"gx": z, "gy": flip_x}
    y_peer = {"gx": z, "gy": flip_y}
    above = {"gx": z + 1, "gy": g}
    below = {"gx": z - 1, "gy": g}
    first_z = z if n_z > 1 else 0
    sends = []

    def send(ok, source, b, h, peer):
        k = len(sends)

        def make():
            return pltpu.make_async_remote_copy(
                src_ref=source,
                dst_ref=out_ref.at[b, h],
                send_sem=send_sem.at[k],
                recv_sem=recv_sem.at[b, h],
                device_id=peer,
                device_id_type=pl.DeviceIdType.MESH,
            )

        sends.append((ok, make))
        run_if(ok, lambda: make().start())

    def arrive(ok, b, h):
        def wait():
            pltpu.make_async_remote_copy(
                src_ref=out_ref.at[b, h],
                dst_ref=out_ref.at[b, h],
                send_sem=send_sem.at[0],
                recv_sem=recv_sem.at[b, h],
                device_id=core,
                device_id_type=pl.DeviceIdType.MESH,
            ).wait_recv()

        run_if(ok, wait)

    local = pltpu.make_async_copy(own_ref, out_ref.at[first_z * span + g], local_sem)
    items = [(True, first_z, 0)]
    for d in range(1, n_z):
        items += [(z >= d, z - d, -d), (z < n_z - d, z + d, d)]

    def first(item):
        ok, owner, d = item
        b = owner * span + g
        if d == 0:
            local.start()
            source = own_ref
        else:
            arrive(ok, b, 0)
            arrive(ok, b, 1)
            source = out_ref.at[b]
        for h in range(2):
            if n_z > 1 and d <= 0:
                send(always(ok, z < n_z - 1), source.at[h], b, h, above)
            if n_z > 1 and d >= 0:
                send(always(ok, z > 0), source.at[h], b, h, below)
        send(ok, source.at[0], b, 0, x_peer)
        send(ok, source.at[1], b, 1, y_peer)
        send(ok, source.at[1], b, 1, x_peer)
        send(ok, source.at[0], b, 0, y_peer)
        send(ok, source.at[0], b, 0, core)
        send(ok, source.at[1], b, 1, core)

    def second(item):
        ok, owner, _ = item
        for side, h, peer in ((flip_x, 0, y_peer), (flip_y, 1, x_peer)):
            b = owner * span + side
            arrive(ok, b, h)
            send(ok, out_ref.at[b, h], b, h, peer)
            send(ok, out_ref.at[b, h], b, h, core)

    def third(item):
        ok, owner, _ = item
        for side, h in ((flip_both, 0), (flip_both, 1), (flip_y, 0), (flip_x, 1)):
            b = owner * span + side
            arrive(ok, b, h)
            send(ok, out_ref.at[b, h], b, h, core)

    n = len(items)

    def step(i):
        if i < n:
            first(items[i])
        if 1 <= i <= n:
            second(items[i - 1])
        if i >= 2:
            third(items[i - 2])

    def finish():
        for ok, owner, _ in items:
            for side in (g, flip_x, flip_y, flip_both):
                for h in range(2):
                    arrive(ok, owner * span + flip(side), h)
        local.wait()
        for ok, make in sends:
            run_if(ok, lambda make=make: make().wait_send())

    return [partial(step, i) for i in range(n + 2)], finish


def greet(n_z):
    z = lax.axis_index("gx")
    g = lax.axis_index("gy")
    peers = [
        (z >= 0, {"gx": z, "gy": g + bit - 2 * bit * ((g // bit) % 2)}) for bit in (1, 2, 4)
    ]
    if n_z > 1:
        peers += [(z < n_z - 1, {"gx": z + 1, "gy": g}), (z > 0, {"gx": z - 1, "gy": g})]
    barrier_with(peers)


def gather_kernel(n_z, span, own_ref, out_ref, send_sem, recv_sem, local_sem):
    greet(n_z)
    steps, finish = gather_steps(n_z, span, own_ref, out_ref, send_sem, recv_sem, local_sem)
    for step in steps:
        step()
    finish()


def all_gather(block, both, collective_id):
    n_z = lax.axis_size("gx") if both else 1
    span = lax.axis_size("gy")
    rows, cols = block.shape
    own = block.reshape(2, rows // 2, cols)
    n_sends = (2 * n_z - 1) * 24
    out = pl.pallas_call(
        partial(gather_kernel, n_z, span),
        out_shape=jax.ShapeDtypeStruct((n_z * span, 2, rows // 2, cols), block.dtype),
        in_specs=[pl.BlockSpec(memory_space=pltpu.VMEM)],
        out_specs=pl.BlockSpec(memory_space=pl.ANY),
        scratch_shapes=[pltpu.SemaphoreType.DMA((n_sends,)), pltpu.SemaphoreType.DMA((n_z * span, 2)), pltpu.SemaphoreType.DMA],
        compiler_params=pltpu.CompilerParams(collective_id=collective_id, has_side_effects=True),
        name="gather_all" if both else "gather_plane",
    )(own)
    return out.reshape(n_z * span * rows, cols)


def add_into(dst, parts, rows):
    step = min(rows, 32)

    @pl.loop(0, rows // step)
    def _(r):
        at = pl.ds(pl.multiple_of(r * step, step), step)
        if len(parts) == 2 and dst.dtype == jnp.bfloat16:
            dst[at, :] = parts[0][at, :] + parts[1][at, :]
        else:
            total = parts[0][at, :].astype(jnp.float32)
            for term in parts[1:]:
                total = total + term[at, :].astype(jnp.float32)
            dst[at, :] = total.astype(dst.dtype)


def scatter_kernel(chain, n_i, rows, part_ref, out_ref, held, from_core, from_a, from_b, from_z,
                   load_sem, core_send, a_send, b_send, z_send, core_recv, a_recv, b_recv, z_recv, beside=None):
    z = lax.axis_index("gx"); g = lax.axis_index("gy")
    flip_x = g + 2 - 4 * ((g // 2) % 2)
    flip_y = g + 4 - 8 * ((g // 4) % 2)
    quads = (flip_x + flip_y - g, flip_x, flip_y, g)
    core = {"gx": z, "gy": flip(g)}
    xn = {"gx": z, "gy": flip_x}
    yn = {"gx": z, "gy": flip_y}
    every = z >= 0
    partners = [(every, core), (every, xn), (every, yn)]
    if chain:
        partners += [(every, {"gx": lax.rem(z + j, n_i), "gy": g}) for j in range(1, n_i)]
    if beside:
        n_z = lax.axis_size("gx")
        partners += [(z < n_z - 1, {"gx": z + 1, "gy": g}), (z > 0, {"gx": z - 1, "gy": g})]
    barrier_with(partners)
    if beside:
        beside[0]()
    mesh_id = pl.DeviceIdType.MESH

    def item(i):
        return lax.rem(z + n_i - 1 - i + n_i, n_i) if chain else i

    def block(it, gg):
        return part_ref.at[it, gg]

    def remote(src, dst, ssem, rsem, dev):
        return pltpu.make_async_remote_copy(src_ref=src, dst_ref=dst, send_sem=ssem, recv_sem=rsem, device_id=dev, device_id_type=mesh_id)

    def core_copy(i, q):
        it = item(i)
        return remote(block(it, flip(quads[q])), from_core.at[it, q], core_send.at[i, q], core_recv.at[it, q], core)

    def load(i, q):
        it = item(i)
        return pltpu.make_async_copy(block(it, quads[q]), held.at[it, q], load_sem.at[i, q])

    a_plan = ((0, 0, 0, xn), (0, 1, 0, yn), (1, 0, 1, xn), (2, 1, 1, yn))
    def a_copy(i, k):
        it = item(i)
        q, h, slot, dev = a_plan[k]
        return remote(held.at[it, q, h], from_a.at[it, h, slot], a_send.at[i, k], a_recv.at[it, h, slot], dev)

    b_plan = ((2, 0, yn), (1, 1, xn))
    def b_copy(i, h):
        it = item(i)
        q, _, dev = b_plan[h]
        return remote(held.at[it, q, h], from_b.at[it, h], b_send.at[i, h], b_recv.at[it, h], dev)

    def z_copy(i):
        it = item(i)
        return remote(held.at[it, 3], from_z.at[z], z_send.at[i], z_recv.at[z], {"gx": it, "gy": g})

    def z_arrival(i):
        it = item(i)
        return remote(held.at[it, 3], from_z.at[it], z_send.at[i], z_recv.at[it], core)

    for i in range(n_i):
        for q in range(4):
            core_copy(i, q).start()
            load(i, q).start()

    def stage_a(i):
        it = item(i)
        for q in range(4):
            load(i, q).wait()
            core_copy(i, q).wait_recv()
            for h in range(2):
                add_into(held.at[it, q, h], (held.at[it, q, h], from_core.at[it, q, h]), rows)
            for k in range(4):
                if a_plan[k][0] == q:
                    a_copy(i, k).start()

    def stage_b(i):
        it = item(i)
        for q, h, slot in ((2, 0, 0), (1, 1, 0), (3, 0, 1), (3, 1, 1)):
            remote(held.at[it, q, h], from_a.at[it, h, slot], a_send.at[i, 0], a_recv.at[it, h, slot], core).wait_recv()
            add_into(held.at[it, q, h], (held.at[it, q, h], from_a.at[it, h, slot]), rows)
            if slot == 0:
                b_copy(i, h).start()

    def stage_c(i):
        it = item(i)
        for h in range(2):
            b_copy(i, h).wait_recv()
            if chain:
                add_into(held.at[it, 3, h], (held.at[it, 3, h], from_b.at[it, h]), rows)
            else:
                add_into(out_ref.at[it, h], (held.at[it, 3, h], from_b.at[it, h]), rows)

    def stage_d(i):
        if i < n_i - 1:
            z_copy(i).start()
        else:
            for j in range(n_i - 1):
                z_arrival(j).wait_recv()
            for h in range(2):
                add_into(
                    out_ref.at[h],
                    [held.at[item(i), 3, h]] + [from_z.at[item(j), h] for j in range(n_i - 1)],
                    rows,
                )

    for i in range(n_i + 2):
        if i < n_i: stage_a(i)
        if 0 <= i - 1 < n_i: stage_b(i - 1)
        if 0 <= i - 2 < n_i: stage_c(i - 2)
        if chain and 0 <= i - 2 < n_i: stage_d(i - 2)
        if beside and i == n_i:
            beside[1][0]()
    if beside:
        for relay in beside[1][1:]:
            relay()
        beside[2]()
    for i in range(n_i):
        for q in range(4): core_copy(i, q).wait_send()
        for k in range(4): a_copy(i, k).wait_send()
        for h in range(2): b_copy(i, h).wait_send()
        if chain and i < n_i - 1: z_copy(i).wait_send()


def scatter_plane(part, collective_id):
    span = lax.axis_size("gy")
    pieces, _, _, rows, cols = part.shape
    dma = pltpu.SemaphoreType.DMA
    half = (rows, cols)
    out = pl.pallas_call(
        partial(scatter_kernel, False, pieces, rows),
        out_shape=jax.ShapeDtypeStruct((pieces, 2, rows, cols), jnp.float32),
        in_specs=[pl.BlockSpec(memory_space=pl.ANY)],
        out_specs=pl.BlockSpec(memory_space=pltpu.VMEM),
        scratch_shapes=[
            pltpu.VMEM((pieces, 4, 2) + half, jnp.bfloat16),
            pltpu.VMEM((pieces, 4, 2) + half, jnp.bfloat16),
            pltpu.VMEM((pieces, 2, 2) + half, jnp.bfloat16),
            pltpu.VMEM((pieces, 2) + half, jnp.bfloat16),
            pltpu.VMEM((1, 2, 16, 128), jnp.bfloat16),
            dma((pieces, 4)),
            dma((pieces, 4)),
            dma((pieces, 4)),
            dma((pieces, 2)),
            dma((pieces,)),
            dma((pieces, 4)),
            dma((pieces, 2, 2)),
            dma((pieces, 2)),
            dma((pieces,)),
        ],
        compiler_params=pltpu.CompilerParams(
            collective_id=collective_id, has_side_effects=True, vmem_limit_bytes=60 << 20
        ),
        name="scatter_plane",
    )(part)
    return out.reshape(pieces * 2 * rows, cols)


def sum_kernel(n_z, bits, vec_ref, out_ref, held, arrived, from_z, send_sem, z_send, recv_sem, z_recv):
    z = lax.axis_index("gx")
    g = lax.axis_index("gy")
    half = vec_ref.shape[1]
    side = lax.rem(g, 2)
    core = {"gx": z, "gy": g + 1 - 2 * (g % 2)}
    peers = [
        {"gx": z, "gy": g + bit - 2 * bit * ((g // bit) % 2)}
        for bit in (2**power for power in range(1, bits))
    ]
    others = [{"gx": lax.rem(z + j, n_z), "gy": g} for j in range(1, n_z)]
    barrier_with([(z >= 0, peer) for peer in (core, *peers, *others)])

    def remote(src, dst, ssem, rsem, peer):
        return pltpu.make_async_remote_copy(
            src_ref=src,
            dst_ref=dst,
            send_sem=ssem,
            recv_sem=rsem,
            device_id=peer,
            device_id_type=pl.DeviceIdType.MESH,
        )

    first = remote(vec_ref.at[1 - side], arrived.at[0], send_sem.at[0], recv_sem.at[0], core)
    first.start()
    first.wait()
    held[0] = vec_ref[side] + arrived[0]
    for k, peer in enumerate(peers, 1):
        step = remote(held.at[k - 1], arrived.at[k], send_sem.at[k], recv_sem.at[k], peer)
        step.start()
        step.wait()
        held[k] = held[k - 1] + arrived[k]
    copies = [
        remote(held.at[bits - 1], from_z.at[j], z_send.at[j], z_recv.at[j], peer)
        for j, peer in enumerate(others)
    ]
    for copy in copies:
        copy.start()
    for copy in copies:
        copy.wait()
    total = jnp.zeros_like(held[0])
    for owner in range(n_z):
        term = held[bits - 1]
        for j in range(1, n_z):
            term = jnp.where(lax.rem(z - j + n_z, n_z) == owner, from_z[j - 1], term)
        total = total + term
    held[bits] = total
    last = remote(held.at[bits], arrived.at[bits], send_sem.at[bits], recv_sem.at[bits], core)
    last.start()
    out_ref[side] = total
    last.wait()
    out_ref[1 - side] = arrived[bits]


def sum_everywhere(vector, collective_id):
    n_z = lax.axis_size("gx")
    bits = lax.axis_size("gy").bit_length() - 1
    lanes = 128
    length = vector.shape[0]
    rows = -(-length // (lanes * 16)) * 8
    padded = jnp.pad(vector, (0, 2 * rows * lanes - length)).reshape(2, rows, lanes)
    dma = pltpu.SemaphoreType.DMA
    out = pl.pallas_call(
        partial(sum_kernel, n_z, bits),
        out_shape=jax.ShapeDtypeStruct((2, rows, lanes), jnp.float32),
        in_specs=[pl.BlockSpec(memory_space=pltpu.VMEM)],
        out_specs=pl.BlockSpec(memory_space=pltpu.VMEM),
        scratch_shapes=[
            pltpu.VMEM((bits + 1, rows, lanes), jnp.float32),
            pltpu.VMEM((bits + 1, rows, lanes), jnp.float32),
            pltpu.VMEM((n_z - 1, rows, lanes), jnp.float32),
            dma((bits + 1,)),
            dma((n_z - 1,)),
            dma((bits + 1,)),
            dma((n_z - 1,)),
        ],
        compiler_params=pltpu.CompilerParams(collective_id=collective_id, has_side_effects=True),
        name="sum_everywhere",
    )(padded)
    return out.reshape(-1)[:length]


def enter_kernel(
    n_z,
    span,
    acts_ref,
    weight_ref,
    cot_ref,
    seq_ref,
    full_ref,
    all_cot_ref,
    send_sem,
    recv_sem,
    local_sem,
    chain_send,
    chain_recv,
    chain_local,
    cot_send,
    cot_recv,
    cot_local,
):
    greet(n_z)
    start, relays, end_chain = chain_gather(
        n_z, weight_ref, full_ref, chain_send, chain_recv, chain_local
    )
    near, end_near = gather_steps(1, span, acts_ref, seq_ref, send_sem, recv_sem, local_sem)
    far, end_far = gather_steps(n_z, span, cot_ref, all_cot_ref, cot_send, cot_recv, cot_local)
    start()
    near[0]()
    far[0]()
    near[1]()
    near[2]()
    for k, step in enumerate(far[1:]):
        if k % 2 == 0 and k // 2 < len(relays):
            relays[k // 2]()
        step()
    for relay in relays[len(far) // 2 :]:
        relay()
    end_chain()
    end_near()
    end_far()


def enter(acts, weights, cotangent, collective_id):
    n_z = lax.axis_size("gx")
    span = lax.axis_size("gy")
    rows, cols = acts.shape
    dma = pltpu.SemaphoreType.DMA
    half = (2, rows // 2, cols)
    seq, full, all_cot = pl.pallas_call(
        partial(enter_kernel, n_z, span),
        out_shape=(
            jax.ShapeDtypeStruct((span,) + half, acts.dtype),
            jax.ShapeDtypeStruct((n_z,) + weights.shape, weights.dtype),
            jax.ShapeDtypeStruct((n_z * span,) + half, cotangent.dtype),
        ),
        in_specs=[pl.BlockSpec(memory_space=pltpu.VMEM)] * 3,
        out_specs=(pl.BlockSpec(memory_space=pl.ANY),) * 3,
        scratch_shapes=[
            dma((24,)),
            dma((span, 2)),
            dma,
            dma((2 * n_z,)),
            dma((n_z,)),
            dma,
            dma((24 * (2 * n_z - 1),)),
            dma((n_z * span, 2)),
            dma,
        ],
        compiler_params=pltpu.CompilerParams(collective_id=collective_id, has_side_effects=True),
        name="enter",
    )(acts.reshape(half), weights, cotangent.reshape(half))
    return (
        seq.reshape(span * rows, cols),
        full.reshape(n_z * weights.shape[0], weights.shape[1]),
        all_cot.reshape(n_z * span * rows, cols),
    )


def chain_scatter(n_z, part_ref, out_ref, from_low, from_high, send_sem, low_recv, high_recv):
    z = lax.axis_index("gx")
    g = lax.axis_index("gy")
    rows = part_ref.shape[1]

    def up(dest):
        return pltpu.make_async_remote_copy(
            src_ref=part_ref.at[dest],
            dst_ref=from_low.at[dest],
            send_sem=send_sem.at[dest],
            recv_sem=low_recv.at[dest],
            device_id={"gx": z + 1, "gy": g},
            device_id_type=pl.DeviceIdType.MESH,
        )

    def down(dest):
        return pltpu.make_async_remote_copy(
            src_ref=part_ref.at[dest],
            dst_ref=from_high.at[dest],
            send_sem=send_sem.at[dest],
            recv_sem=high_recv.at[dest],
            device_id={"gx": z - 1, "gy": g},
            device_id_type=pl.DeviceIdType.MESH,
        )

    def start():
        for k in range(n_z - 1):
            run_if(z == 0, lambda k=k: up(n_z - 1 - k).start())
            run_if(z == n_z - 1, lambda k=k: down(k).start())

    def pass_up(dest):
        up(dest).wait_recv()
        add_into(part_ref.at[dest], (part_ref.at[dest], from_low.at[dest]), rows)
        up(dest).start()

    def pass_down(dest):
        down(dest).wait_recv()
        add_into(part_ref.at[dest], (part_ref.at[dest], from_high.at[dest]), rows)
        down(dest).start()

    def relay(time):
        for k in range(time):
            low, dest = time - k, n_z - 1 - k
            if 0 < low < dest:
                run_if(z == low, partial(pass_up, dest))
            high, dest = n_z - 1 - (time - k), k
            if dest < high < n_z - 1:
                run_if(z == high, partial(pass_down, dest))

    def finish():
        for dest in range(n_z):
            terms = [part_ref.at[dest]]
            terms += [from_low.at[dest]] if dest > 0 else []
            terms += [from_high.at[dest]] if dest < n_z - 1 else []

            def last(dest=dest, terms=terms):
                if dest > 0:
                    up(dest).wait_recv()
                if dest < n_z - 1:
                    down(dest).wait_recv()
                add_into(out_ref, terms, rows)

            run_if(z == dest, last)
        for dest in range(n_z):
            run_if(z != dest, lambda dest=dest: up(dest).wait_send())

    return start, [partial(relay, time) for time in range(1, n_z)], finish


def leave_kernel(
    n_i,
    rows,
    part_ref,
    weight_ref,
    out_ref,
    weight_out,
    held,
    from_core,
    from_a,
    from_b,
    from_z,
    sums,
    from_low,
    from_high,
    load_sem,
    core_send,
    a_send,
    b_send,
    z_send,
    core_recv,
    a_recv,
    b_recv,
    z_recv,
    copy_sem,
    chain_send,
    low_recv,
    high_recv,
):
    n_z = lax.axis_size("gx")
    copy = pltpu.make_async_copy(weight_ref, sums, copy_sem)
    copy.start()
    chain = chain_scatter(
        n_z, sums, weight_out, from_low, from_high, chain_send, low_recv, high_recv
    )

    def start():
        copy.wait()
        chain[0]()

    scatter_kernel(
        False,
        n_i,
        rows,
        part_ref,
        out_ref,
        held,
        from_core,
        from_a,
        from_b,
        from_z,
        load_sem,
        core_send,
        a_send,
        b_send,
        z_send,
        core_recv,
        a_recv,
        b_recv,
        z_recv,
        (start, chain[1], chain[2]),
    )


def leave(part, weight_part, collective_id):
    n_z = lax.axis_size("gx")
    span = lax.axis_size("gy")
    pieces, _, _, rows, cols = part.shape
    total = span * pieces * 2 * rows
    half = (rows, cols)
    dma = pltpu.SemaphoreType.DMA
    block = (weight_part.shape[0] // n_z, weight_part.shape[1])
    out, sums = pl.pallas_call(
        partial(leave_kernel, pieces, rows),
        out_shape=(
            jax.ShapeDtypeStruct((pieces, 2, rows, cols), jnp.float32),
            jax.ShapeDtypeStruct(block, jnp.float32),
        ),
        in_specs=[pl.BlockSpec(memory_space=pl.ANY)] * 2,
        out_specs=(pl.BlockSpec(memory_space=pltpu.VMEM),) * 2,
        scratch_shapes=[
            pltpu.VMEM((pieces, 4, 2) + half, jnp.bfloat16),
            pltpu.VMEM((pieces, 4, 2) + half, jnp.bfloat16),
            pltpu.VMEM((pieces, 2, 2) + half, jnp.bfloat16),
            pltpu.VMEM((pieces, 2) + half, jnp.bfloat16),
            pltpu.VMEM((1, 2, 16, 128), jnp.bfloat16),
            pltpu.VMEM((n_z,) + block, jnp.bfloat16),
            pltpu.VMEM((n_z,) + block, jnp.bfloat16),
            pltpu.VMEM((n_z,) + block, jnp.bfloat16),
            dma((pieces, 4)),
            dma((pieces, 4)),
            dma((pieces, 4)),
            dma((pieces, 2)),
            dma((pieces,)),
            dma((pieces, 4)),
            dma((pieces, 2, 2)),
            dma((pieces, 2)),
            dma((pieces,)),
            dma,
            dma((n_z,)),
            dma((n_z,)),
            dma((n_z,)),
        ],
        compiler_params=pltpu.CompilerParams(
            collective_id=collective_id, has_side_effects=True, vmem_limit_bytes=60 << 20
        ),
        name="leave",
    )(part, weight_part.reshape((n_z,) + block))
    return out.reshape(total // span, cols), sums


def expert_kernel(n_z, span, own_ref, cot_ref, share_ref, gate_ref, up_ref, down_ref,
                  all_ref, pair_ref, dots_ref, down_out, out_ref,
                  moe_buf, cot_buf, share_buf, pair_stage, dots_buf,
                  gate_val, up_val, scaled, scaled_t, down_t,
                  held, from_core, from_a, from_b, from_z,
                  send_sem, recv_sem, local_sem, fetch_sem, store_sem,
                  core_send, a_send, b_send, z_send, core_recv, a_recv, b_recv, z_recv):
    z = lax.axis_index("gx")
    g = lax.axis_index("gy")
    rows = own_ref.shape[1]
    block = 2 * rows
    step_rows = moe_buf.shape[1]
    steps = 2 * n_z
    flip_x = g + 2 - 4 * ((g // 2) % 2)
    flip_y = g + 4 - 8 * ((g // 4) % 2)
    flip_both = flip_x + flip_y - g
    core = {"gx": z, "gy": flip(g)}
    x_peer = {"gx": z, "gy": flip_x}
    y_peer = {"gx": z, "gy": flip_y}
    above = {"gx": z + 1, "gy": g}
    below = {"gx": z - 1, "gy": g}

    order = [z]
    candidates = []
    for d in range(1, n_z):
        candidates += [(z >= d, z - d), (z < n_z - d, z + d)]
    for k in range(1, n_z):
        rank, chosen = 0, 0
        for ok, owner in candidates:
            ok = ok.astype(jnp.int32)
            rank = rank + ok
            chosen = chosen + ok * (rank == k).astype(jnp.int32) * owner
        order.append(chosen)

    onward = [(z < n_z - 1, z > 0)]
    for owner in order[1:]:
        onward.append(
            (
                jnp.logical_and(owner < z, z < n_z - 1),
                jnp.logical_and(owner > z, z > 0),
            )
        )
    along = [{"gx": lax.rem(z + j, n_z), "gy": g} for j in range(1, n_z)]
    barrier_with([(z >= 0, peer) for peer in (core, x_peer, y_peer, *along)])

    def at(owner, gg, h):
        return pl.ds(pl.multiple_of((owner * span + gg) * block + h * rows, rows), rows)

    def copy(k, slot, owner, gg, h, peer, own=False):
        return pltpu.make_async_remote_copy(
            src_ref=own_ref.at[h] if own else all_ref.at[at(owner, gg, h)],
            dst_ref=all_ref.at[at(owner, gg, h)],
            send_sem=send_sem.at[k, slot],
            recv_sem=recv_sem.at[owner * span + gg, h],
            device_id=peer,
            device_id_type=pl.DeviceIdType.MESH,
        )

    sends = []

    def send(ok, *where, **options):
        k = where[0]
        slot = sum(1 for entry in sends if entry[2] == k)
        make = partial(copy, k, slot, *where[1:], **options)
        sends.append((ok, make, k))
        run_if(ok, lambda: make().start())

    def arrive(owner, gg, h):
        copy(0, 0, owner, gg, h, core).wait_recv()

    locals_ = [
        pltpu.make_async_copy(own_ref.at[h], all_ref.at[at(z, g, h)], local_sem.at[h])
        for h in range(2)
    ]

    def first(k):
        owner = order[k]
        own = k == 0
        if own:
            for item in locals_:
                item.start()
        else:
            arrive(owner, g, 0)
            arrive(owner, g, 1)
        go_up, go_down = onward[k]
        for h in range(2):
            send(go_up, k, owner, g, h, above, own=own)
            send(go_down, k, owner, g, h, below, own=own)
        send(True, k, owner, g, 0, x_peer, own=own)
        send(True, k, owner, g, 1, y_peer, own=own)
        send(True, k, owner, g, 1, x_peer, own=own)
        send(True, k, owner, g, 0, y_peer, own=own)
        send(True, k, owner, g, 0, core, own=own)
        send(True, k, owner, g, 1, core, own=own)

    def second(k):
        owner = order[k]
        arrive(owner, flip_x, 0)
        send(True, k, owner, flip_x, 0, y_peer)
        send(True, k, owner, flip_x, 0, core)
        arrive(owner, flip_y, 1)
        send(True, k, owner, flip_y, 1, x_peer)
        send(True, k, owner, flip_y, 1, core)

    def third(k):
        owner = order[k]
        for gg, h in ((flip_y, 0), (flip_x, 1), (flip_both, 0), (flip_both, 1)):
            arrive(owner, gg, h)
            send(True, k, owner, gg, h, core)

    def complete(k):
        for gg in (g, flip_x, flip_y, flip_both):
            for h in range(2):
                arrive(order[k], flip(gg), h)
        if k == 0:
            for item in locals_:
                item.wait()

    def place(s):
        k, side = (s // 2, s % 2) if isinstance(s, int) else (lax.div(s, 2), lax.rem(s, 2))
        if isinstance(s, int):
            owner = order[k]
        else:
            owner = sum((k == j).astype(jnp.int32) * order[j] for j in range(n_z))
        return pl.ds(pl.multiple_of(owner * (span * block) + side * step_rows, step_rows), step_rows)

    def parity(s):
        return s % 2 if isinstance(s, int) else lax.rem(s, 2)

    def fetches(s):
        slot = parity(s)
        return [
            pltpu.make_async_copy(source.at[place(s)], target.at[slot], fetch_sem.at[j, slot])
            for j, (source, target) in enumerate(
                ((all_ref, moe_buf), (cot_ref, cot_buf), (share_ref, share_buf))
            )
        ]

    def stores(s):
        slot = parity(s)
        pairs = ((dots_buf, dots_ref), (pair_stage, pair_ref))
        return [
            pltpu.make_async_copy(
                pairs[j][0].at[slot], pairs[j][1].at[place(s)], store_sem.at[j, slot]
            )
            for j in range(2)
        ]

    f32 = jnp.float32
    dot = partial(lax.dot_general, preferred_element_type=f32)
    plain = (((1,), (0,)), ((), ()))
    last_dims = (((1,), (1,)), ((), ()))
    first_dims = (((0,), (0,)), ((), ()))
    half_width = scaled.shape[1]
    width = moe_buf.shape[2]
    tile = 256

    quads = (flip_both, flip_x, flip_y, g)

    def remote(src, dst, ssem, rsem, peer):
        return pltpu.make_async_remote_copy(
            src_ref=src,
            dst_ref=dst,
            send_sem=ssem,
            recv_sem=rsem,
            device_id=peer,
            device_id_type=pl.DeviceIdType.MESH,
        )

    def core_copy(k, q):
        return remote(
            held.at[k, flip(quads[q])],
            from_core.at[k, q],
            core_send.at[k, q],
            core_recv.at[k, q],
            core,
        )

    a_plan = ((0, 0, 0, x_peer), (0, 1, 0, y_peer), (1, 0, 1, x_peer), (2, 1, 1, y_peer))

    def a_copy(k, j):
        q, h, slot, peer = a_plan[j]
        return remote(
            held.at[k, quads[q], h],
            from_a.at[k, h, slot],
            a_send.at[k, j],
            a_recv.at[k, h, slot],
            peer,
        )

    b_plan = ((2, y_peer), (1, x_peer))

    def b_copy(k, h):
        q, peer = b_plan[h]
        return remote(
            held.at[k, quads[q], h], from_b.at[k, h], b_send.at[k, h], b_recv.at[k, h], peer
        )

    def z_copy(k):
        return remote(
            held.at[k, g], from_z.at[z], z_send.at[k], z_recv.at[z], {"gx": order[k], "gy": g}
        )

    def stage_core(k):
        for q in range(4):
            core_copy(k, q).start()

    def stage_a(k):
        for q in range(4):
            core_copy(k, q).wait_recv()
            for h in range(2):
                mine = held.at[k, quads[q], h]
                add_into(mine, (mine, from_core.at[k, q, h]), rows)
            for j in range(4):
                if a_plan[j][0] == q:
                    a_copy(k, j).start()

    def stage_b(k):
        for q, h, slot in ((2, 0, 0), (1, 1, 0), (3, 0, 1), (3, 1, 1)):
            mine, arrived = held.at[k, quads[q], h], from_a.at[k, h, slot]
            remote(mine, arrived, a_send.at[k, 0], a_recv.at[k, h, slot], core).wait_recv()
            add_into(mine, (mine, arrived), rows)
            if slot == 0:
                b_copy(k, h).start()

    def stage_c(k):
        for h in range(2):
            b_copy(k, h).wait_recv()
            mine = held.at[k, g, h]
            add_into(mine, (mine, from_b.at[k, h]), rows)
        if k > 0:
            z_copy(k).start()

    backs = (
        (stage_core, lambda k: 2 * k + 1, 2),
        (stage_a, lambda k: 2 * k + 2, 2),
        (stage_b, lambda k: 2 * k + 3, 2),
        (stage_c, lambda k: 2 * k + 4, 1),
    )

    def events(s, phase):
        for action, start, when in backs:
            for k in range(n_z):
                if when == phase and start(k) < steps:
                    pl.when(s == start(k))(partial(action, k))
        for k in range(1, n_z):
            if k >= 2 and phase == 1:
                pl.when(s == k - 2)(partial(first, k))
            if phase == 2:
                pl.when(s == 2 * (k - 1))(partial(second, k))
            if phase == 2:
                pl.when(s == 2 * (k - 1) + 1)(partial(third, k))
            if phase == 4:
                pl.when(s == 2 * k - 1)(partial(complete, k))

    first(0)

    @pl.loop(0, width // tile)
    def _(t):
        cols = pl.ds(pl.multiple_of(t * tile, tile), tile)
        down_t[cols, :] = down_ref[:, cols].T

    second(0)
    if n_z > 1:
        first(1)
    third(0)
    complete(0)
    for item in fetches(0):
        item.start()

    @pl.loop(0, steps)
    def _(s):
        slot = lax.rem(s, 2)
        moe, cot, share = moe_buf.at[slot], cot_buf.at[slot], share_buf.at[slot]
        for item in fetches(s):
            item.wait()

        @pl.when(s >= 2)
        def _():
            for item in stores(s - 2):
                item.wait()

        wide = jnp.concatenate([share[...]] * (tile // share.shape[1]), axis=1)

        @pl.loop(0, half_width // tile)
        def _(t):
            cols = pl.ds(pl.multiple_of(t * tile, tile), tile)
            gated = dot(moe[...], gate_ref[:, cols], plain)
            lifted = dot(moe[...], up_ref[:, cols], plain)
            gate_val[:, cols] = gated
            up_val[:, cols] = lifted
            scaled[:, cols] = (gated * jax.nn.sigmoid(gated) * lifted * wide).astype(jnp.bfloat16)

        events(s, 1)
        scaled_t[...] = scaled[...].T

        @pl.loop(0, width // (2 * tile))
        def _(t):
            cols = pl.ds(pl.multiple_of(t * 2 * tile, 2 * tile), 2 * tile)
            sent = dot(scaled[...], down_ref[:, cols], plain).astype(jnp.bfloat16)
            held[lax.div(s, 2), pl.ds(slot * (span // 2), span // 2), :, :, cols] = sent.reshape(
                (span // 2, 2, rows, 2 * tile)
            )

        events(s, 2)
        dots_buf[slot] = jnp.zeros(dots_buf.shape[1:], f32)

        @pl.loop(0, half_width // tile)
        def _(t):
            cols = pl.ds(pl.multiple_of(t * tile, tile), tile)
            pulled = dot(cot[...], down_t[:, cols], plain)
            gated = gate_val[:, cols]
            lifted = up_val[:, cols]
            sig = jax.nn.sigmoid(gated)
            silu = gated * sig
            product = pulled * (silu * lifted)
            lanes = share.shape[1]
            dots_buf[slot] = dots_buf[slot] + sum(
                product[:, j * lanes : (j + 1) * lanes] for j in range(tile // lanes)
            )
            pulled = pulled * wide
            pair_stage[slot, :, cols] = (pulled * lifted * sig * (1.0 + gated * (1.0 - sig))).astype(
                jnp.bfloat16
            )
            more = pl.ds(pl.multiple_of(half_width + t * tile, tile), tile)
            pair_stage[slot, :, more] = (pulled * silu).astype(jnp.bfloat16)

        for item in stores(s):
            item.start()
        events(s, 3)
        events(s, 4)

        @pl.when(s < steps - 1)
        def _():
            for item in fetches(s + 1):
                item.start()

        @pl.loop(0, width // (2 * tile))
        def _(t):
            cols = pl.ds(pl.multiple_of(t * 2 * tile, 2 * tile), 2 * tile)
            grown = dot(scaled_t[...], cot[:, cols], plain)
            down_out[:, cols] = jnp.where(s == 0, 0.0, down_out[:, cols]) + grown

    for t in range(steps, 2 * steps):
        for action, start, _ in backs[::-1]:
            for k in range(n_z):
                if start(k) == t:
                    action(k)
    for s in (steps - 2, steps - 1):
        for item in stores(s):
            item.wait()
    for k in range(1, n_z):
        arrived = from_z.at[order[k]]
        remote(held.at[k, g], arrived, z_send.at[k], z_recv.at[order[k]], core).wait_recv()
    for h in range(2):
        terms = [held.at[0, g, h]] + [from_z.at[order[k], h] for k in range(1, n_z)]
        add_into(out_ref.at[h], terms, rows)
    for k in range(n_z):
        for q in range(4):
            core_copy(k, q).wait_send()
        for j in range(4):
            a_copy(k, j).wait_send()
        for h in range(2):
            b_copy(k, h).wait_send()
        if k > 0:
            z_copy(k).wait_send()
    for ok, make, k in sends:
        run_if(ok, lambda make=make: make().wait_send())


def run_experts(moe_in, all_cot, shares, gate_w, up_w, down_w, collective_id):
    n_z = lax.axis_size("gx")
    span = lax.axis_size("gy")
    rows, width = moe_in.shape
    half = down_w.shape[0]
    total = n_z * span * rows
    step = span * rows // 2
    lanes = shares.shape[1]
    bf16, f32 = jnp.bfloat16, jnp.float32
    dma = pltpu.SemaphoreType.DMA
    vmem = pl.BlockSpec(memory_space=pltpu.VMEM)
    hbm = pl.BlockSpec(memory_space=pl.ANY)
    return pl.pallas_call(
        partial(expert_kernel, n_z, span),
        out_shape=(
            jax.ShapeDtypeStruct((total, width), bf16),
            jax.ShapeDtypeStruct((total, 2 * half), bf16),
            jax.ShapeDtypeStruct((total, lanes), f32),
            jax.ShapeDtypeStruct((half, width), f32),
            jax.ShapeDtypeStruct((2, rows // 2, width), f32),
        ),
        in_specs=[vmem, hbm, hbm, vmem, vmem, vmem],
        out_specs=(hbm, hbm, hbm, vmem, vmem),
        scratch_shapes=[
            pltpu.VMEM((2, step, width), bf16),
            pltpu.VMEM((2, step, width), bf16),
            pltpu.VMEM((2, step, lanes), f32),
            pltpu.VMEM((2, step, 2 * half), bf16),
            pltpu.VMEM((2, step, lanes), f32),
            pltpu.VMEM((step, half), f32),
            pltpu.VMEM((step, half), f32),
            pltpu.VMEM((step, half), bf16),
            pltpu.VMEM((half, step), bf16),
            pltpu.VMEM((width, half), bf16),
            pltpu.VMEM((n_z, span, 2, rows // 2, width), bf16),
            pltpu.VMEM((n_z, 4, 2, rows // 2, width), bf16),
            pltpu.VMEM((n_z, 2, 2, rows // 2, width), bf16),
            pltpu.VMEM((n_z, 2, rows // 2, width), bf16),
            pltpu.VMEM((n_z, 2, rows // 2, width), bf16),
            dma((n_z, 18)),
            dma((n_z * span, 2)),
            dma((2,)),
            dma((3, 2)),
            dma((2, 2)),
            dma((n_z, 4)),
            dma((n_z, 4)),
            dma((n_z, 2)),
            dma((n_z,)),
            dma((n_z, 4)),
            dma((n_z, 2, 2)),
            dma((n_z, 2)),
            dma((n_z,)),
        ],
        compiler_params=pltpu.CompilerParams(
            collective_id=collective_id, has_side_effects=True, vmem_limit_bytes=67043328
        ),
        name="experts",
    )(moe_in.reshape(2, rows // 2, width), all_cot, shares, gate_w, up_w, down_w)


def pull_kernel(n_i, rows, all_ref, pair_ref, gate_ref, up_ref, out_ref, gate_out, up_out,
                held, from_core, from_a, from_b, from_z, moe_buf, pair_buf,
                fetch_sem, core_send, a_send, b_send, z_send, core_recv, a_recv, b_recv, z_recv):
    z = lax.axis_index("gx")
    g = lax.axis_index("gy")
    flip_x = g + 2 - 4 * ((g // 2) % 2)
    flip_y = g + 4 - 8 * ((g // 4) % 2)
    quads = (flip_x + flip_y - g, flip_x, flip_y, g)
    core = {"gx": z, "gy": flip(g)}
    x_peer = {"gx": z, "gy": flip_x}
    y_peer = {"gx": z, "gy": flip_y}
    along = [{"gx": lax.rem(z + j, n_i), "gy": g} for j in range(1, n_i)]
    barrier_with([(z >= 0, peer) for peer in (core, x_peer, y_peer, *along)])
    item_rows = moe_buf.shape[1]
    width = moe_buf.shape[2]
    half_width = gate_out.shape[1]
    owners = [lax.rem(z + n_i - 1 - i + n_i, n_i) for i in range(n_i)]

    def remote(src, dst, ssem, rsem, peer):
        return pltpu.make_async_remote_copy(
            src_ref=src,
            dst_ref=dst,
            send_sem=ssem,
            recv_sem=rsem,
            device_id=peer,
            device_id_type=pl.DeviceIdType.MESH,
        )

    def fetches(i):
        place = pl.ds(pl.multiple_of(owners[i] * item_rows, item_rows), item_rows)
        return [
            pltpu.make_async_copy(all_ref.at[place], moe_buf.at[i % 2], fetch_sem.at[0, i % 2]),
            pltpu.make_async_copy(pair_ref.at[place], pair_buf.at[i % 2], fetch_sem.at[1, i % 2]),
        ]

    def core_copy(i, q):
        return remote(
            held.at[i, flip(quads[q])],
            from_core.at[i, q],
            core_send.at[i, q],
            core_recv.at[i, q],
            core,
        )

    a_plan = ((0, 0, 0, x_peer), (0, 1, 0, y_peer), (1, 0, 1, x_peer), (2, 1, 1, y_peer))

    def a_copy(i, k):
        q, h, slot, peer = a_plan[k]
        return remote(
            held.at[i, quads[q], h],
            from_a.at[i, h, slot],
            a_send.at[i, k],
            a_recv.at[i, h, slot],
            peer,
        )

    b_plan = ((2, y_peer), (1, x_peer))

    def b_copy(i, h):
        q, peer = b_plan[h]
        return remote(
            held.at[i, quads[q], h], from_b.at[i, h], b_send.at[i, h], b_recv.at[i, h], peer
        )

    def z_copy(i):
        return remote(
            held.at[i, g], from_z.at[z], z_send.at[i], z_recv.at[z], {"gx": owners[i], "gy": g}
        )

    dot = partial(lax.dot_general, preferred_element_type=jnp.float32)
    last_dims = (((1,), (1,)), ((), ()))
    first_dims = (((0,), (0,)), ((), ()))

    def multiply(i):
        for copy in fetches(i):
            copy.wait()
        pair = pair_buf.at[i % 2]
        tile = 256

        @pl.loop(0, width // tile)
        def _(t):
            cols = pl.ds(pl.multiple_of(t * tile, tile), tile)
            total = dot(pair[:, :half_width], gate_ref[cols, :], last_dims)
            total = total + dot(pair[:, half_width:], up_ref[cols, :], last_dims)
            held[i, :, :, :, cols] = total.astype(jnp.bfloat16).reshape(held.shape[1:4] + (tile,))

        for q in range(4):
            core_copy(i, q).start()

    def accumulate(i):
        moe, pair = moe_buf.at[i % 2], pair_buf.at[i % 2]
        tile = 256

        @pl.loop(0, width // tile)
        def _(t):
            cols = pl.ds(pl.multiple_of(t * tile, tile), tile)
            grown = dot(moe[:, cols], pair[...], first_dims)
            if i == 0:
                gate_out[cols, :] = grown[:, :half_width]
                up_out[cols, :] = grown[:, half_width:]
            else:
                gate_out[cols, :] = gate_out[cols, :] + grown[:, :half_width]
                up_out[cols, :] = up_out[cols, :] + grown[:, half_width:]

        if i + 2 < n_i:
            for copy in fetches(i + 2):
                copy.start()

    def stage_a(i):
        for q in range(4):
            core_copy(i, q).wait_recv()
            for h in range(2):
                mine = held.at[i, quads[q], h]
                add_into(mine, (mine, from_core.at[i, q, h]), rows)
            for k in range(4):
                if a_plan[k][0] == q:
                    a_copy(i, k).start()

    def stage_b(i):
        for q, h, slot in ((2, 0, 0), (1, 1, 0), (3, 0, 1), (3, 1, 1)):
            mine, arrived = held.at[i, quads[q], h], from_a.at[i, h, slot]
            remote(mine, arrived, a_send.at[i, 0], a_recv.at[i, h, slot], core).wait_recv()
            add_into(mine, (mine, arrived), rows)
            if slot == 0:
                b_copy(i, h).start()

    def stage_c(i):
        for h in range(2):
            b_copy(i, h).wait_recv()
            mine = held.at[i, g, h]
            add_into(mine, (mine, from_b.at[i, h]), rows)
        if i < n_i - 1:
            z_copy(i).start()
        else:
            for j in range(n_i - 1):
                arrived = from_z.at[owners[j]]
                remote(held.at[j, g], arrived, z_send.at[j], z_recv.at[owners[j]], core).wait_recv()
            for h in range(2):
                terms = [held.at[i, g, h]] + [from_z.at[owners[j], h] for j in range(n_i - 1)]
                add_into(out_ref.at[h], terms, rows)

    for i in range(min(2, n_i)):
        for copy in fetches(i):
            copy.start()
    for t in range(n_i + 3):
        if t < n_i:
            multiply(t)
        if 0 <= t - 1 < n_i:
            stage_a(t - 1)
        if 0 <= t - 2 < n_i:
            stage_b(t - 2)
        if 0 <= t - 1 < n_i:
            accumulate(t - 1)
        if 0 <= t - 3 < n_i:
            stage_c(t - 3)
    for i in range(n_i):
        for q in range(4):
            core_copy(i, q).wait_send()
        for k in range(4):
            a_copy(i, k).wait_send()
        for h in range(2):
            b_copy(i, h).wait_send()
        if i < n_i - 1:
            z_copy(i).wait_send()


def pull_experts(all_moe, pair, gate_w, up_w, collective_id):
    n_i = lax.axis_size("gx")
    span = lax.axis_size("gy")
    total, width = all_moe.shape
    half_width = gate_w.shape[1]
    rows = total // (n_i * span) // 2
    half = (rows, width)
    bf16 = jnp.bfloat16
    dma = pltpu.SemaphoreType.DMA
    vmem = pl.BlockSpec(memory_space=pltpu.VMEM)
    hbm = pl.BlockSpec(memory_space=pl.ANY)
    out, gate_part, up_part = pl.pallas_call(
        partial(pull_kernel, n_i, rows),
        out_shape=(
            jax.ShapeDtypeStruct((2,) + half, jnp.float32),
            jax.ShapeDtypeStruct((width, half_width), jnp.float32),
            jax.ShapeDtypeStruct((width, half_width), jnp.float32),
        ),
        in_specs=[hbm, hbm, vmem, vmem],
        out_specs=(vmem, vmem, vmem),
        scratch_shapes=[
            pltpu.VMEM((n_i, span, 2) + half, bf16),
            pltpu.VMEM((n_i, 4, 2) + half, bf16),
            pltpu.VMEM((n_i, 2, 2) + half, bf16),
            pltpu.VMEM((n_i, 2) + half, bf16),
            pltpu.VMEM((n_i, 2) + half, bf16),
            pltpu.VMEM((2, span * 2 * rows, width), bf16),
            pltpu.VMEM((2, span * 2 * rows, 2 * half_width), bf16),
            dma((2, 2)),
            dma((n_i, 4)),
            dma((n_i, 4)),
            dma((n_i, 2)),
            dma((n_i,)),
            dma((n_i, 4)),
            dma((n_i, 2, 2)),
            dma((n_i, 2)),
            dma((n_i,)),
        ],
        compiler_params=pltpu.CompilerParams(
            collective_id=collective_id, has_side_effects=True, vmem_limit_bytes=67043328
        ),
        name="pull_experts",
    )(all_moe, pair, gate_w, up_w)
    return out.reshape(2 * rows, width), gate_part, up_part


def turn(values, cosine, sine):
    return values * cosine + pltpu.roll(values, values.shape[-1] // 2, 1) * sine


def greet_chain(n_z):
    z = lax.axis_index("gx")
    g = lax.axis_index("gy")
    barrier_with([(z < n_z - 1, {"gx": z + 1, "gy": g}), (z > 0, {"gx": z - 1, "gy": g})])


def attend_kernel(
    heads,
    pieces,
    acts_ref,
    weight_ref,
    out_weight_ref,
    query_gain,
    key_gain,
    cosine_ref,
    sine_ref,
    row_docs,
    col_docs,
    part_ref,
    query_raw,
    key_raw,
    ready_ref,
    mixed_ref,
    totals_ref,
    peaks_ref,
    full_out,
    chain_send,
    chain_recv,
    chain_local,
):
    n_z = lax.axis_size("gx")
    greet_chain(n_z)
    start, relays, finish = chain_gather(
        n_z, out_weight_ref, full_out, chain_send, chain_recv, chain_local
    )
    start()
    f32, bf16 = jnp.float32, jnp.bfloat16
    dot = partial(lax.dot_general, preferred_element_type=f32)
    plain = (((1,), (0,)), ((), ()))
    last_dims = (((1,), (1,)), ((), ()))
    length = acts_ref.shape[0]
    span = part_ref.shape[1]
    local = heads * HD
    block = 256
    scale = HD ** (-0.5)

    for source, raw, gain in ((0, query_raw, query_gain), (1, key_raw, key_gain)):
        raw[...] = dot(acts_ref[...], weight_ref[:, source * local : (source + 1) * local], plain)
        for h in range(heads):
            cols = slice(h * HD, (h + 1) * HD)

            @pl.loop(0, length // block)
            def _(t):
                at = pl.ds(pl.multiple_of(t * block, block), block)
                value = raw[at, cols]
                normed = value * lax.rsqrt(jnp.mean(value * value, axis=-1, keepdims=True) + EPSILON)
                turned = turn(normed * gain[...], cosine_ref[at, :], sine_ref[at, :])
                where = source * local + h * HD
                ready_ref[at, where : where + HD] = turned.astype(bf16)

        if source < len(relays) - 1:
            relays[source]()

    ready_ref[:, 2 * local :] = dot(acts_ref[...], weight_ref[:, 2 * local :], plain).astype(bf16)
    lanes = lax.broadcasted_iota(jnp.int32, (block, HD), 1)
    peaks_ref[...] = jnp.full(peaks_ref.shape, NEGATIVE, f32)

    @pl.loop(0, length // block)
    def _(t):
        at = pl.ds(pl.multiple_of(t * block, block), block)
        same = row_docs[at, :1] == col_docs[:1, :]
        kept = jnp.zeros((block, HD), f32)
        for h in range(heads):
            query = ready_ref[at, h * HD : (h + 1) * HD]
            key = ready_ref[:, local + h * HD : local + (h + 1) * HD]
            value = ready_ref[:, 2 * local + h * HD : 2 * local + (h + 1) * HD]
            scores = jnp.where(same, dot(query, key, last_dims) * scale, NEGATIVE)
            highest = jnp.max(scores, axis=-1, keepdims=True)
            weights = jnp.exp(scores - highest)
            total = jnp.sum(weights, axis=-1, keepdims=True)
            shares = (weights * (1.0 / total)).astype(bf16)
            mixed_ref[at, h * HD : (h + 1) * HD] = dot(shares, value, plain).astype(bf16)
            kept = jnp.where(lanes == h, highest + jnp.log(total), kept)
            top = jnp.max(highest, axis=0, keepdims=True)
            peaks_ref[h : h + 1, :] = jnp.maximum(peaks_ref[h : h + 1, :], top)
        totals_ref[at, :] = kept

    for relay in relays[min(2, len(relays) - 1) :]:
        relay()
    finish()
    rows = part_ref.shape[3]
    per_owner = out_weight_ref.shape[1] // block

    @pl.loop(0, n_z * per_owner)
    def _(t):
        cols = pl.ds(pl.multiple_of(t * block, block), block)
        inside = pl.ds(pl.multiple_of(lax.rem(t, per_owner) * block, block), block)
        sent = dot(mixed_ref[...], full_out[lax.div(t, per_owner), :, inside], plain).astype(bf16)
        sent = sent.reshape(span, pieces, 2, rows, block)
        for p in range(pieces):
            part_ref[p, :, :, :, cols] = sent[:, p]


def attend(acts, weights, out_weight, query_gain, key_gain, tables, docs, collective_id, pieces=4):
    length, width = acts.shape
    local = weights.shape[1] // 3
    heads = local // HD
    span = lax.axis_size("gy")
    n_z = lax.axis_size("gx")
    rows = length // (span * pieces * 2)
    f32, bf16 = jnp.float32, jnp.bfloat16
    dma = pltpu.SemaphoreType.DMA
    vmem = pl.BlockSpec(memory_space=pltpu.VMEM)
    return pl.pallas_call(
        partial(attend_kernel, heads, pieces),
        out_shape=(
            jax.ShapeDtypeStruct((pieces, span, 2, rows, width), bf16),
            jax.ShapeDtypeStruct((length, local), f32),
            jax.ShapeDtypeStruct((length, local), f32),
            jax.ShapeDtypeStruct((length, 3 * local), bf16),
            jax.ShapeDtypeStruct((length, local), bf16),
            jax.ShapeDtypeStruct((length, HD), f32),
            jax.ShapeDtypeStruct((8, HD), f32),
            jax.ShapeDtypeStruct((n_z,) + out_weight.shape, bf16),
        ),
        in_specs=[vmem] * 9,
        out_specs=(vmem,) * 8,
        scratch_shapes=[dma((2 * n_z,)), dma((n_z,)), dma],
        compiler_params=pltpu.CompilerParams(
            collective_id=collective_id, has_side_effects=True, vmem_limit_bytes=60 << 20
        ),
        name="attend",
    )(
        acts,
        weights,
        out_weight,
        query_gain.reshape(1, HD),
        key_gain.reshape(1, HD),
        *tables,
        *docs,
    )


def attend_back_kernel(
    heads,
    pieces,
    grad_ref,
    out_weight_ref,
    mixed_ref,
    ready_ref,
    query_raw,
    key_raw,
    totals_ref,
    query_gain,
    key_gain,
    cosine_ref,
    sine_ref,
    row_docs,
    col_docs,
    acts_hbm,
    weight_hbm,
    part_ref,
    weight_part,
    out_sum,
    gain_ref,
    acts_ref,
    weight_ref,
    grad_mixed,
    grad_heads,
    turned,
    key_sum,
    value_sum,
    sums,
    from_low,
    from_high,
    copy_sem,
    chain_send,
    low_recv,
    high_recv,
):
    n_z = lax.axis_size("gx")
    greet_chain(n_z)
    start, relays, finish = chain_scatter(
        n_z, sums, out_sum, from_low, from_high, chain_send, low_recv, high_recv
    )
    f32, bf16 = jnp.float32, jnp.bfloat16
    dot = partial(lax.dot_general, preferred_element_type=f32)
    plain = (((1,), (0,)), ((), ()))
    last_dims = (((1,), (1,)), ((), ()))
    first_dims = (((0,), (0,)), ((), ()))
    length, width = grad_ref.shape
    span = part_ref.shape[1]
    rows = part_ref.shape[3]
    local = heads * HD
    block = 256
    scale = HD ** (-0.5)
    copies = [
        pltpu.make_async_copy(acts_hbm, acts_ref, copy_sem.at[0]),
        pltpu.make_async_copy(weight_hbm, weight_ref, copy_sem.at[1]),
    ]
    for copy in copies:
        copy.start()
    owned = width // n_z

    @pl.loop(0, width // block)
    def _(t):
        cols = pl.ds(pl.multiple_of(t * block, block), block)
        inside = pl.ds(pl.multiple_of(lax.rem(t, owned // block) * block, block), block)
        sums[lax.div(t, owned // block), inside, :] = dot(
            grad_ref[:, cols], mixed_ref[...], first_dims
        ).astype(bf16)

    start()
    total = dot(grad_ref[:, :owned], out_weight_ref[0], last_dims)
    for owner in range(1, n_z):
        cols = slice(owner * owned, (owner + 1) * owned)
        total = total + dot(grad_ref[:, cols], out_weight_ref[owner], last_dims)
    grad_mixed[...] = total.astype(bf16)
    gain_ref[...] = jnp.zeros_like(gain_ref)
    for h in range(heads):
        cols = slice(h * HD, (h + 1) * HD)
        key = ready_ref[:, local + h * HD : local + (h + 1) * HD]
        value = ready_ref[:, 2 * local + h * HD : 2 * local + (h + 1) * HD]
        key_sum[...] = jnp.zeros_like(key_sum)
        value_sum[...] = jnp.zeros_like(value_sum)

        @pl.loop(0, length // block)
        def _(t):
            at = pl.ds(pl.multiple_of(t * block, block), block)
            same = row_docs[at, :1] == col_docs[:1, :]
            query = ready_ref[at, cols]
            grad = grad_mixed[at, cols]
            scores = jnp.where(same, dot(query, key, last_dims) * scale, NEGATIVE)
            weights = jnp.exp(scores - totals_ref[at, h : h + 1])
            value_sum[...] += dot(weights.astype(bf16), grad, first_dims)
            pulled = dot(grad, value, last_dims)
            inner = jnp.sum(weights * pulled, axis=-1, keepdims=True)
            grad_scores = (weights * (pulled - inner)).astype(bf16)
            turned[at, :] = dot(grad_scores, key, plain) * scale
            key_sum[...] += dot(grad_scores, query, first_dims)

        for source, raw, gain, incoming, factor in (
            (0, query_raw, query_gain, turned, 1.0),
            (1, key_raw, key_gain, key_sum, scale),
        ):

            @pl.loop(0, length // block)
            def _(t):
                at = pl.ds(pl.multiple_of(t * block, block), block)
                back = turn(incoming[at, :] * factor, cosine_ref[at, :], -sine_ref[at, :])
                item = raw[at, cols]
                inverse = lax.rsqrt(jnp.mean(item * item, axis=-1, keepdims=True) + EPSILON)
                normed = item * inverse
                gain_ref[source : source + 1, :] += jnp.sum(back * normed, axis=0, keepdims=True)
                inner = back * gain[...]
                pulled = inverse * (
                    inner - normed * jnp.mean(inner * normed, axis=-1, keepdims=True)
                )
                where = source * local + h * HD
                grad_heads[at, where : where + HD] = pulled.astype(bf16)

        where = 2 * local + h * HD
        grad_heads[:, where : where + HD] = value_sum[...].astype(bf16)
        if h < len(relays) - 1:
            relays[h]()

    for relay in relays[min(heads, len(relays) - 1) :]:
        relay()
    finish()

    for copy in copies:
        copy.wait()

    @pl.loop(0, width // block)
    def _(t):
        cols = pl.ds(pl.multiple_of(t * block, block), block)
        weight_part[cols, :] = dot(acts_ref[:, cols], grad_heads[...], first_dims).astype(bf16)
        sent = dot(grad_heads[...], weight_ref[cols, :], last_dims).astype(bf16)
        sent = sent.reshape(span, pieces, 2, rows, block)
        for p in range(pieces):
            part_ref[p, :, :, :, cols] = sent[:, p]


def attend_back(
    seq_grad,
    saved,
    query_gain,
    key_gain,
    tables,
    docs,
    acts,
    weights,
    collective_id,
    pieces=4,
):
    query_raw, key_raw, ready, mixed, totals, out_weight = saved
    n_z = lax.axis_size("gx")
    dma = pltpu.SemaphoreType.DMA
    block = (n_z, acts.shape[1] // n_z, query_raw.shape[1])
    length, width = seq_grad.shape
    local = query_raw.shape[1]
    heads = local // HD
    span = lax.axis_size("gy")
    rows = length // (span * pieces * 2)
    f32, bf16 = jnp.float32, jnp.bfloat16
    vmem = pl.BlockSpec(memory_space=pltpu.VMEM)
    hbm = pl.BlockSpec(memory_space=pl.ANY)
    return pl.pallas_call(
        partial(attend_back_kernel, heads, pieces),
        out_shape=(
            jax.ShapeDtypeStruct((pieces, span, 2, rows, width), bf16),
            jax.ShapeDtypeStruct((width, 3 * local), bf16),
            jax.ShapeDtypeStruct(block[1:], f32),
            jax.ShapeDtypeStruct((8, HD), f32),
        ),
        in_specs=[vmem] * 13 + [hbm] * 2,
        out_specs=(vmem,) * 4,
        scratch_shapes=[
            pltpu.VMEM((length, width), bf16),
            pltpu.VMEM((width, 3 * local), bf16),
            pltpu.VMEM((length, local), bf16),
            pltpu.VMEM((length, 3 * local), bf16),
            pltpu.VMEM((length, HD), f32),
            pltpu.VMEM((length, HD), f32),
            pltpu.VMEM((length, HD), f32),
            pltpu.VMEM(block, bf16),
            pltpu.VMEM(block, bf16),
            pltpu.VMEM(block, bf16),
            dma((2,)),
            dma((n_z,)),
            dma((n_z,)),
            dma((n_z,)),
        ],
        compiler_params=pltpu.CompilerParams(
            collective_id=collective_id, has_side_effects=True, vmem_limit_bytes=60 << 20
        ),
        name="attend_back",
    )(
        seq_grad,
        out_weight,
        mixed,
        ready,
        query_raw,
        key_raw,
        totals,
        query_gain.reshape(1, HD),
        key_gain.reshape(1, HD),
        *tables,
        *docs,
        acts,
        weights,
    )


def norm_rows(values, gain_row):
    return (
        values * lax.rsqrt(jnp.mean(values * values, axis=-1, keepdims=True) + EPSILON) * gain_row
    )


def rotary(values):
    length = values.shape[0]
    halfway = values.shape[-1] // 2
    positions = jnp.arange(length, dtype=jnp.float32)
    frequency = jnp.exp(
        jnp.arange(halfway, dtype=jnp.float32) * (-2.0 * jnp.log(10000.0) / values.shape[-1])
    )
    angles = (positions[:, None] * frequency[None, :])[:, None, :]
    cosine = jnp.cos(angles)
    sine_table = jnp.sin(angles)
    first_half = values[..., :halfway]
    second = values[..., halfway:]
    return jnp.concatenate(
        [first_half * cosine - second * sine_table, second * cosine + first_half * sine_table],
        axis=-1,
    )


def prepare_heads(raw_heads, gain_row):
    return rotary(norm_rows(raw_heads, gain_row))


def route_gates(id_table, logits):
    shares = jax.nn.softmax(logits, axis=-1)
    experts = logits.shape[-1]
    matches = id_table[:, :, None] == jnp.arange(experts, dtype=jnp.int32)[None, None, :]
    chosen = jnp.sum(jnp.where(matches, shares[:, None, :], 0.0), axis=-1)
    return chosen / jnp.sum(chosen, axis=-1, keepdims=True)


def contract_rows(left_side, right_side):
    return lax.dot_general(
        left_side, right_side, (((0,), (0,)), ((), ())), preferred_element_type=jnp.float32
    )


def contract_cols(left_side, right_side):
    return lax.dot_general(
        left_side, right_side, (((1,), (1,)), ((), ())), preferred_element_type=jnp.float32
    )


def routed_experts(
    moe_in, cotangent, expert_ids, gate_share, router_weight, gate_weight, up_weight, down_weight
):
    tok_rows = moe_in.shape[0]
    experts = router_weight.shape[1]
    width_all = moe_in.shape[1]
    capacity = tok_rows * TOP * 3 // (2 * experts)
    route_count = tok_rows * TOP
    flat_ids = expert_ids.reshape(route_count)
    onehot = (flat_ids[:, None] == jnp.arange(experts, dtype=jnp.int32)[None, :]).astype(jnp.int32)
    earlier = jnp.cumsum(onehot, axis=0) - onehot
    slot_index = jnp.sum(earlier * onehot, axis=1)
    target = flat_ids * capacity + slot_index
    source = (
        jnp.full((experts * capacity,), tok_rows, jnp.int32)
        .at[target]
        .set(jnp.arange(route_count, dtype=jnp.int32) // TOP)
    )
    padded_in = jnp.concatenate([moe_in, jnp.zeros((1, width_all), jnp.bfloat16)], axis=0)
    packed = padded_in[source].reshape(experts, 1, capacity, width_all)
    outgoing = jnp.broadcast_to(packed, (experts, 2, capacity, width_all)).reshape(
        2 * experts, capacity, width_all
    )
    arrived = lax.all_to_all(outgoing, ("gx", "gy"), split_axis=0, concat_axis=1, tiled=True)[0]
    gate_in = gate_weight[0]
    up_in = up_weight[0]
    down_in = down_weight[0]
    gate_val = jnp.dot(arrived, gate_in, preferred_element_type=jnp.float32)
    up_val = jnp.dot(arrived, up_in, preferred_element_type=jnp.float32)
    hidden = (jax.nn.silu(gate_val) * up_val).astype(jnp.bfloat16)
    produced = jnp.dot(hidden, down_in, preferred_element_type=jnp.float32).astype(jnp.bfloat16)
    returned = lax.all_to_all(produced[None], ("gx", "gy"), split_axis=1, concat_axis=0, tiled=True)
    summed = (
        returned.reshape(experts, 2, capacity, width_all)
        .astype(jnp.float32)
        .sum(axis=1)
        .reshape(experts * capacity, width_all)
    )
    route_out = summed[target]
    gates_flat = gate_share.reshape(route_count)
    moe_out = jnp.sum((gates_flat[:, None] * route_out).reshape(tok_rows, TOP, width_all), axis=1)
    grad_out = cotangent.astype(jnp.float32)
    grad_gates = jnp.sum(
        route_out.reshape(tok_rows, TOP, width_all) * grad_out[:, None, :], axis=-1
    )
    slot_gate = jnp.zeros((experts * capacity,), jnp.float32).at[target].set(gates_flat)
    padded_grad = jnp.concatenate([grad_out, jnp.zeros((1, width_all), jnp.float32)], axis=0)
    grad_packed = (
        (slot_gate[:, None] * padded_grad[source])
        .astype(jnp.bfloat16)
        .reshape(experts, 1, capacity, width_all)
    )
    grad_outgoing = jnp.broadcast_to(grad_packed, (experts, 2, capacity, width_all)).reshape(
        2 * experts, capacity, width_all
    )
    grad_arrived = lax.all_to_all(
        grad_outgoing, ("gx", "gy"), split_axis=0, concat_axis=1, tiled=True
    )[0]
    rows_in, grad_use = (arrived, grad_arrived)
    gate_use, up_use, hidden_use = (gate_val, up_val, hidden)
    sigmoid_gate = jax.nn.sigmoid(gate_use)
    silu_gate = gate_use * sigmoid_gate
    grad_hidden = contract_cols(grad_use, down_in)
    down_part = contract_rows(hidden_use, grad_use)
    grad_gate = (
        grad_hidden * up_use * sigmoid_gate * (1.0 + gate_use * (1.0 - sigmoid_gate))
    ).astype(jnp.bfloat16)
    grad_up = (grad_hidden * silu_gate).astype(jnp.bfloat16)
    gate_part = contract_rows(rows_in, grad_gate)
    up_part = contract_rows(rows_in, grad_up)
    grad_in = contract_cols(grad_gate, gate_in) + contract_cols(grad_up, up_in)
    grad_back = lax.all_to_all(
        grad_in.astype(jnp.bfloat16)[None], ("gx", "gy"), split_axis=1, concat_axis=0, tiled=True
    )
    grad_summed = (
        grad_back.reshape(experts, 2, capacity, width_all)
        .astype(jnp.float32)
        .sum(axis=1)
        .reshape(experts * capacity, width_all)
    )
    grad_moe_in = jnp.sum(grad_summed[target].reshape(tok_rows, TOP, width_all), axis=1)
    return moe_out, grad_gates, grad_moe_in, gate_part, up_part, down_part


def dense_experts(
    moe_in, all_cot, expert_ids, gate_share, gate_weight, up_weight, down_weight
):
    everyone = ("gx", "gy")
    devices = lax.axis_size("gx") * lax.axis_size("gy")
    experts = devices // 2
    matches = expert_ids[:, :, None] == jnp.arange(experts, dtype=jnp.int32)[None, None, :]
    dense_gates = jnp.sum(jnp.where(matches, gate_share[:, :, None], 0.0), axis=1)
    own_gate = lax.all_to_all(
        jnp.repeat(dense_gates.T, 2, axis=0), everyone, split_axis=0, concat_axis=0, tiled=True
    ).reshape(-1)
    shares = jnp.broadcast_to(own_gate[:, None], (own_gate.shape[0], 128))
    all_moe, pair, gate_dots, down_part, moe_out = run_experts(
        moe_in, all_cot, shares, gate_weight[0], up_weight[0], down_weight[0], 8
    )
    moe_out = moe_out.reshape(moe_in.shape)
    dots_back = lax.all_to_all(
        jnp.sum(gate_dots, axis=-1).reshape(devices, -1),
        everyone,
        split_axis=0,
        concat_axis=0,
        tiled=True,
    )
    dots_experts = dots_back.reshape(experts, 2, -1).sum(axis=1).T
    grad_gates = jnp.sum(jnp.where(matches, dots_experts[:, None, :], 0.0), axis=-1)
    grad_moe_in, gate_part, up_part = pull_experts(all_moe, pair, gate_weight[0], up_weight[0], 9)
    return moe_out, grad_gates, grad_moe_in, gate_part, up_part, down_part


def plain_attention(
    seq_acts, full_in, out_weight, query_gain, key_gain, doc_ids
):
    out_rows = lax.all_gather(out_weight, "gx", axis=1, tiled=True)
    local_width = full_in.shape[1] // 3
    length = seq_acts.shape[0]
    local_heads = local_width // HD
    projected = jnp.dot(seq_acts, full_in, preferred_element_type=jnp.float32)
    queries = projected[:, :local_width]
    key_raw = projected[:, local_width : 2 * local_width]
    value_ready = (
        projected[:, 2 * local_width :].astype(jnp.bfloat16).reshape(length, local_heads, HD)
    )
    query_float, query_pull = jax.vjp(
        prepare_heads, queries.reshape(length, local_heads, HD), query_gain
    )
    key_float, key_pull = jax.vjp(prepare_heads, key_raw.reshape(length, local_heads, HD), key_gain)
    query_ready = query_float.astype(jnp.bfloat16)
    key_ready = key_float.astype(jnp.bfloat16)
    block_rows = min(512, length)
    block_count = length // block_rows
    score_scale = HD ** (-0.5)
    query_blocks = query_ready.reshape(block_count, block_rows, local_heads, HD)
    doc_blocks = doc_ids.reshape(block_count, block_rows)

    def block_scores(query_block, doc_block):
        scores = (
            jnp.einsum("qhd,khd->hqk", query_block, key_ready, preferred_element_type=jnp.float32)
            * score_scale
        )
        same_doc = doc_block[:, None] == doc_ids[None, :]
        return jnp.where(same_doc[None], scores, NEGATIVE)

    def forward_block(pieces):
        scores = block_scores(pieces[0], pieces[1])
        highest = jnp.max(scores, axis=-1, keepdims=True)
        weights = jnp.exp(scores - highest)
        totals = jnp.sum(weights, axis=-1, keepdims=True)
        shares = (weights / totals).astype(jnp.bfloat16)
        mixed_heads = jnp.einsum(
            "hqk,khd->qhd", shares, value_ready, preferred_element_type=jnp.float32
        )
        return (
            mixed_heads.astype(jnp.bfloat16),
            highest[..., 0] + jnp.log(totals[..., 0]),
            jnp.max(highest[..., 0], axis=-1),
        )

    mixed_blocks, log_totals, peak_blocks = lax.map(forward_block, (query_blocks, doc_blocks))
    mixed_seq = mixed_blocks.reshape(length, local_width)
    attended = lax.psum_scatter(
        jnp.dot(mixed_seq, out_rows, preferred_element_type=jnp.float32),
        "gy",
        scatter_dimension=0,
        tiled=True,
    )

    def back(grad_resid):
        seq_grad = lax.all_gather(grad_resid.astype(jnp.bfloat16), "gy", axis=0, tiled=True)
        grad_mixed = contract_cols(seq_grad, out_rows).astype(jnp.bfloat16)
        out_part = contract_rows(seq_grad, mixed_seq)

        def backward_block(running, pieces):
            grad_key, grad_value = running
            query_block, grad_block, log_block, doc_block = pieces
            scores = block_scores(query_block, doc_block)
            weights = jnp.exp(scores - log_block[..., None])
            grad_value = grad_value + jnp.einsum(
                "hqk,qhd->khd",
                weights.astype(jnp.bfloat16),
                grad_block,
                preferred_element_type=jnp.float32,
            )
            grad_weights = jnp.einsum(
                "qhd,khd->hqk", grad_block, value_ready, preferred_element_type=jnp.float32
            )
            inner_sum = jnp.sum(weights * grad_weights, axis=-1, keepdims=True)
            grad_scores = (weights * (grad_weights - inner_sum)).astype(jnp.bfloat16)
            grad_query = (
                jnp.einsum("hqk,khd->qhd", grad_scores, key_ready, preferred_element_type=jnp.float32)
                * score_scale
            )
            grad_key = (
                grad_key
                + jnp.einsum(
                    "hqk,qhd->khd", grad_scores, query_block, preferred_element_type=jnp.float32
                )
                * score_scale
            )
            return ((grad_key, grad_value), grad_query)

        empty_heads = jnp.zeros((length, local_heads, HD), jnp.float32)
        grad_mixed_blocks = grad_mixed.reshape(block_count, block_rows, local_heads, HD)
        (key_grad_heads, value_grad_heads), query_grad_blocks = lax.scan(
            backward_block,
            (empty_heads, empty_heads),
            (query_blocks, grad_mixed_blocks, log_totals, doc_blocks),
        )
        query_raw_grad, query_gain_part = query_pull(query_grad_blocks.reshape(length, local_heads, HD))
        key_raw_grad, key_gain_part = key_pull(key_grad_heads)
        grad_queries = query_raw_grad.reshape(length, local_width).astype(jnp.bfloat16)
        grad_keys = key_raw_grad.reshape(length, local_width).astype(jnp.bfloat16)
        grad_values = value_grad_heads.reshape(length, local_width).astype(jnp.bfloat16)
        grad_heads = jnp.concatenate([grad_queries, grad_keys, grad_values], axis=1)
        acts_part = contract_cols(grad_heads, full_in).astype(jnp.bfloat16)
        in_sum = lax.psum_scatter(
            contract_rows(seq_acts, grad_heads).astype(jnp.bfloat16),
            "gx",
            scatter_dimension=0,
            tiled=True,
        ).astype(jnp.float32)
        grad_acts = lax.psum_scatter(acts_part, "gy", scatter_dimension=0, tiled=True)
        out_sum = lax.psum_scatter(
            out_part.astype(jnp.bfloat16), "gx", scatter_dimension=0, tiled=True
        ).astype(jnp.float32)
        return grad_acts.astype(jnp.float32), in_sum, out_sum, query_gain_part, key_gain_part

    return attended, jnp.max(peak_blocks, axis=0), back


def kernel_attention(
    seq_acts, full_in, out_weight, query_gain, key_gain, doc_ids
):
    length = seq_acts.shape[0]
    halfway = HD // 2
    frequency = jnp.exp(
        jnp.arange(halfway, dtype=jnp.float32) * (-2.0 * jnp.log(10000.0) / HD)
    )
    angles = jnp.arange(length, dtype=jnp.float32)[:, None] * frequency[None, :]
    cosine, sine = jnp.cos(angles), jnp.sin(angles)
    tables = (
        jnp.concatenate([cosine, cosine], axis=1),
        jnp.concatenate([-sine, sine], axis=1),
    )
    docs = (
        jnp.broadcast_to(doc_ids[:, None], (length, HD)),
        jnp.broadcast_to(doc_ids[None, :], (8, length)),
    )
    part, *saved, peaks, out_rows = attend(
        seq_acts, full_in, out_weight, query_gain, key_gain, tables, docs, 10
    )
    saved.append(out_rows)
    attended = scatter_plane(part, 3)
    heads = full_in.shape[1] // (3 * HD)

    def back(grad_resid):
        seq_grad = all_gather(grad_resid.astype(jnp.bfloat16), False, 1)
        part, weight_part, out_sum, gains = attend_back(
            seq_grad, saved, query_gain, key_gain, tables, docs, seq_acts, full_in, 11
        )
        grad_acts, in_sum = leave(part, weight_part, 7)
        return grad_acts, in_sum, out_sum, gains[0], gains[1]

    return attended, peaks[:heads, 0], back


def local(
    tokens,
    cotangent,
    expert_ids,
    doc_ids,
    clip_rank,
    attn_gain,
    moe_gain,
    query_gain,
    key_gain,
    query_weight,
    key_weight,
    value_weight,
    out_weight,
    router_weight,
    gate_weight,
    up_weight,
    down_weight,
):
    inputs = tokens.astype(jnp.float32)
    acts_float, norm_pull = jax.vjp(norm_rows, inputs, attn_gain)
    acts_low = acts_float.astype(jnp.bfloat16)
    in_weights = jnp.concatenate([query_weight, key_weight, value_weight], axis=1)
    by_kernels = lax.axis_size("gy") == 8
    if by_kernels:
        seq_acts, full_in, all_cot = enter(acts_low, in_weights, cotangent, 6)
    else:
        seq_acts = lax.all_gather(acts_low, "gy", axis=0, tiled=True)
        full_in = lax.all_gather(in_weights, "gx", axis=0, tiled=True)
    local_width = query_weight.shape[1]
    local_heads = local_width // HD
    attention = kernel_attention if by_kernels else plain_attention
    attended, own_peaks, attention_back = attention(
        seq_acts, full_in, out_weight, query_gain, key_gain, doc_ids
    )
    start_head = lax.axis_index("gy") * local_heads
    peak_slots = lax.dynamic_update_slice(
        jnp.zeros((lax.axis_size("gx"), NH), jnp.float32),
        own_peaks[None],
        (lax.axis_index("gx"), start_head),
    )
    residual = inputs + attended
    moe_float, moe_pull = jax.vjp(norm_rows, residual, moe_gain)
    moe_in = moe_float.astype(jnp.bfloat16)
    logits = jnp.dot(moe_in, router_weight, preferred_element_type=jnp.float32)
    gate_share, gate_pull = jax.vjp(partial(route_gates, expert_ids), logits)
    if by_kernels and router_weight.shape[1] <= 2 * TOP:
        moe_out, grad_gates, grad_moe_in, gate_part, up_part, down_part = dense_experts(
            moe_in, all_cot, expert_ids, gate_share, gate_weight, up_weight, down_weight
        )
    else:
        moe_out, grad_gates, grad_moe_in, gate_part, up_part, down_part = routed_experts(
            moe_in,
            cotangent,
            expert_ids,
            gate_share,
            router_weight,
            gate_weight,
            up_weight,
            down_weight,
        )
    output = (residual + moe_out).astype(jnp.bfloat16)
    grad_out = cotangent.astype(jnp.float32)
    (grad_logits,) = gate_pull(grad_gates)
    grad_logits_low = grad_logits.astype(jnp.bfloat16)
    router_part = contract_rows(moe_in, grad_logits_low)
    grad_moe_in = grad_moe_in + contract_cols(grad_logits_low, router_weight)
    grad_resid_norm, moe_gain_part = moe_pull(grad_moe_in)
    grad_resid = grad_out + grad_resid_norm
    grad_acts, in_sum, out_sum, query_gain_part, key_gain_part = attention_back(grad_resid)
    query_sum = in_sum[:, :local_width]
    key_sum = in_sum[:, local_width : 2 * local_width]
    value_sum = in_sum[:, 2 * local_width :]
    norm_input_grad, attn_gain_part = norm_pull(grad_acts)
    input_grad = grad_resid + norm_input_grad
    small = (
        attn_gain_part,
        moe_gain_part,
        query_gain_part,
        key_gain_part,
        router_part.T,
        peak_slots,
    )
    summed = sum_everywhere(jnp.concatenate([part.reshape(-1) for part in small]), 5)
    ends = list(accumulate(part.size for part in small))
    attn_gain_grad, moe_gain_grad, query_gain_grad, key_gain_grad, router_flat, peaks = (
        summed[end - part.size : end].reshape(part.shape) for end, part in zip(ends, small)
    )
    router_grad = router_flat.T
    peak_global = jnp.max(peaks, axis=0)
    ranked = -jnp.sort(-peak_global)
    limit = jnp.sum(jnp.where(jnp.arange(NH, dtype=jnp.int32) == clip_rank[0], ranked, 0.0))
    factors = jnp.where(peak_global > limit, limit / peak_global, 1.0)
    own_factors = lax.dynamic_slice_in_dim(factors, start_head, local_heads)
    columns = jnp.repeat(jnp.sqrt(own_factors), HD)
    query_clipped = (query_weight.astype(jnp.float32) * columns[None, :]).astype(jnp.bfloat16)
    key_clipped = (key_weight.astype(jnp.float32) * columns[None, :]).astype(jnp.bfloat16)
    return (
        output,
        input_grad,
        attn_gain_grad,
        moe_gain_grad,
        query_gain_grad,
        key_gain_grad,
        query_sum,
        key_sum,
        value_sum,
        out_sum.T,
        router_grad,
        gate_part[None],
        up_part[None],
        down_part[None],
        query_clipped,
        key_clipped,
        factors,
    )


def solution(mesh):
    placed = (
        P(("gx", "gy"), None),
        P(("gx", "gy"), None),
        P(("gx", "gy"), None),
        P("gx"),
        P(),
        P(),
        P(),
        P(),
        P(),
        P("gx", "gy"),
        P("gx", "gy"),
        P("gx", "gy"),
        P("gy", "gx"),
        P(),
        P(("gx", "gy"), None, None),
        P(("gx", "gy"), None, None),
        P(("gx", "gy"), None, None),
    )
    return jax.shard_map(
        local,
        mesh=mesh,
        in_specs=placed,
        out_specs=(
            P(("gx", "gy"), None),
            P(("gx", "gy"), None),
            P(),
            P(),
            P(),
            P(),
            P("gx", "gy"),
            P("gx", "gy"),
            P("gx", "gy"),
            P("gy", "gx"),
            P(),
            P(("gx", "gy"), None, None),
            P(("gx", "gy"), None, None),
            P(("gx", "gy"), None, None),
            P("gx", "gy"),
            P("gx", "gy"),
            P(),
        ),
        check_vma=False,
    )
```

```python
from functools import partial
from itertools import accumulate

import jax
import jax.numpy as jnp
from jax import lax
from jax.experimental import pallas as pl
from jax.experimental.pallas import tpu as pltpu
from jax.sharding import PartitionSpec as P

NH = 16
HD = 128
TOP = 8


EPSILON = 1e-06
NEGATIVE = -1e30


def flip(index):
    return index + 1 - 2 * (index % 2)


def barrier_with(partners):
    barrier = pltpu.get_barrier_semaphore()
    for ok, device in partners:
        @pl.when(ok)
        def _():
            pl.semaphore_signal(barrier, inc=1, device_id=device, device_id_type=pl.DeviceIdType.MESH)
    pl.semaphore_wait(barrier, sum(ok.astype(jnp.int32) for ok, _ in partners))

def always(ok, other):
    if ok is True:
        return other
    return ok if other is True else jnp.logical_and(ok, other)


def run_if(ok, action):
    if ok is True:
        action()
    else:
        pl.when(ok)(action)


def chain_gather(n_z, own_ref, out_ref, send_sem, recv_sem, local_sem):
    z = lax.axis_index("gx")
    g = lax.axis_index("gy")

    def hop(source, owner, k, peer):
        return pltpu.make_async_remote_copy(
            src_ref=source,
            dst_ref=out_ref.at[owner],
            send_sem=send_sem.at[k],
            recv_sem=recv_sem.at[owner],
            device_id={"gx": peer, "gy": g},
            device_id_type=pl.DeviceIdType.MESH,
        )

    local = pltpu.make_async_copy(own_ref, out_ref.at[z], local_sem)
    upward = [(z < n_z - 1, lambda: hop(own_ref, z, 0, z + 1))]
    downward = [(z > 0, lambda: hop(own_ref, z, n_z, z - 1))]
    for d in range(1, n_z - 1):
        upward.append(
            (
                jnp.logical_and(z >= d, z < n_z - 1),
                lambda d=d: hop(out_ref.at[z - d], z - d, d, z + 1),
            )
        )
        downward.append(
            (
                jnp.logical_and(z < n_z - d, z > 0),
                lambda d=d: hop(out_ref.at[z + d], z + d, n_z + d, z - 1),
            )
        )

    def start():
        local.start()
        for ok, copy in (upward[0], downward[0]):
            run_if(ok, lambda copy=copy: copy().start())

    def relay(d):
        run_if(z >= d, lambda: hop(own_ref, z - d, 0, z).wait_recv())
        if d < n_z - 1:
            run_if(upward[d][0], lambda: upward[d][1]().start())
        run_if(z < n_z - d, lambda: hop(own_ref, z + d, 0, z).wait_recv())
        if d < n_z - 1:
            run_if(downward[d][0], lambda: downward[d][1]().start())

    def finish():
        local.wait()
        for ok, copy in upward + downward:
            run_if(ok, lambda copy=copy: copy().wait_send())

    return start, [partial(relay, d) for d in range(1, n_z)], finish


def gather_steps(n_z, span, own_ref, out_ref, send_sem, recv_sem, local_sem):
    z = lax.axis_index("gx")
    g = lax.axis_index("gy")
    flip_x = g + 2 - 4 * ((g // 2) % 2)
    flip_y = g + 4 - 8 * ((g // 4) % 2)
    flip_both = flip_x + flip_y - g
    core = {"gx": z, "gy": flip(g)}
    x_peer = {"gx": z, "gy": flip_x}
    y_peer = {"gx": z, "gy": flip_y}
    above = {"gx": z + 1, "gy": g}
    below = {"gx": z - 1, "gy": g}
    first_z = z if n_z > 1 else 0
    sends = []

    def send(ok, source, b, h, peer):
        k = len(sends)

        def make():
            return pltpu.make_async_remote_copy(
                src_ref=source,
                dst_ref=out_ref.at[b, h],
                send_sem=send_sem.at[k],
                recv_sem=recv_sem.at[b, h],
                device_id=peer,
                device_id_type=pl.DeviceIdType.MESH,
            )

        sends.append((ok, make))
        run_if(ok, lambda: make().start())

    def arrive(ok, b, h):
        def wait():
            pltpu.make_async_remote_copy(
                src_ref=out_ref.at[b, h],
                dst_ref=out_ref.at[b, h],
                send_sem=send_sem.at[0],
                recv_sem=recv_sem.at[b, h],
                device_id=core,
                device_id_type=pl.DeviceIdType.MESH,
            ).wait_recv()

        run_if(ok, wait)

    local = pltpu.make_async_copy(own_ref, out_ref.at[first_z * span + g], local_sem)
    items = [(True, first_z, 0)]
    for d in range(1, n_z):
        items += [(z >= d, z - d, -d), (z < n_z - d, z + d, d)]

    upward = [always(item[0], z < n_z - 1) for item in items]
    downward = [always(item[0], z > 0) for item in items]

    def first(i):
        ok, owner, d = items[i]
        b = owner * span + g
        if d == 0:
            local.start()
            source = own_ref
        else:
            arrive(ok, b, 0)
            arrive(ok, b, 1)
            source = out_ref.at[b]
        for h in range(2):
            if n_z > 1 and d <= 0:
                send(upward[i], source.at[h], b, h, above)
            if n_z > 1 and d >= 0:
                send(downward[i], source.at[h], b, h, below)
        send(ok, source.at[0], b, 0, x_peer)
        send(ok, source.at[1], b, 1, y_peer)
        send(ok, source.at[1], b, 1, x_peer)
        send(ok, source.at[0], b, 0, y_peer)
        send(ok, source.at[0], b, 0, core)
        send(ok, source.at[1], b, 1, core)

    def second(item):
        ok, owner, _ = item
        for side, h, peer in ((flip_x, 0, y_peer), (flip_y, 1, x_peer)):
            b = owner * span + side
            arrive(ok, b, h)
            send(ok, out_ref.at[b, h], b, h, peer)
            send(ok, out_ref.at[b, h], b, h, core)

    def third(item):
        ok, owner, _ = item
        for side, h in ((flip_both, 0), (flip_both, 1), (flip_y, 0), (flip_x, 1)):
            b = owner * span + side
            arrive(ok, b, h)
            send(ok, out_ref.at[b, h], b, h, core)

    n = len(items)

    def step(i):
        if i < n:
            first(i)
        if 1 <= i <= n:
            second(items[i - 1])
        if i >= 2:
            third(items[i - 2])

    def finish():
        for ok, owner, _ in items:
            for side in (g, flip_x, flip_y, flip_both):
                for h in range(2):
                    arrive(ok, owner * span + flip(side), h)
        local.wait()
        for ok, make in sends:
            run_if(ok, lambda make=make: make().wait_send())

    return [partial(step, i) for i in range(n + 2)], finish


def greet(n_z):
    z = lax.axis_index("gx")
    g = lax.axis_index("gy")
    peers = [
        (z >= 0, {"gx": z, "gy": g + bit - 2 * bit * ((g // bit) % 2)}) for bit in (1, 2, 4)
    ]
    if n_z > 1:
        peers += [(z < n_z - 1, {"gx": z + 1, "gy": g}), (z > 0, {"gx": z - 1, "gy": g})]
    barrier_with(peers)


def gather_kernel(n_z, span, own_ref, out_ref, send_sem, recv_sem, local_sem):
    greet(n_z)
    steps, finish = gather_steps(n_z, span, own_ref, out_ref, send_sem, recv_sem, local_sem)
    for step in steps:
        step()
    finish()


def all_gather(block, both, collective_id):
    n_z = lax.axis_size("gx") if both else 1
    span = lax.axis_size("gy")
    rows, cols = block.shape
    own = block.reshape(2, rows // 2, cols)
    n_sends = (2 * n_z - 1) * 24
    out = pl.pallas_call(
        partial(gather_kernel, n_z, span),
        out_shape=jax.ShapeDtypeStruct((n_z * span, 2, rows // 2, cols), block.dtype),
        in_specs=[pl.BlockSpec(memory_space=pltpu.VMEM)],
        out_specs=pl.BlockSpec(memory_space=pl.ANY),
        scratch_shapes=[pltpu.SemaphoreType.DMA((n_sends,)), pltpu.SemaphoreType.DMA((n_z * span, 2)), pltpu.SemaphoreType.DMA],
        compiler_params=pltpu.CompilerParams(collective_id=collective_id, has_side_effects=True),
        name="gather_all" if both else "gather_plane",
    )(own)
    return out.reshape(n_z * span * rows, cols)


def add_into(dst, parts, rows):
    step = min(rows, 32)

    @pl.loop(0, rows // step)
    def _(r):
        at = pl.ds(pl.multiple_of(r * step, step), step)
        if len(parts) == 2 and dst.dtype == jnp.bfloat16:
            dst[at, :] = parts[0][at, :] + parts[1][at, :]
        else:
            total = parts[0][at, :].astype(jnp.float32)
            for term in parts[1:]:
                total = total + term[at, :].astype(jnp.float32)
            dst[at, :] = total.astype(dst.dtype)


def scatter_kernel(chain, n_i, rows, part_ref, out_ref, held, from_core, from_a, from_b, from_z,
                   load_sem, core_send, a_send, b_send, z_send, core_recv, a_recv, b_recv, z_recv, beside=None, parts=None):
    z = lax.axis_index("gx"); g = lax.axis_index("gy")
    flip_x = g + 2 - 4 * ((g // 2) % 2)
    flip_y = g + 4 - 8 * ((g // 4) % 2)
    quads = (flip_x + flip_y - g, flip_x, flip_y, g)
    core = {"gx": z, "gy": flip(g)}
    xn = {"gx": z, "gy": flip_x}
    yn = {"gx": z, "gy": flip_y}
    every = z >= 0
    partners = [(every, core), (every, xn), (every, yn)]
    if chain:
        partners += [(every, {"gx": lax.rem(z + j, n_i), "gy": g}) for j in range(1, n_i)]
    if beside:
        n_z = lax.axis_size("gx")
        partners += [(z < n_z - 1, {"gx": z + 1, "gy": g}), (z > 0, {"gx": z - 1, "gy": g})]
    if parts is None:
        barrier_with(partners)
    if beside:
        beside[0]()
    mesh_id = pl.DeviceIdType.MESH

    def item(i):
        return lax.rem(z + n_i - 1 - i + n_i, n_i) if chain else i

    def block(it, gg):
        return part_ref.at[it, gg]

    def remote(src, dst, ssem, rsem, dev):
        return pltpu.make_async_remote_copy(src_ref=src, dst_ref=dst, send_sem=ssem, recv_sem=rsem, device_id=dev, device_id_type=mesh_id)

    def core_copy(i, q):
        it = item(i)
        return remote(block(it, flip(quads[q])), from_core.at[it, q], core_send.at[i, q], core_recv.at[it, q], core)

    def load(i, q):
        it = item(i)
        return pltpu.make_async_copy(block(it, quads[q]), held.at[it, q], load_sem.at[i, q])

    a_plan = ((0, 0, 0, xn), (0, 1, 0, yn), (1, 0, 1, xn), (2, 1, 1, yn))
    def a_copy(i, k):
        it = item(i)
        q, h, slot, dev = a_plan[k]
        return remote(held.at[it, q, h], from_a.at[it, h, slot], a_send.at[i, k], a_recv.at[it, h, slot], dev)

    b_plan = ((2, 0, yn), (1, 1, xn))
    def b_copy(i, h):
        it = item(i)
        q, _, dev = b_plan[h]
        return remote(held.at[it, q, h], from_b.at[it, h], b_send.at[i, h], b_recv.at[it, h], dev)

    def z_copy(i):
        it = item(i)
        return remote(held.at[it, 3], from_z.at[z], z_send.at[i], z_recv.at[z], {"gx": it, "gy": g})

    def z_arrival(i):
        it = item(i)
        return remote(held.at[it, 3], from_z.at[it], z_send.at[i], z_recv.at[it], core)

    def begin():
        for i in range(n_i):
            for q in range(4):
                core_copy(i, q).start()
                load(i, q).start()

    def stage_a(i):
        it = item(i)
        for q in range(4):
            load(i, q).wait()
            core_copy(i, q).wait_recv()
            for h in range(2):
                add_into(held.at[it, q, h], (held.at[it, q, h], from_core.at[it, q, h]), rows)
            for k in range(4):
                if a_plan[k][0] == q:
                    a_copy(i, k).start()

    def stage_b(i):
        it = item(i)
        for q, h, slot in ((2, 0, 0), (1, 1, 0), (3, 0, 1), (3, 1, 1)):
            remote(held.at[it, q, h], from_a.at[it, h, slot], a_send.at[i, 0], a_recv.at[it, h, slot], core).wait_recv()
            add_into(held.at[it, q, h], (held.at[it, q, h], from_a.at[it, h, slot]), rows)
            if slot == 0:
                b_copy(i, h).start()

    def stage_c(i):
        it = item(i)
        for h in range(2):
            b_copy(i, h).wait_recv()
            if chain:
                add_into(held.at[it, 3, h], (held.at[it, 3, h], from_b.at[it, h]), rows)
            else:
                add_into(out_ref.at[it, h], (held.at[it, 3, h], from_b.at[it, h]), rows)

    def stage_d(i):
        if i < n_i - 1:
            z_copy(i).start()
        else:
            for j in range(n_i - 1):
                z_arrival(j).wait_recv()
            for h in range(2):
                add_into(
                    out_ref.at[h],
                    [held.at[item(i), 3, h]] + [from_z.at[item(j), h] for j in range(n_i - 1)],
                    rows,
                )

    def step(i):
        if i < n_i:
            stage_a(i)
        if 0 <= i - 1 < n_i:
            stage_b(i - 1)
        if 0 <= i - 2 < n_i:
            stage_c(i - 2)
        if chain and 0 <= i - 2 < n_i:
            stage_d(i - 2)

    def finish():
        for i in range(n_i):
            for q in range(4):
                core_copy(i, q).wait_send()
            for k in range(4):
                a_copy(i, k).wait_send()
            for h in range(2):
                b_copy(i, h).wait_send()
            if chain and i < n_i - 1:
                z_copy(i).wait_send()

    if parts is not None:
        parts.extend([begin] + [partial(step, i) for i in range(n_i + 2)] + [finish])
        return
    begin()
    for i in range(n_i + 2):
        step(i)
        if beside and i == n_i:
            beside[1][0]()
    if beside:
        for relay in beside[1][1:]:
            relay()
        beside[2]()
    finish()


def sum_kernel(n_z, bits, vec_ref, out_ref, held, arrived, from_z, send_sem, z_send, recv_sem, z_recv):
    z = lax.axis_index("gx")
    g = lax.axis_index("gy")
    half = vec_ref.shape[1]
    side = lax.rem(g, 2)
    core = {"gx": z, "gy": g + 1 - 2 * (g % 2)}
    peers = [
        {"gx": z, "gy": g + bit - 2 * bit * ((g // bit) % 2)}
        for bit in (2**power for power in range(1, bits))
    ]
    others = [{"gx": lax.rem(z + j, n_z), "gy": g} for j in range(1, n_z)]
    barrier_with([(z >= 0, peer) for peer in (core, *peers, *others)])

    def remote(src, dst, ssem, rsem, peer):
        return pltpu.make_async_remote_copy(
            src_ref=src,
            dst_ref=dst,
            send_sem=ssem,
            recv_sem=rsem,
            device_id=peer,
            device_id_type=pl.DeviceIdType.MESH,
        )

    first = remote(vec_ref.at[1 - side], arrived.at[0], send_sem.at[0], recv_sem.at[0], core)
    first.start()
    first.wait()
    held[0] = vec_ref[side] + arrived[0]
    for k, peer in enumerate(peers, 1):
        step = remote(held.at[k - 1], arrived.at[k], send_sem.at[k], recv_sem.at[k], peer)
        step.start()
        step.wait()
        held[k] = held[k - 1] + arrived[k]
    copies = [
        remote(held.at[bits - 1], from_z.at[j], z_send.at[j], z_recv.at[j], peer)
        for j, peer in enumerate(others)
    ]
    for copy in copies:
        copy.start()
    for copy in copies:
        copy.wait()
    total = jnp.zeros_like(held[0])
    for owner in range(n_z):
        term = held[bits - 1]
        for j in range(1, n_z):
            term = jnp.where(lax.rem(z - j + n_z, n_z) == owner, from_z[j - 1], term)
        total = total + term
    held[bits] = total
    last = remote(held.at[bits], arrived.at[bits], send_sem.at[bits], recv_sem.at[bits], core)
    last.start()
    out_ref[side] = total
    last.wait()
    out_ref[1 - side] = arrived[bits]


def sum_everywhere(vector, collective_id):
    n_z = lax.axis_size("gx")
    bits = lax.axis_size("gy").bit_length() - 1
    lanes = 128
    length = vector.shape[0]
    rows = -(-length // (lanes * 16)) * 8
    padded = jnp.pad(vector, (0, 2 * rows * lanes - length)).reshape(2, rows, lanes)
    dma = pltpu.SemaphoreType.DMA
    out = pl.pallas_call(
        partial(sum_kernel, n_z, bits),
        out_shape=jax.ShapeDtypeStruct((2, rows, lanes), jnp.float32),
        in_specs=[pl.BlockSpec(memory_space=pltpu.VMEM)],
        out_specs=pl.BlockSpec(memory_space=pltpu.VMEM),
        scratch_shapes=[
            pltpu.VMEM((bits + 1, rows, lanes), jnp.float32),
            pltpu.VMEM((bits + 1, rows, lanes), jnp.float32),
            pltpu.VMEM((n_z - 1, rows, lanes), jnp.float32),
            dma((bits + 1,)),
            dma((n_z - 1,)),
            dma((bits + 1,)),
            dma((n_z - 1,)),
        ],
        compiler_params=pltpu.CompilerParams(collective_id=collective_id, has_side_effects=True),
        name="sum_everywhere",
    )(padded)
    return out.reshape(-1)[:length]


def chain_scatter(n_z, part_ref, out_ref, from_low, from_high, send_sem, low_recv, high_recv):
    z = lax.axis_index("gx")
    g = lax.axis_index("gy")
    rows = part_ref.shape[1]

    def up(dest):
        return pltpu.make_async_remote_copy(
            src_ref=part_ref.at[dest],
            dst_ref=from_low.at[dest],
            send_sem=send_sem.at[dest],
            recv_sem=low_recv.at[dest],
            device_id={"gx": z + 1, "gy": g},
            device_id_type=pl.DeviceIdType.MESH,
        )

    def down(dest):
        return pltpu.make_async_remote_copy(
            src_ref=part_ref.at[dest],
            dst_ref=from_high.at[dest],
            send_sem=send_sem.at[dest],
            recv_sem=high_recv.at[dest],
            device_id={"gx": z - 1, "gy": g},
            device_id_type=pl.DeviceIdType.MESH,
        )

    def start():
        for k in range(n_z - 1):
            run_if(z == 0, lambda k=k: up(n_z - 1 - k).start())
            run_if(z == n_z - 1, lambda k=k: down(k).start())

    def pass_up(dest):
        up(dest).wait_recv()
        add_into(part_ref.at[dest], (part_ref.at[dest], from_low.at[dest]), rows)
        up(dest).start()

    def pass_down(dest):
        down(dest).wait_recv()
        add_into(part_ref.at[dest], (part_ref.at[dest], from_high.at[dest]), rows)
        down(dest).start()

    def relay(time):
        for k in range(time):
            low, dest = time - k, n_z - 1 - k
            if 0 < low < dest:
                run_if(z == low, partial(pass_up, dest))
            high, dest = n_z - 1 - (time - k), k
            if dest < high < n_z - 1:
                run_if(z == high, partial(pass_down, dest))

    def finish():
        for dest in range(n_z):
            terms = [part_ref.at[dest]]
            terms += [from_low.at[dest]] if dest > 0 else []
            terms += [from_high.at[dest]] if dest < n_z - 1 else []

            def last(dest=dest, terms=terms):
                if dest > 0:
                    up(dest).wait_recv()
                if dest < n_z - 1:
                    down(dest).wait_recv()
                add_into(out_ref, terms, rows)

            run_if(z == dest, last)
        for dest in range(n_z):
            run_if(z != dest, lambda dest=dest: up(dest).wait_send())

    return start, [partial(relay, time) for time in range(1, n_z)], finish


def leave_kernel(
    n_i,
    rows,
    part_ref,
    weight_ref,
    out_ref,
    weight_out,
    held,
    from_core,
    from_a,
    from_b,
    from_z,
    sums,
    from_low,
    from_high,
    load_sem,
    core_send,
    a_send,
    b_send,
    z_send,
    core_recv,
    a_recv,
    b_recv,
    z_recv,
    copy_sem,
    chain_send,
    low_recv,
    high_recv,
):
    n_z = lax.axis_size("gx")
    copy = pltpu.make_async_copy(weight_ref, sums, copy_sem)
    copy.start()
    chain = chain_scatter(
        n_z, sums, weight_out, from_low, from_high, chain_send, low_recv, high_recv
    )

    def start():
        copy.wait()
        chain[0]()

    scatter_kernel(
        False,
        n_i,
        rows,
        part_ref,
        out_ref,
        held,
        from_core,
        from_a,
        from_b,
        from_z,
        load_sem,
        core_send,
        a_send,
        b_send,
        z_send,
        core_recv,
        a_recv,
        b_recv,
        z_recv,
        (start, chain[1], chain[2]),
    )


def leave(part, weight_part, collective_id):
    n_z = lax.axis_size("gx")
    span = lax.axis_size("gy")
    pieces, _, _, rows, cols = part.shape
    total = span * pieces * 2 * rows
    half = (rows, cols)
    dma = pltpu.SemaphoreType.DMA
    block = (weight_part.shape[0] // n_z, weight_part.shape[1])
    out, sums = pl.pallas_call(
        partial(leave_kernel, pieces, rows),
        out_shape=(
            jax.ShapeDtypeStruct((pieces, 2, rows, cols), jnp.float32),
            jax.ShapeDtypeStruct(block, jnp.float32),
        ),
        in_specs=[pl.BlockSpec(memory_space=pl.ANY)] * 2,
        out_specs=(pl.BlockSpec(memory_space=pltpu.VMEM),) * 2,
        scratch_shapes=[
            pltpu.VMEM((pieces, 4, 2) + half, jnp.bfloat16),
            pltpu.VMEM((pieces, 4, 2) + half, jnp.bfloat16),
            pltpu.VMEM((pieces, 2, 2) + half, jnp.bfloat16),
            pltpu.VMEM((pieces, 2) + half, jnp.bfloat16),
            pltpu.VMEM((1, 2, 16, 128), jnp.bfloat16),
            pltpu.VMEM((n_z,) + block, jnp.bfloat16),
            pltpu.VMEM((n_z,) + block, jnp.bfloat16),
            pltpu.VMEM((n_z,) + block, jnp.bfloat16),
            dma((pieces, 4)),
            dma((pieces, 4)),
            dma((pieces, 4)),
            dma((pieces, 2)),
            dma((pieces,)),
            dma((pieces, 4)),
            dma((pieces, 2, 2)),
            dma((pieces, 2)),
            dma((pieces,)),
            dma,
            dma((n_z,)),
            dma((n_z,)),
            dma((n_z,)),
        ],
        compiler_params=pltpu.CompilerParams(
            collective_id=collective_id, has_side_effects=True, vmem_limit_bytes=60 << 20
        ),
        name="leave",
    )(part, weight_part.reshape((n_z,) + block))
    return out.reshape(total // span, cols), sums


def expert_kernel(n_z, span, own_ref, cot_ref, share_ref, gate_ref, up_ref, down_ref,
                  all_ref, pair_ref, dots_ref, down_out, out_ref,
                  moe_buf, cot_buf, share_buf, pair_stage, dots_buf,
                  gate_val, up_val, scaled, scaled_t, down_t,
                  held, from_core, from_a, from_b, from_z,
                  send_sem, recv_sem, local_sem, fetch_sem, store_sem,
                  core_send, a_send, b_send, z_send, core_recv, a_recv, b_recv, z_recv,
                  shares_in, dots_own, share_send, share_recv, dots_send, dots_recv):
    z = lax.axis_index("gx")
    g = lax.axis_index("gy")
    rows = own_ref.shape[1]
    block = 2 * rows
    step_rows = moe_buf.shape[1]
    steps = 2 * n_z
    flip_x = g + 2 - 4 * ((g // 2) % 2)
    flip_y = g + 4 - 8 * ((g // 4) % 2)
    flip_both = flip_x + flip_y - g
    core = {"gx": z, "gy": flip(g)}
    x_peer = {"gx": z, "gy": flip_x}
    y_peer = {"gx": z, "gy": flip_y}
    above = {"gx": z + 1, "gy": g}
    below = {"gx": z - 1, "gy": g}

    order = [z]
    candidates = []
    for d in range(1, n_z):
        candidates += [(z >= d, z - d), (z < n_z - d, z + d)]
    for k in range(1, n_z):
        rank, chosen = 0, 0
        for ok, owner in candidates:
            ok = ok.astype(jnp.int32)
            rank = rank + ok
            chosen = chosen + ok * (rank == k).astype(jnp.int32) * owner
        order.append(chosen)

    onward = [(z < n_z - 1, z > 0)]
    for owner in order[1:]:
        onward.append(
            (
                jnp.logical_and(owner < z, z < n_z - 1),
                jnp.logical_and(owner > z, z > 0),
            )
        )
    devices = n_z * span
    rank = z * span + g

    def device(number):
        return {"gx": lax.div(number, span), "gy": lax.rem(number, span)}

    barrier = pltpu.get_barrier_semaphore()

    @pl.loop(1, devices)
    def _(j):
        pl.semaphore_signal(
            barrier,
            inc=1,
            device_id=device(lax.rem(rank + j, devices)),
            device_id_type=pl.DeviceIdType.MESH,
        )

    pl.semaphore_wait(barrier, devices - 1)

    def share_copy(number):
        return pltpu.make_async_remote_copy(
            src_ref=share_ref.at[number],
            dst_ref=shares_in.at[rank],
            send_sem=share_send.at[number],
            recv_sem=share_recv.at[rank],
            device_id=device(number),
            device_id_type=pl.DeviceIdType.MESH,
        )

    def share_arrival(number):
        return pltpu.make_async_remote_copy(
            src_ref=share_ref.at[number],
            dst_ref=shares_in.at[number],
            send_sem=share_send.at[number],
            recv_sem=share_recv.at[number],
            device_id=core,
            device_id_type=pl.DeviceIdType.MESH,
        )

    def dots_copy(number):
        return pltpu.make_async_remote_copy(
            src_ref=dots_own.at[number],
            dst_ref=dots_ref.at[rank],
            send_sem=dots_send.at[number],
            recv_sem=dots_recv.at[rank],
            device_id=device(number),
            device_id_type=pl.DeviceIdType.MESH,
        )

    def dots_arrival(number):
        return pltpu.make_async_remote_copy(
            src_ref=dots_own.at[number],
            dst_ref=dots_ref.at[number],
            send_sem=dots_send.at[number],
            recv_sem=dots_recv.at[number],
            device_id=core,
            device_id_type=pl.DeviceIdType.MESH,
        )

    def for_others(action):
        @pl.loop(1, devices)
        def _(j):
            action(lax.rem(rank + j, devices))

    for_others(lambda number: share_copy(number).start())
    shares_in[rank] = share_ref[rank]

    def at(owner, gg, h):
        return pl.ds(pl.multiple_of((owner * span + gg) * block + h * rows, rows), rows)

    def copy(k, slot, owner, gg, h, peer, own=False):
        return pltpu.make_async_remote_copy(
            src_ref=own_ref.at[h] if own else all_ref.at[at(owner, gg, h)],
            dst_ref=all_ref.at[at(owner, gg, h)],
            send_sem=send_sem.at[k, slot],
            recv_sem=recv_sem.at[owner * span + gg, h],
            device_id=peer,
            device_id_type=pl.DeviceIdType.MESH,
        )

    sends = []

    def send(ok, *where, **options):
        k = where[0]
        slot = sum(1 for entry in sends if entry[2] == k)
        make = partial(copy, k, slot, *where[1:], **options)
        sends.append((ok, make, k))
        run_if(ok, lambda: make().start())

    def arrive(owner, gg, h):
        copy(0, 0, owner, gg, h, core).wait_recv()

    locals_ = [
        pltpu.make_async_copy(own_ref.at[h], all_ref.at[at(z, g, h)], local_sem.at[h])
        for h in range(2)
    ]

    def first(k):
        owner = order[k]
        own = k == 0
        if own:
            for item in locals_:
                item.start()
        else:
            arrive(owner, g, 0)
            arrive(owner, g, 1)
        go_up, go_down = onward[k]
        for h in range(2):
            send(go_up, k, owner, g, h, above, own=own)
            send(go_down, k, owner, g, h, below, own=own)
        send(True, k, owner, g, 0, x_peer, own=own)
        send(True, k, owner, g, 1, y_peer, own=own)
        send(True, k, owner, g, 1, x_peer, own=own)
        send(True, k, owner, g, 0, y_peer, own=own)
        send(True, k, owner, g, 0, core, own=own)
        send(True, k, owner, g, 1, core, own=own)

    def second(k):
        owner = order[k]
        arrive(owner, flip_x, 0)
        send(True, k, owner, flip_x, 0, y_peer)
        send(True, k, owner, flip_x, 0, core)
        arrive(owner, flip_y, 1)
        send(True, k, owner, flip_y, 1, x_peer)
        send(True, k, owner, flip_y, 1, core)

    def third(k):
        owner = order[k]
        for gg, h in ((flip_y, 0), (flip_x, 1), (flip_both, 0), (flip_both, 1)):
            arrive(owner, gg, h)
            send(True, k, owner, gg, h, core)

    def complete(k):
        for gg in (g, flip_x, flip_y, flip_both):
            for h in range(2):
                arrive(order[k], flip(gg), h)
        if k == 0:
            for item in locals_:
                item.wait()

    def owner_of(s):
        if isinstance(s, int):
            return order[s // 2]
        k = lax.div(s, 2)
        return sum((k == j).astype(jnp.int32) * order[j] for j in range(n_z))

    def place(s):
        k, side = (s // 2, s % 2) if isinstance(s, int) else (lax.div(s, 2), lax.rem(s, 2))
        if isinstance(s, int):
            owner = order[k]
        else:
            owner = sum((k == j).astype(jnp.int32) * order[j] for j in range(n_z))
        return pl.ds(pl.multiple_of(owner * (span * block) + side * step_rows, step_rows), step_rows)

    def parity(s):
        return s % 2 if isinstance(s, int) else lax.rem(s, 2)

    def fetches(s):
        slot = parity(s)
        return [
            pltpu.make_async_copy(source.at[place(s)], target.at[slot], fetch_sem.at[j, slot])
            for j, (source, target) in enumerate(
                ((all_ref, moe_buf), (cot_ref, cot_buf))
            )
        ]

    def stores(s):
        slot = parity(s)
        return [
            pltpu.make_async_copy(
                pair_stage.at[slot], pair_ref.at[place(s)], store_sem.at[0, slot]
            )
        ]

    f32 = jnp.float32
    dot = partial(lax.dot_general, preferred_element_type=f32)
    plain = (((1,), (0,)), ((), ()))
    last_dims = (((1,), (1,)), ((), ()))
    first_dims = (((0,), (0,)), ((), ()))
    half_width = scaled.shape[1]
    width = moe_buf.shape[2]
    tile = 256

    quads = (flip_both, flip_x, flip_y, g)

    def remote(src, dst, ssem, rsem, peer):
        return pltpu.make_async_remote_copy(
            src_ref=src,
            dst_ref=dst,
            send_sem=ssem,
            recv_sem=rsem,
            device_id=peer,
            device_id_type=pl.DeviceIdType.MESH,
        )

    def core_copy(k, q):
        return remote(
            held.at[k, flip(quads[q])],
            from_core.at[k, q],
            core_send.at[k, q],
            core_recv.at[k, q],
            core,
        )

    a_plan = ((0, 0, 0, x_peer), (0, 1, 0, y_peer), (1, 0, 1, x_peer), (2, 1, 1, y_peer))

    def a_copy(k, j):
        q, h, slot, peer = a_plan[j]
        return remote(
            held.at[k, quads[q], h],
            from_a.at[k, h, slot],
            a_send.at[k, j],
            a_recv.at[k, h, slot],
            peer,
        )

    b_plan = ((2, y_peer), (1, x_peer))

    def b_copy(k, h):
        q, peer = b_plan[h]
        return remote(
            held.at[k, quads[q], h], from_b.at[k, h], b_send.at[k, h], b_recv.at[k, h], peer
        )

    def z_copy(k):
        return remote(
            held.at[k, g], from_z.at[z], z_send.at[k], z_recv.at[z], {"gx": order[k], "gy": g}
        )

    def stage_core(k):
        for q in range(4):
            core_copy(k, q).start()

    def stage_a(k):
        for q in range(4):
            core_copy(k, q).wait_recv()
            for h in range(2):
                mine = held.at[k, quads[q], h]
                add_into(mine, (mine, from_core.at[k, q, h]), rows)
            for j in range(4):
                if a_plan[j][0] == q:
                    a_copy(k, j).start()

    def stage_b(k):
        for q, h, slot in ((2, 0, 0), (1, 1, 0), (3, 0, 1), (3, 1, 1)):
            mine, arrived = held.at[k, quads[q], h], from_a.at[k, h, slot]
            remote(mine, arrived, a_send.at[k, 0], a_recv.at[k, h, slot], core).wait_recv()
            add_into(mine, (mine, arrived), rows)
            if slot == 0:
                b_copy(k, h).start()

    def stage_c(k):
        for h in range(2):
            b_copy(k, h).wait_recv()
            mine = held.at[k, g, h]
            add_into(mine, (mine, from_b.at[k, h]), rows)
        if k > 0:
            z_copy(k).start()

    backs = (
        (stage_core, lambda k: 2 * k + 1, 2),
        (stage_a, lambda k: 2 * k + 2, 2),
        (stage_b, lambda k: 2 * k + 3, 2),
        (stage_c, lambda k: 2 * k + 4, 1),
    )

    def events(s, phase):
        for action, start, when in backs:
            for k in range(n_z):
                if when == phase and start(k) < steps:
                    pl.when(s == start(k))(partial(action, k))
        for k in range(1, n_z):
            if k >= 2 and phase == 1:
                pl.when(s == k - 2)(partial(first, k))
            if phase == 2:
                pl.when(s == 2 * (k - 1))(partial(second, k))
            if phase == 2:
                pl.when(s == 2 * (k - 1) + 1)(partial(third, k))
            if phase == 4:
                pl.when(s == 2 * k - 1)(partial(complete, k))

    first(0)

    @pl.loop(0, width // tile)
    def _(t):
        cols = pl.ds(pl.multiple_of(t * tile, tile), tile)
        down_t[cols, :] = down_ref[:, cols].T

    second(0)
    if n_z > 1:
        first(1)
    third(0)
    complete(0)
    for item in fetches(0):
        item.start()
    for_others(lambda number: share_arrival(number).wait_recv())

    @pl.loop(0, steps)
    def _(s):
        slot = lax.rem(s, 2)
        moe, cot, share = moe_buf.at[slot], cot_buf.at[slot], share_buf
        first_device = owner_of(s) * span + slot * (span // 2)
        for item in fetches(s):
            item.wait()

        @pl.when(s >= 2)
        def _():
            for item in stores(s - 2):
                item.wait()

        for j in range(span // 2):
            column = jnp.broadcast_to(shares_in[first_device + j], (block, block)).T
            share[j * block : (j + 1) * block, :] = column
        wide = jnp.concatenate([share[...]] * (tile // share.shape[1]), axis=1)

        @pl.loop(0, half_width // tile)
        def _(t):
            cols = pl.ds(pl.multiple_of(t * tile, tile), tile)
            gated = dot(moe[...], gate_ref[:, cols], plain)
            lifted = dot(moe[...], up_ref[:, cols], plain)
            gate_val[:, cols] = gated
            up_val[:, cols] = lifted
            scaled[:, cols] = (gated * jax.nn.sigmoid(gated) * lifted * wide).astype(jnp.bfloat16)

        events(s, 1)
        scaled_t[...] = scaled[...].T

        @pl.loop(0, width // (2 * tile))
        def _(t):
            cols = pl.ds(pl.multiple_of(t * 2 * tile, 2 * tile), 2 * tile)
            sent = dot(scaled[...], down_ref[:, cols], plain).astype(jnp.bfloat16)
            held[lax.div(s, 2), pl.ds(slot * (span // 2), span // 2), :, :, cols] = sent.reshape(
                (span // 2, 2, rows, 2 * tile)
            )

        events(s, 2)
        dots_buf[...] = jnp.zeros(dots_buf.shape, f32)

        @pl.loop(0, half_width // tile)
        def _(t):
            cols = pl.ds(pl.multiple_of(t * tile, tile), tile)
            pulled = dot(cot[...], down_t[:, cols], plain)
            gated = gate_val[:, cols]
            lifted = up_val[:, cols]
            sig = jax.nn.sigmoid(gated)
            silu = gated * sig
            product = pulled * (silu * lifted)
            lanes = share.shape[1]
            dots_buf[...] = dots_buf[...] + sum(
                product[:, j * lanes : (j + 1) * lanes] for j in range(tile // lanes)
            )
            pulled = pulled * wide
            pair_stage[slot, :, cols] = (pulled * lifted * sig * (1.0 + gated * (1.0 - sig))).astype(
                jnp.bfloat16
            )
            more = pl.ds(pl.multiple_of(half_width + t * tile, tile), tile)
            pair_stage[slot, :, more] = (pulled * silu).astype(jnp.bfloat16)

        for item in stores(s):
            item.start()
        for j in range(span // 2):
            number = first_device + j
            rows_of = dots_buf[j * block : (j + 1) * block, :]
            dots_own[number] = jnp.sum(rows_of.T, axis=0, keepdims=True)

        for j in range(span // 2):
            number = first_device + j

            @pl.when(number != rank)
            def _():
                dots_copy(number).start()

        events(s, 3)
        events(s, 4)

        @pl.when(s < steps - 1)
        def _():
            for item in fetches(s + 1):
                item.start()

        @pl.loop(0, width // (2 * tile))
        def _(t):
            cols = pl.ds(pl.multiple_of(t * 2 * tile, 2 * tile), 2 * tile)
            grown = dot(scaled_t[...], cot[:, cols], plain)
            down_out[:, cols] = jnp.where(s == 0, 0.0, down_out[:, cols]) + grown

    for t in range(steps, 2 * steps):
        for action, start, _ in backs[::-1]:
            for k in range(n_z):
                if start(k) == t:
                    action(k)
    for s in (steps - 2, steps - 1):
        for item in stores(s):
            item.wait()
    for k in range(1, n_z):
        arrived = from_z.at[order[k]]
        remote(held.at[k, g], arrived, z_send.at[k], z_recv.at[order[k]], core).wait_recv()
    for h in range(2):
        terms = [held.at[0, g, h]] + [from_z.at[order[k], h] for k in range(1, n_z)]
        add_into(out_ref.at[h], terms, rows)
    for k in range(n_z):
        for q in range(4):
            core_copy(k, q).wait_send()
        for j in range(4):
            a_copy(k, j).wait_send()
        for h in range(2):
            b_copy(k, h).wait_send()
        if k > 0:
            z_copy(k).wait_send()
    for ok, make, k in sends:
        run_if(ok, lambda make=make: make().wait_send())
    dots_ref[rank] = dots_own[rank]
    for_others(lambda number: dots_arrival(number).wait_recv())
    for_others(lambda number: share_copy(number).wait_send())
    for_others(lambda number: dots_copy(number).wait_send())


def run_experts(moe_in, all_cot, shares, gate_w, up_w, down_w, collective_id):
    n_z = lax.axis_size("gx")
    span = lax.axis_size("gy")
    rows, width = moe_in.shape
    half = down_w.shape[0]
    total = n_z * span * rows
    step = span * rows // 2
    lanes = 128
    devices = n_z * span
    bf16, f32 = jnp.bfloat16, jnp.float32
    dma = pltpu.SemaphoreType.DMA
    vmem = pl.BlockSpec(memory_space=pltpu.VMEM)
    hbm = pl.BlockSpec(memory_space=pl.ANY)
    return pl.pallas_call(
        partial(expert_kernel, n_z, span),
        out_shape=(
            jax.ShapeDtypeStruct((total, width), bf16),
            jax.ShapeDtypeStruct((total, 2 * half), bf16),
            jax.ShapeDtypeStruct((devices, 1, rows), f32),
            jax.ShapeDtypeStruct((half, width), f32),
            jax.ShapeDtypeStruct((2, rows // 2, width), f32),
        ),
        in_specs=[vmem, hbm, vmem, vmem, vmem, vmem],
        out_specs=(hbm, hbm, vmem, vmem, vmem),
        scratch_shapes=[
            pltpu.VMEM((2, step, width), bf16),
            pltpu.VMEM((2, step, width), bf16),
            pltpu.VMEM((step, lanes), f32),
            pltpu.VMEM((2, step, 2 * half), bf16),
            pltpu.VMEM((step, lanes), f32),
            pltpu.VMEM((step, half), f32),
            pltpu.VMEM((step, half), f32),
            pltpu.VMEM((step, half), bf16),
            pltpu.VMEM((half, step), bf16),
            pltpu.VMEM((width, half), bf16),
            pltpu.VMEM((n_z, span, 2, rows // 2, width), bf16),
            pltpu.VMEM((n_z, 4, 2, rows // 2, width), bf16),
            pltpu.VMEM((n_z, 2, 2, rows // 2, width), bf16),
            pltpu.VMEM((n_z, 2, rows // 2, width), bf16),
            pltpu.VMEM((n_z, 2, rows // 2, width), bf16),
            dma((n_z, 18)),
            dma((n_z * span, 2)),
            dma((2,)),
            dma((3, 2)),
            dma((2, 2)),
            dma((n_z, 4)),
            dma((n_z, 4)),
            dma((n_z, 2)),
            dma((n_z,)),
            dma((n_z, 4)),
            dma((n_z, 2, 2)),
            dma((n_z, 2)),
            dma((n_z,)),
            pltpu.VMEM((devices, 1, rows), f32),
            pltpu.VMEM((devices, 1, rows), f32),
            dma((devices,)),
            dma((devices,)),
            dma((devices,)),
            dma((devices,)),
        ],
        compiler_params=pltpu.CompilerParams(
            collective_id=collective_id, has_side_effects=True, vmem_limit_bytes=67043328
        ),
        name="experts",
    )(moe_in.reshape(2, rows // 2, width), all_cot, shares, gate_w, up_w, down_w)


def pull_kernel(n_i, rows, all_ref, pair_ref, gate_ref, up_ref, out_ref, gate_out, up_out,
                held, from_core, from_a, from_b, from_z, moe_buf, pair_buf,
                fetch_sem, core_send, a_send, b_send, z_send, core_recv, a_recv, b_recv, z_recv):
    z = lax.axis_index("gx")
    g = lax.axis_index("gy")
    flip_x = g + 2 - 4 * ((g // 2) % 2)
    flip_y = g + 4 - 8 * ((g // 4) % 2)
    quads = (flip_x + flip_y - g, flip_x, flip_y, g)
    core = {"gx": z, "gy": flip(g)}
    x_peer = {"gx": z, "gy": flip_x}
    y_peer = {"gx": z, "gy": flip_y}
    along = [{"gx": lax.rem(z + j, n_i), "gy": g} for j in range(1, n_i)]
    barrier_with([(z >= 0, peer) for peer in (core, x_peer, y_peer, *along)])
    item_rows = moe_buf.shape[1]
    width = moe_buf.shape[2]
    half_width = gate_out.shape[1]
    owners = [lax.rem(z + n_i - 1 - i + n_i, n_i) for i in range(n_i)]

    def remote(src, dst, ssem, rsem, peer):
        return pltpu.make_async_remote_copy(
            src_ref=src,
            dst_ref=dst,
            send_sem=ssem,
            recv_sem=rsem,
            device_id=peer,
            device_id_type=pl.DeviceIdType.MESH,
        )

    def fetches(i):
        place = pl.ds(pl.multiple_of(owners[i] * item_rows, item_rows), item_rows)
        return [
            pltpu.make_async_copy(all_ref.at[place], moe_buf.at[i % 2], fetch_sem.at[0, i % 2]),
            pltpu.make_async_copy(pair_ref.at[place], pair_buf.at[i % 2], fetch_sem.at[1, i % 2]),
        ]

    def core_copy(i, q):
        return remote(
            held.at[i, flip(quads[q])],
            from_core.at[i, q],
            core_send.at[i, q],
            core_recv.at[i, q],
            core,
        )

    a_plan = ((0, 0, 0, x_peer), (0, 1, 0, y_peer), (1, 0, 1, x_peer), (2, 1, 1, y_peer))

    def a_copy(i, k):
        q, h, slot, peer = a_plan[k]
        return remote(
            held.at[i, quads[q], h],
            from_a.at[i, h, slot],
            a_send.at[i, k],
            a_recv.at[i, h, slot],
            peer,
        )

    b_plan = ((2, y_peer), (1, x_peer))

    def b_copy(i, h):
        q, peer = b_plan[h]
        return remote(
            held.at[i, quads[q], h], from_b.at[i, h], b_send.at[i, h], b_recv.at[i, h], peer
        )

    def z_copy(i):
        return remote(
            held.at[i, g], from_z.at[z], z_send.at[i], z_recv.at[z], {"gx": owners[i], "gy": g}
        )

    dot = partial(lax.dot_general, preferred_element_type=jnp.float32)
    last_dims = (((1,), (1,)), ((), ()))
    first_dims = (((0,), (0,)), ((), ()))

    def multiply(i):
        for copy in fetches(i):
            copy.wait()
        pair = pair_buf.at[i % 2]
        tile = 256

        @pl.loop(0, width // tile)
        def _(t):
            cols = pl.ds(pl.multiple_of(t * tile, tile), tile)
            total = dot(pair[:, :half_width], gate_ref[cols, :], last_dims)
            total = total + dot(pair[:, half_width:], up_ref[cols, :], last_dims)
            held[i, :, :, :, cols] = total.astype(jnp.bfloat16).reshape(held.shape[1:4] + (tile,))

        for q in range(4):
            core_copy(i, q).start()

    def accumulate(i):
        moe, pair = moe_buf.at[i % 2], pair_buf.at[i % 2]
        tile = 256

        @pl.loop(0, width // tile)
        def _(t):
            cols = pl.ds(pl.multiple_of(t * tile, tile), tile)
            grown = dot(moe[:, cols], pair[...], first_dims)
            if i == 0:
                gate_out[cols, :] = grown[:, :half_width]
                up_out[cols, :] = grown[:, half_width:]
            else:
                gate_out[cols, :] = gate_out[cols, :] + grown[:, :half_width]
                up_out[cols, :] = up_out[cols, :] + grown[:, half_width:]

        if i + 2 < n_i:
            for copy in fetches(i + 2):
                copy.start()

    def stage_a(i):
        for q in range(4):
            core_copy(i, q).wait_recv()
            for h in range(2):
                mine = held.at[i, quads[q], h]
                add_into(mine, (mine, from_core.at[i, q, h]), rows)
            for k in range(4):
                if a_plan[k][0] == q:
                    a_copy(i, k).start()

    def stage_b(i):
        for q, h, slot in ((2, 0, 0), (1, 1, 0), (3, 0, 1), (3, 1, 1)):
            mine, arrived = held.at[i, quads[q], h], from_a.at[i, h, slot]
            remote(mine, arrived, a_send.at[i, 0], a_recv.at[i, h, slot], core).wait_recv()
            add_into(mine, (mine, arrived), rows)
            if slot == 0:
                b_copy(i, h).start()

    def stage_c(i):
        for h in range(2):
            b_copy(i, h).wait_recv()
            mine = held.at[i, g, h]
            add_into(mine, (mine, from_b.at[i, h]), rows)
        if i < n_i - 1:
            z_copy(i).start()
        else:
            for j in range(n_i - 1):
                arrived = from_z.at[owners[j]]
                remote(held.at[j, g], arrived, z_send.at[j], z_recv.at[owners[j]], core).wait_recv()
            for h in range(2):
                terms = [held.at[i, g, h]] + [from_z.at[owners[j], h] for j in range(n_i - 1)]
                add_into(out_ref.at[h], terms, rows)

    for i in range(min(2, n_i)):
        for copy in fetches(i):
            copy.start()
    for t in range(n_i + 3):
        if t < n_i:
            multiply(t)
        if 0 <= t - 1 < n_i:
            stage_a(t - 1)
        if 0 <= t - 2 < n_i:
            stage_b(t - 2)
        if 0 <= t - 1 < n_i:
            accumulate(t - 1)
        if 0 <= t - 3 < n_i:
            stage_c(t - 3)
    for i in range(n_i):
        for q in range(4):
            core_copy(i, q).wait_send()
        for k in range(4):
            a_copy(i, k).wait_send()
        for h in range(2):
            b_copy(i, h).wait_send()
        if i < n_i - 1:
            z_copy(i).wait_send()


def pull_experts(all_moe, pair, gate_w, up_w, collective_id):
    n_i = lax.axis_size("gx")
    span = lax.axis_size("gy")
    total, width = all_moe.shape
    half_width = gate_w.shape[1]
    rows = total // (n_i * span) // 2
    half = (rows, width)
    bf16 = jnp.bfloat16
    dma = pltpu.SemaphoreType.DMA
    vmem = pl.BlockSpec(memory_space=pltpu.VMEM)
    hbm = pl.BlockSpec(memory_space=pl.ANY)
    out, gate_part, up_part = pl.pallas_call(
        partial(pull_kernel, n_i, rows),
        out_shape=(
            jax.ShapeDtypeStruct((2,) + half, jnp.float32),
            jax.ShapeDtypeStruct((width, half_width), jnp.float32),
            jax.ShapeDtypeStruct((width, half_width), jnp.float32),
        ),
        in_specs=[hbm, hbm, vmem, vmem],
        out_specs=(vmem, vmem, vmem),
        scratch_shapes=[
            pltpu.VMEM((n_i, span, 2) + half, bf16),
            pltpu.VMEM((n_i, 4, 2) + half, bf16),
            pltpu.VMEM((n_i, 2, 2) + half, bf16),
            pltpu.VMEM((n_i, 2) + half, bf16),
            pltpu.VMEM((n_i, 2) + half, bf16),
            pltpu.VMEM((2, span * 2 * rows, width), bf16),
            pltpu.VMEM((2, span * 2 * rows, 2 * half_width), bf16),
            dma((2, 2)),
            dma((n_i, 4)),
            dma((n_i, 4)),
            dma((n_i, 2)),
            dma((n_i,)),
            dma((n_i, 4)),
            dma((n_i, 2, 2)),
            dma((n_i, 2)),
            dma((n_i,)),
        ],
        compiler_params=pltpu.CompilerParams(
            collective_id=collective_id, has_side_effects=True, vmem_limit_bytes=67043328
        ),
        name="pull_experts",
    )(all_moe, pair, gate_w, up_w)
    return out.reshape(2 * rows, width), gate_part, up_part


def turn(values, cosine, sine):
    return values * cosine + pltpu.roll(values, values.shape[-1] // 2, 1) * sine


def greet_chain(n_z):
    z = lax.axis_index("gx")
    g = lax.axis_index("gy")
    barrier_with([(z < n_z - 1, {"gx": z + 1, "gy": g}), (z > 0, {"gx": z - 1, "gy": g})])


def attend_kernel(
    heads,
    pieces,
    own_acts,
    own_weight,
    own_out_weight,
    own_cot,
    query_gain,
    key_gain,
    cosine_ref,
    sine_ref,
    row_docs,
    col_docs,
    attended_ref,
    acts_out,
    weight_out,
    full_out,
    all_cot,
    query_raw,
    key_raw,
    ready_ref,
    mixed_ref,
    totals_ref,
    peaks_ref,
    part_ref,
    held,
    from_core,
    from_a,
    from_b,
    from_z,
    near_send,
    near_recv,
    near_local,
    far_send,
    far_recv,
    far_local,
    in_send,
    in_recv,
    in_local,
    out_send,
    out_recv,
    out_local,
    load_sem,
    core_send,
    a_send,
    b_send,
    z_send,
    core_recv,
    a_recv,
    b_recv,
    z_recv,
):
    n_z = lax.axis_size("gx")
    span = lax.axis_size("gy")
    greet(n_z)
    in_start, in_relays, in_finish = chain_gather(
        n_z, own_weight, weight_out, in_send, in_recv, in_local
    )
    out_start, out_relays, out_finish = chain_gather(
        n_z, own_out_weight, full_out, out_send, out_recv, out_local
    )
    near, near_finish = gather_steps(1, span, own_acts, acts_out, near_send, near_recv, near_local)
    far, far_finish = gather_steps(n_z, span, own_cot, all_cot, far_send, far_recv, far_local)
    back = []
    scatter_kernel(
        False,
        pieces,
        part_ref.shape[3],
        part_ref,
        attended_ref,
        held,
        from_core,
        from_a,
        from_b,
        from_z,
        load_sem,
        core_send,
        a_send,
        b_send,
        z_send,
        core_recv,
        a_recv,
        b_recv,
        z_recv,
        parts=back,
    )
    f32, bf16 = jnp.float32, jnp.bfloat16
    dot = partial(lax.dot_general, preferred_element_type=f32)
    plain = (((1,), (0,)), ((), ()))
    last_dims = (((1,), (1,)), ((), ()))
    length = query_raw.shape[0]
    width = acts_out.shape[3]
    local = heads * HD
    block = 256
    scale = HD ** (-0.5)

    in_start()
    near[0]()
    far[0]()
    near[1]()
    near[2]()
    later = far[1:]
    for relay in in_relays:
        relay()
        for step in later[:1]:
            step()
        later = later[1:]
    out_start()
    in_finish()
    near_finish()
    waiting = [list(out_relays), list(later)]

    def pull(which):
        if waiting[which]:
            waiting[which].pop(0)()

    def project(source):
        cols = slice(source * local, (source + 1) * local)
        acts = acts_out[...].reshape(length, width)
        total = jnp.zeros((length, local), f32)
        depth = own_weight.shape[0]
        for owner in range(n_z):
            total = total + dot(
                acts[:, owner * depth : (owner + 1) * depth], weight_out[owner, :, cols], plain
            )
        return total

    for source, raw, gain in ((0, query_raw, query_gain), (1, key_raw, key_gain)):
        raw[...] = project(source)
        for h in range(heads):
            cols = slice(h * HD, (h + 1) * HD)

            @pl.loop(0, length // block)
            def _(t):
                at = pl.ds(pl.multiple_of(t * block, block), block)
                value = raw[at, cols]
                normed = value * lax.rsqrt(jnp.mean(value * value, axis=-1, keepdims=True) + EPSILON)
                turned = turn(normed * gain[...], cosine_ref[at, :], sine_ref[at, :])
                where = source * local + h * HD
                ready_ref[at, where : where + HD] = turned.astype(bf16)

        pull(source)

    ready_ref[:, 2 * local :] = project(2).astype(bf16)
    pull(0)
    lanes = lax.broadcasted_iota(jnp.int32, (block, HD), 1)
    peaks_ref[...] = jnp.full(peaks_ref.shape, NEGATIVE, f32)

    def mix(t):
        at = pl.ds(pl.multiple_of(t * block, block), block)
        same = row_docs[at, :1] == col_docs[:1, :]
        kept = jnp.zeros((block, HD), f32)
        for h in range(heads):
            query = ready_ref[at, h * HD : (h + 1) * HD]
            key = ready_ref[:, local + h * HD : local + (h + 1) * HD]
            value = ready_ref[:, 2 * local + h * HD : 2 * local + (h + 1) * HD]
            scores = jnp.where(same, dot(query, key, last_dims) * scale, NEGATIVE)
            highest = jnp.max(scores, axis=-1, keepdims=True)
            weights = jnp.exp(scores - highest)
            total = jnp.sum(weights, axis=-1, keepdims=True)
            shares = (weights * (1.0 / total)).astype(bf16)
            mixed_ref[at, h * HD : (h + 1) * HD] = dot(shares, value, plain).astype(bf16)
            kept = jnp.where(lanes == h, highest + jnp.log(total), kept)
            top = jnp.max(highest, axis=0, keepdims=True)
            peaks_ref[h : h + 1, :] = jnp.maximum(peaks_ref[h : h + 1, :], top)
        totals_ref[at, :] = kept

    blocks = length // block
    for quarter in range(2):

        @pl.loop(quarter * blocks // 2, (quarter + 1) * blocks // 2)
        def _(t):
            mix(t)

        pull(1)
    for relay in waiting[0]:
        relay()
    out_finish()
    rows = part_ref.shape[3]
    per_owner = own_out_weight.shape[1] // block

    @pl.loop(0, n_z * per_owner)
    def _(t):
        cols = pl.ds(pl.multiple_of(t * block, block), block)
        inside = pl.ds(pl.multiple_of(lax.rem(t, per_owner) * block, block), block)
        sent = dot(mixed_ref[...], full_out[lax.div(t, per_owner), :, inside], plain).astype(bf16)
        sent = sent.reshape(span, pieces, 2, rows, block)
        for p in range(pieces):
            part_ref[p, :, :, :, cols] = sent[:, p]

    for step in back[:-1]:
        step()
        pull(1)
    for step in waiting[1]:
        step()
    back[-1]()
    far_finish()


def attend(
    acts, weights, out_weight, cot, query_gain, key_gain, tables, docs, collective_id, pieces=4
):
    tokens, width = acts.shape
    local = weights.shape[1] // 3
    heads = local // HD
    n_z = lax.axis_size("gx")
    span = lax.axis_size("gy")
    length = span * tokens
    rows = tokens // (pieces * 2)
    half = (2, tokens // 2, width)
    piece = (rows, width)
    f32, bf16 = jnp.float32, jnp.bfloat16
    dma = pltpu.SemaphoreType.DMA
    vmem = pl.BlockSpec(memory_space=pltpu.VMEM)
    hbm = pl.BlockSpec(memory_space=pl.ANY)
    attended, seq, full, full_out, all_cot, *saved, peaks = pl.pallas_call(
        partial(attend_kernel, heads, pieces),
        out_shape=(
            jax.ShapeDtypeStruct((pieces, 2) + piece, f32),
            jax.ShapeDtypeStruct((span,) + half, bf16),
            jax.ShapeDtypeStruct((n_z,) + weights.shape, bf16),
            jax.ShapeDtypeStruct((n_z,) + out_weight.shape, bf16),
            jax.ShapeDtypeStruct((n_z * span,) + half, bf16),
            jax.ShapeDtypeStruct((length, local), f32),
            jax.ShapeDtypeStruct((length, local), f32),
            jax.ShapeDtypeStruct((length, 3 * local), bf16),
            jax.ShapeDtypeStruct((length, local), bf16),
            jax.ShapeDtypeStruct((length, HD), f32),
            jax.ShapeDtypeStruct((8, HD), f32),
        ),
        in_specs=[vmem] * 10,
        out_specs=(vmem, vmem, vmem, vmem, hbm) + (vmem,) * 6,
        scratch_shapes=[
            pltpu.VMEM((pieces, span, 2) + piece, bf16),
            pltpu.VMEM((pieces, 4, 2) + piece, bf16),
            pltpu.VMEM((pieces, 4, 2) + piece, bf16),
            pltpu.VMEM((pieces, 2, 2) + piece, bf16),
            pltpu.VMEM((pieces, 2) + piece, bf16),
            pltpu.VMEM((1, 2, 16, 128), bf16),
            dma((24,)),
            dma((span, 2)),
            dma,
            dma((24 * (2 * n_z - 1),)),
            dma((n_z * span, 2)),
            dma,
            dma((2 * n_z,)),
            dma((n_z,)),
            dma,
            dma((2 * n_z,)),
            dma((n_z,)),
            dma,
            dma((pieces, 4)),
            dma((pieces, 4)),
            dma((pieces, 4)),
            dma((pieces, 2)),
            dma((pieces,)),
            dma((pieces, 4)),
            dma((pieces, 2, 2)),
            dma((pieces, 2)),
            dma((pieces,)),
        ],
        compiler_params=pltpu.CompilerParams(
            collective_id=collective_id, has_side_effects=True, vmem_limit_bytes=60 << 20
        ),
        name="attend",
    )(
        acts.reshape(half),
        weights,
        out_weight,
        cot.reshape(half),
        query_gain.reshape(1, HD),
        key_gain.reshape(1, HD),
        *tables,
        *docs,
    )
    return (
        attended.reshape(tokens, width),
        seq.reshape(length, width),
        full.reshape(n_z * weights.shape[0], weights.shape[1]),
        all_cot.reshape(n_z * span * tokens, width),
        (*saved, full_out),
        peaks,
    )


def attend_back_kernel(
    heads,
    pieces,
    grad_ref,
    out_weight_ref,
    mixed_ref,
    ready_ref,
    query_raw,
    key_raw,
    totals_ref,
    query_gain,
    key_gain,
    cosine_ref,
    sine_ref,
    row_docs,
    col_docs,
    acts_hbm,
    weight_hbm,
    part_ref,
    weight_part,
    out_sum,
    gain_ref,
    acts_ref,
    weight_ref,
    grad_mixed,
    grad_heads,
    turned,
    key_sum,
    value_sum,
    sums,
    from_low,
    from_high,
    copy_sem,
    chain_send,
    low_recv,
    high_recv,
):
    n_z = lax.axis_size("gx")
    greet_chain(n_z)
    start, relays, finish = chain_scatter(
        n_z, sums, out_sum, from_low, from_high, chain_send, low_recv, high_recv
    )
    f32, bf16 = jnp.float32, jnp.bfloat16
    dot = partial(lax.dot_general, preferred_element_type=f32)
    plain = (((1,), (0,)), ((), ()))
    last_dims = (((1,), (1,)), ((), ()))
    first_dims = (((0,), (0,)), ((), ()))
    length, width = grad_ref.shape
    span = part_ref.shape[1]
    rows = part_ref.shape[3]
    local = heads * HD
    block = 256
    scale = HD ** (-0.5)
    copies = [
        pltpu.make_async_copy(acts_hbm, acts_ref, copy_sem.at[0]),
        pltpu.make_async_copy(weight_hbm, weight_ref, copy_sem.at[1]),
    ]
    for copy in copies:
        copy.start()
    owned = width // n_z

    @pl.loop(0, width // block)
    def _(t):
        cols = pl.ds(pl.multiple_of(t * block, block), block)
        inside = pl.ds(pl.multiple_of(lax.rem(t, owned // block) * block, block), block)
        sums[lax.div(t, owned // block), inside, :] = dot(
            grad_ref[:, cols], mixed_ref[...], first_dims
        ).astype(bf16)

    start()
    total = dot(grad_ref[:, :owned], out_weight_ref[0], last_dims)
    for owner in range(1, n_z):
        cols = slice(owner * owned, (owner + 1) * owned)
        total = total + dot(grad_ref[:, cols], out_weight_ref[owner], last_dims)
    grad_mixed[...] = total.astype(bf16)
    gain_ref[...] = jnp.zeros_like(gain_ref)
    for h in range(heads):
        cols = slice(h * HD, (h + 1) * HD)
        key = ready_ref[:, local + h * HD : local + (h + 1) * HD]
        value = ready_ref[:, 2 * local + h * HD : 2 * local + (h + 1) * HD]
        key_sum[...] = jnp.zeros_like(key_sum)
        value_sum[...] = jnp.zeros_like(value_sum)

        @pl.loop(0, length // block)
        def _(t):
            at = pl.ds(pl.multiple_of(t * block, block), block)
            same = row_docs[at, :1] == col_docs[:1, :]
            query = ready_ref[at, cols]
            grad = grad_mixed[at, cols]
            scores = jnp.where(same, dot(query, key, last_dims) * scale, NEGATIVE)
            weights = jnp.exp(scores - totals_ref[at, h : h + 1])
            value_sum[...] += dot(weights.astype(bf16), grad, first_dims)
            pulled = dot(grad, value, last_dims)
            inner = jnp.sum(weights * pulled, axis=-1, keepdims=True)
            grad_scores = (weights * (pulled - inner)).astype(bf16)
            turned[at, :] = dot(grad_scores, key, plain) * scale
            key_sum[...] += dot(grad_scores, query, first_dims)

        for source, raw, gain, incoming, factor in (
            (0, query_raw, query_gain, turned, 1.0),
            (1, key_raw, key_gain, key_sum, scale),
        ):

            @pl.loop(0, length // block)
            def _(t):
                at = pl.ds(pl.multiple_of(t * block, block), block)
                back = turn(incoming[at, :] * factor, cosine_ref[at, :], -sine_ref[at, :])
                item = raw[at, cols]
                inverse = lax.rsqrt(jnp.mean(item * item, axis=-1, keepdims=True) + EPSILON)
                normed = item * inverse
                gain_ref[source : source + 1, :] += jnp.sum(back * normed, axis=0, keepdims=True)
                inner = back * gain[...]
                pulled = inverse * (
                    inner - normed * jnp.mean(inner * normed, axis=-1, keepdims=True)
                )
                where = source * local + h * HD
                grad_heads[at, where : where + HD] = pulled.astype(bf16)

        where = 2 * local + h * HD
        grad_heads[:, where : where + HD] = value_sum[...].astype(bf16)
        if h < len(relays) - 1:
            relays[h]()

    for relay in relays[min(heads, len(relays) - 1) :]:
        relay()
    finish()

    for copy in copies:
        copy.wait()

    @pl.loop(0, width // block)
    def _(t):
        cols = pl.ds(pl.multiple_of(t * block, block), block)
        weight_part[cols, :] = dot(acts_ref[:, cols], grad_heads[...], first_dims).astype(bf16)
        sent = dot(grad_heads[...], weight_ref[cols, :], last_dims).astype(bf16)
        sent = sent.reshape(span, pieces, 2, rows, block)
        for p in range(pieces):
            part_ref[p, :, :, :, cols] = sent[:, p]


def attend_back(
    seq_grad,
    saved,
    query_gain,
    key_gain,
    tables,
    docs,
    acts,
    weights,
    collective_id,
    pieces=4,
):
    query_raw, key_raw, ready, mixed, totals, out_weight = saved
    n_z = lax.axis_size("gx")
    dma = pltpu.SemaphoreType.DMA
    block = (n_z, acts.shape[1] // n_z, query_raw.shape[1])
    length, width = seq_grad.shape
    local = query_raw.shape[1]
    heads = local // HD
    span = lax.axis_size("gy")
    rows = length // (span * pieces * 2)
    f32, bf16 = jnp.float32, jnp.bfloat16
    vmem = pl.BlockSpec(memory_space=pltpu.VMEM)
    hbm = pl.BlockSpec(memory_space=pl.ANY)
    return pl.pallas_call(
        partial(attend_back_kernel, heads, pieces),
        out_shape=(
            jax.ShapeDtypeStruct((pieces, span, 2, rows, width), bf16),
            jax.ShapeDtypeStruct((width, 3 * local), bf16),
            jax.ShapeDtypeStruct(block[1:], f32),
            jax.ShapeDtypeStruct((8, HD), f32),
        ),
        in_specs=[vmem] * 13 + [hbm] * 2,
        out_specs=(vmem,) * 4,
        scratch_shapes=[
            pltpu.VMEM((length, width), bf16),
            pltpu.VMEM((width, 3 * local), bf16),
            pltpu.VMEM((length, local), bf16),
            pltpu.VMEM((length, 3 * local), bf16),
            pltpu.VMEM((length, HD), f32),
            pltpu.VMEM((length, HD), f32),
            pltpu.VMEM((length, HD), f32),
            pltpu.VMEM(block, bf16),
            pltpu.VMEM(block, bf16),
            pltpu.VMEM(block, bf16),
            dma((2,)),
            dma((n_z,)),
            dma((n_z,)),
            dma((n_z,)),
        ],
        compiler_params=pltpu.CompilerParams(
            collective_id=collective_id, has_side_effects=True, vmem_limit_bytes=60 << 20
        ),
        name="attend_back",
    )(
        seq_grad,
        out_weight,
        mixed,
        ready,
        query_raw,
        key_raw,
        totals,
        query_gain.reshape(1, HD),
        key_gain.reshape(1, HD),
        *tables,
        *docs,
        acts,
        weights,
    )


def norm_rows(values, gain_row):
    return (
        values * lax.rsqrt(jnp.mean(values * values, axis=-1, keepdims=True) + EPSILON) * gain_row
    )


def rotary(values):
    length = values.shape[0]
    halfway = values.shape[-1] // 2
    positions = jnp.arange(length, dtype=jnp.float32)
    frequency = jnp.exp(
        jnp.arange(halfway, dtype=jnp.float32) * (-2.0 * jnp.log(10000.0) / values.shape[-1])
    )
    angles = (positions[:, None] * frequency[None, :])[:, None, :]
    cosine = jnp.cos(angles)
    sine_table = jnp.sin(angles)
    first_half = values[..., :halfway]
    second = values[..., halfway:]
    return jnp.concatenate(
        [first_half * cosine - second * sine_table, second * cosine + first_half * sine_table],
        axis=-1,
    )


def prepare_heads(raw_heads, gain_row):
    return rotary(norm_rows(raw_heads, gain_row))


def route_gates(id_table, logits):
    shares = jax.nn.softmax(logits, axis=-1)
    experts = logits.shape[-1]
    matches = id_table[:, :, None] == jnp.arange(experts, dtype=jnp.int32)[None, None, :]
    chosen = jnp.sum(jnp.where(matches, shares[:, None, :], 0.0), axis=-1)
    return chosen / jnp.sum(chosen, axis=-1, keepdims=True)


def contract_rows(left_side, right_side):
    return lax.dot_general(
        left_side, right_side, (((0,), (0,)), ((), ())), preferred_element_type=jnp.float32
    )


def contract_cols(left_side, right_side):
    return lax.dot_general(
        left_side, right_side, (((1,), (1,)), ((), ())), preferred_element_type=jnp.float32
    )


def routed_experts(
    moe_in, cotangent, expert_ids, gate_share, router_weight, gate_weight, up_weight, down_weight
):
    tok_rows = moe_in.shape[0]
    experts = router_weight.shape[1]
    width_all = moe_in.shape[1]
    capacity = tok_rows * TOP * 3 // (2 * experts)
    route_count = tok_rows * TOP
    flat_ids = expert_ids.reshape(route_count)
    onehot = (flat_ids[:, None] == jnp.arange(experts, dtype=jnp.int32)[None, :]).astype(jnp.int32)
    earlier = jnp.cumsum(onehot, axis=0) - onehot
    slot_index = jnp.sum(earlier * onehot, axis=1)
    target = flat_ids * capacity + slot_index
    source = (
        jnp.full((experts * capacity,), tok_rows, jnp.int32)
        .at[target]
        .set(jnp.arange(route_count, dtype=jnp.int32) // TOP)
    )
    padded_in = jnp.concatenate([moe_in, jnp.zeros((1, width_all), jnp.bfloat16)], axis=0)
    packed = padded_in[source].reshape(experts, 1, capacity, width_all)
    outgoing = jnp.broadcast_to(packed, (experts, 2, capacity, width_all)).reshape(
        2 * experts, capacity, width_all
    )
    arrived = lax.all_to_all(outgoing, ("gx", "gy"), split_axis=0, concat_axis=1, tiled=True)[0]
    gate_in = gate_weight[0]
    up_in = up_weight[0]
    down_in = down_weight[0]
    gate_val = jnp.dot(arrived, gate_in, preferred_element_type=jnp.float32)
    up_val = jnp.dot(arrived, up_in, preferred_element_type=jnp.float32)
    hidden = (jax.nn.silu(gate_val) * up_val).astype(jnp.bfloat16)
    produced = jnp.dot(hidden, down_in, preferred_element_type=jnp.float32).astype(jnp.bfloat16)
    returned = lax.all_to_all(produced[None], ("gx", "gy"), split_axis=1, concat_axis=0, tiled=True)
    summed = (
        returned.reshape(experts, 2, capacity, width_all)
        .astype(jnp.float32)
        .sum(axis=1)
        .reshape(experts * capacity, width_all)
    )
    route_out = summed[target]
    gates_flat = gate_share.reshape(route_count)
    moe_out = jnp.sum((gates_flat[:, None] * route_out).reshape(tok_rows, TOP, width_all), axis=1)
    grad_out = cotangent.astype(jnp.float32)
    grad_gates = jnp.sum(
        route_out.reshape(tok_rows, TOP, width_all) * grad_out[:, None, :], axis=-1
    )
    slot_gate = jnp.zeros((experts * capacity,), jnp.float32).at[target].set(gates_flat)
    padded_grad = jnp.concatenate([grad_out, jnp.zeros((1, width_all), jnp.float32)], axis=0)
    grad_packed = (
        (slot_gate[:, None] * padded_grad[source])
        .astype(jnp.bfloat16)
        .reshape(experts, 1, capacity, width_all)
    )
    grad_outgoing = jnp.broadcast_to(grad_packed, (experts, 2, capacity, width_all)).reshape(
        2 * experts, capacity, width_all
    )
    grad_arrived = lax.all_to_all(
        grad_outgoing, ("gx", "gy"), split_axis=0, concat_axis=1, tiled=True
    )[0]
    rows_in, grad_use = (arrived, grad_arrived)
    gate_use, up_use, hidden_use = (gate_val, up_val, hidden)
    sigmoid_gate = jax.nn.sigmoid(gate_use)
    silu_gate = gate_use * sigmoid_gate
    grad_hidden = contract_cols(grad_use, down_in)
    down_part = contract_rows(hidden_use, grad_use)
    grad_gate = (
        grad_hidden * up_use * sigmoid_gate * (1.0 + gate_use * (1.0 - sigmoid_gate))
    ).astype(jnp.bfloat16)
    grad_up = (grad_hidden * silu_gate).astype(jnp.bfloat16)
    gate_part = contract_rows(rows_in, grad_gate)
    up_part = contract_rows(rows_in, grad_up)
    grad_in = contract_cols(grad_gate, gate_in) + contract_cols(grad_up, up_in)
    grad_back = lax.all_to_all(
        grad_in.astype(jnp.bfloat16)[None], ("gx", "gy"), split_axis=1, concat_axis=0, tiled=True
    )
    grad_summed = (
        grad_back.reshape(experts, 2, capacity, width_all)
        .astype(jnp.float32)
        .sum(axis=1)
        .reshape(experts * capacity, width_all)
    )
    grad_moe_in = jnp.sum(grad_summed[target].reshape(tok_rows, TOP, width_all), axis=1)
    return moe_out, grad_gates, grad_moe_in, gate_part, up_part, down_part


def dense_experts(
    moe_in, all_cot, expert_ids, gate_share, gate_weight, up_weight, down_weight
):
    devices = lax.axis_size("gx") * lax.axis_size("gy")
    experts = devices // 2
    matches = expert_ids[:, :, None] == jnp.arange(experts, dtype=jnp.int32)[None, None, :]
    dense_gates = jnp.sum(jnp.where(matches, gate_share[:, :, None], 0.0), axis=1)
    shares = jnp.repeat(dense_gates.T, 2, axis=0)[:, None, :]
    all_moe, pair, gate_dots, down_part, moe_out = run_experts(
        moe_in, all_cot, shares, gate_weight[0], up_weight[0], down_weight[0], 8
    )
    moe_out = moe_out.reshape(moe_in.shape)
    dots_experts = gate_dots.reshape(experts, 2, -1).sum(axis=1).T
    grad_gates = jnp.sum(jnp.where(matches, dots_experts[:, None, :], 0.0), axis=-1)
    grad_moe_in, gate_part, up_part = pull_experts(all_moe, pair, gate_weight[0], up_weight[0], 9)
    return moe_out, grad_gates, grad_moe_in, gate_part, up_part, down_part


def plain_attention(
    acts, in_weights, out_weight, query_gain, key_gain, doc_ids, cotangent
):
    seq_acts = lax.all_gather(acts, "gy", axis=0, tiled=True)
    full_in = lax.all_gather(in_weights, "gx", axis=0, tiled=True)
    out_rows = lax.all_gather(out_weight, "gx", axis=1, tiled=True)
    local_width = full_in.shape[1] // 3
    length = seq_acts.shape[0]
    local_heads = local_width // HD
    projected = jnp.dot(seq_acts, full_in, preferred_element_type=jnp.float32)
    queries = projected[:, :local_width]
    key_raw = projected[:, local_width : 2 * local_width]
    value_ready = (
        projected[:, 2 * local_width :].astype(jnp.bfloat16).reshape(length, local_heads, HD)
    )
    query_float, query_pull = jax.vjp(
        prepare_heads, queries.reshape(length, local_heads, HD), query_gain
    )
    key_float, key_pull = jax.vjp(prepare_heads, key_raw.reshape(length, local_heads, HD), key_gain)
    query_ready = query_float.astype(jnp.bfloat16)
    key_ready = key_float.astype(jnp.bfloat16)
    block_rows = min(512, length)
    block_count = length // block_rows
    score_scale = HD ** (-0.5)
    query_blocks = query_ready.reshape(block_count, block_rows, local_heads, HD)
    doc_blocks = doc_ids.reshape(block_count, block_rows)

    def block_scores(query_block, doc_block):
        scores = (
            jnp.einsum("qhd,khd->hqk", query_block, key_ready, preferred_element_type=jnp.float32)
            * score_scale
        )
        same_doc = doc_block[:, None] == doc_ids[None, :]
        return jnp.where(same_doc[None], scores, NEGATIVE)

    def forward_block(pieces):
        scores = block_scores(pieces[0], pieces[1])
        highest = jnp.max(scores, axis=-1, keepdims=True)
        weights = jnp.exp(scores - highest)
        totals = jnp.sum(weights, axis=-1, keepdims=True)
        shares = (weights / totals).astype(jnp.bfloat16)
        mixed_heads = jnp.einsum(
            "hqk,khd->qhd", shares, value_ready, preferred_element_type=jnp.float32
        )
        return (
            mixed_heads.astype(jnp.bfloat16),
            highest[..., 0] + jnp.log(totals[..., 0]),
            jnp.max(highest[..., 0], axis=-1),
        )

    mixed_blocks, log_totals, peak_blocks = lax.map(forward_block, (query_blocks, doc_blocks))
    mixed_seq = mixed_blocks.reshape(length, local_width)
    attended = lax.psum_scatter(
        jnp.dot(mixed_seq, out_rows, preferred_element_type=jnp.float32),
        "gy",
        scatter_dimension=0,
        tiled=True,
    )

    def back(grad_resid):
        seq_grad = lax.all_gather(grad_resid.astype(jnp.bfloat16), "gy", axis=0, tiled=True)
        grad_mixed = contract_cols(seq_grad, out_rows).astype(jnp.bfloat16)
        out_part = contract_rows(seq_grad, mixed_seq)

        def backward_block(running, pieces):
            grad_key, grad_value = running
            query_block, grad_block, log_block, doc_block = pieces
            scores = block_scores(query_block, doc_block)
            weights = jnp.exp(scores - log_block[..., None])
            grad_value = grad_value + jnp.einsum(
                "hqk,qhd->khd",
                weights.astype(jnp.bfloat16),
                grad_block,
                preferred_element_type=jnp.float32,
            )
            grad_weights = jnp.einsum(
                "qhd,khd->hqk", grad_block, value_ready, preferred_element_type=jnp.float32
            )
            inner_sum = jnp.sum(weights * grad_weights, axis=-1, keepdims=True)
            grad_scores = (weights * (grad_weights - inner_sum)).astype(jnp.bfloat16)
            grad_query = (
                jnp.einsum("hqk,khd->qhd", grad_scores, key_ready, preferred_element_type=jnp.float32)
                * score_scale
            )
            grad_key = (
                grad_key
                + jnp.einsum(
                    "hqk,qhd->khd", grad_scores, query_block, preferred_element_type=jnp.float32
                )
                * score_scale
            )
            return ((grad_key, grad_value), grad_query)

        empty_heads = jnp.zeros((length, local_heads, HD), jnp.float32)
        grad_mixed_blocks = grad_mixed.reshape(block_count, block_rows, local_heads, HD)
        (key_grad_heads, value_grad_heads), query_grad_blocks = lax.scan(
            backward_block,
            (empty_heads, empty_heads),
            (query_blocks, grad_mixed_blocks, log_totals, doc_blocks),
        )
        query_raw_grad, query_gain_part = query_pull(query_grad_blocks.reshape(length, local_heads, HD))
        key_raw_grad, key_gain_part = key_pull(key_grad_heads)
        grad_queries = query_raw_grad.reshape(length, local_width).astype(jnp.bfloat16)
        grad_keys = key_raw_grad.reshape(length, local_width).astype(jnp.bfloat16)
        grad_values = value_grad_heads.reshape(length, local_width).astype(jnp.bfloat16)
        grad_heads = jnp.concatenate([grad_queries, grad_keys, grad_values], axis=1)
        acts_part = contract_cols(grad_heads, full_in).astype(jnp.bfloat16)
        in_sum = lax.psum_scatter(
            contract_rows(seq_acts, grad_heads).astype(jnp.bfloat16),
            "gx",
            scatter_dimension=0,
            tiled=True,
        ).astype(jnp.float32)
        grad_acts = lax.psum_scatter(acts_part, "gy", scatter_dimension=0, tiled=True)
        out_sum = lax.psum_scatter(
            out_part.astype(jnp.bfloat16), "gx", scatter_dimension=0, tiled=True
        ).astype(jnp.float32)
        return grad_acts.astype(jnp.float32), in_sum, out_sum, query_gain_part, key_gain_part

    return attended, jnp.max(peak_blocks, axis=0), None, back


def kernel_attention(
    acts, in_weights, out_weight, query_gain, key_gain, doc_ids, cotangent
):
    length = doc_ids.shape[0]
    halfway = HD // 2
    frequency = jnp.exp(
        jnp.arange(halfway, dtype=jnp.float32) * (-2.0 * jnp.log(10000.0) / HD)
    )
    angles = jnp.arange(length, dtype=jnp.float32)[:, None] * frequency[None, :]
    cosine, sine = jnp.cos(angles), jnp.sin(angles)
    tables = (
        jnp.concatenate([cosine, cosine], axis=1),
        jnp.concatenate([-sine, sine], axis=1),
    )
    docs = (
        jnp.broadcast_to(doc_ids[:, None], (length, HD)),
        jnp.broadcast_to(doc_ids[None, :], (8, length)),
    )
    attended, seq_acts, full_in, all_cot, saved, peaks = attend(
        acts, in_weights, out_weight, cotangent, query_gain, key_gain, tables, docs, 10
    )
    heads = in_weights.shape[1] // (3 * HD)

    def back(grad_resid):
        seq_grad = all_gather(grad_resid.astype(jnp.bfloat16), False, 1)
        part, weight_part, out_sum, gains = attend_back(
            seq_grad, saved, query_gain, key_gain, tables, docs, seq_acts, full_in, 11
        )
        grad_acts, in_sum = leave(part, weight_part, 7)
        return grad_acts, in_sum, out_sum, gains[0], gains[1]

    return attended, peaks[:heads, 0], all_cot, back


def local(
    tokens,
    cotangent,
    expert_ids,
    doc_ids,
    clip_rank,
    attn_gain,
    moe_gain,
    query_gain,
    key_gain,
    query_weight,
    key_weight,
    value_weight,
    out_weight,
    router_weight,
    gate_weight,
    up_weight,
    down_weight,
):
    inputs = tokens.astype(jnp.float32)
    acts_float, norm_pull = jax.vjp(norm_rows, inputs, attn_gain)
    acts_low = acts_float.astype(jnp.bfloat16)
    in_weights = jnp.concatenate([query_weight, key_weight, value_weight], axis=1)
    by_kernels = lax.axis_size("gy") == 8
    local_width = query_weight.shape[1]
    local_heads = local_width // HD
    attention = kernel_attention if by_kernels else plain_attention
    attended, own_peaks, all_cot, attention_back = attention(
        acts_low, in_weights, out_weight, query_gain, key_gain, doc_ids, cotangent
    )
    start_head = lax.axis_index("gy") * local_heads
    peak_slots = lax.dynamic_update_slice(
        jnp.zeros((lax.axis_size("gx"), NH), jnp.float32),
        own_peaks[None],
        (lax.axis_index("gx"), start_head),
    )
    residual = inputs + attended
    moe_float, moe_pull = jax.vjp(norm_rows, residual, moe_gain)
    moe_in = moe_float.astype(jnp.bfloat16)
    logits = jnp.dot(moe_in, router_weight, preferred_element_type=jnp.float32)
    gate_share, gate_pull = jax.vjp(partial(route_gates, expert_ids), logits)
    if by_kernels and router_weight.shape[1] <= 2 * TOP:
        moe_out, grad_gates, grad_moe_in, gate_part, up_part, down_part = dense_experts(
            moe_in, all_cot, expert_ids, gate_share, gate_weight, up_weight, down_weight
        )
    else:
        moe_out, grad_gates, grad_moe_in, gate_part, up_part, down_part = routed_experts(
            moe_in,
            cotangent,
            expert_ids,
            gate_share,
            router_weight,
            gate_weight,
            up_weight,
            down_weight,
        )
    output = (residual + moe_out).astype(jnp.bfloat16)
    grad_out = cotangent.astype(jnp.float32)
    (grad_logits,) = gate_pull(grad_gates)
    grad_logits_low = grad_logits.astype(jnp.bfloat16)
    router_part = contract_rows(moe_in, grad_logits_low)
    grad_moe_in = grad_moe_in + contract_cols(grad_logits_low, router_weight)
    grad_resid_norm, moe_gain_part = moe_pull(grad_moe_in)
    grad_resid = grad_out + grad_resid_norm
    grad_acts, in_sum, out_sum, query_gain_part, key_gain_part = attention_back(grad_resid)
    query_sum = in_sum[:, :local_width]
    key_sum = in_sum[:, local_width : 2 * local_width]
    value_sum = in_sum[:, 2 * local_width :]
    norm_input_grad, attn_gain_part = norm_pull(grad_acts)
    input_grad = grad_resid + norm_input_grad
    small = (
        attn_gain_part,
        moe_gain_part,
        query_gain_part,
        key_gain_part,
        router_part.T,
        peak_slots,
    )
    summed = sum_everywhere(jnp.concatenate([part.reshape(-1) for part in small]), 5)
    ends = list(accumulate(part.size for part in small))
    attn_gain_grad, moe_gain_grad, query_gain_grad, key_gain_grad, router_flat, peaks = (
        summed[end - part.size : end].reshape(part.shape) for end, part in zip(ends, small)
    )
    router_grad = router_flat.T
    peak_global = jnp.max(peaks, axis=0)
    ranked = -jnp.sort(-peak_global)
    limit = jnp.sum(jnp.where(jnp.arange(NH, dtype=jnp.int32) == clip_rank[0], ranked, 0.0))
    factors = jnp.where(peak_global > limit, limit / peak_global, 1.0)
    own_factors = lax.dynamic_slice_in_dim(factors, start_head, local_heads)
    columns = jnp.repeat(jnp.sqrt(own_factors), HD)
    query_clipped = (query_weight.astype(jnp.float32) * columns[None, :]).astype(jnp.bfloat16)
    key_clipped = (key_weight.astype(jnp.float32) * columns[None, :]).astype(jnp.bfloat16)
    return (
        output,
        input_grad,
        attn_gain_grad,
        moe_gain_grad,
        query_gain_grad,
        key_gain_grad,
        query_sum,
        key_sum,
        value_sum,
        out_sum.T,
        router_grad,
        gate_part[None],
        up_part[None],
        down_part[None],
        query_clipped,
        key_clipped,
        factors,
    )


def solution(mesh):
    placed = (
        P(("gx", "gy"), None),
        P(("gx", "gy"), None),
        P(("gx", "gy"), None),
        P("gx"),
        P(),
        P(),
        P(),
        P(),
        P(),
        P("gx", "gy"),
        P("gx", "gy"),
        P("gx", "gy"),
        P("gy", "gx"),
        P(),
        P(("gx", "gy"), None, None),
        P(("gx", "gy"), None, None),
        P(("gx", "gy"), None, None),
    )
    return jax.shard_map(
        local,
        mesh=mesh,
        in_specs=placed,
        out_specs=(
            P(("gx", "gy"), None),
            P(("gx", "gy"), None),
            P(),
            P(),
            P(),
            P(),
            P("gx", "gy"),
            P("gx", "gy"),
            P("gx", "gy"),
            P("gy", "gx"),
            P(),
            P(("gx", "gy"), None, None),
            P(("gx", "gy"), None, None),
            P(("gx", "gy"), None, None),
            P("gx", "gy"),
            P("gx", "gy"),
            P(),
        ),
        check_vma=False,
    )
```

```python
from functools import partial
from itertools import accumulate

import jax
import jax.numpy as jnp
from jax import lax
from jax.experimental import pallas as pl
from jax.experimental.pallas import tpu as pltpu
from jax.sharding import PartitionSpec as P

NH = 16
HD = 128
TOP = 8


EPSILON = 1e-06
NEGATIVE = -1e30


def flip(index):
    return index + 1 - 2 * (index % 2)


def barrier_with(partners):
    barrier = pltpu.get_barrier_semaphore()
    for ok, device in partners:
        @pl.when(ok)
        def _():
            pl.semaphore_signal(barrier, inc=1, device_id=device, device_id_type=pl.DeviceIdType.MESH)
    pl.semaphore_wait(barrier, sum(ok.astype(jnp.int32) for ok, _ in partners))

def always(ok, other):
    if ok is True:
        return other
    return ok if other is True else jnp.logical_and(ok, other)


def run_if(ok, action):
    if ok is True:
        action()
    else:
        pl.when(ok)(action)


def chain_gather(n_z, own_ref, out_ref, send_sem, recv_sem, local_sem):
    z = lax.axis_index("gx")
    g = lax.axis_index("gy")

    def hop(source, owner, k, peer):
        return pltpu.make_async_remote_copy(
            src_ref=source,
            dst_ref=out_ref.at[owner],
            send_sem=send_sem.at[k],
            recv_sem=recv_sem.at[owner],
            device_id={"gx": peer, "gy": g},
            device_id_type=pl.DeviceIdType.MESH,
        )

    local = pltpu.make_async_copy(own_ref, out_ref.at[z], local_sem)
    upward = [(z < n_z - 1, lambda: hop(own_ref, z, 0, z + 1))]
    downward = [(z > 0, lambda: hop(own_ref, z, n_z, z - 1))]
    for d in range(1, n_z - 1):
        upward.append(
            (
                jnp.logical_and(z >= d, z < n_z - 1),
                lambda d=d: hop(out_ref.at[z - d], z - d, d, z + 1),
            )
        )
        downward.append(
            (
                jnp.logical_and(z < n_z - d, z > 0),
                lambda d=d: hop(out_ref.at[z + d], z + d, n_z + d, z - 1),
            )
        )

    def start():
        local.start()
        for ok, copy in (upward[0], downward[0]):
            run_if(ok, lambda copy=copy: copy().start())

    def relay(d):
        run_if(z >= d, lambda: hop(own_ref, z - d, 0, z).wait_recv())
        if d < n_z - 1:
            run_if(upward[d][0], lambda: upward[d][1]().start())
        run_if(z < n_z - d, lambda: hop(own_ref, z + d, 0, z).wait_recv())
        if d < n_z - 1:
            run_if(downward[d][0], lambda: downward[d][1]().start())

    def finish():
        local.wait()
        for ok, copy in upward + downward:
            run_if(ok, lambda copy=copy: copy().wait_send())

    return start, [partial(relay, d) for d in range(1, n_z)], finish


def gather_steps(n_z, span, own_ref, out_ref, send_sem, recv_sem, local_sem):
    z = lax.axis_index("gx")
    g = lax.axis_index("gy")
    flip_x = g + 2 - 4 * ((g // 2) % 2)
    flip_y = g + 4 - 8 * ((g // 4) % 2)
    flip_both = flip_x + flip_y - g
    core = {"gx": z, "gy": flip(g)}
    x_peer = {"gx": z, "gy": flip_x}
    y_peer = {"gx": z, "gy": flip_y}
    above = {"gx": z + 1, "gy": g}
    below = {"gx": z - 1, "gy": g}
    first_z = z if n_z > 1 else 0
    sends = []

    def send(ok, b, h, peer, own=False):
        k = len(sends)

        def make():
            return pltpu.make_async_remote_copy(
                src_ref=own_ref.at[h] if own else out_ref.at[b, h],
                dst_ref=out_ref.at[b, h],
                send_sem=send_sem.at[k],
                recv_sem=recv_sem.at[b, h],
                device_id=peer,
                device_id_type=pl.DeviceIdType.MESH,
            )

        sends.append((ok, make))
        run_if(ok, lambda: make().start())

    def arrive(ok, b, h):
        def wait():
            pltpu.make_async_remote_copy(
                src_ref=out_ref.at[b, h],
                dst_ref=out_ref.at[b, h],
                send_sem=send_sem.at[0],
                recv_sem=recv_sem.at[b, h],
                device_id=core,
                device_id_type=pl.DeviceIdType.MESH,
            ).wait_recv()

        run_if(ok, wait)

    local = pltpu.make_async_copy(own_ref, out_ref.at[first_z * span + g], local_sem)
    items = [(True, first_z, 0)]
    for d in range(1, n_z):
        items += [(z >= d, z - d, -d), (z < n_z - d, z + d, d)]

    upward = [always(item[0], z < n_z - 1) for item in items]
    downward = [always(item[0], z > 0) for item in items]

    near_b = [owner * span + g for _, owner, _ in items]
    x_b = [owner * span + flip_x for _, owner, _ in items]
    y_b = [owner * span + flip_y for _, owner, _ in items]
    both_b = [owner * span + flip_both for _, owner, _ in items]

    def first(i):
        ok, _, d = items[i]
        b = near_b[i]
        own = d == 0
        if own:
            local.start()
        else:
            arrive(ok, b, 0)
            arrive(ok, b, 1)
        for h in range(2):
            if n_z > 1 and d <= 0:
                send(upward[i], b, h, above, own)
            if n_z > 1 and d >= 0:
                send(downward[i], b, h, below, own)
        for h, peer in ((0, x_peer), (1, y_peer), (1, x_peer), (0, y_peer), (0, core), (1, core)):
            send(ok, b, h, peer, own)

    def second(i):
        ok = items[i][0]
        for b, h, peer in ((x_b[i], 0, y_peer), (y_b[i], 1, x_peer)):
            arrive(ok, b, h)
            send(ok, b, h, peer)
            send(ok, b, h, core)

    def third(i):
        ok = items[i][0]
        for b, h in ((both_b[i], 0), (both_b[i], 1), (y_b[i], 0), (x_b[i], 1)):
            arrive(ok, b, h)
            send(ok, b, h, core)

    n = len(items)

    def step(i):
        if i < n:
            first(i)
        if 1 <= i <= n:
            second(i - 1)
        if i >= 2:
            third(i - 2)

    def finish():
        for ok, owner, _ in items:
            for side in (g, flip_x, flip_y, flip_both):
                for h in range(2):
                    arrive(ok, owner * span + flip(side), h)
        local.wait()
        for ok, make in sends:
            run_if(ok, lambda make=make: make().wait_send())

    return [partial(step, i) for i in range(n + 2)], finish


def greet(n_z):
    z = lax.axis_index("gx")
    g = lax.axis_index("gy")
    peers = [
        (z >= 0, {"gx": z, "gy": g + bit - 2 * bit * ((g // bit) % 2)}) for bit in (1, 2, 4)
    ]
    if n_z > 1:
        peers += [(z < n_z - 1, {"gx": z + 1, "gy": g}), (z > 0, {"gx": z - 1, "gy": g})]
    barrier_with(peers)


def add_into(dst, parts, rows):
    step = min(rows, 32)

    @pl.loop(0, rows // step)
    def _(r):
        at = pl.ds(pl.multiple_of(r * step, step), step)
        if len(parts) == 2 and dst.dtype == jnp.bfloat16:
            dst[at, :] = parts[0][at, :] + parts[1][at, :]
        else:
            total = parts[0][at, :].astype(jnp.float32)
            for term in parts[1:]:
                total = total + term[at, :].astype(jnp.float32)
            dst[at, :] = total.astype(dst.dtype)


def scatter_kernel(chain, n_i, rows, part_ref, out_ref, held, from_core, from_a, from_b, from_z,
                   load_sem, core_send, a_send, b_send, z_send, core_recv, a_recv, b_recv, z_recv, beside=None, parts=None):
    z = lax.axis_index("gx"); g = lax.axis_index("gy")
    flip_x = g + 2 - 4 * ((g // 2) % 2)
    flip_y = g + 4 - 8 * ((g // 4) % 2)
    quads = (flip_x + flip_y - g, flip_x, flip_y, g)
    core = {"gx": z, "gy": flip(g)}
    xn = {"gx": z, "gy": flip_x}
    yn = {"gx": z, "gy": flip_y}
    every = z >= 0
    partners = [(every, core), (every, xn), (every, yn)]
    if chain:
        partners += [(every, {"gx": lax.rem(z + j, n_i), "gy": g}) for j in range(1, n_i)]
    if beside:
        n_z = lax.axis_size("gx")
        partners += [(z < n_z - 1, {"gx": z + 1, "gy": g}), (z > 0, {"gx": z - 1, "gy": g})]
    if parts is None:
        barrier_with(partners)
    if beside:
        beside[0]()
    mesh_id = pl.DeviceIdType.MESH

    def item(i):
        return lax.rem(z + n_i - 1 - i + n_i, n_i) if chain else i

    def block(it, gg):
        return part_ref.at[it, gg]

    def remote(src, dst, ssem, rsem, dev):
        return pltpu.make_async_remote_copy(src_ref=src, dst_ref=dst, send_sem=ssem, recv_sem=rsem, device_id=dev, device_id_type=mesh_id)

    def core_copy(i, q):
        it = item(i)
        return remote(block(it, flip(quads[q])), from_core.at[it, q], core_send.at[i, q], core_recv.at[it, q], core)

    def load(i, q):
        it = item(i)
        return pltpu.make_async_copy(block(it, quads[q]), held.at[it, q], load_sem.at[i, q])

    a_plan = ((0, 0, 0, xn), (0, 1, 0, yn), (1, 0, 1, xn), (2, 1, 1, yn))
    def a_copy(i, k):
        it = item(i)
        q, h, slot, dev = a_plan[k]
        return remote(held.at[it, q, h], from_a.at[it, h, slot], a_send.at[i, k], a_recv.at[it, h, slot], dev)

    b_plan = ((2, 0, yn), (1, 1, xn))
    def b_copy(i, h):
        it = item(i)
        q, _, dev = b_plan[h]
        return remote(held.at[it, q, h], from_b.at[it, h], b_send.at[i, h], b_recv.at[it, h], dev)

    def z_copy(i):
        it = item(i)
        return remote(held.at[it, 3], from_z.at[z], z_send.at[i], z_recv.at[z], {"gx": it, "gy": g})

    def z_arrival(i):
        it = item(i)
        return remote(held.at[it, 3], from_z.at[it], z_send.at[i], z_recv.at[it], core)

    def begin():
        for i in range(n_i):
            for q in range(4):
                core_copy(i, q).start()
                load(i, q).start()

    def stage_a(i):
        it = item(i)
        for q in range(4):
            load(i, q).wait()
            core_copy(i, q).wait_recv()
            for h in range(2):
                add_into(held.at[it, q, h], (held.at[it, q, h], from_core.at[it, q, h]), rows)
            for k in range(4):
                if a_plan[k][0] == q:
                    a_copy(i, k).start()

    def stage_b(i):
        it = item(i)
        for q, h, slot in ((2, 0, 0), (1, 1, 0), (3, 0, 1), (3, 1, 1)):
            remote(held.at[it, q, h], from_a.at[it, h, slot], a_send.at[i, 0], a_recv.at[it, h, slot], core).wait_recv()
            add_into(held.at[it, q, h], (held.at[it, q, h], from_a.at[it, h, slot]), rows)
            if slot == 0:
                b_copy(i, h).start()

    def stage_c(i):
        it = item(i)
        for h in range(2):
            b_copy(i, h).wait_recv()
            if chain:
                add_into(held.at[it, 3, h], (held.at[it, 3, h], from_b.at[it, h]), rows)
            else:
                add_into(out_ref.at[it, h], (held.at[it, 3, h], from_b.at[it, h]), rows)

    def stage_d(i):
        if i < n_i - 1:
            z_copy(i).start()
        else:
            for j in range(n_i - 1):
                z_arrival(j).wait_recv()
            for h in range(2):
                add_into(
                    out_ref.at[h],
                    [held.at[item(i), 3, h]] + [from_z.at[item(j), h] for j in range(n_i - 1)],
                    rows,
                )

    def step(i):
        if i < n_i:
            stage_a(i)
        if 0 <= i - 1 < n_i:
            stage_b(i - 1)
        if 0 <= i - 2 < n_i:
            stage_c(i - 2)
        if chain and 0 <= i - 2 < n_i:
            stage_d(i - 2)

    def finish():
        for i in range(n_i):
            for q in range(4):
                core_copy(i, q).wait_send()
            for k in range(4):
                a_copy(i, k).wait_send()
            for h in range(2):
                b_copy(i, h).wait_send()
            if chain and i < n_i - 1:
                z_copy(i).wait_send()

    if parts is not None:
        parts.extend([begin] + [partial(step, i) for i in range(n_i + 2)] + [finish])
        return
    begin()
    for i in range(n_i + 2):
        step(i)
        if beside and i == n_i:
            beside[1][0]()
    if beside:
        for relay in beside[1][1:]:
            relay()
        beside[2]()
    finish()


def sum_steps(n_z, bits, vec_ref, out_ref, held, arrived, from_z, send_sem, z_send, recv_sem, z_recv):
    z = lax.axis_index("gx")
    g = lax.axis_index("gy")
    side = lax.rem(g, 2)
    peers = [
        {"gx": z, "gy": g + bit - 2 * bit * ((g // bit) % 2)}
        for bit in (2**power for power in range(bits))
    ]
    others = [{"gx": lax.rem(z + j, n_z), "gy": g} for j in range(1, n_z)]

    def remote(src, dst, ssem, rsem, peer):
        return pltpu.make_async_remote_copy(
            src_ref=src,
            dst_ref=dst,
            send_sem=ssem,
            recv_sem=rsem,
            device_id=peer,
            device_id_type=pl.DeviceIdType.MESH,
        )

    def hop(k):
        source = vec_ref.at[1 - side] if k == 0 else held.at[k - 1]
        return remote(source, arrived.at[k], send_sem.at[k], recv_sem.at[k], peers[k])

    def across(j):
        return remote(held.at[bits - 1], from_z.at[j], z_send.at[j], z_recv.at[j], others[j])

    def back():
        return remote(held.at[bits], arrived.at[bits], send_sem.at[bits], recv_sem.at[bits], peers[0])

    def onward(k):
        hop(k).wait()
        held[k] = (vec_ref[side] if k == 0 else held[k - 1]) + arrived[k]
        if k + 1 < bits:
            hop(k + 1).start()
        else:
            for j in range(n_z - 1):
                across(j).start()

    def gather():
        for j in range(n_z - 1):
            across(j).wait()
        total = jnp.zeros_like(held[0])
        for owner in range(n_z):
            term = held[bits - 1]
            for j in range(1, n_z):
                term = jnp.where(lax.rem(z - j + n_z, n_z) == owner, from_z[j - 1], term)
            total = total + term
        held[bits] = total
        back().start()
        out_ref[side] = total

    def finish():
        back().wait()
        out_ref[1 - side] = arrived[bits]

    return [lambda: hop(0).start()] + [partial(onward, k) for k in range(bits)] + [gather, finish]


def sum_kernel(n_z, bits, *refs):
    z = lax.axis_index("gx")
    g = lax.axis_index("gy")
    peers = [
        {"gx": z, "gy": g + bit - 2 * bit * ((g // bit) % 2)}
        for bit in (2**power for power in range(bits))
    ]
    peers += [{"gx": lax.rem(z + j, n_z), "gy": g} for j in range(1, n_z)]
    barrier_with([(z >= 0, peer) for peer in peers])
    for step in sum_steps(n_z, bits, *refs):
        step()


def folded(vector):
    rows = -(-vector.shape[0] // (128 * 16)) * 8
    return jnp.pad(vector, (0, 2 * rows * 128 - vector.shape[0])).reshape(2, rows, 128)


def sum_scratch(n_z, bits, rows):
    dma = pltpu.SemaphoreType.DMA
    return [
        pltpu.VMEM((bits + 1, rows, 128), jnp.float32),
        pltpu.VMEM((bits + 1, rows, 128), jnp.float32),
        pltpu.VMEM((n_z - 1, rows, 128), jnp.float32),
        dma((bits + 1,)),
        dma((n_z - 1,)),
        dma((bits + 1,)),
        dma((n_z - 1,)),
    ]


def sum_everywhere(vector, collective_id):
    n_z = lax.axis_size("gx")
    bits = lax.axis_size("gy").bit_length() - 1
    halves = folded(vector)
    out = pl.pallas_call(
        partial(sum_kernel, n_z, bits),
        out_shape=jax.ShapeDtypeStruct(halves.shape, jnp.float32),
        in_specs=[pl.BlockSpec(memory_space=pltpu.VMEM)],
        out_specs=pl.BlockSpec(memory_space=pltpu.VMEM),
        scratch_shapes=sum_scratch(n_z, bits, halves.shape[1]),
        compiler_params=pltpu.CompilerParams(collective_id=collective_id, has_side_effects=True),
        name="sum_everywhere",
    )(halves)
    return out.reshape(-1)[: vector.shape[0]]


def chain_scatter(n_z, part_ref, out_ref, from_low, from_high, send_sem, low_recv, high_recv):
    z = lax.axis_index("gx")
    g = lax.axis_index("gy")
    rows = part_ref.shape[1]

    def up(dest):
        return pltpu.make_async_remote_copy(
            src_ref=part_ref.at[dest],
            dst_ref=from_low.at[dest],
            send_sem=send_sem.at[dest],
            recv_sem=low_recv.at[dest],
            device_id={"gx": z + 1, "gy": g},
            device_id_type=pl.DeviceIdType.MESH,
        )

    def down(dest):
        return pltpu.make_async_remote_copy(
            src_ref=part_ref.at[dest],
            dst_ref=from_high.at[dest],
            send_sem=send_sem.at[dest],
            recv_sem=high_recv.at[dest],
            device_id={"gx": z - 1, "gy": g},
            device_id_type=pl.DeviceIdType.MESH,
        )

    def start():
        for k in range(n_z - 1):
            run_if(z == 0, lambda k=k: up(n_z - 1 - k).start())
            run_if(z == n_z - 1, lambda k=k: down(k).start())

    def pass_up(dest):
        up(dest).wait_recv()
        add_into(part_ref.at[dest], (part_ref.at[dest], from_low.at[dest]), rows)
        up(dest).start()

    def pass_down(dest):
        down(dest).wait_recv()
        add_into(part_ref.at[dest], (part_ref.at[dest], from_high.at[dest]), rows)
        down(dest).start()

    def relay(time):
        for k in range(time):
            low, dest = time - k, n_z - 1 - k
            if 0 < low < dest:
                run_if(z == low, partial(pass_up, dest))
            high, dest = n_z - 1 - (time - k), k
            if dest < high < n_z - 1:
                run_if(z == high, partial(pass_down, dest))

    def finish():
        for dest in range(n_z):
            terms = [part_ref.at[dest]]
            terms += [from_low.at[dest]] if dest > 0 else []
            terms += [from_high.at[dest]] if dest < n_z - 1 else []

            def last(dest=dest, terms=terms):
                if dest > 0:
                    up(dest).wait_recv()
                if dest < n_z - 1:
                    down(dest).wait_recv()
                add_into(out_ref, terms, rows)

            run_if(z == dest, last)
        for dest in range(n_z):
            run_if(z != dest, lambda dest=dest: up(dest).wait_send())

    return start, [partial(relay, time) for time in range(1, n_z)], finish


def expert_kernel(n_z, span, own_ref, cot_ref, share_ref, gate_ref, up_ref, down_ref,
                  all_ref, pair_ref, dots_ref, down_out, out_ref,
                  moe_buf, cot_buf, share_buf, pair_stage, dots_buf,
                  gate_val, up_val, scaled, scaled_t, down_t,
                  held, from_core, from_a, from_b, from_z,
                  send_sem, recv_sem, local_sem, fetch_sem, store_sem,
                  core_send, a_send, b_send, z_send, core_recv, a_recv, b_recv, z_recv,
                  shares_in, dots_own, share_send, share_recv, dots_send, dots_recv):
    z = lax.axis_index("gx")
    g = lax.axis_index("gy")
    rows = own_ref.shape[1]
    block = 2 * rows
    step_rows = moe_buf.shape[1]
    steps = 2 * n_z
    flip_x = g + 2 - 4 * ((g // 2) % 2)
    flip_y = g + 4 - 8 * ((g // 4) % 2)
    flip_both = flip_x + flip_y - g
    core = {"gx": z, "gy": flip(g)}
    x_peer = {"gx": z, "gy": flip_x}
    y_peer = {"gx": z, "gy": flip_y}
    above = {"gx": z + 1, "gy": g}
    below = {"gx": z - 1, "gy": g}

    order = [z]
    candidates = []
    for d in range(1, n_z):
        candidates += [(z >= d, z - d), (z < n_z - d, z + d)]
    for k in range(1, n_z):
        rank, chosen = 0, 0
        for ok, owner in candidates:
            ok = ok.astype(jnp.int32)
            rank = rank + ok
            chosen = chosen + ok * (rank == k).astype(jnp.int32) * owner
        order.append(chosen)

    onward = [(z < n_z - 1, z > 0)]
    for owner in order[1:]:
        onward.append(
            (
                jnp.logical_and(owner < z, z < n_z - 1),
                jnp.logical_and(owner > z, z > 0),
            )
        )
    devices = n_z * span
    rank = z * span + g

    def device(number):
        return {"gx": lax.div(number, span), "gy": lax.rem(number, span)}

    barrier = pltpu.get_barrier_semaphore()

    @pl.loop(1, devices)
    def _(j):
        pl.semaphore_signal(
            barrier,
            inc=1,
            device_id=device(lax.rem(rank + j, devices)),
            device_id_type=pl.DeviceIdType.MESH,
        )

    pl.semaphore_wait(barrier, devices - 1)

    def share_copy(number):
        return pltpu.make_async_remote_copy(
            src_ref=share_ref.at[number],
            dst_ref=shares_in.at[rank],
            send_sem=share_send.at[number],
            recv_sem=share_recv.at[rank],
            device_id=device(number),
            device_id_type=pl.DeviceIdType.MESH,
        )

    def share_arrival(number):
        return pltpu.make_async_remote_copy(
            src_ref=share_ref.at[number],
            dst_ref=shares_in.at[number],
            send_sem=share_send.at[number],
            recv_sem=share_recv.at[number],
            device_id=core,
            device_id_type=pl.DeviceIdType.MESH,
        )

    def dots_copy(number):
        return pltpu.make_async_remote_copy(
            src_ref=dots_own.at[number],
            dst_ref=dots_ref.at[rank],
            send_sem=dots_send.at[number],
            recv_sem=dots_recv.at[rank],
            device_id=device(number),
            device_id_type=pl.DeviceIdType.MESH,
        )

    def dots_arrival(number):
        return pltpu.make_async_remote_copy(
            src_ref=dots_own.at[number],
            dst_ref=dots_ref.at[number],
            send_sem=dots_send.at[number],
            recv_sem=dots_recv.at[number],
            device_id=core,
            device_id_type=pl.DeviceIdType.MESH,
        )

    def for_others(action):
        @pl.loop(1, devices)
        def _(j):
            action(lax.rem(rank + j, devices))

    for_others(lambda number: share_copy(number).start())
    shares_in[rank] = share_ref[rank]

    def at(owner, gg, h):
        return pl.ds(pl.multiple_of((owner * span + gg) * block + h * rows, rows), rows)

    def copy(k, slot, owner, gg, h, peer, own=False):
        return pltpu.make_async_remote_copy(
            src_ref=own_ref.at[h] if own else all_ref.at[at(owner, gg, h)],
            dst_ref=all_ref.at[at(owner, gg, h)],
            send_sem=send_sem.at[k, slot],
            recv_sem=recv_sem.at[owner * span + gg, h],
            device_id=peer,
            device_id_type=pl.DeviceIdType.MESH,
        )

    sends = []

    def send(ok, *where, **options):
        k = where[0]
        slot = sum(1 for entry in sends if entry[2] == k)
        make = partial(copy, k, slot, *where[1:], **options)
        sends.append((ok, make, k))
        run_if(ok, lambda: make().start())

    def arrive(owner, gg, h):
        copy(0, 0, owner, gg, h, core).wait_recv()

    locals_ = [
        pltpu.make_async_copy(own_ref.at[h], all_ref.at[at(z, g, h)], local_sem.at[h])
        for h in range(2)
    ]

    def first(k):
        owner = order[k]
        own = k == 0
        if own:
            for item in locals_:
                item.start()
        else:
            arrive(owner, g, 0)
            arrive(owner, g, 1)
        go_up, go_down = onward[k]
        for h in range(2):
            send(go_up, k, owner, g, h, above, own=own)
            send(go_down, k, owner, g, h, below, own=own)
        send(True, k, owner, g, 0, x_peer, own=own)
        send(True, k, owner, g, 1, y_peer, own=own)
        send(True, k, owner, g, 1, x_peer, own=own)
        send(True, k, owner, g, 0, y_peer, own=own)
        send(True, k, owner, g, 0, core, own=own)
        send(True, k, owner, g, 1, core, own=own)

    def second(k):
        owner = order[k]
        arrive(owner, flip_x, 0)
        send(True, k, owner, flip_x, 0, y_peer)
        send(True, k, owner, flip_x, 0, core)
        arrive(owner, flip_y, 1)
        send(True, k, owner, flip_y, 1, x_peer)
        send(True, k, owner, flip_y, 1, core)

    def third(k):
        owner = order[k]
        for gg, h in ((flip_y, 0), (flip_x, 1), (flip_both, 0), (flip_both, 1)):
            arrive(owner, gg, h)
            send(True, k, owner, gg, h, core)

    def complete(k):
        for gg in (g, flip_x, flip_y, flip_both):
            for h in range(2):
                arrive(order[k], flip(gg), h)
        if k == 0:
            for item in locals_:
                item.wait()

    def owner_of(s):
        if isinstance(s, int):
            return order[s // 2]
        k = lax.div(s, 2)
        return sum((k == j).astype(jnp.int32) * order[j] for j in range(n_z))

    def place(s):
        k, side = (s // 2, s % 2) if isinstance(s, int) else (lax.div(s, 2), lax.rem(s, 2))
        if isinstance(s, int):
            owner = order[k]
        else:
            owner = sum((k == j).astype(jnp.int32) * order[j] for j in range(n_z))
        return pl.ds(pl.multiple_of(owner * (span * block) + side * step_rows, step_rows), step_rows)

    def parity(s):
        return s % 2 if isinstance(s, int) else lax.rem(s, 2)

    def fetches(s):
        slot = parity(s)
        return [
            pltpu.make_async_copy(source.at[place(s)], target.at[slot], fetch_sem.at[j, slot])
            for j, (source, target) in enumerate(
                ((all_ref, moe_buf), (cot_ref, cot_buf))
            )
        ]

    def stores(s):
        slot = parity(s)
        return [
            pltpu.make_async_copy(
                pair_stage.at[slot], pair_ref.at[place(s)], store_sem.at[0, slot]
            )
        ]

    f32 = jnp.float32
    dot = partial(lax.dot_general, preferred_element_type=f32)
    plain = (((1,), (0,)), ((), ()))
    last_dims = (((1,), (1,)), ((), ()))
    first_dims = (((0,), (0,)), ((), ()))
    half_width = scaled.shape[1]
    width = moe_buf.shape[2]
    tile = 256

    quads = (flip_both, flip_x, flip_y, g)

    def remote(src, dst, ssem, rsem, peer):
        return pltpu.make_async_remote_copy(
            src_ref=src,
            dst_ref=dst,
            send_sem=ssem,
            recv_sem=rsem,
            device_id=peer,
            device_id_type=pl.DeviceIdType.MESH,
        )

    def core_copy(k, q):
        return remote(
            held.at[k, flip(quads[q])],
            from_core.at[k, q],
            core_send.at[k, q],
            core_recv.at[k, q],
            core,
        )

    a_plan = ((0, 0, 0, x_peer), (0, 1, 0, y_peer), (1, 0, 1, x_peer), (2, 1, 1, y_peer))

    def a_copy(k, j):
        q, h, slot, peer = a_plan[j]
        return remote(
            held.at[k, quads[q], h],
            from_a.at[k, h, slot],
            a_send.at[k, j],
            a_recv.at[k, h, slot],
            peer,
        )

    b_plan = ((2, y_peer), (1, x_peer))

    def b_copy(k, h):
        q, peer = b_plan[h]
        return remote(
            held.at[k, quads[q], h], from_b.at[k, h], b_send.at[k, h], b_recv.at[k, h], peer
        )

    def z_copy(k):
        return remote(
            held.at[k, g], from_z.at[z], z_send.at[k], z_recv.at[z], {"gx": order[k], "gy": g}
        )

    def stage_core(k):
        for q in range(4):
            core_copy(k, q).start()

    def stage_a(k):
        for q in range(4):
            core_copy(k, q).wait_recv()
            for h in range(2):
                mine = held.at[k, quads[q], h]
                add_into(mine, (mine, from_core.at[k, q, h]), rows)
            for j in range(4):
                if a_plan[j][0] == q:
                    a_copy(k, j).start()

    def stage_b(k):
        for q, h, slot in ((2, 0, 0), (1, 1, 0), (3, 0, 1), (3, 1, 1)):
            mine, arrived = held.at[k, quads[q], h], from_a.at[k, h, slot]
            remote(mine, arrived, a_send.at[k, 0], a_recv.at[k, h, slot], core).wait_recv()
            add_into(mine, (mine, arrived), rows)
            if slot == 0:
                b_copy(k, h).start()

    def stage_c(k):
        for h in range(2):
            b_copy(k, h).wait_recv()
            mine = held.at[k, g, h]
            add_into(mine, (mine, from_b.at[k, h]), rows)
        if k > 0:
            z_copy(k).start()

    backs = (
        (stage_core, lambda k: 2 * k + 1, 2),
        (stage_a, lambda k: 2 * k + 2, 2),
        (stage_b, lambda k: 2 * k + 3, 2),
        (stage_c, lambda k: 2 * k + 4, 1),
    )

    def events(s, phase):
        for action, start, when in backs:
            for k in range(n_z):
                if when == phase and start(k) < steps:
                    pl.when(s == start(k))(partial(action, k))
        for k in range(1, n_z):
            if k >= 2 and phase == 1:
                pl.when(s == k - 2)(partial(first, k))
            if phase == 2:
                pl.when(s == 2 * (k - 1))(partial(second, k))
            if phase == 2:
                pl.when(s == 2 * (k - 1) + 1)(partial(third, k))
            if phase == 4:
                pl.when(s == 2 * k - 1)(partial(complete, k))

    first(0)

    @pl.loop(0, width // tile)
    def _(t):
        cols = pl.ds(pl.multiple_of(t * tile, tile), tile)
        down_t[cols, :] = down_ref[:, cols].T

    second(0)
    if n_z > 1:
        first(1)
    third(0)
    complete(0)
    for item in fetches(0):
        item.start()
    for_others(lambda number: share_arrival(number).wait_recv())

    @pl.loop(0, steps)
    def _(s):
        slot = lax.rem(s, 2)
        moe, cot, share = moe_buf.at[slot], cot_buf.at[slot], share_buf
        first_device = owner_of(s) * span + slot * (span // 2)
        for item in fetches(s):
            item.wait()

        @pl.when(s >= 2)
        def _():
            for item in stores(s - 2):
                item.wait()

        for j in range(span // 2):
            column = jnp.broadcast_to(shares_in[first_device + j], (block, block)).T
            share[j * block : (j + 1) * block, :] = column
        wide = jnp.concatenate([share[...]] * (tile // share.shape[1]), axis=1)

        @pl.loop(0, half_width // tile)
        def _(t):
            cols = pl.ds(pl.multiple_of(t * tile, tile), tile)
            gated = dot(moe[...], gate_ref[:, cols], plain)
            lifted = dot(moe[...], up_ref[:, cols], plain)
            gate_val[:, cols] = gated
            up_val[:, cols] = lifted
            scaled[:, cols] = (gated * jax.nn.sigmoid(gated) * lifted * wide).astype(jnp.bfloat16)

        events(s, 1)
        scaled_t[...] = scaled[...].T

        @pl.loop(0, width // (2 * tile))
        def _(t):
            cols = pl.ds(pl.multiple_of(t * 2 * tile, 2 * tile), 2 * tile)
            sent = dot(scaled[...], down_ref[:, cols], plain).astype(jnp.bfloat16)
            held[lax.div(s, 2), pl.ds(slot * (span // 2), span // 2), :, :, cols] = sent.reshape(
                (span // 2, 2, rows, 2 * tile)
            )

        events(s, 2)
        dots_buf[...] = jnp.zeros(dots_buf.shape, f32)

        @pl.loop(0, half_width // tile)
        def _(t):
            cols = pl.ds(pl.multiple_of(t * tile, tile), tile)
            pulled = dot(cot[...], down_t[:, cols], plain)
            gated = gate_val[:, cols]
            lifted = up_val[:, cols]
            sig = jax.nn.sigmoid(gated)
            silu = gated * sig
            product = pulled * (silu * lifted)
            lanes = share.shape[1]
            dots_buf[...] = dots_buf[...] + sum(
                product[:, j * lanes : (j + 1) * lanes] for j in range(tile // lanes)
            )
            pulled = pulled * wide
            pair_stage[slot, :, cols] = (pulled * lifted * sig * (1.0 + gated * (1.0 - sig))).astype(
                jnp.bfloat16
            )
            more = pl.ds(pl.multiple_of(half_width + t * tile, tile), tile)
            pair_stage[slot, :, more] = (pulled * silu).astype(jnp.bfloat16)

        for item in stores(s):
            item.start()
        for j in range(span // 2):
            number = first_device + j
            rows_of = dots_buf[j * block : (j + 1) * block, :]
            dots_own[number] = jnp.sum(rows_of.T, axis=0, keepdims=True)

        for j in range(span // 2):
            number = first_device + j

            @pl.when(number != rank)
            def _():
                dots_copy(number).start()

        events(s, 3)
        events(s, 4)

        @pl.when(s < steps - 1)
        def _():
            for item in fetches(s + 1):
                item.start()

        @pl.loop(0, width // (2 * tile))
        def _(t):
            cols = pl.ds(pl.multiple_of(t * 2 * tile, 2 * tile), 2 * tile)
            grown = dot(scaled_t[...], cot[:, cols], plain)
            down_out[:, cols] = jnp.where(s == 0, 0.0, down_out[:, cols]) + grown

    for t in range(steps, 2 * steps):
        for action, start, _ in backs[::-1]:
            for k in range(n_z):
                if start(k) == t:
                    action(k)
    for s in (steps - 2, steps - 1):
        for item in stores(s):
            item.wait()
    for k in range(1, n_z):
        arrived = from_z.at[order[k]]
        remote(held.at[k, g], arrived, z_send.at[k], z_recv.at[order[k]], core).wait_recv()
    for h in range(2):
        terms = [held.at[0, g, h]] + [from_z.at[order[k], h] for k in range(1, n_z)]
        add_into(out_ref.at[h], terms, rows)
    for k in range(n_z):
        for q in range(4):
            core_copy(k, q).wait_send()
        for j in range(4):
            a_copy(k, j).wait_send()
        for h in range(2):
            b_copy(k, h).wait_send()
        if k > 0:
            z_copy(k).wait_send()
    for ok, make, k in sends:
        run_if(ok, lambda make=make: make().wait_send())
    dots_ref[rank] = dots_own[rank]
    for_others(lambda number: dots_arrival(number).wait_recv())
    for_others(lambda number: share_copy(number).wait_send())
    for_others(lambda number: dots_copy(number).wait_send())


def run_experts(moe_in, all_cot, shares, gate_w, up_w, down_w, collective_id):
    n_z = lax.axis_size("gx")
    span = lax.axis_size("gy")
    rows, width = moe_in.shape
    half = down_w.shape[0]
    total = n_z * span * rows
    step = span * rows // 2
    lanes = 128
    devices = n_z * span
    bf16, f32 = jnp.bfloat16, jnp.float32
    dma = pltpu.SemaphoreType.DMA
    vmem = pl.BlockSpec(memory_space=pltpu.VMEM)
    hbm = pl.BlockSpec(memory_space=pl.ANY)
    return pl.pallas_call(
        partial(expert_kernel, n_z, span),
        out_shape=(
            jax.ShapeDtypeStruct((total, width), bf16),
            jax.ShapeDtypeStruct((total, 2 * half), bf16),
            jax.ShapeDtypeStruct((devices, 1, rows), f32),
            jax.ShapeDtypeStruct((half, width), f32),
            jax.ShapeDtypeStruct((2, rows // 2, width), f32),
        ),
        in_specs=[vmem, hbm, vmem, vmem, vmem, vmem],
        out_specs=(hbm, hbm, vmem, vmem, vmem),
        scratch_shapes=[
            pltpu.VMEM((2, step, width), bf16),
            pltpu.VMEM((2, step, width), bf16),
            pltpu.VMEM((step, lanes), f32),
            pltpu.VMEM((2, step, 2 * half), bf16),
            pltpu.VMEM((step, lanes), f32),
            pltpu.VMEM((step, half), f32),
            pltpu.VMEM((step, half), f32),
            pltpu.VMEM((step, half), bf16),
            pltpu.VMEM((half, step), bf16),
            pltpu.VMEM((width, half), bf16),
            pltpu.VMEM((n_z, span, 2, rows // 2, width), bf16),
            pltpu.VMEM((n_z, 4, 2, rows // 2, width), bf16),
            pltpu.VMEM((n_z, 2, 2, rows // 2, width), bf16),
            pltpu.VMEM((n_z, 2, rows // 2, width), bf16),
            pltpu.VMEM((n_z, 2, rows // 2, width), bf16),
            dma((n_z, 18)),
            dma((n_z * span, 2)),
            dma((2,)),
            dma((3, 2)),
            dma((2, 2)),
            dma((n_z, 4)),
            dma((n_z, 4)),
            dma((n_z, 2)),
            dma((n_z,)),
            dma((n_z, 4)),
            dma((n_z, 2, 2)),
            dma((n_z, 2)),
            dma((n_z,)),
            pltpu.VMEM((devices, 1, rows), f32),
            pltpu.VMEM((devices, 1, rows), f32),
            dma((devices,)),
            dma((devices,)),
            dma((devices,)),
            dma((devices,)),
        ],
        compiler_params=pltpu.CompilerParams(
            collective_id=collective_id, has_side_effects=True, vmem_limit_bytes=67043328
        ),
        name="experts",
    )(moe_in.reshape(2, rows // 2, width), all_cot, shares, gate_w, up_w, down_w)


def pull_kernel(n_i, rows, all_ref, pair_ref, gate_ref, up_ref, out_ref, gate_out, up_out,
                held, from_core, from_a, from_b, from_z, moe_buf, pair_buf,
                fetch_sem, core_send, a_send, b_send, z_send, core_recv, a_recv, b_recv, z_recv):
    z = lax.axis_index("gx")
    g = lax.axis_index("gy")
    flip_x = g + 2 - 4 * ((g // 2) % 2)
    flip_y = g + 4 - 8 * ((g // 4) % 2)
    quads = (flip_x + flip_y - g, flip_x, flip_y, g)
    core = {"gx": z, "gy": flip(g)}
    x_peer = {"gx": z, "gy": flip_x}
    y_peer = {"gx": z, "gy": flip_y}
    along = [{"gx": lax.rem(z + j, n_i), "gy": g} for j in range(1, n_i)]
    barrier_with([(z >= 0, peer) for peer in (core, x_peer, y_peer, *along)])
    item_rows = moe_buf.shape[1]
    width = moe_buf.shape[2]
    half_width = gate_out.shape[1]
    owners = [lax.rem(z + n_i - 1 - i + n_i, n_i) for i in range(n_i)]

    def remote(src, dst, ssem, rsem, peer):
        return pltpu.make_async_remote_copy(
            src_ref=src,
            dst_ref=dst,
            send_sem=ssem,
            recv_sem=rsem,
            device_id=peer,
            device_id_type=pl.DeviceIdType.MESH,
        )

    def fetches(i):
        place = pl.ds(pl.multiple_of(owners[i] * item_rows, item_rows), item_rows)
        return [
            pltpu.make_async_copy(all_ref.at[place], moe_buf.at[i % 2], fetch_sem.at[0, i % 2]),
            pltpu.make_async_copy(pair_ref.at[place], pair_buf.at[i % 2], fetch_sem.at[1, i % 2]),
        ]

    def core_copy(i, q):
        return remote(
            held.at[i, flip(quads[q])],
            from_core.at[i, q],
            core_send.at[i, q],
            core_recv.at[i, q],
            core,
        )

    a_plan = ((0, 0, 0, x_peer), (0, 1, 0, y_peer), (1, 0, 1, x_peer), (2, 1, 1, y_peer))

    def a_copy(i, k):
        q, h, slot, peer = a_plan[k]
        return remote(
            held.at[i, quads[q], h],
            from_a.at[i, h, slot],
            a_send.at[i, k],
            a_recv.at[i, h, slot],
            peer,
        )

    b_plan = ((2, y_peer), (1, x_peer))

    def b_copy(i, h):
        q, peer = b_plan[h]
        return remote(
            held.at[i, quads[q], h], from_b.at[i, h], b_send.at[i, h], b_recv.at[i, h], peer
        )

    def z_copy(i):
        return remote(
            held.at[i, g], from_z.at[z], z_send.at[i], z_recv.at[z], {"gx": owners[i], "gy": g}
        )

    dot = partial(lax.dot_general, preferred_element_type=jnp.float32)
    last_dims = (((1,), (1,)), ((), ()))
    first_dims = (((0,), (0,)), ((), ()))

    def multiply(i):
        for copy in fetches(i):
            copy.wait()
        pair = pair_buf.at[i % 2]
        tile = 256

        @pl.loop(0, width // tile)
        def _(t):
            cols = pl.ds(pl.multiple_of(t * tile, tile), tile)
            total = dot(pair[:, :half_width], gate_ref[cols, :], last_dims)
            total = total + dot(pair[:, half_width:], up_ref[cols, :], last_dims)
            held[i, :, :, :, cols] = total.astype(jnp.bfloat16).reshape(held.shape[1:4] + (tile,))

        for q in range(4):
            core_copy(i, q).start()

    def accumulate(i):
        moe, pair = moe_buf.at[i % 2], pair_buf.at[i % 2]
        tile = 256

        @pl.loop(0, width // tile)
        def _(t):
            cols = pl.ds(pl.multiple_of(t * tile, tile), tile)
            grown = dot(moe[:, cols], pair[...], first_dims)
            if i == 0:
                gate_out[cols, :] = grown[:, :half_width]
                up_out[cols, :] = grown[:, half_width:]
            else:
                gate_out[cols, :] = gate_out[cols, :] + grown[:, :half_width]
                up_out[cols, :] = up_out[cols, :] + grown[:, half_width:]

        if i + 2 < n_i:
            for copy in fetches(i + 2):
                copy.start()

    def stage_a(i):
        for q in range(4):
            core_copy(i, q).wait_recv()
            for h in range(2):
                mine = held.at[i, quads[q], h]
                add_into(mine, (mine, from_core.at[i, q, h]), rows)
            for k in range(4):
                if a_plan[k][0] == q:
                    a_copy(i, k).start()

    def stage_b(i):
        for q, h, slot in ((2, 0, 0), (1, 1, 0), (3, 0, 1), (3, 1, 1)):
            mine, arrived = held.at[i, quads[q], h], from_a.at[i, h, slot]
            remote(mine, arrived, a_send.at[i, 0], a_recv.at[i, h, slot], core).wait_recv()
            add_into(mine, (mine, arrived), rows)
            if slot == 0:
                b_copy(i, h).start()

    def stage_c(i):
        for h in range(2):
            b_copy(i, h).wait_recv()
            mine = held.at[i, g, h]
            add_into(mine, (mine, from_b.at[i, h]), rows)
        if i < n_i - 1:
            z_copy(i).start()
        else:
            for j in range(n_i - 1):
                arrived = from_z.at[owners[j]]
                remote(held.at[j, g], arrived, z_send.at[j], z_recv.at[owners[j]], core).wait_recv()
            for h in range(2):
                terms = [held.at[i, g, h]] + [from_z.at[owners[j], h] for j in range(n_i - 1)]
                add_into(out_ref.at[h], terms, rows)

    for i in range(min(2, n_i)):
        for copy in fetches(i):
            copy.start()
    for t in range(n_i + 3):
        if t < n_i:
            multiply(t)
        if 0 <= t - 1 < n_i:
            stage_a(t - 1)
        if 0 <= t - 2 < n_i:
            stage_b(t - 2)
        if 0 <= t - 1 < n_i:
            accumulate(t - 1)
        if 0 <= t - 3 < n_i:
            stage_c(t - 3)
    for i in range(n_i):
        for q in range(4):
            core_copy(i, q).wait_send()
        for k in range(4):
            a_copy(i, k).wait_send()
        for h in range(2):
            b_copy(i, h).wait_send()
        if i < n_i - 1:
            z_copy(i).wait_send()


def pull_experts(all_moe, pair, gate_w, up_w, collective_id):
    n_i = lax.axis_size("gx")
    span = lax.axis_size("gy")
    total, width = all_moe.shape
    half_width = gate_w.shape[1]
    rows = total // (n_i * span) // 2
    half = (rows, width)
    bf16 = jnp.bfloat16
    dma = pltpu.SemaphoreType.DMA
    vmem = pl.BlockSpec(memory_space=pltpu.VMEM)
    hbm = pl.BlockSpec(memory_space=pl.ANY)
    out, gate_part, up_part = pl.pallas_call(
        partial(pull_kernel, n_i, rows),
        out_shape=(
            jax.ShapeDtypeStruct((2,) + half, jnp.float32),
            jax.ShapeDtypeStruct((width, half_width), jnp.float32),
            jax.ShapeDtypeStruct((width, half_width), jnp.float32),
        ),
        in_specs=[hbm, hbm, vmem, vmem],
        out_specs=(vmem, vmem, vmem),
        scratch_shapes=[
            pltpu.VMEM((n_i, span, 2) + half, bf16),
            pltpu.VMEM((n_i, 4, 2) + half, bf16),
            pltpu.VMEM((n_i, 2, 2) + half, bf16),
            pltpu.VMEM((n_i, 2) + half, bf16),
            pltpu.VMEM((n_i, 2) + half, bf16),
            pltpu.VMEM((2, span * 2 * rows, width), bf16),
            pltpu.VMEM((2, span * 2 * rows, 2 * half_width), bf16),
            dma((2, 2)),
            dma((n_i, 4)),
            dma((n_i, 4)),
            dma((n_i, 2)),
            dma((n_i,)),
            dma((n_i, 4)),
            dma((n_i, 2, 2)),
            dma((n_i, 2)),
            dma((n_i,)),
        ],
        compiler_params=pltpu.CompilerParams(
            collective_id=collective_id, has_side_effects=True, vmem_limit_bytes=67043328
        ),
        name="pull_experts",
    )(all_moe, pair, gate_w, up_w)
    return out.reshape(2 * rows, width), gate_part, up_part


def turn(values, cosine, sine):
    return values * cosine + pltpu.roll(values, values.shape[-1] // 2, 1) * sine


def spread_docs(docs_ref, row_docs, col_docs):
    lanes = docs_ref.shape[1]
    for j in range(docs_ref.shape[0]):
        line = docs_ref[j : j + 1, :].astype(jnp.float32)
        row_docs[j * lanes : (j + 1) * lanes, :] = jnp.broadcast_to(line, (lanes, lanes)).T
        col_docs[:, j * lanes : (j + 1) * lanes] = jnp.broadcast_to(line, (8, lanes))


def attend_kernel(
    heads,
    pieces,
    own_acts,
    query_weight,
    key_weight,
    value_weight,
    own_out_weight,
    own_cot,
    query_gain,
    key_gain,
    cosine_ref,
    sine_ref,
    docs_ref,
    attended_ref,
    acts_out,
    weight_out,
    full_out,
    all_cot,
    query_raw,
    key_raw,
    ready_ref,
    mixed_ref,
    totals_ref,
    peaks_ref,
    own_weight,
    row_docs,
    col_docs,
    part_ref,
    held,
    from_core,
    from_a,
    from_b,
    from_z,
    near_send,
    near_recv,
    near_local,
    far_send,
    far_recv,
    far_local,
    in_send,
    in_recv,
    in_local,
    out_send,
    out_recv,
    out_local,
    load_sem,
    core_send,
    a_send,
    b_send,
    z_send,
    core_recv,
    a_recv,
    b_recv,
    z_recv,
):
    n_z = lax.axis_size("gx")
    span = lax.axis_size("gy")
    for j, item in enumerate((query_weight, key_weight, value_weight)):
        own_weight[:, j * item.shape[1] : (j + 1) * item.shape[1]] = item[...]
    greet(n_z)
    in_start, in_relays, in_finish = chain_gather(
        n_z, own_weight, weight_out, in_send, in_recv, in_local
    )
    out_start, out_relays, out_finish = chain_gather(
        n_z, own_out_weight, full_out, out_send, out_recv, out_local
    )
    near, near_finish = gather_steps(1, span, own_acts, acts_out, near_send, near_recv, near_local)
    far, far_finish = gather_steps(n_z, span, own_cot, all_cot, far_send, far_recv, far_local)
    back = []
    scatter_kernel(
        False,
        pieces,
        part_ref.shape[3],
        part_ref,
        attended_ref,
        held,
        from_core,
        from_a,
        from_b,
        from_z,
        load_sem,
        core_send,
        a_send,
        b_send,
        z_send,
        core_recv,
        a_recv,
        b_recv,
        z_recv,
        parts=back,
    )
    f32, bf16 = jnp.float32, jnp.bfloat16
    dot = partial(lax.dot_general, preferred_element_type=f32)
    plain = (((1,), (0,)), ((), ()))
    last_dims = (((1,), (1,)), ((), ()))
    length = query_raw.shape[0]
    width = acts_out.shape[3]
    local = heads * HD
    block = 256
    scale = HD ** (-0.5)

    in_start()
    near[0]()
    far[0]()
    spread_docs(docs_ref, row_docs, col_docs)
    near[1]()
    near[2]()
    later = far[1:]
    for relay in in_relays:
        relay()
        for step in later[:1]:
            step()
        later = later[1:]
    out_start()
    in_finish()
    near_finish()
    waiting = [list(out_relays), list(later)]

    def pull(which):
        if waiting[which]:
            waiting[which].pop(0)()

    def project(source):
        cols = slice(source * local, (source + 1) * local)
        acts = acts_out[...].reshape(length, width)
        total = jnp.zeros((length, local), f32)
        depth = own_weight.shape[0]
        for owner in range(n_z):
            total = total + dot(
                acts[:, owner * depth : (owner + 1) * depth], weight_out[owner, :, cols], plain
            )
        return total

    for source, raw, gain in ((0, query_raw, query_gain), (1, key_raw, key_gain)):
        raw[...] = project(source)
        for h in range(heads):
            cols = slice(h * HD, (h + 1) * HD)

            @pl.loop(0, length // block)
            def _(t):
                at = pl.ds(pl.multiple_of(t * block, block), block)
                value = raw[at, cols]
                normed = value * lax.rsqrt(jnp.mean(value * value, axis=-1, keepdims=True) + EPSILON)
                turned = turn(normed * gain[...], cosine_ref[at, :], sine_ref[at, :])
                where = source * local + h * HD
                ready_ref[at, where : where + HD] = turned.astype(bf16)

        pull(source)

    ready_ref[:, 2 * local :] = project(2).astype(bf16)
    pull(0)
    lanes = lax.broadcasted_iota(jnp.int32, (block, HD), 1)
    peaks_ref[...] = jnp.full(peaks_ref.shape, NEGATIVE, f32)

    def mix(t):
        at = pl.ds(pl.multiple_of(t * block, block), block)
        same = row_docs[at, :1] == col_docs[:1, :]
        kept = jnp.zeros((block, HD), f32)
        for h in range(heads):
            query = ready_ref[at, h * HD : (h + 1) * HD]
            key = ready_ref[:, local + h * HD : local + (h + 1) * HD]
            value = ready_ref[:, 2 * local + h * HD : 2 * local + (h + 1) * HD]
            scores = jnp.where(same, dot(query, key, last_dims) * scale, NEGATIVE)
            highest = jnp.max(scores, axis=-1, keepdims=True)
            weights = jnp.exp(scores - highest)
            total = jnp.sum(weights, axis=-1, keepdims=True)
            shares = (weights * (1.0 / total)).astype(bf16)
            mixed_ref[at, h * HD : (h + 1) * HD] = dot(shares, value, plain).astype(bf16)
            kept = jnp.where(lanes == h, highest + jnp.log(total), kept)
            top = jnp.max(highest, axis=0, keepdims=True)
            peaks_ref[h : h + 1, :] = jnp.maximum(peaks_ref[h : h + 1, :], top)
        totals_ref[at, :] = kept

    blocks = length // block
    between = waiting[1].pop(0) if waiting[1] else lambda: None

    @pl.loop(0, blocks)
    def _(t):
        mix(t)
        pl.when(t == blocks // 2 - 1)(between)

    pull(1)
    for relay in waiting[0]:
        relay()
    out_finish()
    rows = part_ref.shape[3]
    per_owner = own_out_weight.shape[1] // block

    @pl.loop(0, n_z * per_owner)
    def _(t):
        cols = pl.ds(pl.multiple_of(t * block, block), block)
        inside = pl.ds(pl.multiple_of(lax.rem(t, per_owner) * block, block), block)
        sent = dot(mixed_ref[...], full_out[lax.div(t, per_owner), :, inside], plain).astype(bf16)
        sent = sent.reshape(span, pieces, 2, rows, block)
        for p in range(pieces):
            part_ref[p, :, :, :, cols] = sent[:, p]

    for step in back[:-1]:
        step()
        pull(1)
    for step in waiting[1]:
        step()
    back[-1]()
    far_finish()


def attend(
    acts, weights, out_weight, cot, query_gain, key_gain, tables, docs, collective_id, pieces=4
):
    tokens, width = acts.shape
    depth, local = weights[0].shape
    heads = local // HD
    n_z = lax.axis_size("gx")
    span = lax.axis_size("gy")
    length = span * tokens
    rows = tokens // (pieces * 2)
    half = (2, tokens // 2, width)
    piece = (rows, width)
    f32, bf16 = jnp.float32, jnp.bfloat16
    dma = pltpu.SemaphoreType.DMA
    vmem = pl.BlockSpec(memory_space=pltpu.VMEM)
    hbm = pl.BlockSpec(memory_space=pl.ANY)
    attended, seq, full, full_out, all_cot, *saved, peaks = pl.pallas_call(
        partial(attend_kernel, heads, pieces),
        out_shape=(
            jax.ShapeDtypeStruct((pieces, 2) + piece, f32),
            jax.ShapeDtypeStruct((span,) + half, bf16),
            jax.ShapeDtypeStruct((n_z, depth, 3 * local), bf16),
            jax.ShapeDtypeStruct((n_z,) + out_weight.shape, bf16),
            jax.ShapeDtypeStruct((n_z * span,) + half, bf16),
            jax.ShapeDtypeStruct((length, local), f32),
            jax.ShapeDtypeStruct((length, local), f32),
            jax.ShapeDtypeStruct((length, 3 * local), bf16),
            jax.ShapeDtypeStruct((length, local), bf16),
            jax.ShapeDtypeStruct((length, HD), f32),
            jax.ShapeDtypeStruct((8, HD), f32),
        ),
        in_specs=[vmem] * 11,
        out_specs=(vmem, vmem, vmem, vmem, hbm) + (vmem,) * 6,
        scratch_shapes=[
            pltpu.VMEM((depth, 3 * local), bf16),
            pltpu.VMEM((length, 128), f32),
            pltpu.VMEM((8, length), f32),
            pltpu.VMEM((pieces, span, 2) + piece, bf16),
            pltpu.VMEM((pieces, 4, 2) + piece, bf16),
            pltpu.VMEM((pieces, 4, 2) + piece, bf16),
            pltpu.VMEM((pieces, 2, 2) + piece, bf16),
            pltpu.VMEM((pieces, 2) + piece, bf16),
            pltpu.VMEM((1, 2, 16, 128), bf16),
            dma((24,)),
            dma((span, 2)),
            dma,
            dma((24 * (2 * n_z - 1),)),
            dma((n_z * span, 2)),
            dma,
            dma((2 * n_z,)),
            dma((n_z,)),
            dma,
            dma((2 * n_z,)),
            dma((n_z,)),
            dma,
            dma((pieces, 4)),
            dma((pieces, 4)),
            dma((pieces, 4)),
            dma((pieces, 2)),
            dma((pieces,)),
            dma((pieces, 4)),
            dma((pieces, 2, 2)),
            dma((pieces, 2)),
            dma((pieces,)),
        ],
        compiler_params=pltpu.CompilerParams(
            collective_id=collective_id, has_side_effects=True, vmem_limit_bytes=60 << 20
        ),
        name="attend",
    )(
        acts.reshape(half),
        *weights,
        out_weight,
        cot.reshape(half),
        query_gain.reshape(1, HD),
        key_gain.reshape(1, HD),
        *tables,
        docs,
    )
    return (
        attended.reshape(tokens, width),
        seq.reshape(length, width),
        full.reshape(n_z * depth, 3 * local),
        all_cot.reshape(n_z * span * tokens, width),
        (*saved, full_out),
        peaks,
    )


def attend_back_kernel(
    heads,
    pieces,
    own_grad,
    out_weight_ref,
    mixed_ref,
    ready_ref,
    query_raw,
    key_raw,
    totals_ref,
    query_gain,
    key_gain,
    cosine_ref,
    sine_ref,
    docs_ref,
    small_ref,
    acts_hbm,
    weight_hbm,
    grad_acts,
    weight_sum,
    out_sum,
    gain_ref,
    small_sum,
    row_docs,
    col_docs,
    seq_ref,
    part_ref,
    acts_ref,
    weight_ref,
    grad_mixed,
    grad_heads,
    one_head,
    turned,
    key_sum,
    value_sum,
    out_sums,
    out_low,
    out_high,
    in_sums,
    in_low,
    in_high,
    held,
    from_core,
    from_a,
    from_b,
    from_z,
    copy_sem,
    near_send,
    near_recv,
    near_local,
    out_send,
    out_low_recv,
    out_high_recv,
    in_send,
    in_low_recv,
    in_high_recv,
    load_sem,
    core_send,
    a_send,
    b_send,
    z_send,
    core_recv,
    a_recv,
    b_recv,
    z_recv,
    *small_scratch,
):
    n_z = lax.axis_size("gx")
    span = lax.axis_size("gy")
    z = lax.axis_index("gx")
    g = lax.axis_index("gy")
    peers = [{"gx": z, "gy": g + bit - 2 * bit * ((g // bit) % 2)} for bit in (1, 2, 4)]
    peers += [{"gx": lax.rem(z + j, n_z), "gy": g} for j in range(1, n_z)]
    barrier_with([(z >= 0, peer) for peer in peers])
    out_start, out_relays, out_finish = chain_scatter(
        n_z, out_sums, out_sum, out_low, out_high, out_send, out_low_recv, out_high_recv
    )
    chains = [
        chain_scatter(
            n_z,
            in_sums.at[h],
            weight_sum.at[h],
            in_low.at[h],
            in_high.at[h],
            in_send.at[h],
            in_low_recv.at[h],
            in_high_recv.at[h],
        )
        for h in range(heads)
    ]
    near, near_finish = gather_steps(1, span, own_grad, seq_ref, near_send, near_recv, near_local)
    small = sum_steps(n_z, span.bit_length() - 1, small_ref, small_sum, *small_scratch)
    back = []
    scatter_kernel(
        False,
        pieces,
        part_ref.shape[3],
        part_ref,
        grad_acts,
        held,
        from_core,
        from_a,
        from_b,
        from_z,
        load_sem,
        core_send,
        a_send,
        b_send,
        z_send,
        core_recv,
        a_recv,
        b_recv,
        z_recv,
        parts=back,
    )
    f32, bf16 = jnp.float32, jnp.bfloat16
    dot = partial(lax.dot_general, preferred_element_type=f32)
    plain = (((1,), (0,)), ((), ()))
    last_dims = (((1,), (1,)), ((), ()))
    first_dims = (((0,), (0,)), ((), ()))
    length, local = query_raw.shape
    width = acts_ref.shape[1]
    rows = part_ref.shape[3]
    block = 256
    scale = HD ** (-0.5)
    copies = [
        pltpu.make_async_copy(acts_hbm, acts_ref, copy_sem.at[0]),
        pltpu.make_async_copy(weight_hbm, weight_ref, copy_sem.at[1]),
    ]
    near[0]()
    small[0]()
    spread_docs(docs_ref, row_docs, col_docs)
    for copy in copies:
        copy.start()
    near[1]()
    small[1]()
    near[2]()
    small[2]()
    near_finish()
    owned = width // n_z

    @pl.loop(0, width // block)
    def _(t):
        cols = pl.ds(pl.multiple_of(t * block, block), block)
        inside = pl.ds(pl.multiple_of(lax.rem(t, owned // block) * block, block), block)
        grad = seq_ref[:, :, :, cols].reshape(length, block)
        out_sums[lax.div(t, owned // block), inside, :] = dot(
            grad, mixed_ref[...], first_dims
        ).astype(bf16)

    out_start()
    total = jnp.zeros((length, local), f32)
    for owner in range(n_z):
        cols = slice(owner * owned, (owner + 1) * owned)
        grad = seq_ref[:, :, :, cols].reshape(length, owned)
        total = total + dot(grad, out_weight_ref[owner], last_dims)
    grad_mixed[...] = total.astype(bf16)
    small[3]()
    gain_ref[...] = jnp.zeros_like(gain_ref)
    for h in range(heads):
        cols = slice(h * HD, (h + 1) * HD)
        key = ready_ref[:, local + h * HD : local + (h + 1) * HD]
        value = ready_ref[:, 2 * local + h * HD : 2 * local + (h + 1) * HD]
        key_sum[...] = jnp.zeros_like(key_sum)
        value_sum[...] = jnp.zeros_like(value_sum)

        @pl.loop(0, length // block)
        def _(t):
            at = pl.ds(pl.multiple_of(t * block, block), block)
            same = row_docs[at, :1] == col_docs[:1, :]
            query = ready_ref[at, cols]
            grad = grad_mixed[at, cols]
            scores = jnp.where(same, dot(query, key, last_dims) * scale, NEGATIVE)
            weights = jnp.exp(scores - totals_ref[at, h : h + 1])
            value_sum[...] += dot(weights.astype(bf16), grad, first_dims)
            pulled = dot(grad, value, last_dims)
            inner = jnp.sum(weights * pulled, axis=-1, keepdims=True)
            grad_scores = (weights * (pulled - inner)).astype(bf16)
            turned[at, :] = dot(grad_scores, key, plain) * scale
            key_sum[...] += dot(grad_scores, query, first_dims)

        for source, raw, gain, incoming, factor in (
            (0, query_raw, query_gain, turned, 1.0),
            (1, key_raw, key_gain, key_sum, scale),
        ):

            @pl.loop(0, length // block)
            def _(t):
                at = pl.ds(pl.multiple_of(t * block, block), block)
                back = turn(incoming[at, :] * factor, cosine_ref[at, :], -sine_ref[at, :])
                item = raw[at, cols]
                inverse = lax.rsqrt(jnp.mean(item * item, axis=-1, keepdims=True) + EPSILON)
                normed = item * inverse
                gain_ref[source : source + 1, :] += jnp.sum(back * normed, axis=0, keepdims=True)
                inner = back * gain[...]
                pulled = inverse * (
                    inner - normed * jnp.mean(inner * normed, axis=-1, keepdims=True)
                )
                where = source * local + h * HD
                grad_heads[at, where : where + HD] = pulled.astype(bf16)
                one_head[at, source * HD : (source + 1) * HD] = pulled.astype(bf16)

        where = 2 * local + h * HD
        grad_heads[:, where : where + HD] = value_sum[...].astype(bf16)
        one_head[:, 2 * HD :] = value_sum[...].astype(bf16)
        if h == 0:
            for copy in copies:
                copy.wait()
            for relay in out_relays:
                relay()
            out_finish()
            small[4]()
        else:
            chains[h - 1][1][0]()

        @pl.loop(0, width // block)
        def _(t):
            cols = pl.ds(pl.multiple_of(t * block, block), block)
            inside = pl.ds(pl.multiple_of(lax.rem(t, owned // block) * block, block), block)
            in_sums[h, lax.div(t, owned // block), inside, :] = dot(
                acts_ref[:, cols], one_head[...], first_dims
            ).astype(bf16)

        chains[h][0]()

    for chain in chains[:-1]:
        for relay in chain[1][1:2]:
            relay()

    @pl.loop(0, width // block)
    def _(t):
        cols = pl.ds(pl.multiple_of(t * block, block), block)
        sent = dot(grad_heads[...], weight_ref[cols, :], last_dims).astype(bf16)
        sent = sent.reshape(span, pieces, 2, rows, block)
        for p in range(pieces):
            part_ref[p, :, :, :, cols] = sent[:, p]

    small[5]()
    waiting = [relay for chain in chains[:-1] for relay in chain[1][2:]] + list(chains[-1][1])
    for i, step in enumerate(back[:-1]):
        step()
        if i % 2 == 0 and waiting:
            waiting.pop(0)()
    for relay in waiting:
        relay()
    for chain in chains:
        chain[2]()
    back[-1]()


def attend_back(
    grad,
    saved,
    query_gain,
    key_gain,
    tables,
    docs,
    acts,
    weights,
    small,
    collective_id,
    pieces=4,
):
    query_raw, key_raw, ready, mixed, totals, out_weight = saved
    n_z = lax.axis_size("gx")
    span = lax.axis_size("gy")
    bits = span.bit_length() - 1
    tokens, width = grad.shape
    length, local = query_raw.shape
    heads = local // HD
    rows = tokens // (pieces * 2)
    halves = folded(small)
    half = (2, tokens // 2, width)
    piece = (rows, width)
    out_block = (n_z, width // n_z, local)
    in_block = (heads, n_z, width // n_z, 3 * HD)
    f32, bf16 = jnp.float32, jnp.bfloat16
    dma = pltpu.SemaphoreType.DMA
    vmem = pl.BlockSpec(memory_space=pltpu.VMEM)
    hbm = pl.BlockSpec(memory_space=pl.ANY)
    grad_acts, weight_sum, out_sum, gains, small_sum = pl.pallas_call(
        partial(attend_back_kernel, heads, pieces),
        out_shape=(
            jax.ShapeDtypeStruct((pieces, 2) + piece, f32),
            jax.ShapeDtypeStruct((heads,) + in_block[2:], f32),
            jax.ShapeDtypeStruct(out_block[1:], f32),
            jax.ShapeDtypeStruct((8, HD), f32),
            jax.ShapeDtypeStruct(halves.shape, f32),
        ),
        in_specs=[vmem] * 13 + [hbm] * 2,
        out_specs=(vmem,) * 5,
        scratch_shapes=[
            pltpu.VMEM((length, 128), f32),
            pltpu.VMEM((8, length), f32),
            pltpu.VMEM((span,) + half, bf16),
            pltpu.VMEM((pieces, span, 2) + piece, bf16),
            pltpu.VMEM((length, width), bf16),
            pltpu.VMEM((width, 3 * local), bf16),
            pltpu.VMEM((length, local), bf16),
            pltpu.VMEM((length, 3 * local), bf16),
            pltpu.VMEM((length, 3 * HD), bf16),
            pltpu.VMEM((length, HD), f32),
            pltpu.VMEM((length, HD), f32),
            pltpu.VMEM((length, HD), f32),
            pltpu.VMEM(out_block, bf16),
            pltpu.VMEM(out_block, bf16),
            pltpu.VMEM(out_block, bf16),
            pltpu.VMEM(in_block, bf16),
            pltpu.VMEM(in_block, bf16),
            pltpu.VMEM(in_block, bf16),
            pltpu.VMEM((pieces, 4, 2) + piece, bf16),
            pltpu.VMEM((pieces, 4, 2) + piece, bf16),
            pltpu.VMEM((pieces, 2, 2) + piece, bf16),
            pltpu.VMEM((pieces, 2) + piece, bf16),
            pltpu.VMEM((1, 2, 16, 128), bf16),
            dma((2,)),
            dma((24,)),
            dma((span, 2)),
            dma,
            dma((n_z,)),
            dma((n_z,)),
            dma((n_z,)),
            dma((heads, n_z)),
            dma((heads, n_z)),
            dma((heads, n_z)),
            dma((pieces, 4)),
            dma((pieces, 4)),
            dma((pieces, 4)),
            dma((pieces, 2)),
            dma((pieces,)),
            dma((pieces, 4)),
            dma((pieces, 2, 2)),
            dma((pieces, 2)),
            dma((pieces,)),
        ]
        + sum_scratch(n_z, bits, halves.shape[1]),
        compiler_params=pltpu.CompilerParams(
            collective_id=collective_id, has_side_effects=True, vmem_limit_bytes=67043328
        ),
        name="attend_back",
    )(
        grad.reshape(half),
        out_weight,
        mixed,
        ready,
        query_raw,
        key_raw,
        totals,
        query_gain.reshape(1, HD),
        key_gain.reshape(1, HD),
        *tables,
        docs,
        halves,
        acts,
        weights,
    )
    weight_sum = weight_sum.reshape(heads, -1, 3, HD).transpose(1, 2, 0, 3)
    return (
        grad_acts.reshape(tokens, width),
        weight_sum.reshape(-1, 3 * local),
        out_sum,
        gains,
        small_sum.reshape(-1)[: small.shape[0]],
    )


def flat(parts):
    return jnp.concatenate([part.reshape(-1) for part in parts])


def unflat(vector, parts):
    ends = accumulate(part.size for part in parts)
    return [vector[end - part.size : end].reshape(part.shape) for end, part in zip(ends, parts)]


def norm_rows(values, gain_row):
    return (
        values * lax.rsqrt(jnp.mean(values * values, axis=-1, keepdims=True) + EPSILON) * gain_row
    )


def rotary(values):
    length = values.shape[0]
    halfway = values.shape[-1] // 2
    positions = jnp.arange(length, dtype=jnp.float32)
    frequency = jnp.exp(
        jnp.arange(halfway, dtype=jnp.float32) * (-2.0 * jnp.log(10000.0) / values.shape[-1])
    )
    angles = (positions[:, None] * frequency[None, :])[:, None, :]
    cosine = jnp.cos(angles)
    sine_table = jnp.sin(angles)
    first_half = values[..., :halfway]
    second = values[..., halfway:]
    return jnp.concatenate(
        [first_half * cosine - second * sine_table, second * cosine + first_half * sine_table],
        axis=-1,
    )


def prepare_heads(raw_heads, gain_row):
    return rotary(norm_rows(raw_heads, gain_row))


def route_gates(id_table, logits):
    shares = jax.nn.softmax(logits, axis=-1)
    experts = logits.shape[-1]
    matches = id_table[:, :, None] == jnp.arange(experts, dtype=jnp.int32)[None, None, :]
    chosen = jnp.sum(jnp.where(matches, shares[:, None, :], 0.0), axis=-1)
    return chosen / jnp.sum(chosen, axis=-1, keepdims=True)


def contract_rows(left_side, right_side):
    return lax.dot_general(
        left_side, right_side, (((0,), (0,)), ((), ())), preferred_element_type=jnp.float32
    )


def contract_cols(left_side, right_side):
    return lax.dot_general(
        left_side, right_side, (((1,), (1,)), ((), ())), preferred_element_type=jnp.float32
    )


def routed_experts(
    moe_in, cotangent, expert_ids, gate_share, router_weight, gate_weight, up_weight, down_weight
):
    tok_rows = moe_in.shape[0]
    experts = router_weight.shape[1]
    width_all = moe_in.shape[1]
    capacity = tok_rows * TOP * 3 // (2 * experts)
    route_count = tok_rows * TOP
    flat_ids = expert_ids.reshape(route_count)
    onehot = (flat_ids[:, None] == jnp.arange(experts, dtype=jnp.int32)[None, :]).astype(jnp.int32)
    earlier = jnp.cumsum(onehot, axis=0) - onehot
    slot_index = jnp.sum(earlier * onehot, axis=1)
    target = flat_ids * capacity + slot_index
    source = (
        jnp.full((experts * capacity,), tok_rows, jnp.int32)
        .at[target]
        .set(jnp.arange(route_count, dtype=jnp.int32) // TOP)
    )
    padded_in = jnp.concatenate([moe_in, jnp.zeros((1, width_all), jnp.bfloat16)], axis=0)
    packed = padded_in[source].reshape(experts, 1, capacity, width_all)
    outgoing = jnp.broadcast_to(packed, (experts, 2, capacity, width_all)).reshape(
        2 * experts, capacity, width_all
    )
    arrived = lax.all_to_all(outgoing, ("gx", "gy"), split_axis=0, concat_axis=1, tiled=True)[0]
    gate_in = gate_weight[0]
    up_in = up_weight[0]
    down_in = down_weight[0]
    gate_val = jnp.dot(arrived, gate_in, preferred_element_type=jnp.float32)
    up_val = jnp.dot(arrived, up_in, preferred_element_type=jnp.float32)
    hidden = (jax.nn.silu(gate_val) * up_val).astype(jnp.bfloat16)
    produced = jnp.dot(hidden, down_in, preferred_element_type=jnp.float32).astype(jnp.bfloat16)
    returned = lax.all_to_all(produced[None], ("gx", "gy"), split_axis=1, concat_axis=0, tiled=True)
    summed = (
        returned.reshape(experts, 2, capacity, width_all)
        .astype(jnp.float32)
        .sum(axis=1)
        .reshape(experts * capacity, width_all)
    )
    route_out = summed[target]
    gates_flat = gate_share.reshape(route_count)
    moe_out = jnp.sum((gates_flat[:, None] * route_out).reshape(tok_rows, TOP, width_all), axis=1)
    grad_out = cotangent.astype(jnp.float32)
    grad_gates = jnp.sum(
        route_out.reshape(tok_rows, TOP, width_all) * grad_out[:, None, :], axis=-1
    )
    slot_gate = jnp.zeros((experts * capacity,), jnp.float32).at[target].set(gates_flat)
    padded_grad = jnp.concatenate([grad_out, jnp.zeros((1, width_all), jnp.float32)], axis=0)
    grad_packed = (
        (slot_gate[:, None] * padded_grad[source])
        .astype(jnp.bfloat16)
        .reshape(experts, 1, capacity, width_all)
    )
    grad_outgoing = jnp.broadcast_to(grad_packed, (experts, 2, capacity, width_all)).reshape(
        2 * experts, capacity, width_all
    )
    grad_arrived = lax.all_to_all(
        grad_outgoing, ("gx", "gy"), split_axis=0, concat_axis=1, tiled=True
    )[0]
    rows_in, grad_use = (arrived, grad_arrived)
    gate_use, up_use, hidden_use = (gate_val, up_val, hidden)
    sigmoid_gate = jax.nn.sigmoid(gate_use)
    silu_gate = gate_use * sigmoid_gate
    grad_hidden = contract_cols(grad_use, down_in)
    down_part = contract_rows(hidden_use, grad_use)
    grad_gate = (
        grad_hidden * up_use * sigmoid_gate * (1.0 + gate_use * (1.0 - sigmoid_gate))
    ).astype(jnp.bfloat16)
    grad_up = (grad_hidden * silu_gate).astype(jnp.bfloat16)
    gate_part = contract_rows(rows_in, grad_gate)
    up_part = contract_rows(rows_in, grad_up)
    grad_in = contract_cols(grad_gate, gate_in) + contract_cols(grad_up, up_in)
    grad_back = lax.all_to_all(
        grad_in.astype(jnp.bfloat16)[None], ("gx", "gy"), split_axis=1, concat_axis=0, tiled=True
    )
    grad_summed = (
        grad_back.reshape(experts, 2, capacity, width_all)
        .astype(jnp.float32)
        .sum(axis=1)
        .reshape(experts * capacity, width_all)
    )
    grad_moe_in = jnp.sum(grad_summed[target].reshape(tok_rows, TOP, width_all), axis=1)
    return moe_out, grad_gates, grad_moe_in, gate_part, up_part, down_part


def dense_experts(
    moe_in, all_cot, expert_ids, gate_share, gate_weight, up_weight, down_weight
):
    devices = lax.axis_size("gx") * lax.axis_size("gy")
    experts = devices // 2
    matches = expert_ids[:, :, None] == jnp.arange(experts, dtype=jnp.int32)[None, None, :]
    dense_gates = jnp.sum(jnp.where(matches, gate_share[:, :, None], 0.0), axis=1)
    shares = jnp.repeat(dense_gates.T, 2, axis=0)[:, None, :]
    all_moe, pair, gate_dots, down_part, moe_out = run_experts(
        moe_in, all_cot, shares, gate_weight[0], up_weight[0], down_weight[0], 8
    )
    moe_out = moe_out.reshape(moe_in.shape)
    dots_experts = gate_dots.reshape(experts, 2, -1).sum(axis=1).T
    grad_gates = jnp.sum(jnp.where(matches, dots_experts[:, None, :], 0.0), axis=-1)
    grad_moe_in, gate_part, up_part = pull_experts(all_moe, pair, gate_weight[0], up_weight[0], 9)
    return moe_out, grad_gates, grad_moe_in, gate_part, up_part, down_part


def plain_attention(
    acts, in_weights, out_weight, query_gain, key_gain, doc_ids, cotangent
):
    seq_acts = lax.all_gather(acts, "gy", axis=0, tiled=True)
    full_in = lax.all_gather(jnp.concatenate(in_weights, axis=1), "gx", axis=0, tiled=True)
    out_rows = lax.all_gather(out_weight, "gx", axis=1, tiled=True)
    local_width = full_in.shape[1] // 3
    length = seq_acts.shape[0]
    local_heads = local_width // HD
    projected = jnp.dot(seq_acts, full_in, preferred_element_type=jnp.float32)
    queries = projected[:, :local_width]
    key_raw = projected[:, local_width : 2 * local_width]
    value_ready = (
        projected[:, 2 * local_width :].astype(jnp.bfloat16).reshape(length, local_heads, HD)
    )
    query_float, query_pull = jax.vjp(
        prepare_heads, queries.reshape(length, local_heads, HD), query_gain
    )
    key_float, key_pull = jax.vjp(prepare_heads, key_raw.reshape(length, local_heads, HD), key_gain)
    query_ready = query_float.astype(jnp.bfloat16)
    key_ready = key_float.astype(jnp.bfloat16)
    block_rows = min(512, length)
    block_count = length // block_rows
    score_scale = HD ** (-0.5)
    query_blocks = query_ready.reshape(block_count, block_rows, local_heads, HD)
    doc_blocks = doc_ids.reshape(block_count, block_rows)

    def block_scores(query_block, doc_block):
        scores = (
            jnp.einsum("qhd,khd->hqk", query_block, key_ready, preferred_element_type=jnp.float32)
            * score_scale
        )
        same_doc = doc_block[:, None] == doc_ids[None, :]
        return jnp.where(same_doc[None], scores, NEGATIVE)

    def forward_block(pieces):
        scores = block_scores(pieces[0], pieces[1])
        highest = jnp.max(scores, axis=-1, keepdims=True)
        weights = jnp.exp(scores - highest)
        totals = jnp.sum(weights, axis=-1, keepdims=True)
        shares = (weights / totals).astype(jnp.bfloat16)
        mixed_heads = jnp.einsum(
            "hqk,khd->qhd", shares, value_ready, preferred_element_type=jnp.float32
        )
        return (
            mixed_heads.astype(jnp.bfloat16),
            highest[..., 0] + jnp.log(totals[..., 0]),
            jnp.max(highest[..., 0], axis=-1),
        )

    mixed_blocks, log_totals, peak_blocks = lax.map(forward_block, (query_blocks, doc_blocks))
    mixed_seq = mixed_blocks.reshape(length, local_width)
    attended = lax.psum_scatter(
        jnp.dot(mixed_seq, out_rows, preferred_element_type=jnp.float32),
        "gy",
        scatter_dimension=0,
        tiled=True,
    )

    def back(grad_resid, small):
        seq_grad = lax.all_gather(grad_resid.astype(jnp.bfloat16), "gy", axis=0, tiled=True)
        grad_mixed = contract_cols(seq_grad, out_rows).astype(jnp.bfloat16)
        out_part = contract_rows(seq_grad, mixed_seq)

        def backward_block(running, pieces):
            grad_key, grad_value = running
            query_block, grad_block, log_block, doc_block = pieces
            scores = block_scores(query_block, doc_block)
            weights = jnp.exp(scores - log_block[..., None])
            grad_value = grad_value + jnp.einsum(
                "hqk,qhd->khd",
                weights.astype(jnp.bfloat16),
                grad_block,
                preferred_element_type=jnp.float32,
            )
            grad_weights = jnp.einsum(
                "qhd,khd->hqk", grad_block, value_ready, preferred_element_type=jnp.float32
            )
            inner_sum = jnp.sum(weights * grad_weights, axis=-1, keepdims=True)
            grad_scores = (weights * (grad_weights - inner_sum)).astype(jnp.bfloat16)
            grad_query = (
                jnp.einsum("hqk,khd->qhd", grad_scores, key_ready, preferred_element_type=jnp.float32)
                * score_scale
            )
            grad_key = (
                grad_key
                + jnp.einsum(
                    "hqk,qhd->khd", grad_scores, query_block, preferred_element_type=jnp.float32
                )
                * score_scale
            )
            return ((grad_key, grad_value), grad_query)

        empty_heads = jnp.zeros((length, local_heads, HD), jnp.float32)
        grad_mixed_blocks = grad_mixed.reshape(block_count, block_rows, local_heads, HD)
        (key_grad_heads, value_grad_heads), query_grad_blocks = lax.scan(
            backward_block,
            (empty_heads, empty_heads),
            (query_blocks, grad_mixed_blocks, log_totals, doc_blocks),
        )
        query_raw_grad, query_gain_part = query_pull(query_grad_blocks.reshape(length, local_heads, HD))
        key_raw_grad, key_gain_part = key_pull(key_grad_heads)
        grad_queries = query_raw_grad.reshape(length, local_width).astype(jnp.bfloat16)
        grad_keys = key_raw_grad.reshape(length, local_width).astype(jnp.bfloat16)
        grad_values = value_grad_heads.reshape(length, local_width).astype(jnp.bfloat16)
        grad_heads = jnp.concatenate([grad_queries, grad_keys, grad_values], axis=1)
        acts_part = contract_cols(grad_heads, full_in).astype(jnp.bfloat16)
        in_sum = lax.psum_scatter(
            contract_rows(seq_acts, grad_heads).astype(jnp.bfloat16),
            "gx",
            scatter_dimension=0,
            tiled=True,
        ).astype(jnp.float32)
        grad_acts = lax.psum_scatter(acts_part, "gy", scatter_dimension=0, tiled=True)
        out_sum = lax.psum_scatter(
            out_part.astype(jnp.bfloat16), "gx", scatter_dimension=0, tiled=True
        ).astype(jnp.float32)
        return grad_acts.astype(jnp.float32), in_sum, out_sum, query_gain_part, key_gain_part, sum_everywhere(small, 12)

    return attended, jnp.max(peak_blocks, axis=0), None, back


def kernel_attention(
    acts, in_weights, out_weight, query_gain, key_gain, doc_ids, cotangent
):
    length = doc_ids.shape[0]
    halfway = HD // 2
    frequency = jnp.exp(
        jnp.arange(halfway, dtype=jnp.float32) * (-2.0 * jnp.log(10000.0) / HD)
    )
    angles = jnp.arange(length, dtype=jnp.float32)[:, None] * frequency[None, :]
    cosine, sine = jnp.cos(angles), jnp.sin(angles)
    tables = (
        jnp.concatenate([cosine, cosine], axis=1),
        jnp.concatenate([-sine, sine], axis=1),
    )
    docs = doc_ids.reshape(-1, 128)
    attended, seq_acts, full_in, all_cot, saved, peaks = attend(
        acts, in_weights, out_weight, cotangent, query_gain, key_gain, tables, docs, 10
    )
    heads = in_weights[0].shape[1] // HD

    def back(grad_resid, small):
        grad_acts, in_sum, out_sum, gains, small_sum = attend_back(
            grad_resid.astype(jnp.bfloat16),
            saved,
            query_gain,
            key_gain,
            tables,
            docs,
            seq_acts,
            full_in,
            small,
            11,
        )
        return grad_acts, in_sum, out_sum, gains[0], gains[1], small_sum

    return attended, peaks[:heads, 0], all_cot, back


def local(
    tokens,
    cotangent,
    expert_ids,
    doc_ids,
    clip_rank,
    attn_gain,
    moe_gain,
    query_gain,
    key_gain,
    query_weight,
    key_weight,
    value_weight,
    out_weight,
    router_weight,
    gate_weight,
    up_weight,
    down_weight,
):
    inputs = tokens.astype(jnp.float32)
    acts_float, norm_pull = jax.vjp(norm_rows, inputs, attn_gain)
    acts_low = acts_float.astype(jnp.bfloat16)
    in_weights = (query_weight, key_weight, value_weight)
    by_kernels = lax.axis_size("gy") == 8
    local_width = query_weight.shape[1]
    local_heads = local_width // HD
    attention = kernel_attention if by_kernels else plain_attention
    attended, own_peaks, all_cot, attention_back = attention(
        acts_low, in_weights, out_weight, query_gain, key_gain, doc_ids, cotangent
    )
    start_head = lax.axis_index("gy") * local_heads
    peak_slots = lax.dynamic_update_slice(
        jnp.zeros((lax.axis_size("gx"), NH), jnp.float32),
        own_peaks[None],
        (lax.axis_index("gx"), start_head),
    )
    residual = inputs + attended
    moe_float, moe_pull = jax.vjp(norm_rows, residual, moe_gain)
    moe_in = moe_float.astype(jnp.bfloat16)
    logits = jnp.dot(moe_in, router_weight, preferred_element_type=jnp.float32)
    gate_share, gate_pull = jax.vjp(partial(route_gates, expert_ids), logits)
    if by_kernels and router_weight.shape[1] <= 2 * TOP:
        moe_out, grad_gates, grad_moe_in, gate_part, up_part, down_part = dense_experts(
            moe_in, all_cot, expert_ids, gate_share, gate_weight, up_weight, down_weight
        )
    else:
        moe_out, grad_gates, grad_moe_in, gate_part, up_part, down_part = routed_experts(
            moe_in,
            cotangent,
            expert_ids,
            gate_share,
            router_weight,
            gate_weight,
            up_weight,
            down_weight,
        )
    output = (residual + moe_out).astype(jnp.bfloat16)
    grad_out = cotangent.astype(jnp.float32)
    (grad_logits,) = gate_pull(grad_gates)
    grad_logits_low = grad_logits.astype(jnp.bfloat16)
    router_part = contract_rows(moe_in, grad_logits_low)
    grad_moe_in = grad_moe_in + contract_cols(grad_logits_low, router_weight)
    grad_resid_norm, moe_gain_part = moe_pull(grad_moe_in)
    grad_resid = grad_out + grad_resid_norm
    early = (moe_gain_part, router_part.T, peak_slots)
    grad_acts, in_sum, out_sum, query_gain_part, key_gain_part, early_sum = attention_back(
        grad_resid, flat(early)
    )
    moe_gain_grad, router_flat, peaks = unflat(early_sum, early)
    query_sum = in_sum[:, :local_width]
    key_sum = in_sum[:, local_width : 2 * local_width]
    value_sum = in_sum[:, 2 * local_width :]
    norm_input_grad, attn_gain_part = norm_pull(grad_acts)
    input_grad = grad_resid + norm_input_grad
    late = (attn_gain_part, query_gain_part, key_gain_part)
    attn_gain_grad, query_gain_grad, key_gain_grad = unflat(sum_everywhere(flat(late), 5), late)
    router_grad = router_flat.T
    peak_global = jnp.max(peaks, axis=0)
    ranked = -jnp.sort(-peak_global)
    limit = jnp.sum(jnp.where(jnp.arange(NH, dtype=jnp.int32) == clip_rank[0], ranked, 0.0))
    factors = jnp.where(peak_global > limit, limit / peak_global, 1.0)
    own_factors = lax.dynamic_slice_in_dim(factors, start_head, local_heads)
    columns = jnp.repeat(jnp.sqrt(own_factors), HD)
    query_clipped = (query_weight.astype(jnp.float32) * columns[None, :]).astype(jnp.bfloat16)
    key_clipped = (key_weight.astype(jnp.float32) * columns[None, :]).astype(jnp.bfloat16)
    return (
        output,
        input_grad,
        attn_gain_grad,
        moe_gain_grad,
        query_gain_grad,
        key_gain_grad,
        query_sum,
        key_sum,
        value_sum,
        out_sum.T,
        router_grad,
        gate_part[None],
        up_part[None],
        down_part[None],
        query_clipped,
        key_clipped,
        factors,
    )


def solution(mesh):
    placed = (
        P(("gx", "gy"), None),
        P(("gx", "gy"), None),
        P(("gx", "gy"), None),
        P("gx"),
        P(),
        P(),
        P(),
        P(),
        P(),
        P("gx", "gy"),
        P("gx", "gy"),
        P("gx", "gy"),
        P("gy", "gx"),
        P(),
        P(("gx", "gy"), None, None),
        P(("gx", "gy"), None, None),
        P(("gx", "gy"), None, None),
    )
    return jax.shard_map(
        local,
        mesh=mesh,
        in_specs=placed,
        out_specs=(
            P(("gx", "gy"), None),
            P(("gx", "gy"), None),
            P(),
            P(),
            P(),
            P(),
            P("gx", "gy"),
            P("gx", "gy"),
            P("gx", "gy"),
            P("gy", "gx"),
            P(),
            P(("gx", "gy"), None, None),
            P(("gx", "gy"), None, None),
            P(("gx", "gy"), None, None),
            P("gx", "gy"),
            P("gx", "gy"),
            P(),
        ),
        check_vma=False,
    )
```

```python
from functools import partial
from itertools import accumulate

import jax
import jax.numpy as jnp
from jax import lax
from jax.experimental import pallas as pl
from jax.experimental.pallas import tpu as pltpu
from jax.sharding import PartitionSpec as P

NH = 16
HD = 128
TOP = 8


EPSILON = 1e-06
NEGATIVE = -1e30


def flip(index):
    return index + 1 - 2 * (index % 2)


def barrier_with(partners):
    barrier = pltpu.get_barrier_semaphore()
    for ok, device in partners:
        @pl.when(ok)
        def _():
            pl.semaphore_signal(barrier, inc=1, device_id=device, device_id_type=pl.DeviceIdType.MESH)
    pl.semaphore_wait(barrier, sum(ok.astype(jnp.int32) for ok, _ in partners))

def always(ok, other):
    if ok is True:
        return other
    return ok if other is True else jnp.logical_and(ok, other)


def run_if(ok, action):
    if ok is True:
        action()
    else:
        pl.when(ok)(action)


def chain_gather(n_z, own_ref, out_ref, send_sem, recv_sem, local_sem):
    z = lax.axis_index("gx")
    g = lax.axis_index("gy")

    def hop(source, owner, k, peer):
        return pltpu.make_async_remote_copy(
            src_ref=source,
            dst_ref=out_ref.at[owner],
            send_sem=send_sem.at[k],
            recv_sem=recv_sem.at[owner],
            device_id={"gx": peer, "gy": g},
            device_id_type=pl.DeviceIdType.MESH,
        )

    local = pltpu.make_async_copy(own_ref, out_ref.at[z], local_sem)
    upward = [(z < n_z - 1, lambda: hop(own_ref, z, 0, z + 1))]
    downward = [(z > 0, lambda: hop(own_ref, z, n_z, z - 1))]
    for d in range(1, n_z - 1):
        upward.append(
            (
                jnp.logical_and(z >= d, z < n_z - 1),
                lambda d=d: hop(out_ref.at[z - d], z - d, d, z + 1),
            )
        )
        downward.append(
            (
                jnp.logical_and(z < n_z - d, z > 0),
                lambda d=d: hop(out_ref.at[z + d], z + d, n_z + d, z - 1),
            )
        )

    def start():
        local.start()
        for ok, copy in (upward[0], downward[0]):
            run_if(ok, lambda copy=copy: copy().start())

    def relay(d):
        run_if(z >= d, lambda: hop(own_ref, z - d, 0, z).wait_recv())
        if d < n_z - 1:
            run_if(upward[d][0], lambda: upward[d][1]().start())
        run_if(z < n_z - d, lambda: hop(own_ref, z + d, 0, z).wait_recv())
        if d < n_z - 1:
            run_if(downward[d][0], lambda: downward[d][1]().start())

    def finish():
        local.wait()
        for ok, copy in upward + downward:
            run_if(ok, lambda copy=copy: copy().wait_send())

    return start, [partial(relay, d) for d in range(1, n_z)], finish


def gather_steps(n_z, span, own_ref, out_ref, send_sem, recv_sem, local_sem):
    z = lax.axis_index("gx")
    g = lax.axis_index("gy")
    flip_x = g + 2 - 4 * ((g // 2) % 2)
    flip_y = g + 4 - 8 * ((g // 4) % 2)
    flip_both = flip_x + flip_y - g
    core = {"gx": z, "gy": flip(g)}
    x_peer = {"gx": z, "gy": flip_x}
    y_peer = {"gx": z, "gy": flip_y}
    above = {"gx": z + 1, "gy": g}
    below = {"gx": z - 1, "gy": g}
    first_z = z if n_z > 1 else 0
    sends = []

    def send(ok, b, h, peer, own=False):
        k = len(sends)

        def make():
            return pltpu.make_async_remote_copy(
                src_ref=own_ref.at[h] if own else out_ref.at[b, h],
                dst_ref=out_ref.at[b, h],
                send_sem=send_sem.at[k],
                recv_sem=recv_sem.at[b, h],
                device_id=peer,
                device_id_type=pl.DeviceIdType.MESH,
            )

        sends.append((ok, make))
        run_if(ok, lambda: make().start())

    def arrive(ok, b, h):
        def wait():
            pltpu.make_async_remote_copy(
                src_ref=out_ref.at[b, h],
                dst_ref=out_ref.at[b, h],
                send_sem=send_sem.at[0],
                recv_sem=recv_sem.at[b, h],
                device_id=core,
                device_id_type=pl.DeviceIdType.MESH,
            ).wait_recv()

        run_if(ok, wait)

    local = pltpu.make_async_copy(own_ref, out_ref.at[first_z * span + g], local_sem)
    items = [(True, first_z, 0)]
    for d in range(1, n_z):
        items += [(z >= d, z - d, -d), (z < n_z - d, z + d, d)]

    upward = [always(item[0], z < n_z - 1) for item in items]
    downward = [always(item[0], z > 0) for item in items]

    near_b = [owner * span + g for _, owner, _ in items]
    x_b = [owner * span + flip_x for _, owner, _ in items]
    y_b = [owner * span + flip_y for _, owner, _ in items]
    both_b = [owner * span + flip_both for _, owner, _ in items]

    def first(i):
        ok, _, d = items[i]
        b = near_b[i]
        own = d == 0
        if own:
            local.start()
        else:
            arrive(ok, b, 0)
            arrive(ok, b, 1)
        for h in range(2):
            if n_z > 1 and d <= 0:
                send(upward[i], b, h, above, own)
            if n_z > 1 and d >= 0:
                send(downward[i], b, h, below, own)
        for h, peer in ((0, x_peer), (1, y_peer), (1, x_peer), (0, y_peer), (0, core), (1, core)):
            send(ok, b, h, peer, own)

    def second(i):
        ok = items[i][0]
        for b, h, peer in ((x_b[i], 0, y_peer), (y_b[i], 1, x_peer)):
            arrive(ok, b, h)
            send(ok, b, h, peer)
            send(ok, b, h, core)

    def third(i):
        ok = items[i][0]
        for b, h in ((both_b[i], 0), (both_b[i], 1), (y_b[i], 0), (x_b[i], 1)):
            arrive(ok, b, h)
            send(ok, b, h, core)

    n = len(items)

    def step(i):
        if i < n:
            first(i)
        if 1 <= i <= n:
            second(i - 1)
        if i >= 2:
            third(i - 2)

    def finish():
        for ok, owner, _ in items:
            for side in (g, flip_x, flip_y, flip_both):
                for h in range(2):
                    arrive(ok, owner * span + flip(side), h)
        local.wait()
        for ok, make in sends:
            run_if(ok, lambda make=make: make().wait_send())

    return [partial(step, i) for i in range(n + 2)], finish


def greet(n_z):
    z = lax.axis_index("gx")
    g = lax.axis_index("gy")
    peers = [
        (z >= 0, {"gx": z, "gy": g + bit - 2 * bit * ((g // bit) % 2)}) for bit in (1, 2, 4)
    ]
    if n_z > 1:
        peers += [(z < n_z - 1, {"gx": z + 1, "gy": g}), (z > 0, {"gx": z - 1, "gy": g})]
    barrier_with(peers)


def add_into(dst, parts, rows):
    step = min(rows, 32)

    @pl.loop(0, rows // step)
    def _(r):
        at = pl.ds(pl.multiple_of(r * step, step), step)
        if len(parts) == 2 and dst.dtype == jnp.bfloat16:
            dst[at, :] = parts[0][at, :] + parts[1][at, :]
        else:
            total = parts[0][at, :].astype(jnp.float32)
            for term in parts[1:]:
                total = total + term[at, :].astype(jnp.float32)
            dst[at, :] = total.astype(dst.dtype)


def scatter_kernel(chain, n_i, rows, part_ref, out_ref, held, from_core, from_a, from_b, from_z,
                   load_sem, core_send, a_send, b_send, z_send, core_recv, a_recv, b_recv, z_recv, beside=None, parts=None):
    z = lax.axis_index("gx"); g = lax.axis_index("gy")
    flip_x = g + 2 - 4 * ((g // 2) % 2)
    flip_y = g + 4 - 8 * ((g // 4) % 2)
    quads = (flip_x + flip_y - g, flip_x, flip_y, g)
    core = {"gx": z, "gy": flip(g)}
    xn = {"gx": z, "gy": flip_x}
    yn = {"gx": z, "gy": flip_y}
    every = z >= 0
    partners = [(every, core), (every, xn), (every, yn)]
    if chain:
        partners += [(every, {"gx": lax.rem(z + j, n_i), "gy": g}) for j in range(1, n_i)]
    if beside:
        n_z = lax.axis_size("gx")
        partners += [(z < n_z - 1, {"gx": z + 1, "gy": g}), (z > 0, {"gx": z - 1, "gy": g})]
    if parts is None:
        barrier_with(partners)
    if beside:
        beside[0]()
    mesh_id = pl.DeviceIdType.MESH

    def item(i):
        return lax.rem(z + n_i - 1 - i + n_i, n_i) if chain else i

    def block(it, gg):
        return part_ref.at[it, gg]

    def remote(src, dst, ssem, rsem, dev):
        return pltpu.make_async_remote_copy(src_ref=src, dst_ref=dst, send_sem=ssem, recv_sem=rsem, device_id=dev, device_id_type=mesh_id)

    def core_copy(i, q):
        it = item(i)
        return remote(block(it, flip(quads[q])), from_core.at[it, q], core_send.at[i, q], core_recv.at[it, q], core)

    def load(i, q):
        it = item(i)
        return pltpu.make_async_copy(block(it, quads[q]), held.at[it, q], load_sem.at[i, q])

    a_plan = ((0, 0, 0, xn), (0, 1, 0, yn), (1, 0, 1, xn), (2, 1, 1, yn))
    def a_copy(i, k):
        it = item(i)
        q, h, slot, dev = a_plan[k]
        return remote(held.at[it, q, h], from_a.at[it, h, slot], a_send.at[i, k], a_recv.at[it, h, slot], dev)

    b_plan = ((2, 0, yn), (1, 1, xn))
    def b_copy(i, h):
        it = item(i)
        q, _, dev = b_plan[h]
        return remote(held.at[it, q, h], from_b.at[it, h], b_send.at[i, h], b_recv.at[it, h], dev)

    def z_copy(i):
        it = item(i)
        return remote(held.at[it, 3], from_z.at[z], z_send.at[i], z_recv.at[z], {"gx": it, "gy": g})

    def z_arrival(i):
        it = item(i)
        return remote(held.at[it, 3], from_z.at[it], z_send.at[i], z_recv.at[it], core)

    def begin():
        for i in range(n_i):
            for q in range(4):
                core_copy(i, q).start()
                load(i, q).start()

    def stage_a(i):
        it = item(i)
        for q in range(4):
            load(i, q).wait()
            core_copy(i, q).wait_recv()
            for h in range(2):
                add_into(held.at[it, q, h], (held.at[it, q, h], from_core.at[it, q, h]), rows)
            for k in range(4):
                if a_plan[k][0] == q:
                    a_copy(i, k).start()

    def stage_b(i):
        it = item(i)
        for q, h, slot in ((2, 0, 0), (1, 1, 0), (3, 0, 1), (3, 1, 1)):
            remote(held.at[it, q, h], from_a.at[it, h, slot], a_send.at[i, 0], a_recv.at[it, h, slot], core).wait_recv()
            add_into(held.at[it, q, h], (held.at[it, q, h], from_a.at[it, h, slot]), rows)
            if slot == 0:
                b_copy(i, h).start()

    def stage_c(i):
        it = item(i)
        for h in range(2):
            b_copy(i, h).wait_recv()
            if chain:
                add_into(held.at[it, 3, h], (held.at[it, 3, h], from_b.at[it, h]), rows)
            else:
                add_into(out_ref.at[it, h], (held.at[it, 3, h], from_b.at[it, h]), rows)

    def stage_d(i):
        if i < n_i - 1:
            z_copy(i).start()
        else:
            for j in range(n_i - 1):
                z_arrival(j).wait_recv()
            for h in range(2):
                add_into(
                    out_ref.at[h],
                    [held.at[item(i), 3, h]] + [from_z.at[item(j), h] for j in range(n_i - 1)],
                    rows,
                )

    def step(i):
        if i < n_i:
            stage_a(i)
        if 0 <= i - 1 < n_i:
            stage_b(i - 1)
        if 0 <= i - 2 < n_i:
            stage_c(i - 2)
        if chain and 0 <= i - 2 < n_i:
            stage_d(i - 2)

    def finish():
        for i in range(n_i):
            for q in range(4):
                core_copy(i, q).wait_send()
            for k in range(4):
                a_copy(i, k).wait_send()
            for h in range(2):
                b_copy(i, h).wait_send()
            if chain and i < n_i - 1:
                z_copy(i).wait_send()

    if parts is not None:
        parts.extend([begin] + [partial(step, i) for i in range(n_i + 2)] + [finish])
        return
    begin()
    for i in range(n_i + 2):
        step(i)
        if beside and i == n_i:
            beside[1][0]()
    if beside:
        for relay in beside[1][1:]:
            relay()
        beside[2]()
    finish()


def sum_steps(n_z, bits, vec_ref, out_ref, held, arrived, from_z, send_sem, z_send, recv_sem, z_recv):
    z = lax.axis_index("gx")
    g = lax.axis_index("gy")
    side = lax.rem(g, 2)
    peers = [
        {"gx": z, "gy": g + bit - 2 * bit * ((g // bit) % 2)}
        for bit in (2**power for power in range(bits))
    ]
    others = [{"gx": lax.rem(z + j, n_z), "gy": g} for j in range(1, n_z)]

    def remote(src, dst, ssem, rsem, peer):
        return pltpu.make_async_remote_copy(
            src_ref=src,
            dst_ref=dst,
            send_sem=ssem,
            recv_sem=rsem,
            device_id=peer,
            device_id_type=pl.DeviceIdType.MESH,
        )

    def hop(k):
        source = vec_ref.at[1 - side] if k == 0 else held.at[k - 1]
        return remote(source, arrived.at[k], send_sem.at[k], recv_sem.at[k], peers[k])

    def across(j):
        return remote(held.at[bits - 1], from_z.at[j], z_send.at[j], z_recv.at[j], others[j])

    def back():
        return remote(held.at[bits], arrived.at[bits], send_sem.at[bits], recv_sem.at[bits], peers[0])

    def onward(k):
        hop(k).wait()
        held[k] = (vec_ref[side] if k == 0 else held[k - 1]) + arrived[k]
        if k + 1 < bits:
            hop(k + 1).start()
        else:
            for j in range(n_z - 1):
                across(j).start()

    def gather():
        for j in range(n_z - 1):
            across(j).wait()
        total = jnp.zeros_like(held[0])
        for owner in range(n_z):
            term = held[bits - 1]
            for j in range(1, n_z):
                term = jnp.where(lax.rem(z - j + n_z, n_z) == owner, from_z[j - 1], term)
            total = total + term
        held[bits] = total
        back().start()
        out_ref[side] = total

    def finish():
        back().wait()
        out_ref[1 - side] = arrived[bits]

    return [lambda: hop(0).start()] + [partial(onward, k) for k in range(bits)] + [gather, finish]


def sum_kernel(n_z, bits, *refs):
    z = lax.axis_index("gx")
    g = lax.axis_index("gy")
    peers = [
        {"gx": z, "gy": g + bit - 2 * bit * ((g // bit) % 2)}
        for bit in (2**power for power in range(bits))
    ]
    peers += [{"gx": lax.rem(z + j, n_z), "gy": g} for j in range(1, n_z)]
    barrier_with([(z >= 0, peer) for peer in peers])
    for step in sum_steps(n_z, bits, *refs):
        step()


def folded(vector):
    rows = -(-vector.shape[0] // (128 * 16)) * 8
    return jnp.pad(vector, (0, 2 * rows * 128 - vector.shape[0])).reshape(2, rows, 128)


def sum_scratch(n_z, bits, rows):
    dma = pltpu.SemaphoreType.DMA
    return [
        pltpu.VMEM((bits + 1, rows, 128), jnp.float32),
        pltpu.VMEM((bits + 1, rows, 128), jnp.float32),
        pltpu.VMEM((n_z - 1, rows, 128), jnp.float32),
        dma((bits + 1,)),
        dma((n_z - 1,)),
        dma((bits + 1,)),
        dma((n_z - 1,)),
    ]


def sum_everywhere(vector, collective_id):
    n_z = lax.axis_size("gx")
    bits = lax.axis_size("gy").bit_length() - 1
    halves = folded(vector)
    out = pl.pallas_call(
        partial(sum_kernel, n_z, bits),
        out_shape=jax.ShapeDtypeStruct(halves.shape, jnp.float32),
        in_specs=[pl.BlockSpec(memory_space=pltpu.VMEM)],
        out_specs=pl.BlockSpec(memory_space=pltpu.VMEM),
        scratch_shapes=sum_scratch(n_z, bits, halves.shape[1]),
        compiler_params=pltpu.CompilerParams(collective_id=collective_id, has_side_effects=True),
        name="sum_everywhere",
    )(halves)
    return out.reshape(-1)[: vector.shape[0]]


def chain_scatter(n_z, part_ref, out_ref, from_low, from_high, send_sem, low_recv, high_recv):
    z = lax.axis_index("gx")
    g = lax.axis_index("gy")
    rows = part_ref.shape[1]

    def up(dest):
        return pltpu.make_async_remote_copy(
            src_ref=part_ref.at[dest],
            dst_ref=from_low.at[dest],
            send_sem=send_sem.at[dest],
            recv_sem=low_recv.at[dest],
            device_id={"gx": z + 1, "gy": g},
            device_id_type=pl.DeviceIdType.MESH,
        )

    def down(dest):
        return pltpu.make_async_remote_copy(
            src_ref=part_ref.at[dest],
            dst_ref=from_high.at[dest],
            send_sem=send_sem.at[dest],
            recv_sem=high_recv.at[dest],
            device_id={"gx": z - 1, "gy": g},
            device_id_type=pl.DeviceIdType.MESH,
        )

    def start():
        for k in range(n_z - 1):
            run_if(z == 0, lambda k=k: up(n_z - 1 - k).start())
            run_if(z == n_z - 1, lambda k=k: down(k).start())

    def pass_up(dest):
        up(dest).wait_recv()
        add_into(part_ref.at[dest], (part_ref.at[dest], from_low.at[dest]), rows)
        up(dest).start()

    def pass_down(dest):
        down(dest).wait_recv()
        add_into(part_ref.at[dest], (part_ref.at[dest], from_high.at[dest]), rows)
        down(dest).start()

    def relay(time):
        for k in range(time):
            low, dest = time - k, n_z - 1 - k
            if 0 < low < dest:
                run_if(z == low, partial(pass_up, dest))
            high, dest = n_z - 1 - (time - k), k
            if dest < high < n_z - 1:
                run_if(z == high, partial(pass_down, dest))

    def finish():
        for dest in range(n_z):
            terms = [part_ref.at[dest]]
            terms += [from_low.at[dest]] if dest > 0 else []
            terms += [from_high.at[dest]] if dest < n_z - 1 else []

            def last(dest=dest, terms=terms):
                if dest > 0:
                    up(dest).wait_recv()
                if dest < n_z - 1:
                    down(dest).wait_recv()
                add_into(out_ref, terms, rows)

            run_if(z == dest, last)
        for dest in range(n_z):
            run_if(z != dest, lambda dest=dest: up(dest).wait_send())

    return start, [partial(relay, time) for time in range(1, n_z)], finish


def expert_kernel(n_z, span, own_ref, cot_ref, share_ref, gate_ref, up_ref, down_ref,
                  all_ref, pair_ref, dots_ref, down_out, out_ref,
                  moe_buf, cot_buf, share_buf, pair_stage, dots_buf,
                  gate_val, up_val, scaled, scaled_t, down_t,
                  held, from_core, from_a, from_b, from_z,
                  send_sem, recv_sem, local_sem, fetch_sem, store_sem,
                  core_send, a_send, b_send, z_send, core_recv, a_recv, b_recv, z_recv,
                  shares_in, dots_own, share_send, share_recv, dots_send, dots_recv):
    z = lax.axis_index("gx")
    g = lax.axis_index("gy")
    rows = own_ref.shape[1]
    block = 2 * rows
    step_rows = moe_buf.shape[1]
    steps = 2 * n_z
    flip_x = g + 2 - 4 * ((g // 2) % 2)
    flip_y = g + 4 - 8 * ((g // 4) % 2)
    flip_both = flip_x + flip_y - g
    core = {"gx": z, "gy": flip(g)}
    x_peer = {"gx": z, "gy": flip_x}
    y_peer = {"gx": z, "gy": flip_y}
    above = {"gx": z + 1, "gy": g}
    below = {"gx": z - 1, "gy": g}

    order = [z]
    candidates = []
    for d in range(1, n_z):
        candidates += [(z >= d, z - d), (z < n_z - d, z + d)]
    for k in range(1, n_z):
        rank, chosen = 0, 0
        for ok, owner in candidates:
            ok = ok.astype(jnp.int32)
            rank = rank + ok
            chosen = chosen + ok * (rank == k).astype(jnp.int32) * owner
        order.append(chosen)

    onward = [(z < n_z - 1, z > 0)]
    for owner in order[1:]:
        onward.append(
            (
                jnp.logical_and(owner < z, z < n_z - 1),
                jnp.logical_and(owner > z, z > 0),
            )
        )
    devices = n_z * span
    rank = z * span + g

    def device(number):
        return {"gx": lax.div(number, span), "gy": lax.rem(number, span)}

    barrier = pltpu.get_barrier_semaphore()

    @pl.loop(1, devices)
    def _(j):
        pl.semaphore_signal(
            barrier,
            inc=1,
            device_id=device(lax.rem(rank + j, devices)),
            device_id_type=pl.DeviceIdType.MESH,
        )

    pl.semaphore_wait(barrier, devices - 1)

    def share_copy(number):
        return pltpu.make_async_remote_copy(
            src_ref=share_ref.at[number],
            dst_ref=shares_in.at[rank],
            send_sem=share_send.at[number],
            recv_sem=share_recv.at[rank],
            device_id=device(number),
            device_id_type=pl.DeviceIdType.MESH,
        )

    def share_arrival(number):
        return pltpu.make_async_remote_copy(
            src_ref=share_ref.at[number],
            dst_ref=shares_in.at[number],
            send_sem=share_send.at[number],
            recv_sem=share_recv.at[number],
            device_id=core,
            device_id_type=pl.DeviceIdType.MESH,
        )

    def dots_copy(number):
        return pltpu.make_async_remote_copy(
            src_ref=dots_own.at[number],
            dst_ref=dots_ref.at[rank],
            send_sem=dots_send.at[number],
            recv_sem=dots_recv.at[rank],
            device_id=device(number),
            device_id_type=pl.DeviceIdType.MESH,
        )

    def dots_arrival(number):
        return pltpu.make_async_remote_copy(
            src_ref=dots_own.at[number],
            dst_ref=dots_ref.at[number],
            send_sem=dots_send.at[number],
            recv_sem=dots_recv.at[number],
            device_id=core,
            device_id_type=pl.DeviceIdType.MESH,
        )

    def for_others(action):
        @pl.loop(1, devices)
        def _(j):
            action(lax.rem(rank + j, devices))

    for_others(lambda number: share_copy(number).start())
    shares_in[rank] = share_ref[rank]

    def at(owner, gg, h):
        return pl.ds(pl.multiple_of((owner * span + gg) * block + h * rows, rows), rows)

    def copy(k, slot, owner, gg, h, peer, own=False):
        return pltpu.make_async_remote_copy(
            src_ref=own_ref.at[h] if own else all_ref.at[at(owner, gg, h)],
            dst_ref=all_ref.at[at(owner, gg, h)],
            send_sem=send_sem.at[k, slot],
            recv_sem=recv_sem.at[owner * span + gg, h],
            device_id=peer,
            device_id_type=pl.DeviceIdType.MESH,
        )

    sends = []

    def send(ok, *where, **options):
        k = where[0]
        slot = sum(1 for entry in sends if entry[2] == k)
        make = partial(copy, k, slot, *where[1:], **options)
        sends.append((ok, make, k))
        run_if(ok, lambda: make().start())

    def arrive(owner, gg, h):
        copy(0, 0, owner, gg, h, core).wait_recv()

    locals_ = [
        pltpu.make_async_copy(own_ref.at[h], all_ref.at[at(z, g, h)], local_sem.at[h])
        for h in range(2)
    ]

    def first(k):
        owner = order[k]
        own = k == 0
        if own:
            for item in locals_:
                item.start()
        else:
            arrive(owner, g, 0)
            arrive(owner, g, 1)
        go_up, go_down = onward[k]
        for h in range(2):
            send(go_up, k, owner, g, h, above, own=own)
            send(go_down, k, owner, g, h, below, own=own)
        send(True, k, owner, g, 0, x_peer, own=own)
        send(True, k, owner, g, 1, y_peer, own=own)
        send(True, k, owner, g, 1, x_peer, own=own)
        send(True, k, owner, g, 0, y_peer, own=own)
        send(True, k, owner, g, 0, core, own=own)
        send(True, k, owner, g, 1, core, own=own)

    def second(k):
        owner = order[k]
        arrive(owner, flip_x, 0)
        send(True, k, owner, flip_x, 0, y_peer)
        send(True, k, owner, flip_x, 0, core)
        arrive(owner, flip_y, 1)
        send(True, k, owner, flip_y, 1, x_peer)
        send(True, k, owner, flip_y, 1, core)

    def third(k):
        owner = order[k]
        for gg, h in ((flip_y, 0), (flip_x, 1), (flip_both, 0), (flip_both, 1)):
            arrive(owner, gg, h)
            send(True, k, owner, gg, h, core)

    def complete(k):
        for gg in (g, flip_x, flip_y, flip_both):
            for h in range(2):
                arrive(order[k], flip(gg), h)
        if k == 0:
            for item in locals_:
                item.wait()

    def owner_of(s):
        if isinstance(s, int):
            return order[s // 2]
        k = lax.div(s, 2)
        return sum((k == j).astype(jnp.int32) * order[j] for j in range(n_z))

    def place(s):
        k, side = (s // 2, s % 2) if isinstance(s, int) else (lax.div(s, 2), lax.rem(s, 2))
        if isinstance(s, int):
            owner = order[k]
        else:
            owner = sum((k == j).astype(jnp.int32) * order[j] for j in range(n_z))
        return pl.ds(pl.multiple_of(owner * (span * block) + side * step_rows, step_rows), step_rows)

    def parity(s):
        return s % 2 if isinstance(s, int) else lax.rem(s, 2)

    def fetches(s):
        slot = parity(s)
        return [
            pltpu.make_async_copy(source.at[place(s)], target.at[slot], fetch_sem.at[j, slot])
            for j, (source, target) in enumerate(
                ((all_ref, moe_buf), (cot_ref, cot_buf))
            )
        ]

    def stores(s):
        slot = parity(s)
        return [
            pltpu.make_async_copy(
                pair_stage.at[slot], pair_ref.at[place(s)], store_sem.at[0, slot]
            )
        ]

    f32 = jnp.float32
    dot = partial(lax.dot_general, preferred_element_type=f32)
    plain = (((1,), (0,)), ((), ()))
    last_dims = (((1,), (1,)), ((), ()))
    first_dims = (((0,), (0,)), ((), ()))
    half_width = scaled.shape[1]
    width = moe_buf.shape[2]
    tile = 256

    quads = (flip_both, flip_x, flip_y, g)

    def remote(src, dst, ssem, rsem, peer):
        return pltpu.make_async_remote_copy(
            src_ref=src,
            dst_ref=dst,
            send_sem=ssem,
            recv_sem=rsem,
            device_id=peer,
            device_id_type=pl.DeviceIdType.MESH,
        )

    def core_copy(k, q):
        return remote(
            held.at[k, flip(quads[q])],
            from_core.at[k, q],
            core_send.at[k, q],
            core_recv.at[k, q],
            core,
        )

    a_plan = ((0, 0, 0, x_peer), (0, 1, 0, y_peer), (1, 0, 1, x_peer), (2, 1, 1, y_peer))

    def a_copy(k, j):
        q, h, slot, peer = a_plan[j]
        return remote(
            held.at[k, quads[q], h],
            from_a.at[k, h, slot],
            a_send.at[k, j],
            a_recv.at[k, h, slot],
            peer,
        )

    b_plan = ((2, y_peer), (1, x_peer))

    def b_copy(k, h):
        q, peer = b_plan[h]
        return remote(
            held.at[k, quads[q], h], from_b.at[k, h], b_send.at[k, h], b_recv.at[k, h], peer
        )

    def z_copy(k):
        return remote(
            held.at[k, g], from_z.at[z], z_send.at[k], z_recv.at[z], {"gx": order[k], "gy": g}
        )

    def stage_core(k):
        for q in range(4):
            core_copy(k, q).start()

    def stage_a(k):
        for q in range(4):
            core_copy(k, q).wait_recv()
            for h in range(2):
                mine = held.at[k, quads[q], h]
                add_into(mine, (mine, from_core.at[k, q, h]), rows)
            for j in range(4):
                if a_plan[j][0] == q:
                    a_copy(k, j).start()

    def stage_b(k):
        for q, h, slot in ((2, 0, 0), (1, 1, 0), (3, 0, 1), (3, 1, 1)):
            mine, arrived = held.at[k, quads[q], h], from_a.at[k, h, slot]
            remote(mine, arrived, a_send.at[k, 0], a_recv.at[k, h, slot], core).wait_recv()
            add_into(mine, (mine, arrived), rows)
            if slot == 0:
                b_copy(k, h).start()

    def stage_c(k):
        for h in range(2):
            b_copy(k, h).wait_recv()
            mine = held.at[k, g, h]
            add_into(mine, (mine, from_b.at[k, h]), rows)
        if k > 0:
            z_copy(k).start()

    backs = (
        (stage_core, lambda k: 2 * k + 1, 2),
        (stage_a, lambda k: 2 * k + 1, 4),
        (stage_b, lambda k: 2 * k + 2, 4),
        (stage_c, lambda k: 2 * k + 3, 4),
    )

    def events(s, phase):
        for action, start, when in backs:
            for k in range(n_z):
                if when == phase and start(k) < steps:
                    pl.when(s == start(k))(partial(action, k))
        for k in range(1, n_z):
            if k >= 2 and phase == 1:
                pl.when(s == k - 2)(partial(first, k))
            if phase == 2:
                pl.when(s == 2 * (k - 1))(partial(second, k))
            if phase == 2:
                pl.when(s == 2 * (k - 1) + 1)(partial(third, k))
            if phase == 4:
                pl.when(s == 2 * k - 1)(partial(complete, k))

    first(0)

    @pl.loop(0, width // tile)
    def _(t):
        cols = pl.ds(pl.multiple_of(t * tile, tile), tile)
        down_t[cols, :] = down_ref[:, cols].T

    second(0)
    if n_z > 1:
        first(1)
    third(0)
    complete(0)
    for item in fetches(0):
        item.start()
    for_others(lambda number: share_arrival(number).wait_recv())

    @pl.loop(0, steps)
    def _(s):
        slot = lax.rem(s, 2)
        moe, cot, share = moe_buf.at[slot], cot_buf.at[slot], share_buf
        first_device = owner_of(s) * span + slot * (span // 2)
        for item in fetches(s):
            item.wait()

        @pl.when(s >= 2)
        def _():
            for item in stores(s - 2):
                item.wait()

        for j in range(span // 2):
            column = jnp.broadcast_to(shares_in[first_device + j], (block, block)).T
            share[j * block : (j + 1) * block, :] = column
        wide = jnp.concatenate([share[...]] * (tile // share.shape[1]), axis=1)

        @pl.loop(0, half_width // tile)
        def _(t):
            cols = pl.ds(pl.multiple_of(t * tile, tile), tile)
            gated = dot(moe[...], gate_ref[:, cols], plain)
            lifted = dot(moe[...], up_ref[:, cols], plain)
            gate_val[:, cols] = gated
            up_val[:, cols] = lifted
            scaled[:, cols] = (gated * jax.nn.sigmoid(gated) * lifted * wide).astype(jnp.bfloat16)

        events(s, 1)
        scaled_t[...] = scaled[...].T

        @pl.loop(0, width // (2 * tile))
        def _(t):
            cols = pl.ds(pl.multiple_of(t * 2 * tile, 2 * tile), 2 * tile)
            sent = dot(scaled[...], down_ref[:, cols], plain).astype(jnp.bfloat16)
            held[lax.div(s, 2), pl.ds(slot * (span // 2), span // 2), :, :, cols] = sent.reshape(
                (span // 2, 2, rows, 2 * tile)
            )

        events(s, 2)
        dots_buf[...] = jnp.zeros(dots_buf.shape, f32)

        @pl.loop(0, half_width // tile)
        def _(t):
            cols = pl.ds(pl.multiple_of(t * tile, tile), tile)
            pulled = dot(cot[...], down_t[:, cols], plain)
            gated = gate_val[:, cols]
            lifted = up_val[:, cols]
            sig = jax.nn.sigmoid(gated)
            silu = gated * sig
            product = pulled * (silu * lifted)
            lanes = share.shape[1]
            dots_buf[...] = dots_buf[...] + sum(
                product[:, j * lanes : (j + 1) * lanes] for j in range(tile // lanes)
            )
            pulled = pulled * wide
            pair_stage[slot, :, cols] = (pulled * lifted * sig * (1.0 + gated * (1.0 - sig))).astype(
                jnp.bfloat16
            )
            more = pl.ds(pl.multiple_of(half_width + t * tile, tile), tile)
            pair_stage[slot, :, more] = (pulled * silu).astype(jnp.bfloat16)

        for item in stores(s):
            item.start()
        for j in range(span // 2):
            number = first_device + j
            rows_of = dots_buf[j * block : (j + 1) * block, :]
            dots_own[number] = jnp.sum(rows_of.T, axis=0, keepdims=True)

        for j in range(span // 2):
            number = first_device + j

            @pl.when(number != rank)
            def _():
                dots_copy(number).start()

        events(s, 3)
        events(s, 4)

        @pl.when(s < steps - 1)
        def _():
            for item in fetches(s + 1):
                item.start()

        @pl.loop(0, width // (2 * tile))
        def _(t):
            cols = pl.ds(pl.multiple_of(t * 2 * tile, 2 * tile), 2 * tile)
            grown = dot(scaled_t[...], cot[:, cols], plain)
            down_out[:, cols] = jnp.where(s == 0, 0.0, down_out[:, cols]) + grown

    for t in range(steps, 2 * steps):
        for action, start, _ in backs[::-1]:
            for k in range(n_z):
                if start(k) == t:
                    action(k)
    for s in (steps - 2, steps - 1):
        for item in stores(s):
            item.wait()
    for k in range(1, n_z):
        arrived = from_z.at[order[k]]
        remote(held.at[k, g], arrived, z_send.at[k], z_recv.at[order[k]], core).wait_recv()
    for h in range(2):
        terms = [held.at[0, g, h]] + [from_z.at[order[k], h] for k in range(1, n_z)]
        add_into(out_ref.at[h], terms, rows)
    for k in range(n_z):
        for q in range(4):
            core_copy(k, q).wait_send()
        for j in range(4):
            a_copy(k, j).wait_send()
        for h in range(2):
            b_copy(k, h).wait_send()
        if k > 0:
            z_copy(k).wait_send()
    for ok, make, k in sends:
        run_if(ok, lambda make=make: make().wait_send())
    dots_ref[rank] = dots_own[rank]
    for_others(lambda number: dots_arrival(number).wait_recv())
    for_others(lambda number: share_copy(number).wait_send())
    for_others(lambda number: dots_copy(number).wait_send())


def run_experts(moe_in, all_cot, shares, gate_w, up_w, down_w, collective_id):
    n_z = lax.axis_size("gx")
    span = lax.axis_size("gy")
    rows, width = moe_in.shape
    half = down_w.shape[0]
    total = n_z * span * rows
    step = span * rows // 2
    lanes = 128
    devices = n_z * span
    bf16, f32 = jnp.bfloat16, jnp.float32
    dma = pltpu.SemaphoreType.DMA
    vmem = pl.BlockSpec(memory_space=pltpu.VMEM)
    hbm = pl.BlockSpec(memory_space=pl.ANY)
    return pl.pallas_call(
        partial(expert_kernel, n_z, span),
        out_shape=(
            jax.ShapeDtypeStruct((total, width), bf16),
            jax.ShapeDtypeStruct((total, 2 * half), bf16),
            jax.ShapeDtypeStruct((devices, 1, rows), f32),
            jax.ShapeDtypeStruct((half, width), f32),
            jax.ShapeDtypeStruct((2, rows // 2, width), f32),
        ),
        in_specs=[vmem, hbm, vmem, vmem, vmem, vmem],
        out_specs=(hbm, hbm, vmem, vmem, vmem),
        scratch_shapes=[
            pltpu.VMEM((2, step, width), bf16),
            pltpu.VMEM((2, step, width), bf16),
            pltpu.VMEM((step, lanes), f32),
            pltpu.VMEM((2, step, 2 * half), bf16),
            pltpu.VMEM((step, lanes), f32),
            pltpu.VMEM((step, half), f32),
            pltpu.VMEM((step, half), f32),
            pltpu.VMEM((step, half), bf16),
            pltpu.VMEM((half, step), bf16),
            pltpu.VMEM((width, half), bf16),
            pltpu.VMEM((n_z, span, 2, rows // 2, width), bf16),
            pltpu.VMEM((n_z, 4, 2, rows // 2, width), bf16),
            pltpu.VMEM((n_z, 2, 2, rows // 2, width), bf16),
            pltpu.VMEM((n_z, 2, rows // 2, width), bf16),
            pltpu.VMEM((n_z, 2, rows // 2, width), bf16),
            dma((n_z, 18)),
            dma((n_z * span, 2)),
            dma((2,)),
            dma((3, 2)),
            dma((2, 2)),
            dma((n_z, 4)),
            dma((n_z, 4)),
            dma((n_z, 2)),
            dma((n_z,)),
            dma((n_z, 4)),
            dma((n_z, 2, 2)),
            dma((n_z, 2)),
            dma((n_z,)),
            pltpu.VMEM((devices, 1, rows), f32),
            pltpu.VMEM((devices, 1, rows), f32),
            dma((devices,)),
            dma((devices,)),
            dma((devices,)),
            dma((devices,)),
        ],
        compiler_params=pltpu.CompilerParams(
            collective_id=collective_id, has_side_effects=True, vmem_limit_bytes=67043328
        ),
        name="experts",
    )(moe_in.reshape(2, rows // 2, width), all_cot, shares, gate_w, up_w, down_w)


def pull_kernel(n_i, rows, all_ref, pair_ref, gate_ref, up_ref, out_ref, gate_out, up_out,
                held, from_core, from_a, from_b, from_z, moe_buf, pair_buf,
                fetch_sem, core_send, a_send, b_send, z_send, core_recv, a_recv, b_recv, z_recv):
    z = lax.axis_index("gx")
    g = lax.axis_index("gy")
    flip_x = g + 2 - 4 * ((g // 2) % 2)
    flip_y = g + 4 - 8 * ((g // 4) % 2)
    quads = (flip_x + flip_y - g, flip_x, flip_y, g)
    core = {"gx": z, "gy": flip(g)}
    x_peer = {"gx": z, "gy": flip_x}
    y_peer = {"gx": z, "gy": flip_y}
    along = [{"gx": lax.rem(z + j, n_i), "gy": g} for j in range(1, n_i)]
    barrier_with([(z >= 0, peer) for peer in (core, x_peer, y_peer, *along)])
    item_rows = moe_buf.shape[1]
    width = moe_buf.shape[2]
    half_width = gate_out.shape[1]
    owners = [lax.rem(z + n_i - 1 - i + n_i, n_i) for i in range(n_i)]

    def remote(src, dst, ssem, rsem, peer):
        return pltpu.make_async_remote_copy(
            src_ref=src,
            dst_ref=dst,
            send_sem=ssem,
            recv_sem=rsem,
            device_id=peer,
            device_id_type=pl.DeviceIdType.MESH,
        )

    def fetches(i):
        place = pl.ds(pl.multiple_of(owners[i] * item_rows, item_rows), item_rows)
        return [
            pltpu.make_async_copy(all_ref.at[place], moe_buf.at[i % 2], fetch_sem.at[0, i % 2]),
            pltpu.make_async_copy(pair_ref.at[place], pair_buf.at[i % 2], fetch_sem.at[1, i % 2]),
        ]

    def core_copy(i, q):
        return remote(
            held.at[i, flip(quads[q])],
            from_core.at[i, q],
            core_send.at[i, q],
            core_recv.at[i, q],
            core,
        )

    a_plan = ((0, 0, 0, x_peer), (0, 1, 0, y_peer), (1, 0, 1, x_peer), (2, 1, 1, y_peer))

    def a_copy(i, k):
        q, h, slot, peer = a_plan[k]
        return remote(
            held.at[i, quads[q], h],
            from_a.at[i, h, slot],
            a_send.at[i, k],
            a_recv.at[i, h, slot],
            peer,
        )

    b_plan = ((2, y_peer), (1, x_peer))

    def b_copy(i, h):
        q, peer = b_plan[h]
        return remote(
            held.at[i, quads[q], h], from_b.at[i, h], b_send.at[i, h], b_recv.at[i, h], peer
        )

    def z_copy(i):
        return remote(
            held.at[i, g], from_z.at[z], z_send.at[i], z_recv.at[z], {"gx": owners[i], "gy": g}
        )

    dot = partial(lax.dot_general, preferred_element_type=jnp.float32)
    last_dims = (((1,), (1,)), ((), ()))
    first_dims = (((0,), (0,)), ((), ()))

    def multiply(i):
        for copy in fetches(i):
            copy.wait()
        pair = pair_buf.at[i % 2]
        tile = 256

        @pl.loop(0, width // tile)
        def _(t):
            cols = pl.ds(pl.multiple_of(t * tile, tile), tile)
            total = dot(pair[:, :half_width], gate_ref[cols, :], last_dims)
            total = total + dot(pair[:, half_width:], up_ref[cols, :], last_dims)
            held[i, :, :, :, cols] = total.astype(jnp.bfloat16).reshape(held.shape[1:4] + (tile,))

        for q in range(4):
            core_copy(i, q).start()

    def accumulate(i):
        moe, pair = moe_buf.at[i % 2], pair_buf.at[i % 2]
        tile = 256

        @pl.loop(0, width // tile)
        def _(t):
            cols = pl.ds(pl.multiple_of(t * tile, tile), tile)
            grown = dot(moe[:, cols], pair[...], first_dims)
            if i == 0:
                gate_out[cols, :] = grown[:, :half_width]
                up_out[cols, :] = grown[:, half_width:]
            else:
                gate_out[cols, :] = gate_out[cols, :] + grown[:, :half_width]
                up_out[cols, :] = up_out[cols, :] + grown[:, half_width:]

        if i + 2 < n_i:
            for copy in fetches(i + 2):
                copy.start()

    def stage_a(i):
        for q in range(4):
            core_copy(i, q).wait_recv()
            for h in range(2):
                mine = held.at[i, quads[q], h]
                add_into(mine, (mine, from_core.at[i, q, h]), rows)
            for k in range(4):
                if a_plan[k][0] == q:
                    a_copy(i, k).start()

    def stage_b(i):
        for q, h, slot in ((2, 0, 0), (1, 1, 0), (3, 0, 1), (3, 1, 1)):
            mine, arrived = held.at[i, quads[q], h], from_a.at[i, h, slot]
            remote(mine, arrived, a_send.at[i, 0], a_recv.at[i, h, slot], core).wait_recv()
            add_into(mine, (mine, arrived), rows)
            if slot == 0:
                b_copy(i, h).start()

    def stage_c(i):
        for h in range(2):
            b_copy(i, h).wait_recv()
            mine = held.at[i, g, h]
            add_into(mine, (mine, from_b.at[i, h]), rows)
        if i < n_i - 1:
            z_copy(i).start()
        else:
            for j in range(n_i - 1):
                arrived = from_z.at[owners[j]]
                remote(held.at[j, g], arrived, z_send.at[j], z_recv.at[owners[j]], core).wait_recv()
            for h in range(2):
                terms = [held.at[i, g, h]] + [from_z.at[owners[j], h] for j in range(n_i - 1)]
                add_into(out_ref.at[h], terms, rows)

    for i in range(min(2, n_i)):
        for copy in fetches(i):
            copy.start()
    for t in range(n_i + 3):
        if t < n_i:
            multiply(t)
        if 0 <= t - 1 < n_i:
            stage_a(t - 1)
        if 0 <= t - 2 < n_i:
            stage_b(t - 2)
        if 0 <= t - 1 < n_i:
            accumulate(t - 1)
        if 0 <= t - 3 < n_i:
            stage_c(t - 3)
    for i in range(n_i):
        for q in range(4):
            core_copy(i, q).wait_send()
        for k in range(4):
            a_copy(i, k).wait_send()
        for h in range(2):
            b_copy(i, h).wait_send()
        if i < n_i - 1:
            z_copy(i).wait_send()


def pull_experts(all_moe, pair, gate_w, up_w, collective_id):
    n_i = lax.axis_size("gx")
    span = lax.axis_size("gy")
    total, width = all_moe.shape
    half_width = gate_w.shape[1]
    rows = total // (n_i * span) // 2
    half = (rows, width)
    bf16 = jnp.bfloat16
    dma = pltpu.SemaphoreType.DMA
    vmem = pl.BlockSpec(memory_space=pltpu.VMEM)
    hbm = pl.BlockSpec(memory_space=pl.ANY)
    out, gate_part, up_part = pl.pallas_call(
        partial(pull_kernel, n_i, rows),
        out_shape=(
            jax.ShapeDtypeStruct((2,) + half, jnp.float32),
            jax.ShapeDtypeStruct((width, half_width), jnp.float32),
            jax.ShapeDtypeStruct((width, half_width), jnp.float32),
        ),
        in_specs=[hbm, hbm, vmem, vmem],
        out_specs=(vmem, vmem, vmem),
        scratch_shapes=[
            pltpu.VMEM((n_i, span, 2) + half, bf16),
            pltpu.VMEM((n_i, 4, 2) + half, bf16),
            pltpu.VMEM((n_i, 2, 2) + half, bf16),
            pltpu.VMEM((n_i, 2) + half, bf16),
            pltpu.VMEM((n_i, 2) + half, bf16),
            pltpu.VMEM((2, span * 2 * rows, width), bf16),
            pltpu.VMEM((2, span * 2 * rows, 2 * half_width), bf16),
            dma((2, 2)),
            dma((n_i, 4)),
            dma((n_i, 4)),
            dma((n_i, 2)),
            dma((n_i,)),
            dma((n_i, 4)),
            dma((n_i, 2, 2)),
            dma((n_i, 2)),
            dma((n_i,)),
        ],
        compiler_params=pltpu.CompilerParams(
            collective_id=collective_id, has_side_effects=True, vmem_limit_bytes=67043328
        ),
        name="pull_experts",
    )(all_moe, pair, gate_w, up_w)
    return out.reshape(2 * rows, width), gate_part, up_part


def turn(values, cosine, sine):
    return values * cosine + pltpu.roll(values, values.shape[-1] // 2, 1) * sine


def spread_docs(docs_ref, row_docs, col_docs):
    lanes = docs_ref.shape[1]
    for j in range(docs_ref.shape[0]):
        line = docs_ref[j : j + 1, :].astype(jnp.float32)
        row_docs[j * lanes : (j + 1) * lanes, :] = jnp.broadcast_to(line, (lanes, lanes)).T
        col_docs[:, j * lanes : (j + 1) * lanes] = jnp.broadcast_to(line, (8, lanes))


def attend_kernel(
    heads,
    pieces,
    own_acts,
    query_weight,
    key_weight,
    value_weight,
    own_out_weight,
    own_cot,
    query_gain,
    key_gain,
    cosine_ref,
    sine_ref,
    docs_ref,
    attended_ref,
    acts_out,
    weight_out,
    full_out,
    all_cot,
    query_raw,
    key_raw,
    ready_ref,
    mixed_ref,
    totals_ref,
    peaks_ref,
    own_weight,
    row_docs,
    col_docs,
    part_ref,
    held,
    from_core,
    from_a,
    from_b,
    from_z,
    near_send,
    near_recv,
    near_local,
    far_send,
    far_recv,
    far_local,
    in_send,
    in_recv,
    in_local,
    out_send,
    out_recv,
    out_local,
    load_sem,
    core_send,
    a_send,
    b_send,
    z_send,
    core_recv,
    a_recv,
    b_recv,
    z_recv,
):
    n_z = lax.axis_size("gx")
    span = lax.axis_size("gy")
    for j, item in enumerate((query_weight, key_weight, value_weight)):
        own_weight[:, j * item.shape[1] : (j + 1) * item.shape[1]] = item[...]
    greet(n_z)
    in_start, in_relays, in_finish = chain_gather(
        n_z, own_weight, weight_out, in_send, in_recv, in_local
    )
    out_start, out_relays, out_finish = chain_gather(
        n_z, own_out_weight, full_out, out_send, out_recv, out_local
    )
    near, near_finish = gather_steps(1, span, own_acts, acts_out, near_send, near_recv, near_local)
    far, far_finish = gather_steps(n_z, span, own_cot, all_cot, far_send, far_recv, far_local)
    back = []
    scatter_kernel(
        False,
        pieces,
        part_ref.shape[3],
        part_ref,
        attended_ref,
        held,
        from_core,
        from_a,
        from_b,
        from_z,
        load_sem,
        core_send,
        a_send,
        b_send,
        z_send,
        core_recv,
        a_recv,
        b_recv,
        z_recv,
        parts=back,
    )
    f32, bf16 = jnp.float32, jnp.bfloat16
    dot = partial(lax.dot_general, preferred_element_type=f32)
    plain = (((1,), (0,)), ((), ()))
    last_dims = (((1,), (1,)), ((), ()))
    length = query_raw.shape[0]
    width = acts_out.shape[3]
    local = heads * HD
    block = 256
    scale = HD ** (-0.5)

    in_start()
    near[0]()
    far[0]()
    spread_docs(docs_ref, row_docs, col_docs)
    near[1]()
    near[2]()
    later = far[1:]
    for relay in in_relays:
        relay()
        for step in later[:1]:
            step()
        later = later[1:]
    out_start()
    in_finish()
    near_finish()
    waiting = [list(out_relays), list(later)]

    def pull(which):
        if waiting[which]:
            waiting[which].pop(0)()

    def project(source):
        cols = slice(source * local, (source + 1) * local)
        acts = acts_out[...].reshape(length, width)
        total = jnp.zeros((length, local), f32)
        depth = own_weight.shape[0]
        for owner in range(n_z):
            total = total + dot(
                acts[:, owner * depth : (owner + 1) * depth], weight_out[owner, :, cols], plain
            )
        return total

    for source, raw, gain in ((0, query_raw, query_gain), (1, key_raw, key_gain)):
        raw[...] = project(source)
        for h in range(heads):
            cols = slice(h * HD, (h + 1) * HD)

            @pl.loop(0, length // block)
            def _(t):
                at = pl.ds(pl.multiple_of(t * block, block), block)
                value = raw[at, cols]
                normed = value * lax.rsqrt(jnp.mean(value * value, axis=-1, keepdims=True) + EPSILON)
                turned = turn(normed * gain[...], cosine_ref[at, :], sine_ref[at, :])
                where = source * local + h * HD
                ready_ref[at, where : where + HD] = turned.astype(bf16)

        pull(source)

    ready_ref[:, 2 * local :] = project(2).astype(bf16)
    pull(0)
    lanes = lax.broadcasted_iota(jnp.int32, (block, HD), 1)
    peaks_ref[...] = jnp.full(peaks_ref.shape, NEGATIVE, f32)

    def mix(t):
        at = pl.ds(pl.multiple_of(t * block, block), block)
        same = row_docs[at, :1] == col_docs[:1, :]
        kept = jnp.zeros((block, HD), f32)
        for h in range(heads):
            query = ready_ref[at, h * HD : (h + 1) * HD]
            key = ready_ref[:, local + h * HD : local + (h + 1) * HD]
            value = ready_ref[:, 2 * local + h * HD : 2 * local + (h + 1) * HD]
            scores = jnp.where(same, dot(query, key, last_dims) * scale, NEGATIVE)
            highest = jnp.max(scores, axis=-1, keepdims=True)
            weights = jnp.exp(scores - highest)
            total = jnp.sum(weights, axis=-1, keepdims=True)
            shares = (weights * (1.0 / total)).astype(bf16)
            mixed_ref[at, h * HD : (h + 1) * HD] = dot(shares, value, plain).astype(bf16)
            kept = jnp.where(lanes == h, highest + jnp.log(total), kept)
            top = jnp.max(highest, axis=0, keepdims=True)
            peaks_ref[h : h + 1, :] = jnp.maximum(peaks_ref[h : h + 1, :], top)
        totals_ref[at, :] = kept

    blocks = length // block
    between = waiting[1].pop(0) if waiting[1] else lambda: None

    @pl.loop(0, blocks)
    def _(t):
        mix(t)
        pl.when(t == blocks // 2 - 1)(between)

    pull(1)
    for relay in waiting[0]:
        relay()
    out_finish()
    rows = part_ref.shape[3]
    per_owner = own_out_weight.shape[1] // block

    @pl.loop(0, n_z * per_owner)
    def _(t):
        cols = pl.ds(pl.multiple_of(t * block, block), block)
        inside = pl.ds(pl.multiple_of(lax.rem(t, per_owner) * block, block), block)
        sent = dot(mixed_ref[...], full_out[lax.div(t, per_owner), :, inside], plain).astype(bf16)
        sent = sent.reshape(span, pieces, 2, rows, block)
        for p in range(pieces):
            part_ref[p, :, :, :, cols] = sent[:, p]

    for step in back[:-1]:
        step()
        pull(1)
    for step in waiting[1]:
        step()
    back[-1]()
    far_finish()


def attend(
    acts, weights, out_weight, cot, query_gain, key_gain, tables, docs, collective_id, pieces=4
):
    tokens, width = acts.shape
    depth, local = weights[0].shape
    heads = local // HD
    n_z = lax.axis_size("gx")
    span = lax.axis_size("gy")
    length = span * tokens
    rows = tokens // (pieces * 2)
    half = (2, tokens // 2, width)
    piece = (rows, width)
    f32, bf16 = jnp.float32, jnp.bfloat16
    dma = pltpu.SemaphoreType.DMA
    vmem = pl.BlockSpec(memory_space=pltpu.VMEM)
    hbm = pl.BlockSpec(memory_space=pl.ANY)
    attended, seq, full, full_out, all_cot, *saved, peaks = pl.pallas_call(
        partial(attend_kernel, heads, pieces),
        out_shape=(
            jax.ShapeDtypeStruct((pieces, 2) + piece, f32),
            jax.ShapeDtypeStruct((span,) + half, bf16),
            jax.ShapeDtypeStruct((n_z, depth, 3 * local), bf16),
            jax.ShapeDtypeStruct((n_z,) + out_weight.shape, bf16),
            jax.ShapeDtypeStruct((n_z * span,) + half, bf16),
            jax.ShapeDtypeStruct((length, local), f32),
            jax.ShapeDtypeStruct((length, local), f32),
            jax.ShapeDtypeStruct((length, 3 * local), bf16),
            jax.ShapeDtypeStruct((length, local), bf16),
            jax.ShapeDtypeStruct((length, HD), f32),
            jax.ShapeDtypeStruct((8, HD), f32),
        ),
        in_specs=[vmem] * 11,
        out_specs=(vmem, vmem, vmem, vmem, hbm) + (vmem,) * 6,
        scratch_shapes=[
            pltpu.VMEM((depth, 3 * local), bf16),
            pltpu.VMEM((length, 128), f32),
            pltpu.VMEM((8, length), f32),
            pltpu.VMEM((pieces, span, 2) + piece, bf16),
            pltpu.VMEM((pieces, 4, 2) + piece, bf16),
            pltpu.VMEM((pieces, 4, 2) + piece, bf16),
            pltpu.VMEM((pieces, 2, 2) + piece, bf16),
            pltpu.VMEM((pieces, 2) + piece, bf16),
            pltpu.VMEM((1, 2, 16, 128), bf16),
            dma((24,)),
            dma((span, 2)),
            dma,
            dma((24 * (2 * n_z - 1),)),
            dma((n_z * span, 2)),
            dma,
            dma((2 * n_z,)),
            dma((n_z,)),
            dma,
            dma((2 * n_z,)),
            dma((n_z,)),
            dma,
            dma((pieces, 4)),
            dma((pieces, 4)),
            dma((pieces, 4)),
            dma((pieces, 2)),
            dma((pieces,)),
            dma((pieces, 4)),
            dma((pieces, 2, 2)),
            dma((pieces, 2)),
            dma((pieces,)),
        ],
        compiler_params=pltpu.CompilerParams(
            collective_id=collective_id, has_side_effects=True, vmem_limit_bytes=60 << 20
        ),
        name="attend",
    )(
        acts.reshape(half),
        *weights,
        out_weight,
        cot.reshape(half),
        query_gain.reshape(1, HD),
        key_gain.reshape(1, HD),
        *tables,
        docs,
    )
    return (
        attended.reshape(tokens, width),
        seq.reshape(length, width),
        full.reshape(n_z * depth, 3 * local),
        all_cot.reshape(n_z * span * tokens, width),
        (*saved, full_out),
        peaks,
    )


def attend_back_kernel(
    heads,
    pieces,
    own_grad,
    out_weight_ref,
    mixed_ref,
    ready_ref,
    query_raw,
    key_raw,
    totals_ref,
    query_gain,
    key_gain,
    attn_gain,
    cosine_ref,
    sine_ref,
    docs_ref,
    small_ref,
    acts_hbm,
    weight_hbm,
    grad_acts,
    query_sum,
    key_sum_out,
    value_sum_out,
    out_sum,
    small_sum,
    late_sum,
    weight_sum,
    gain_ref,
    late_ref,
    row_docs,
    col_docs,
    seq_ref,
    part_ref,
    acts_ref,
    weight_ref,
    grad_mixed,
    grad_heads,
    one_head,
    turned,
    key_sum,
    value_sum,
    out_sums,
    out_low,
    out_high,
    in_sums,
    in_low,
    in_high,
    held,
    from_core,
    from_a,
    from_b,
    from_z,
    copy_sem,
    near_send,
    near_recv,
    near_local,
    out_send,
    out_low_recv,
    out_high_recv,
    in_send,
    in_low_recv,
    in_high_recv,
    load_sem,
    core_send,
    a_send,
    b_send,
    z_send,
    core_recv,
    a_recv,
    b_recv,
    z_recv,
    *small_scratch,
):
    n_z = lax.axis_size("gx")
    span = lax.axis_size("gy")
    z = lax.axis_index("gx")
    g = lax.axis_index("gy")
    peers = [{"gx": z, "gy": g + bit - 2 * bit * ((g // bit) % 2)} for bit in (1, 2, 4)]
    peers += [{"gx": lax.rem(z + j, n_z), "gy": g} for j in range(1, n_z)]
    barrier_with([(z >= 0, peer) for peer in peers])
    out_start, out_relays, out_finish = chain_scatter(
        n_z, out_sums, out_sum, out_low, out_high, out_send, out_low_recv, out_high_recv
    )
    chains = [
        chain_scatter(
            n_z,
            in_sums.at[h],
            weight_sum.at[h],
            in_low.at[h],
            in_high.at[h],
            in_send.at[h],
            in_low_recv.at[h],
            in_high_recv.at[h],
        )
        for h in range(heads)
    ]
    near, near_finish = gather_steps(1, span, own_grad, seq_ref, near_send, near_recv, near_local)
    bits = span.bit_length() - 1
    half_scratch = len(small_scratch) // 2
    small = sum_steps(n_z, bits, small_ref, small_sum, *small_scratch[:half_scratch])
    late = sum_steps(n_z, bits, late_ref, late_sum, *small_scratch[half_scratch:])
    back = []
    scatter_kernel(
        False,
        pieces,
        part_ref.shape[3],
        part_ref,
        grad_acts,
        held,
        from_core,
        from_a,
        from_b,
        from_z,
        load_sem,
        core_send,
        a_send,
        b_send,
        z_send,
        core_recv,
        a_recv,
        b_recv,
        z_recv,
        parts=back,
    )
    f32, bf16 = jnp.float32, jnp.bfloat16
    dot = partial(lax.dot_general, preferred_element_type=f32)
    plain = (((1,), (0,)), ((), ()))
    last_dims = (((1,), (1,)), ((), ()))
    first_dims = (((0,), (0,)), ((), ()))
    length, local = query_raw.shape
    width = acts_ref.shape[1]
    rows = part_ref.shape[3]
    block = 256
    scale = HD ** (-0.5)
    copies = [
        pltpu.make_async_copy(acts_hbm, acts_ref, copy_sem.at[0]),
        pltpu.make_async_copy(weight_hbm, weight_ref, copy_sem.at[1]),
    ]
    near[0]()
    small[0]()
    spread_docs(docs_ref, row_docs, col_docs)
    for copy in copies:
        copy.start()
    near[1]()
    small[1]()
    near[2]()
    small[2]()
    near_finish()
    owned = width // n_z

    @pl.loop(0, width // block)
    def _(t):
        cols = pl.ds(pl.multiple_of(t * block, block), block)
        inside = pl.ds(pl.multiple_of(lax.rem(t, owned // block) * block, block), block)
        grad = seq_ref[:, :, :, cols].reshape(length, block)
        out_sums[lax.div(t, owned // block), inside, :] = dot(
            grad, mixed_ref[...], first_dims
        ).astype(bf16)

    out_start()
    total = jnp.zeros((length, local), f32)
    for owner in range(n_z):
        cols = slice(owner * owned, (owner + 1) * owned)
        grad = seq_ref[:, :, :, cols].reshape(length, owned)
        total = total + dot(grad, out_weight_ref[owner], last_dims)
    grad_mixed[...] = total.astype(bf16)
    small[3]()
    gain_ref[...] = jnp.zeros_like(gain_ref)
    late_ref[...] = jnp.zeros_like(late_ref)
    for h in range(heads):
        cols = slice(h * HD, (h + 1) * HD)
        key = ready_ref[:, local + h * HD : local + (h + 1) * HD]
        value = ready_ref[:, 2 * local + h * HD : 2 * local + (h + 1) * HD]
        key_sum[...] = jnp.zeros_like(key_sum)
        value_sum[...] = jnp.zeros_like(value_sum)

        @pl.loop(0, length // block)
        def _(t):
            at = pl.ds(pl.multiple_of(t * block, block), block)
            same = row_docs[at, :1] == col_docs[:1, :]
            query = ready_ref[at, cols]
            grad = grad_mixed[at, cols]
            scores = jnp.where(same, dot(query, key, last_dims) * scale, NEGATIVE)
            weights = jnp.exp(scores - totals_ref[at, h : h + 1])
            value_sum[...] += dot(weights.astype(bf16), grad, first_dims)
            pulled = dot(grad, value, last_dims)
            inner = jnp.sum(weights * pulled, axis=-1, keepdims=True)
            grad_scores = (weights * (pulled - inner)).astype(bf16)
            turned[at, :] = dot(grad_scores, key, plain) * scale
            key_sum[...] += dot(grad_scores, query, first_dims)

        for source, raw, gain, incoming, factor in (
            (0, query_raw, query_gain, turned, 1.0),
            (1, key_raw, key_gain, key_sum, scale),
        ):

            @pl.loop(0, length // block)
            def _(t):
                at = pl.ds(pl.multiple_of(t * block, block), block)
                back = turn(incoming[at, :] * factor, cosine_ref[at, :], -sine_ref[at, :])
                item = raw[at, cols]
                inverse = lax.rsqrt(jnp.mean(item * item, axis=-1, keepdims=True) + EPSILON)
                normed = item * inverse
                gain_ref[source : source + 1, :] += jnp.sum(back * normed, axis=0, keepdims=True)
                inner = back * gain[...]
                pulled = inverse * (
                    inner - normed * jnp.mean(inner * normed, axis=-1, keepdims=True)
                )
                where = source * local + h * HD
                grad_heads[at, where : where + HD] = pulled.astype(bf16)
                one_head[at, source * HD : (source + 1) * HD] = pulled.astype(bf16)

        where = 2 * local + h * HD
        grad_heads[:, where : where + HD] = value_sum[...].astype(bf16)
        one_head[:, 2 * HD :] = value_sum[...].astype(bf16)
        if h == 0:
            for copy in copies:
                copy.wait()
            for relay in out_relays:
                relay()
            out_finish()
            small[4]()
        else:
            chains[h - 1][1][0]()

        @pl.loop(0, width // block)
        def _(t):
            cols = pl.ds(pl.multiple_of(t * block, block), block)
            inside = pl.ds(pl.multiple_of(lax.rem(t, owned // block) * block, block), block)
            in_sums[h, lax.div(t, owned // block), inside, :] = dot(
                acts_ref[:, cols], one_head[...], first_dims
            ).astype(bf16)

        chains[h][0]()

    for chain in chains[:-1]:
        for relay in chain[1][1:2]:
            relay()

    @pl.loop(0, width // block)
    def _(t):
        cols = pl.ds(pl.multiple_of(t * block, block), block)
        pulled = dot(grad_heads[...], weight_ref[cols, :], last_dims)
        gained = jnp.sum(pulled * acts_ref[:, cols].astype(f32), axis=0, keepdims=True)
        gained = gained / attn_gain[:, cols]
        for j in range(block // 128):
            late_ref[0, pl.ds(t * (block // 128) + j, 1), :] = gained[:, j * 128 : (j + 1) * 128]
        sent = pulled.astype(bf16).reshape(span, pieces, 2, rows, block)
        for p in range(pieces):
            part_ref[p, :, :, :, cols] = sent[:, p]

    late_ref[1, :8, :] = gain_ref[...]
    small[5]()
    waiting = [relay for chain in chains[:-1] for relay in chain[1][2:]] + list(chains[-1][1])
    for i, step in enumerate(back[:-1]):
        step()
        if i < len(late) - 2:
            late[i]()
        if i % 2 == 0 and waiting:
            waiting.pop(0)()
    for relay in waiting:
        relay()
    for chain in chains:
        chain[2]()
    for step in late[min(len(late) - 2, len(back) - 1) :]:
        step()
    for h in range(heads):
        for j, target in enumerate((query_sum, key_sum_out, value_sum_out)):
            target[:, h * HD : (h + 1) * HD] = weight_sum[h, :, j * HD : (j + 1) * HD]
    back[-1]()


def attend_back(
    grad,
    saved,
    query_gain,
    key_gain,
    attn_gain,
    tables,
    docs,
    acts,
    weights,
    small,
    collective_id,
    pieces=4,
):
    query_raw, key_raw, ready, mixed, totals, out_weight = saved
    n_z = lax.axis_size("gx")
    span = lax.axis_size("gy")
    bits = span.bit_length() - 1
    tokens, width = grad.shape
    length, local = query_raw.shape
    heads = local // HD
    rows = tokens // (pieces * 2)
    halves = folded(small)
    half = (2, tokens // 2, width)
    piece = (rows, width)
    out_block = (n_z, width // n_z, local)
    in_block = (heads, n_z, width // n_z, 3 * HD)
    f32, bf16 = jnp.float32, jnp.bfloat16
    dma = pltpu.SemaphoreType.DMA
    vmem = pl.BlockSpec(memory_space=pltpu.VMEM)
    hbm = pl.BlockSpec(memory_space=pl.ANY)
    late_shape = (2, -(-width // (128 * 8)) * 8, 128)
    grad_acts, *in_sums, out_sum, small_sum, late_sum = pl.pallas_call(
        partial(attend_back_kernel, heads, pieces),
        out_shape=(
            jax.ShapeDtypeStruct((pieces, 2) + piece, f32),
            jax.ShapeDtypeStruct((in_block[2], local), f32),
            jax.ShapeDtypeStruct((in_block[2], local), f32),
            jax.ShapeDtypeStruct((in_block[2], local), f32),
            jax.ShapeDtypeStruct(out_block[1:], f32),
            jax.ShapeDtypeStruct(halves.shape, f32),
            jax.ShapeDtypeStruct(late_shape, f32),
        ),
        in_specs=[vmem] * 14 + [hbm] * 2,
        out_specs=(vmem,) * 7,
        scratch_shapes=[
            pltpu.VMEM((heads,) + in_block[2:], f32),
            pltpu.VMEM((8, HD), f32),
            pltpu.VMEM(late_shape, f32),
            pltpu.VMEM((length, 128), f32),
            pltpu.VMEM((8, length), f32),
            pltpu.VMEM((span,) + half, bf16),
            pltpu.VMEM((pieces, span, 2) + piece, bf16),
            pltpu.VMEM((length, width), bf16),
            pltpu.VMEM((width, 3 * local), bf16),
            pltpu.VMEM((length, local), bf16),
            pltpu.VMEM((length, 3 * local), bf16),
            pltpu.VMEM((length, 3 * HD), bf16),
            pltpu.VMEM((length, HD), f32),
            pltpu.VMEM((length, HD), f32),
            pltpu.VMEM((length, HD), f32),
            pltpu.VMEM(out_block, bf16),
            pltpu.VMEM(out_block, bf16),
            pltpu.VMEM(out_block, bf16),
            pltpu.VMEM(in_block, bf16),
            pltpu.VMEM(in_block, bf16),
            pltpu.VMEM(in_block, bf16),
            pltpu.VMEM((pieces, 4, 2) + piece, bf16),
            pltpu.VMEM((pieces, 4, 2) + piece, bf16),
            pltpu.VMEM((pieces, 2, 2) + piece, bf16),
            pltpu.VMEM((pieces, 2) + piece, bf16),
            pltpu.VMEM((1, 2, 16, 128), bf16),
            dma((2,)),
            dma((24,)),
            dma((span, 2)),
            dma,
            dma((n_z,)),
            dma((n_z,)),
            dma((n_z,)),
            dma((heads, n_z)),
            dma((heads, n_z)),
            dma((heads, n_z)),
            dma((pieces, 4)),
            dma((pieces, 4)),
            dma((pieces, 4)),
            dma((pieces, 2)),
            dma((pieces,)),
            dma((pieces, 4)),
            dma((pieces, 2, 2)),
            dma((pieces, 2)),
            dma((pieces,)),
        ]
        + sum_scratch(n_z, bits, halves.shape[1])
        + sum_scratch(n_z, bits, late_shape[1]),
        compiler_params=pltpu.CompilerParams(
            collective_id=collective_id, has_side_effects=True, vmem_limit_bytes=67043328
        ),
        name="attend_back",
    )(
        grad.reshape(half),
        out_weight,
        mixed,
        ready,
        query_raw,
        key_raw,
        totals,
        query_gain.reshape(1, HD),
        key_gain.reshape(1, HD),
        attn_gain.reshape(1, width),
        *tables,
        docs,
        halves,
        acts,
        weights,
    )
    return (
        grad_acts.reshape(tokens, width),
        in_sums,
        out_sum,
        small_sum.reshape(-1)[: small.shape[0]],
        (late_sum[0].reshape(-1)[:width], late_sum[1, 0], late_sum[1, 1]),
    )


def flat(parts):
    return jnp.concatenate([part.reshape(-1) for part in parts])


def unflat(vector, parts):
    ends = accumulate(part.size for part in parts)
    return [vector[end - part.size : end].reshape(part.shape) for end, part in zip(ends, parts)]


def norm_rows(values, gain_row):
    return (
        values * lax.rsqrt(jnp.mean(values * values, axis=-1, keepdims=True) + EPSILON) * gain_row
    )


def rotary(values):
    length = values.shape[0]
    halfway = values.shape[-1] // 2
    positions = jnp.arange(length, dtype=jnp.float32)
    frequency = jnp.exp(
        jnp.arange(halfway, dtype=jnp.float32) * (-2.0 * jnp.log(10000.0) / values.shape[-1])
    )
    angles = (positions[:, None] * frequency[None, :])[:, None, :]
    cosine = jnp.cos(angles)
    sine_table = jnp.sin(angles)
    first_half = values[..., :halfway]
    second = values[..., halfway:]
    return jnp.concatenate(
        [first_half * cosine - second * sine_table, second * cosine + first_half * sine_table],
        axis=-1,
    )


def prepare_heads(raw_heads, gain_row):
    return rotary(norm_rows(raw_heads, gain_row))


def route_gates(id_table, logits):
    shares = jax.nn.softmax(logits, axis=-1)
    experts = logits.shape[-1]
    matches = id_table[:, :, None] == jnp.arange(experts, dtype=jnp.int32)[None, None, :]
    chosen = jnp.sum(jnp.where(matches, shares[:, None, :], 0.0), axis=-1)
    return chosen / jnp.sum(chosen, axis=-1, keepdims=True)


def contract_rows(left_side, right_side):
    return lax.dot_general(
        left_side, right_side, (((0,), (0,)), ((), ())), preferred_element_type=jnp.float32
    )


def contract_cols(left_side, right_side):
    return lax.dot_general(
        left_side, right_side, (((1,), (1,)), ((), ())), preferred_element_type=jnp.float32
    )


def routed_experts(
    moe_in, cotangent, expert_ids, gate_share, router_weight, gate_weight, up_weight, down_weight
):
    tok_rows = moe_in.shape[0]
    experts = router_weight.shape[1]
    width_all = moe_in.shape[1]
    capacity = tok_rows * TOP * 3 // (2 * experts)
    route_count = tok_rows * TOP
    flat_ids = expert_ids.reshape(route_count)
    onehot = (flat_ids[:, None] == jnp.arange(experts, dtype=jnp.int32)[None, :]).astype(jnp.int32)
    earlier = jnp.cumsum(onehot, axis=0) - onehot
    slot_index = jnp.sum(earlier * onehot, axis=1)
    target = flat_ids * capacity + slot_index
    source = (
        jnp.full((experts * capacity,), tok_rows, jnp.int32)
        .at[target]
        .set(jnp.arange(route_count, dtype=jnp.int32) // TOP)
    )
    padded_in = jnp.concatenate([moe_in, jnp.zeros((1, width_all), jnp.bfloat16)], axis=0)
    packed = padded_in[source].reshape(experts, 1, capacity, width_all)
    outgoing = jnp.broadcast_to(packed, (experts, 2, capacity, width_all)).reshape(
        2 * experts, capacity, width_all
    )
    arrived = lax.all_to_all(outgoing, ("gx", "gy"), split_axis=0, concat_axis=1, tiled=True)[0]
    gate_in = gate_weight[0]
    up_in = up_weight[0]
    down_in = down_weight[0]
    gate_val = jnp.dot(arrived, gate_in, preferred_element_type=jnp.float32)
    up_val = jnp.dot(arrived, up_in, preferred_element_type=jnp.float32)
    hidden = (jax.nn.silu(gate_val) * up_val).astype(jnp.bfloat16)
    produced = jnp.dot(hidden, down_in, preferred_element_type=jnp.float32).astype(jnp.bfloat16)
    returned = lax.all_to_all(produced[None], ("gx", "gy"), split_axis=1, concat_axis=0, tiled=True)
    summed = (
        returned.reshape(experts, 2, capacity, width_all)
        .astype(jnp.float32)
        .sum(axis=1)
        .reshape(experts * capacity, width_all)
    )
    route_out = summed[target]
    gates_flat = gate_share.reshape(route_count)
    moe_out = jnp.sum((gates_flat[:, None] * route_out).reshape(tok_rows, TOP, width_all), axis=1)
    grad_out = cotangent.astype(jnp.float32)
    grad_gates = jnp.sum(
        route_out.reshape(tok_rows, TOP, width_all) * grad_out[:, None, :], axis=-1
    )
    slot_gate = jnp.zeros((experts * capacity,), jnp.float32).at[target].set(gates_flat)
    padded_grad = jnp.concatenate([grad_out, jnp.zeros((1, width_all), jnp.float32)], axis=0)
    grad_packed = (
        (slot_gate[:, None] * padded_grad[source])
        .astype(jnp.bfloat16)
        .reshape(experts, 1, capacity, width_all)
    )
    grad_outgoing = jnp.broadcast_to(grad_packed, (experts, 2, capacity, width_all)).reshape(
        2 * experts, capacity, width_all
    )
    grad_arrived = lax.all_to_all(
        grad_outgoing, ("gx", "gy"), split_axis=0, concat_axis=1, tiled=True
    )[0]
    rows_in, grad_use = (arrived, grad_arrived)
    gate_use, up_use, hidden_use = (gate_val, up_val, hidden)
    sigmoid_gate = jax.nn.sigmoid(gate_use)
    silu_gate = gate_use * sigmoid_gate
    grad_hidden = contract_cols(grad_use, down_in)
    down_part = contract_rows(hidden_use, grad_use)
    grad_gate = (
        grad_hidden * up_use * sigmoid_gate * (1.0 + gate_use * (1.0 - sigmoid_gate))
    ).astype(jnp.bfloat16)
    grad_up = (grad_hidden * silu_gate).astype(jnp.bfloat16)
    gate_part = contract_rows(rows_in, grad_gate)
    up_part = contract_rows(rows_in, grad_up)
    grad_in = contract_cols(grad_gate, gate_in) + contract_cols(grad_up, up_in)
    grad_back = lax.all_to_all(
        grad_in.astype(jnp.bfloat16)[None], ("gx", "gy"), split_axis=1, concat_axis=0, tiled=True
    )
    grad_summed = (
        grad_back.reshape(experts, 2, capacity, width_all)
        .astype(jnp.float32)
        .sum(axis=1)
        .reshape(experts * capacity, width_all)
    )
    grad_moe_in = jnp.sum(grad_summed[target].reshape(tok_rows, TOP, width_all), axis=1)
    return moe_out, grad_gates, grad_moe_in, gate_part, up_part, down_part


def dense_experts(
    moe_in, all_cot, expert_ids, gate_share, gate_weight, up_weight, down_weight
):
    devices = lax.axis_size("gx") * lax.axis_size("gy")
    experts = devices // 2
    matches = expert_ids[:, :, None] == jnp.arange(experts, dtype=jnp.int32)[None, None, :]
    dense_gates = jnp.sum(jnp.where(matches, gate_share[:, :, None], 0.0), axis=1)
    shares = jnp.repeat(dense_gates.T, 2, axis=0)[:, None, :]
    all_moe, pair, gate_dots, down_part, moe_out = run_experts(
        moe_in, all_cot, shares, gate_weight[0], up_weight[0], down_weight[0], 8
    )
    moe_out = moe_out.reshape(moe_in.shape)
    dots_experts = gate_dots.reshape(experts, 2, -1).sum(axis=1).T
    grad_gates = jnp.sum(jnp.where(matches, dots_experts[:, None, :], 0.0), axis=-1)
    grad_moe_in, gate_part, up_part = pull_experts(all_moe, pair, gate_weight[0], up_weight[0], 9)
    return moe_out, grad_gates, grad_moe_in, gate_part, up_part, down_part


def plain_attention(
    acts, in_weights, out_weight, query_gain, key_gain, attn_gain, doc_ids, cotangent
):
    seq_acts = lax.all_gather(acts, "gy", axis=0, tiled=True)
    full_in = lax.all_gather(jnp.concatenate(in_weights, axis=1), "gx", axis=0, tiled=True)
    out_rows = lax.all_gather(out_weight, "gx", axis=1, tiled=True)
    local_width = full_in.shape[1] // 3
    length = seq_acts.shape[0]
    local_heads = local_width // HD
    projected = jnp.dot(seq_acts, full_in, preferred_element_type=jnp.float32)
    queries = projected[:, :local_width]
    key_raw = projected[:, local_width : 2 * local_width]
    value_ready = (
        projected[:, 2 * local_width :].astype(jnp.bfloat16).reshape(length, local_heads, HD)
    )
    query_float, query_pull = jax.vjp(
        prepare_heads, queries.reshape(length, local_heads, HD), query_gain
    )
    key_float, key_pull = jax.vjp(prepare_heads, key_raw.reshape(length, local_heads, HD), key_gain)
    query_ready = query_float.astype(jnp.bfloat16)
    key_ready = key_float.astype(jnp.bfloat16)
    block_rows = min(512, length)
    block_count = length // block_rows
    score_scale = HD ** (-0.5)
    query_blocks = query_ready.reshape(block_count, block_rows, local_heads, HD)
    doc_blocks = doc_ids.reshape(block_count, block_rows)

    def block_scores(query_block, doc_block):
        scores = (
            jnp.einsum("qhd,khd->hqk", query_block, key_ready, preferred_element_type=jnp.float32)
            * score_scale
        )
        same_doc = doc_block[:, None] == doc_ids[None, :]
        return jnp.where(same_doc[None], scores, NEGATIVE)

    def forward_block(pieces):
        scores = block_scores(pieces[0], pieces[1])
        highest = jnp.max(scores, axis=-1, keepdims=True)
        weights = jnp.exp(scores - highest)
        totals = jnp.sum(weights, axis=-1, keepdims=True)
        shares = (weights / totals).astype(jnp.bfloat16)
        mixed_heads = jnp.einsum(
            "hqk,khd->qhd", shares, value_ready, preferred_element_type=jnp.float32
        )
        return (
            mixed_heads.astype(jnp.bfloat16),
            highest[..., 0] + jnp.log(totals[..., 0]),
            jnp.max(highest[..., 0], axis=-1),
        )

    mixed_blocks, log_totals, peak_blocks = lax.map(forward_block, (query_blocks, doc_blocks))
    mixed_seq = mixed_blocks.reshape(length, local_width)
    attended = lax.psum_scatter(
        jnp.dot(mixed_seq, out_rows, preferred_element_type=jnp.float32),
        "gy",
        scatter_dimension=0,
        tiled=True,
    )

    def back(grad_resid, small):
        seq_grad = lax.all_gather(grad_resid.astype(jnp.bfloat16), "gy", axis=0, tiled=True)
        grad_mixed = contract_cols(seq_grad, out_rows).astype(jnp.bfloat16)
        out_part = contract_rows(seq_grad, mixed_seq)

        def backward_block(running, pieces):
            grad_key, grad_value = running
            query_block, grad_block, log_block, doc_block = pieces
            scores = block_scores(query_block, doc_block)
            weights = jnp.exp(scores - log_block[..., None])
            grad_value = grad_value + jnp.einsum(
                "hqk,qhd->khd",
                weights.astype(jnp.bfloat16),
                grad_block,
                preferred_element_type=jnp.float32,
            )
            grad_weights = jnp.einsum(
                "qhd,khd->hqk", grad_block, value_ready, preferred_element_type=jnp.float32
            )
            inner_sum = jnp.sum(weights * grad_weights, axis=-1, keepdims=True)
            grad_scores = (weights * (grad_weights - inner_sum)).astype(jnp.bfloat16)
            grad_query = (
                jnp.einsum("hqk,khd->qhd", grad_scores, key_ready, preferred_element_type=jnp.float32)
                * score_scale
            )
            grad_key = (
                grad_key
                + jnp.einsum(
                    "hqk,qhd->khd", grad_scores, query_block, preferred_element_type=jnp.float32
                )
                * score_scale
            )
            return ((grad_key, grad_value), grad_query)

        empty_heads = jnp.zeros((length, local_heads, HD), jnp.float32)
        grad_mixed_blocks = grad_mixed.reshape(block_count, block_rows, local_heads, HD)
        (key_grad_heads, value_grad_heads), query_grad_blocks = lax.scan(
            backward_block,
            (empty_heads, empty_heads),
            (query_blocks, grad_mixed_blocks, log_totals, doc_blocks),
        )
        query_raw_grad, query_gain_part = query_pull(query_grad_blocks.reshape(length, local_heads, HD))
        key_raw_grad, key_gain_part = key_pull(key_grad_heads)
        grad_queries = query_raw_grad.reshape(length, local_width).astype(jnp.bfloat16)
        grad_keys = key_raw_grad.reshape(length, local_width).astype(jnp.bfloat16)
        grad_values = value_grad_heads.reshape(length, local_width).astype(jnp.bfloat16)
        grad_heads = jnp.concatenate([grad_queries, grad_keys, grad_values], axis=1)
        acts_part = contract_cols(grad_heads, full_in).astype(jnp.bfloat16)
        in_sum = lax.psum_scatter(
            contract_rows(seq_acts, grad_heads).astype(jnp.bfloat16),
            "gx",
            scatter_dimension=0,
            tiled=True,
        ).astype(jnp.float32)
        grad_acts = lax.psum_scatter(acts_part, "gy", scatter_dimension=0, tiled=True)
        out_sum = lax.psum_scatter(
            out_part.astype(jnp.bfloat16), "gx", scatter_dimension=0, tiled=True
        ).astype(jnp.float32)
        in_sums = (in_sum[:, :local_width], in_sum[:, local_width : 2 * local_width], in_sum[:, 2 * local_width :])
        gain_parts = (None, query_gain_part, key_gain_part)
        return grad_acts.astype(jnp.float32), in_sums, out_sum, sum_everywhere(small, 12), gain_parts

    return attended, jnp.max(peak_blocks, axis=0), None, back


def kernel_attention(
    acts, in_weights, out_weight, query_gain, key_gain, attn_gain, doc_ids, cotangent
):
    length = doc_ids.shape[0]
    halfway = HD // 2
    frequency = jnp.exp(
        jnp.arange(halfway, dtype=jnp.float32) * (-2.0 * jnp.log(10000.0) / HD)
    )
    angles = jnp.arange(length, dtype=jnp.float32)[:, None] * frequency[None, :]
    cosine, sine = jnp.cos(angles), jnp.sin(angles)
    tables = (
        jnp.concatenate([cosine, cosine], axis=1),
        jnp.concatenate([-sine, sine], axis=1),
    )
    docs = doc_ids.reshape(-1, 128)
    attended, seq_acts, full_in, all_cot, saved, peaks = attend(
        acts, in_weights, out_weight, cotangent, query_gain, key_gain, tables, docs, 10
    )
    heads = in_weights[0].shape[1] // HD

    def back(grad_resid, small):
        return attend_back(
            grad_resid.astype(jnp.bfloat16),
            saved,
            query_gain,
            key_gain,
            attn_gain,
            tables,
            docs,
            seq_acts,
            full_in,
            small,
            11,
        )

    return attended, peaks[:heads, 0], all_cot, back


def local(
    tokens,
    cotangent,
    expert_ids,
    doc_ids,
    clip_rank,
    attn_gain,
    moe_gain,
    query_gain,
    key_gain,
    query_weight,
    key_weight,
    value_weight,
    out_weight,
    router_weight,
    gate_weight,
    up_weight,
    down_weight,
):
    inputs = tokens.astype(jnp.float32)
    acts_float, norm_pull = jax.vjp(norm_rows, inputs, attn_gain)
    acts_low = acts_float.astype(jnp.bfloat16)
    in_weights = (query_weight, key_weight, value_weight)
    by_kernels = lax.axis_size("gy") == 8
    local_width = query_weight.shape[1]
    local_heads = local_width // HD
    attention = kernel_attention if by_kernels else plain_attention
    attended, own_peaks, all_cot, attention_back = attention(
        acts_low, in_weights, out_weight, query_gain, key_gain, attn_gain, doc_ids, cotangent
    )
    start_head = lax.axis_index("gy") * local_heads
    peak_slots = lax.dynamic_update_slice(
        jnp.zeros((lax.axis_size("gx"), NH), jnp.float32),
        own_peaks[None],
        (lax.axis_index("gx"), start_head),
    )
    residual = inputs + attended
    moe_float, moe_pull = jax.vjp(norm_rows, residual, moe_gain)
    moe_in = moe_float.astype(jnp.bfloat16)
    logits = jnp.dot(moe_in, router_weight, preferred_element_type=jnp.float32)
    gate_share, gate_pull = jax.vjp(partial(route_gates, expert_ids), logits)
    if by_kernels and router_weight.shape[1] <= 2 * TOP:
        moe_out, grad_gates, grad_moe_in, gate_part, up_part, down_part = dense_experts(
            moe_in, all_cot, expert_ids, gate_share, gate_weight, up_weight, down_weight
        )
    else:
        moe_out, grad_gates, grad_moe_in, gate_part, up_part, down_part = routed_experts(
            moe_in,
            cotangent,
            expert_ids,
            gate_share,
            router_weight,
            gate_weight,
            up_weight,
            down_weight,
        )
    output = (residual + moe_out).astype(jnp.bfloat16)
    grad_out = cotangent.astype(jnp.float32)
    (grad_logits,) = gate_pull(grad_gates)
    grad_logits_low = grad_logits.astype(jnp.bfloat16)
    router_part = contract_rows(moe_in, grad_logits_low)
    grad_moe_in = grad_moe_in + contract_cols(grad_logits_low, router_weight)
    grad_resid_norm, moe_gain_part = moe_pull(grad_moe_in)
    grad_resid = grad_out + grad_resid_norm
    early = (moe_gain_part, router_part.T, peak_slots)
    grad_acts, in_sums, out_sum, early_sum, late = attention_back(grad_resid, flat(early))
    query_sum, key_sum, value_sum = in_sums
    moe_gain_grad, router_flat, peaks = unflat(early_sum, early)
    norm_input_grad, attn_gain_part = norm_pull(grad_acts)
    input_grad = grad_resid + norm_input_grad
    if late[0] is None:
        late = (attn_gain_part, *late[1:])
        late = unflat(sum_everywhere(flat(late), 5), late)
    attn_gain_grad, query_gain_grad, key_gain_grad = late
    router_grad = router_flat.T
    peak_global = jnp.max(peaks, axis=0)
    ranked = -jnp.sort(-peak_global)
    limit = jnp.sum(jnp.where(jnp.arange(NH, dtype=jnp.int32) == clip_rank[0], ranked, 0.0))
    factors = jnp.where(peak_global > limit, limit / peak_global, 1.0)
    own_factors = lax.dynamic_slice_in_dim(factors, start_head, local_heads)
    columns = jnp.repeat(jnp.sqrt(own_factors), HD)
    query_clipped = (query_weight.astype(jnp.float32) * columns[None, :]).astype(jnp.bfloat16)
    key_clipped = (key_weight.astype(jnp.float32) * columns[None, :]).astype(jnp.bfloat16)
    return (
        output,
        input_grad,
        attn_gain_grad,
        moe_gain_grad,
        query_gain_grad,
        key_gain_grad,
        query_sum,
        key_sum,
        value_sum,
        out_sum.T,
        router_grad,
        gate_part[None],
        up_part[None],
        down_part[None],
        query_clipped,
        key_clipped,
        factors,
    )


def solution(mesh):
    placed = (
        P(("gx", "gy"), None),
        P(("gx", "gy"), None),
        P(("gx", "gy"), None),
        P("gx"),
        P(),
        P(),
        P(),
        P(),
        P(),
        P("gx", "gy"),
        P("gx", "gy"),
        P("gx", "gy"),
        P("gy", "gx"),
        P(),
        P(("gx", "gy"), None, None),
        P(("gx", "gy"), None, None),
        P(("gx", "gy"), None, None),
    )
    return jax.shard_map(
        local,
        mesh=mesh,
        in_specs=placed,
        out_specs=(
            P(("gx", "gy"), None),
            P(("gx", "gy"), None),
            P(),
            P(),
            P(),
            P(),
            P("gx", "gy"),
            P("gx", "gy"),
            P("gx", "gy"),
            P("gy", "gx"),
            P(),
            P(("gx", "gy"), None, None),
            P(("gx", "gy"), None, None),
            P(("gx", "gy"), None, None),
            P("gx", "gy"),
            P("gx", "gy"),
            P(),
        ),
        check_vma=False,
    )
```

```python
from functools import partial
from itertools import accumulate

import jax
import jax.numpy as jnp
from jax import lax
from jax.experimental import pallas as pl
from jax.experimental.pallas import tpu as pltpu
from jax.sharding import PartitionSpec as P

NH = 16
HD = 128
TOP = 8


EPSILON = 1e-06
NEGATIVE = -1e30


def flip(index):
    return index + 1 - 2 * (index % 2)


def barrier_with(partners):
    barrier = pltpu.get_barrier_semaphore()
    for ok, device in partners:
        @pl.when(ok)
        def _():
            pl.semaphore_signal(barrier, inc=1, device_id=device, device_id_type=pl.DeviceIdType.MESH)
    pl.semaphore_wait(barrier, sum(ok.astype(jnp.int32) for ok, _ in partners))

def always(ok, other):
    if ok is True:
        return other
    return ok if other is True else jnp.logical_and(ok, other)


def run_if(ok, action):
    if ok is True:
        action()
    else:
        pl.when(ok)(action)


def chain_gather(n_z, own_ref, out_ref, send_sem, recv_sem, local_sem):
    z = lax.axis_index("gx")
    g = lax.axis_index("gy")

    def hop(source, owner, k, peer):
        return pltpu.make_async_remote_copy(
            src_ref=source,
            dst_ref=out_ref.at[owner],
            send_sem=send_sem.at[k],
            recv_sem=recv_sem.at[owner],
            device_id={"gx": peer, "gy": g},
            device_id_type=pl.DeviceIdType.MESH,
        )

    local = pltpu.make_async_copy(own_ref, out_ref.at[z], local_sem)
    upward = [(z < n_z - 1, lambda: hop(own_ref, z, 0, z + 1))]
    downward = [(z > 0, lambda: hop(own_ref, z, n_z, z - 1))]
    for d in range(1, n_z - 1):
        upward.append(
            (
                jnp.logical_and(z >= d, z < n_z - 1),
                lambda d=d: hop(out_ref.at[z - d], z - d, d, z + 1),
            )
        )
        downward.append(
            (
                jnp.logical_and(z < n_z - d, z > 0),
                lambda d=d: hop(out_ref.at[z + d], z + d, n_z + d, z - 1),
            )
        )

    def start():
        local.start()
        for ok, copy in (upward[0], downward[0]):
            run_if(ok, lambda copy=copy: copy().start())

    def relay(d):
        run_if(z >= d, lambda: hop(own_ref, z - d, 0, z).wait_recv())
        if d < n_z - 1:
            run_if(upward[d][0], lambda: upward[d][1]().start())
        run_if(z < n_z - d, lambda: hop(own_ref, z + d, 0, z).wait_recv())
        if d < n_z - 1:
            run_if(downward[d][0], lambda: downward[d][1]().start())

    def finish():
        local.wait()
        for ok, copy in upward + downward:
            run_if(ok, lambda copy=copy: copy().wait_send())

    return start, [partial(relay, d) for d in range(1, n_z)], finish


def gather_steps(n_z, span, own_ref, out_ref, send_sem, recv_sem, local_sem):
    z = lax.axis_index("gx")
    g = lax.axis_index("gy")
    flip_x = g + 2 - 4 * ((g // 2) % 2)
    flip_y = g + 4 - 8 * ((g // 4) % 2)
    flip_both = flip_x + flip_y - g
    core = {"gx": z, "gy": flip(g)}
    x_peer = {"gx": z, "gy": flip_x}
    y_peer = {"gx": z, "gy": flip_y}
    above = {"gx": z + 1, "gy": g}
    below = {"gx": z - 1, "gy": g}
    first_z = z if n_z > 1 else 0
    sends = []

    def send(ok, b, h, peer, own=False):
        k = len(sends)

        def make():
            return pltpu.make_async_remote_copy(
                src_ref=own_ref.at[h] if own else out_ref.at[b, h],
                dst_ref=out_ref.at[b, h],
                send_sem=send_sem.at[k],
                recv_sem=recv_sem.at[b, h],
                device_id=peer,
                device_id_type=pl.DeviceIdType.MESH,
            )

        sends.append((ok, make))
        run_if(ok, lambda: make().start())

    def arrive(ok, b, h):
        def wait():
            pltpu.make_async_remote_copy(
                src_ref=out_ref.at[b, h],
                dst_ref=out_ref.at[b, h],
                send_sem=send_sem.at[0],
                recv_sem=recv_sem.at[b, h],
                device_id=core,
                device_id_type=pl.DeviceIdType.MESH,
            ).wait_recv()

        run_if(ok, wait)

    local = pltpu.make_async_copy(own_ref, out_ref.at[first_z * span + g], local_sem)
    items = [(True, first_z, 0)]
    for d in range(1, n_z):
        items += [(z >= d, z - d, -d), (z < n_z - d, z + d, d)]

    upward = [always(item[0], z < n_z - 1) for item in items]
    downward = [always(item[0], z > 0) for item in items]

    near_b = [owner * span + g for _, owner, _ in items]
    x_b = [owner * span + flip_x for _, owner, _ in items]
    y_b = [owner * span + flip_y for _, owner, _ in items]
    both_b = [owner * span + flip_both for _, owner, _ in items]

    def first(i):
        ok, _, d = items[i]
        b = near_b[i]
        own = d == 0
        if own:
            local.start()
        else:
            arrive(ok, b, 0)
            arrive(ok, b, 1)
        for h in range(2):
            if n_z > 1 and d <= 0:
                send(upward[i], b, h, above, own)
            if n_z > 1 and d >= 0:
                send(downward[i], b, h, below, own)
        for h, peer in ((0, x_peer), (1, y_peer), (1, x_peer), (0, y_peer), (0, core), (1, core)):
            send(ok, b, h, peer, own)

    def second(i):
        ok = items[i][0]
        for b, h, peer in ((x_b[i], 0, y_peer), (y_b[i], 1, x_peer)):
            arrive(ok, b, h)
            send(ok, b, h, peer)
            send(ok, b, h, core)

    def third(i):
        ok = items[i][0]
        for b, h in ((both_b[i], 0), (both_b[i], 1), (y_b[i], 0), (x_b[i], 1)):
            arrive(ok, b, h)
            send(ok, b, h, core)

    n = len(items)

    def step(i):
        if i < n:
            first(i)
        if 1 <= i <= n:
            second(i - 1)
        if i >= 2:
            third(i - 2)

    def finish():
        for ok, owner, _ in items:
            for side in (g, flip_x, flip_y, flip_both):
                for h in range(2):
                    arrive(ok, owner * span + flip(side), h)
        local.wait()
        for ok, make in sends:
            run_if(ok, lambda make=make: make().wait_send())

    return [partial(step, i) for i in range(n + 2)], finish


def greet(n_z):
    z = lax.axis_index("gx")
    g = lax.axis_index("gy")
    peers = [
        (z >= 0, {"gx": z, "gy": g + bit - 2 * bit * ((g // bit) % 2)}) for bit in (1, 2, 4)
    ]
    if n_z > 1:
        peers += [(z < n_z - 1, {"gx": z + 1, "gy": g}), (z > 0, {"gx": z - 1, "gy": g})]
    barrier_with(peers)


def add_into(dst, parts, rows):
    step = min(rows, 32)

    @pl.loop(0, rows // step)
    def _(r):
        at = pl.ds(pl.multiple_of(r * step, step), step)
        if len(parts) == 2 and dst.dtype == jnp.bfloat16:
            dst[at, :] = parts[0][at, :] + parts[1][at, :]
        else:
            total = parts[0][at, :].astype(jnp.float32)
            for term in parts[1:]:
                total = total + term[at, :].astype(jnp.float32)
            dst[at, :] = total.astype(dst.dtype)


def scatter_kernel(chain, n_i, rows, part_ref, out_ref, held, from_core, from_a, from_b, from_z,
                   load_sem, core_send, a_send, b_send, z_send, core_recv, a_recv, b_recv, z_recv, beside=None, parts=None):
    z = lax.axis_index("gx"); g = lax.axis_index("gy")
    flip_x = g + 2 - 4 * ((g // 2) % 2)
    flip_y = g + 4 - 8 * ((g // 4) % 2)
    quads = (flip_x + flip_y - g, flip_x, flip_y, g)
    core = {"gx": z, "gy": flip(g)}
    xn = {"gx": z, "gy": flip_x}
    yn = {"gx": z, "gy": flip_y}
    every = z >= 0
    partners = [(every, core), (every, xn), (every, yn)]
    if chain:
        partners += [(every, {"gx": lax.rem(z + j, n_i), "gy": g}) for j in range(1, n_i)]
    if beside:
        n_z = lax.axis_size("gx")
        partners += [(z < n_z - 1, {"gx": z + 1, "gy": g}), (z > 0, {"gx": z - 1, "gy": g})]
    if parts is None:
        barrier_with(partners)
    if beside:
        beside[0]()
    mesh_id = pl.DeviceIdType.MESH

    def item(i):
        return lax.rem(z + n_i - 1 - i + n_i, n_i) if chain else i

    def block(it, gg):
        return part_ref.at[it, gg]

    def remote(src, dst, ssem, rsem, dev):
        return pltpu.make_async_remote_copy(src_ref=src, dst_ref=dst, send_sem=ssem, recv_sem=rsem, device_id=dev, device_id_type=mesh_id)

    def core_copy(i, q):
        it = item(i)
        return remote(block(it, flip(quads[q])), from_core.at[it, q], core_send.at[i, q], core_recv.at[it, q], core)

    def load(i, q):
        it = item(i)
        return pltpu.make_async_copy(block(it, quads[q]), held.at[it, q], load_sem.at[i, q])

    a_plan = ((0, 0, 0, xn), (0, 1, 0, yn), (1, 0, 1, xn), (2, 1, 1, yn))
    def a_copy(i, k):
        it = item(i)
        q, h, slot, dev = a_plan[k]
        return remote(held.at[it, q, h], from_a.at[it, h, slot], a_send.at[i, k], a_recv.at[it, h, slot], dev)

    b_plan = ((2, 0, yn), (1, 1, xn))
    def b_copy(i, h):
        it = item(i)
        q, _, dev = b_plan[h]
        return remote(held.at[it, q, h], from_b.at[it, h], b_send.at[i, h], b_recv.at[it, h], dev)

    def z_copy(i):
        it = item(i)
        return remote(held.at[it, 3], from_z.at[z], z_send.at[i], z_recv.at[z], {"gx": it, "gy": g})

    def z_arrival(i):
        it = item(i)
        return remote(held.at[it, 3], from_z.at[it], z_send.at[i], z_recv.at[it], core)

    def begin():
        for i in range(n_i):
            for q in range(4):
                core_copy(i, q).start()
                load(i, q).start()

    def stage_a(i):
        it = item(i)
        for q in range(4):
            load(i, q).wait()
            core_copy(i, q).wait_recv()
            for h in range(2):
                add_into(held.at[it, q, h], (held.at[it, q, h], from_core.at[it, q, h]), rows)
            for k in range(4):
                if a_plan[k][0] == q:
                    a_copy(i, k).start()

    def stage_b(i):
        it = item(i)
        for q, h, slot in ((2, 0, 0), (1, 1, 0), (3, 0, 1), (3, 1, 1)):
            remote(held.at[it, q, h], from_a.at[it, h, slot], a_send.at[i, 0], a_recv.at[it, h, slot], core).wait_recv()
            add_into(held.at[it, q, h], (held.at[it, q, h], from_a.at[it, h, slot]), rows)
            if slot == 0:
                b_copy(i, h).start()

    def stage_c(i):
        it = item(i)
        for h in range(2):
            b_copy(i, h).wait_recv()
            if chain:
                add_into(held.at[it, 3, h], (held.at[it, 3, h], from_b.at[it, h]), rows)
            else:
                add_into(out_ref.at[it, h], (held.at[it, 3, h], from_b.at[it, h]), rows)

    def stage_d(i):
        if i < n_i - 1:
            z_copy(i).start()
        else:
            for j in range(n_i - 1):
                z_arrival(j).wait_recv()
            for h in range(2):
                add_into(
                    out_ref.at[h],
                    [held.at[item(i), 3, h]] + [from_z.at[item(j), h] for j in range(n_i - 1)],
                    rows,
                )

    def step(i):
        if i < n_i:
            stage_a(i)
        if 0 <= i - 1 < n_i:
            stage_b(i - 1)
        if 0 <= i - 2 < n_i:
            stage_c(i - 2)
        if chain and 0 <= i - 2 < n_i:
            stage_d(i - 2)

    def finish():
        for i in range(n_i):
            for q in range(4):
                core_copy(i, q).wait_send()
            for k in range(4):
                a_copy(i, k).wait_send()
            for h in range(2):
                b_copy(i, h).wait_send()
            if chain and i < n_i - 1:
                z_copy(i).wait_send()

    if parts is not None:
        parts.extend([begin] + [partial(step, i) for i in range(n_i + 2)] + [finish])
        return
    begin()
    for i in range(n_i + 2):
        step(i)
        if beside and i == n_i:
            beside[1][0]()
    if beside:
        for relay in beside[1][1:]:
            relay()
        beside[2]()
    finish()


def sum_steps(n_z, bits, vec_ref, out_ref, held, arrived, from_z, send_sem, z_send, recv_sem, z_recv):
    z = lax.axis_index("gx")
    g = lax.axis_index("gy")
    side = lax.rem(g, 2)
    peers = [
        {"gx": z, "gy": g + bit - 2 * bit * ((g // bit) % 2)}
        for bit in (2**power for power in range(bits))
    ]
    others = [{"gx": lax.rem(z + j, n_z), "gy": g} for j in range(1, n_z)]

    def remote(src, dst, ssem, rsem, peer):
        return pltpu.make_async_remote_copy(
            src_ref=src,
            dst_ref=dst,
            send_sem=ssem,
            recv_sem=rsem,
            device_id=peer,
            device_id_type=pl.DeviceIdType.MESH,
        )

    def hop(k):
        source = vec_ref.at[1 - side] if k == 0 else held.at[k - 1]
        return remote(source, arrived.at[k], send_sem.at[k], recv_sem.at[k], peers[k])

    def across(j):
        return remote(held.at[bits - 1], from_z.at[j], z_send.at[j], z_recv.at[j], others[j])

    def back():
        return remote(held.at[bits], arrived.at[bits], send_sem.at[bits], recv_sem.at[bits], peers[0])

    def onward(k):
        hop(k).wait()
        held[k] = (vec_ref[side] if k == 0 else held[k - 1]) + arrived[k]
        if k + 1 < bits:
            hop(k + 1).start()
        else:
            for j in range(n_z - 1):
                across(j).start()

    def gather():
        for j in range(n_z - 1):
            across(j).wait()
        total = jnp.zeros_like(held[0])
        for owner in range(n_z):
            term = held[bits - 1]
            for j in range(1, n_z):
                term = jnp.where(lax.rem(z - j + n_z, n_z) == owner, from_z[j - 1], term)
            total = total + term
        held[bits] = total
        back().start()
        out_ref[side] = total

    def finish():
        back().wait()
        out_ref[1 - side] = arrived[bits]

    return [lambda: hop(0).start()] + [partial(onward, k) for k in range(bits)] + [gather, finish]


def sum_kernel(n_z, bits, *refs):
    z = lax.axis_index("gx")
    g = lax.axis_index("gy")
    peers = [
        {"gx": z, "gy": g + bit - 2 * bit * ((g // bit) % 2)}
        for bit in (2**power for power in range(bits))
    ]
    peers += [{"gx": lax.rem(z + j, n_z), "gy": g} for j in range(1, n_z)]
    barrier_with([(z >= 0, peer) for peer in peers])
    for step in sum_steps(n_z, bits, *refs):
        step()


def folded(vector):
    rows = -(-vector.shape[0] // (128 * 16)) * 8
    return jnp.pad(vector, (0, 2 * rows * 128 - vector.shape[0])).reshape(2, rows, 128)


def sum_scratch(n_z, bits, rows):
    dma = pltpu.SemaphoreType.DMA
    return [
        pltpu.VMEM((bits + 1, rows, 128), jnp.float32),
        pltpu.VMEM((bits + 1, rows, 128), jnp.float32),
        pltpu.VMEM((n_z - 1, rows, 128), jnp.float32),
        dma((bits + 1,)),
        dma((n_z - 1,)),
        dma((bits + 1,)),
        dma((n_z - 1,)),
    ]


def sum_everywhere(vector, collective_id):
    n_z = lax.axis_size("gx")
    bits = lax.axis_size("gy").bit_length() - 1
    halves = folded(vector)
    out = pl.pallas_call(
        partial(sum_kernel, n_z, bits),
        out_shape=jax.ShapeDtypeStruct(halves.shape, jnp.float32),
        in_specs=[pl.BlockSpec(memory_space=pltpu.VMEM)],
        out_specs=pl.BlockSpec(memory_space=pltpu.VMEM),
        scratch_shapes=sum_scratch(n_z, bits, halves.shape[1]),
        compiler_params=pltpu.CompilerParams(collective_id=collective_id, has_side_effects=True),
        name="sum_everywhere",
    )(halves)
    return out.reshape(-1)[: vector.shape[0]]


def chain_scatter(n_z, part_ref, out_ref, from_low, from_high, send_sem, low_recv, high_recv):
    z = lax.axis_index("gx")
    g = lax.axis_index("gy")
    rows = part_ref.shape[1]

    def up(dest):
        return pltpu.make_async_remote_copy(
            src_ref=part_ref.at[dest],
            dst_ref=from_low.at[dest],
            send_sem=send_sem.at[dest],
            recv_sem=low_recv.at[dest],
            device_id={"gx": z + 1, "gy": g},
            device_id_type=pl.DeviceIdType.MESH,
        )

    def down(dest):
        return pltpu.make_async_remote_copy(
            src_ref=part_ref.at[dest],
            dst_ref=from_high.at[dest],
            send_sem=send_sem.at[dest],
            recv_sem=high_recv.at[dest],
            device_id={"gx": z - 1, "gy": g},
            device_id_type=pl.DeviceIdType.MESH,
        )

    def start():
        for k in range(n_z - 1):
            run_if(z == 0, lambda k=k: up(n_z - 1 - k).start())
            run_if(z == n_z - 1, lambda k=k: down(k).start())

    def pass_up(dest):
        up(dest).wait_recv()
        add_into(part_ref.at[dest], (part_ref.at[dest], from_low.at[dest]), rows)
        up(dest).start()

    def pass_down(dest):
        down(dest).wait_recv()
        add_into(part_ref.at[dest], (part_ref.at[dest], from_high.at[dest]), rows)
        down(dest).start()

    def relay(time):
        for k in range(time):
            low, dest = time - k, n_z - 1 - k
            if 0 < low < dest:
                run_if(z == low, partial(pass_up, dest))
            high, dest = n_z - 1 - (time - k), k
            if dest < high < n_z - 1:
                run_if(z == high, partial(pass_down, dest))

    def finish():
        for dest in range(n_z):
            terms = [part_ref.at[dest]]
            terms += [from_low.at[dest]] if dest > 0 else []
            terms += [from_high.at[dest]] if dest < n_z - 1 else []

            def last(dest=dest, terms=terms):
                if dest > 0:
                    up(dest).wait_recv()
                if dest < n_z - 1:
                    down(dest).wait_recv()
                add_into(out_ref, terms, rows)

            run_if(z == dest, last)
        for dest in range(n_z):
            run_if(z != dest, lambda dest=dest: up(dest).wait_send())

    return start, [partial(relay, time) for time in range(1, n_z)], finish


def expert_kernel(n_z, span, own_ref, cot_ref, share_ref, gate_ref, up_ref, down_ref,
                  all_ref, pair_ref, dots_ref, down_out, out_ref,
                  moe_buf, cot_buf, share_buf, pair_stage, dots_buf,
                  gate_val, up_val, scaled, scaled_t, down_t,
                  held, from_core, from_a, from_b, from_z,
                  send_sem, recv_sem, local_sem, fetch_sem, store_sem,
                  core_send, a_send, b_send, z_send, core_recv, a_recv, b_recv, z_recv,
                  shares_in, dots_own, share_send, share_recv, dots_send, dots_recv):
    z = lax.axis_index("gx")
    g = lax.axis_index("gy")
    rows = own_ref.shape[1]
    block = 2 * rows
    step_rows = moe_buf.shape[1]
    steps = 2 * n_z
    flip_x = g + 2 - 4 * ((g // 2) % 2)
    flip_y = g + 4 - 8 * ((g // 4) % 2)
    flip_both = flip_x + flip_y - g
    core = {"gx": z, "gy": flip(g)}
    x_peer = {"gx": z, "gy": flip_x}
    y_peer = {"gx": z, "gy": flip_y}
    above = {"gx": z + 1, "gy": g}
    below = {"gx": z - 1, "gy": g}

    order = [z]
    candidates = []
    for d in range(1, n_z):
        candidates += [(z >= d, z - d), (z < n_z - d, z + d)]
    for k in range(1, n_z):
        rank, chosen = 0, 0
        for ok, owner in candidates:
            ok = ok.astype(jnp.int32)
            rank = rank + ok
            chosen = chosen + ok * (rank == k).astype(jnp.int32) * owner
        order.append(chosen)

    onward = [(z < n_z - 1, z > 0)]
    for owner in order[1:]:
        onward.append(
            (
                jnp.logical_and(owner < z, z < n_z - 1),
                jnp.logical_and(owner > z, z > 0),
            )
        )
    devices = n_z * span
    rank = z * span + g

    def device(number):
        return {"gx": lax.div(number, span), "gy": lax.rem(number, span)}

    barrier = pltpu.get_barrier_semaphore()

    @pl.loop(1, devices)
    def _(j):
        pl.semaphore_signal(
            barrier,
            inc=1,
            device_id=device(lax.rem(rank + j, devices)),
            device_id_type=pl.DeviceIdType.MESH,
        )

    pl.semaphore_wait(barrier, devices - 1)

    def share_copy(number):
        return pltpu.make_async_remote_copy(
            src_ref=share_ref.at[number],
            dst_ref=shares_in.at[rank],
            send_sem=share_send.at[number],
            recv_sem=share_recv.at[rank],
            device_id=device(number),
            device_id_type=pl.DeviceIdType.MESH,
        )

    def share_arrival(number):
        return pltpu.make_async_remote_copy(
            src_ref=share_ref.at[number],
            dst_ref=shares_in.at[number],
            send_sem=share_send.at[number],
            recv_sem=share_recv.at[number],
            device_id=core,
            device_id_type=pl.DeviceIdType.MESH,
        )

    def dots_copy(number):
        return pltpu.make_async_remote_copy(
            src_ref=dots_own.at[number],
            dst_ref=dots_ref.at[rank],
            send_sem=dots_send.at[number],
            recv_sem=dots_recv.at[rank],
            device_id=device(number),
            device_id_type=pl.DeviceIdType.MESH,
        )

    def dots_arrival(number):
        return pltpu.make_async_remote_copy(
            src_ref=dots_own.at[number],
            dst_ref=dots_ref.at[number],
            send_sem=dots_send.at[number],
            recv_sem=dots_recv.at[number],
            device_id=core,
            device_id_type=pl.DeviceIdType.MESH,
        )

    def for_others(action):
        @pl.loop(1, devices)
        def _(j):
            action(lax.rem(rank + j, devices))

    for_others(lambda number: share_copy(number).start())
    shares_in[rank] = share_ref[rank]

    def at(owner, gg, h):
        return pl.ds(pl.multiple_of((owner * span + gg) * block + h * rows, rows), rows)

    def copy(k, slot, owner, gg, h, peer, own=False):
        return pltpu.make_async_remote_copy(
            src_ref=own_ref.at[h] if own else all_ref.at[at(owner, gg, h)],
            dst_ref=all_ref.at[at(owner, gg, h)],
            send_sem=send_sem.at[k, slot],
            recv_sem=recv_sem.at[owner * span + gg, h],
            device_id=peer,
            device_id_type=pl.DeviceIdType.MESH,
        )

    sends = []

    def send(ok, *where, **options):
        k = where[0]
        slot = sum(1 for entry in sends if entry[2] == k)
        make = partial(copy, k, slot, *where[1:], **options)
        sends.append((ok, make, k))
        run_if(ok, lambda: make().start())

    def arrive(owner, gg, h):
        copy(0, 0, owner, gg, h, core).wait_recv()

    locals_ = [
        pltpu.make_async_copy(own_ref.at[h], all_ref.at[at(z, g, h)], local_sem.at[h])
        for h in range(2)
    ]

    def first(k):
        owner = order[k]
        own = k == 0
        if own:
            for item in locals_:
                item.start()
        else:
            arrive(owner, g, 0)
            arrive(owner, g, 1)
        go_up, go_down = onward[k]
        for h in range(2):
            send(go_up, k, owner, g, h, above, own=own)
            send(go_down, k, owner, g, h, below, own=own)
        send(True, k, owner, g, 0, x_peer, own=own)
        send(True, k, owner, g, 1, y_peer, own=own)
        send(True, k, owner, g, 1, x_peer, own=own)
        send(True, k, owner, g, 0, y_peer, own=own)
        send(True, k, owner, g, 0, core, own=own)
        send(True, k, owner, g, 1, core, own=own)

    def second(k):
        owner = order[k]
        arrive(owner, flip_x, 0)
        send(True, k, owner, flip_x, 0, y_peer)
        send(True, k, owner, flip_x, 0, core)
        arrive(owner, flip_y, 1)
        send(True, k, owner, flip_y, 1, x_peer)
        send(True, k, owner, flip_y, 1, core)

    def third(k):
        owner = order[k]
        for gg, h in ((flip_y, 0), (flip_x, 1), (flip_both, 0), (flip_both, 1)):
            arrive(owner, gg, h)
            send(True, k, owner, gg, h, core)

    def complete(k):
        for gg in (g, flip_x, flip_y, flip_both):
            for h in range(2):
                arrive(order[k], flip(gg), h)
        if k == 0:
            for item in locals_:
                item.wait()

    def owner_of(s):
        if isinstance(s, int):
            return order[s // 2]
        k = lax.div(s, 2)
        return sum((k == j).astype(jnp.int32) * order[j] for j in range(n_z))

    def place(s):
        k, side = (s // 2, s % 2) if isinstance(s, int) else (lax.div(s, 2), lax.rem(s, 2))
        if isinstance(s, int):
            owner = order[k]
        else:
            owner = sum((k == j).astype(jnp.int32) * order[j] for j in range(n_z))
        return pl.ds(pl.multiple_of(owner * (span * block) + side * step_rows, step_rows), step_rows)

    def parity(s):
        return s % 2 if isinstance(s, int) else lax.rem(s, 2)

    def fetches(s):
        slot = parity(s)
        return [
            pltpu.make_async_copy(source.at[place(s)], target.at[slot], fetch_sem.at[j, slot])
            for j, (source, target) in enumerate(
                ((all_ref, moe_buf), (cot_ref, cot_buf))
            )
        ]

    def stores(s):
        slot = parity(s)
        return [
            pltpu.make_async_copy(
                pair_stage.at[slot], pair_ref.at[place(s)], store_sem.at[0, slot]
            )
        ]

    f32 = jnp.float32
    dot = partial(lax.dot_general, preferred_element_type=f32)
    plain = (((1,), (0,)), ((), ()))
    last_dims = (((1,), (1,)), ((), ()))
    first_dims = (((0,), (0,)), ((), ()))
    half_width = scaled.shape[1]
    width = moe_buf.shape[2]
    tile = 256

    quads = (flip_both, flip_x, flip_y, g)

    def remote(src, dst, ssem, rsem, peer):
        return pltpu.make_async_remote_copy(
            src_ref=src,
            dst_ref=dst,
            send_sem=ssem,
            recv_sem=rsem,
            device_id=peer,
            device_id_type=pl.DeviceIdType.MESH,
        )

    def core_copy(k, q):
        return remote(
            held.at[k, flip(quads[q])],
            from_core.at[k, q],
            core_send.at[k, q],
            core_recv.at[k, q],
            core,
        )

    a_plan = ((0, 0, 0, x_peer), (0, 1, 0, y_peer), (1, 0, 1, x_peer), (2, 1, 1, y_peer))

    def a_copy(k, j):
        q, h, slot, peer = a_plan[j]
        return remote(
            held.at[k, quads[q], h],
            from_a.at[k, h, slot],
            a_send.at[k, j],
            a_recv.at[k, h, slot],
            peer,
        )

    b_plan = ((2, y_peer), (1, x_peer))

    def b_copy(k, h):
        q, peer = b_plan[h]
        return remote(
            held.at[k, quads[q], h], from_b.at[k, h], b_send.at[k, h], b_recv.at[k, h], peer
        )

    def z_copy(k):
        return remote(
            held.at[k, g], from_z.at[z], z_send.at[k], z_recv.at[z], {"gx": order[k], "gy": g}
        )

    def stage_core(k):
        for q in range(4):
            core_copy(k, q).start()

    def stage_a(k):
        for q in range(4):
            core_copy(k, q).wait_recv()
            for h in range(2):
                mine = held.at[k, quads[q], h]
                add_into(mine, (mine, from_core.at[k, q, h]), rows)
            for j in range(4):
                if a_plan[j][0] == q:
                    a_copy(k, j).start()

    def stage_b(k):
        for q, h, slot in ((2, 0, 0), (1, 1, 0), (3, 0, 1), (3, 1, 1)):
            mine, arrived = held.at[k, quads[q], h], from_a.at[k, h, slot]
            remote(mine, arrived, a_send.at[k, 0], a_recv.at[k, h, slot], core).wait_recv()
            add_into(mine, (mine, arrived), rows)
            if slot == 0:
                b_copy(k, h).start()

    def stage_c(k):
        for h in range(2):
            b_copy(k, h).wait_recv()
            mine = held.at[k, g, h]
            add_into(mine, (mine, from_b.at[k, h]), rows)
        if k > 0:
            z_copy(k).start()

    backs = (
        (stage_core, lambda k: 2 * k + 1, 2),
        (stage_a, lambda k: 2 * k + 1, 4),
        (stage_b, lambda k: 2 * k + 2, 4),
        (stage_c, lambda k: 2 * k + 3, 4),
    )

    def events(s, phase):
        for action, start, when in backs:
            for k in range(n_z):
                if when == phase and start(k) < steps:
                    pl.when(s == start(k))(partial(action, k))
        for k in range(1, n_z):
            if k >= 2 and phase == 1:
                pl.when(s == k - 2)(partial(first, k))
            if phase == 2:
                pl.when(s == 2 * (k - 1))(partial(second, k))
            if phase == 2:
                pl.when(s == 2 * (k - 1) + 1)(partial(third, k))
            if phase == 4:
                pl.when(s == 2 * k - 1)(partial(complete, k))

    first(0)

    @pl.loop(0, width // tile)
    def _(t):
        cols = pl.ds(pl.multiple_of(t * tile, tile), tile)
        down_t[cols, :] = down_ref[:, cols].T

    second(0)
    if n_z > 1:
        first(1)
    third(0)
    complete(0)
    for item in fetches(0):
        item.start()
    for_others(lambda number: share_arrival(number).wait_recv())

    @pl.loop(0, steps)
    def _(s):
        slot = lax.rem(s, 2)
        moe, cot, share = moe_buf.at[slot], cot_buf.at[slot], share_buf
        first_device = owner_of(s) * span + slot * (span // 2)
        for item in fetches(s):
            item.wait()

        @pl.when(s >= 2)
        def _():
            for item in stores(s - 2):
                item.wait()

        for j in range(span // 2):
            column = jnp.broadcast_to(shares_in[first_device + j], (block, block)).T
            share[j * block : (j + 1) * block, :] = column
        wide = jnp.concatenate([share[...]] * (tile // share.shape[1]), axis=1)

        @pl.loop(0, half_width // tile)
        def _(t):
            cols = pl.ds(pl.multiple_of(t * tile, tile), tile)
            gated = dot(moe[...], gate_ref[:, cols], plain)
            lifted = dot(moe[...], up_ref[:, cols], plain)
            gate_val[:, cols] = gated
            up_val[:, cols] = lifted
            scaled[:, cols] = (gated * jax.nn.sigmoid(gated) * lifted * wide).astype(jnp.bfloat16)

        events(s, 1)
        scaled_t[...] = scaled[...].T

        @pl.loop(0, width // (2 * tile))
        def _(t):
            cols = pl.ds(pl.multiple_of(t * 2 * tile, 2 * tile), 2 * tile)
            sent = dot(scaled[...], down_ref[:, cols], plain).astype(jnp.bfloat16)
            held[lax.div(s, 2), pl.ds(slot * (span // 2), span // 2), :, :, cols] = sent.reshape(
                (span // 2, 2, rows, 2 * tile)
            )

        events(s, 2)
        dots_buf[...] = jnp.zeros(dots_buf.shape, f32)

        @pl.loop(0, half_width // tile)
        def _(t):
            cols = pl.ds(pl.multiple_of(t * tile, tile), tile)
            pulled = dot(cot[...], down_t[:, cols], plain)
            gated = gate_val[:, cols]
            lifted = up_val[:, cols]
            sig = jax.nn.sigmoid(gated)
            silu = gated * sig
            product = pulled * (silu * lifted)
            lanes = share.shape[1]
            dots_buf[...] = dots_buf[...] + sum(
                product[:, j * lanes : (j + 1) * lanes] for j in range(tile // lanes)
            )
            pulled = pulled * wide
            pair_stage[slot, :, cols] = (pulled * lifted * sig * (1.0 + gated * (1.0 - sig))).astype(
                jnp.bfloat16
            )
            more = pl.ds(pl.multiple_of(half_width + t * tile, tile), tile)
            pair_stage[slot, :, more] = (pulled * silu).astype(jnp.bfloat16)

        for item in stores(s):
            item.start()
        for j in range(span // 2):
            number = first_device + j
            rows_of = dots_buf[j * block : (j + 1) * block, :]
            dots_own[number] = jnp.sum(rows_of.T, axis=0, keepdims=True)

        for j in range(span // 2):
            number = first_device + j

            @pl.when(number != rank)
            def _():
                dots_copy(number).start()

        events(s, 3)
        events(s, 4)

        @pl.when(s < steps - 1)
        def _():
            for item in fetches(s + 1):
                item.start()

        @pl.loop(0, width // (2 * tile))
        def _(t):
            cols = pl.ds(pl.multiple_of(t * 2 * tile, 2 * tile), 2 * tile)
            grown = dot(scaled_t[...], cot[:, cols], plain)
            down_out[:, cols] = jnp.where(s == 0, 0.0, down_out[:, cols]) + grown

    for t in range(steps, 2 * steps):
        for action, start, _ in backs[::-1]:
            for k in range(n_z):
                if start(k) == t:
                    action(k)
    for s in (steps - 2, steps - 1):
        for item in stores(s):
            item.wait()
    for k in range(1, n_z):
        arrived = from_z.at[order[k]]
        remote(held.at[k, g], arrived, z_send.at[k], z_recv.at[order[k]], core).wait_recv()
    for h in range(2):
        terms = [held.at[0, g, h]] + [from_z.at[order[k], h] for k in range(1, n_z)]
        add_into(out_ref.at[h], terms, rows)
    for k in range(n_z):
        for q in range(4):
            core_copy(k, q).wait_send()
        for j in range(4):
            a_copy(k, j).wait_send()
        for h in range(2):
            b_copy(k, h).wait_send()
        if k > 0:
            z_copy(k).wait_send()
    for ok, make, k in sends:
        run_if(ok, lambda make=make: make().wait_send())
    dots_ref[rank] = dots_own[rank]
    for_others(lambda number: dots_arrival(number).wait_recv())
    for_others(lambda number: share_copy(number).wait_send())
    for_others(lambda number: dots_copy(number).wait_send())


def run_experts(moe_in, all_cot, shares, gate_w, up_w, down_w, collective_id):
    n_z = lax.axis_size("gx")
    span = lax.axis_size("gy")
    rows, width = moe_in.shape
    half = down_w.shape[0]
    total = n_z * span * rows
    step = span * rows // 2
    lanes = 128
    devices = n_z * span
    bf16, f32 = jnp.bfloat16, jnp.float32
    dma = pltpu.SemaphoreType.DMA
    vmem = pl.BlockSpec(memory_space=pltpu.VMEM)
    hbm = pl.BlockSpec(memory_space=pl.ANY)
    return pl.pallas_call(
        partial(expert_kernel, n_z, span),
        out_shape=(
            jax.ShapeDtypeStruct((total, width), bf16),
            jax.ShapeDtypeStruct((total, 2 * half), bf16),
            jax.ShapeDtypeStruct((devices, 1, rows), f32),
            jax.ShapeDtypeStruct((half, width), f32),
            jax.ShapeDtypeStruct((2, rows // 2, width), f32),
        ),
        in_specs=[vmem, hbm, vmem, vmem, vmem, vmem],
        out_specs=(hbm, hbm, vmem, vmem, vmem),
        scratch_shapes=[
            pltpu.VMEM((2, step, width), bf16),
            pltpu.VMEM((2, step, width), bf16),
            pltpu.VMEM((step, lanes), f32),
            pltpu.VMEM((2, step, 2 * half), bf16),
            pltpu.VMEM((step, lanes), f32),
            pltpu.VMEM((step, half), f32),
            pltpu.VMEM((step, half), f32),
            pltpu.VMEM((step, half), bf16),
            pltpu.VMEM((half, step), bf16),
            pltpu.VMEM((width, half), bf16),
            pltpu.VMEM((n_z, span, 2, rows // 2, width), bf16),
            pltpu.VMEM((n_z, 4, 2, rows // 2, width), bf16),
            pltpu.VMEM((n_z, 2, 2, rows // 2, width), bf16),
            pltpu.VMEM((n_z, 2, rows // 2, width), bf16),
            pltpu.VMEM((n_z, 2, rows // 2, width), bf16),
            dma((n_z, 18)),
            dma((n_z * span, 2)),
            dma((2,)),
            dma((3, 2)),
            dma((2, 2)),
            dma((n_z, 4)),
            dma((n_z, 4)),
            dma((n_z, 2)),
            dma((n_z,)),
            dma((n_z, 4)),
            dma((n_z, 2, 2)),
            dma((n_z, 2)),
            dma((n_z,)),
            pltpu.VMEM((devices, 1, rows), f32),
            pltpu.VMEM((devices, 1, rows), f32),
            dma((devices,)),
            dma((devices,)),
            dma((devices,)),
            dma((devices,)),
        ],
        compiler_params=pltpu.CompilerParams(
            collective_id=collective_id, has_side_effects=True, vmem_limit_bytes=67043328
        ),
        name="experts",
    )(moe_in.reshape(2, rows // 2, width), all_cot, shares, gate_w, up_w, down_w)


def pull_kernel(n_i, rows, all_ref, pair_ref, gate_ref, up_ref, out_ref, gate_out, up_out,
                held, from_core, from_a, from_b, from_z, moe_buf, pair_buf,
                fetch_sem, core_send, a_send, b_send, z_send, core_recv, a_recv, b_recv, z_recv):
    z = lax.axis_index("gx")
    g = lax.axis_index("gy")
    flip_x = g + 2 - 4 * ((g // 2) % 2)
    flip_y = g + 4 - 8 * ((g // 4) % 2)
    quads = (flip_x + flip_y - g, flip_x, flip_y, g)
    core = {"gx": z, "gy": flip(g)}
    x_peer = {"gx": z, "gy": flip_x}
    y_peer = {"gx": z, "gy": flip_y}
    along = [{"gx": lax.rem(z + j, n_i), "gy": g} for j in range(1, n_i)]
    barrier_with([(z >= 0, peer) for peer in (core, x_peer, y_peer, *along)])
    item_rows = moe_buf.shape[1]
    width = moe_buf.shape[2]
    half_width = gate_out.shape[1]
    owners = [lax.rem(z + n_i - 1 - i + n_i, n_i) for i in range(n_i)]

    def remote(src, dst, ssem, rsem, peer):
        return pltpu.make_async_remote_copy(
            src_ref=src,
            dst_ref=dst,
            send_sem=ssem,
            recv_sem=rsem,
            device_id=peer,
            device_id_type=pl.DeviceIdType.MESH,
        )

    def fetches(i):
        place = pl.ds(pl.multiple_of(owners[i] * item_rows, item_rows), item_rows)
        return [
            pltpu.make_async_copy(all_ref.at[place], moe_buf.at[i % 2], fetch_sem.at[0, i % 2]),
            pltpu.make_async_copy(pair_ref.at[place], pair_buf.at[i % 2], fetch_sem.at[1, i % 2]),
        ]

    def core_copy(i, q):
        return remote(
            held.at[i, flip(quads[q])],
            from_core.at[i, q],
            core_send.at[i, q],
            core_recv.at[i, q],
            core,
        )

    a_plan = ((0, 0, 0, x_peer), (0, 1, 0, y_peer), (1, 0, 1, x_peer), (2, 1, 1, y_peer))

    def a_copy(i, k):
        q, h, slot, peer = a_plan[k]
        return remote(
            held.at[i, quads[q], h],
            from_a.at[i, h, slot],
            a_send.at[i, k],
            a_recv.at[i, h, slot],
            peer,
        )

    b_plan = ((2, y_peer), (1, x_peer))

    def b_copy(i, h):
        q, peer = b_plan[h]
        return remote(
            held.at[i, quads[q], h], from_b.at[i, h], b_send.at[i, h], b_recv.at[i, h], peer
        )

    def z_copy(i):
        return remote(
            held.at[i, g], from_z.at[z], z_send.at[i], z_recv.at[z], {"gx": owners[i], "gy": g}
        )

    dot = partial(lax.dot_general, preferred_element_type=jnp.float32)
    last_dims = (((1,), (1,)), ((), ()))
    first_dims = (((0,), (0,)), ((), ()))

    def multiply(i):
        for copy in fetches(i):
            copy.wait()
        pair = pair_buf.at[i % 2]
        tile = 256

        @pl.loop(0, width // tile)
        def _(t):
            cols = pl.ds(pl.multiple_of(t * tile, tile), tile)
            total = dot(pair[:, :half_width], gate_ref[cols, :], last_dims)
            total = total + dot(pair[:, half_width:], up_ref[cols, :], last_dims)
            held[i, :, :, :, cols] = total.astype(jnp.bfloat16).reshape(held.shape[1:4] + (tile,))

        for q in range(4):
            core_copy(i, q).start()

    def accumulate(i):
        moe, pair = moe_buf.at[i % 2], pair_buf.at[i % 2]
        tile = 512

        @pl.loop(0, width // tile)
        def _(t):
            cols = pl.ds(pl.multiple_of(t * tile, tile), tile)
            grown = dot(moe[:, cols], pair[...], first_dims)
            if i == 0:
                gate_out[cols, :] = grown[:, :half_width]
                up_out[cols, :] = grown[:, half_width:]
            else:
                gate_out[cols, :] = gate_out[cols, :] + grown[:, :half_width]
                up_out[cols, :] = up_out[cols, :] + grown[:, half_width:]

        if i + 2 < n_i:
            for copy in fetches(i + 2):
                copy.start()

    def stage_a(i):
        for q in range(4):
            core_copy(i, q).wait_recv()
            for h in range(2):
                mine = held.at[i, quads[q], h]
                add_into(mine, (mine, from_core.at[i, q, h]), rows)
            for k in range(4):
                if a_plan[k][0] == q:
                    a_copy(i, k).start()

    def stage_b(i):
        for q, h, slot in ((2, 0, 0), (1, 1, 0), (3, 0, 1), (3, 1, 1)):
            mine, arrived = held.at[i, quads[q], h], from_a.at[i, h, slot]
            remote(mine, arrived, a_send.at[i, 0], a_recv.at[i, h, slot], core).wait_recv()
            add_into(mine, (mine, arrived), rows)
            if slot == 0:
                b_copy(i, h).start()

    def stage_c(i):
        for h in range(2):
            b_copy(i, h).wait_recv()
            mine = held.at[i, g, h]
            add_into(mine, (mine, from_b.at[i, h]), rows)
        if i < n_i - 1:
            z_copy(i).start()
        else:
            for j in range(n_i - 1):
                arrived = from_z.at[owners[j]]
                remote(held.at[j, g], arrived, z_send.at[j], z_recv.at[owners[j]], core).wait_recv()
            for h in range(2):
                terms = [held.at[i, g, h]] + [from_z.at[owners[j], h] for j in range(n_i - 1)]
                add_into(out_ref.at[h], terms, rows)

    for i in range(min(2, n_i)):
        for copy in fetches(i):
            copy.start()
    for t in range(n_i + 3):
        if t < n_i:
            multiply(t)
        if 0 <= t - 1 < n_i:
            stage_a(t - 1)
        if 0 <= t - 1 < n_i:
            accumulate(t - 1)
        if 0 <= t - 1 < n_i:
            stage_b(t - 1)
        if 0 <= t - 2 < n_i:
            stage_c(t - 2)
    for i in range(n_i):
        for q in range(4):
            core_copy(i, q).wait_send()
        for k in range(4):
            a_copy(i, k).wait_send()
        for h in range(2):
            b_copy(i, h).wait_send()
        if i < n_i - 1:
            z_copy(i).wait_send()


def pull_experts(all_moe, pair, gate_w, up_w, collective_id):
    n_i = lax.axis_size("gx")
    span = lax.axis_size("gy")
    total, width = all_moe.shape
    half_width = gate_w.shape[1]
    rows = total // (n_i * span) // 2
    half = (rows, width)
    bf16 = jnp.bfloat16
    dma = pltpu.SemaphoreType.DMA
    vmem = pl.BlockSpec(memory_space=pltpu.VMEM)
    hbm = pl.BlockSpec(memory_space=pl.ANY)
    out, gate_part, up_part = pl.pallas_call(
        partial(pull_kernel, n_i, rows),
        out_shape=(
            jax.ShapeDtypeStruct((2,) + half, jnp.float32),
            jax.ShapeDtypeStruct((width, half_width), jnp.float32),
            jax.ShapeDtypeStruct((width, half_width), jnp.float32),
        ),
        in_specs=[hbm, hbm, vmem, vmem],
        out_specs=(vmem, vmem, vmem),
        scratch_shapes=[
            pltpu.VMEM((n_i, span, 2) + half, bf16),
            pltpu.VMEM((n_i, 4, 2) + half, bf16),
            pltpu.VMEM((n_i, 2, 2) + half, bf16),
            pltpu.VMEM((n_i, 2) + half, bf16),
            pltpu.VMEM((n_i, 2) + half, bf16),
            pltpu.VMEM((2, span * 2 * rows, width), bf16),
            pltpu.VMEM((2, span * 2 * rows, 2 * half_width), bf16),
            dma((2, 2)),
            dma((n_i, 4)),
            dma((n_i, 4)),
            dma((n_i, 2)),
            dma((n_i,)),
            dma((n_i, 4)),
            dma((n_i, 2, 2)),
            dma((n_i, 2)),
            dma((n_i,)),
        ],
        compiler_params=pltpu.CompilerParams(
            collective_id=collective_id, has_side_effects=True, vmem_limit_bytes=67043328
        ),
        name="pull_experts",
    )(all_moe, pair, gate_w, up_w)
    return out.reshape(2 * rows, width), gate_part, up_part


def turn(values, cosine, sine):
    return values * cosine + pltpu.roll(values, values.shape[-1] // 2, 1) * sine


def spread_docs(docs_ref, row_docs, col_docs):
    lanes = docs_ref.shape[1]
    for j in range(docs_ref.shape[0]):
        line = docs_ref[j : j + 1, :].astype(jnp.float32)
        row_docs[j * lanes : (j + 1) * lanes, :] = jnp.broadcast_to(line, (lanes, lanes)).T
        col_docs[:, j * lanes : (j + 1) * lanes] = jnp.broadcast_to(line, (8, lanes))


def attend_kernel(
    heads,
    pieces,
    own_acts,
    query_weight,
    key_weight,
    value_weight,
    own_out_weight,
    own_cot,
    query_gain,
    key_gain,
    cosine_ref,
    sine_ref,
    docs_ref,
    attended_ref,
    acts_out,
    weight_out,
    full_out,
    all_cot,
    query_raw,
    key_raw,
    ready_ref,
    mixed_ref,
    totals_ref,
    peaks_ref,
    own_weight,
    row_docs,
    col_docs,
    part_ref,
    held,
    from_core,
    from_a,
    from_b,
    from_z,
    near_send,
    near_recv,
    near_local,
    far_send,
    far_recv,
    far_local,
    in_send,
    in_recv,
    in_local,
    out_send,
    out_recv,
    out_local,
    load_sem,
    core_send,
    a_send,
    b_send,
    z_send,
    core_recv,
    a_recv,
    b_recv,
    z_recv,
):
    n_z = lax.axis_size("gx")
    span = lax.axis_size("gy")
    for j, item in enumerate((query_weight, key_weight, value_weight)):
        own_weight[:, j * item.shape[1] : (j + 1) * item.shape[1]] = item[...]
    greet(n_z)
    in_start, in_relays, in_finish = chain_gather(
        n_z, own_weight, weight_out, in_send, in_recv, in_local
    )
    out_start, out_relays, out_finish = chain_gather(
        n_z, own_out_weight, full_out, out_send, out_recv, out_local
    )
    near, near_finish = gather_steps(1, span, own_acts, acts_out, near_send, near_recv, near_local)
    far, far_finish = gather_steps(n_z, span, own_cot, all_cot, far_send, far_recv, far_local)
    back = []
    scatter_kernel(
        False,
        pieces,
        part_ref.shape[3],
        part_ref,
        attended_ref,
        held,
        from_core,
        from_a,
        from_b,
        from_z,
        load_sem,
        core_send,
        a_send,
        b_send,
        z_send,
        core_recv,
        a_recv,
        b_recv,
        z_recv,
        parts=back,
    )
    f32, bf16 = jnp.float32, jnp.bfloat16
    dot = partial(lax.dot_general, preferred_element_type=f32)
    plain = (((1,), (0,)), ((), ()))
    last_dims = (((1,), (1,)), ((), ()))
    length = query_raw.shape[0]
    width = acts_out.shape[3]
    local = heads * HD
    block = 256
    scale = HD ** (-0.5)

    in_start()
    near[0]()
    far[0]()
    spread_docs(docs_ref, row_docs, col_docs)
    near[1]()
    near[2]()
    later = far[1:]
    for relay in in_relays:
        relay()
        for step in later[:1]:
            step()
        later = later[1:]
    out_start()
    in_finish()
    near_finish()
    waiting = [list(out_relays), list(later)]

    def pull(which):
        if waiting[which]:
            waiting[which].pop(0)()

    def project(source):
        cols = slice(source * local, (source + 1) * local)
        acts = acts_out[...].reshape(length, width)
        total = jnp.zeros((length, local), f32)
        depth = own_weight.shape[0]
        for owner in range(n_z):
            total = total + dot(
                acts[:, owner * depth : (owner + 1) * depth], weight_out[owner, :, cols], plain
            )
        return total

    for source, raw, gain in ((0, query_raw, query_gain), (1, key_raw, key_gain)):
        raw[...] = project(source)
        for h in range(heads):
            cols = slice(h * HD, (h + 1) * HD)

            @pl.loop(0, length // block)
            def _(t):
                at = pl.ds(pl.multiple_of(t * block, block), block)
                value = raw[at, cols]
                normed = value * lax.rsqrt(jnp.mean(value * value, axis=-1, keepdims=True) + EPSILON)
                turned = turn(normed * gain[...], cosine_ref[at, :], sine_ref[at, :])
                where = source * local + h * HD
                ready_ref[at, where : where + HD] = turned.astype(bf16)

        pull(source)

    ready_ref[:, 2 * local :] = project(2).astype(bf16)
    pull(0)
    lanes = lax.broadcasted_iota(jnp.int32, (block, HD), 1)
    peaks_ref[...] = jnp.full(peaks_ref.shape, NEGATIVE, f32)

    def mix(t):
        at = pl.ds(pl.multiple_of(t * block, block), block)
        same = row_docs[at, :1] == col_docs[:1, :]
        kept = jnp.zeros((block, HD), f32)
        for h in range(heads):
            query = ready_ref[at, h * HD : (h + 1) * HD]
            key = ready_ref[:, local + h * HD : local + (h + 1) * HD]
            value = ready_ref[:, 2 * local + h * HD : 2 * local + (h + 1) * HD]
            scores = jnp.where(same, dot(query, key, last_dims) * scale, NEGATIVE)
            highest = jnp.max(scores, axis=-1, keepdims=True)
            weights = jnp.exp(scores - highest)
            total = jnp.sum(weights, axis=-1, keepdims=True)
            shares = (weights * (1.0 / total)).astype(bf16)
            mixed_ref[at, h * HD : (h + 1) * HD] = dot(shares, value, plain).astype(bf16)
            kept = jnp.where(lanes == h, highest + jnp.log(total), kept)
            top = jnp.max(highest, axis=0, keepdims=True)
            peaks_ref[h : h + 1, :] = jnp.maximum(peaks_ref[h : h + 1, :], top)
        totals_ref[at, :] = kept

    blocks = length // block
    between = waiting[1].pop(0) if waiting[1] else lambda: None

    @pl.loop(0, blocks)
    def _(t):
        mix(t)
        pl.when(t == blocks // 2 - 1)(between)

    pull(1)
    for relay in waiting[0]:
        relay()
    out_finish()
    rows = part_ref.shape[3]
    per_owner = own_out_weight.shape[1] // block

    @pl.loop(0, n_z * per_owner)
    def _(t):
        cols = pl.ds(pl.multiple_of(t * block, block), block)
        inside = pl.ds(pl.multiple_of(lax.rem(t, per_owner) * block, block), block)
        sent = dot(mixed_ref[...], full_out[lax.div(t, per_owner), :, inside], plain).astype(bf16)
        sent = sent.reshape(span, pieces, 2, rows, block)
        for p in range(pieces):
            part_ref[p, :, :, :, cols] = sent[:, p]

    for step in back[:-1]:
        step()
        pull(1)
    for step in waiting[1]:
        step()
    back[-1]()
    far_finish()


def attend(
    acts, weights, out_weight, cot, query_gain, key_gain, tables, docs, collective_id, pieces=4
):
    tokens, width = acts.shape
    depth, local = weights[0].shape
    heads = local // HD
    n_z = lax.axis_size("gx")
    span = lax.axis_size("gy")
    length = span * tokens
    rows = tokens // (pieces * 2)
    half = (2, tokens // 2, width)
    piece = (rows, width)
    f32, bf16 = jnp.float32, jnp.bfloat16
    dma = pltpu.SemaphoreType.DMA
    vmem = pl.BlockSpec(memory_space=pltpu.VMEM)
    hbm = pl.BlockSpec(memory_space=pl.ANY)
    attended, seq, full, full_out, all_cot, *saved, peaks = pl.pallas_call(
        partial(attend_kernel, heads, pieces),
        out_shape=(
            jax.ShapeDtypeStruct((pieces, 2) + piece, f32),
            jax.ShapeDtypeStruct((span,) + half, bf16),
            jax.ShapeDtypeStruct((n_z, depth, 3 * local), bf16),
            jax.ShapeDtypeStruct((n_z,) + out_weight.shape, bf16),
            jax.ShapeDtypeStruct((n_z * span,) + half, bf16),
            jax.ShapeDtypeStruct((length, local), f32),
            jax.ShapeDtypeStruct((length, local), f32),
            jax.ShapeDtypeStruct((length, 3 * local), bf16),
            jax.ShapeDtypeStruct((length, local), bf16),
            jax.ShapeDtypeStruct((length, HD), f32),
            jax.ShapeDtypeStruct((8, HD), f32),
        ),
        in_specs=[vmem] * 11,
        out_specs=(vmem, vmem, vmem, vmem, hbm) + (vmem,) * 6,
        scratch_shapes=[
            pltpu.VMEM((depth, 3 * local), bf16),
            pltpu.VMEM((length, 128), f32),
            pltpu.VMEM((8, length), f32),
            pltpu.VMEM((pieces, span, 2) + piece, bf16),
            pltpu.VMEM((pieces, 4, 2) + piece, bf16),
            pltpu.VMEM((pieces, 4, 2) + piece, bf16),
            pltpu.VMEM((pieces, 2, 2) + piece, bf16),
            pltpu.VMEM((pieces, 2) + piece, bf16),
            pltpu.VMEM((1, 2, 16, 128), bf16),
            dma((24,)),
            dma((span, 2)),
            dma,
            dma((24 * (2 * n_z - 1),)),
            dma((n_z * span, 2)),
            dma,
            dma((2 * n_z,)),
            dma((n_z,)),
            dma,
            dma((2 * n_z,)),
            dma((n_z,)),
            dma,
            dma((pieces, 4)),
            dma((pieces, 4)),
            dma((pieces, 4)),
            dma((pieces, 2)),
            dma((pieces,)),
            dma((pieces, 4)),
            dma((pieces, 2, 2)),
            dma((pieces, 2)),
            dma((pieces,)),
        ],
        compiler_params=pltpu.CompilerParams(
            collective_id=collective_id, has_side_effects=True, vmem_limit_bytes=60 << 20
        ),
        name="attend",
    )(
        acts.reshape(half),
        *weights,
        out_weight,
        cot.reshape(half),
        query_gain.reshape(1, HD),
        key_gain.reshape(1, HD),
        *tables,
        docs,
    )
    return (
        attended.reshape(tokens, width),
        seq.reshape(length, width),
        full.reshape(n_z * depth, 3 * local),
        all_cot.reshape(n_z * span * tokens, width),
        (*saved, full_out),
        peaks,
    )


def attend_back_kernel(
    heads,
    pieces,
    own_grad,
    out_weight_ref,
    mixed_ref,
    ready_ref,
    query_raw,
    key_raw,
    totals_ref,
    query_gain,
    key_gain,
    attn_gain,
    cosine_ref,
    sine_ref,
    docs_ref,
    small_ref,
    acts_hbm,
    weight_hbm,
    grad_acts,
    query_sum,
    key_sum_out,
    value_sum_out,
    out_sum,
    small_sum,
    late_sum,
    weight_sum,
    gain_ref,
    late_ref,
    row_docs,
    col_docs,
    seq_ref,
    part_ref,
    acts_ref,
    weight_ref,
    grad_mixed,
    grad_heads,
    one_head,
    turned,
    key_sum,
    value_sum,
    out_sums,
    out_low,
    out_high,
    in_sums,
    in_low,
    in_high,
    held,
    from_core,
    from_a,
    from_b,
    from_z,
    copy_sem,
    near_send,
    near_recv,
    near_local,
    out_send,
    out_low_recv,
    out_high_recv,
    in_send,
    in_low_recv,
    in_high_recv,
    load_sem,
    core_send,
    a_send,
    b_send,
    z_send,
    core_recv,
    a_recv,
    b_recv,
    z_recv,
    *small_scratch,
):
    n_z = lax.axis_size("gx")
    span = lax.axis_size("gy")
    z = lax.axis_index("gx")
    g = lax.axis_index("gy")
    peers = [{"gx": z, "gy": g + bit - 2 * bit * ((g // bit) % 2)} for bit in (1, 2, 4)]
    peers += [{"gx": lax.rem(z + j, n_z), "gy": g} for j in range(1, n_z)]
    barrier_with([(z >= 0, peer) for peer in peers])
    out_start, out_relays, out_finish = chain_scatter(
        n_z, out_sums, out_sum, out_low, out_high, out_send, out_low_recv, out_high_recv
    )
    chains = [
        chain_scatter(
            n_z,
            in_sums.at[h],
            weight_sum.at[h],
            in_low.at[h],
            in_high.at[h],
            in_send.at[h],
            in_low_recv.at[h],
            in_high_recv.at[h],
        )
        for h in range(heads)
    ]
    near, near_finish = gather_steps(1, span, own_grad, seq_ref, near_send, near_recv, near_local)
    bits = span.bit_length() - 1
    half_scratch = len(small_scratch) // 2
    small = sum_steps(n_z, bits, small_ref, small_sum, *small_scratch[:half_scratch])
    late = sum_steps(n_z, bits, late_ref, late_sum, *small_scratch[half_scratch:])
    back = []
    scatter_kernel(
        False,
        pieces,
        part_ref.shape[3],
        part_ref,
        grad_acts,
        held,
        from_core,
        from_a,
        from_b,
        from_z,
        load_sem,
        core_send,
        a_send,
        b_send,
        z_send,
        core_recv,
        a_recv,
        b_recv,
        z_recv,
        parts=back,
    )
    f32, bf16 = jnp.float32, jnp.bfloat16
    dot = partial(lax.dot_general, preferred_element_type=f32)
    plain = (((1,), (0,)), ((), ()))
    last_dims = (((1,), (1,)), ((), ()))
    first_dims = (((0,), (0,)), ((), ()))
    length, local = query_raw.shape
    width = acts_ref.shape[1]
    rows = part_ref.shape[3]
    block = 256
    scale = HD ** (-0.5)
    copies = [
        pltpu.make_async_copy(acts_hbm, acts_ref, copy_sem.at[0]),
        pltpu.make_async_copy(weight_hbm, weight_ref, copy_sem.at[1]),
    ]
    near[0]()
    small[0]()
    spread_docs(docs_ref, row_docs, col_docs)
    for copy in copies:
        copy.start()
    near[1]()
    small[1]()
    near[2]()
    small[2]()
    near_finish()
    owned = width // n_z

    @pl.loop(0, width // block)
    def _(t):
        cols = pl.ds(pl.multiple_of(t * block, block), block)
        inside = pl.ds(pl.multiple_of(lax.rem(t, owned // block) * block, block), block)
        grad = seq_ref[:, :, :, cols].reshape(length, block)
        out_sums[lax.div(t, owned // block), inside, :] = dot(
            grad, mixed_ref[...], first_dims
        ).astype(bf16)

    out_start()
    total = jnp.zeros((length, local), f32)
    for owner in range(n_z):
        cols = slice(owner * owned, (owner + 1) * owned)
        grad = seq_ref[:, :, :, cols].reshape(length, owned)
        total = total + dot(grad, out_weight_ref[owner], last_dims)
    grad_mixed[...] = total.astype(bf16)
    small[3]()
    gain_ref[...] = jnp.zeros_like(gain_ref)
    late_ref[...] = jnp.zeros_like(late_ref)
    for h in range(heads):
        cols = slice(h * HD, (h + 1) * HD)
        key = ready_ref[:, local + h * HD : local + (h + 1) * HD]
        value = ready_ref[:, 2 * local + h * HD : 2 * local + (h + 1) * HD]
        key_sum[...] = jnp.zeros_like(key_sum)
        value_sum[...] = jnp.zeros_like(value_sum)

        @pl.loop(0, length // block)
        def _(t):
            at = pl.ds(pl.multiple_of(t * block, block), block)
            same = row_docs[at, :1] == col_docs[:1, :]
            query = ready_ref[at, cols]
            grad = grad_mixed[at, cols]
            scores = jnp.where(same, dot(query, key, last_dims) * scale, NEGATIVE)
            weights = jnp.exp(scores - totals_ref[at, h : h + 1])
            value_sum[...] += dot(weights.astype(bf16), grad, first_dims)
            pulled = dot(grad, value, last_dims)
            inner = jnp.sum(weights * pulled, axis=-1, keepdims=True)
            grad_scores = (weights * (pulled - inner)).astype(bf16)
            turned[at, :] = dot(grad_scores, key, plain) * scale
            key_sum[...] += dot(grad_scores, query, first_dims)

        for source, raw, gain, incoming, factor in (
            (0, query_raw, query_gain, turned, 1.0),
            (1, key_raw, key_gain, key_sum, scale),
        ):

            @pl.loop(0, length // block)
            def _(t):
                at = pl.ds(pl.multiple_of(t * block, block), block)
                back = turn(incoming[at, :] * factor, cosine_ref[at, :], -sine_ref[at, :])
                item = raw[at, cols]
                inverse = lax.rsqrt(jnp.mean(item * item, axis=-1, keepdims=True) + EPSILON)
                normed = item * inverse
                gain_ref[source : source + 1, :] += jnp.sum(back * normed, axis=0, keepdims=True)
                inner = back * gain[...]
                pulled = inverse * (
                    inner - normed * jnp.mean(inner * normed, axis=-1, keepdims=True)
                )
                where = source * local + h * HD
                grad_heads[at, where : where + HD] = pulled.astype(bf16)
                one_head[at, source * HD : (source + 1) * HD] = pulled.astype(bf16)

        where = 2 * local + h * HD
        grad_heads[:, where : where + HD] = value_sum[...].astype(bf16)
        one_head[:, 2 * HD :] = value_sum[...].astype(bf16)
        if h == 0:
            for copy in copies:
                copy.wait()
            for relay in out_relays:
                relay()
            out_finish()
            small[4]()
        else:
            chains[h - 1][1][0]()

        @pl.loop(0, width // block)
        def _(t):
            cols = pl.ds(pl.multiple_of(t * block, block), block)
            inside = pl.ds(pl.multiple_of(lax.rem(t, owned // block) * block, block), block)
            in_sums[h, lax.div(t, owned // block), inside, :] = dot(
                acts_ref[:, cols], one_head[...], first_dims
            ).astype(bf16)

        chains[h][0]()

    for chain in chains[:-1]:
        for relay in chain[1][1:2]:
            relay()

    @pl.loop(0, width // block)
    def _(t):
        cols = pl.ds(pl.multiple_of(t * block, block), block)
        pulled = dot(grad_heads[...], weight_ref[cols, :], last_dims)
        gained = jnp.sum(pulled * acts_ref[:, cols].astype(f32), axis=0, keepdims=True)
        gained = gained / attn_gain[:, cols]
        for j in range(block // 128):
            late_ref[0, pl.ds(t * (block // 128) + j, 1), :] = gained[:, j * 128 : (j + 1) * 128]
        sent = pulled.astype(bf16).reshape(span, pieces, 2, rows, block)
        for p in range(pieces):
            part_ref[p, :, :, :, cols] = sent[:, p]

    late_ref[1, :8, :] = gain_ref[...]
    small[5]()
    waiting = [relay for chain in chains[:-1] for relay in chain[1][2:]] + list(chains[-1][1])
    for i, step in enumerate(back[:-1]):
        step()
        if i < len(late) - 2:
            late[i]()
        if i % 2 == 0 and waiting:
            waiting.pop(0)()
    for relay in waiting:
        relay()
    for chain in chains:
        chain[2]()
    for step in late[min(len(late) - 2, len(back) - 1) :]:
        step()
    for h in range(heads):
        for j, target in enumerate((query_sum, key_sum_out, value_sum_out)):
            target[:, h * HD : (h + 1) * HD] = weight_sum[h, :, j * HD : (j + 1) * HD]
    back[-1]()


def attend_back(
    grad,
    saved,
    query_gain,
    key_gain,
    attn_gain,
    tables,
    docs,
    acts,
    weights,
    small,
    collective_id,
    pieces=4,
):
    query_raw, key_raw, ready, mixed, totals, out_weight = saved
    n_z = lax.axis_size("gx")
    span = lax.axis_size("gy")
    bits = span.bit_length() - 1
    tokens, width = grad.shape
    length, local = query_raw.shape
    heads = local // HD
    rows = tokens // (pieces * 2)
    halves = folded(small)
    half = (2, tokens // 2, width)
    piece = (rows, width)
    out_block = (n_z, width // n_z, local)
    in_block = (heads, n_z, width // n_z, 3 * HD)
    f32, bf16 = jnp.float32, jnp.bfloat16
    dma = pltpu.SemaphoreType.DMA
    vmem = pl.BlockSpec(memory_space=pltpu.VMEM)
    hbm = pl.BlockSpec(memory_space=pl.ANY)
    late_shape = (2, -(-width // (128 * 8)) * 8, 128)
    grad_acts, *in_sums, out_sum, small_sum, late_sum = pl.pallas_call(
        partial(attend_back_kernel, heads, pieces),
        out_shape=(
            jax.ShapeDtypeStruct((pieces, 2) + piece, f32),
            jax.ShapeDtypeStruct((in_block[2], local), f32),
            jax.ShapeDtypeStruct((in_block[2], local), f32),
            jax.ShapeDtypeStruct((in_block[2], local), f32),
            jax.ShapeDtypeStruct(out_block[1:], f32),
            jax.ShapeDtypeStruct(halves.shape, f32),
            jax.ShapeDtypeStruct(late_shape, f32),
        ),
        in_specs=[vmem] * 14 + [hbm] * 2,
        out_specs=(vmem,) * 7,
        scratch_shapes=[
            pltpu.VMEM((heads,) + in_block[2:], f32),
            pltpu.VMEM((8, HD), f32),
            pltpu.VMEM(late_shape, f32),
            pltpu.VMEM((length, 128), f32),
            pltpu.VMEM((8, length), f32),
            pltpu.VMEM((span,) + half, bf16),
            pltpu.VMEM((pieces, span, 2) + piece, bf16),
            pltpu.VMEM((length, width), bf16),
            pltpu.VMEM((width, 3 * local), bf16),
            pltpu.VMEM((length, local), bf16),
            pltpu.VMEM((length, 3 * local), bf16),
            pltpu.VMEM((length, 3 * HD), bf16),
            pltpu.VMEM((length, HD), f32),
            pltpu.VMEM((length, HD), f32),
            pltpu.VMEM((length, HD), f32),
            pltpu.VMEM(out_block, bf16),
            pltpu.VMEM(out_block, bf16),
            pltpu.VMEM(out_block, bf16),
            pltpu.VMEM(in_block, bf16),
            pltpu.VMEM(in_block, bf16),
            pltpu.VMEM(in_block, bf16),
            pltpu.VMEM((pieces, 4, 2) + piece, bf16),
            pltpu.VMEM((pieces, 4, 2) + piece, bf16),
            pltpu.VMEM((pieces, 2, 2) + piece, bf16),
            pltpu.VMEM((pieces, 2) + piece, bf16),
            pltpu.VMEM((1, 2, 16, 128), bf16),
            dma((2,)),
            dma((24,)),
            dma((span, 2)),
            dma,
            dma((n_z,)),
            dma((n_z,)),
            dma((n_z,)),
            dma((heads, n_z)),
            dma((heads, n_z)),
            dma((heads, n_z)),
            dma((pieces, 4)),
            dma((pieces, 4)),
            dma((pieces, 4)),
            dma((pieces, 2)),
            dma((pieces,)),
            dma((pieces, 4)),
            dma((pieces, 2, 2)),
            dma((pieces, 2)),
            dma((pieces,)),
        ]
        + sum_scratch(n_z, bits, halves.shape[1])
        + sum_scratch(n_z, bits, late_shape[1]),
        compiler_params=pltpu.CompilerParams(
            collective_id=collective_id, has_side_effects=True, vmem_limit_bytes=67043328
        ),
        name="attend_back",
    )(
        grad.reshape(half),
        out_weight,
        mixed,
        ready,
        query_raw,
        key_raw,
        totals,
        query_gain.reshape(1, HD),
        key_gain.reshape(1, HD),
        attn_gain.reshape(1, width),
        *tables,
        docs,
        halves,
        acts,
        weights,
    )
    return (
        grad_acts.reshape(tokens, width),
        in_sums,
        out_sum,
        small_sum.reshape(-1)[: small.shape[0]],
        (late_sum[0].reshape(-1)[:width], late_sum[1, 0], late_sum[1, 1]),
    )


def flat(parts):
    return jnp.concatenate([part.reshape(-1) for part in parts])


def unflat(vector, parts):
    ends = accumulate(part.size for part in parts)
    return [vector[end - part.size : end].reshape(part.shape) for end, part in zip(ends, parts)]


def norm_rows(values, gain_row):
    return (
        values * lax.rsqrt(jnp.mean(values * values, axis=-1, keepdims=True) + EPSILON) * gain_row
    )


def rotary(values):
    length = values.shape[0]
    halfway = values.shape[-1] // 2
    positions = jnp.arange(length, dtype=jnp.float32)
    frequency = jnp.exp(
        jnp.arange(halfway, dtype=jnp.float32) * (-2.0 * jnp.log(10000.0) / values.shape[-1])
    )
    angles = (positions[:, None] * frequency[None, :])[:, None, :]
    cosine = jnp.cos(angles)
    sine_table = jnp.sin(angles)
    first_half = values[..., :halfway]
    second = values[..., halfway:]
    return jnp.concatenate(
        [first_half * cosine - second * sine_table, second * cosine + first_half * sine_table],
        axis=-1,
    )


def prepare_heads(raw_heads, gain_row):
    return rotary(norm_rows(raw_heads, gain_row))


def route_gates(id_table, logits):
    shares = jax.nn.softmax(logits, axis=-1)
    experts = logits.shape[-1]
    matches = id_table[:, :, None] == jnp.arange(experts, dtype=jnp.int32)[None, None, :]
    chosen = jnp.sum(jnp.where(matches, shares[:, None, :], 0.0), axis=-1)
    return chosen / jnp.sum(chosen, axis=-1, keepdims=True)


def contract_rows(left_side, right_side):
    return lax.dot_general(
        left_side, right_side, (((0,), (0,)), ((), ())), preferred_element_type=jnp.float32
    )


def contract_cols(left_side, right_side):
    return lax.dot_general(
        left_side, right_side, (((1,), (1,)), ((), ())), preferred_element_type=jnp.float32
    )


def routed_experts(
    moe_in, cotangent, expert_ids, gate_share, router_weight, gate_weight, up_weight, down_weight
):
    tok_rows = moe_in.shape[0]
    experts = router_weight.shape[1]
    width_all = moe_in.shape[1]
    capacity = tok_rows * TOP * 3 // (2 * experts)
    route_count = tok_rows * TOP
    flat_ids = expert_ids.reshape(route_count)
    onehot = (flat_ids[:, None] == jnp.arange(experts, dtype=jnp.int32)[None, :]).astype(jnp.int32)
    earlier = jnp.cumsum(onehot, axis=0) - onehot
    slot_index = jnp.sum(earlier * onehot, axis=1)
    target = flat_ids * capacity + slot_index
    source = (
        jnp.full((experts * capacity,), tok_rows, jnp.int32)
        .at[target]
        .set(jnp.arange(route_count, dtype=jnp.int32) // TOP)
    )
    padded_in = jnp.concatenate([moe_in, jnp.zeros((1, width_all), jnp.bfloat16)], axis=0)
    packed = padded_in[source].reshape(experts, 1, capacity, width_all)
    outgoing = jnp.broadcast_to(packed, (experts, 2, capacity, width_all)).reshape(
        2 * experts, capacity, width_all
    )
    arrived = lax.all_to_all(outgoing, ("gx", "gy"), split_axis=0, concat_axis=1, tiled=True)[0]
    gate_in = gate_weight[0]
    up_in = up_weight[0]
    down_in = down_weight[0]
    gate_val = jnp.dot(arrived, gate_in, preferred_element_type=jnp.float32)
    up_val = jnp.dot(arrived, up_in, preferred_element_type=jnp.float32)
    hidden = (jax.nn.silu(gate_val) * up_val).astype(jnp.bfloat16)
    produced = jnp.dot(hidden, down_in, preferred_element_type=jnp.float32).astype(jnp.bfloat16)
    returned = lax.all_to_all(produced[None], ("gx", "gy"), split_axis=1, concat_axis=0, tiled=True)
    summed = (
        returned.reshape(experts, 2, capacity, width_all)
        .astype(jnp.float32)
        .sum(axis=1)
        .reshape(experts * capacity, width_all)
    )
    route_out = summed[target]
    gates_flat = gate_share.reshape(route_count)
    moe_out = jnp.sum((gates_flat[:, None] * route_out).reshape(tok_rows, TOP, width_all), axis=1)
    grad_out = cotangent.astype(jnp.float32)
    grad_gates = jnp.sum(
        route_out.reshape(tok_rows, TOP, width_all) * grad_out[:, None, :], axis=-1
    )
    slot_gate = jnp.zeros((experts * capacity,), jnp.float32).at[target].set(gates_flat)
    padded_grad = jnp.concatenate([grad_out, jnp.zeros((1, width_all), jnp.float32)], axis=0)
    grad_packed = (
        (slot_gate[:, None] * padded_grad[source])
        .astype(jnp.bfloat16)
        .reshape(experts, 1, capacity, width_all)
    )
    grad_outgoing = jnp.broadcast_to(grad_packed, (experts, 2, capacity, width_all)).reshape(
        2 * experts, capacity, width_all
    )
    grad_arrived = lax.all_to_all(
        grad_outgoing, ("gx", "gy"), split_axis=0, concat_axis=1, tiled=True
    )[0]
    rows_in, grad_use = (arrived, grad_arrived)
    gate_use, up_use, hidden_use = (gate_val, up_val, hidden)
    sigmoid_gate = jax.nn.sigmoid(gate_use)
    silu_gate = gate_use * sigmoid_gate
    grad_hidden = contract_cols(grad_use, down_in)
    down_part = contract_rows(hidden_use, grad_use)
    grad_gate = (
        grad_hidden * up_use * sigmoid_gate * (1.0 + gate_use * (1.0 - sigmoid_gate))
    ).astype(jnp.bfloat16)
    grad_up = (grad_hidden * silu_gate).astype(jnp.bfloat16)
    gate_part = contract_rows(rows_in, grad_gate)
    up_part = contract_rows(rows_in, grad_up)
    grad_in = contract_cols(grad_gate, gate_in) + contract_cols(grad_up, up_in)
    grad_back = lax.all_to_all(
        grad_in.astype(jnp.bfloat16)[None], ("gx", "gy"), split_axis=1, concat_axis=0, tiled=True
    )
    grad_summed = (
        grad_back.reshape(experts, 2, capacity, width_all)
        .astype(jnp.float32)
        .sum(axis=1)
        .reshape(experts * capacity, width_all)
    )
    grad_moe_in = jnp.sum(grad_summed[target].reshape(tok_rows, TOP, width_all), axis=1)
    return moe_out, grad_gates, grad_moe_in, gate_part, up_part, down_part


def dense_experts(
    moe_in, all_cot, expert_ids, gate_share, gate_weight, up_weight, down_weight
):
    devices = lax.axis_size("gx") * lax.axis_size("gy")
    experts = devices // 2
    matches = expert_ids[:, :, None] == jnp.arange(experts, dtype=jnp.int32)[None, None, :]
    dense_gates = jnp.sum(jnp.where(matches, gate_share[:, :, None], 0.0), axis=1)
    shares = jnp.repeat(dense_gates.T, 2, axis=0)[:, None, :]
    all_moe, pair, gate_dots, down_part, moe_out = run_experts(
        moe_in, all_cot, shares, gate_weight[0], up_weight[0], down_weight[0], 8
    )
    moe_out = moe_out.reshape(moe_in.shape)
    dots_experts = gate_dots.reshape(experts, 2, -1).sum(axis=1).T
    grad_gates = jnp.sum(jnp.where(matches, dots_experts[:, None, :], 0.0), axis=-1)
    grad_moe_in, gate_part, up_part = pull_experts(all_moe, pair, gate_weight[0], up_weight[0], 9)
    return moe_out, grad_gates, grad_moe_in, gate_part, up_part, down_part


def plain_attention(
    acts, in_weights, out_weight, query_gain, key_gain, attn_gain, doc_ids, cotangent
):
    seq_acts = lax.all_gather(acts, "gy", axis=0, tiled=True)
    full_in = lax.all_gather(jnp.concatenate(in_weights, axis=1), "gx", axis=0, tiled=True)
    out_rows = lax.all_gather(out_weight, "gx", axis=1, tiled=True)
    local_width = full_in.shape[1] // 3
    length = seq_acts.shape[0]
    local_heads = local_width // HD
    projected = jnp.dot(seq_acts, full_in, preferred_element_type=jnp.float32)
    queries = projected[:, :local_width]
    key_raw = projected[:, local_width : 2 * local_width]
    value_ready = (
        projected[:, 2 * local_width :].astype(jnp.bfloat16).reshape(length, local_heads, HD)
    )
    query_float, query_pull = jax.vjp(
        prepare_heads, queries.reshape(length, local_heads, HD), query_gain
    )
    key_float, key_pull = jax.vjp(prepare_heads, key_raw.reshape(length, local_heads, HD), key_gain)
    query_ready = query_float.astype(jnp.bfloat16)
    key_ready = key_float.astype(jnp.bfloat16)
    block_rows = min(512, length)
    block_count = length // block_rows
    score_scale = HD ** (-0.5)
    query_blocks = query_ready.reshape(block_count, block_rows, local_heads, HD)
    doc_blocks = doc_ids.reshape(block_count, block_rows)

    def block_scores(query_block, doc_block):
        scores = (
            jnp.einsum("qhd,khd->hqk", query_block, key_ready, preferred_element_type=jnp.float32)
            * score_scale
        )
        same_doc = doc_block[:, None] == doc_ids[None, :]
        return jnp.where(same_doc[None], scores, NEGATIVE)

    def forward_block(pieces):
        scores = block_scores(pieces[0], pieces[1])
        highest = jnp.max(scores, axis=-1, keepdims=True)
        weights = jnp.exp(scores - highest)
        totals = jnp.sum(weights, axis=-1, keepdims=True)
        shares = (weights / totals).astype(jnp.bfloat16)
        mixed_heads = jnp.einsum(
            "hqk,khd->qhd", shares, value_ready, preferred_element_type=jnp.float32
        )
        return (
            mixed_heads.astype(jnp.bfloat16),
            highest[..., 0] + jnp.log(totals[..., 0]),
            jnp.max(highest[..., 0], axis=-1),
        )

    mixed_blocks, log_totals, peak_blocks = lax.map(forward_block, (query_blocks, doc_blocks))
    mixed_seq = mixed_blocks.reshape(length, local_width)
    attended = lax.psum_scatter(
        jnp.dot(mixed_seq, out_rows, preferred_element_type=jnp.float32),
        "gy",
        scatter_dimension=0,
        tiled=True,
    )

    def back(grad_resid, small):
        seq_grad = lax.all_gather(grad_resid.astype(jnp.bfloat16), "gy", axis=0, tiled=True)
        grad_mixed = contract_cols(seq_grad, out_rows).astype(jnp.bfloat16)
        out_part = contract_rows(seq_grad, mixed_seq)

        def backward_block(running, pieces):
            grad_key, grad_value = running
            query_block, grad_block, log_block, doc_block = pieces
            scores = block_scores(query_block, doc_block)
            weights = jnp.exp(scores - log_block[..., None])
            grad_value = grad_value + jnp.einsum(
                "hqk,qhd->khd",
                weights.astype(jnp.bfloat16),
                grad_block,
                preferred_element_type=jnp.float32,
            )
            grad_weights = jnp.einsum(
                "qhd,khd->hqk", grad_block, value_ready, preferred_element_type=jnp.float32
            )
            inner_sum = jnp.sum(weights * grad_weights, axis=-1, keepdims=True)
            grad_scores = (weights * (grad_weights - inner_sum)).astype(jnp.bfloat16)
            grad_query = (
                jnp.einsum("hqk,khd->qhd", grad_scores, key_ready, preferred_element_type=jnp.float32)
                * score_scale
            )
            grad_key = (
                grad_key
                + jnp.einsum(
                    "hqk,qhd->khd", grad_scores, query_block, preferred_element_type=jnp.float32
                )
                * score_scale
            )
            return ((grad_key, grad_value), grad_query)

        empty_heads = jnp.zeros((length, local_heads, HD), jnp.float32)
        grad_mixed_blocks = grad_mixed.reshape(block_count, block_rows, local_heads, HD)
        (key_grad_heads, value_grad_heads), query_grad_blocks = lax.scan(
            backward_block,
            (empty_heads, empty_heads),
            (query_blocks, grad_mixed_blocks, log_totals, doc_blocks),
        )
        query_raw_grad, query_gain_part = query_pull(query_grad_blocks.reshape(length, local_heads, HD))
        key_raw_grad, key_gain_part = key_pull(key_grad_heads)
        grad_queries = query_raw_grad.reshape(length, local_width).astype(jnp.bfloat16)
        grad_keys = key_raw_grad.reshape(length, local_width).astype(jnp.bfloat16)
        grad_values = value_grad_heads.reshape(length, local_width).astype(jnp.bfloat16)
        grad_heads = jnp.concatenate([grad_queries, grad_keys, grad_values], axis=1)
        acts_part = contract_cols(grad_heads, full_in).astype(jnp.bfloat16)
        in_sum = lax.psum_scatter(
            contract_rows(seq_acts, grad_heads).astype(jnp.bfloat16),
            "gx",
            scatter_dimension=0,
            tiled=True,
        ).astype(jnp.float32)
        grad_acts = lax.psum_scatter(acts_part, "gy", scatter_dimension=0, tiled=True)
        out_sum = lax.psum_scatter(
            out_part.astype(jnp.bfloat16), "gx", scatter_dimension=0, tiled=True
        ).astype(jnp.float32)
        in_sums = (in_sum[:, :local_width], in_sum[:, local_width : 2 * local_width], in_sum[:, 2 * local_width :])
        gain_parts = (None, query_gain_part, key_gain_part)
        return grad_acts.astype(jnp.float32), in_sums, out_sum, sum_everywhere(small, 12), gain_parts

    return attended, jnp.max(peak_blocks, axis=0), None, back


def kernel_attention(
    acts, in_weights, out_weight, query_gain, key_gain, attn_gain, doc_ids, cotangent
):
    length = doc_ids.shape[0]
    halfway = HD // 2
    frequency = jnp.exp(
        jnp.arange(halfway, dtype=jnp.float32) * (-2.0 * jnp.log(10000.0) / HD)
    )
    angles = jnp.arange(length, dtype=jnp.float32)[:, None] * frequency[None, :]
    cosine, sine = jnp.cos(angles), jnp.sin(angles)
    tables = (
        jnp.concatenate([cosine, cosine], axis=1),
        jnp.concatenate([-sine, sine], axis=1),
    )
    docs = doc_ids.reshape(-1, 128)
    attended, seq_acts, full_in, all_cot, saved, peaks = attend(
        acts, in_weights, out_weight, cotangent, query_gain, key_gain, tables, docs, 10
    )
    heads = in_weights[0].shape[1] // HD

    def back(grad_resid, small):
        return attend_back(
            grad_resid.astype(jnp.bfloat16),
            saved,
            query_gain,
            key_gain,
            attn_gain,
            tables,
            docs,
            seq_acts,
            full_in,
            small,
            11,
        )

    return attended, peaks[:heads, 0], all_cot, back


def local(
    tokens,
    cotangent,
    expert_ids,
    doc_ids,
    clip_rank,
    attn_gain,
    moe_gain,
    query_gain,
    key_gain,
    query_weight,
    key_weight,
    value_weight,
    out_weight,
    router_weight,
    gate_weight,
    up_weight,
    down_weight,
):
    inputs = tokens.astype(jnp.float32)
    acts_float, norm_pull = jax.vjp(norm_rows, inputs, attn_gain)
    acts_low = acts_float.astype(jnp.bfloat16)
    in_weights = (query_weight, key_weight, value_weight)
    by_kernels = lax.axis_size("gy") == 8
    local_width = query_weight.shape[1]
    local_heads = local_width // HD
    attention = kernel_attention if by_kernels else plain_attention
    attended, own_peaks, all_cot, attention_back = attention(
        acts_low, in_weights, out_weight, query_gain, key_gain, attn_gain, doc_ids, cotangent
    )
    start_head = lax.axis_index("gy") * local_heads
    peak_slots = lax.dynamic_update_slice(
        jnp.zeros((lax.axis_size("gx"), NH), jnp.float32),
        own_peaks[None],
        (lax.axis_index("gx"), start_head),
    )
    residual = inputs + attended
    moe_float, moe_pull = jax.vjp(norm_rows, residual, moe_gain)
    moe_in = moe_float.astype(jnp.bfloat16)
    logits = jnp.dot(moe_in, router_weight, preferred_element_type=jnp.float32)
    gate_share, gate_pull = jax.vjp(partial(route_gates, expert_ids), logits)
    if by_kernels and router_weight.shape[1] <= 2 * TOP:
        moe_out, grad_gates, grad_moe_in, gate_part, up_part, down_part = dense_experts(
            moe_in, all_cot, expert_ids, gate_share, gate_weight, up_weight, down_weight
        )
    else:
        moe_out, grad_gates, grad_moe_in, gate_part, up_part, down_part = routed_experts(
            moe_in,
            cotangent,
            expert_ids,
            gate_share,
            router_weight,
            gate_weight,
            up_weight,
            down_weight,
        )
    output = (residual + moe_out).astype(jnp.bfloat16)
    grad_out = cotangent.astype(jnp.float32)
    (grad_logits,) = gate_pull(grad_gates)
    grad_logits_low = grad_logits.astype(jnp.bfloat16)
    router_part = contract_rows(moe_in, grad_logits_low)
    grad_moe_in = grad_moe_in + contract_cols(grad_logits_low, router_weight)
    grad_resid_norm, moe_gain_part = moe_pull(grad_moe_in)
    grad_resid = grad_out + grad_resid_norm
    early = (moe_gain_part, router_part.T, peak_slots)
    grad_acts, in_sums, out_sum, early_sum, late = attention_back(grad_resid, flat(early))
    query_sum, key_sum, value_sum = in_sums
    moe_gain_grad, router_flat, peaks = unflat(early_sum, early)
    norm_input_grad, attn_gain_part = norm_pull(grad_acts)
    input_grad = grad_resid + norm_input_grad
    if late[0] is None:
        late = (attn_gain_part, *late[1:])
        late = unflat(sum_everywhere(flat(late), 5), late)
    attn_gain_grad, query_gain_grad, key_gain_grad = late
    router_grad = router_flat.T
    peak_global = jnp.max(peaks, axis=0)
    ranked = -jnp.sort(-peak_global)
    limit = jnp.sum(jnp.where(jnp.arange(NH, dtype=jnp.int32) == clip_rank[0], ranked, 0.0))
    factors = jnp.where(peak_global > limit, limit / peak_global, 1.0)
    own_factors = lax.dynamic_slice_in_dim(factors, start_head, local_heads)
    columns = jnp.repeat(jnp.sqrt(own_factors), HD)
    query_clipped = (query_weight.astype(jnp.float32) * columns[None, :]).astype(jnp.bfloat16)
    key_clipped = (key_weight.astype(jnp.float32) * columns[None, :]).astype(jnp.bfloat16)
    return (
        output,
        input_grad,
        attn_gain_grad,
        moe_gain_grad,
        query_gain_grad,
        key_gain_grad,
        query_sum,
        key_sum,
        value_sum,
        out_sum.T,
        router_grad,
        gate_part[None],
        up_part[None],
        down_part[None],
        query_clipped,
        key_clipped,
        factors,
    )


def solution(mesh):
    placed = (
        P(("gx", "gy"), None),
        P(("gx", "gy"), None),
        P(("gx", "gy"), None),
        P("gx"),
        P(),
        P(),
        P(),
        P(),
        P(),
        P("gx", "gy"),
        P("gx", "gy"),
        P("gx", "gy"),
        P("gy", "gx"),
        P(),
        P(("gx", "gy"), None, None),
        P(("gx", "gy"), None, None),
        P(("gx", "gy"), None, None),
    )
    return jax.shard_map(
        local,
        mesh=mesh,
        in_specs=placed,
        out_specs=(
            P(("gx", "gy"), None),
            P(("gx", "gy"), None),
            P(),
            P(),
            P(),
            P(),
            P("gx", "gy"),
            P("gx", "gy"),
            P("gx", "gy"),
            P("gy", "gx"),
            P(),
            P(("gx", "gy"), None, None),
            P(("gx", "gy"), None, None),
            P(("gx", "gy"), None, None),
            P("gx", "gy"),
            P("gx", "gy"),
            P(),
        ),
        check_vma=False,
    )
```

```python
from functools import partial
from itertools import accumulate

import jax
import jax.numpy as jnp
from jax import lax
from jax.experimental import pallas as pl
from jax.experimental.pallas import tpu as pltpu
from jax.sharding import PartitionSpec as P

NH = 16
HD = 128
TOP = 8


EPSILON = 1e-06
NEGATIVE = -1e30


def flip(index):
    return index + 1 - 2 * (index % 2)


def barrier_with(partners):
    barrier = pltpu.get_barrier_semaphore()
    for ok, device in partners:
        @pl.when(ok)
        def _():
            pl.semaphore_signal(barrier, inc=1, device_id=device, device_id_type=pl.DeviceIdType.MESH)
    pl.semaphore_wait(barrier, sum(ok.astype(jnp.int32) for ok, _ in partners))

def always(ok, other):
    if ok is True:
        return other
    return ok if other is True else jnp.logical_and(ok, other)


def run_if(ok, action):
    if ok is True:
        action()
    else:
        pl.when(ok)(action)


def chain_gather(n_z, own_ref, out_ref, send_sem, recv_sem, local_sem):
    z = lax.axis_index("gx")
    g = lax.axis_index("gy")

    def hop(source, owner, k, peer):
        return pltpu.make_async_remote_copy(
            src_ref=source,
            dst_ref=out_ref.at[owner],
            send_sem=send_sem.at[k],
            recv_sem=recv_sem.at[owner],
            device_id={"gx": peer, "gy": g},
            device_id_type=pl.DeviceIdType.MESH,
        )

    local = pltpu.make_async_copy(own_ref, out_ref.at[z], local_sem)
    upward = [(z < n_z - 1, lambda: hop(own_ref, z, 0, z + 1))]
    downward = [(z > 0, lambda: hop(own_ref, z, n_z, z - 1))]
    for d in range(1, n_z - 1):
        upward.append(
            (
                jnp.logical_and(z >= d, z < n_z - 1),
                lambda d=d: hop(out_ref.at[z - d], z - d, d, z + 1),
            )
        )
        downward.append(
            (
                jnp.logical_and(z < n_z - d, z > 0),
                lambda d=d: hop(out_ref.at[z + d], z + d, n_z + d, z - 1),
            )
        )

    def start():
        local.start()
        for ok, copy in (upward[0], downward[0]):
            run_if(ok, lambda copy=copy: copy().start())

    def relay(d):
        run_if(z >= d, lambda: hop(own_ref, z - d, 0, z).wait_recv())
        if d < n_z - 1:
            run_if(upward[d][0], lambda: upward[d][1]().start())
        run_if(z < n_z - d, lambda: hop(own_ref, z + d, 0, z).wait_recv())
        if d < n_z - 1:
            run_if(downward[d][0], lambda: downward[d][1]().start())

    def finish():
        local.wait()
        for ok, copy in upward + downward:
            run_if(ok, lambda copy=copy: copy().wait_send())

    return start, [partial(relay, d) for d in range(1, n_z)], finish


def gather_steps(n_z, span, own_ref, out_ref, send_sem, recv_sem, local_sem):
    z = lax.axis_index("gx")
    g = lax.axis_index("gy")
    flip_x = g + 2 - 4 * ((g // 2) % 2)
    flip_y = g + 4 - 8 * ((g // 4) % 2)
    flip_both = flip_x + flip_y - g
    core = {"gx": z, "gy": flip(g)}
    x_peer = {"gx": z, "gy": flip_x}
    y_peer = {"gx": z, "gy": flip_y}
    above = {"gx": z + 1, "gy": g}
    below = {"gx": z - 1, "gy": g}
    first_z = z if n_z > 1 else 0
    sends = []

    def send(ok, b, h, peer, own=False):
        k = len(sends)

        def make():
            return pltpu.make_async_remote_copy(
                src_ref=own_ref.at[h] if own else out_ref.at[b, h],
                dst_ref=out_ref.at[b, h],
                send_sem=send_sem.at[k],
                recv_sem=recv_sem.at[b, h],
                device_id=peer,
                device_id_type=pl.DeviceIdType.MESH,
            )

        sends.append((ok, make))
        run_if(ok, lambda: make().start())

    def arrive(ok, b, h):
        def wait():
            pltpu.make_async_remote_copy(
                src_ref=out_ref.at[b, h],
                dst_ref=out_ref.at[b, h],
                send_sem=send_sem.at[0],
                recv_sem=recv_sem.at[b, h],
                device_id=core,
                device_id_type=pl.DeviceIdType.MESH,
            ).wait_recv()

        run_if(ok, wait)

    local = pltpu.make_async_copy(own_ref, out_ref.at[first_z * span + g], local_sem)
    items = [(True, first_z, 0)]
    for d in range(1, n_z):
        items += [(z >= d, z - d, -d), (z < n_z - d, z + d, d)]

    upward = [always(item[0], z < n_z - 1) for item in items]
    downward = [always(item[0], z > 0) for item in items]

    near_b = [owner * span + g for _, owner, _ in items]
    x_b = [owner * span + flip_x for _, owner, _ in items]
    y_b = [owner * span + flip_y for _, owner, _ in items]
    both_b = [owner * span + flip_both for _, owner, _ in items]

    def first(i):
        ok, _, d = items[i]
        b = near_b[i]
        own = d == 0
        if own:
            local.start()
        else:
            arrive(ok, b, 0)
            arrive(ok, b, 1)
        for h in range(2):
            if n_z > 1 and d <= 0:
                send(upward[i], b, h, above, own)
            if n_z > 1 and d >= 0:
                send(downward[i], b, h, below, own)
        for h, peer in ((0, x_peer), (1, y_peer), (1, x_peer), (0, y_peer), (0, core), (1, core)):
            send(ok, b, h, peer, own)

    def second(i):
        ok = items[i][0]
        for b, h, peer in ((x_b[i], 0, y_peer), (y_b[i], 1, x_peer)):
            arrive(ok, b, h)
            send(ok, b, h, peer)
            send(ok, b, h, core)

    def third(i):
        ok = items[i][0]
        for b, h in ((both_b[i], 0), (both_b[i], 1), (y_b[i], 0), (x_b[i], 1)):
            arrive(ok, b, h)
            send(ok, b, h, core)

    n = len(items)

    def step(i):
        if i < n:
            first(i)
        if 1 <= i <= n:
            second(i - 1)
        if i >= 2:
            third(i - 2)

    def finish():
        for ok, owner, _ in items:
            for side in (g, flip_x, flip_y, flip_both):
                for h in range(2):
                    arrive(ok, owner * span + flip(side), h)
        local.wait()
        for ok, make in sends:
            run_if(ok, lambda make=make: make().wait_send())

    return [partial(step, i) for i in range(n + 2)], finish


def greet(n_z):
    z = lax.axis_index("gx")
    g = lax.axis_index("gy")
    peers = [
        (z >= 0, {"gx": z, "gy": g + bit - 2 * bit * ((g // bit) % 2)}) for bit in (1, 2, 4)
    ]
    if n_z > 1:
        peers += [(z < n_z - 1, {"gx": z + 1, "gy": g}), (z > 0, {"gx": z - 1, "gy": g})]
    barrier_with(peers)


def add_into(dst, parts, rows):
    step = min(rows, 32)

    @pl.loop(0, rows // step)
    def _(r):
        at = pl.ds(pl.multiple_of(r * step, step), step)
        if len(parts) == 2 and dst.dtype == jnp.bfloat16:
            dst[at, :] = parts[0][at, :] + parts[1][at, :]
        else:
            total = parts[0][at, :].astype(jnp.float32)
            for term in parts[1:]:
                total = total + term[at, :].astype(jnp.float32)
            dst[at, :] = total.astype(dst.dtype)


def scatter_kernel(chain, n_i, rows, part_ref, out_ref, held, from_core, from_a, from_b, from_z,
                   load_sem, core_send, a_send, b_send, z_send, core_recv, a_recv, b_recv, z_recv, beside=None, parts=None):
    z = lax.axis_index("gx"); g = lax.axis_index("gy")
    flip_x = g + 2 - 4 * ((g // 2) % 2)
    flip_y = g + 4 - 8 * ((g // 4) % 2)
    quads = (flip_x + flip_y - g, flip_x, flip_y, g)
    core = {"gx": z, "gy": flip(g)}
    xn = {"gx": z, "gy": flip_x}
    yn = {"gx": z, "gy": flip_y}
    every = z >= 0
    partners = [(every, core), (every, xn), (every, yn)]
    if chain:
        partners += [(every, {"gx": lax.rem(z + j, n_i), "gy": g}) for j in range(1, n_i)]
    if beside:
        n_z = lax.axis_size("gx")
        partners += [(z < n_z - 1, {"gx": z + 1, "gy": g}), (z > 0, {"gx": z - 1, "gy": g})]
    if parts is None:
        barrier_with(partners)
    if beside:
        beside[0]()
    mesh_id = pl.DeviceIdType.MESH

    def item(i):
        return lax.rem(z + n_i - 1 - i + n_i, n_i) if chain else i

    def block(it, gg):
        return part_ref.at[it, gg]

    def remote(src, dst, ssem, rsem, dev):
        return pltpu.make_async_remote_copy(src_ref=src, dst_ref=dst, send_sem=ssem, recv_sem=rsem, device_id=dev, device_id_type=mesh_id)

    def core_copy(i, q):
        it = item(i)
        return remote(block(it, flip(quads[q])), from_core.at[it, q], core_send.at[i, q], core_recv.at[it, q], core)

    def load(i, q):
        it = item(i)
        return pltpu.make_async_copy(block(it, quads[q]), held.at[it, q], load_sem.at[i, q])

    a_plan = ((0, 0, 0, xn), (0, 1, 0, yn), (1, 0, 1, xn), (2, 1, 1, yn))
    def a_copy(i, k):
        it = item(i)
        q, h, slot, dev = a_plan[k]
        return remote(held.at[it, q, h], from_a.at[it, h, slot], a_send.at[i, k], a_recv.at[it, h, slot], dev)

    b_plan = ((2, 0, yn), (1, 1, xn))
    def b_copy(i, h):
        it = item(i)
        q, _, dev = b_plan[h]
        return remote(held.at[it, q, h], from_b.at[it, h], b_send.at[i, h], b_recv.at[it, h], dev)

    def z_copy(i):
        it = item(i)
        return remote(held.at[it, 3], from_z.at[z], z_send.at[i], z_recv.at[z], {"gx": it, "gy": g})

    def z_arrival(i):
        it = item(i)
        return remote(held.at[it, 3], from_z.at[it], z_send.at[i], z_recv.at[it], core)

    def begin():
        for i in range(n_i):
            for q in range(4):
                core_copy(i, q).start()
                load(i, q).start()

    def stage_a(i):
        it = item(i)
        for q in range(4):
            load(i, q).wait()
            core_copy(i, q).wait_recv()
            for h in range(2):
                add_into(held.at[it, q, h], (held.at[it, q, h], from_core.at[it, q, h]), rows)
            for k in range(4):
                if a_plan[k][0] == q:
                    a_copy(i, k).start()

    def stage_b(i):
        it = item(i)
        for q, h, slot in ((2, 0, 0), (1, 1, 0), (3, 0, 1), (3, 1, 1)):
            remote(held.at[it, q, h], from_a.at[it, h, slot], a_send.at[i, 0], a_recv.at[it, h, slot], core).wait_recv()
            add_into(held.at[it, q, h], (held.at[it, q, h], from_a.at[it, h, slot]), rows)
            if slot == 0:
                b_copy(i, h).start()

    def stage_c(i):
        it = item(i)
        for h in range(2):
            b_copy(i, h).wait_recv()
            if chain:
                add_into(held.at[it, 3, h], (held.at[it, 3, h], from_b.at[it, h]), rows)
            else:
                add_into(out_ref.at[it, h], (held.at[it, 3, h], from_b.at[it, h]), rows)

    def stage_d(i):
        if i < n_i - 1:
            z_copy(i).start()
        else:
            for j in range(n_i - 1):
                z_arrival(j).wait_recv()
            for h in range(2):
                add_into(
                    out_ref.at[h],
                    [held.at[item(i), 3, h]] + [from_z.at[item(j), h] for j in range(n_i - 1)],
                    rows,
                )

    def step(i):
        if i < n_i:
            stage_a(i)
        if 0 <= i - 1 < n_i:
            stage_b(i - 1)
        if 0 <= i - 2 < n_i:
            stage_c(i - 2)
        if chain and 0 <= i - 2 < n_i:
            stage_d(i - 2)

    def finish():
        for i in range(n_i):
            for q in range(4):
                core_copy(i, q).wait_send()
            for k in range(4):
                a_copy(i, k).wait_send()
            for h in range(2):
                b_copy(i, h).wait_send()
            if chain and i < n_i - 1:
                z_copy(i).wait_send()

    if parts is not None:
        parts.extend([begin] + [partial(step, i) for i in range(n_i + 2)] + [finish])
        return
    begin()
    for i in range(n_i + 2):
        step(i)
        if beside and i == n_i:
            beside[1][0]()
    if beside:
        for relay in beside[1][1:]:
            relay()
        beside[2]()
    finish()


def sum_steps(n_z, bits, vec_ref, out_ref, held, arrived, from_z, send_sem, z_send, recv_sem, z_recv):
    z = lax.axis_index("gx")
    g = lax.axis_index("gy")
    side = lax.rem(g, 2)
    peers = [
        {"gx": z, "gy": g + bit - 2 * bit * ((g // bit) % 2)}
        for bit in (2**power for power in range(bits))
    ]
    others = [{"gx": lax.rem(z + j, n_z), "gy": g} for j in range(1, n_z)]

    def remote(src, dst, ssem, rsem, peer):
        return pltpu.make_async_remote_copy(
            src_ref=src,
            dst_ref=dst,
            send_sem=ssem,
            recv_sem=rsem,
            device_id=peer,
            device_id_type=pl.DeviceIdType.MESH,
        )

    def hop(k):
        source = vec_ref.at[1 - side] if k == 0 else held.at[k - 1]
        return remote(source, arrived.at[k], send_sem.at[k], recv_sem.at[k], peers[k])

    def across(j):
        return remote(held.at[bits - 1], from_z.at[j], z_send.at[j], z_recv.at[j], others[j])

    def back():
        return remote(held.at[bits], arrived.at[bits], send_sem.at[bits], recv_sem.at[bits], peers[0])

    def onward(k):
        hop(k).wait()
        held[k] = (vec_ref[side] if k == 0 else held[k - 1]) + arrived[k]
        if k + 1 < bits:
            hop(k + 1).start()
        else:
            for j in range(n_z - 1):
                across(j).start()

    def gather():
        for j in range(n_z - 1):
            across(j).wait()
        total = jnp.zeros_like(held[0])
        for owner in range(n_z):
            term = held[bits - 1]
            for j in range(1, n_z):
                term = jnp.where(lax.rem(z - j + n_z, n_z) == owner, from_z[j - 1], term)
            total = total + term
        held[bits] = total
        back().start()
        out_ref[side] = total

    def finish():
        back().wait()
        out_ref[1 - side] = arrived[bits]

    return [lambda: hop(0).start()] + [partial(onward, k) for k in range(bits)] + [gather, finish]


def sum_kernel(n_z, bits, *refs):
    z = lax.axis_index("gx")
    g = lax.axis_index("gy")
    peers = [
        {"gx": z, "gy": g + bit - 2 * bit * ((g // bit) % 2)}
        for bit in (2**power for power in range(bits))
    ]
    peers += [{"gx": lax.rem(z + j, n_z), "gy": g} for j in range(1, n_z)]
    barrier_with([(z >= 0, peer) for peer in peers])
    for step in sum_steps(n_z, bits, *refs):
        step()


def folded(vector):
    rows = -(-vector.shape[0] // (128 * 16)) * 8
    return jnp.pad(vector, (0, 2 * rows * 128 - vector.shape[0])).reshape(2, rows, 128)


def sum_scratch(n_z, bits, rows):
    dma = pltpu.SemaphoreType.DMA
    return [
        pltpu.VMEM((bits + 1, rows, 128), jnp.float32),
        pltpu.VMEM((bits + 1, rows, 128), jnp.float32),
        pltpu.VMEM((n_z - 1, rows, 128), jnp.float32),
        dma((bits + 1,)),
        dma((n_z - 1,)),
        dma((bits + 1,)),
        dma((n_z - 1,)),
    ]


def sum_everywhere(vector, collective_id):
    n_z = lax.axis_size("gx")
    bits = lax.axis_size("gy").bit_length() - 1
    halves = folded(vector)
    out = pl.pallas_call(
        partial(sum_kernel, n_z, bits),
        out_shape=jax.ShapeDtypeStruct(halves.shape, jnp.float32),
        in_specs=[pl.BlockSpec(memory_space=pltpu.VMEM)],
        out_specs=pl.BlockSpec(memory_space=pltpu.VMEM),
        scratch_shapes=sum_scratch(n_z, bits, halves.shape[1]),
        compiler_params=pltpu.CompilerParams(collective_id=collective_id, has_side_effects=True),
        name="sum_everywhere",
    )(halves)
    return out.reshape(-1)[: vector.shape[0]]


def chain_scatter(n_z, part_ref, out_ref, from_low, from_high, send_sem, low_recv, high_recv):
    z = lax.axis_index("gx")
    g = lax.axis_index("gy")
    rows = part_ref.shape[1]

    def up(dest):
        return pltpu.make_async_remote_copy(
            src_ref=part_ref.at[dest],
            dst_ref=from_low.at[dest],
            send_sem=send_sem.at[dest],
            recv_sem=low_recv.at[dest],
            device_id={"gx": z + 1, "gy": g},
            device_id_type=pl.DeviceIdType.MESH,
        )

    def down(dest):
        return pltpu.make_async_remote_copy(
            src_ref=part_ref.at[dest],
            dst_ref=from_high.at[dest],
            send_sem=send_sem.at[dest],
            recv_sem=high_recv.at[dest],
            device_id={"gx": z - 1, "gy": g},
            device_id_type=pl.DeviceIdType.MESH,
        )

    def start():
        for k in range(n_z - 1):
            run_if(z == 0, lambda k=k: up(n_z - 1 - k).start())
            run_if(z == n_z - 1, lambda k=k: down(k).start())

    def pass_up(dest):
        up(dest).wait_recv()
        add_into(part_ref.at[dest], (part_ref.at[dest], from_low.at[dest]), rows)
        up(dest).start()

    def pass_down(dest):
        down(dest).wait_recv()
        add_into(part_ref.at[dest], (part_ref.at[dest], from_high.at[dest]), rows)
        down(dest).start()

    def relay(time):
        for k in range(time):
            low, dest = time - k, n_z - 1 - k
            if 0 < low < dest:
                run_if(z == low, partial(pass_up, dest))
            high, dest = n_z - 1 - (time - k), k
            if dest < high < n_z - 1:
                run_if(z == high, partial(pass_down, dest))

    def finish():
        for dest in range(n_z):
            terms = [part_ref.at[dest]]
            terms += [from_low.at[dest]] if dest > 0 else []
            terms += [from_high.at[dest]] if dest < n_z - 1 else []

            def last(dest=dest, terms=terms):
                if dest > 0:
                    up(dest).wait_recv()
                if dest < n_z - 1:
                    down(dest).wait_recv()
                add_into(out_ref, terms, rows)

            run_if(z == dest, last)
        for dest in range(n_z):
            run_if(z != dest, lambda dest=dest: up(dest).wait_send())

    return start, [partial(relay, time) for time in range(1, n_z)], finish


def expert_kernel(n_z, span, own_ref, cot_ref, share_ref, gate_ref, up_ref, down_ref,
                  all_ref, pair_ref, dots_ref, down_out, out_ref,
                  moe_buf, cot_buf, share_buf, pair_stage, dots_buf,
                  gate_val, up_val, scaled, scaled_t, down_t,
                  held, from_core, from_a, from_b, from_z,
                  send_sem, recv_sem, local_sem, fetch_sem, store_sem,
                  core_send, a_send, b_send, z_send, core_recv, a_recv, b_recv, z_recv,
                  shares_in, dots_own, share_send, share_recv, dots_send, dots_recv):
    z = lax.axis_index("gx")
    g = lax.axis_index("gy")
    rows = own_ref.shape[1]
    block = 2 * rows
    step_rows = moe_buf.shape[1]
    steps = 2 * n_z
    flip_x = g + 2 - 4 * ((g // 2) % 2)
    flip_y = g + 4 - 8 * ((g // 4) % 2)
    flip_both = flip_x + flip_y - g
    core = {"gx": z, "gy": flip(g)}
    x_peer = {"gx": z, "gy": flip_x}
    y_peer = {"gx": z, "gy": flip_y}
    above = {"gx": z + 1, "gy": g}
    below = {"gx": z - 1, "gy": g}

    order = [z]
    candidates = []
    for d in range(1, n_z):
        candidates += [(z >= d, z - d), (z < n_z - d, z + d)]
    for k in range(1, n_z):
        rank, chosen = 0, 0
        for ok, owner in candidates:
            ok = ok.astype(jnp.int32)
            rank = rank + ok
            chosen = chosen + ok * (rank == k).astype(jnp.int32) * owner
        order.append(chosen)

    onward = [(z < n_z - 1, z > 0)]
    for owner in order[1:]:
        onward.append(
            (
                jnp.logical_and(owner < z, z < n_z - 1),
                jnp.logical_and(owner > z, z > 0),
            )
        )
    devices = n_z * span
    rank = z * span + g

    def device(number):
        return {"gx": lax.div(number, span), "gy": lax.rem(number, span)}

    barrier = pltpu.get_barrier_semaphore()

    @pl.loop(1, devices)
    def _(j):
        pl.semaphore_signal(
            barrier,
            inc=1,
            device_id=device(lax.rem(rank + j, devices)),
            device_id_type=pl.DeviceIdType.MESH,
        )

    pl.semaphore_wait(barrier, devices - 1)

    def share_copy(number):
        return pltpu.make_async_remote_copy(
            src_ref=share_ref.at[number],
            dst_ref=shares_in.at[rank],
            send_sem=share_send.at[number],
            recv_sem=share_recv.at[rank],
            device_id=device(number),
            device_id_type=pl.DeviceIdType.MESH,
        )

    def share_arrival(number):
        return pltpu.make_async_remote_copy(
            src_ref=share_ref.at[number],
            dst_ref=shares_in.at[number],
            send_sem=share_send.at[number],
            recv_sem=share_recv.at[number],
            device_id=core,
            device_id_type=pl.DeviceIdType.MESH,
        )

    def dots_copy(number):
        return pltpu.make_async_remote_copy(
            src_ref=dots_own.at[number],
            dst_ref=dots_ref.at[rank],
            send_sem=dots_send.at[number],
            recv_sem=dots_recv.at[rank],
            device_id=device(number),
            device_id_type=pl.DeviceIdType.MESH,
        )

    def dots_arrival(number):
        return pltpu.make_async_remote_copy(
            src_ref=dots_own.at[number],
            dst_ref=dots_ref.at[number],
            send_sem=dots_send.at[number],
            recv_sem=dots_recv.at[number],
            device_id=core,
            device_id_type=pl.DeviceIdType.MESH,
        )

    def for_others(action):
        @pl.loop(1, devices)
        def _(j):
            action(lax.rem(rank + j, devices))

    for_others(lambda number: share_copy(number).start())
    shares_in[rank] = share_ref[rank]

    def at(owner, gg, h):
        return pl.ds(pl.multiple_of((owner * span + gg) * block + h * rows, rows), rows)

    def copy(k, slot, owner, gg, h, peer, own=False):
        return pltpu.make_async_remote_copy(
            src_ref=own_ref.at[h] if own else all_ref.at[at(owner, gg, h)],
            dst_ref=all_ref.at[at(owner, gg, h)],
            send_sem=send_sem.at[k, slot],
            recv_sem=recv_sem.at[owner * span + gg, h],
            device_id=peer,
            device_id_type=pl.DeviceIdType.MESH,
        )

    sends = []

    def send(ok, *where, **options):
        k = where[0]
        slot = sum(1 for entry in sends if entry[2] == k)
        make = partial(copy, k, slot, *where[1:], **options)
        sends.append((ok, make, k))
        run_if(ok, lambda: make().start())

    def arrive(owner, gg, h):
        copy(0, 0, owner, gg, h, core).wait_recv()

    locals_ = [
        pltpu.make_async_copy(own_ref.at[h], all_ref.at[at(z, g, h)], local_sem.at[h])
        for h in range(2)
    ]

    def first(k):
        owner = order[k]
        own = k == 0
        if own:
            for item in locals_:
                item.start()
        else:
            arrive(owner, g, 0)
            arrive(owner, g, 1)
        go_up, go_down = onward[k]
        for h in range(2):
            send(go_up, k, owner, g, h, above, own=own)
            send(go_down, k, owner, g, h, below, own=own)
        send(True, k, owner, g, 0, x_peer, own=own)
        send(True, k, owner, g, 1, y_peer, own=own)
        send(True, k, owner, g, 1, x_peer, own=own)
        send(True, k, owner, g, 0, y_peer, own=own)
        send(True, k, owner, g, 0, core, own=own)
        send(True, k, owner, g, 1, core, own=own)

    def second(k):
        owner = order[k]
        arrive(owner, flip_x, 0)
        send(True, k, owner, flip_x, 0, y_peer)
        send(True, k, owner, flip_x, 0, core)
        arrive(owner, flip_y, 1)
        send(True, k, owner, flip_y, 1, x_peer)
        send(True, k, owner, flip_y, 1, core)

    def third(k):
        owner = order[k]
        for gg, h in ((flip_y, 0), (flip_x, 1), (flip_both, 0), (flip_both, 1)):
            arrive(owner, gg, h)
            send(True, k, owner, gg, h, core)

    def complete(k):
        for gg in (g, flip_x, flip_y, flip_both):
            for h in range(2):
                arrive(order[k], flip(gg), h)
        if k == 0:
            for item in locals_:
                item.wait()

    def owner_of(s):
        if isinstance(s, int):
            return order[s // 2]
        k = lax.div(s, 2)
        return sum((k == j).astype(jnp.int32) * order[j] for j in range(n_z))

    def place(s):
        k, side = (s // 2, s % 2) if isinstance(s, int) else (lax.div(s, 2), lax.rem(s, 2))
        if isinstance(s, int):
            owner = order[k]
        else:
            owner = sum((k == j).astype(jnp.int32) * order[j] for j in range(n_z))
        return pl.ds(pl.multiple_of(owner * (span * block) + side * step_rows, step_rows), step_rows)

    def parity(s):
        return s % 2 if isinstance(s, int) else lax.rem(s, 2)

    def fetches(s):
        slot = parity(s)
        return [
            pltpu.make_async_copy(source.at[place(s)], target.at[slot], fetch_sem.at[j, slot])
            for j, (source, target) in enumerate(
                ((all_ref, moe_buf), (cot_ref, cot_buf))
            )
        ]

    def stores(s):
        slot = parity(s)
        return [
            pltpu.make_async_copy(
                pair_stage.at[slot], pair_ref.at[place(s)], store_sem.at[0, slot]
            )
        ]

    f32 = jnp.float32
    dot = partial(lax.dot_general, preferred_element_type=f32)
    plain = (((1,), (0,)), ((), ()))
    last_dims = (((1,), (1,)), ((), ()))
    first_dims = (((0,), (0,)), ((), ()))
    half_width = scaled.shape[1]
    width = moe_buf.shape[2]
    tile = 256

    quads = (flip_both, flip_x, flip_y, g)

    def remote(src, dst, ssem, rsem, peer):
        return pltpu.make_async_remote_copy(
            src_ref=src,
            dst_ref=dst,
            send_sem=ssem,
            recv_sem=rsem,
            device_id=peer,
            device_id_type=pl.DeviceIdType.MESH,
        )

    def core_copy(k, q):
        return remote(
            held.at[k, flip(quads[q])],
            from_core.at[k, q],
            core_send.at[k, q],
            core_recv.at[k, q],
            core,
        )

    a_plan = ((0, 0, 0, x_peer), (0, 1, 0, y_peer), (1, 0, 1, x_peer), (2, 1, 1, y_peer))

    def a_copy(k, j):
        q, h, slot, peer = a_plan[j]
        return remote(
            held.at[k, quads[q], h],
            from_a.at[k, h, slot],
            a_send.at[k, j],
            a_recv.at[k, h, slot],
            peer,
        )

    b_plan = ((2, y_peer), (1, x_peer))

    def b_copy(k, h):
        q, peer = b_plan[h]
        return remote(
            held.at[k, quads[q], h], from_b.at[k, h], b_send.at[k, h], b_recv.at[k, h], peer
        )

    def z_copy(k):
        return remote(
            held.at[k, g], from_z.at[z], z_send.at[k], z_recv.at[z], {"gx": order[k], "gy": g}
        )

    def stage_core(k):
        for q in range(4):
            core_copy(k, q).start()

    def stage_a(k):
        for q in range(4):
            core_copy(k, q).wait_recv()
            for h in range(2):
                mine = held.at[k, quads[q], h]
                add_into(mine, (mine, from_core.at[k, q, h]), rows)
            for j in range(4):
                if a_plan[j][0] == q:
                    a_copy(k, j).start()

    def stage_b(k):
        for q, h, slot in ((2, 0, 0), (1, 1, 0), (3, 0, 1), (3, 1, 1)):
            mine, arrived = held.at[k, quads[q], h], from_a.at[k, h, slot]
            remote(mine, arrived, a_send.at[k, 0], a_recv.at[k, h, slot], core).wait_recv()
            add_into(mine, (mine, arrived), rows)
            if slot == 0:
                b_copy(k, h).start()

    def stage_c(k):
        for h in range(2):
            b_copy(k, h).wait_recv()
            mine = held.at[k, g, h]
            add_into(mine, (mine, from_b.at[k, h]), rows)
        if k > 0:
            z_copy(k).start()

    backs = (
        (stage_core, lambda k: 2 * k + 1, 2),
        (stage_a, lambda k: 2 * k + 1, 4),
        (stage_b, lambda k: 2 * k + 2, 4),
        (stage_c, lambda k: 2 * k + 3, 4),
    )

    def events(s, phase):
        for action, start, when in backs:
            for k in range(n_z):
                if when == phase and start(k) < steps:
                    pl.when(s == start(k))(partial(action, k))
        for k in range(1, n_z):
            if k >= 2 and phase == 1:
                pl.when(s == k - 2)(partial(first, k))
            if phase == 2:
                pl.when(s == 2 * (k - 1))(partial(second, k))
            if phase == 2:
                pl.when(s == 2 * (k - 1) + 1)(partial(third, k))
            if phase == 4:
                pl.when(s == 2 * k - 1)(partial(complete, k))

    first(0)

    @pl.loop(0, width // tile)
    def _(t):
        cols = pl.ds(pl.multiple_of(t * tile, tile), tile)
        down_t[cols, :] = down_ref[:, cols].T

    second(0)
    if n_z > 1:
        first(1)
    third(0)
    complete(0)
    for item in fetches(0):
        item.start()
    for_others(lambda number: share_arrival(number).wait_recv())

    @pl.loop(0, steps)
    def _(s):
        slot = lax.rem(s, 2)
        moe, cot, share = moe_buf.at[slot], cot_buf.at[slot], share_buf
        first_device = owner_of(s) * span + slot * (span // 2)
        for item in fetches(s):
            item.wait()

        @pl.when(s >= 2)
        def _():
            for item in stores(s - 2):
                item.wait()

        for j in range(span // 2):
            column = jnp.broadcast_to(shares_in[first_device + j], (block, block)).T
            share[j * block : (j + 1) * block, :] = column
        wide = jnp.concatenate([share[...]] * (tile // share.shape[1]), axis=1)

        @pl.loop(0, half_width // tile)
        def _(t):
            cols = pl.ds(pl.multiple_of(t * tile, tile), tile)
            gated = dot(moe[...], gate_ref[:, cols], plain)
            lifted = dot(moe[...], up_ref[:, cols], plain)
            gate_val[:, cols] = gated
            up_val[:, cols] = lifted
            scaled[:, cols] = (gated * jax.nn.sigmoid(gated) * lifted * wide).astype(jnp.bfloat16)

        events(s, 1)
        scaled_t[...] = scaled[...].T

        @pl.loop(0, width // (2 * tile))
        def _(t):
            cols = pl.ds(pl.multiple_of(t * 2 * tile, 2 * tile), 2 * tile)
            sent = dot(scaled[...], down_ref[:, cols], plain).astype(jnp.bfloat16)
            held[lax.div(s, 2), pl.ds(slot * (span // 2), span // 2), :, :, cols] = sent.reshape(
                (span // 2, 2, rows, 2 * tile)
            )

        events(s, 2)
        dots_buf[...] = jnp.zeros(dots_buf.shape, f32)

        @pl.loop(0, half_width // tile)
        def _(t):
            cols = pl.ds(pl.multiple_of(t * tile, tile), tile)
            pulled = dot(cot[...], down_t[:, cols], plain)
            gated = gate_val[:, cols]
            lifted = up_val[:, cols]
            sig = jax.nn.sigmoid(gated)
            silu = gated * sig
            product = pulled * (silu * lifted)
            lanes = share.shape[1]
            dots_buf[...] = dots_buf[...] + sum(
                product[:, j * lanes : (j + 1) * lanes] for j in range(tile // lanes)
            )
            pulled = pulled * wide
            pair_stage[slot, :, cols] = (pulled * lifted * sig * (1.0 + gated * (1.0 - sig))).astype(
                jnp.bfloat16
            )
            more = pl.ds(pl.multiple_of(half_width + t * tile, tile), tile)
            pair_stage[slot, :, more] = (pulled * silu).astype(jnp.bfloat16)

        for item in stores(s):
            item.start()
        for j in range(span // 2):
            number = first_device + j
            rows_of = dots_buf[j * block : (j + 1) * block, :]
            dots_own[number] = jnp.sum(rows_of.T, axis=0, keepdims=True)

        for j in range(span // 2):
            number = first_device + j

            @pl.when(number != rank)
            def _():
                dots_copy(number).start()

        events(s, 3)
        events(s, 4)

        @pl.when(s < steps - 1)
        def _():
            for item in fetches(s + 1):
                item.start()

        @pl.loop(0, width // (2 * tile))
        def _(t):
            cols = pl.ds(pl.multiple_of(t * 2 * tile, 2 * tile), 2 * tile)
            grown = dot(scaled_t[...], cot[:, cols], plain)
            down_out[:, cols] = jnp.where(s == 0, 0.0, down_out[:, cols]) + grown

    for t in range(steps, 2 * steps):
        for action, start, _ in backs[::-1]:
            for k in range(n_z):
                if start(k) == t:
                    action(k)
    for s in (steps - 2, steps - 1):
        for item in stores(s):
            item.wait()
    for k in range(1, n_z):
        arrived = from_z.at[order[k]]
        remote(held.at[k, g], arrived, z_send.at[k], z_recv.at[order[k]], core).wait_recv()
    for h in range(2):
        terms = [held.at[0, g, h]] + [from_z.at[order[k], h] for k in range(1, n_z)]
        add_into(out_ref.at[h], terms, rows)
    for k in range(n_z):
        for q in range(4):
            core_copy(k, q).wait_send()
        for j in range(4):
            a_copy(k, j).wait_send()
        for h in range(2):
            b_copy(k, h).wait_send()
        if k > 0:
            z_copy(k).wait_send()
    for ok, make, k in sends:
        run_if(ok, lambda make=make: make().wait_send())
    dots_ref[rank] = dots_own[rank]
    for_others(lambda number: dots_arrival(number).wait_recv())
    for_others(lambda number: share_copy(number).wait_send())
    for_others(lambda number: dots_copy(number).wait_send())


def run_experts(moe_in, all_cot, shares, gate_w, up_w, down_w, collective_id):
    n_z = lax.axis_size("gx")
    span = lax.axis_size("gy")
    rows, width = moe_in.shape
    half = down_w.shape[0]
    total = n_z * span * rows
    step = span * rows // 2
    lanes = 128
    devices = n_z * span
    bf16, f32 = jnp.bfloat16, jnp.float32
    dma = pltpu.SemaphoreType.DMA
    vmem = pl.BlockSpec(memory_space=pltpu.VMEM)
    hbm = pl.BlockSpec(memory_space=pl.ANY)
    return pl.pallas_call(
        partial(expert_kernel, n_z, span),
        out_shape=(
            jax.ShapeDtypeStruct((total, width), bf16),
            jax.ShapeDtypeStruct((total, 2 * half), bf16),
            jax.ShapeDtypeStruct((devices, 1, rows), f32),
            jax.ShapeDtypeStruct((half, width), f32),
            jax.ShapeDtypeStruct((2, rows // 2, width), f32),
        ),
        in_specs=[vmem, hbm, vmem, vmem, vmem, vmem],
        out_specs=(hbm, hbm, vmem, vmem, vmem),
        scratch_shapes=[
            pltpu.VMEM((2, step, width), bf16),
            pltpu.VMEM((2, step, width), bf16),
            pltpu.VMEM((step, lanes), f32),
            pltpu.VMEM((2, step, 2 * half), bf16),
            pltpu.VMEM((step, lanes), f32),
            pltpu.VMEM((step, half), f32),
            pltpu.VMEM((step, half), f32),
            pltpu.VMEM((step, half), bf16),
            pltpu.VMEM((half, step), bf16),
            pltpu.VMEM((width, half), bf16),
            pltpu.VMEM((n_z, span, 2, rows // 2, width), bf16),
            pltpu.VMEM((n_z, 4, 2, rows // 2, width), bf16),
            pltpu.VMEM((n_z, 2, 2, rows // 2, width), bf16),
            pltpu.VMEM((n_z, 2, rows // 2, width), bf16),
            pltpu.VMEM((n_z, 2, rows // 2, width), bf16),
            dma((n_z, 18)),
            dma((n_z * span, 2)),
            dma((2,)),
            dma((3, 2)),
            dma((2, 2)),
            dma((n_z, 4)),
            dma((n_z, 4)),
            dma((n_z, 2)),
            dma((n_z,)),
            dma((n_z, 4)),
            dma((n_z, 2, 2)),
            dma((n_z, 2)),
            dma((n_z,)),
            pltpu.VMEM((devices, 1, rows), f32),
            pltpu.VMEM((devices, 1, rows), f32),
            dma((devices,)),
            dma((devices,)),
            dma((devices,)),
            dma((devices,)),
        ],
        compiler_params=pltpu.CompilerParams(
            collective_id=collective_id, has_side_effects=True, vmem_limit_bytes=67043328
        ),
        name="experts",
    )(moe_in.reshape(2, rows // 2, width), all_cot, shares, gate_w, up_w, down_w)


def pull_kernel(n_i, rows, all_ref, pair_ref, gate_ref, up_ref, out_ref, gate_out, up_out,
                held, from_core, from_a, from_b, from_z, moe_buf, pair_buf,
                fetch_sem, core_send, a_send, b_send, z_send, core_recv, a_recv, b_recv, z_recv):
    z = lax.axis_index("gx")
    g = lax.axis_index("gy")
    flip_x = g + 2 - 4 * ((g // 2) % 2)
    flip_y = g + 4 - 8 * ((g // 4) % 2)
    quads = (flip_x + flip_y - g, flip_x, flip_y, g)
    core = {"gx": z, "gy": flip(g)}
    x_peer = {"gx": z, "gy": flip_x}
    y_peer = {"gx": z, "gy": flip_y}
    along = [{"gx": lax.rem(z + j, n_i), "gy": g} for j in range(1, n_i)]
    barrier_with([(z >= 0, peer) for peer in (core, x_peer, y_peer, *along)])
    item_rows = moe_buf.shape[1]
    width = moe_buf.shape[2]
    half_width = gate_out.shape[1]
    owners = [lax.rem(z + n_i - 1 - i + n_i, n_i) for i in range(n_i)]

    def remote(src, dst, ssem, rsem, peer):
        return pltpu.make_async_remote_copy(
            src_ref=src,
            dst_ref=dst,
            send_sem=ssem,
            recv_sem=rsem,
            device_id=peer,
            device_id_type=pl.DeviceIdType.MESH,
        )

    def fetches(i):
        place = pl.ds(pl.multiple_of(owners[i] * item_rows, item_rows), item_rows)
        return [
            pltpu.make_async_copy(all_ref.at[place], moe_buf.at[i % 2], fetch_sem.at[0, i % 2]),
            pltpu.make_async_copy(pair_ref.at[place], pair_buf.at[i % 2], fetch_sem.at[1, i % 2]),
        ]

    def core_copy(i, q):
        return remote(
            held.at[i, flip(quads[q])],
            from_core.at[i, q],
            core_send.at[i, q],
            core_recv.at[i, q],
            core,
        )

    a_plan = ((0, 0, 0, x_peer), (0, 1, 0, y_peer), (1, 0, 1, x_peer), (2, 1, 1, y_peer))

    def a_copy(i, k):
        q, h, slot, peer = a_plan[k]
        return remote(
            held.at[i, quads[q], h],
            from_a.at[i, h, slot],
            a_send.at[i, k],
            a_recv.at[i, h, slot],
            peer,
        )

    b_plan = ((2, y_peer), (1, x_peer))

    def b_copy(i, h):
        q, peer = b_plan[h]
        return remote(
            held.at[i, quads[q], h], from_b.at[i, h], b_send.at[i, h], b_recv.at[i, h], peer
        )

    def z_copy(i):
        return remote(
            held.at[i, g], from_z.at[z], z_send.at[i], z_recv.at[z], {"gx": owners[i], "gy": g}
        )

    dot = partial(lax.dot_general, preferred_element_type=jnp.float32)
    last_dims = (((1,), (1,)), ((), ()))
    first_dims = (((0,), (0,)), ((), ()))

    def multiply(i):
        for copy in fetches(i):
            copy.wait()
        pair = pair_buf.at[i % 2]
        tile = 256

        @pl.loop(0, width // tile)
        def _(t):
            cols = pl.ds(pl.multiple_of(t * tile, tile), tile)
            total = dot(pair[:, :half_width], gate_ref[cols, :], last_dims)
            total = total + dot(pair[:, half_width:], up_ref[cols, :], last_dims)
            held[i, :, :, :, cols] = total.astype(jnp.bfloat16).reshape(held.shape[1:4] + (tile,))

        for q in range(4):
            core_copy(i, q).start()

    def accumulate(i):
        moe, pair = moe_buf.at[i % 2], pair_buf.at[i % 2]
        tile = 512

        @pl.loop(0, width // tile)
        def _(t):
            cols = pl.ds(pl.multiple_of(t * tile, tile), tile)
            grown = dot(moe[:, cols], pair[...], first_dims)
            if i == 0:
                gate_out[cols, :] = grown[:, :half_width]
                up_out[cols, :] = grown[:, half_width:]
            else:
                gate_out[cols, :] = gate_out[cols, :] + grown[:, :half_width]
                up_out[cols, :] = up_out[cols, :] + grown[:, half_width:]

        if i + 2 < n_i:
            for copy in fetches(i + 2):
                copy.start()

    def stage_a(i):
        for q in range(4):
            core_copy(i, q).wait_recv()
            for h in range(2):
                mine = held.at[i, quads[q], h]
                add_into(mine, (mine, from_core.at[i, q, h]), rows)
            for k in range(4):
                if a_plan[k][0] == q:
                    a_copy(i, k).start()

    def stage_b(i):
        for q, h, slot in ((2, 0, 0), (1, 1, 0), (3, 0, 1), (3, 1, 1)):
            mine, arrived = held.at[i, quads[q], h], from_a.at[i, h, slot]
            remote(mine, arrived, a_send.at[i, 0], a_recv.at[i, h, slot], core).wait_recv()
            add_into(mine, (mine, arrived), rows)
            if slot == 0:
                b_copy(i, h).start()

    def stage_c(i):
        for h in range(2):
            b_copy(i, h).wait_recv()
            mine = held.at[i, g, h]
            add_into(mine, (mine, from_b.at[i, h]), rows)
        if i < n_i - 1:
            z_copy(i).start()
        else:
            for j in range(n_i - 1):
                arrived = from_z.at[owners[j]]
                remote(held.at[j, g], arrived, z_send.at[j], z_recv.at[owners[j]], core).wait_recv()
            for h in range(2):
                terms = [held.at[i, g, h]] + [from_z.at[owners[j], h] for j in range(n_i - 1)]
                add_into(out_ref.at[h], terms, rows)

    for i in range(min(2, n_i)):
        for copy in fetches(i):
            copy.start()
    for t in range(n_i + 3):
        if t < n_i:
            multiply(t)
        if 0 <= t - 1 < n_i:
            stage_a(t - 1)
        if 0 <= t - 2 < n_i:
            stage_c(t - 2)
        if 0 <= t - 1 < n_i:
            accumulate(t - 1)
            stage_b(t - 1)
    for i in range(n_i):
        for q in range(4):
            core_copy(i, q).wait_send()
        for k in range(4):
            a_copy(i, k).wait_send()
        for h in range(2):
            b_copy(i, h).wait_send()
        if i < n_i - 1:
            z_copy(i).wait_send()


def pull_experts(all_moe, pair, gate_w, up_w, collective_id):
    n_i = lax.axis_size("gx")
    span = lax.axis_size("gy")
    total, width = all_moe.shape
    half_width = gate_w.shape[1]
    rows = total // (n_i * span) // 2
    half = (rows, width)
    bf16 = jnp.bfloat16
    dma = pltpu.SemaphoreType.DMA
    vmem = pl.BlockSpec(memory_space=pltpu.VMEM)
    hbm = pl.BlockSpec(memory_space=pl.ANY)
    out, gate_part, up_part = pl.pallas_call(
        partial(pull_kernel, n_i, rows),
        out_shape=(
            jax.ShapeDtypeStruct((2,) + half, jnp.float32),
            jax.ShapeDtypeStruct((width, half_width), jnp.float32),
            jax.ShapeDtypeStruct((width, half_width), jnp.float32),
        ),
        in_specs=[hbm, hbm, vmem, vmem],
        out_specs=(vmem, vmem, vmem),
        scratch_shapes=[
            pltpu.VMEM((n_i, span, 2) + half, bf16),
            pltpu.VMEM((n_i, 4, 2) + half, bf16),
            pltpu.VMEM((n_i, 2, 2) + half, bf16),
            pltpu.VMEM((n_i, 2) + half, bf16),
            pltpu.VMEM((n_i, 2) + half, bf16),
            pltpu.VMEM((2, span * 2 * rows, width), bf16),
            pltpu.VMEM((2, span * 2 * rows, 2 * half_width), bf16),
            dma((2, 2)),
            dma((n_i, 4)),
            dma((n_i, 4)),
            dma((n_i, 2)),
            dma((n_i,)),
            dma((n_i, 4)),
            dma((n_i, 2, 2)),
            dma((n_i, 2)),
            dma((n_i,)),
        ],
        compiler_params=pltpu.CompilerParams(
            collective_id=collective_id, has_side_effects=True, vmem_limit_bytes=67043328
        ),
        name="pull_experts",
    )(all_moe, pair, gate_w, up_w)
    return out.reshape(2 * rows, width), gate_part, up_part


def turn(values, cosine, sine):
    return values * cosine + pltpu.roll(values, values.shape[-1] // 2, 1) * sine


def spread_docs(docs_ref, row_docs, col_docs):
    lanes = docs_ref.shape[1]
    for j in range(docs_ref.shape[0]):
        line = docs_ref[j : j + 1, :].astype(jnp.float32)
        row_docs[j * lanes : (j + 1) * lanes, :] = jnp.broadcast_to(line, (lanes, lanes)).T
        col_docs[:, j * lanes : (j + 1) * lanes] = jnp.broadcast_to(line, (8, lanes))


def attend_kernel(
    heads,
    pieces,
    own_acts,
    query_weight,
    key_weight,
    value_weight,
    own_out_weight,
    own_cot,
    query_gain,
    key_gain,
    cosine_ref,
    sine_ref,
    docs_ref,
    attended_ref,
    acts_out,
    weight_out,
    full_out,
    all_cot,
    query_raw,
    key_raw,
    ready_ref,
    mixed_ref,
    totals_ref,
    peaks_ref,
    own_weight,
    row_docs,
    col_docs,
    part_ref,
    held,
    from_core,
    from_a,
    from_b,
    from_z,
    near_send,
    near_recv,
    near_local,
    far_send,
    far_recv,
    far_local,
    in_send,
    in_recv,
    in_local,
    out_send,
    out_recv,
    out_local,
    load_sem,
    core_send,
    a_send,
    b_send,
    z_send,
    core_recv,
    a_recv,
    b_recv,
    z_recv,
):
    n_z = lax.axis_size("gx")
    span = lax.axis_size("gy")
    for j, item in enumerate((query_weight, key_weight, value_weight)):
        own_weight[:, j * item.shape[1] : (j + 1) * item.shape[1]] = item[...]
    greet(n_z)
    in_start, in_relays, in_finish = chain_gather(
        n_z, own_weight, weight_out, in_send, in_recv, in_local
    )
    out_start, out_relays, out_finish = chain_gather(
        n_z, own_out_weight, full_out, out_send, out_recv, out_local
    )
    near, near_finish = gather_steps(1, span, own_acts, acts_out, near_send, near_recv, near_local)
    far, far_finish = gather_steps(n_z, span, own_cot, all_cot, far_send, far_recv, far_local)
    back = []
    scatter_kernel(
        False,
        pieces,
        part_ref.shape[3],
        part_ref,
        attended_ref,
        held,
        from_core,
        from_a,
        from_b,
        from_z,
        load_sem,
        core_send,
        a_send,
        b_send,
        z_send,
        core_recv,
        a_recv,
        b_recv,
        z_recv,
        parts=back,
    )
    f32, bf16 = jnp.float32, jnp.bfloat16
    dot = partial(lax.dot_general, preferred_element_type=f32)
    plain = (((1,), (0,)), ((), ()))
    last_dims = (((1,), (1,)), ((), ()))
    length = query_raw.shape[0]
    width = acts_out.shape[3]
    local = heads * HD
    block = 256
    scale = HD ** (-0.5)

    in_start()
    near[0]()
    far[0]()
    spread_docs(docs_ref, row_docs, col_docs)
    near[1]()
    near[2]()
    later = far[1:]
    for relay in in_relays:
        relay()
        for step in later[:1]:
            step()
        later = later[1:]
    out_start()
    in_finish()
    near_finish()
    waiting = [list(out_relays), list(later)]

    def pull(which):
        if waiting[which]:
            waiting[which].pop(0)()

    def project(source):
        cols = slice(source * local, (source + 1) * local)
        acts = acts_out[...].reshape(length, width)
        total = jnp.zeros((length, local), f32)
        depth = own_weight.shape[0]
        for owner in range(n_z):
            total = total + dot(
                acts[:, owner * depth : (owner + 1) * depth], weight_out[owner, :, cols], plain
            )
        return total

    for source, raw, gain in ((0, query_raw, query_gain), (1, key_raw, key_gain)):
        raw[...] = project(source)
        for h in range(heads):
            cols = slice(h * HD, (h + 1) * HD)

            @pl.loop(0, length // block)
            def _(t):
                at = pl.ds(pl.multiple_of(t * block, block), block)
                value = raw[at, cols]
                normed = value * lax.rsqrt(jnp.mean(value * value, axis=-1, keepdims=True) + EPSILON)
                turned = turn(normed * gain[...], cosine_ref[at, :], sine_ref[at, :])
                where = source * local + h * HD
                ready_ref[at, where : where + HD] = turned.astype(bf16)

        pull(source)

    ready_ref[:, 2 * local :] = project(2).astype(bf16)
    pull(0)
    lanes = lax.broadcasted_iota(jnp.int32, (block, HD), 1)
    peaks_ref[...] = jnp.full(peaks_ref.shape, NEGATIVE, f32)

    def mix(t):
        at = pl.ds(pl.multiple_of(t * block, block), block)
        same = row_docs[at, :1] == col_docs[:1, :]
        kept = jnp.zeros((block, HD), f32)
        for h in range(heads):
            query = ready_ref[at, h * HD : (h + 1) * HD]
            key = ready_ref[:, local + h * HD : local + (h + 1) * HD]
            value = ready_ref[:, 2 * local + h * HD : 2 * local + (h + 1) * HD]
            scores = jnp.where(same, dot(query, key, last_dims) * scale, NEGATIVE)
            highest = jnp.max(scores, axis=-1, keepdims=True)
            weights = jnp.exp(scores - highest)
            total = jnp.sum(weights, axis=-1, keepdims=True)
            shares = (weights * (1.0 / total)).astype(bf16)
            mixed_ref[at, h * HD : (h + 1) * HD] = dot(shares, value, plain).astype(bf16)
            kept = jnp.where(lanes == h, highest + jnp.log(total), kept)
            top = jnp.max(highest, axis=0, keepdims=True)
            peaks_ref[h : h + 1, :] = jnp.maximum(peaks_ref[h : h + 1, :], top)
        totals_ref[at, :] = kept

    blocks = length // block
    between = waiting[1].pop(0) if waiting[1] else lambda: None

    @pl.loop(0, blocks)
    def _(t):
        mix(t)
        pl.when(t == blocks // 2 - 1)(between)

    pull(1)
    for relay in waiting[0]:
        relay()
    out_finish()
    rows = part_ref.shape[3]
    per_owner = own_out_weight.shape[1] // block

    @pl.loop(0, n_z * per_owner)
    def _(t):
        cols = pl.ds(pl.multiple_of(t * block, block), block)
        inside = pl.ds(pl.multiple_of(lax.rem(t, per_owner) * block, block), block)
        sent = dot(mixed_ref[...], full_out[lax.div(t, per_owner), :, inside], plain).astype(bf16)
        sent = sent.reshape(span, pieces, 2, rows, block)
        for p in range(pieces):
            part_ref[p, :, :, :, cols] = sent[:, p]

    for step in back[:-1]:
        step()
        pull(1)
    for step in waiting[1]:
        step()
    back[-1]()
    far_finish()


def attend(
    acts, weights, out_weight, cot, query_gain, key_gain, tables, docs, collective_id, pieces=4
):
    tokens, width = acts.shape
    depth, local = weights[0].shape
    heads = local // HD
    n_z = lax.axis_size("gx")
    span = lax.axis_size("gy")
    length = span * tokens
    rows = tokens // (pieces * 2)
    half = (2, tokens // 2, width)
    piece = (rows, width)
    f32, bf16 = jnp.float32, jnp.bfloat16
    dma = pltpu.SemaphoreType.DMA
    vmem = pl.BlockSpec(memory_space=pltpu.VMEM)
    hbm = pl.BlockSpec(memory_space=pl.ANY)
    attended, seq, full, full_out, all_cot, *saved, peaks = pl.pallas_call(
        partial(attend_kernel, heads, pieces),
        out_shape=(
            jax.ShapeDtypeStruct((pieces, 2) + piece, f32),
            jax.ShapeDtypeStruct((span,) + half, bf16),
            jax.ShapeDtypeStruct((n_z, depth, 3 * local), bf16),
            jax.ShapeDtypeStruct((n_z,) + out_weight.shape, bf16),
            jax.ShapeDtypeStruct((n_z * span,) + half, bf16),
            jax.ShapeDtypeStruct((length, local), f32),
            jax.ShapeDtypeStruct((length, local), f32),
            jax.ShapeDtypeStruct((length, 3 * local), bf16),
            jax.ShapeDtypeStruct((length, local), bf16),
            jax.ShapeDtypeStruct((length, HD), f32),
            jax.ShapeDtypeStruct((8, HD), f32),
        ),
        in_specs=[vmem] * 11,
        out_specs=(vmem, vmem, vmem, vmem, hbm) + (vmem,) * 6,
        scratch_shapes=[
            pltpu.VMEM((depth, 3 * local), bf16),
            pltpu.VMEM((length, 128), f32),
            pltpu.VMEM((8, length), f32),
            pltpu.VMEM((pieces, span, 2) + piece, bf16),
            pltpu.VMEM((pieces, 4, 2) + piece, bf16),
            pltpu.VMEM((pieces, 4, 2) + piece, bf16),
            pltpu.VMEM((pieces, 2, 2) + piece, bf16),
            pltpu.VMEM((pieces, 2) + piece, bf16),
            pltpu.VMEM((1, 2, 16, 128), bf16),
            dma((24,)),
            dma((span, 2)),
            dma,
            dma((24 * (2 * n_z - 1),)),
            dma((n_z * span, 2)),
            dma,
            dma((2 * n_z,)),
            dma((n_z,)),
            dma,
            dma((2 * n_z,)),
            dma((n_z,)),
            dma,
            dma((pieces, 4)),
            dma((pieces, 4)),
            dma((pieces, 4)),
            dma((pieces, 2)),
            dma((pieces,)),
            dma((pieces, 4)),
            dma((pieces, 2, 2)),
            dma((pieces, 2)),
            dma((pieces,)),
        ],
        compiler_params=pltpu.CompilerParams(
            collective_id=collective_id, has_side_effects=True, vmem_limit_bytes=60 << 20
        ),
        name="attend",
    )(
        acts.reshape(half),
        *weights,
        out_weight,
        cot.reshape(half),
        query_gain.reshape(1, HD),
        key_gain.reshape(1, HD),
        *tables,
        docs,
    )
    return (
        attended.reshape(tokens, width),
        seq.reshape(length, width),
        full.reshape(n_z * depth, 3 * local),
        all_cot.reshape(n_z * span * tokens, width),
        (*saved, full_out),
        peaks,
    )


def attend_back_kernel(
    heads,
    pieces,
    own_grad,
    out_weight_ref,
    mixed_ref,
    ready_ref,
    query_raw,
    key_raw,
    totals_ref,
    query_gain,
    key_gain,
    attn_gain,
    cosine_ref,
    sine_ref,
    docs_ref,
    small_ref,
    acts_hbm,
    weight_hbm,
    grad_acts,
    query_sum,
    key_sum_out,
    value_sum_out,
    out_sum,
    small_sum,
    late_sum,
    weight_sum,
    gain_ref,
    late_ref,
    row_docs,
    col_docs,
    seq_ref,
    part_ref,
    acts_ref,
    weight_ref,
    grad_mixed,
    grad_heads,
    one_head,
    turned,
    key_sum,
    value_sum,
    out_sums,
    out_low,
    out_high,
    in_sums,
    in_low,
    in_high,
    held,
    from_core,
    from_a,
    from_b,
    from_z,
    copy_sem,
    near_send,
    near_recv,
    near_local,
    out_send,
    out_low_recv,
    out_high_recv,
    in_send,
    in_low_recv,
    in_high_recv,
    load_sem,
    core_send,
    a_send,
    b_send,
    z_send,
    core_recv,
    a_recv,
    b_recv,
    z_recv,
    *small_scratch,
):
    n_z = lax.axis_size("gx")
    span = lax.axis_size("gy")
    z = lax.axis_index("gx")
    g = lax.axis_index("gy")
    peers = [{"gx": z, "gy": g + bit - 2 * bit * ((g // bit) % 2)} for bit in (1, 2, 4)]
    peers += [{"gx": lax.rem(z + j, n_z), "gy": g} for j in range(1, n_z)]
    barrier_with([(z >= 0, peer) for peer in peers])
    out_start, out_relays, out_finish = chain_scatter(
        n_z, out_sums, out_sum, out_low, out_high, out_send, out_low_recv, out_high_recv
    )
    chains = [
        chain_scatter(
            n_z,
            in_sums.at[h],
            weight_sum.at[h],
            in_low.at[h],
            in_high.at[h],
            in_send.at[h],
            in_low_recv.at[h],
            in_high_recv.at[h],
        )
        for h in range(heads)
    ]
    near, near_finish = gather_steps(1, span, own_grad, seq_ref, near_send, near_recv, near_local)
    bits = span.bit_length() - 1
    half_scratch = len(small_scratch) // 2
    small = sum_steps(n_z, bits, small_ref, small_sum, *small_scratch[:half_scratch])
    late = sum_steps(n_z, bits, late_ref, late_sum, *small_scratch[half_scratch:])
    back = []
    scatter_kernel(
        False,
        pieces,
        part_ref.shape[3],
        part_ref,
        grad_acts,
        held,
        from_core,
        from_a,
        from_b,
        from_z,
        load_sem,
        core_send,
        a_send,
        b_send,
        z_send,
        core_recv,
        a_recv,
        b_recv,
        z_recv,
        parts=back,
    )
    f32, bf16 = jnp.float32, jnp.bfloat16
    dot = partial(lax.dot_general, preferred_element_type=f32)
    plain = (((1,), (0,)), ((), ()))
    last_dims = (((1,), (1,)), ((), ()))
    first_dims = (((0,), (0,)), ((), ()))
    length, local = query_raw.shape
    width = acts_ref.shape[1]
    rows = part_ref.shape[3]
    block = 256
    scale = HD ** (-0.5)
    copies = [
        pltpu.make_async_copy(acts_hbm, acts_ref, copy_sem.at[0]),
        pltpu.make_async_copy(weight_hbm, weight_ref, copy_sem.at[1]),
    ]
    near[0]()
    small[0]()
    spread_docs(docs_ref, row_docs, col_docs)
    for copy in copies:
        copy.start()
    near[1]()
    small[1]()
    near[2]()
    small[2]()
    near_finish()
    owned = width // n_z

    @pl.loop(0, width // block)
    def _(t):
        cols = pl.ds(pl.multiple_of(t * block, block), block)
        inside = pl.ds(pl.multiple_of(lax.rem(t, owned // block) * block, block), block)
        grad = seq_ref[:, :, :, cols].reshape(length, block)
        out_sums[lax.div(t, owned // block), inside, :] = dot(
            grad, mixed_ref[...], first_dims
        ).astype(bf16)

    out_start()
    total = jnp.zeros((length, local), f32)
    for owner in range(n_z):
        cols = slice(owner * owned, (owner + 1) * owned)
        grad = seq_ref[:, :, :, cols].reshape(length, owned)
        total = total + dot(grad, out_weight_ref[owner], last_dims)
    grad_mixed[...] = total.astype(bf16)
    small[3]()
    gain_ref[...] = jnp.zeros_like(gain_ref)
    late_ref[...] = jnp.zeros_like(late_ref)
    for h in range(heads):
        cols = slice(h * HD, (h + 1) * HD)
        key = ready_ref[:, local + h * HD : local + (h + 1) * HD]
        value = ready_ref[:, 2 * local + h * HD : 2 * local + (h + 1) * HD]
        key_sum[...] = jnp.zeros_like(key_sum)
        value_sum[...] = jnp.zeros_like(value_sum)

        @pl.loop(0, length // block)
        def _(t):
            at = pl.ds(pl.multiple_of(t * block, block), block)
            same = row_docs[at, :1] == col_docs[:1, :]
            query = ready_ref[at, cols]
            grad = grad_mixed[at, cols]
            scores = jnp.where(same, dot(query, key, last_dims) * scale, NEGATIVE)
            weights = jnp.exp(scores - totals_ref[at, h : h + 1])
            value_sum[...] += dot(weights.astype(bf16), grad, first_dims)
            pulled = dot(grad, value, last_dims)
            inner = jnp.sum(weights * pulled, axis=-1, keepdims=True)
            grad_scores = (weights * (pulled - inner)).astype(bf16)
            turned[at, :] = dot(grad_scores, key, plain) * scale
            key_sum[...] += dot(grad_scores, query, first_dims)

        for source, raw, gain, incoming, factor in (
            (0, query_raw, query_gain, turned, 1.0),
            (1, key_raw, key_gain, key_sum, scale),
        ):

            @pl.loop(0, length // block)
            def _(t):
                at = pl.ds(pl.multiple_of(t * block, block), block)
                back = turn(incoming[at, :] * factor, cosine_ref[at, :], -sine_ref[at, :])
                item = raw[at, cols]
                inverse = lax.rsqrt(jnp.mean(item * item, axis=-1, keepdims=True) + EPSILON)
                normed = item * inverse
                gain_ref[source : source + 1, :] += jnp.sum(back * normed, axis=0, keepdims=True)
                inner = back * gain[...]
                pulled = inverse * (
                    inner - normed * jnp.mean(inner * normed, axis=-1, keepdims=True)
                )
                where = source * local + h * HD
                grad_heads[at, where : where + HD] = pulled.astype(bf16)
                one_head[at, source * HD : (source + 1) * HD] = pulled.astype(bf16)

        where = 2 * local + h * HD
        grad_heads[:, where : where + HD] = value_sum[...].astype(bf16)
        one_head[:, 2 * HD :] = value_sum[...].astype(bf16)
        if h == 0:
            for copy in copies:
                copy.wait()
            for relay in out_relays:
                relay()
            out_finish()
            small[4]()
        else:
            chains[h - 1][1][0]()

        @pl.loop(0, width // block)
        def _(t):
            cols = pl.ds(pl.multiple_of(t * block, block), block)
            inside = pl.ds(pl.multiple_of(lax.rem(t, owned // block) * block, block), block)
            in_sums[h, lax.div(t, owned // block), inside, :] = dot(
                acts_ref[:, cols], one_head[...], first_dims
            ).astype(bf16)

        chains[h][0]()

    for chain in chains[:-1]:
        for relay in chain[1][1:2]:
            relay()

    @pl.loop(0, width // block)
    def _(t):
        cols = pl.ds(pl.multiple_of(t * block, block), block)
        pulled = dot(grad_heads[...], weight_ref[cols, :], last_dims)
        gained = jnp.sum(pulled * acts_ref[:, cols].astype(f32), axis=0, keepdims=True)
        gained = gained / attn_gain[:, cols]
        for j in range(block // 128):
            late_ref[0, pl.ds(t * (block // 128) + j, 1), :] = gained[:, j * 128 : (j + 1) * 128]
        sent = pulled.astype(bf16).reshape(span, pieces, 2, rows, block)
        for p in range(pieces):
            part_ref[p, :, :, :, cols] = sent[:, p]

    late_ref[1, :8, :] = gain_ref[...]
    small[5]()
    waiting = [relay for chain in chains[:-1] for relay in chain[1][2:]] + list(chains[-1][1])
    for i, step in enumerate(back[:-1]):
        step()
        if i < len(late) - 2:
            late[i]()
        if i % 2 == 0 and waiting:
            waiting.pop(0)()
    for relay in waiting:
        relay()
    for chain in chains:
        chain[2]()
    for step in late[min(len(late) - 2, len(back) - 1) :]:
        step()
    for h in range(heads):
        for j, target in enumerate((query_sum, key_sum_out, value_sum_out)):
            target[:, h * HD : (h + 1) * HD] = weight_sum[h, :, j * HD : (j + 1) * HD]
    back[-1]()


def attend_back(
    grad,
    saved,
    query_gain,
    key_gain,
    attn_gain,
    tables,
    docs,
    acts,
    weights,
    small,
    collective_id,
    pieces=4,
):
    query_raw, key_raw, ready, mixed, totals, out_weight = saved
    n_z = lax.axis_size("gx")
    span = lax.axis_size("gy")
    bits = span.bit_length() - 1
    tokens, width = grad.shape
    length, local = query_raw.shape
    heads = local // HD
    rows = tokens // (pieces * 2)
    halves = folded(small)
    half = (2, tokens // 2, width)
    piece = (rows, width)
    out_block = (n_z, width // n_z, local)
    in_block = (heads, n_z, width // n_z, 3 * HD)
    f32, bf16 = jnp.float32, jnp.bfloat16
    dma = pltpu.SemaphoreType.DMA
    vmem = pl.BlockSpec(memory_space=pltpu.VMEM)
    hbm = pl.BlockSpec(memory_space=pl.ANY)
    late_shape = (2, -(-width // (128 * 8)) * 8, 128)
    grad_acts, *in_sums, out_sum, small_sum, late_sum = pl.pallas_call(
        partial(attend_back_kernel, heads, pieces),
        out_shape=(
            jax.ShapeDtypeStruct((pieces, 2) + piece, f32),
            jax.ShapeDtypeStruct((in_block[2], local), f32),
            jax.ShapeDtypeStruct((in_block[2], local), f32),
            jax.ShapeDtypeStruct((in_block[2], local), f32),
            jax.ShapeDtypeStruct(out_block[1:], f32),
            jax.ShapeDtypeStruct(halves.shape, f32),
            jax.ShapeDtypeStruct(late_shape, f32),
        ),
        in_specs=[vmem] * 14 + [hbm] * 2,
        out_specs=(vmem,) * 7,
        scratch_shapes=[
            pltpu.VMEM((heads,) + in_block[2:], f32),
            pltpu.VMEM((8, HD), f32),
            pltpu.VMEM(late_shape, f32),
            pltpu.VMEM((length, 128), f32),
            pltpu.VMEM((8, length), f32),
            pltpu.VMEM((span,) + half, bf16),
            pltpu.VMEM((pieces, span, 2) + piece, bf16),
            pltpu.VMEM((length, width), bf16),
            pltpu.VMEM((width, 3 * local), bf16),
            pltpu.VMEM((length, local), bf16),
            pltpu.VMEM((length, 3 * local), bf16),
            pltpu.VMEM((length, 3 * HD), bf16),
            pltpu.VMEM((length, HD), f32),
            pltpu.VMEM((length, HD), f32),
            pltpu.VMEM((length, HD), f32),
            pltpu.VMEM(out_block, bf16),
            pltpu.VMEM(out_block, bf16),
            pltpu.VMEM(out_block, bf16),
            pltpu.VMEM(in_block, bf16),
            pltpu.VMEM(in_block, bf16),
            pltpu.VMEM(in_block, bf16),
            pltpu.VMEM((pieces, 4, 2) + piece, bf16),
            pltpu.VMEM((pieces, 4, 2) + piece, bf16),
            pltpu.VMEM((pieces, 2, 2) + piece, bf16),
            pltpu.VMEM((pieces, 2) + piece, bf16),
            pltpu.VMEM((1, 2, 16, 128), bf16),
            dma((2,)),
            dma((24,)),
            dma((span, 2)),
            dma,
            dma((n_z,)),
            dma((n_z,)),
            dma((n_z,)),
            dma((heads, n_z)),
            dma((heads, n_z)),
            dma((heads, n_z)),
            dma((pieces, 4)),
            dma((pieces, 4)),
            dma((pieces, 4)),
            dma((pieces, 2)),
            dma((pieces,)),
            dma((pieces, 4)),
            dma((pieces, 2, 2)),
            dma((pieces, 2)),
            dma((pieces,)),
        ]
        + sum_scratch(n_z, bits, halves.shape[1])
        + sum_scratch(n_z, bits, late_shape[1]),
        compiler_params=pltpu.CompilerParams(
            collective_id=collective_id, has_side_effects=True, vmem_limit_bytes=67043328
        ),
        name="attend_back",
    )(
        grad.reshape(half),
        out_weight,
        mixed,
        ready,
        query_raw,
        key_raw,
        totals,
        query_gain.reshape(1, HD),
        key_gain.reshape(1, HD),
        attn_gain.reshape(1, width),
        *tables,
        docs,
        halves,
        acts,
        weights,
    )
    return (
        grad_acts.reshape(tokens, width),
        in_sums,
        out_sum,
        small_sum.reshape(-1)[: small.shape[0]],
        (late_sum[0].reshape(-1)[:width], late_sum[1, 0], late_sum[1, 1]),
    )


def flat(parts):
    return jnp.concatenate([part.reshape(-1) for part in parts])


def unflat(vector, parts):
    ends = accumulate(part.size for part in parts)
    return [vector[end - part.size : end].reshape(part.shape) for end, part in zip(ends, parts)]


def norm_rows(values, gain_row):
    return (
        values * lax.rsqrt(jnp.mean(values * values, axis=-1, keepdims=True) + EPSILON) * gain_row
    )


def rotary(values):
    length = values.shape[0]
    halfway = values.shape[-1] // 2
    positions = jnp.arange(length, dtype=jnp.float32)
    frequency = jnp.exp(
        jnp.arange(halfway, dtype=jnp.float32) * (-2.0 * jnp.log(10000.0) / values.shape[-1])
    )
    angles = (positions[:, None] * frequency[None, :])[:, None, :]
    cosine = jnp.cos(angles)
    sine_table = jnp.sin(angles)
    first_half = values[..., :halfway]
    second = values[..., halfway:]
    return jnp.concatenate(
        [first_half * cosine - second * sine_table, second * cosine + first_half * sine_table],
        axis=-1,
    )


def prepare_heads(raw_heads, gain_row):
    return rotary(norm_rows(raw_heads, gain_row))


def route_gates(id_table, logits):
    shares = jax.nn.softmax(logits, axis=-1)
    experts = logits.shape[-1]
    matches = id_table[:, :, None] == jnp.arange(experts, dtype=jnp.int32)[None, None, :]
    chosen = jnp.sum(jnp.where(matches, shares[:, None, :], 0.0), axis=-1)
    return chosen / jnp.sum(chosen, axis=-1, keepdims=True)


def contract_rows(left_side, right_side):
    return lax.dot_general(
        left_side, right_side, (((0,), (0,)), ((), ())), preferred_element_type=jnp.float32
    )


def contract_cols(left_side, right_side):
    return lax.dot_general(
        left_side, right_side, (((1,), (1,)), ((), ())), preferred_element_type=jnp.float32
    )


def routed_experts(
    moe_in, cotangent, expert_ids, gate_share, router_weight, gate_weight, up_weight, down_weight
):
    tok_rows = moe_in.shape[0]
    experts = router_weight.shape[1]
    width_all = moe_in.shape[1]
    capacity = tok_rows * TOP * 3 // (2 * experts)
    route_count = tok_rows * TOP
    flat_ids = expert_ids.reshape(route_count)
    onehot = (flat_ids[:, None] == jnp.arange(experts, dtype=jnp.int32)[None, :]).astype(jnp.int32)
    earlier = jnp.cumsum(onehot, axis=0) - onehot
    slot_index = jnp.sum(earlier * onehot, axis=1)
    target = flat_ids * capacity + slot_index
    source = (
        jnp.full((experts * capacity,), tok_rows, jnp.int32)
        .at[target]
        .set(jnp.arange(route_count, dtype=jnp.int32) // TOP)
    )
    padded_in = jnp.concatenate([moe_in, jnp.zeros((1, width_all), jnp.bfloat16)], axis=0)
    packed = padded_in[source].reshape(experts, 1, capacity, width_all)
    outgoing = jnp.broadcast_to(packed, (experts, 2, capacity, width_all)).reshape(
        2 * experts, capacity, width_all
    )
    arrived = lax.all_to_all(outgoing, ("gx", "gy"), split_axis=0, concat_axis=1, tiled=True)[0]
    gate_in = gate_weight[0]
    up_in = up_weight[0]
    down_in = down_weight[0]
    gate_val = jnp.dot(arrived, gate_in, preferred_element_type=jnp.float32)
    up_val = jnp.dot(arrived, up_in, preferred_element_type=jnp.float32)
    hidden = (jax.nn.silu(gate_val) * up_val).astype(jnp.bfloat16)
    produced = jnp.dot(hidden, down_in, preferred_element_type=jnp.float32).astype(jnp.bfloat16)
    returned = lax.all_to_all(produced[None], ("gx", "gy"), split_axis=1, concat_axis=0, tiled=True)
    summed = (
        returned.reshape(experts, 2, capacity, width_all)
        .astype(jnp.float32)
        .sum(axis=1)
        .reshape(experts * capacity, width_all)
    )
    route_out = summed[target]
    gates_flat = gate_share.reshape(route_count)
    moe_out = jnp.sum((gates_flat[:, None] * route_out).reshape(tok_rows, TOP, width_all), axis=1)
    grad_out = cotangent.astype(jnp.float32)
    grad_gates = jnp.sum(
        route_out.reshape(tok_rows, TOP, width_all) * grad_out[:, None, :], axis=-1
    )
    slot_gate = jnp.zeros((experts * capacity,), jnp.float32).at[target].set(gates_flat)
    padded_grad = jnp.concatenate([grad_out, jnp.zeros((1, width_all), jnp.float32)], axis=0)
    grad_packed = (
        (slot_gate[:, None] * padded_grad[source])
        .astype(jnp.bfloat16)
        .reshape(experts, 1, capacity, width_all)
    )
    grad_outgoing = jnp.broadcast_to(grad_packed, (experts, 2, capacity, width_all)).reshape(
        2 * experts, capacity, width_all
    )
    grad_arrived = lax.all_to_all(
        grad_outgoing, ("gx", "gy"), split_axis=0, concat_axis=1, tiled=True
    )[0]
    rows_in, grad_use = (arrived, grad_arrived)
    gate_use, up_use, hidden_use = (gate_val, up_val, hidden)
    sigmoid_gate = jax.nn.sigmoid(gate_use)
    silu_gate = gate_use * sigmoid_gate
    grad_hidden = contract_cols(grad_use, down_in)
    down_part = contract_rows(hidden_use, grad_use)
    grad_gate = (
        grad_hidden * up_use * sigmoid_gate * (1.0 + gate_use * (1.0 - sigmoid_gate))
    ).astype(jnp.bfloat16)
    grad_up = (grad_hidden * silu_gate).astype(jnp.bfloat16)
    gate_part = contract_rows(rows_in, grad_gate)
    up_part = contract_rows(rows_in, grad_up)
    grad_in = contract_cols(grad_gate, gate_in) + contract_cols(grad_up, up_in)
    grad_back = lax.all_to_all(
        grad_in.astype(jnp.bfloat16)[None], ("gx", "gy"), split_axis=1, concat_axis=0, tiled=True
    )
    grad_summed = (
        grad_back.reshape(experts, 2, capacity, width_all)
        .astype(jnp.float32)
        .sum(axis=1)
        .reshape(experts * capacity, width_all)
    )
    grad_moe_in = jnp.sum(grad_summed[target].reshape(tok_rows, TOP, width_all), axis=1)
    return moe_out, grad_gates, grad_moe_in, gate_part, up_part, down_part


def dense_experts(
    moe_in, all_cot, expert_ids, gate_share, gate_weight, up_weight, down_weight
):
    devices = lax.axis_size("gx") * lax.axis_size("gy")
    experts = devices // 2
    matches = expert_ids[:, :, None] == jnp.arange(experts, dtype=jnp.int32)[None, None, :]
    dense_gates = jnp.sum(jnp.where(matches, gate_share[:, :, None], 0.0), axis=1)
    shares = jnp.repeat(dense_gates.T, 2, axis=0)[:, None, :]
    all_moe, pair, gate_dots, down_part, moe_out = run_experts(
        moe_in, all_cot, shares, gate_weight[0], up_weight[0], down_weight[0], 8
    )
    moe_out = moe_out.reshape(moe_in.shape)
    dots_experts = gate_dots.reshape(experts, 2, -1).sum(axis=1).T
    grad_gates = jnp.sum(jnp.where(matches, dots_experts[:, None, :], 0.0), axis=-1)
    grad_moe_in, gate_part, up_part = pull_experts(all_moe, pair, gate_weight[0], up_weight[0], 9)
    return moe_out, grad_gates, grad_moe_in, gate_part, up_part, down_part


def plain_attention(
    acts, in_weights, out_weight, query_gain, key_gain, attn_gain, doc_ids, cotangent
):
    seq_acts = lax.all_gather(acts, "gy", axis=0, tiled=True)
    full_in = lax.all_gather(jnp.concatenate(in_weights, axis=1), "gx", axis=0, tiled=True)
    out_rows = lax.all_gather(out_weight, "gx", axis=1, tiled=True)
    local_width = full_in.shape[1] // 3
    length = seq_acts.shape[0]
    local_heads = local_width // HD
    projected = jnp.dot(seq_acts, full_in, preferred_element_type=jnp.float32)
    queries = projected[:, :local_width]
    key_raw = projected[:, local_width : 2 * local_width]
    value_ready = (
        projected[:, 2 * local_width :].astype(jnp.bfloat16).reshape(length, local_heads, HD)
    )
    query_float, query_pull = jax.vjp(
        prepare_heads, queries.reshape(length, local_heads, HD), query_gain
    )
    key_float, key_pull = jax.vjp(prepare_heads, key_raw.reshape(length, local_heads, HD), key_gain)
    query_ready = query_float.astype(jnp.bfloat16)
    key_ready = key_float.astype(jnp.bfloat16)
    block_rows = min(512, length)
    block_count = length // block_rows
    score_scale = HD ** (-0.5)
    query_blocks = query_ready.reshape(block_count, block_rows, local_heads, HD)
    doc_blocks = doc_ids.reshape(block_count, block_rows)

    def block_scores(query_block, doc_block):
        scores = (
            jnp.einsum("qhd,khd->hqk", query_block, key_ready, preferred_element_type=jnp.float32)
            * score_scale
        )
        same_doc = doc_block[:, None] == doc_ids[None, :]
        return jnp.where(same_doc[None], scores, NEGATIVE)

    def forward_block(pieces):
        scores = block_scores(pieces[0], pieces[1])
        highest = jnp.max(scores, axis=-1, keepdims=True)
        weights = jnp.exp(scores - highest)
        totals = jnp.sum(weights, axis=-1, keepdims=True)
        shares = (weights / totals).astype(jnp.bfloat16)
        mixed_heads = jnp.einsum(
            "hqk,khd->qhd", shares, value_ready, preferred_element_type=jnp.float32
        )
        return (
            mixed_heads.astype(jnp.bfloat16),
            highest[..., 0] + jnp.log(totals[..., 0]),
            jnp.max(highest[..., 0], axis=-1),
        )

    mixed_blocks, log_totals, peak_blocks = lax.map(forward_block, (query_blocks, doc_blocks))
    mixed_seq = mixed_blocks.reshape(length, local_width)
    attended = lax.psum_scatter(
        jnp.dot(mixed_seq, out_rows, preferred_element_type=jnp.float32),
        "gy",
        scatter_dimension=0,
        tiled=True,
    )

    def back(grad_resid, small):
        seq_grad = lax.all_gather(grad_resid.astype(jnp.bfloat16), "gy", axis=0, tiled=True)
        grad_mixed = contract_cols(seq_grad, out_rows).astype(jnp.bfloat16)
        out_part = contract_rows(seq_grad, mixed_seq)

        def backward_block(running, pieces):
            grad_key, grad_value = running
            query_block, grad_block, log_block, doc_block = pieces
            scores = block_scores(query_block, doc_block)
            weights = jnp.exp(scores - log_block[..., None])
            grad_value = grad_value + jnp.einsum(
                "hqk,qhd->khd",
                weights.astype(jnp.bfloat16),
                grad_block,
                preferred_element_type=jnp.float32,
            )
            grad_weights = jnp.einsum(
                "qhd,khd->hqk", grad_block, value_ready, preferred_element_type=jnp.float32
            )
            inner_sum = jnp.sum(weights * grad_weights, axis=-1, keepdims=True)
            grad_scores = (weights * (grad_weights - inner_sum)).astype(jnp.bfloat16)
            grad_query = (
                jnp.einsum("hqk,khd->qhd", grad_scores, key_ready, preferred_element_type=jnp.float32)
                * score_scale
            )
            grad_key = (
                grad_key
                + jnp.einsum(
                    "hqk,qhd->khd", grad_scores, query_block, preferred_element_type=jnp.float32
                )
                * score_scale
            )
            return ((grad_key, grad_value), grad_query)

        empty_heads = jnp.zeros((length, local_heads, HD), jnp.float32)
        grad_mixed_blocks = grad_mixed.reshape(block_count, block_rows, local_heads, HD)
        (key_grad_heads, value_grad_heads), query_grad_blocks = lax.scan(
            backward_block,
            (empty_heads, empty_heads),
            (query_blocks, grad_mixed_blocks, log_totals, doc_blocks),
        )
        query_raw_grad, query_gain_part = query_pull(query_grad_blocks.reshape(length, local_heads, HD))
        key_raw_grad, key_gain_part = key_pull(key_grad_heads)
        grad_queries = query_raw_grad.reshape(length, local_width).astype(jnp.bfloat16)
        grad_keys = key_raw_grad.reshape(length, local_width).astype(jnp.bfloat16)
        grad_values = value_grad_heads.reshape(length, local_width).astype(jnp.bfloat16)
        grad_heads = jnp.concatenate([grad_queries, grad_keys, grad_values], axis=1)
        acts_part = contract_cols(grad_heads, full_in).astype(jnp.bfloat16)
        in_sum = lax.psum_scatter(
            contract_rows(seq_acts, grad_heads).astype(jnp.bfloat16),
            "gx",
            scatter_dimension=0,
            tiled=True,
        ).astype(jnp.float32)
        grad_acts = lax.psum_scatter(acts_part, "gy", scatter_dimension=0, tiled=True)
        out_sum = lax.psum_scatter(
            out_part.astype(jnp.bfloat16), "gx", scatter_dimension=0, tiled=True
        ).astype(jnp.float32)
        in_sums = (in_sum[:, :local_width], in_sum[:, local_width : 2 * local_width], in_sum[:, 2 * local_width :])
        gain_parts = (None, query_gain_part, key_gain_part)
        return grad_acts.astype(jnp.float32), in_sums, out_sum, sum_everywhere(small, 12), gain_parts

    return attended, jnp.max(peak_blocks, axis=0), None, back


def kernel_attention(
    acts, in_weights, out_weight, query_gain, key_gain, attn_gain, doc_ids, cotangent
):
    length = doc_ids.shape[0]
    halfway = HD // 2
    frequency = jnp.exp(
        jnp.arange(halfway, dtype=jnp.float32) * (-2.0 * jnp.log(10000.0) / HD)
    )
    angles = jnp.arange(length, dtype=jnp.float32)[:, None] * frequency[None, :]
    cosine, sine = jnp.cos(angles), jnp.sin(angles)
    tables = (
        jnp.concatenate([cosine, cosine], axis=1),
        jnp.concatenate([-sine, sine], axis=1),
    )
    docs = doc_ids.reshape(-1, 128)
    attended, seq_acts, full_in, all_cot, saved, peaks = attend(
        acts, in_weights, out_weight, cotangent, query_gain, key_gain, tables, docs, 10
    )
    heads = in_weights[0].shape[1] // HD

    def back(grad_resid, small):
        return attend_back(
            grad_resid.astype(jnp.bfloat16),
            saved,
            query_gain,
            key_gain,
            attn_gain,
            tables,
            docs,
            seq_acts,
            full_in,
            small,
            11,
        )

    return attended, peaks[:heads, 0], all_cot, back


def local(
    tokens,
    cotangent,
    expert_ids,
    doc_ids,
    clip_rank,
    attn_gain,
    moe_gain,
    query_gain,
    key_gain,
    query_weight,
    key_weight,
    value_weight,
    out_weight,
    router_weight,
    gate_weight,
    up_weight,
    down_weight,
):
    inputs = tokens.astype(jnp.float32)
    acts_float, norm_pull = jax.vjp(norm_rows, inputs, attn_gain)
    acts_low = acts_float.astype(jnp.bfloat16)
    in_weights = (query_weight, key_weight, value_weight)
    by_kernels = lax.axis_size("gy") == 8
    local_width = query_weight.shape[1]
    local_heads = local_width // HD
    attention = kernel_attention if by_kernels else plain_attention
    attended, own_peaks, all_cot, attention_back = attention(
        acts_low, in_weights, out_weight, query_gain, key_gain, attn_gain, doc_ids, cotangent
    )
    start_head = lax.axis_index("gy") * local_heads
    peak_slots = lax.dynamic_update_slice(
        jnp.zeros((lax.axis_size("gx"), NH), jnp.float32),
        own_peaks[None],
        (lax.axis_index("gx"), start_head),
    )
    residual = inputs + attended
    moe_float, moe_pull = jax.vjp(norm_rows, residual, moe_gain)
    moe_in = moe_float.astype(jnp.bfloat16)
    logits = jnp.dot(moe_in, router_weight, preferred_element_type=jnp.float32)
    gate_share, gate_pull = jax.vjp(partial(route_gates, expert_ids), logits)
    if by_kernels and router_weight.shape[1] <= 2 * TOP:
        moe_out, grad_gates, grad_moe_in, gate_part, up_part, down_part = dense_experts(
            moe_in, all_cot, expert_ids, gate_share, gate_weight, up_weight, down_weight
        )
    else:
        moe_out, grad_gates, grad_moe_in, gate_part, up_part, down_part = routed_experts(
            moe_in,
            cotangent,
            expert_ids,
            gate_share,
            router_weight,
            gate_weight,
            up_weight,
            down_weight,
        )
    output = (residual + moe_out).astype(jnp.bfloat16)
    grad_out = cotangent.astype(jnp.float32)
    (grad_logits,) = gate_pull(grad_gates)
    grad_logits_low = grad_logits.astype(jnp.bfloat16)
    router_part = contract_rows(moe_in, grad_logits_low)
    grad_moe_in = grad_moe_in + contract_cols(grad_logits_low, router_weight)
    grad_resid_norm, moe_gain_part = moe_pull(grad_moe_in)
    grad_resid = grad_out + grad_resid_norm
    early = (moe_gain_part, router_part.T, peak_slots)
    grad_acts, in_sums, out_sum, early_sum, late = attention_back(grad_resid, flat(early))
    query_sum, key_sum, value_sum = in_sums
    moe_gain_grad, router_flat, peaks = unflat(early_sum, early)
    norm_input_grad, attn_gain_part = norm_pull(grad_acts)
    input_grad = grad_resid + norm_input_grad
    if late[0] is None:
        late = (attn_gain_part, *late[1:])
        late = unflat(sum_everywhere(flat(late), 5), late)
    attn_gain_grad, query_gain_grad, key_gain_grad = late
    router_grad = router_flat.T
    peak_global = jnp.max(peaks, axis=0)
    ranked = -jnp.sort(-peak_global)
    limit = jnp.sum(jnp.where(jnp.arange(NH, dtype=jnp.int32) == clip_rank[0], ranked, 0.0))
    factors = jnp.where(peak_global > limit, limit / peak_global, 1.0)
    own_factors = lax.dynamic_slice_in_dim(factors, start_head, local_heads)
    columns = jnp.repeat(jnp.sqrt(own_factors), HD)
    query_clipped = (query_weight.astype(jnp.float32) * columns[None, :]).astype(jnp.bfloat16)
    key_clipped = (key_weight.astype(jnp.float32) * columns[None, :]).astype(jnp.bfloat16)
    return (
        output,
        input_grad,
        attn_gain_grad,
        moe_gain_grad,
        query_gain_grad,
        key_gain_grad,
        query_sum,
        key_sum,
        value_sum,
        out_sum.T,
        router_grad,
        gate_part[None],
        up_part[None],
        down_part[None],
        query_clipped,
        key_clipped,
        factors,
    )


def solution(mesh):
    placed = (
        P(("gx", "gy"), None),
        P(("gx", "gy"), None),
        P(("gx", "gy"), None),
        P("gx"),
        P(),
        P(),
        P(),
        P(),
        P(),
        P("gx", "gy"),
        P("gx", "gy"),
        P("gx", "gy"),
        P("gy", "gx"),
        P(),
        P(("gx", "gy"), None, None),
        P(("gx", "gy"), None, None),
        P(("gx", "gy"), None, None),
    )
    return jax.shard_map(
        local,
        mesh=mesh,
        in_specs=placed,
        out_specs=(
            P(("gx", "gy"), None),
            P(("gx", "gy"), None),
            P(),
            P(),
            P(),
            P(),
            P("gx", "gy"),
            P("gx", "gy"),
            P("gx", "gy"),
            P("gy", "gx"),
            P(),
            P(("gx", "gy"), None, None),
            P(("gx", "gy"), None, None),
            P(("gx", "gy"), None, None),
            P("gx", "gy"),
            P("gx", "gy"),
            P(),
        ),
        check_vma=False,
    )
```
